32 devices in a mesh: batch: 8 (over z, x), mp: 4 (over y, core).
Axes of the slice: x: 2, y: 2, z: 4, core: 2. Of those that a mesh axis runs over, the one named last changes fastest.
Arguments:
- image_states: bfloat16 [96, 197, 768], P('batch'), may hold values from -6 to 6
- text_states: bfloat16 [96, 40, 768], P('batch'), may hold values from -6 to 6
- caption_lengths: int32 [96], P('batch'), may hold values from 8 to 40, as said below
- image_cotangent: bfloat16 [96, 197, 768], P('batch'), may hold values from -6 to 6
- text_cotangent: bfloat16 [96, 40, 768], P('batch'), may hold values from -6 to 6
- first_gain: float32 [768], replicated, may hold values from 0.5 to 1.5
- first_shift: float32 [768], replicated, may hold values from -0.6 to 0.6
- query_key_value: bfloat16 [768, 3, 768], P(None, None, 'mp'), may hold values from -0.21875 to 0.21875
- query_value_bias: float32 [2, 768], P(None, 'mp'), may hold values from -1.2 to 1.2
- output_weight: bfloat16 [768, 768], P('mp'), may hold values from -1.25 to 1.25
- output_bias: float32 [768], replicated, may hold values from -0.6 to 0.6
- attention_scale: float32 [768], replicated, may hold values from 0.5 to 1.5
- expert_gain: float32 [2, 768], replicated, may hold values from 0.5 to 1.5
- expert_shift: float32 [2, 768], replicated, may hold values from -0.6 to 0.6
- expert_up: bfloat16 [2, 768, 3072], P(None, None, 'mp'), may hold values from -0.21875 to 0.21875
- expert_up_bias: float32 [2, 3072], P(None, 'mp'), may hold values from -1.2 to 1.2
- expert_down: bfloat16 [2, 3072, 768], P(None, 'mp'), may hold values from -0.109375 to 0.109375
- expert_down_bias: float32 [2, 768], replicated, may hold values from -0.6 to 0.6
- feedforward_scale: float32 [768], replicated, may hold values from 0.5 to 1.5
- head_gain: float32 [2, 768], replicated, may hold values from 0.5 to 1.5
- head_shift: float32 [2, 768], replicated, may hold values from -0.6 to 0.6
- head_weight: bfloat16 [2, 768, 768], replicated, may hold values from -0.21875 to 0.21875
- logit_scale: float32 [1], replicated, may hold values from 3.7 to 4.4
Outputs:
- image_output: bfloat16 [96, 197, 768], P('batch')
- text_output: bfloat16 [96, 40, 768], P('batch')
- contrast_loss: float32 [1], replicated
- image_grad: bfloat16 [96, 197, 768], P('batch')
- text_grad: bfloat16 [96, 40, 768], P('batch')
- grad_first_gain: float32 [768], P('batch')
- grad_first_shift: float32 [768], P('batch')
- grad_query_key_value: float32 [768, 3, 768], P('batch', None, 'mp')
- grad_query_value_bias: float32 [2, 768], P(None, 'mp')
- grad_output_weight: float32 [768, 768], P('mp', 'batch')
- grad_output_bias: float32 [768], P('batch')
- grad_attention_scale: float32 [768], P('batch')
- grad_expert_gain: float32 [2, 768], P(None, 'batch')
- grad_expert_shift: float32 [2, 768], P(None, 'batch')
- grad_expert_up: float32 [2, 768, 3072], P(None, 'batch', 'mp')
- grad_expert_up_bias: float32 [2, 3072], P(None, 'mp')
- grad_expert_down: float32 [2, 3072, 768], P(None, 'mp', 'batch')
- grad_expert_down_bias: float32 [2, 768], P(None, 'batch')
- grad_feedforward_scale: float32 [768], P('batch')
- grad_head_gain: float32 [2, 768], P(None, 'batch')
- grad_head_shift: float32 [2, 768], P(None, 'batch')
- grad_head_weight: float32 [2, 768, 768], P(None, 'batch')
- grad_logit_scale: float32 [1], replicated
The draws below stay inside these ranges and needn't reach their ends.
Inputs may be any that keep to these rules, and one draw needn't show every extreme that they name: Caption p occupies positions 0 to caption_lengths[p] - 1 of its row; the rest is padding. In every draw some caption has all 40 positions.
All inputs are finite; a program needn't handle non-finite values.
Results may differ from the reference program's by a relative error of at most 0.02.
Values may be sent and summed in bfloat16 or wider, within the bound.
A program may use at most 256 MiB of HBM per device.

```python
import jax
import jax.numpy as jnp
from jax import lax

D = 768
HEADS = 12
HEAD_DIM = 64
FF = 3072
EMBED = 768
PATCHES = 197
CAPTION = 40
PAIRS_DEV = 12
PAIRS = 96
N_BATCH = 8


def draw_caption_lengths(key, part):
    drawn = jax.random.randint(jax.random.fold_in(key, 11), (PAIRS,), CAPTION // 5, CAPTION + 1, dtype=jnp.int32)
    longest = jax.random.randint(jax.random.fold_in(key, 12), (), 0, PAIRS, dtype=jnp.int32)
    return jnp.where(jnp.arange(PAIRS, dtype=jnp.int32) == longest, CAPTION, drawn).astype(jnp.int32)


def spiked(values, stream_key, source, target, shards_of, factor):
    def block_of(axis_at):
        return (jnp.arange(values.shape[axis_at]) // (values.shape[axis_at] // shards_of)).reshape((-1,) + (1,) * (values.ndim - 1 - axis_at))

    one_side = jax.random.permutation(stream_key, shards_of)[block_of(target)]
    far = (block_of(target) + shards_of // 2) % shards_of
    return jnp.where((block_of(source) == one_side) | (block_of(source) == far), factor * values, values)


def block_scale(rng, dims, cuts, least, high):
    level, own = 1.0, jax.random.fold_in(rng, 6)
    for axis_at, blocks in cuts:
        heights = jnp.exp(jax.random.uniform(jax.random.fold_in(own, axis_at), (blocks,), jnp.float32, least / len(cuts), high / len(cuts)))
        level = level * jnp.repeat(heights, dims[axis_at] // blocks).reshape([-1 if axis == axis_at else 1 for axis in range(len(dims))])
    return level


def noise(rng, shape, spread, limit, split=(), kind=jnp.bfloat16):
    entries = jax.random.normal(rng, shape, jnp.float32) * spread
    if len(split) > 0:
        entries = block_scale(rng, shape, split, -0.22, 0.18) * entries
    return jnp.clip(entries, min=-limit, max=limit).astype(kind)


def heavy_noise(key, extent, width, most, pieces, heavy, kind=jnp.bfloat16):
    entries = width * jax.random.normal(key, extent, jnp.float32)
    if pieces:
        entries = entries * block_scale(key, extent, pieces, -0.22, 0.18)
    return jnp.clip(spiked(entries, jax.random.fold_in(key, 3), *heavy), -most, most).astype(kind)


def setup_inputs(seed: int = 0) -> dict:
    arg_keys = jax.random.split(jax.random.key(seed), 24)
    return {
        "image_states": noise(arg_keys[0], (PAIRS, PATCHES, D), 1.0, 6.0, ((0, 8),)),
        "text_states": noise(arg_keys[1], (PAIRS, CAPTION, D), 1.0, 6.0, ((0, 8),)),
        "caption_lengths": draw_caption_lengths(jax.random.fold_in(arg_keys[23], 71), 0),
        "image_cotangent": heavy_noise(arg_keys[3], (PAIRS, PATCHES, D), 1.0, 6.0, ((0, 8),), (0, 2, 8, 2.0)),
        "text_cotangent": heavy_noise(arg_keys[4], (PAIRS, CAPTION, D), 1.0, 6.0, ((0, 8),), (0, 2, 8, 2.0)),
        "first_gain": jnp.clip(1.0 + 0.1 * jax.random.normal(arg_keys[5], (D,), jnp.float32), 0.5, 1.5),
        "first_shift": noise(arg_keys[6], (D,), 0.1, 0.6, (), jnp.float32),
        "query_key_value": noise(arg_keys[7], (D, 3, D), D ** -0.5, 0.21875, ((2, 4),)),
        "query_value_bias": noise(arg_keys[8], (2, D), 0.2, 1.2, ((1, 4),), jnp.float32),
        "output_weight": noise(arg_keys[9], (D, D), (D // 32) ** -0.5, 1.25, ((0, 4),)),
        "output_bias": noise(arg_keys[10], (D,), 0.1, 0.6, (), jnp.float32),
        "attention_scale": jnp.clip(1.0 + 0.1 * jax.random.normal(arg_keys[11], (D,), jnp.float32), 0.5, 1.5),
        "expert_gain": jnp.clip(1.0 + 0.1 * jax.random.normal(arg_keys[12], (2, D), jnp.float32), 0.5, 1.5),
        "expert_shift": noise(arg_keys[13], (2, D), 0.1, 0.6, (), jnp.float32),
        "expert_up": noise(arg_keys[14], (2, D, FF), D ** -0.5, 0.21875, ((2, 4),)),
        "expert_up_bias": noise(arg_keys[15], (2, FF), 0.2, 1.2, ((1, 4),), jnp.float32),
        "expert_down": noise(arg_keys[16], (2, FF, D), FF ** -0.5, 0.109375, ((1, 4),)),
        "expert_down_bias": noise(arg_keys[17], (2, D), 0.1, 0.6, (), jnp.float32),
        "feedforward_scale": jnp.clip(1.0 + 0.1 * jax.random.normal(arg_keys[18], (D,), jnp.float32), 0.5, 1.5),
        "head_gain": jnp.clip(1.0 + 0.1 * jax.random.normal(arg_keys[19], (2, D), jnp.float32), 0.5, 1.5),
        "head_shift": noise(arg_keys[20], (2, D), 0.1, 0.6, (), jnp.float32),
        "head_weight": noise(arg_keys[21], (2, D, EMBED), D ** -0.5, 0.21875),
        "logit_scale": jnp.clip(jax.random.uniform(arg_keys[22], (1,), jnp.float32, 3.7, 4.4), 3.7, 4.4),
    }


@jax.custom_vjp
def low(v):
    return lax.optimization_barrier(v.astype(jnp.bfloat16)).astype(jnp.float32)

@jax.custom_vjp
def low_back(v):
    return v

def low_keep(v):
    return (low(v), None)

def low_pass(kept, grad):
    return (grad,)

def back_keep(v):
    return (v, None)

def back_low(kept, grad):
    return (low(grad),)
low.defvjp(low_keep, low_pass)
low_back.defvjp(back_keep, back_low)
precise = lax.Precision.HIGHEST

def layer_norm(values, scales, shifts):
    centred = values - lax.optimization_barrier(jnp.mean(values, axis=-1, keepdims=True))
    variance = lax.optimization_barrier(jnp.mean(centred * centred, axis=-1, keepdims=True))
    return centred * lax.rsqrt(variance + 1e-05) * scales + shifts

def attend(normed, query_key_value, query_value_bias, output_weight, valid):
    groups, positions, model_width = normed.shape
    projected = jnp.einsum('gsd,dtf->gstf', normed, query_key_value, precision=precise)
    bias_full = jnp.stack([query_value_bias[0], jnp.zeros_like(query_value_bias[0]), query_value_bias[1]])
    projected = low(low_back(projected + bias_full))
    split_heads = projected.reshape(groups, positions, 3, HEADS, HEAD_DIM)
    query_heads = split_heads[:, :, 0]
    key_heads = split_heads[:, :, 1]
    value_heads = split_heads[:, :, 2]
    scaled = low_back(HEAD_DIM ** (-0.5) * jnp.einsum('gqhe,gkhe->ghqk', query_heads, key_heads, precision=precise))
    masked = jnp.where(valid[:, None, None, :], scaled, -1000000000.0)
    weights = low(jax.nn.softmax(masked, axis=-1))
    mixed_heads = low(low_back(jnp.einsum('ghqk,gkhe->gqhe', weights, value_heads, precision=precise)))
    mixed_heads = mixed_heads.reshape(groups, positions, model_width)
    return low_back(jnp.einsum('gsd,de->gse', mixed_heads, output_weight, precision=precise))

def encode(states, valid, modality, params):
    first_gain, first_shift, query_key_value, query_value_bias, output_weight, output_bias, attention_scale, expert_gain, expert_shift, expert_up, expert_up_bias, expert_down, expert_down_bias, feedforward_scale, head_gain, head_shift, head_weight, logit_scale = params
    normed = low(layer_norm(states, first_gain, first_shift))
    branch_attention = attend(normed, query_key_value, query_value_bias, output_weight, valid)
    attended = states + attention_scale * (branch_attention + output_bias)
    expert_in = low(layer_norm(attended, expert_gain[modality], expert_shift[modality]))
    upward = low_back(jnp.einsum('gsd,df->gsf', expert_in, expert_up[modality], precision=precise)) + expert_up_bias[modality]
    activated = low(jax.nn.gelu(upward, approximate=False))
    downward = low_back(jnp.einsum('gsf,fd->gsd', activated, expert_down[modality], precision=precise))
    final = attended + feedforward_scale * (downward + expert_down_bias[modality])
    head_in = low(layer_norm(final[:, 0, :], head_gain[modality], head_shift[modality]))
    head_proj = low_back(jnp.dot(head_in, head_weight[modality], precision=precise, preferred_element_type=jnp.float32))
    embedded = low(head_proj * lax.rsqrt(lax.optimization_barrier(jnp.sum(head_proj * head_proj, axis=-1, keepdims=True)) + 1e-06))
    return (final, embedded)

def contrast(image_embed, text_embed, logit_scale):
    sharpness = jnp.exp(logit_scale[0])
    logits = sharpness * jnp.dot(image_embed, text_embed.T, precision=precise, preferred_element_type=jnp.float32)
    diagonal = jnp.diagonal(logits)
    row_total = jnp.sum(jax.nn.logsumexp(logits, axis=1) - diagonal)
    column_total = jnp.sum(jax.nn.logsumexp(logits, axis=0) - diagonal)
    return (row_total + column_total) / (2 * PAIRS)

def forward(params, image_float, text_float, text_valid):
    image_valid = jnp.ones((PAIRS_DEV, PATCHES), dtype=bool)

    def group_step(running, inputs):
        image_group, text_group, text_mask = inputs
        image_final, image_embed = encode(image_group, image_valid, 0, params)
        text_final, text_embed = encode(text_group, text_mask, 1, params)
        return (running, (image_final, text_final, image_embed, text_embed))
    image_groups = image_float.reshape(N_BATCH, PAIRS_DEV, PATCHES, D)
    text_groups = text_float.reshape(N_BATCH, PAIRS_DEV, CAPTION, D)
    mask_groups = text_valid.reshape(N_BATCH, PAIRS_DEV, CAPTION)
    unused, stacked = lax.scan(jax.checkpoint(group_step), jnp.zeros((), jnp.float32), (image_groups, text_groups, mask_groups))
    image_final = stacked[0].reshape(PAIRS, PATCHES, D)
    text_final = stacked[1].reshape(PAIRS, CAPTION, D)
    image_embed = stacked[2].reshape(PAIRS, EMBED)
    text_embed = stacked[3].reshape(PAIRS, EMBED)
    loss_value = contrast(image_embed, text_embed, params[17])
    return (image_final, text_final, loss_value.reshape(1))

def reference(image_states, text_states, caption_lengths, image_cotangent, text_cotangent, first_gain, first_shift, query_key_value, query_value_bias, output_weight, output_bias, attention_scale, expert_gain, expert_shift, expert_up, expert_up_bias, expert_down, expert_down_bias, feedforward_scale, head_gain, head_shift, head_weight, logit_scale):
    params = (first_gain.astype(jnp.float32), first_shift.astype(jnp.float32), query_key_value.astype(jnp.float32), query_value_bias.astype(jnp.float32), output_weight.astype(jnp.float32), output_bias.astype(jnp.float32), attention_scale.astype(jnp.float32), expert_gain.astype(jnp.float32), expert_shift.astype(jnp.float32), expert_up.astype(jnp.float32), expert_up_bias.astype(jnp.float32), expert_down.astype(jnp.float32), expert_down_bias.astype(jnp.float32), feedforward_scale.astype(jnp.float32), head_gain.astype(jnp.float32), head_shift.astype(jnp.float32), head_weight.astype(jnp.float32), logit_scale.astype(jnp.float32))
    text_valid = jnp.arange(CAPTION, dtype=jnp.int32)[None, :] < caption_lengths[:, None].astype(jnp.int32)

    def objective(param_set, image_float, text_float):
        return forward(param_set, image_float, text_float, text_valid)
    outputs, pullback = jax.vjp(objective, params, image_states.astype(jnp.float32), text_states.astype(jnp.float32))
    image_final, text_final, loss_value = outputs
    param_grads, image_gradient, text_gradient = pullback((image_cotangent.astype(jnp.float32), text_cotangent.astype(jnp.float32), jnp.ones((1,), jnp.float32)))
    return (image_final.astype(jnp.bfloat16), text_final.astype(jnp.bfloat16), loss_value, image_gradient.astype(jnp.bfloat16), text_gradient.astype(jnp.bfloat16), param_grads[0], param_grads[1], param_grads[2], param_grads[3], param_grads[4], param_grads[5], param_grads[6], param_grads[7], param_grads[8], param_grads[9], param_grads[10], param_grads[11], param_grads[12], param_grads[13], param_grads[14], param_grads[15], param_grads[16], param_grads[17])
```

```python
import functools

import jax
import jax.numpy as jnp
from jax import lax
from jax.experimental import pallas as pl
from jax.experimental.pallas import tpu as pltpu
from jax.sharding import PartitionSpec as P

HEAD_DIM = 64
F32 = jnp.float32
BF16 = jnp.bfloat16
NEG = -1e9
EPS = 1e-5
ORDER = (0, 2, 1, 3)

VMEM_LIMIT = 60 * 1024 * 1024


def params(**kw):
    return pltpu.CompilerParams(vmem_limit_bytes=VMEM_LIMIT, **kw)


def up16(n):
    return -(-n // 16) * 16


def dot(a, b):
    return jnp.dot(a, b, preferred_element_type=F32)


def dot_t(a, b):
    return lax.dot_general(a, b, (((1,), (1,)), ((), ())), preferred_element_type=F32)


def t_dot(a, b):
    return lax.dot_general(a, b, (((0,), (0,)), ((), ())), preferred_element_type=F32)


def normalise(x):
    c = x - jnp.mean(x, axis=-1, keepdims=True)
    v = jnp.mean(c * c, axis=-1, keepdims=True)
    r = lax.rsqrt(v + EPS)
    return c * r, r


def norm_back(n, r, dn):
    a = jnp.mean(dn, axis=-1, keepdims=True)
    b = jnp.mean(dn * n, axis=-1, keepdims=True)
    return (dn - a - n * b) * r


def gelu_parts(u):
    big = 0.5 * (1.0 + lax.erf(u * 0.7071067811865476))
    small = 0.3989422804014327 * jnp.exp(-0.5 * u * u)
    return big, small


def gelu_low(u):
    return (u * (0.5 * (1.0 + lax.erf(u * 0.7071067811865476)))).astype(BF16)


def softmax_rows(scores):
    m = jnp.max(scores, axis=-1, keepdims=True)
    e = jnp.exp(scores - m)
    return e * (1.0 / jnp.sum(e, axis=-1, keepdims=True))


def attend_kernel(dims, order, lens, img, txt, gain, shift, wt, bias, ow,
                  normed, qkv, mixed, keep, send, rows):
    patches, caption, ip, tp, quarter, width = dims
    i = pl.program_id(0)
    slab = ip + tp

    @pl.when(i == 0)
    def _():
        rows[...] = jnp.zeros_like(rows)

    def one_norm(p, c):
        rows[0:patches, :] = img[p].astype(F32)
        rows[ip:ip + caption, :] = txt[p].astype(F32)
        n, _ = normalise(rows[...])
        normed[p] = (n * gain[...] + shift[...]).astype(BF16)
        return c

    lax.fori_loop(0, quarter, one_norm, 0)
    model = normed.shape[-1]
    proj = dot_t(normed[...].reshape(quarter * slab, model), wt[...]) + bias[...]
    qkv[...] = proj.astype(BF16).reshape(quarter, slab, 3 * width)
    low = lax.broadcasted_iota(jnp.int32, (1, 128), 1) < HEAD_DIM
    img_ok = lax.broadcasted_iota(jnp.int32, (1, ip), 1) < patches
    txt_at = lax.broadcasted_iota(jnp.int32, (1, tp), 1)

    def one_pair(p, c):
        length = lens[order[i] * quarter + p]
        for lo, hi, ok in ((0, ip, img_ok), (ip, slab, txt_at < length)):
            for g in range(width // 128):
                q = qkv[p, lo:hi, g * 128:(g + 1) * 128] * jnp.asarray(HEAD_DIM ** -0.5, BF16)
                k = qkv[p, lo:hi, width + g * 128:width + (g + 1) * 128]
                v = qkv[p, lo:hi, 2 * width + g * 128:2 * width + (g + 1) * 128]
                outs = []
                for sel in (low, ~low):
                    s = dot_t(jnp.where(sel, q, jnp.zeros_like(q)), k)
                    w = softmax_rows(jnp.where(ok, s, NEG)).astype(BF16)
                    outs.append(dot(w, v))
                mixed[p, lo:hi, g * 128:(g + 1) * 128] = jnp.where(low, outs[0], outs[1]).astype(BF16)
        return c

    lax.fori_loop(0, quarter, one_pair, 0)
    part = dot(mixed[...].reshape(quarter * slab, width), ow[...])
    part = part.astype(BF16).reshape(quarter, slab, model)

    @pl.when(i < 2)
    def _():
        keep[...] = part

    @pl.when(i >= 2)
    def _():
        send[...] = part


def attend(dims, order, lens, img, txt, gain, shift, wt, bias, ow):
    patches, caption, ip, tp, quarter, width = dims
    model = img.shape[-1]
    slab = ip + tp
    pairs = 4 * quarter
    whole = lambda a: pl.BlockSpec(a.shape, lambda i, o, n: (0,) * a.ndim)
    block = lambda cols, at: pl.BlockSpec((quarter, slab, cols), at)
    return pl.pallas_call(
        functools.partial(attend_kernel, dims),
        grid_spec=pltpu.PrefetchScalarGridSpec(
            num_scalar_prefetch=2,
            grid=(4,),
            in_specs=[
                pl.BlockSpec((quarter, patches, model), lambda i, o, n: (o[i], 0, 0)),
                pl.BlockSpec((quarter, caption, model), lambda i, o, n: (o[i], 0, 0)),
                whole(gain), whole(shift), whole(wt), whole(bias), whole(ow),
            ],
            out_specs=[
                block(model, lambda i, o, n: (i, 0, 0)),
                block(3 * width, lambda i, o, n: (i, 0, 0)),
                block(width, lambda i, o, n: (i, 0, 0)),
                block(model, lambda i, o, n: (jnp.minimum(i, 1), 0, 0)),
                block(model, lambda i, o, n: (jnp.maximum(i - 2, 0), 0, 0)),
            ],
            scratch_shapes=[pltpu.VMEM((slab, model), F32)],
        ),
        out_shape=[
            jax.ShapeDtypeStruct((pairs, slab, model), BF16),
            jax.ShapeDtypeStruct((pairs, slab, 3 * width), BF16),
            jax.ShapeDtypeStruct((pairs, slab, width), BF16),
            jax.ShapeDtypeStruct((2 * quarter, slab, model), BF16),
            jax.ShapeDtypeStruct((2 * quarter, slab, model), BF16),
        ],
        compiler_params=params(),
        cost_estimate=pl.CostEstimate(
            flops=2 * pairs * slab * model * width * 4, bytes_accessed=30_000_000, transcendentals=0),
        name="attend",
    )(order, lens, img, txt, gain, shift, wt, bias, ow)


def residual_kernel(dims, order, keep, recv, img, txt, scale, bias, gain, shift, attended, expert, rows):
    patches, caption, ip, tp, quarter, width = dims

    @pl.when(pl.program_id(0) == 0)
    def _():
        rows[...] = jnp.zeros_like(rows)

    def one(p, c):
        rows[0:patches, :] = img[p].astype(F32)
        rows[ip:ip + caption, :] = txt[p].astype(F32)
        a = keep[p].astype(F32) + recv[p].astype(F32)
        x = rows[...] + scale[...] * (a + bias[...])
        attended[p] = x
        n, _ = normalise(x)
        expert[p, 0:ip, :] = (n[0:ip] * gain[0:1] + shift[0:1]).astype(BF16)
        expert[p, ip:, :] = (n[ip:] * gain[1:2] + shift[1:2]).astype(BF16)
        return c

    lax.fori_loop(0, quarter, one, 0)


def residual(dims, order, keep, recv, img, txt, scale, bias, gain, shift):
    patches, caption, ip, tp, quarter, width = dims
    model = img.shape[-1]
    slab = ip + tp
    whole = lambda a: pl.BlockSpec(a.shape, lambda i, o: (0,) * a.ndim)
    block = pl.BlockSpec((quarter, slab, model), lambda i, o: (i, 0, 0))
    return pl.pallas_call(
        functools.partial(residual_kernel, dims),
        grid_spec=pltpu.PrefetchScalarGridSpec(
            num_scalar_prefetch=1,
            grid=(2,),
            in_specs=[
                block, block,
                pl.BlockSpec((quarter, patches, model), lambda i, o: (o[i], 0, 0)),
                pl.BlockSpec((quarter, caption, model), lambda i, o: (o[i], 0, 0)),
                whole(scale), whole(bias), whole(gain), whole(shift),
            ],
            out_specs=[block, block],
            scratch_shapes=[pltpu.VMEM((slab, model), F32)],
        ),
        out_shape=[
            jax.ShapeDtypeStruct((2 * quarter, slab, model), F32),
            jax.ShapeDtypeStruct((2 * quarter, slab, model), BF16),
        ],
        compiler_params=params(),
        cost_estimate=pl.CostEstimate(flops=40_000_000, bytes_accessed=20_000_000, transcendentals=0),
        name="residual",
    )(order, keep, recv, img, txt, scale, bias, gain, shift)


def expert_kernel(dims, order, own, peer, img, txt, scale, up, up_bias, down,
                  act, dup, ddown, down_keep, down_send, dexp_keep, dexp_send, bias_grad, ins, rows):
    patches, caption, ip, tp, quarter, width = dims
    slab = ip + tp
    i = pl.program_id(0)
    model = own.shape[-1]

    @pl.when(i == 0)
    def _():
        rows[...] = jnp.zeros_like(rows)
        bias_grad[...] = jnp.zeros_like(bias_grad)

    @pl.when(i < 2)
    def _():
        ins[...] = own[...]

    @pl.when(i >= 2)
    def _():
        ins[...] = peer[...]

    at = lax.broadcasted_iota(jnp.int32, (slab, 1), 0)
    inner = (at != 0) & (at != ip)

    def one(p, c):
        rows[0:patches, :] = img[p].astype(F32)
        rows[ip:ip + caption, :] = txt[p].astype(F32)
        ddown[p] = jnp.where(inner, rows[...] * scale[...], 0.0).astype(BF16)
        return c

    lax.fori_loop(0, quarter, one, 0)
    for m, lo, hi in ((0, 0, ip), (1, ip, slab)):
        count = quarter * (hi - lo)
        e = ins[:, lo:hi, :].reshape(count, model)
        u = dot(e, up[m]) + up_bias[m:m + 1]
        big, small = gelu_parts(u)
        a = (u * big).astype(BF16)
        act[:, lo:hi, :] = a.reshape(quarter, hi - lo, -1)
        slope = big + u * small
        d = dot(a, down[m]).astype(BF16).reshape(quarter, hi - lo, model)
        g = ddown[:, lo:hi, :].reshape(count, model)
        du = dot_t(g, down[m]) * slope
        bias_grad[m:m + 1, :] += jnp.sum(du, axis=0, keepdims=True)
        low = du.astype(BF16)
        dup[:, lo:hi, :] = low.reshape(quarter, hi - lo, -1)
        x = dot_t(low, up[m]).astype(BF16).reshape(quarter, hi - lo, model)

        @pl.when(i < 2)
        def _():
            down_keep[:, lo:hi, :] = d
            dexp_keep[:, lo:hi, :] = x

        @pl.when(i >= 2)
        def _():
            down_send[:, lo:hi, :] = d
            dexp_send[:, lo:hi, :] = x


def experts(dims, order, own, peer, img, txt, scale, up, up_bias, down):
    patches, caption, ip, tp, quarter, width = dims
    model = own.shape[-1]
    hidden = up.shape[-1]
    slab = ip + tp
    pairs = 4 * quarter
    whole = lambda a: pl.BlockSpec(a.shape, lambda i, o: (0,) * a.ndim)
    first = pl.BlockSpec((quarter, slab, model), lambda i, o: (jnp.minimum(i, 1), 0, 0))
    last = pl.BlockSpec((quarter, slab, model), lambda i, o: (jnp.maximum(i - 2, 0), 0, 0))
    half = jax.ShapeDtypeStruct((2 * quarter, slab, model), BF16)
    return pl.pallas_call(
        functools.partial(expert_kernel, dims),
        grid_spec=pltpu.PrefetchScalarGridSpec(
            num_scalar_prefetch=1,
            grid=(4,),
            in_specs=[
                first, last,
                pl.BlockSpec((quarter, patches, model), lambda i, o: (o[i], 0, 0)),
                pl.BlockSpec((quarter, caption, model), lambda i, o: (o[i], 0, 0)),
                whole(scale), whole(up), whole(up_bias), whole(down),
            ],
            out_specs=[
                pl.BlockSpec((quarter, slab, hidden), lambda i, o: (i, 0, 0)),
                pl.BlockSpec((quarter, slab, hidden), lambda i, o: (i, 0, 0)),
                pl.BlockSpec((quarter, slab, model), lambda i, o: (i, 0, 0)),
                first, last, first, last,
                pl.BlockSpec((2, hidden), lambda i, o: (0, 0)),
            ],
            scratch_shapes=[pltpu.VMEM((quarter, slab, model), BF16), pltpu.VMEM((slab, model), F32)],
        ),
        out_shape=[
            jax.ShapeDtypeStruct((pairs, slab, hidden), BF16),
            jax.ShapeDtypeStruct((pairs, slab, hidden), BF16),
            jax.ShapeDtypeStruct((pairs, slab, model), BF16),
            half, half, half, half,
            jax.ShapeDtypeStruct((2, hidden), F32),
        ],
        compiler_params=params(),
        cost_estimate=pl.CostEstimate(
            flops=8 * pairs * slab * model * hidden, bytes_accessed=40_000_000, transcendentals=0),
        name="experts",
    )(order, own, peer, img, txt, scale, up, up_bias, down)


def expert_grads_kernel(dims, own, peer, act, dup, ddown, ce, ca, cu, cd, out, acc):
    patches, caption, ip, tp, quarter, width = dims
    slab = ip + tp
    i = pl.program_id(0)

    def add(src):
        for m, lo, hi in ((0, 0, ip), (1, ip, slab)):
            count = quarter * (hi - lo)
            e = src[:, lo:hi, :].reshape(count, -1)
            acc[m] += t_dot(e, dup[:, lo:hi, :].reshape(count, -1))

    @pl.when(i == 0)
    def _():
        for m in range(2):
            acc[m] = t_dot(ce[m], cu[m])
            acc[2 + m] = t_dot(cd[m], ca[m])

    for m, lo, hi in ((0, 0, ip), (1, ip, slab)):
        count = quarter * (hi - lo)
        acc[2 + m] += t_dot(ddown[:, lo:hi, :].reshape(count, -1), act[:, lo:hi, :].reshape(count, -1))

    @pl.when(i < 2)
    def _():
        add(own)

    @pl.when(i >= 2)
    def _():
        add(peer)

    @pl.when(i == 3)
    def _():
        out[...] = acc[...].astype(BF16)


def expert_grads(dims, own, peer, act, dup, ddown, ce, ca, cu, cd):
    patches, caption, ip, tp, quarter, width = dims
    model = own.shape[-1]
    hidden = act.shape[-1]
    slab = ip + tp
    assert hidden == model
    whole = lambda a: pl.BlockSpec(a.shape, lambda i: (0,) * a.ndim)
    first = pl.BlockSpec((quarter, slab, model), lambda i: (jnp.minimum(i, 1), 0, 0))
    last = pl.BlockSpec((quarter, slab, model), lambda i: (jnp.maximum(i - 2, 0), 0, 0))
    block = pl.BlockSpec((quarter, slab, hidden), lambda i: (i, 0, 0))
    return pl.pallas_call(
        functools.partial(expert_grads_kernel, dims),
        grid=(4,),
        in_specs=[first, last, block, block, block, whole(ce), whole(ca), whole(cu), whole(cd)],
        out_specs=pl.BlockSpec((4, model, hidden), lambda i: (0, 0, 0)),
        scratch_shapes=[pltpu.VMEM((4, model, hidden), F32)],
        out_shape=jax.ShapeDtypeStruct((4, model, hidden), BF16),
        compiler_params=params(),
        cost_estimate=pl.CostEstimate(
            flops=4 * 4 * quarter * slab * model * hidden, bytes_accessed=40_000_000, transcendentals=0),
        name="expert_grads",
    )(own, peer, act, dup, ddown, ce, ca, cu, cd)


def class_forward_kernel(e, up, up_bias, down, out):
    for m in range(2):
        u = dot(e[m], up[m]) + up_bias[m:m + 1]
        out[m] = dot(gelu_low(u), down[m])


def class_forward(e, up, up_bias, down):
    return pl.pallas_call(
        class_forward_kernel,
        out_shape=jax.ShapeDtypeStruct(e.shape, F32),
        compiler_params=params(),
        cost_estimate=pl.CostEstimate(flops=200_000_000, bytes_accessed=5_000_000, transcendentals=0),
        name="class_forward",
    )(e, up, up_bias, down)


def class_back_kernel(e, cot, dclass, scale, up, up_bias, down, act, dup, ddown, dexp, bias_grad):
    for m in range(2):
        u = dot(e[m], up[m]) + up_bias[m:m + 1]
        big, small = gelu_parts(u)
        act[m] = (u * big).astype(BF16)
        g = ((cot[m] + dclass[m]) * scale[...]).astype(BF16)
        ddown[m] = g
        du = dot_t(g, down[m]) * (big + u * small)
        bias_grad[m:m + 1, :] = jnp.sum(du, axis=0, keepdims=True)
        low = du.astype(BF16)
        dup[m] = low
        dexp[m] = dot_t(low, up[m])


def class_back(e, cot, dclass, scale, up, up_bias, down):
    hidden = up.shape[-1]
    shape = e.shape[:2] + (hidden,)
    return pl.pallas_call(
        class_back_kernel,
        out_shape=[
            jax.ShapeDtypeStruct(shape, BF16),
            jax.ShapeDtypeStruct(shape, BF16),
            jax.ShapeDtypeStruct(e.shape, BF16),
            jax.ShapeDtypeStruct(e.shape, F32),
            jax.ShapeDtypeStruct((2, hidden), F32),
        ],
        compiler_params=params(),
        cost_estimate=pl.CostEstimate(flops=300_000_000, bytes_accessed=5_000_000, transcendentals=0),
        name="class_back",
    )(e, cot, dclass, scale, up, up_bias, down)


def contrast_kernel(cls, gain, shift, weight, scale, head_in, dproj, dcls, gains, shifts, scalars):
    total = cls.shape[1]
    sharp = jnp.exp(scale[...])
    normal, inverse, proj, unit, embed = [], [], [], [], []
    for m in range(2):
        n, r = normalise(cls[m])
        h = (n * gain[m:m + 1] + shift[m:m + 1]).astype(BF16)
        head_in[m] = h
        y = dot(h, weight[m])
        u = lax.rsqrt(jnp.sum(y * y, axis=-1, keepdims=True) + 1e-6)
        normal.append(n)
        inverse.append(r)
        proj.append(y)
        unit.append(u)
        embed.append((y * u).astype(BF16))
    logits = sharp * dot_t(embed[0], embed[1])
    row_max = jnp.max(logits, axis=1, keepdims=True)
    row_lse = row_max + jnp.log(jnp.sum(jnp.exp(logits - row_max), axis=1, keepdims=True))
    col_max = jnp.max(logits, axis=0, keepdims=True)
    col_lse = col_max + jnp.log(jnp.sum(jnp.exp(logits - col_max), axis=0, keepdims=True))
    same = (lax.broadcasted_iota(jnp.int32, (total, total), 0)
            == lax.broadcasted_iota(jnp.int32, (total, total), 1))
    both = jnp.exp(logits - row_lse) + jnp.exp(logits - col_lse)
    dlogits = jnp.where(same, both - 2.0, both) * (1.0 / (2 * total))
    diagonal = jnp.sum(jnp.where(same, logits, 0.0), axis=1, keepdims=True)
    loss = (jnp.sum(row_lse - diagonal, keepdims=True) + jnp.sum(col_lse, keepdims=True)
            - jnp.sum(diagonal, keepdims=True)) * (1.0 / (2 * total))
    slope = jnp.sum(jnp.sum(dlogits * logits, axis=1, keepdims=True), axis=0, keepdims=True)
    scalars[0:1, :] = jnp.broadcast_to(loss.reshape(1, 1), (1, 128))
    scalars[1:2, :] = jnp.broadcast_to(slope, (1, 128))
    high = lax.Precision.HIGHEST
    wide = [e.astype(F32) for e in embed]
    dembed = [
        sharp * jnp.dot(dlogits, wide[1], precision=high, preferred_element_type=F32),
        sharp * lax.dot_general(dlogits, wide[0], (((0,), (0,)), ((), ())), precision=high,
                                preferred_element_type=F32),
    ]
    for m in range(2):
        u, y, d = unit[m], proj[m], dembed[m]
        dp = (u * d - u * u * u * y * jnp.sum(y * d, axis=-1, keepdims=True)).astype(BF16)
        dproj[m] = dp
        dh = dot_t(dp, weight[m])
        gains[m:m + 1, :] = jnp.sum(dh * normal[m], axis=0, keepdims=True)
        shifts[m:m + 1, :] = jnp.sum(dh, axis=0, keepdims=True)
        dcls[m] = norm_back(normal[m], inverse[m], dh * gain[m:m + 1])


def contrast(cls, gain, shift, weight, scale):
    model = cls.shape[-1]
    return pl.pallas_call(
        contrast_kernel,
        out_shape=[
            jax.ShapeDtypeStruct(cls.shape, BF16),
            jax.ShapeDtypeStruct(cls.shape[:2] + (weight.shape[-1],), BF16),
            jax.ShapeDtypeStruct(cls.shape, F32),
            jax.ShapeDtypeStruct((2, model), F32),
            jax.ShapeDtypeStruct((2, model), F32),
            jax.ShapeDtypeStruct((2, 128), F32),
        ],
        compiler_params=params(),
        cost_estimate=pl.CostEstimate(flops=1_000_000_000, bytes_accessed=5_000_000, transcendentals=0),
        name="contrast",
    )(cls, gain, shift, weight, scale)


def load_rows(dims, p, img, txt, rows):
    patches, caption, ip, tp, quarter, width = dims
    rows[0:patches, :] = img[p].astype(F32)
    rows[ip:ip + caption, :] = txt[p].astype(F32)


def final_kernel(dims, order, keep, recv, far, attended, img, txt, dclass, scale, bias, fin_img, fin_txt, sums, rows, cls):
    patches, caption, ip, tp, quarter, width = dims
    rows[...] = jnp.zeros_like(rows)
    sums[...] = jnp.zeros_like(sums)
    cls[...] = jnp.zeros_like(cls)

    def one(p, c):
        load_rows(dims, p, img, txt, rows)
        rows[0:1, :] += dclass[p, 0:1, :]
        rows[ip:ip + 1, :] += dclass[p, 1:2, :]
        d = keep[p].astype(F32) + recv[p].astype(F32) + far[p].astype(F32)
        for m, lo, hi in ((0, 0, ip), (1, ip, ip + tp)):
            b = d[lo:hi] + bias[m:m + 1]
            f = attended[p, lo:hi, :] + scale[...] * b
            if m == 0:
                fin_img[p] = f[0:patches].astype(BF16)
            else:
                fin_txt[p] = f[0:caption].astype(BF16)
            g = rows[lo:hi, :]
            sums[0:1, :] += jnp.sum(g * b, axis=0, keepdims=True)
            sums[1 + m:2 + m, :] += jnp.sum(g, axis=0, keepdims=True) * scale[...]
        return c

    lax.fori_loop(0, quarter, one, 0)


def final_rows(dims, order, keep, recv, far, attended, img, txt, dclass, scale, bias):
    patches, caption, ip, tp, quarter, width = dims
    model = img.shape[-1]
    slab = ip + tp
    whole = lambda a: pl.BlockSpec(a.shape, lambda i, o: (0,) * a.ndim)
    block = pl.BlockSpec((quarter, slab, model), lambda i, o: (0, 0, 0))
    return pl.pallas_call(
        functools.partial(final_kernel, dims),
        grid_spec=pltpu.PrefetchScalarGridSpec(
            num_scalar_prefetch=1,
            grid=(1,),
            in_specs=[
                block, block, block, block,
                pl.BlockSpec((quarter, patches, model), lambda i, o: (o[0], 0, 0)),
                pl.BlockSpec((quarter, caption, model), lambda i, o: (o[0], 0, 0)),
                whole(dclass), whole(scale), whole(bias),
            ],
            out_specs=[
                pl.BlockSpec((quarter, patches, model), lambda i, o: (0, 0, 0)),
                pl.BlockSpec((quarter, caption, model), lambda i, o: (0, 0, 0)),
                pl.BlockSpec((3, model), lambda i, o: (0, 0)),
            ],
            scratch_shapes=[pltpu.VMEM((slab, model), F32), pltpu.VMEM((8, model), F32)],
        ),
        out_shape=[
            jax.ShapeDtypeStruct((quarter, patches, model), BF16),
            jax.ShapeDtypeStruct((quarter, caption, model), BF16),
            jax.ShapeDtypeStruct((3, model), F32),
        ],
        compiler_params=params(),
        cost_estimate=pl.CostEstimate(flops=20_000_000, bytes_accessed=10_000_000, transcendentals=0),
        name="final_rows",
    )(order, keep, recv, far, attended, img, txt, dclass, scale, bias)


def norm_two_kernel(dims, order, keep, recv, far, extra, attended, a_keep, a_recv, img, txt, dclass,
                    gain, scale, bias, dattended, dattn, sums, rows, ups):
    patches, caption, ip, tp, quarter, width = dims
    rows[...] = jnp.zeros_like(rows)
    sums[...] = jnp.zeros_like(sums)

    def one(p, c):
        load_rows(dims, p, img, txt, rows)
        rows[0:1, :] += dclass[p, 0:1, :]
        rows[ip:ip + 1, :] += dclass[p, 1:2, :]
        ups[...] = keep[p].astype(F32) + recv[p].astype(F32) + far[p].astype(F32)
        ups[0:1, :] += extra[p, 0:1, :]
        ups[ip:ip + 1, :] += extra[p, 1:2, :]
        for m, lo, hi in ((0, 0, ip), (1, ip, ip + tp)):
            n, r = normalise(attended[p, lo:hi, :])
            dy = ups[lo:hi, :]
            sums[m:m + 1, :] += jnp.sum(dy * n, axis=0, keepdims=True)
            sums[2 + m:3 + m, :] += jnp.sum(dy, axis=0, keepdims=True)
            d = rows[lo:hi, :] + norm_back(n, r, dy * gain[m:m + 1])
            dattended[p, lo:hi, :] = d
            sd = d * scale[...]
            dattn[p, lo:hi, :] = sd.astype(BF16)
            a = a_keep[p, lo:hi, :].astype(F32) + a_recv[p, lo:hi, :].astype(F32) + bias[...]
            sums[4:5, :] += jnp.sum(d * a, axis=0, keepdims=True)
            sums[5:6, :] += jnp.sum(sd, axis=0, keepdims=True)
        return c

    lax.fori_loop(0, quarter, one, 0)


def norm_two(dims, order, keep, recv, far, extra, attended, a_keep, a_recv, img, txt, dclass, gain, scale, bias):
    patches, caption, ip, tp, quarter, width = dims
    model = img.shape[-1]
    slab = ip + tp
    whole = lambda a: pl.BlockSpec(a.shape, lambda i, o: (0,) * a.ndim)
    block = pl.BlockSpec((quarter, slab, model), lambda i, o: (0, 0, 0))
    return pl.pallas_call(
        functools.partial(norm_two_kernel, dims),
        grid_spec=pltpu.PrefetchScalarGridSpec(
            num_scalar_prefetch=1,
            grid=(1,),
            in_specs=[
                block, block, block, whole(extra), block, block, block,
                pl.BlockSpec((quarter, patches, model), lambda i, o: (o[0], 0, 0)),
                pl.BlockSpec((quarter, caption, model), lambda i, o: (o[0], 0, 0)),
                whole(dclass), whole(gain), whole(scale), whole(bias),
            ],
            out_specs=[block, block, pl.BlockSpec((6, model), lambda i, o: (0, 0))],
            scratch_shapes=[pltpu.VMEM((slab, model), F32), pltpu.VMEM((slab, model), F32)],
        ),
        out_shape=[
            jax.ShapeDtypeStruct((quarter, slab, model), F32),
            jax.ShapeDtypeStruct((quarter, slab, model), BF16),
            jax.ShapeDtypeStruct((6, model), F32),
        ],
        compiler_params=params(),
        cost_estimate=pl.CostEstimate(flops=40_000_000, bytes_accessed=15_000_000, transcendentals=0),
        name="norm_two",
    )(order, keep, recv, far, extra, attended, a_keep, a_recv, img, txt, dclass, gain, scale, bias)


def attend_back_kernel(dims, order, lens, d_own, d_peer, normed, qkv, mixed, wt, ow,
                       keep, send, grad_own, grad_peer, col_sums, dattn, dmixed, dqkv, acc):
    patches, caption, ip, tp, quarter, width = dims
    i = pl.program_id(0)
    slab = ip + tp
    count = quarter * slab
    model = normed.shape[-1]

    @pl.when(i == 0)
    def _():
        dattn[...] = d_own[...]
        acc[...] = jnp.zeros_like(acc)
        col_sums[...] = jnp.zeros_like(col_sums)

    @pl.when(i == 1)
    def _():
        dattn[...] = d_peer[...]

    d_rows = dattn[...].reshape(count, model)
    dmixed[...] = dot_t(d_rows, ow[...]).astype(BF16).reshape(quarter, slab, width)
    low = lax.broadcasted_iota(jnp.int32, (1, 128), 1) < HEAD_DIM
    img_ok = lax.broadcasted_iota(jnp.int32, (1, ip), 1) < patches
    txt_at = lax.broadcasted_iota(jnp.int32, (1, tp), 1)
    eighth = HEAD_DIM ** -0.5

    def one_pair(p, c):
        length = lens[order[2 * i] * quarter + p]
        for lo, hi, ok in ((0, ip, img_ok), (ip, slab, txt_at < length)):
            for g in range(width // 128):
                c0 = slice(g * 128, (g + 1) * 128)
                c1 = slice(width + g * 128, width + (g + 1) * 128)
                c2 = slice(2 * width + g * 128, 2 * width + (g + 1) * 128)
                q = qkv[p, lo:hi, c0] * jnp.asarray(eighth, BF16)
                k = qkv[p, lo:hi, c1]
                v = qkv[p, lo:hi, c2]
                do = dmixed[p, lo:hi, c0]
                dqs, dks, dvs = [], [], []
                for sel in (low, ~low):
                    s = dot_t(jnp.where(sel, q, jnp.zeros_like(q)), k)
                    w = softmax_rows(jnp.where(ok, s, NEG))
                    dw = dot_t(jnp.where(sel, do, jnp.zeros_like(do)), v)
                    dvs.append(t_dot(w.astype(BF16), do))
                    ds = (w * (dw - jnp.sum(w * dw, axis=-1, keepdims=True))).astype(BF16)
                    dqs.append(dot(ds, k))
                    dks.append(t_dot(ds, q))
                dqkv[p, lo:hi, c0] = (jnp.where(low, dqs[0], dqs[1]) * eighth).astype(BF16)
                dqkv[p, lo:hi, c1] = jnp.where(low, dks[0], dks[1]).astype(BF16)
                dqkv[p, lo:hi, c2] = jnp.where(low, dvs[0], dvs[1]).astype(BF16)
        return c

    lax.fori_loop(0, quarter, one_pair, 0)
    dp = dqkv[...].reshape(count, 3 * width)
    part = dot(dp, wt[...]).astype(BF16).reshape(quarter, slab, model)
    acc[:, 0:3 * width] += t_dot(normed[...].reshape(count, model), dp)
    acc[:, 3 * width:] += t_dot(d_rows, mixed[...].reshape(count, width))
    col_sums[...] += jnp.sum(dp.astype(F32), axis=0, keepdims=True)

    @pl.when(i == 0)
    def _():
        keep[...] = part

    @pl.when(i == 1)
    def _():
        send[...] = part
        half = width // 2
        for t in range(4):
            grad_own[:, t * half:(t + 1) * half] = acc[:, t * width:t * width + half].astype(BF16)
            grad_peer[:, t * half:(t + 1) * half] = acc[:, t * width + half:(t + 1) * width].astype(BF16)


def attend_back(dims, order, lens, d_own, d_peer, normed, qkv, mixed, wt, ow):
    patches, caption, ip, tp, quarter, width = dims
    model = normed.shape[-1]
    slab = ip + tp
    whole = lambda a: pl.BlockSpec(a.shape, lambda i, o, n: (0,) * a.ndim)
    one = pl.BlockSpec((quarter, slab, model), lambda i, o, n: (0, 0, 0))
    step = lambda cols: pl.BlockSpec((quarter, slab, cols), lambda i, o, n: (2 * i, 0, 0))
    grad = pl.BlockSpec((model, 2 * width), lambda i, o, n: (0, 0))
    return pl.pallas_call(
        functools.partial(attend_back_kernel, dims),
        grid_spec=pltpu.PrefetchScalarGridSpec(
            num_scalar_prefetch=2,
            grid=(2,),
            in_specs=[one, one, step(model), step(3 * width), step(width), whole(wt), whole(ow)],
            out_specs=[one, one, grad, grad, pl.BlockSpec((1, 3 * width), lambda i, o, n: (0, 0))],
            scratch_shapes=[
                pltpu.VMEM((quarter, slab, model), BF16),
                pltpu.VMEM((quarter, slab, width), BF16),
                pltpu.VMEM((quarter, slab, 3 * width), BF16),
                pltpu.VMEM((model, 4 * width), F32),
            ],
        ),
        out_shape=[
            jax.ShapeDtypeStruct((quarter, slab, model), BF16),
            jax.ShapeDtypeStruct((quarter, slab, model), BF16),
            jax.ShapeDtypeStruct((model, 2 * width), BF16),
            jax.ShapeDtypeStruct((model, 2 * width), BF16),
            jax.ShapeDtypeStruct((1, 3 * width), F32),
        ],
        compiler_params=params(),
        cost_estimate=pl.CostEstimate(
            flops=4 * 2 * quarter * slab * model * width * 4, bytes_accessed=20_000_000, transcendentals=0),
        name="attend_back",
    )(order, lens, d_own, d_peer, normed, qkv, mixed, wt, ow)


def norm_one_kernel(dims, order, keep, recv, dattended, img, txt, gain, d_img, d_txt, sums, rows):
    patches, caption, ip, tp, quarter, width = dims
    rows[...] = jnp.zeros_like(rows)
    sums[...] = jnp.zeros_like(sums)

    def one(p, c):
        load_rows(dims, p, img, txt, rows)
        n, r = normalise(rows[...])
        dy = keep[p].astype(F32) + recv[p].astype(F32)
        sums[0:1, :] += jnp.sum(dy * n, axis=0, keepdims=True)
        sums[1:2, :] += jnp.sum(dy, axis=0, keepdims=True)
        d = dattended[p] + norm_back(n, r, dy * gain[...])
        d_img[p] = d[0:patches].astype(BF16)
        d_txt[p] = d[ip:ip + caption].astype(BF16)
        return c

    lax.fori_loop(0, quarter, one, 0)


def norm_one(dims, order, keep, recv, dattended, img, txt, gain):
    patches, caption, ip, tp, quarter, width = dims
    model = img.shape[-1]
    slab = ip + tp
    whole = lambda a: pl.BlockSpec(a.shape, lambda i, o: (0,) * a.ndim)
    block = pl.BlockSpec((quarter, slab, model), lambda i, o: (0, 0, 0))
    return pl.pallas_call(
        functools.partial(norm_one_kernel, dims),
        grid_spec=pltpu.PrefetchScalarGridSpec(
            num_scalar_prefetch=1,
            grid=(1,),
            in_specs=[
                block, block, block,
                pl.BlockSpec((quarter, patches, model), lambda i, o: (o[0], 0, 0)),
                pl.BlockSpec((quarter, caption, model), lambda i, o: (o[0], 0, 0)),
                whole(gain),
            ],
            out_specs=[
                pl.BlockSpec((quarter, patches, model), lambda i, o: (0, 0, 0)),
                pl.BlockSpec((quarter, caption, model), lambda i, o: (0, 0, 0)),
                pl.BlockSpec((2, model), lambda i, o: (0, 0)),
            ],
            scratch_shapes=[pltpu.VMEM((slab, model), F32)],
        ),
        out_shape=[
            jax.ShapeDtypeStruct((quarter, patches, model), BF16),
            jax.ShapeDtypeStruct((quarter, caption, model), BF16),
            jax.ShapeDtypeStruct((2, model), F32),
        ],
        compiler_params=params(),
        cost_estimate=pl.CostEstimate(flops=20_000_000, bytes_accessed=10_000_000, transcendentals=0),
        name="norm_one",
    )(order, keep, recv, dattended, img, txt, gain)


def swap(value, axis, bit):
    size = lax.axis_size(axis)
    return lax.ppermute(value, axis, [(j, j ^ bit) for j in range(size)])


def to_core(value):
    return swap(value, "mp", 1)


def to_y(value):
    return swap(value, "mp", 2)


def sum_over(value, axis):
    bit = 1
    while bit < lax.axis_size(axis):
        value = value + swap(value, axis, bit)
        bit *= 2
    return value


def gather_batch(value):
    at = lax.axis_index("batch")
    bit = 1
    while bit < lax.axis_size("batch"):
        other = swap(value, "batch", bit)
        mine_first = (at & bit) == 0
        value = jnp.concatenate(
            [jnp.where(mine_first, value, other), jnp.where(mine_first, other, value)], axis=1)
        bit *= 2
    return value


def absolute(value, quarter, me):
    parts = [value[:, r * quarter:(r + 1) * quarter] for r in range(4)]
    by_xor = [parts[ORDER.index(x)] for x in range(4)]
    out = []
    for q in range(4):
        pick = by_xor[q]
        for m in range(1, 4):
            pick = jnp.where(me == m, by_xor[q ^ m], pick)
        out.append(pick)
    return jnp.concatenate(out, axis=1)


def gather_rows(own, me):
    quarter = own.shape[0]
    near = jnp.stack([own, to_y(own)])
    far = to_core(near)
    out = jnp.zeros((4,) + own.shape, own.dtype)
    for r, value in enumerate((near[0], near[1], far[0], far[1])):
        out = lax.dynamic_update_slice(out, value[None], (me ^ ORDER[r],) + (0,) * own.ndim)
    return out.reshape((4 * quarter,) + own.shape[1:])


def add_low(a, b):
    return (a.astype(F32) + b.astype(F32)).astype(BF16)


def per_device(
    image_states, text_states, caption_lengths, image_cotangent, text_cotangent,
    first_gain, first_shift, query_key_value, query_value_bias, output_weight, output_bias,
    attention_scale, expert_gain, expert_shift, expert_up, expert_up_bias, expert_down,
    expert_down_bias, feedforward_scale, head_gain, head_shift, head_weight, logit_scale,
):
    pairs, patches, model = image_states.shape
    caption = text_states.shape[1]
    local = query_key_value.shape[2]
    width = 2 * local
    quarter = pairs // 4
    assert lax.axis_size("mp") == 4 and pairs == 4 * quarter and width % 128 == 0
    ip, tp = up16(patches), up16(caption)
    dims = (patches, caption, ip, tp, quarter, width)
    me = lax.axis_index("mp")
    batch_at = lax.axis_index("batch")
    batch_size = lax.axis_size("batch")
    order = me ^ jnp.asarray(ORDER, jnp.int32)
    row = lambda v: v.reshape(1, -1)

    own_w = jnp.transpose(query_key_value, (1, 2, 0)).reshape(3 * local, model)
    both = jnp.concatenate([own_w, output_weight])
    far = to_y(both)
    far_bias = to_y(query_value_bias)
    wt = jnp.concatenate(
        [own_w.reshape(3, local, model), far[:3 * local].reshape(3, local, model)], axis=1
    ).reshape(3 * width, model)
    ow = jnp.concatenate([output_weight, far[3 * local:]])
    bias_pair = jnp.concatenate([query_value_bias, far_bias], axis=1)
    bias = jnp.concatenate([bias_pair[0], jnp.zeros_like(bias_pair[0]), bias_pair[1]]).reshape(1, -1)

    normed, qkv, mixed, a_keep, a_send = attend(
        dims, order, caption_lengths, image_states, text_states, row(first_gain), row(first_shift), wt, bias, ow)
    a_recv = to_core(a_send)
    attended, e_own = residual(
        dims, order, a_keep, a_recv, image_states, text_states, row(attention_scale), row(output_bias),
        expert_gain, expert_shift)
    e_peer = to_core(e_own)

    pad = lambda v: jnp.pad(v, ((0, 0), (0, up16(pairs) - pairs), (0, 0)))
    class_of = lambda v: jnp.stack([v[:, 0], v[:, ip]])
    class_att = class_of(attended)
    class_att = jnp.concatenate([class_att, to_core(class_att)], axis=1)
    class_e = pad(jnp.concatenate([class_of(e_own), class_of(e_peer)], axis=1))
    class_cot = jnp.stack([image_cotangent[:, 0], text_cotangent[:, 0]]).astype(F32)
    class_cot = class_cot.reshape(2, 4, quarter, model)
    class_cot = jnp.concatenate(
        [lax.dynamic_index_in_dim(class_cot, order[r], 1, keepdims=False) for r in range(4)], axis=1)

    def sum_mp(value):
        other = to_core(value)
        value = value + jnp.concatenate([other[:, 2 * quarter:], other[:, :2 * quarter]], axis=1)
        other = to_y(value)
        parts = [other[:, r * quarter:(r + 1) * quarter] for r in (1, 0, 3, 2)]
        return value + jnp.concatenate(parts, axis=1)

    class_down = sum_mp(class_forward(class_e, expert_up, expert_up_bias, expert_down)[:, :pairs])
    class_final = class_att + feedforward_scale * (class_down + expert_down_bias[:, None, :])
    all_class = gather_batch(absolute(class_final, quarter, me))
    head_in, dproj, dcls, grad_head_gain, grad_head_shift, scalars = contrast(
        all_class, head_gain, head_shift, head_weight, logit_scale.reshape(1, 1))
    contrast_loss = scalars[0, :1]
    grad_logit_scale = scalars[1, :1]
    cols = model // batch_size
    head_cols = lax.dynamic_slice_in_dim(head_in, batch_at * cols, cols, axis=2)
    grad_head_weight = jnp.einsum("mnc,mne->mce", head_cols, dproj, preferred_element_type=F32)
    mine = lax.dynamic_slice_in_dim(dcls, batch_at * pairs, pairs, axis=1).reshape(2, 4, quarter, model)
    dclass = jnp.concatenate(
        [lax.dynamic_index_in_dim(mine, order[r], 1, keepdims=False) for r in range(4)], axis=1)
    c_act, c_dup, c_ddown, c_dexp, c_bias = class_back(
        class_e, pad(class_cot), pad(dclass), row(feedforward_scale), expert_up, expert_up_bias, expert_down)
    extra = sum_mp(c_dexp[:, :pairs])[:, :quarter]
    extra = jnp.transpose(extra, (1, 0, 2))
    dclass_own = jnp.transpose(dclass[:, :quarter], (1, 0, 2))

    act, dup, ddown, d_keep, d_send, x_keep, x_send, up_bias_part = experts(
        dims, order, e_own, e_peer, image_cotangent, text_cotangent, row(feedforward_scale),
        expert_up, expert_up_bias, expert_down)
    x_recv = to_core(x_send)
    x_far = to_y(add_low(x_keep[quarter:], x_recv[quarter:]))
    d_recv = to_core(d_send)
    d_far = to_y(add_low(d_keep[quarter:], d_recv[quarter:]))
    expert_grad = expert_grads(dims, e_own, e_peer, act, dup, ddown, class_e, c_act, c_dup, c_ddown)
    expert_grad = lax.psum_scatter(expert_grad, "batch", scatter_dimension=1, tiled=True).astype(F32)
    grad_expert_up = expert_grad[:2]
    grad_expert_down = jnp.transpose(expert_grad[2:], (0, 2, 1))

    dattended, dattn, sums_two = norm_two(
        dims, order, x_keep, x_recv, x_far, extra, attended, a_keep, a_recv, image_cotangent, text_cotangent,
        dclass_own, expert_gain, row(attention_scale), row(output_bias))
    dattn_peer = to_core(dattn)
    fin_img, fin_txt, sums_fin = final_rows(
        dims, order, d_keep, d_recv, d_far, attended, image_cotangent, text_cotangent, dclass_own,
        row(feedforward_scale), expert_down_bias)
    image_output = gather_rows(fin_img, me)
    text_output = gather_rows(fin_txt, me)

    n_keep, n_send, grad_own, grad_peer, col_sums = attend_back(
        dims, order, caption_lengths, dattn, dattn_peer, normed, qkv, mixed, wt, ow)
    n_recv = to_core(n_send)
    d_img, d_txt, sums_one = norm_one(
        dims, order, n_keep, n_recv, dattended, image_states, text_states, row(first_gain))
    image_grad = gather_rows(d_img, me)
    text_grad = gather_rows(d_txt, me)

    attn_grad = jnp.concatenate([grad_own, grad_peer], axis=1)
    attn_grad = lax.psum_scatter(attn_grad, "batch", scatter_dimension=0, tiled=True)
    attn_grad = attn_grad[:, :2 * width].astype(F32) + to_y(attn_grad[:, 2 * width:]).astype(F32)
    grad_query_key_value = attn_grad[:, :3 * local].reshape(cols, 3, local)
    grad_output_weight = jnp.transpose(attn_grad[:, 3 * local:])

    own_sums = jnp.concatenate([sums_one, sums_two, sums_fin])
    own_sums = sum_over(own_sums, "mp")
    heads = col_sums.reshape(3, 2, local)[::2]
    heads = heads[:, 0] + to_y(heads[:, 1])
    up_sums = up_bias_part + c_bias
    flat = jnp.concatenate([own_sums.reshape(-1), heads.reshape(-1), up_sums.reshape(-1)])
    count = flat.shape[0]
    flat = jnp.pad(flat, (0, -count % 1024)).reshape(-1, 128)
    flat = sum_over(flat, "batch").reshape(-1)[:count]
    rows_done = own_sums.shape[0]
    own_sums = flat[:rows_done * model].reshape(rows_done, model)
    heads = flat[rows_done * model:rows_done * model + 2 * local].reshape(2, local)
    grad_expert_up_bias = flat[rows_done * model + 2 * local:].reshape(up_sums.shape)
    mine = lax.dynamic_slice_in_dim(own_sums, batch_at * cols, cols, axis=1)
    head_gain_mine = lax.dynamic_slice_in_dim(grad_head_gain, batch_at * cols, cols, axis=1)
    head_shift_mine = lax.dynamic_slice_in_dim(grad_head_shift, batch_at * cols, cols, axis=1)
    return (
        image_output,
        text_output,
        contrast_loss,
        image_grad,
        text_grad,
        mine[0],
        mine[1],
        grad_query_key_value,
        heads,
        grad_output_weight,
        mine[7],
        mine[6],
        mine[2:4],
        mine[4:6],
        grad_expert_up,
        grad_expert_up_bias,
        grad_expert_down,
        mine[9:11],
        mine[8],
        head_gain_mine,
        head_shift_mine,
        grad_head_weight,
        grad_logit_scale,
    )


def solution(mesh):
    return jax.shard_map(
        per_device,
        mesh=mesh,
        in_specs=(
            P("batch", None, None),
            P("batch", None, None),
            P("batch"),
            P("batch", None, None),
            P("batch", None, None),
            P(),
            P(),
            P(None, None, "mp"),
            P(None, "mp"),
            P("mp", None),
            P(),
            P(),
            P(),
            P(),
            P(None, None, "mp"),
            P(None, "mp"),
            P(None, "mp", None),
            P(),
            P(),
            P(),
            P(),
            P(),
            P(),
        ),
        out_specs=(
            P("batch", None, None),
            P("batch", None, None),
            P(),
            P("batch", None, None),
            P("batch", None, None),
            P("batch"),
            P("batch"),
            P("batch", None, "mp"),
            P(None, "mp"),
            P("mp", "batch"),
            P("batch"),
            P("batch"),
            P(None, "batch"),
            P(None, "batch"),
            P(None, "batch", "mp"),
            P(None, "mp"),
            P(None, "mp", "batch"),
            P(None, "batch"),
            P("batch"),
            P(None, "batch"),
            P(None, "batch"),
            P(None, "batch", None),
            P(),
        ),
        check_vma=False,
    )
```

```python
import functools
from typing import NamedTuple

import jax
import jax.numpy as jnp
from jax import lax
from jax.experimental import pallas as pl
from jax.experimental.pallas import tpu as pltpu
from jax.sharding import PartitionSpec as P

HEAD_DIM = 64
F32 = jnp.float32
BF16 = jnp.bfloat16
NEG = -1e9
EPS = 1e-5
ORDER = (0, 2, 1, 3)

VMEM_LIMIT = 60 * 1024 * 1024


def params(**kw):
    return pltpu.CompilerParams(vmem_limit_bytes=VMEM_LIMIT, **kw)


def up16(n):
    return -(-n // 16) * 16


def dot(a, b):
    return jnp.dot(a, b, preferred_element_type=F32)


def dot_t(a, b):
    return lax.dot_general(a, b, (((1,), (1,)), ((), ())), preferred_element_type=F32)


def t_dot(a, b):
    return lax.dot_general(a, b, (((0,), (0,)), ((), ())), preferred_element_type=F32)


def normalise(x):
    c = x - jnp.mean(x, axis=-1, keepdims=True)
    v = jnp.mean(c * c, axis=-1, keepdims=True)
    r = lax.rsqrt(v + EPS)
    return c * r, r


def norm_back(n, r, dn):
    a = jnp.mean(dn, axis=-1, keepdims=True)
    b = jnp.mean(dn * n, axis=-1, keepdims=True)
    return (dn - a - n * b) * r


def gelu_parts(u):
    big = 0.5 * (1.0 + lax.erf(u * 0.7071067811865476))
    small = 0.3989422804014327 * jnp.exp(-0.5 * u * u)
    return big, small


def gelu_low(u):
    return (u * (0.5 * (1.0 + lax.erf(u * 0.7071067811865476)))).astype(BF16)


def softmax_rows(scores):
    m = jnp.max(scores, axis=-1, keepdims=True)
    e = jnp.exp(scores - m)
    return e * (1.0 / jnp.sum(e, axis=-1, keepdims=True))


def tie(value, *after):
    return lax.optimization_barrier((value,) + after)[0]


def load_rows(dims, p, img, txt, rows):
    rows[0:dims.patches, :] = img[p].astype(F32)
    rows[dims.ip:dims.ip + dims.caption, :] = txt[p].astype(F32)


def spec_whole(a):
    return pl.BlockSpec(a.shape, lambda *_: (0,) * a.ndim)


class Dims(NamedTuple):
    patches: int
    caption: int
    ip: int
    tp: int
    slab: int
    quarter: int
    local: int


GAIN1, SHIFT1, A_SCALE, A_BIAS, GAIN2, SHIFT2, F_SCALE, F_BIAS, H_GAIN, H_SHIFT = 0, 1, 2, 3, 4, 6, 8, 9, 11, 13


def vector(table, at, count=1):
    return table[at:at + count, :]


def copy_rows(dst, at, src, start, count):
    dst[at:at + count, :] = src[start:start + count, :]


def parts_of(dims):
    return 2 * HEAD_DIM, HEAD_DIM


def key_tail(dims, length):
    at = dims.patches // 16 * 16
    return ((0, dims.ip, at, dims.patches), (dims.ip, dims.slab, 0, length))


def hide(scores, start, limit):
    if start >= scores.shape[0]:
        return scores
    tail = scores[start:]
    at = start + lax.broadcasted_iota(jnp.int32, (tail.shape[0], 1), 0)
    tail = jnp.where(at < limit, tail, NEG)
    return tail if start == 0 else jnp.concatenate([scores[:start], tail], axis=0)


def split_pair(value):
    low = lax.broadcasted_iota(jnp.int32, (1, 128), 1) < HEAD_DIM
    zero = jnp.zeros_like(value)
    return jnp.concatenate([jnp.where(low, value, zero), jnp.where(low, zero, value)], axis=0)


def join_pair(value):
    low = lax.broadcasted_iota(jnp.int32, (1, 128), 1) < HEAD_DIM
    half = value.shape[0] // 2
    return jnp.where(low, value[:half], value[half:])


def softmax_keys(scores):
    e = jnp.exp(scores - jnp.max(scores, axis=0, keepdims=True))
    return e * (1.0 / jnp.sum(e, axis=0, keepdims=True))


def pair_weights(q, k, start, limit):
    return softmax_keys(hide(dot_t(k, split_pair(q)), start, limit))


def scaled(q):
    return q * jnp.asarray(HEAD_DIM ** -0.5, BF16)


def attend_tiles(dims, lens, quarter_at, qkv, mixed):
    tiles = mixed.shape[-1] // 128

    def one_pair(p, c):
        length = lens[quarter_at * dims.quarter + p]
        for lo, hi, start, limit in key_tail(dims, length):
            for g in range(tiles):
                q, k, v = [qkv[p, lo:hi, (t * tiles + g) * 128:(t * tiles + g + 1) * 128] for t in range(3)]
                w = pair_weights(scaled(q), k, start, limit).astype(BF16)
                mixed[p, lo:hi, g * 128:(g + 1) * 128] = join_pair(t_dot(w, v)).astype(BF16)
        return c

    lax.fori_loop(0, dims.quarter, one_pair, 0)


def attend_own_kernel(dims, order, lens, img, txt, vec, bias, wo, normed, qkv, rest, mixed, rows, w, b):
    i = pl.program_id(0)
    local = dims.local
    two, one_head = parts_of(dims)

    @pl.when(i == 0)
    def _():
        rows[...] = jnp.zeros_like(rows)
        w[...] = jnp.zeros_like(w)
        b[...] = jnp.zeros_like(b)
        for t in range(3):
            copy_rows(w, t * 2 * two, wo, t * local, local)
        b[0:1, 0:local] = bias[0:1, :]
        b[0:1, 4 * two:4 * two + local] = bias[1:2, :]

    def one_norm(p, c):
        load_rows(dims, p, img, txt, rows)
        n, _ = normalise(rows[...])
        normed[p] = (n * vector(vec, GAIN1) + vector(vec, SHIFT1)).astype(BF16)
        return c

    lax.fori_loop(0, dims.quarter, one_norm, 0)
    model = normed.shape[-1]
    proj = (dot_t(normed[...].reshape(dims.quarter * dims.slab, model), w[...]) + b[0:1, :]).astype(BF16)
    proj = proj.reshape(dims.quarter, dims.slab, 6 * two)
    for t in range(3):
        qkv[:, :, t * two:(t + 1) * two] = proj[:, :, 2 * t * two:(2 * t + 1) * two]
        rest[:, :, t * two:(t + 1) * two] = proj[:, :, (2 * t + 1) * two:(2 * t + 2) * two]
    attend_tiles(dims, lens, order[i], qkv, mixed)


def attend_own(dims, order, lens, img, txt, vec, bias, wo):
    model = img.shape[-1]
    pairs = 4 * dims.quarter
    block = lambda cols: pl.BlockSpec((dims.quarter, dims.slab, cols), lambda i, o, n: (i, 0, 0))
    shape = lambda cols: jax.ShapeDtypeStruct((pairs, dims.slab, cols), BF16)
    return pl.pallas_call(
        functools.partial(attend_own_kernel, dims),
        grid_spec=pltpu.PrefetchScalarGridSpec(
            num_scalar_prefetch=2,
            grid=(4,),
            in_specs=[
                pl.BlockSpec((dims.quarter, dims.patches, model), lambda i, o, n: (o[i], 0, 0)),
                pl.BlockSpec((dims.quarter, dims.caption, model), lambda i, o, n: (o[i], 0, 0)),
                spec_whole(vec), spec_whole(bias), spec_whole(wo),
            ],
            out_specs=[block(model), block(384), block(384), block(128)],
            scratch_shapes=[pltpu.VMEM((dims.slab, model), F32), pltpu.VMEM((768, model), BF16),
                            pltpu.VMEM((8, 768), F32)],
        ),
        out_shape=[shape(model), shape(384), shape(384), shape(128)],
        compiler_params=params(),
        cost_estimate=pl.CostEstimate(
            flops=1536 * pairs * dims.slab * model, bytes_accessed=30_000_000, transcendentals=0),
        name="attend_own",
    )(order, lens, img, txt, vec, bias, wo)


def attend_far_kernel(dims, order, lens, normed, rest, own, bias, wo, wf, qkv, mixed, keep, send, w, ow, b):
    i = pl.program_id(0)
    local = dims.local
    two, one_head = parts_of(dims)
    count = dims.quarter * dims.slab
    model = normed.shape[-1]

    @pl.when(i == 0)
    def _():
        w[...] = jnp.zeros_like(w)
        b[...] = jnp.zeros_like(b)
        for t in range(3):
            copy_rows(w, t * 2 * two, wf, t * local, two)
            copy_rows(w, t * 2 * two + two + one_head, wf, t * local + two, one_head)
        for t, at in ((0, 0), (1, 4 * two)):
            b[0:1, at:at + two] = bias[t:t + 1, 0:two]
            b[0:1, at + two + one_head:at + 2 * two] = bias[t:t + 1, two:]
        copy_rows(ow, 0, wo, 3 * local, two)
        copy_rows(ow, two, wf, 3 * local, two)
        copy_rows(ow, 2 * two, wo, 3 * local + two, one_head)
        copy_rows(ow, 2 * two + one_head, wf, 3 * local + two, one_head)

    proj = (dot_t(normed[...].reshape(count, model), w[...]) + b[0:1, :]).astype(BF16)
    proj = proj.reshape(dims.quarter, dims.slab, 6 * two)
    for t in range(3):
        at = 2 * t * two
        qkv[:, :, at:at + two] = proj[:, :, at:at + two]
        qkv[:, :, at + two:at + 2 * two] = proj[:, :, at + two:at + 2 * two] + rest[:, :, t * two:(t + 1) * two]
    attend_tiles(dims, lens, order[(i + 2) % 4], qkv, mixed)
    part = dot(own[...].reshape(count, two), ow[0:two, :])
    part = part + dot(mixed[...].reshape(count, 2 * two), ow[two:, :])
    part = part.astype(BF16).reshape(dims.quarter, dims.slab, model)

    @pl.when(i < 2)
    def _():
        send[...] = part

    @pl.when(i >= 2)
    def _():
        keep[...] = part


def attend_far(dims, order, lens, normed, rest, own, bias, wo, wf):
    model = normed.shape[-1]
    pairs = 4 * dims.quarter
    at = lambda i: (i + 2) % 4
    block = lambda cols, f: pl.BlockSpec((dims.quarter, dims.slab, cols), lambda i, o, n: (f(i), 0, 0))
    shape = lambda count, cols: jax.ShapeDtypeStruct((count, dims.slab, cols), BF16)
    return pl.pallas_call(
        functools.partial(attend_far_kernel, dims),
        grid_spec=pltpu.PrefetchScalarGridSpec(
            num_scalar_prefetch=2,
            grid=(4,),
            in_specs=[
                block(model, at), block(384, at), block(128, at),
                spec_whole(bias), spec_whole(wo), spec_whole(wf),
            ],
            out_specs=[
                block(768, at), block(256, at),
                block(model, lambda i: jnp.maximum(i - 2, 0)), block(model, lambda i: jnp.minimum(i, 1)),
            ],
            scratch_shapes=[pltpu.VMEM((768, model), BF16), pltpu.VMEM((384, model), BF16),
                            pltpu.VMEM((8, 768), F32)],
        ),
        out_shape=[
            shape(pairs, 768), shape(pairs, 256),
            shape(2 * dims.quarter, model), shape(2 * dims.quarter, model),
        ],
        compiler_params=params(),
        cost_estimate=pl.CostEstimate(
            flops=2304 * pairs * dims.slab * model, bytes_accessed=30_000_000, transcendentals=0),
        name="attend_far",
    )(order, lens, normed, rest, own, bias, wo, wf)


def residual_kernel(dims, order, keep, recv, img, txt, vec, attended, expert, cls, rows):
    i = pl.program_id(0)
    ip = dims.ip

    @pl.when(i == 0)
    def _():
        rows[...] = jnp.zeros_like(rows)
        cls[...] = jnp.zeros_like(cls)

    load_rows(dims, 0, img, txt, rows)
    a = keep[0].astype(F32) + recv[0].astype(F32)
    x = rows[...] + vector(vec, A_SCALE) * (a + vector(vec, A_BIAS))
    n, _ = normalise(x)
    e_img = n[0:ip] * vector(vec, GAIN2) + vector(vec, SHIFT2)
    e_txt = n[ip:] * vector(vec, GAIN2 + 1) + vector(vec, SHIFT2 + 1)
    expert[0, 0:ip, :] = e_img.astype(BF16)
    expert[0, ip:, :] = e_txt.astype(BF16)
    for j, v in enumerate((x[0:1], x[ip:ip + 1], e_img[0:1], e_txt[0:1])):
        cls[j, pl.ds(i, 1), :] = v

    @pl.when(i < dims.quarter)
    def _():
        attended[0] = x


def residual(dims, order, keep, recv, img, txt, vec):
    model = img.shape[-1]
    quarter = dims.quarter
    block = pl.BlockSpec((1, dims.slab, model), lambda i, o: (i, 0, 0))
    pair = lambda i, o: (o[i // quarter] * quarter + i % quarter, 0, 0)
    return pl.pallas_call(
        functools.partial(residual_kernel, dims),
        grid_spec=pltpu.PrefetchScalarGridSpec(
            num_scalar_prefetch=1,
            grid=(2 * quarter,),
            in_specs=[
                block, block,
                pl.BlockSpec((1, dims.patches, model), pair),
                pl.BlockSpec((1, dims.caption, model), pair),
                spec_whole(vec),
            ],
            out_specs=[
                pl.BlockSpec((1, dims.slab, model), lambda i, o: (jnp.minimum(i, quarter - 1), 0, 0)),
                block,
                pl.BlockSpec((4, 8, model), lambda i, o: (0, 0, 0)),
            ],
            scratch_shapes=[pltpu.VMEM((dims.slab, model), F32)],
        ),
        out_shape=[
            jax.ShapeDtypeStruct((quarter, dims.slab, model), F32),
            jax.ShapeDtypeStruct((2 * quarter, dims.slab, model), BF16),
            jax.ShapeDtypeStruct((4, 8, model), F32),
        ],
        compiler_params=params(),
        cost_estimate=pl.CostEstimate(flops=40_000_000, bytes_accessed=20_000_000, transcendentals=0),
        name="residual",
    )(order, keep, recv, img, txt, vec)


def expert_kernel(dims, seq, peer, own, img, txt, vec, up, up_bias, down,
                  act, dup, ddown, d_send, d_keep, x_send, x_keep, bias_grad, cot, ins, rows):
    ip, slab, quarter = dims.ip, dims.slab, dims.quarter
    i = pl.program_id(0)
    model = own.shape[-1]

    @pl.when(i == 0)
    def _():
        rows[...] = jnp.zeros_like(rows)
        bias_grad[...] = jnp.zeros_like(bias_grad)
        cot[...] = jnp.zeros_like(cot)
        ins[...] = peer[...]

    @pl.when(i == 1)
    def _():
        ins[...] = own[...]

    at = lax.broadcasted_iota(jnp.int32, (slab, 1), 0)
    inner = (at != 0) & (at != ip)

    def one(p, c):
        load_rows(dims, p, img, txt, rows)
        cot[0, pl.ds(8 * i + p, 1), :] = rows[0:1, :]
        cot[1, pl.ds(8 * i + p, 1), :] = rows[ip:ip + 1, :]
        ddown[p] = jnp.where(inner, rows[...] * vector(vec, F_SCALE), 0.0).astype(BF16)
        return c

    lax.fori_loop(0, quarter, one, 0)
    for m, lo, hi in ((0, 0, ip), (1, ip, slab)):
        count = quarter * (hi - lo)
        e = ins[:, lo:hi, :].reshape(count, model)
        u = dot(e, up[m]) + up_bias[m:m + 1]
        big, small = gelu_parts(u)
        a = (u * big).astype(BF16)
        act[:, lo:hi, :] = a.reshape(quarter, hi - lo, -1)
        slope = big + u * small
        d = dot(a, down[m]).astype(BF16).reshape(quarter, hi - lo, model)
        g = ddown[:, lo:hi, :].reshape(count, model)
        du = dot_t(g, down[m]) * slope
        bias_grad[m:m + 1, :] += jnp.sum(du, axis=0, keepdims=True)
        low = du.astype(BF16)
        dup[:, lo:hi, :] = low.reshape(quarter, hi - lo, -1)
        x = dot_t(low, up[m]).astype(BF16).reshape(quarter, hi - lo, model)

        @pl.when(i == 0)
        def _():
            d_send[:, lo:hi, :] = d
            x_send[:, lo:hi, :] = x

        @pl.when(i == 1)
        def _():
            d_keep[:, lo:hi, :] = d
            x_keep[:, lo:hi, :] = x


def experts(dims, name, half, seq, peer, own, img, txt, vec, up, up_bias, down):
    model = own.shape[-1]
    hidden = up.shape[-1]
    slab, quarter = dims.slab, dims.quarter
    fixed = pl.BlockSpec((quarter, slab, model), lambda i, o: (half, 0, 0))
    first = pl.BlockSpec((quarter, slab, model), lambda i, o: (0, 0, 0))
    step = lambda cols: pl.BlockSpec((quarter, slab, cols), lambda i, o: (i, 0, 0))
    shape = lambda n, cols: jax.ShapeDtypeStruct((n * quarter, slab, cols), BF16)
    return pl.pallas_call(
        functools.partial(expert_kernel, dims),
        grid_spec=pltpu.PrefetchScalarGridSpec(
            num_scalar_prefetch=1,
            grid=(2,),
            in_specs=[
                fixed, fixed,
                pl.BlockSpec((quarter, dims.patches, model), lambda i, o: (o[i], 0, 0)),
                pl.BlockSpec((quarter, dims.caption, model), lambda i, o: (o[i], 0, 0)),
                spec_whole(vec), spec_whole(up), spec_whole(up_bias), spec_whole(down),
            ],
            out_specs=[
                step(hidden), step(hidden), step(model),
                first, first, first, first,
                pl.BlockSpec((2, hidden), lambda i, o: (0, 0)),
                pl.BlockSpec((2, 16, model), lambda i, o: (0, 0, 0)),
            ],
            scratch_shapes=[pltpu.VMEM((quarter, slab, model), BF16), pltpu.VMEM((slab, model), F32)],
        ),
        out_shape=[
            shape(2, hidden), shape(2, hidden), shape(2, model),
            shape(1, model), shape(1, model), shape(1, model), shape(1, model),
            jax.ShapeDtypeStruct((2, hidden), F32),
            jax.ShapeDtypeStruct((2, 16, model), F32),
        ],
        compiler_params=params(),
        cost_estimate=pl.CostEstimate(
            flops=16 * quarter * slab * model * hidden, bytes_accessed=20_000_000, transcendentals=0),
        name=name,
    )(seq, peer, own, img, txt, vec, up, up_bias, down)


def expert_grads_kernel(dims, peer, own, act_a, dup_a, ddn_a, act_b, dup_b, ddn_b, ce, ca, cu, cd, out, acc):
    i = pl.program_id(0)

    def add(e, dup, ddn, act):
        for m, lo, hi in ((0, 0, dims.ip), (1, dims.ip, dims.slab)):
            count = dims.quarter * (hi - lo)
            flat = lambda ref: ref[:, lo:hi, :].reshape(count, -1)
            acc[m] += t_dot(flat(e), flat(dup))
            acc[2 + m] += t_dot(flat(ddn), flat(act))

    @pl.when(i == 0)
    def _():
        for m in range(2):
            acc[m] = t_dot(ce[m], cu[m])
            acc[2 + m] = t_dot(cd[m], ca[m])

    for j, refs in enumerate((
        (peer, dup_a, ddn_a, act_a), (own, dup_a, ddn_a, act_a),
        (peer, dup_b, ddn_b, act_b), (own, dup_b, ddn_b, act_b),
    )):
        @pl.when(i == j)
        def _():
            add(*refs)

    @pl.when(i == 3)
    def _():
        out[...] = acc[...].astype(BF16)


def expert_grads(dims, peer, own, act_a, dup_a, ddn_a, act_b, dup_b, ddn_b, ce, ca, cu, cd):
    model = own.shape[-1]
    hidden = act_a.shape[-1]
    slab, quarter = dims.slab, dims.quarter
    assert hidden == model
    half = pl.BlockSpec((quarter, slab, model), lambda i: (jnp.where(i < 2, 1, 0), 0, 0))
    first = pl.BlockSpec((quarter, slab, hidden), lambda i: (jnp.minimum(i, 1), 0, 0))
    last = pl.BlockSpec((quarter, slab, hidden), lambda i: (jnp.maximum(i - 2, 0), 0, 0))
    return pl.pallas_call(
        functools.partial(expert_grads_kernel, dims),
        grid=(4,),
        in_specs=[half, half, first, first, first, last, last, last] + [spec_whole(v) for v in (ce, ca, cu, cd)],
        out_specs=pl.BlockSpec((4, model, hidden), lambda i: (0, 0, 0)),
        scratch_shapes=[pltpu.VMEM((4, model, hidden), F32)],
        out_shape=jax.ShapeDtypeStruct((4, model, hidden), BF16),
        compiler_params=params(),
        cost_estimate=pl.CostEstimate(
            flops=16 * quarter * slab * model * hidden, bytes_accessed=40_000_000, transcendentals=0),
        name="expert_grads",
    )(peer, own, act_a, dup_a, ddn_a, act_b, dup_b, ddn_b, ce, ca, cu, cd)


def own_row(dims, r, p):
    return 8 * (r // 2) + dims.quarter * (r % 2) + p


def class_forward_kernel(dims, near, far, up, up_bias, down, out, rows):
    for m in range(2):
        e = jnp.concatenate([near[2 + m], far[2 + m]], axis=0).astype(BF16)
        rows[m] = e
        u = dot(e, up[m]) + up_bias[m:m + 1]
        out[m] = dot(gelu_low(u), down[m])


def class_forward(dims, near, far, up, up_bias, down):
    shape = (2, 16, near.shape[-1])
    return pl.pallas_call(
        functools.partial(class_forward_kernel, dims),
        out_shape=[jax.ShapeDtypeStruct(shape, F32), jax.ShapeDtypeStruct(shape, BF16)],
        compiler_params=params(),
        cost_estimate=pl.CostEstimate(flops=200_000_000, bytes_accessed=5_000_000, transcendentals=0),
        name="class_forward",
    )(near, far, up, up_bias, down)


def class_final_kernel(dims, order, near, far, d0, d1, d2, d3, vec, out):
    q = dims.quarter
    for m in range(2):
        out[m] = jnp.zeros(out.shape[1:], F32)
        for r in range(4):
            half, at = (near, far)[r // 2], q * (r % 2)
            for p in range(q):
                rows = [d[m, own_row(dims, s, p):own_row(dims, s, p) + 1, :]
                        for d, s in ((d0, r), (d1, r ^ 2), (d2, r ^ 1), (d3, r ^ 3))]
                total = (rows[0] + rows[1]) + (rows[2] + rows[3])
                x = half[m, at + p:at + p + 1, :] + vector(vec, F_SCALE) * (total + vector(vec, F_BIAS + m))
                out[m, pl.ds(4 * order[r] + p, 1), :] = x


def class_final(dims, order, near, far, parts, vec):
    shape = (2, 16, near.shape[-1])
    args = (near, far) + tuple(parts) + (vec,)
    return pl.pallas_call(
        functools.partial(class_final_kernel, dims),
        grid_spec=pltpu.PrefetchScalarGridSpec(
            num_scalar_prefetch=1, grid=(1,),
            in_specs=[spec_whole(v) for v in args],
            out_specs=pl.BlockSpec(shape, lambda i, o: (0, 0, 0)),
        ),
        out_shape=jax.ShapeDtypeStruct(shape, F32),
        compiler_params=params(),
        cost_estimate=pl.CostEstimate(flops=1_000_000, bytes_accessed=1_000_000, transcendentals=0),
        name="class_final",
    )(order, *args)


def class_back_kernel(dims, order, e, cot_a, cot_b, dclass, vec, up, up_bias, down,
                      act, dup, ddown, dexp, bias_grad, dcls, rows):
    q = dims.quarter
    rows[...] = jnp.zeros_like(rows)
    dcls[...] = jnp.zeros_like(dcls)
    for m in range(2):
        for r in range(4):
            cot, base = (cot_b, cot_a)[r % 2], 8 * (1 - r // 2)
            for p in range(q):
                d = dclass[m, pl.ds(4 * order[r] + p, 1), :]
                at = own_row(dims, r, p)
                rows[m, at:at + 1, :] = cot[m, base + p:base + p + 1, :] + d
                if r == 0:
                    dcls[p, m:m + 1, :] = d
        u = dot(e[m], up[m]) + up_bias[m:m + 1]
        big, small = gelu_parts(u)
        act[m] = (u * big).astype(BF16)
        g = (rows[m] * vector(vec, F_SCALE)).astype(BF16)
        ddown[m] = g
        du = dot_t(g, down[m]) * (big + u * small)
        bias_grad[m:m + 1, :] = jnp.sum(du, axis=0, keepdims=True)
        low = du.astype(BF16)
        dup[m] = low
        dexp[m] = dot_t(low, up[m])


def class_back(dims, order, e, cot_a, cot_b, dclass, vec, up, up_bias, down):
    hidden, model = up.shape[-1], e.shape[-1]
    args = (e, cot_a, cot_b, dclass, vec, up, up_bias, down)
    shapes = [((2, 16, hidden), BF16), ((2, 16, hidden), BF16), ((2, 16, model), BF16), ((2, 16, model), F32),
              ((2, hidden), F32), ((dims.quarter, 8, model), F32)]
    return pl.pallas_call(
        functools.partial(class_back_kernel, dims),
        grid_spec=pltpu.PrefetchScalarGridSpec(
            num_scalar_prefetch=1, grid=(1,),
            in_specs=[spec_whole(v) for v in args],
            out_specs=[pl.BlockSpec(s, lambda i, o, n=len(s): (0,) * n) for s, _ in shapes],
            scratch_shapes=[pltpu.VMEM((2, 16, model), F32)],
        ),
        out_shape=[jax.ShapeDtypeStruct(s, t) for s, t in shapes],
        compiler_params=params(),
        cost_estimate=pl.CostEstimate(flops=300_000_000, bytes_accessed=5_000_000, transcendentals=0),
        name="class_back",
    )(order, *args)


def contrast_kernel(dims, total, at, blocks, vec, weight, scale,
                    head_in, dproj, dcls, gains, shifts, scalars, cls, back):
    me = at[0]
    span = blocks[0].shape[0]
    for k, block in enumerate(blocks):
        for j in range(span):
            for m in range(2):
                cls[m, pl.ds(pl.multiple_of(16 * (me ^ (k * span + j)), 16), 16), :] = block[j, m]
    n_rows = cls.shape[1]
    sharp = jnp.exp(scale[...])
    col_at = lax.broadcasted_iota(jnp.int32, (1, n_rows), 1)
    row_at = lax.broadcasted_iota(jnp.int32, (n_rows, 1), 0)
    col_ok = (col_at % 4) < dims.quarter
    row_ok = (row_at % 4) < dims.quarter
    normal, inverse, proj, unit, embed = [], [], [], [], []
    for m in range(2):
        n, r = normalise(cls[m])
        h = (n * vector(vec, H_GAIN + m) + vector(vec, H_SHIFT + m)).astype(BF16)
        head_in[m] = h
        y = dot(h, weight[m])
        u = lax.rsqrt(jnp.sum(y * y, axis=-1, keepdims=True) + 1e-6)
        normal.append(n)
        inverse.append(r)
        proj.append(y)
        unit.append(u)
        embed.append((y * u).astype(BF16))
    ok = row_ok & col_ok
    logits = sharp * dot_t(embed[0], embed[1])
    masked = jnp.where(ok, logits, -1e30)
    row_max = jnp.max(masked, axis=1, keepdims=True)
    row_lse = row_max + jnp.log(jnp.sum(jnp.exp(masked - row_max), axis=1, keepdims=True))
    col_max = jnp.max(masked, axis=0, keepdims=True)
    col_lse = col_max + jnp.log(jnp.sum(jnp.exp(masked - col_max), axis=0, keepdims=True))
    same = (row_at == col_at) & ok
    both = jnp.exp(masked - row_lse) + jnp.exp(masked - col_lse)
    dlogits = jnp.where(ok, jnp.where(same, both - 2.0, both) * (1.0 / (2 * total)), 0.0)
    diagonal = jnp.sum(jnp.where(same, logits, 0.0), axis=1, keepdims=True)
    rows = jnp.where(row_ok, row_lse - 2.0 * diagonal, 0.0)
    cols = jnp.where(col_ok, col_lse, 0.0)
    loss = (jnp.sum(rows, axis=0, keepdims=True) + jnp.sum(cols, axis=1, keepdims=True)) * (1.0 / (2 * total))
    slope = jnp.sum(jnp.sum(dlogits * logits, axis=1, keepdims=True), axis=0, keepdims=True)
    scalars[0:1, :] = jnp.broadcast_to(loss, (1, 128))
    scalars[1:2, :] = jnp.broadcast_to(slope, (1, 128))
    high = lax.Precision.HIGHEST
    wide = [e.astype(F32) for e in embed]
    dembed = [
        sharp * jnp.dot(dlogits, wide[1], precision=high, preferred_element_type=F32),
        sharp * lax.dot_general(dlogits, wide[0], (((0,), (0,)), ((), ())), precision=high,
                                preferred_element_type=F32),
    ]
    for m in range(2):
        u, y, d = unit[m], proj[m], dembed[m]
        dp = (u * d - u * u * u * y * jnp.sum(y * d, axis=-1, keepdims=True)).astype(BF16)
        dproj[m] = dp
        dh = dot_t(dp, weight[m])
        gains[m:m + 1, :] = jnp.sum(dh * normal[m], axis=0, keepdims=True)
        shifts[m:m + 1, :] = jnp.sum(dh, axis=0, keepdims=True)
        back[m] = norm_back(normal[m], inverse[m], dh * vector(vec, H_GAIN + m))
        dcls[m] = back[m, pl.ds(pl.multiple_of(16 * me, 16), 16), :]


def contrast(dims, total, at, blocks, vec, weight, scale):
    model = weight.shape[1]
    rows = 16 * len(blocks) * blocks[0].shape[0]
    args = tuple(blocks) + (vec, weight, scale)
    shapes = [((2, rows, model), BF16), ((2, rows, weight.shape[2]), BF16), ((2, 16, model), F32),
              ((2, model), F32), ((2, model), F32), ((2, 128), F32)]

    def kernel(at, *refs):
        contrast_kernel(dims, total, at, refs[:len(blocks)], *refs[len(blocks):])

    return pl.pallas_call(
        kernel,
        grid_spec=pltpu.PrefetchScalarGridSpec(
            num_scalar_prefetch=1, grid=(1,),
            in_specs=[spec_whole(v) for v in args],
            out_specs=[pl.BlockSpec(s, lambda i, o, n=len(s): (0,) * n) for s, _ in shapes],
            scratch_shapes=[pltpu.VMEM((2, rows, model), F32)] * 2,
        ),
        out_shape=[jax.ShapeDtypeStruct(s, t) for s, t in shapes],
        compiler_params=params(),
        cost_estimate=pl.CostEstimate(flops=1_000_000_000, bytes_accessed=5_000_000, transcendentals=0),
        name="contrast",
    )(at, *args)


def contrast_large(dims, total, at, blocks, vec, weight, scale):
    model = weight.shape[1]
    held = jnp.concatenate(blocks)
    held = held[jnp.arange(held.shape[0]) ^ at[0]]
    rows = jnp.asarray([r for r in range(16) if r % 4 < dims.quarter])
    cls = jnp.transpose(held[:, :, rows], (1, 0, 2, 3)).reshape(2, -1, model)
    gain, shift = vec[H_GAIN:H_GAIN + 2, None], vec[H_SHIFT:H_SHIFT + 2, None]
    n, r = normalise(cls)
    head_in = (n * gain + shift).astype(BF16)
    proj = jnp.einsum("mrc,mce->mre", head_in, weight, preferred_element_type=F32)
    unit = lax.rsqrt(jnp.sum(proj * proj, axis=-1, keepdims=True) + 1e-6)
    embed = (proj * unit).astype(BF16)
    sharp = jnp.exp(scale[0, 0])
    logits = sharp * dot_t(embed[0], embed[1])
    row_lse = jax.nn.logsumexp(logits, axis=1, keepdims=True)
    col_lse = jax.nn.logsumexp(logits, axis=0, keepdims=True)
    dlogits = jnp.exp(logits - row_lse) + jnp.exp(logits - col_lse) - 2.0 * jnp.eye(total, dtype=F32)
    dlogits = dlogits / (2 * total)
    loss = (jnp.sum(row_lse) + jnp.sum(col_lse) - 2.0 * jnp.trace(logits)) / (2 * total)
    slope = jnp.sum(dlogits * logits)
    high = lax.Precision.HIGHEST
    wide = embed.astype(F32)
    dembed = sharp * jnp.stack([
        jnp.dot(dlogits, wide[1], precision=high, preferred_element_type=F32),
        jnp.dot(dlogits.T, wide[0], precision=high, preferred_element_type=F32)])
    dproj = (unit * dembed - unit ** 3 * proj * jnp.sum(proj * dembed, axis=-1, keepdims=True)).astype(BF16)
    dh = jnp.einsum("mre,mce->mrc", dproj, weight, preferred_element_type=F32)
    back = norm_back(n, r, dh * gain)
    pairs = 4 * dims.quarter
    own = lax.dynamic_slice_in_dim(back, at[0] * pairs, pairs, axis=1)
    dcls = jnp.zeros((2, 16, model), F32).at[:, rows].set(own)
    scalars = jnp.broadcast_to(jnp.stack([loss, slope])[:, None], (2, 128))
    return head_in, dproj, dcls, jnp.sum(dh * n, axis=1), jnp.sum(dh, axis=1), scalars


def own_pair(rows_of):
    return lambda i, o: (o[0] * rows_of + i, 0, 0)


def own_call(kernel, dims, name, order, blocks, img, txt, others, outs, scratch):
    model = img.shape[-1]
    block = pl.BlockSpec((1, dims.slab, model), lambda i, o: (i, 0, 0))
    specs = {
        "slab": (block, (dims.quarter, dims.slab, model)),
        "img": (pl.BlockSpec((1, dims.patches, model), lambda i, o: (i, 0, 0)), (dims.quarter, dims.patches, model)),
        "txt": (pl.BlockSpec((1, dims.caption, model), lambda i, o: (i, 0, 0)), (dims.quarter, dims.caption, model)),
        "sums": (pl.BlockSpec((8, model), lambda i, o: (0, 0)), (8, model)),
    }
    return pl.pallas_call(
        functools.partial(kernel, dims),
        grid_spec=pltpu.PrefetchScalarGridSpec(
            num_scalar_prefetch=1,
            grid=(dims.quarter,),
            in_specs=[block] * len(blocks) + [
                pl.BlockSpec((1, dims.patches, model), own_pair(dims.quarter)),
                pl.BlockSpec((1, dims.caption, model), own_pair(dims.quarter)),
            ] + [spec_whole(v) for v in others],
            out_specs=[specs[kind][0] for kind, _ in outs],
            scratch_shapes=[pltpu.VMEM((dims.slab, model), F32)] * scratch,
        ),
        out_shape=[jax.ShapeDtypeStruct(specs[kind][1], dtype) for kind, dtype in outs],
        compiler_params=params(),
        cost_estimate=pl.CostEstimate(flops=40_000_000, bytes_accessed=15_000_000, transcendentals=0),
        name=name,
    )(order, *blocks, img, txt, *others)


def start_own(rows, sums):
    @pl.when(pl.program_id(0) == 0)
    def _():
        rows[...] = jnp.zeros_like(rows)
        sums[...] = jnp.zeros_like(sums)


def add_class(dims, dcls, rows):
    i = pl.program_id(0)
    rows[0:1, :] += dcls[i, 0:1, :]
    rows[dims.ip:dims.ip + 1, :] += dcls[i, 1:2, :]


def final_kernel(dims, order, keep, recv, far, attended, img, txt, dcls, vec, fin_img, fin_txt, sums, rows):
    start_own(rows, sums)
    load_rows(dims, 0, img, txt, rows)
    add_class(dims, dcls, rows)
    for m, lo, hi in ((0, 0, dims.ip), (1, dims.ip, dims.slab)):
        b = keep[0, lo:hi].astype(F32) + recv[0, lo:hi].astype(F32) + far[0, lo:hi].astype(F32)
        b = b + vector(vec, F_BIAS + m)
        f = attended[0, lo:hi, :] + vector(vec, F_SCALE) * b
        if m == 0:
            fin_img[0] = f[0:dims.patches].astype(BF16)
        else:
            fin_txt[0] = f[0:dims.caption].astype(BF16)
        g = rows[lo:hi, :]
        sums[0:1, :] += jnp.sum(g * b, axis=0, keepdims=True)
        sums[1 + m:2 + m, :] += jnp.sum(g, axis=0, keepdims=True) * vector(vec, F_SCALE)


def final_rows(dims, order, keep, recv, far, attended, img, txt, dcls, vec):
    return own_call(final_kernel, dims, "final_rows", order, (keep, recv, far, attended), img, txt,
                    (dcls, vec), (("img", BF16), ("txt", BF16), ("sums", F32)), 1)


def norm_two_kernel(dims, order, keep, recv, far, attended, a_keep, a_recv, img, txt, dcls, x0, x1, x2, x3,
                    vec, dattended, dattn, sums, rows, ups):
    i = pl.program_id(0)
    start_own(rows, sums)
    load_rows(dims, 0, img, txt, rows)
    add_class(dims, dcls, rows)
    ups[...] = keep[0].astype(F32) + recv[0].astype(F32) + far[0].astype(F32)
    for m, at in ((0, 0), (1, dims.ip)):
        extra = [x[m, pl.ds(own_row(dims, r, 0) + i, 1), :] for x, r in ((x0, 0), (x1, 2), (x2, 1), (x3, 3))]
        ups[at:at + 1, :] += (extra[0] + extra[1]) + (extra[2] + extra[3])
    for m, lo, hi in ((0, 0, dims.ip), (1, dims.ip, dims.slab)):
        n, r = normalise(attended[0, lo:hi, :])
        dy = ups[lo:hi, :]
        sums[m:m + 1, :] += jnp.sum(dy * n, axis=0, keepdims=True)
        sums[2 + m:3 + m, :] += jnp.sum(dy, axis=0, keepdims=True)
        d = rows[lo:hi, :] + norm_back(n, r, dy * vector(vec, GAIN2 + m))
        dattended[0, lo:hi, :] = d
        sd = d * vector(vec, A_SCALE)
        dattn[0, lo:hi, :] = sd.astype(BF16)
        a = a_keep[0, lo:hi, :].astype(F32) + a_recv[0, lo:hi, :].astype(F32) + vector(vec, A_BIAS)
        sums[4:5, :] += jnp.sum(d * a, axis=0, keepdims=True)
        sums[5:6, :] += jnp.sum(sd, axis=0, keepdims=True)


def norm_two(dims, order, keep, recv, far, attended, a_keep, a_recv, img, txt, dcls, parts, vec):
    return own_call(norm_two_kernel, dims, "norm_two", order, (keep, recv, far, attended, a_keep, a_recv), img, txt,
                    (dcls,) + tuple(parts) + (vec,), (("slab", F32), ("slab", BF16), ("sums", F32)), 2)


def norm_one_kernel(dims, order, keep, recv, dattended, img, txt, vec, d_img, d_txt, sums, rows):
    start_own(rows, sums)
    load_rows(dims, 0, img, txt, rows)
    n, r = normalise(rows[...])
    dy = keep[0].astype(F32) + recv[0].astype(F32)
    sums[0:1, :] += jnp.sum(dy * n, axis=0, keepdims=True)
    sums[1:2, :] += jnp.sum(dy, axis=0, keepdims=True)
    d = dattended[0] + norm_back(n, r, dy * vector(vec, GAIN1))
    d_img[0] = d[0:dims.patches].astype(BF16)
    d_txt[0] = d[dims.ip:dims.ip + dims.caption].astype(BF16)


def norm_one(dims, order, keep, recv, dattended, img, txt, vec):
    return own_call(norm_one_kernel, dims, "norm_one", order, (keep, recv, dattended), img, txt,
                    (vec,), (("img", BF16), ("txt", BF16), ("sums", F32)), 1)


def attend_back_kernel(dims, far, order, lens, d_own, d_peer, normed, qkv, mixed, wo, wf, *refs):
    if far:
        keep, send, grad, grad_rest, col_sums, dattn, dmixed, dqkv, acc, w, ow = refs
    else:
        prior_keep, prior_send, keep, send, grad, col_sums, dattn, dmixed, dqkv, acc, w, ow = refs
    i = pl.program_id(0)
    slab, quarter, local = dims.slab, dims.quarter, dims.local
    two, one_head = parts_of(dims)
    tiles = 2 if far else 1
    width = tiles * two
    count = quarter * slab
    model = normed.shape[-1]

    @pl.when(i == 0)
    def _():
        dattn[...] = d_own[...]
        acc[...] = jnp.zeros_like(acc)
        col_sums[...] = jnp.zeros_like(col_sums)
        for t in range(4):
            dst, at = (w, t * width) if t < 3 else (ow, 0)
            if far:
                copy_rows(dst, at, wf, t * local, two)
                copy_rows(dst, at + two, wo, t * local + two, one_head)
                copy_rows(dst, at + two + one_head, wf, t * local + two, one_head)
            else:
                copy_rows(dst, at, wo, t * local, two)

    @pl.when(i == 1)
    def _():
        dattn[...] = d_peer[...]

    d_rows = dattn[...].reshape(count, model)
    dmixed[...] = dot_t(d_rows, ow[...]).astype(BF16).reshape(quarter, slab, width)

    def one_pair(p, c):
        length = lens[order[2 * i] * quarter + p]
        for lo, hi, start, limit in key_tail(dims, length):
            for g in range(tiles):
                at = [slice((t * tiles + g) * 128, (t * tiles + g + 1) * 128) for t in range(3)]
                q, k, v = [qkv[p, lo:hi, c] for c in at]
                q = scaled(q)
                qq = split_pair(q)
                dd = split_pair(dmixed[p, lo:hi, g * 128:(g + 1) * 128])
                w_ = softmax_keys(hide(dot_t(k, qq), start, limit))
                dw = dot_t(v, dd)
                dqkv[p, lo:hi, at[2]] = dot(w_.astype(BF16), dd).astype(BF16)
                ds = (w_ * (dw - jnp.sum(w_ * dw, axis=0, keepdims=True))).astype(BF16)
                dqkv[p, lo:hi, at[1]] = dot(ds, qq).astype(BF16)
                dqkv[p, lo:hi, at[0]] = (join_pair(t_dot(ds, k)) * HEAD_DIM ** -0.5).astype(BF16)
        return c

    lax.fori_loop(0, quarter, one_pair, 0)
    dp = dqkv[...].reshape(count, 3 * width)
    part = dot(dp, w[...])
    acc[:, 0:3 * width] += t_dot(normed[...].reshape(count, model), dp)
    acc[:, 3 * width:] += t_dot(d_rows, mixed[...].reshape(count, width))
    col_sums[...] += jnp.sum(dp.astype(F32), axis=0, keepdims=True)

    @pl.when(i == 0)
    def _():
        prior = 0.0 if far else prior_keep[...].reshape(count, model).astype(F32)
        keep[...] = (part + prior).astype(BF16).reshape(quarter, slab, model)

    @pl.when(i == 1)
    def _():
        prior = 0.0 if far else prior_send[...].reshape(count, model).astype(F32)
        send[...] = (part + prior).astype(BF16).reshape(quarter, slab, model)
        for t in range(4):
            grad[:, t * two:(t + 1) * two] = acc[:, t * width:t * width + two].astype(BF16)
            if far:
                at = t * width + two
                to = 4 * two + t * one_head
                grad[:, to:to + one_head] = acc[:, at + one_head:at + two].astype(BF16)
                grad_rest[:, t * one_head:(t + 1) * one_head] = acc[:, at:at + one_head].astype(BF16)


def attend_back(dims, far, order, lens, d_own, d_peer, normed, qkv, mixed, wo, wf, prior=()):
    model = normed.shape[-1]
    slab, quarter = dims.slab, dims.quarter
    width = 256 if far else 128
    one = pl.BlockSpec((quarter, slab, model), lambda i, o, n: (0, 0, 0))
    step = lambda cols: pl.BlockSpec((quarter, slab, cols), lambda i, o, n: (2 * i, 0, 0))
    grads = (768, 256) if far else (512,)
    return pl.pallas_call(
        functools.partial(attend_back_kernel, dims, far),
        grid_spec=pltpu.PrefetchScalarGridSpec(
            num_scalar_prefetch=2,
            grid=(2,),
            in_specs=[one, one, step(model), step(3 * width), step(width), spec_whole(wo), spec_whole(wf)]
            + [one] * len(prior),
            out_specs=[one, one] + [pl.BlockSpec((model, n), lambda i, o, n: (0, 0)) for n in grads]
            + [pl.BlockSpec((1, 3 * width), lambda i, o, n: (0, 0))],
            scratch_shapes=[
                pltpu.VMEM((quarter, slab, model), BF16),
                pltpu.VMEM((quarter, slab, width), BF16),
                pltpu.VMEM((quarter, slab, 3 * width), BF16),
                pltpu.VMEM((model, 4 * width), F32),
                pltpu.VMEM((3 * width, model), BF16),
                pltpu.VMEM((width, model), BF16),
            ],
        ),
        out_shape=[
            jax.ShapeDtypeStruct((quarter, slab, model), BF16),
            jax.ShapeDtypeStruct((quarter, slab, model), BF16),
        ] + [jax.ShapeDtypeStruct((model, n), BF16) for n in grads] + [jax.ShapeDtypeStruct((1, 3 * width), F32)],
        compiler_params=params(),
        cost_estimate=pl.CostEstimate(
            flops=32 * quarter * slab * model * width, bytes_accessed=20_000_000, transcendentals=0),
        name="attend_back_far" if far else "attend_back_own",
    )(order, lens, d_own, d_peer, normed, qkv, mixed, wo, wf, *prior)


def swap(value, axis, bit):
    size = lax.axis_size(axis)
    return lax.ppermute(value, axis, [(j, j ^ bit) for j in range(size)])


def to_core(value):
    return swap(value, "mp", 1)


def to_y(value):
    return swap(value, "mp", 2)


def from_others(value, axis, first, count):
    return [value] + [swap(value, axis, k * first) for k in range(1, count)]


def add_tree(parts):
    while len(parts) > 1:
        parts = [a + b for a, b in zip(parts[::2], parts[1::2])]
    return parts[0]


def sum_over(value, axis):
    first = 1
    while first < lax.axis_size(axis):
        count = min(8, lax.axis_size(axis) // first)
        value = add_tree(from_others(value, axis, first, count))
        first *= count
    return value


def gather_batch(value):
    parts = [value]
    first = 1
    size = lax.axis_size("batch")
    while first < size:
        count = min(8, size // first)
        whole = jnp.concatenate(parts) if len(parts) > 1 else parts[0]
        parts = from_others(whole, "batch", first, count)
        first *= count
    return parts


def gather_rows(own, me):
    near = jnp.stack([own, to_y(own)])
    far = to_core(near)
    out = jnp.zeros((4,) + own.shape, own.dtype)
    for r, value in enumerate((near[0], near[1], far[0], far[1])):
        out = lax.dynamic_update_slice(out, value[None], (me ^ ORDER[r],) + (0,) * own.ndim)
    return out.reshape((4 * own.shape[0],) + own.shape[1:])


def add_low(a, b):
    return (a.astype(F32) + b.astype(F32)).astype(BF16)


MESH = pl.DeviceIdType.MESH
V_ROWS = 16
V_MP, V_HEADS = 11, 13


def finish_kernel(dims, n_keep, n_send, dattended, states_img, states_txt, vec, fin_img, fin_txt, near_img, near_txt,
                  grad_pair, grad_single, grad_far, v_in, v_far, out_img, out_txt, back_img, back_txt, grad_out, v_out,
                  n_recv, s_img, s_txt, d_img, d_txt, rows, xs, xr, zs, zr, vs, vr, local_sem, send_sem, recv_sem):
    quarter = dims.quarter
    b, m = lax.axis_index("batch"), lax.axis_index("mp")
    z, x = b // 2, b % 2
    y, c = m // 2, m % 2
    core = (b, 2 * y + 1 - c)
    near = (b, 2 * (1 - y) + c)
    side = (2 * z + 1 - x, m)
    along = [(2 * ((z + k) % 4) + x, m) for k in range(1, 4)]
    peers = [core, near, side] + along
    near_quarter = 2 * (1 - y) + c
    used = [0]

    def remote(src, dst, device):
        at = used[0]
        used[0] += 1
        return pltpu.make_async_remote_copy(
            src_ref=src, dst_ref=dst, send_sem=send_sem.at[at], recv_sem=recv_sem.at[at],
            device_id=device, device_id_type=MESH)

    loaded = [pltpu.make_async_copy(states_img.at[pl.ds(m * quarter, quarter)], s_img, local_sem.at[0]),
              pltpu.make_async_copy(states_txt.at[pl.ds(m * quarter, quarter)], s_txt, local_sem.at[1])]
    for copy in loaded:
        copy.start()
    barrier = pltpu.get_barrier_semaphore()
    for peer in peers:
        pl.semaphore_signal(barrier, inc=1, device_id=peer, device_id_type=MESH)
    pl.semaphore_wait(barrier, len(peers))

    n_copies = [remote(n_send.at[p], n_recv.at[p], core) for p in range(quarter)]
    for copy in n_copies:
        copy.start()
    piece = xs.shape[1]
    pairs_wide = grad_pair.shape[1]

    def both(block, cols):
        at = pl.multiple_of(block * piece, piece)
        lo, hi = cols
        own = grad_pair[pl.ds(at, piece), :] if lo == 0 else grad_single[pl.ds(at, piece), :]
        return own.astype(F32) + grad_far[pl.ds(at, piece), lo:hi].astype(F32)

    spans = ((0, pairs_wide), (pairs_wide, grad_far.shape[1]))
    x_copies = []
    for j in range(4):
        for cols in spans:
            xs[j, :, cols[0]:cols[1]] = both(2 * j + 1 - x, cols).astype(BF16)
        x_copies.append(remote(xs.at[j], xr.at[j], side))
        x_copies[-1].start()

    whole = lambda q: pl.ds(q * quarter, quarter)
    fin_local, fin_remote = [], []
    for j, (src, dst, q) in enumerate((
        (fin_img, out_img, m), (fin_txt, out_txt, m),
        (near_img, out_img, near_quarter), (near_txt, out_txt, near_quarter),
    )):
        fin_local.append(pltpu.make_async_copy(src, dst.at[whole(q)], local_sem.at[2 + j]))
        fin_remote.append(remote(src, dst.at[whole(q)], core))

    rows[...] = jnp.zeros_like(rows)
    for copy in loaded:
        copy.wait()
    total = [jnp.zeros((1, rows.shape[1]), F32)] * 2
    back_local, to_near, to_core_ = [], [], []
    for p in range(quarter):
        load_rows(dims, p, s_img, s_txt, rows)
        n, r = normalise(rows[...])
        n_copies[p].wait_recv()
        dy = n_keep[p].astype(F32) + n_recv[p].astype(F32)
        total[0] = total[0] + jnp.sum(dy * n, axis=0, keepdims=True)
        total[1] = total[1] + jnp.sum(dy, axis=0, keepdims=True)
        d = dattended[p] + norm_back(n, r, dy * vector(vec, GAIN1))
        d_img[p] = d[0:dims.patches].astype(BF16)
        d_txt[p] = d[dims.ip:dims.ip + dims.caption].astype(BF16)
        for j, (src, dst) in enumerate(((d_img, back_img), (d_txt, back_txt))):
            at = dst.at[m * quarter + p]
            to_near.append(remote(src.at[p], at, near))
            to_near[-1].start()
            to_core_.append(remote(src.at[p], at, core))
            to_core_[-1].start()
            back_local.append(pltpu.make_async_copy(src.at[p], at, local_sem.at[6 + 2 * p + j]))
            back_local[-1].start()
    for copy in fin_local + fin_remote:
        copy.start()

    z_copies = []
    for j in range(4):
        x_copies[j].wait_recv()
        for cols in spans:
            zs[j, :, cols[0]:cols[1]] = (
                both(2 * j + x, cols) + xr[j, :, cols[0]:cols[1]].astype(F32)).astype(BF16)
    for k in range(1, 4):
        z_copies.append(remote(zs.at[(z + k) % 4], zr.at[k - 1], along[k - 1]))
        z_copies[-1].start()

    at = lax.broadcasted_iota(jnp.int32, (V_ROWS, 1), 0)
    v = v_in[...]
    v = jnp.where(at == 0, total[0], jnp.where(at == 1, total[1], v))
    v_copies = []

    def exchange(step, value, device):
        vs[step] = value
        copy = remote(vs.at[step], vr.at[step], device)
        copy.start()
        copy.wait_recv()
        v_copies.append(copy)
        return vr[step]

    v = v + jnp.where(at < V_MP, exchange(0, v, core), 0.0)
    v = v + jnp.where((at < V_MP) | (at >= V_HEADS), exchange(1, jnp.where(at >= V_HEADS, v_far[...], v), near), 0.0)
    v = v + exchange(2, v, side)
    vs[3] = v
    vr[3 + z] = v
    around = [remote(vs.at[3], vr.at[3 + z], along[k - 1]) for k in range(1, 4)]
    for copy in around:
        copy.start()
    for copy in around:
        copy.wait_recv()
    v_out[...] = (vr[3] + vr[4]) + (vr[5] + vr[6])
    for copy in z_copies:
        copy.wait_recv()
    for cols in spans:
        lo, hi = cols
        g = both(2 * z + x, cols) + xr[z, :, lo:hi].astype(F32)
        for k in range(3):
            g = g + zr[k, :, lo:hi].astype(F32)
        grad_out[:, lo:hi] = g

    onward = []
    for p in range(quarter):
        for j, dst in enumerate((back_img, back_txt)):
            to_near[2 * p + j].wait_recv()
            at_near = dst.at[near_quarter * quarter + p]
            onward.append(remote(at_near, at_near, core))
            onward[-1].start()
    for copy in fin_local + back_local:
        copy.wait()
    for copy in to_core_ + fin_remote + onward:
        copy.wait()
    for copy in n_copies + x_copies + to_near + z_copies + v_copies + around:
        copy.wait_send()


def finish(dims, n_keep, n_send, dattended, states_img, states_txt, vec, fin_img, fin_txt, near_img, near_txt,
           grad_pair, grad_single, grad_far, v_in, v_far):
    pairs, patches, model = states_img.shape
    caption = states_txt.shape[1]
    quarter, slab = dims.quarter, dims.slab
    piece = model // 8
    held = pl.BlockSpec(memory_space=pltpu.VMEM)
    away = pl.BlockSpec(memory_space=pl.ANY)
    n_remote = 7 * quarter + 18
    return pl.pallas_call(
        functools.partial(finish_kernel, dims),
        in_specs=[held] * 3 + [away] * 2 + [held] * 10,
        out_specs=[away] * 4 + [held] * 2,
        out_shape=[
            jax.ShapeDtypeStruct((pairs, patches, model), BF16),
            jax.ShapeDtypeStruct((pairs, caption, model), BF16),
            jax.ShapeDtypeStruct((pairs, patches, model), BF16),
            jax.ShapeDtypeStruct((pairs, caption, model), BF16),
            jax.ShapeDtypeStruct((piece, grad_far.shape[1]), F32),
            jax.ShapeDtypeStruct((V_ROWS, model), F32),
        ],
        scratch_shapes=[
            pltpu.VMEM((quarter, slab, model), BF16),
            pltpu.VMEM((quarter, patches, model), BF16),
            pltpu.VMEM((quarter, caption, model), BF16),
            pltpu.VMEM((quarter, patches, model), BF16),
            pltpu.VMEM((quarter, caption, model), BF16),
            pltpu.VMEM((slab, model), F32),
        ] + [pltpu.VMEM((4, piece, grad_far.shape[1]), BF16)] * 4 + [
            pltpu.VMEM((4, V_ROWS, model), F32),
            pltpu.VMEM((7, V_ROWS, model), F32),
            pltpu.SemaphoreType.DMA((6 + 2 * quarter,)),
            pltpu.SemaphoreType.DMA((n_remote,)),
            pltpu.SemaphoreType.DMA((n_remote,)),
        ],
        compiler_params=params(collective_id=1, has_side_effects=True),
        name="finish",
    )(n_keep, n_send, dattended, states_img, states_txt, vec, fin_img, fin_txt, near_img, near_txt,
      grad_pair, grad_single, grad_far, v_in, v_far)


def per_device(
    image_states, text_states, caption_lengths, image_cotangent, text_cotangent,
    first_gain, first_shift, query_key_value, query_value_bias, output_weight, output_bias,
    attention_scale, expert_gain, expert_shift, expert_up, expert_up_bias, expert_down,
    expert_down_bias, feedforward_scale, head_gain, head_shift, head_weight, logit_scale,
):
    pairs, patches, model = image_states.shape
    caption = text_states.shape[1]
    local = query_key_value.shape[2]
    quarter = pairs // 4
    batch_size = lax.axis_size("batch")
    assert lax.axis_size("mp") == 4 and pairs == 4 * quarter and quarter <= 3
    assert batch_size & (batch_size - 1) == 0
    assert local == 3 * HEAD_DIM
    ip, tp = up16(patches), up16(caption)
    dims = Dims(patches, caption, ip, tp, ip + tp, quarter, local)
    me = lax.axis_index("mp")
    batch_at = lax.axis_index("batch")
    order = me ^ jnp.asarray(ORDER, jnp.int32)
    vec = jnp.concatenate([
        first_gain[None], first_shift[None], attention_scale[None], output_bias[None], expert_gain, expert_shift,
        feedforward_scale[None], expert_down_bias, head_gain, head_shift, jnp.zeros((1, model), F32)])

    wo = jnp.concatenate([jnp.transpose(query_key_value, (1, 2, 0)).reshape(3 * local, model), output_weight])
    wf = to_y(wo)
    far_bias = to_y(query_value_bias)
    normed, qkv_own, rest, mixed_own = attend_own(
        dims, order, caption_lengths, image_states, text_states, vec, query_value_bias, wo)
    qkv_far, mixed_far, a_keep, a_send = attend_far(
        dims, order, caption_lengths, normed, rest, mixed_own, far_bias, wo, wf)
    a_recv = to_core(a_send)
    attended, e_own, cls_own = residual(
        dims, order, a_keep, a_recv, image_states, text_states, vec)
    e_peer = to_core(e_own)
    cls_peer = to_core(cls_own)
    class_part, class_e = class_forward(dims, cls_own, cls_peer, expert_up, expert_up_bias, expert_down)
    class_parts = from_others(class_part, "mp", 1, 4)

    act_a, dup_a, ddn_a, d_send3, d_keep1, x_send3, x_keep1, bias_a, cot_a = experts(
        dims, "experts_a", 1, order[jnp.asarray([3, 1])], e_peer, e_own, image_cotangent, text_cotangent,
        tie(vec, class_part), expert_up, expert_up_bias, expert_down)
    x_recv1 = to_core(x_send3)
    d_recv1 = to_core(d_send3)
    final_class = class_final(
        dims, order, cls_own, cls_peer, class_parts, tie(vec, bias_a))
    class_blocks = gather_batch(final_class[None])
    x_near = add_low(x_keep1, x_recv1)
    x_far = to_y(x_near)
    act_b, dup_b, ddn_b, d_send2, d_keep0, x_send2, x_keep0, bias_b, cot_b = experts(
        dims, "experts_b", 0, order[jnp.asarray([2, 0])], e_peer, e_own, image_cotangent, text_cotangent,
        tie(vec, final_class, x_near), expert_up, expert_up_bias, expert_down)
    x_recv0 = to_core(x_send2)
    d_recv0 = to_core(d_send2)

    head_in, dproj, dclass, grad_head_gain, grad_head_shift, scalars = (contrast if batch_size <= 8 else contrast_large)(
        dims, pairs * batch_size, batch_at.reshape(1), class_blocks, tie(vec, bias_b), head_weight,
         logit_scale.reshape(1, 1))
    contrast_loss = scalars[0, :1]
    grad_logit_scale = scalars[1, :1]
    c_act, c_dup, c_ddn, c_dexp, c_bias, dcls = class_back(
        dims, order, class_e, cot_a, cot_b, dclass, vec, expert_up, expert_up_bias, expert_down)
    extras = from_others(c_dexp, "mp", 1, 4)
    d_far = to_y(add_low(d_keep1, tie(d_recv1, c_dexp)))
    expert_grad = expert_grads(
        dims, e_peer, e_own, act_a, dup_a, ddn_a, act_b, dup_b, ddn_b, class_e, c_act, c_dup, c_ddn)
    expert_sum = lax.psum_scatter(expert_grad, "batch", scatter_dimension=1, tiled=True)

    dattended, dattn, sums_two = norm_two(
        dims, order, x_keep0, x_recv0, x_far, attended, a_keep, a_recv, image_cotangent, text_cotangent,
        dcls, extras, tie(vec, expert_grad))
    dattn_peer = to_core(dattn)
    fin_img, fin_txt, sums_fin = final_rows(
        dims, order, d_keep0, d_recv0, d_far, attended, image_cotangent, text_cotangent, dcls,
        tie(vec, sums_two))
    n_keep, n_send, grad_far, grad_o2, cols_far = attend_back(
        dims, True, order, caption_lengths, dattn, tie(dattn_peer, sums_fin), normed, qkv_far, mixed_far, wo, wf)
    n_keep, n_send, grad_o01, cols_own = attend_back(
        dims, False, order, caption_lengths, dattn, dattn_peer, normed, qkv_own, mixed_own, wo, wf,
        prior=(n_keep, n_send))
    cols = model // batch_size
    mine = lambda v, axis: lax.dynamic_slice_in_dim(v, batch_at * cols, cols, axis=axis)
    grad_head_weight = jnp.einsum("mnc,mne->mce", mine(head_in, 2), dproj, preferred_element_type=F32)
    grad_expert_up = expert_sum[:2].astype(F32)
    grad_expert_down = jnp.transpose(expert_sum[2:].astype(F32), (0, 2, 1))
    pair, single = 2 * HEAD_DIM, HEAD_DIM
    cols_own = cols_own.reshape(3, pair)[::2]
    cols_far = cols_far.reshape(3, 2 * pair)[::2]
    heads = jnp.concatenate([cols_own, cols_far[:, pair:pair + single]], axis=1)
    heads_far = jnp.concatenate([cols_far[:, :pair], cols_far[:, pair + single:]], axis=1)
    up_sums = bias_a + bias_b + c_bias

    if batch_size == 8 and cols % 32 == 0 and up_sums.shape[1] == model:
        wide = lambda h: jnp.pad(h, ((0, 0), (0, model - local)))
        v_in = jnp.concatenate([
            jnp.zeros((2, model), F32), sums_two[:6], sums_fin[:3], up_sums, wide(heads), jnp.zeros((1, model), F32)])
        v_far = jnp.pad(heads_far, ((V_HEADS, V_ROWS - V_HEADS - 2), (0, model - local)))
        image_output, text_output, image_grad, text_grad, attn_grad, sums = finish(
            dims, n_keep, n_send, dattended, image_states, text_states, vec, fin_img, fin_txt,
            to_y(fin_img), to_y(fin_txt), grad_o01, grad_o2, to_y(grad_far), v_in, v_far)
        grad_expert_up_bias = sums[V_MP:V_MP + 2]
        heads = sums[V_HEADS:V_HEADS + 2, :local]
        own_sums = mine(sums[:V_MP], 1)
    else:
        n_recv = to_core(n_send)
        d_img, d_txt, sums_one = norm_one(
            dims, order, n_keep, n_recv, dattended, image_states, text_states, vec)
        image_output = gather_rows(fin_img, me)
        text_output = gather_rows(fin_txt, me)
        image_grad = gather_rows(d_img, me)
        text_grad = gather_rows(d_txt, me)
        grad_own = jnp.concatenate([grad_o01, grad_o2], axis=1)
        grad_far = lax.psum_scatter(grad_far, "batch", scatter_dimension=0, tiled=True)
        grad_own = lax.psum_scatter(grad_own, "batch", scatter_dimension=0, tiled=True)
        attn_grad = grad_own.astype(F32) + to_y(grad_far).astype(F32)
        heads = heads + to_y(heads_far)
        own_sums = sum_over(jnp.concatenate([sums_one[:2], sums_two[:6], sums_fin[:3]]), "mp")
        flat = jnp.concatenate([own_sums.reshape(-1), heads.reshape(-1), up_sums.reshape(-1)])
        count = flat.shape[0]
        flat = jnp.pad(flat, (0, -count % 1024)).reshape(-1, 128)
        flat = sum_over(flat, "batch").reshape(-1)[:count]
        done = own_sums.shape[0]
        own_sums = mine(flat[:done * model].reshape(done, model), 1)
        heads = flat[done * model:done * model + 2 * local].reshape(2, local)
        grad_expert_up_bias = flat[done * model + 2 * local:].reshape(up_sums.shape)
    attn_grad = jnp.concatenate(
        [attn_grad[:, :4 * pair].reshape(cols, 4, pair), attn_grad[:, 4 * pair:].reshape(cols, 4, single)], axis=2)
    grad_query_key_value = attn_grad[:, :3]
    grad_output_weight = jnp.transpose(attn_grad[:, 3])
    return (
        image_output,
        text_output,
        contrast_loss,
        image_grad,
        text_grad,
        own_sums[0],
        own_sums[1],
        grad_query_key_value,
        heads,
        grad_output_weight,
        own_sums[7],
        own_sums[6],
        own_sums[2:4],
        own_sums[4:6],
        grad_expert_up,
        grad_expert_up_bias,
        grad_expert_down,
        own_sums[9:11],
        own_sums[8],
        mine(grad_head_gain, 1),
        mine(grad_head_shift, 1),
        grad_head_weight,
        grad_logit_scale,
    )


def solution(mesh):
    return jax.shard_map(
        per_device,
        mesh=mesh,
        in_specs=(
            P("batch", None, None),
            P("batch", None, None),
            P("batch"),
            P("batch", None, None),
            P("batch", None, None),
            P(),
            P(),
            P(None, None, "mp"),
            P(None, "mp"),
            P("mp", None),
            P(),
            P(),
            P(),
            P(),
            P(None, None, "mp"),
            P(None, "mp"),
            P(None, "mp", None),
            P(),
            P(),
            P(),
            P(),
            P(),
            P(),
        ),
        out_specs=(
            P("batch", None, None),
            P("batch", None, None),
            P(),
            P("batch", None, None),
            P("batch", None, None),
            P("batch"),
            P("batch"),
            P("batch", None, "mp"),
            P(None, "mp"),
            P("mp", "batch"),
            P("batch"),
            P("batch"),
            P(None, "batch"),
            P(None, "batch"),
            P(None, "batch", "mp"),
            P(None, "mp"),
            P(None, "mp", "batch"),
            P(None, "batch"),
            P("batch"),
            P(None, "batch"),
            P(None, "batch"),
            P(None, "batch", None),
            P(),
        ),
        check_vma=False,
    )
```

```python
import functools
from typing import NamedTuple

import jax
import jax.numpy as jnp
from jax import lax
from jax.experimental import pallas as pl
from jax.experimental.pallas import tpu as pltpu
from jax.sharding import PartitionSpec as P

HEAD_DIM = 64
F32 = jnp.float32
BF16 = jnp.bfloat16
NEG = -1e9
EPS = 1e-5
ORDER = (0, 2, 1, 3)

VMEM_LIMIT = 60 * 1024 * 1024


def params(**kw):
    return pltpu.CompilerParams(vmem_limit_bytes=VMEM_LIMIT, **kw)


def up16(n):
    return -(-n // 16) * 16


def dot(a, b):
    return jnp.dot(a, b, preferred_element_type=F32)


def dot_t(a, b):
    return lax.dot_general(a, b, (((1,), (1,)), ((), ())), preferred_element_type=F32)


def t_dot(a, b):
    return lax.dot_general(a, b, (((0,), (0,)), ((), ())), preferred_element_type=F32)


def normalise(x):
    c = x - jnp.mean(x, axis=-1, keepdims=True)
    v = jnp.mean(c * c, axis=-1, keepdims=True)
    r = lax.rsqrt(v + EPS)
    return c * r, r


def norm_back(n, r, dn):
    a = jnp.mean(dn, axis=-1, keepdims=True)
    b = jnp.mean(dn * n, axis=-1, keepdims=True)
    return (dn - a - n * b) * r


def gelu_parts(u):
    big = 0.5 * (1.0 + lax.erf(u * 0.7071067811865476))
    small = 0.3989422804014327 * jnp.exp(-0.5 * u * u)
    return big, small


def gelu_low(u):
    return (u * (0.5 * (1.0 + lax.erf(u * 0.7071067811865476)))).astype(BF16)


def softmax_rows(scores):
    m = jnp.max(scores, axis=-1, keepdims=True)
    e = jnp.exp(scores - m)
    return e * (1.0 / jnp.sum(e, axis=-1, keepdims=True))


def tie(value, *after):
    return lax.optimization_barrier((value,) + after)[0]


def load_rows(dims, p, img, txt, rows):
    rows[0:dims.patches, :] = img[p].astype(F32)
    rows[dims.ip:dims.ip + dims.caption, :] = txt[p].astype(F32)


def spec_whole(a):
    return pl.BlockSpec(a.shape, lambda *_: (0,) * a.ndim)


class Dims(NamedTuple):
    patches: int
    caption: int
    ip: int
    tp: int
    slab: int
    quarter: int
    local: int


GAIN1, SHIFT1, A_SCALE, A_BIAS, GAIN2, SHIFT2, F_SCALE, F_BIAS, H_GAIN, H_SHIFT = 0, 1, 2, 3, 4, 6, 8, 9, 11, 13


def vector(table, at, count=1):
    return table[at:at + count, :]


def copy_rows(dst, at, src, start, count):
    dst[at:at + count, :] = src[start:start + count, :]


def parts_of(dims):
    return 2 * HEAD_DIM, HEAD_DIM


def key_tail(dims, length):
    at = dims.patches // 16 * 16
    return ((0, dims.ip, at, dims.patches), (dims.ip, dims.slab, 0, length))


def hide(scores, start, limit):
    if start >= scores.shape[0]:
        return scores
    tail = scores[start:]
    at = start + lax.broadcasted_iota(jnp.int32, (tail.shape[0], 1), 0)
    tail = jnp.where(at < limit, tail, NEG)
    return tail if start == 0 else jnp.concatenate([scores[:start], tail], axis=0)


def split_pair(value):
    low = lax.broadcasted_iota(jnp.int32, (1, 128), 1) < HEAD_DIM
    zero = jnp.zeros_like(value)
    return jnp.concatenate([jnp.where(low, value, zero), jnp.where(low, zero, value)], axis=0)


def join_pair(value):
    low = lax.broadcasted_iota(jnp.int32, (1, 128), 1) < HEAD_DIM
    half = value.shape[0] // 2
    return jnp.where(low, value[:half], value[half:])


def softmax_keys(scores):
    e = jnp.exp(scores - jnp.max(scores, axis=0, keepdims=True))
    return e * (1.0 / jnp.sum(e, axis=0, keepdims=True))


def pair_weights(q, k, start, limit):
    return softmax_keys(hide(dot_t(k, split_pair(q)), start, limit))


def scaled(q):
    return q * jnp.asarray(HEAD_DIM ** -0.5, BF16)


def attend_tiles(dims, lens, quarter_at, qkv, mixed):
    tiles = mixed.shape[-1] // 128

    def one_pair(p, c):
        length = lens[quarter_at * dims.quarter + p]
        for lo, hi, start, limit in key_tail(dims, length):
            for g in range(tiles):
                q, k, v = [qkv[p, lo:hi, (t * tiles + g) * 128:(t * tiles + g + 1) * 128] for t in range(3)]
                w = pair_weights(scaled(q), k, start, limit).astype(BF16)
                mixed[p, lo:hi, g * 128:(g + 1) * 128] = join_pair(t_dot(w, v)).astype(BF16)
        return c

    lax.fori_loop(0, dims.quarter, one_pair, 0)


def attend_own_kernel(dims, order, lens, img, txt, vec, bias, wo, normed, qkv, rest, mixed, rows, w, b):
    i = pl.program_id(0)
    local = dims.local
    two, one_head = parts_of(dims)

    @pl.when(i == 0)
    def _():
        rows[...] = jnp.zeros_like(rows)
        w[...] = jnp.zeros_like(w)
        b[...] = jnp.zeros_like(b)
        for t in range(3):
            copy_rows(w, t * 2 * two, wo, t * local, local)
        b[0:1, 0:local] = bias[0:1, :]
        b[0:1, 4 * two:4 * two + local] = bias[1:2, :]

    def one_norm(p, c):
        load_rows(dims, p, img, txt, rows)
        n, _ = normalise(rows[...])
        normed[p] = (n * vector(vec, GAIN1) + vector(vec, SHIFT1)).astype(BF16)
        return c

    lax.fori_loop(0, dims.quarter, one_norm, 0)
    model = normed.shape[-1]
    proj = (dot_t(normed[...].reshape(dims.quarter * dims.slab, model), w[...]) + b[0:1, :]).astype(BF16)
    proj = proj.reshape(dims.quarter, dims.slab, 6 * two)
    for t in range(3):
        qkv[:, :, t * two:(t + 1) * two] = proj[:, :, 2 * t * two:(2 * t + 1) * two]
        rest[:, :, t * two:(t + 1) * two] = proj[:, :, (2 * t + 1) * two:(2 * t + 2) * two]
    attend_tiles(dims, lens, order[i], qkv, mixed)


def attend_own(dims, order, lens, img, txt, vec, bias, wo):
    model = img.shape[-1]
    pairs = 4 * dims.quarter
    block = lambda cols: pl.BlockSpec((dims.quarter, dims.slab, cols), lambda i, o, n: (i, 0, 0))
    shape = lambda cols: jax.ShapeDtypeStruct((pairs, dims.slab, cols), BF16)
    return pl.pallas_call(
        functools.partial(attend_own_kernel, dims),
        grid_spec=pltpu.PrefetchScalarGridSpec(
            num_scalar_prefetch=2,
            grid=(4,),
            in_specs=[
                pl.BlockSpec((dims.quarter, dims.patches, model), lambda i, o, n: (o[i], 0, 0)),
                pl.BlockSpec((dims.quarter, dims.caption, model), lambda i, o, n: (o[i], 0, 0)),
                spec_whole(vec), spec_whole(bias), spec_whole(wo),
            ],
            out_specs=[block(model), block(384), block(384), block(128)],
            scratch_shapes=[pltpu.VMEM((dims.slab, model), F32), pltpu.VMEM((768, model), BF16),
                            pltpu.VMEM((8, 768), F32)],
        ),
        out_shape=[shape(model), shape(384), shape(384), shape(128)],
        compiler_params=params(),
        cost_estimate=pl.CostEstimate(
            flops=1536 * pairs * dims.slab * model, bytes_accessed=30_000_000, transcendentals=0),
        name="attend_own",
    )(order, lens, img, txt, vec, bias, wo)


def attend_far_kernel(dims, order, lens, normed, rest, own, bias, wo, wf, qkv, mixed, keep, send, w, ow, b):
    i = pl.program_id(0)
    local = dims.local
    two, one_head = parts_of(dims)
    count = dims.quarter * dims.slab
    model = normed.shape[-1]

    @pl.when(i == 0)
    def _():
        w[...] = jnp.zeros_like(w)
        b[...] = jnp.zeros_like(b)
        for t in range(3):
            copy_rows(w, t * 2 * two, wf, t * local, two)
            copy_rows(w, t * 2 * two + two + one_head, wf, t * local + two, one_head)
        for t, at in ((0, 0), (1, 4 * two)):
            b[0:1, at:at + two] = bias[t:t + 1, 0:two]
            b[0:1, at + two + one_head:at + 2 * two] = bias[t:t + 1, two:]
        copy_rows(ow, 0, wo, 3 * local, two)
        copy_rows(ow, two, wf, 3 * local, two)
        copy_rows(ow, 2 * two, wo, 3 * local + two, one_head)
        copy_rows(ow, 2 * two + one_head, wf, 3 * local + two, one_head)

    proj = (dot_t(normed[...].reshape(count, model), w[...]) + b[0:1, :]).astype(BF16)
    proj = proj.reshape(dims.quarter, dims.slab, 6 * two)
    for t in range(3):
        at = 2 * t * two
        qkv[:, :, at:at + two] = proj[:, :, at:at + two]
        qkv[:, :, at + two:at + 2 * two] = proj[:, :, at + two:at + 2 * two] + rest[:, :, t * two:(t + 1) * two]
    attend_tiles(dims, lens, order[(i + 2) % 4], qkv, mixed)
    part = dot(own[...].reshape(count, two), ow[0:two, :])
    part = part + dot(mixed[...].reshape(count, 2 * two), ow[two:, :])
    part = part.astype(BF16).reshape(dims.quarter, dims.slab, model)

    @pl.when(i < 2)
    def _():
        send[...] = part

    @pl.when(i >= 2)
    def _():
        keep[...] = part


def attend_far(dims, order, lens, normed, rest, own, bias, wo, wf):
    model = normed.shape[-1]
    pairs = 4 * dims.quarter
    at = lambda i: (i + 2) % 4
    block = lambda cols, f: pl.BlockSpec((dims.quarter, dims.slab, cols), lambda i, o, n: (f(i), 0, 0))
    shape = lambda count, cols: jax.ShapeDtypeStruct((count, dims.slab, cols), BF16)
    return pl.pallas_call(
        functools.partial(attend_far_kernel, dims),
        grid_spec=pltpu.PrefetchScalarGridSpec(
            num_scalar_prefetch=2,
            grid=(4,),
            in_specs=[
                block(model, at), block(384, at), block(128, at),
                spec_whole(bias), spec_whole(wo), spec_whole(wf),
            ],
            out_specs=[
                block(768, at), block(256, at),
                block(model, lambda i: jnp.maximum(i - 2, 0)), block(model, lambda i: jnp.minimum(i, 1)),
            ],
            scratch_shapes=[pltpu.VMEM((768, model), BF16), pltpu.VMEM((384, model), BF16),
                            pltpu.VMEM((8, 768), F32)],
        ),
        out_shape=[
            shape(pairs, 768), shape(pairs, 256),
            shape(2 * dims.quarter, model), shape(2 * dims.quarter, model),
        ],
        compiler_params=params(),
        cost_estimate=pl.CostEstimate(
            flops=2304 * pairs * dims.slab * model, bytes_accessed=30_000_000, transcendentals=0),
        name="attend_far",
    )(order, lens, normed, rest, own, bias, wo, wf)


def residual_kernel(dims, order, keep, recv, img, txt, vec, attended, attn, expert, cls, rows):
    i = pl.program_id(0)
    ip = dims.ip

    @pl.when(i == 0)
    def _():
        rows[...] = jnp.zeros_like(rows)
        cls[...] = jnp.zeros_like(cls)

    load_rows(dims, 0, img, txt, rows)
    a = keep[0].astype(F32) + recv[0].astype(F32)
    x = rows[...] + vector(vec, A_SCALE) * (a + vector(vec, A_BIAS))
    n, _ = normalise(x)
    e_img = n[0:ip] * vector(vec, GAIN2) + vector(vec, SHIFT2)
    e_txt = n[ip:] * vector(vec, GAIN2 + 1) + vector(vec, SHIFT2 + 1)
    expert[0, 0:ip, :] = e_img.astype(BF16)
    expert[0, ip:, :] = e_txt.astype(BF16)
    for j, v in enumerate((x[0:1], x[ip:ip + 1], e_img[0:1], e_txt[0:1])):
        cls[j, pl.ds(i, 1), :] = v

    @pl.when(i < dims.quarter)
    def _():
        attended[0] = x
        attn[0] = a


def residual(dims, order, keep, recv, img, txt, vec):
    model = img.shape[-1]
    quarter = dims.quarter
    block = pl.BlockSpec((1, dims.slab, model), lambda i, o: (i, 0, 0))
    pair = lambda i, o: (o[i // quarter] * quarter + i % quarter, 0, 0)
    return pl.pallas_call(
        functools.partial(residual_kernel, dims),
        grid_spec=pltpu.PrefetchScalarGridSpec(
            num_scalar_prefetch=1,
            grid=(2 * quarter,),
            in_specs=[
                block, block,
                pl.BlockSpec((1, dims.patches, model), pair),
                pl.BlockSpec((1, dims.caption, model), pair),
                spec_whole(vec),
            ],
            out_specs=[
                pl.BlockSpec((1, dims.slab, model), lambda i, o: (jnp.minimum(i, quarter - 1), 0, 0)),
                pl.BlockSpec((1, dims.slab, model), lambda i, o: (jnp.minimum(i, quarter - 1), 0, 0)),
                block,
                pl.BlockSpec((4, 8, model), lambda i, o: (0, 0, 0)),
            ],
            scratch_shapes=[pltpu.VMEM((dims.slab, model), F32)],
        ),
        out_shape=[
            jax.ShapeDtypeStruct((quarter, dims.slab, model), F32),
            jax.ShapeDtypeStruct((quarter, dims.slab, model), F32),
            jax.ShapeDtypeStruct((2 * quarter, dims.slab, model), BF16),
            jax.ShapeDtypeStruct((4, 8, model), F32),
        ],
        compiler_params=params(),
        cost_estimate=pl.CostEstimate(flops=40_000_000, bytes_accessed=20_000_000, transcendentals=0),
        name="residual",
    )(order, keep, recv, img, txt, vec)


def expert_kernel(dims, seq, peer, own, img, txt, vec, up, up_bias, down,
                  act, dup, ddown, d_send, d_keep, x_send, x_keep, bias_grad, cot, ins, rows):
    ip, slab, quarter = dims.ip, dims.slab, dims.quarter
    i = pl.program_id(0)
    model = own.shape[-1]

    @pl.when(i == 0)
    def _():
        rows[...] = jnp.zeros_like(rows)
        bias_grad[...] = jnp.zeros_like(bias_grad)
        cot[...] = jnp.zeros_like(cot)
        ins[...] = peer[...]

    @pl.when(i == 1)
    def _():
        ins[...] = own[...]

    at = lax.broadcasted_iota(jnp.int32, (slab, 1), 0)
    inner = (at != 0) & (at != ip)

    def one(p, c):
        load_rows(dims, p, img, txt, rows)
        cot[0, pl.ds(8 * i + p, 1), :] = rows[0:1, :]
        cot[1, pl.ds(8 * i + p, 1), :] = rows[ip:ip + 1, :]
        ddown[p] = jnp.where(inner, rows[...] * vector(vec, F_SCALE), 0.0).astype(BF16)
        return c

    lax.fori_loop(0, quarter, one, 0)
    for m, lo, hi in ((0, 0, ip), (1, ip, slab)):
        count = quarter * (hi - lo)
        e = ins[:, lo:hi, :].reshape(count, model)
        u = dot(e, up[m]) + up_bias[m:m + 1]
        big, small = gelu_parts(u)
        a = (u * big).astype(BF16)
        act[:, lo:hi, :] = a.reshape(quarter, hi - lo, -1)
        slope = big + u * small
        d = dot(a, down[m]).astype(BF16).reshape(quarter, hi - lo, model)
        g = ddown[:, lo:hi, :].reshape(count, model)
        du = dot_t(g, down[m]) * slope
        bias_grad[m:m + 1, :] += jnp.sum(du, axis=0, keepdims=True)
        low = du.astype(BF16)
        dup[:, lo:hi, :] = low.reshape(quarter, hi - lo, -1)
        x = dot_t(low, up[m]).astype(BF16).reshape(quarter, hi - lo, model)

        @pl.when(i == 0)
        def _():
            d_send[:, lo:hi, :] = d
            x_send[:, lo:hi, :] = x

        @pl.when(i == 1)
        def _():
            d_keep[:, lo:hi, :] = d
            x_keep[:, lo:hi, :] = x


def experts(dims, name, half, seq, peer, own, img, txt, vec, up, up_bias, down):
    model = own.shape[-1]
    hidden = up.shape[-1]
    slab, quarter = dims.slab, dims.quarter
    fixed = pl.BlockSpec((quarter, slab, model), lambda i, o: (half, 0, 0))
    first = pl.BlockSpec((quarter, slab, model), lambda i, o: (0, 0, 0))
    step = lambda cols: pl.BlockSpec((quarter, slab, cols), lambda i, o: (i, 0, 0))
    shape = lambda n, cols: jax.ShapeDtypeStruct((n * quarter, slab, cols), BF16)
    return pl.pallas_call(
        functools.partial(expert_kernel, dims),
        grid_spec=pltpu.PrefetchScalarGridSpec(
            num_scalar_prefetch=1,
            grid=(2,),
            in_specs=[
                fixed, fixed,
                pl.BlockSpec((quarter, dims.patches, model), lambda i, o: (o[i], 0, 0)),
                pl.BlockSpec((quarter, dims.caption, model), lambda i, o: (o[i], 0, 0)),
                spec_whole(vec), spec_whole(up), spec_whole(up_bias), spec_whole(down),
            ],
            out_specs=[
                step(hidden), step(hidden), step(model),
                first, first, first, first,
                pl.BlockSpec((2, hidden), lambda i, o: (0, 0)),
                pl.BlockSpec((2, 16, model), lambda i, o: (0, 0, 0)),
            ],
            scratch_shapes=[pltpu.VMEM((quarter, slab, model), BF16), pltpu.VMEM((slab, model), F32)],
        ),
        out_shape=[
            shape(2, hidden), shape(2, hidden), shape(2, model),
            shape(1, model), shape(1, model), shape(1, model), shape(1, model),
            jax.ShapeDtypeStruct((2, hidden), F32),
            jax.ShapeDtypeStruct((2, 16, model), F32),
        ],
        compiler_params=params(),
        cost_estimate=pl.CostEstimate(
            flops=16 * quarter * slab * model * hidden, bytes_accessed=20_000_000, transcendentals=0),
        name=name,
    )(seq, peer, own, img, txt, vec, up, up_bias, down)


def expert_grads_kernel(dims, peer, own, act_a, dup_a, ddn_a, act_b, dup_b, ddn_b, ce, ca, cu, cd, out, acc):
    i = pl.program_id(0)

    def add(e, dup, ddn, act):
        for m, lo, hi in ((0, 0, dims.ip), (1, dims.ip, dims.slab)):
            count = dims.quarter * (hi - lo)
            flat = lambda ref: ref[:, lo:hi, :].reshape(count, -1)
            acc[m] += t_dot(flat(e), flat(dup))
            acc[2 + m] += t_dot(flat(ddn), flat(act))

    @pl.when(i == 0)
    def _():
        for m in range(2):
            acc[m] = t_dot(ce[m], cu[m])
            acc[2 + m] = t_dot(cd[m], ca[m])

    for j, refs in enumerate((
        (peer, dup_a, ddn_a, act_a), (own, dup_a, ddn_a, act_a),
        (peer, dup_b, ddn_b, act_b), (own, dup_b, ddn_b, act_b),
    )):
        @pl.when(i == j)
        def _():
            add(*refs)

    @pl.when(i == 3)
    def _():
        out[...] = acc[...].astype(BF16)


def expert_grads(dims, peer, own, act_a, dup_a, ddn_a, act_b, dup_b, ddn_b, ce, ca, cu, cd):
    model = own.shape[-1]
    hidden = act_a.shape[-1]
    slab, quarter = dims.slab, dims.quarter
    assert hidden == model
    half = pl.BlockSpec((quarter, slab, model), lambda i: (jnp.where(i < 2, 1, 0), 0, 0))
    first = pl.BlockSpec((quarter, slab, hidden), lambda i: (jnp.minimum(i, 1), 0, 0))
    last = pl.BlockSpec((quarter, slab, hidden), lambda i: (jnp.maximum(i - 2, 0), 0, 0))
    return pl.pallas_call(
        functools.partial(expert_grads_kernel, dims),
        grid=(4,),
        in_specs=[half, half, first, first, first, last, last, last] + [spec_whole(v) for v in (ce, ca, cu, cd)],
        out_specs=pl.BlockSpec((4, model, hidden), lambda i: (0, 0, 0)),
        scratch_shapes=[pltpu.VMEM((4, model, hidden), F32)],
        out_shape=jax.ShapeDtypeStruct((4, model, hidden), BF16),
        compiler_params=params(),
        cost_estimate=pl.CostEstimate(
            flops=16 * quarter * slab * model * hidden, bytes_accessed=40_000_000, transcendentals=0),
        name="expert_grads",
    )(peer, own, act_a, dup_a, ddn_a, act_b, dup_b, ddn_b, ce, ca, cu, cd)


def own_row(dims, r, p):
    return 8 * (r // 2) + dims.quarter * (r % 2) + p


def class_forward_kernel(dims, near, far, up, up_bias, down, out, rows):
    for m in range(2):
        e = jnp.concatenate([near[2 + m], far[2 + m]], axis=0).astype(BF16)
        rows[m] = e
        u = dot(e, up[m]) + up_bias[m:m + 1]
        out[m] = dot(gelu_low(u), down[m])


def class_forward(dims, near, far, up, up_bias, down):
    shape = (2, 16, near.shape[-1])
    return pl.pallas_call(
        functools.partial(class_forward_kernel, dims),
        out_shape=[jax.ShapeDtypeStruct(shape, F32), jax.ShapeDtypeStruct(shape, BF16)],
        compiler_params=params(),
        cost_estimate=pl.CostEstimate(flops=200_000_000, bytes_accessed=5_000_000, transcendentals=0),
        name="class_forward",
    )(near, far, up, up_bias, down)


def class_final_kernel(dims, order, near, far, d0, d1, d2, d3, vec, out):
    q = dims.quarter
    for m in range(2):
        out[m] = jnp.zeros(out.shape[1:], F32)
        for r in range(4):
            half, at = (near, far)[r // 2], q * (r % 2)
            for p in range(q):
                rows = [d[m, own_row(dims, s, p):own_row(dims, s, p) + 1, :]
                        for d, s in ((d0, r), (d1, r ^ 2), (d2, r ^ 1), (d3, r ^ 3))]
                total = (rows[0] + rows[1]) + (rows[2] + rows[3])
                x = half[m, at + p:at + p + 1, :] + vector(vec, F_SCALE) * (total + vector(vec, F_BIAS + m))
                out[m, pl.ds(4 * order[r] + p, 1), :] = x


def class_final(dims, order, near, far, parts, vec):
    shape = (2, 16, near.shape[-1])
    args = (near, far) + tuple(parts) + (vec,)
    return pl.pallas_call(
        functools.partial(class_final_kernel, dims),
        grid_spec=pltpu.PrefetchScalarGridSpec(
            num_scalar_prefetch=1, grid=(1,),
            in_specs=[spec_whole(v) for v in args],
            out_specs=pl.BlockSpec(shape, lambda i, o: (0, 0, 0)),
        ),
        out_shape=jax.ShapeDtypeStruct(shape, F32),
        compiler_params=params(),
        cost_estimate=pl.CostEstimate(flops=1_000_000, bytes_accessed=1_000_000, transcendentals=0),
        name="class_final",
    )(order, *args)


def class_back_kernel(dims, order, e, cot_a, cot_b, dclass, vec, up, up_bias, down,
                      act, dup, ddown, dexp, bias_grad, dcls, rows):
    q = dims.quarter
    rows[...] = jnp.zeros_like(rows)
    dcls[...] = jnp.zeros_like(dcls)
    for m in range(2):
        for r in range(4):
            cot, base = (cot_b, cot_a)[r % 2], 8 * (1 - r // 2)
            for p in range(q):
                d = dclass[m, pl.ds(4 * order[r] + p, 1), :]
                at = own_row(dims, r, p)
                rows[m, at:at + 1, :] = cot[m, base + p:base + p + 1, :] + d
                if r == 0:
                    dcls[p, m:m + 1, :] = d
        u = dot(e[m], up[m]) + up_bias[m:m + 1]
        big, small = gelu_parts(u)
        act[m] = (u * big).astype(BF16)
        g = (rows[m] * vector(vec, F_SCALE)).astype(BF16)
        ddown[m] = g
        du = dot_t(g, down[m]) * (big + u * small)
        bias_grad[m:m + 1, :] = jnp.sum(du, axis=0, keepdims=True)
        low = du.astype(BF16)
        dup[m] = low
        dexp[m] = dot_t(low, up[m])


def class_back(dims, order, e, cot_a, cot_b, dclass, vec, up, up_bias, down):
    hidden, model = up.shape[-1], e.shape[-1]
    args = (e, cot_a, cot_b, dclass, vec, up, up_bias, down)
    shapes = [((2, 16, hidden), BF16), ((2, 16, hidden), BF16), ((2, 16, model), BF16), ((2, 16, model), F32),
              ((2, hidden), F32), ((dims.quarter, 8, model), F32)]
    return pl.pallas_call(
        functools.partial(class_back_kernel, dims),
        grid_spec=pltpu.PrefetchScalarGridSpec(
            num_scalar_prefetch=1, grid=(1,),
            in_specs=[spec_whole(v) for v in args],
            out_specs=[pl.BlockSpec(s, lambda i, o, n=len(s): (0,) * n) for s, _ in shapes],
            scratch_shapes=[pltpu.VMEM((2, 16, model), F32)],
        ),
        out_shape=[jax.ShapeDtypeStruct(s, t) for s, t in shapes],
        compiler_params=params(),
        cost_estimate=pl.CostEstimate(flops=300_000_000, bytes_accessed=5_000_000, transcendentals=0),
        name="class_back",
    )(order, *args)


def contrast_kernel(dims, total, at, blocks, vec, weight, scale,
                    head_in, dproj, dcls, gains, shifts, scalars, cls, back):
    me = at[0]
    span = blocks[0].shape[0]
    for k, block in enumerate(blocks):
        for j in range(span):
            for m in range(2):
                cls[m, pl.ds(pl.multiple_of(16 * (me ^ (k * span + j)), 16), 16), :] = block[j, m]
    n_rows = cls.shape[1]
    sharp = jnp.exp(scale[...])
    col_at = lax.broadcasted_iota(jnp.int32, (1, n_rows), 1)
    row_at = lax.broadcasted_iota(jnp.int32, (n_rows, 1), 0)
    col_ok = (col_at % 4) < dims.quarter
    row_ok = (row_at % 4) < dims.quarter
    normal, inverse, proj, unit, embed = [], [], [], [], []
    for m in range(2):
        n, r = normalise(cls[m])
        h = (n * vector(vec, H_GAIN + m) + vector(vec, H_SHIFT + m)).astype(BF16)
        head_in[m] = h
        y = dot(h, weight[m])
        u = lax.rsqrt(jnp.sum(y * y, axis=-1, keepdims=True) + 1e-6)
        normal.append(n)
        inverse.append(r)
        proj.append(y)
        unit.append(u)
        embed.append((y * u).astype(BF16))
    ok = row_ok & col_ok
    logits = sharp * dot_t(embed[0], embed[1])
    masked = jnp.where(ok, logits, -1e30)
    row_max = jnp.max(masked, axis=1, keepdims=True)
    row_lse = row_max + jnp.log(jnp.sum(jnp.exp(masked - row_max), axis=1, keepdims=True))
    col_max = jnp.max(masked, axis=0, keepdims=True)
    col_lse = col_max + jnp.log(jnp.sum(jnp.exp(masked - col_max), axis=0, keepdims=True))
    same = (row_at == col_at) & ok
    both = jnp.exp(masked - row_lse) + jnp.exp(masked - col_lse)
    dlogits = jnp.where(ok, jnp.where(same, both - 2.0, both) * (1.0 / (2 * total)), 0.0)
    diagonal = jnp.sum(jnp.where(same, logits, 0.0), axis=1, keepdims=True)
    rows = jnp.where(row_ok, row_lse - 2.0 * diagonal, 0.0)
    cols = jnp.where(col_ok, col_lse, 0.0)
    loss = (jnp.sum(rows, axis=0, keepdims=True) + jnp.sum(cols, axis=1, keepdims=True)) * (1.0 / (2 * total))
    slope = jnp.sum(jnp.sum(dlogits * logits, axis=1, keepdims=True), axis=0, keepdims=True)
    scalars[0:1, :] = jnp.broadcast_to(loss, (1, 128))
    scalars[1:2, :] = jnp.broadcast_to(slope, (1, 128))
    high = lax.Precision.HIGHEST
    wide = [e.astype(F32) for e in embed]
    dembed = [
        sharp * jnp.dot(dlogits, wide[1], precision=high, preferred_element_type=F32),
        sharp * lax.dot_general(dlogits, wide[0], (((0,), (0,)), ((), ())), precision=high,
                                preferred_element_type=F32),
    ]
    for m in range(2):
        u, y, d = unit[m], proj[m], dembed[m]
        dp = (u * d - u * u * u * y * jnp.sum(y * d, axis=-1, keepdims=True)).astype(BF16)
        dproj[m] = dp
        dh = dot_t(dp, weight[m])
        gains[m:m + 1, :] = jnp.sum(dh * normal[m], axis=0, keepdims=True)
        shifts[m:m + 1, :] = jnp.sum(dh, axis=0, keepdims=True)
        back[m] = norm_back(normal[m], inverse[m], dh * vector(vec, H_GAIN + m))
        dcls[m] = back[m, pl.ds(pl.multiple_of(16 * me, 16), 16), :]


def contrast(dims, total, at, blocks, vec, weight, scale):
    model = weight.shape[1]
    rows = 16 * len(blocks) * blocks[0].shape[0]
    args = tuple(blocks) + (vec, weight, scale)
    shapes = [((2, rows, model), BF16), ((2, rows, weight.shape[2]), BF16), ((2, 16, model), F32),
              ((2, model), F32), ((2, model), F32), ((2, 128), F32)]

    def kernel(at, *refs):
        contrast_kernel(dims, total, at, refs[:len(blocks)], *refs[len(blocks):])

    return pl.pallas_call(
        kernel,
        grid_spec=pltpu.PrefetchScalarGridSpec(
            num_scalar_prefetch=1, grid=(1,),
            in_specs=[spec_whole(v) for v in args],
            out_specs=[pl.BlockSpec(s, lambda i, o, n=len(s): (0,) * n) for s, _ in shapes],
            scratch_shapes=[pltpu.VMEM((2, rows, model), F32)] * 2,
        ),
        out_shape=[jax.ShapeDtypeStruct(s, t) for s, t in shapes],
        compiler_params=params(),
        cost_estimate=pl.CostEstimate(flops=1_000_000_000, bytes_accessed=5_000_000, transcendentals=0),
        name="contrast",
    )(at, *args)


def contrast_large(dims, total, at, blocks, vec, weight, scale):
    model = weight.shape[1]
    held = jnp.concatenate(blocks)
    held = held[jnp.arange(held.shape[0]) ^ at[0]]
    rows = jnp.asarray([r for r in range(16) if r % 4 < dims.quarter])
    cls = jnp.transpose(held[:, :, rows], (1, 0, 2, 3)).reshape(2, -1, model)
    gain, shift = vec[H_GAIN:H_GAIN + 2, None], vec[H_SHIFT:H_SHIFT + 2, None]
    n, r = normalise(cls)
    head_in = (n * gain + shift).astype(BF16)
    proj = jnp.einsum("mrc,mce->mre", head_in, weight, preferred_element_type=F32)
    unit = lax.rsqrt(jnp.sum(proj * proj, axis=-1, keepdims=True) + 1e-6)
    embed = (proj * unit).astype(BF16)
    sharp = jnp.exp(scale[0, 0])
    logits = sharp * dot_t(embed[0], embed[1])
    row_lse = jax.nn.logsumexp(logits, axis=1, keepdims=True)
    col_lse = jax.nn.logsumexp(logits, axis=0, keepdims=True)
    dlogits = jnp.exp(logits - row_lse) + jnp.exp(logits - col_lse) - 2.0 * jnp.eye(total, dtype=F32)
    dlogits = dlogits / (2 * total)
    loss = (jnp.sum(row_lse) + jnp.sum(col_lse) - 2.0 * jnp.trace(logits)) / (2 * total)
    slope = jnp.sum(dlogits * logits)
    high = lax.Precision.HIGHEST
    wide = embed.astype(F32)
    dembed = sharp * jnp.stack([
        jnp.dot(dlogits, wide[1], precision=high, preferred_element_type=F32),
        jnp.dot(dlogits.T, wide[0], precision=high, preferred_element_type=F32)])
    dproj = (unit * dembed - unit ** 3 * proj * jnp.sum(proj * dembed, axis=-1, keepdims=True)).astype(BF16)
    dh = jnp.einsum("mre,mce->mrc", dproj, weight, preferred_element_type=F32)
    back = norm_back(n, r, dh * gain)
    pairs = 4 * dims.quarter
    own = lax.dynamic_slice_in_dim(back, at[0] * pairs, pairs, axis=1)
    dcls = jnp.zeros((2, 16, model), F32).at[:, rows].set(own)
    scalars = jnp.broadcast_to(jnp.stack([loss, slope])[:, None], (2, 128))
    return head_in, dproj, dcls, jnp.sum(dh * n, axis=1), jnp.sum(dh, axis=1), scalars


def own_pair(rows_of):
    return lambda i, o: (o[0] * rows_of + i, 0, 0)


def own_call(kernel, dims, name, order, blocks, img, txt, others, outs, scratch):
    model = img.shape[-1]
    block = pl.BlockSpec((1, dims.slab, model), lambda i, o: (i, 0, 0))
    specs = {
        "slab": (block, (dims.quarter, dims.slab, model)),
        "img": (pl.BlockSpec((1, dims.patches, model), lambda i, o: (i, 0, 0)), (dims.quarter, dims.patches, model)),
        "txt": (pl.BlockSpec((1, dims.caption, model), lambda i, o: (i, 0, 0)), (dims.quarter, dims.caption, model)),
        "sums": (pl.BlockSpec((8, model), lambda i, o: (0, 0)), (8, model)),
    }
    return pl.pallas_call(
        functools.partial(kernel, dims),
        grid_spec=pltpu.PrefetchScalarGridSpec(
            num_scalar_prefetch=1,
            grid=(dims.quarter,),
            in_specs=[block] * len(blocks) + [
                pl.BlockSpec((1, dims.patches, model), own_pair(dims.quarter)),
                pl.BlockSpec((1, dims.caption, model), own_pair(dims.quarter)),
            ] + [spec_whole(v) for v in others],
            out_specs=[specs[kind][0] for kind, _ in outs],
            scratch_shapes=[pltpu.VMEM((dims.slab, model), F32)] * scratch,
        ),
        out_shape=[jax.ShapeDtypeStruct(specs[kind][1], dtype) for kind, dtype in outs],
        compiler_params=params(),
        cost_estimate=pl.CostEstimate(flops=40_000_000, bytes_accessed=15_000_000, transcendentals=0),
        name=name,
    )(order, *blocks, img, txt, *others)


def start_own(rows, sums):
    @pl.when(pl.program_id(0) == 0)
    def _():
        rows[...] = jnp.zeros_like(rows)
        sums[...] = jnp.zeros_like(sums)


def add_class(dims, dcls, rows):
    i = pl.program_id(0)
    rows[0:1, :] += dcls[i, 0:1, :]
    rows[dims.ip:dims.ip + 1, :] += dcls[i, 1:2, :]


def final_kernel(dims, order, keep, recv, far, attended, img, txt, dcls, vec, fin_img, fin_txt, sums, rows):
    start_own(rows, sums)
    load_rows(dims, 0, img, txt, rows)
    add_class(dims, dcls, rows)
    for m, lo, hi in ((0, 0, dims.ip), (1, dims.ip, dims.slab)):
        b = keep[0, lo:hi].astype(F32) + recv[0, lo:hi].astype(F32) + far[0, lo:hi].astype(F32)
        b = b + vector(vec, F_BIAS + m)
        f = attended[0, lo:hi, :] + vector(vec, F_SCALE) * b
        if m == 0:
            fin_img[0] = f[0:dims.patches].astype(BF16)
        else:
            fin_txt[0] = f[0:dims.caption].astype(BF16)
        g = rows[lo:hi, :]
        sums[0:1, :] += jnp.sum(g * b, axis=0, keepdims=True)
        sums[1 + m:2 + m, :] += jnp.sum(g, axis=0, keepdims=True) * vector(vec, F_SCALE)


def final_rows(dims, order, keep, recv, far, attended, img, txt, dcls, vec):
    return own_call(final_kernel, dims, "final_rows", order, (keep, recv, far, attended), img, txt,
                    (dcls, vec), (("img", BF16), ("txt", BF16), ("sums", F32)), 1)


def norm_two_kernel(dims, order, keep, recv, far, attended, a_keep, a_recv, img, txt, dcls, x0, x1, x2, x3,
                    vec, dattended, dattn, sums, rows, ups):
    i = pl.program_id(0)
    start_own(rows, sums)
    load_rows(dims, 0, img, txt, rows)
    add_class(dims, dcls, rows)
    ups[...] = keep[0].astype(F32) + recv[0].astype(F32) + far[0].astype(F32)
    for m, at in ((0, 0), (1, dims.ip)):
        extra = [x[m, pl.ds(own_row(dims, r, 0) + i, 1), :] for x, r in ((x0, 0), (x1, 2), (x2, 1), (x3, 3))]
        ups[at:at + 1, :] += (extra[0] + extra[1]) + (extra[2] + extra[3])
    for m, lo, hi in ((0, 0, dims.ip), (1, dims.ip, dims.slab)):
        n, r = normalise(attended[0, lo:hi, :])
        dy = ups[lo:hi, :]
        sums[m:m + 1, :] += jnp.sum(dy * n, axis=0, keepdims=True)
        sums[2 + m:3 + m, :] += jnp.sum(dy, axis=0, keepdims=True)
        d = rows[lo:hi, :] + norm_back(n, r, dy * vector(vec, GAIN2 + m))
        dattended[0, lo:hi, :] = d
        sd = d * vector(vec, A_SCALE)
        dattn[0, lo:hi, :] = sd.astype(BF16)
        a = a_keep[0, lo:hi, :].astype(F32) + a_recv[0, lo:hi, :].astype(F32) + vector(vec, A_BIAS)
        sums[4:5, :] += jnp.sum(d * a, axis=0, keepdims=True)
        sums[5:6, :] += jnp.sum(sd, axis=0, keepdims=True)


def norm_two(dims, order, keep, recv, far, attended, a_keep, a_recv, img, txt, dcls, parts, vec):
    return own_call(norm_two_kernel, dims, "norm_two", order, (keep, recv, far, attended, a_keep, a_recv), img, txt,
                    (dcls,) + tuple(parts) + (vec,), (("slab", F32), ("slab", BF16), ("sums", F32)), 2)


def norm_one_kernel(dims, order, keep, recv, dattended, img, txt, vec, d_img, d_txt, sums, rows):
    start_own(rows, sums)
    load_rows(dims, 0, img, txt, rows)
    n, r = normalise(rows[...])
    dy = keep[0].astype(F32) + recv[0].astype(F32)
    sums[0:1, :] += jnp.sum(dy * n, axis=0, keepdims=True)
    sums[1:2, :] += jnp.sum(dy, axis=0, keepdims=True)
    d = dattended[0] + norm_back(n, r, dy * vector(vec, GAIN1))
    d_img[0] = d[0:dims.patches].astype(BF16)
    d_txt[0] = d[dims.ip:dims.ip + dims.caption].astype(BF16)


def norm_one(dims, order, keep, recv, dattended, img, txt, vec):
    return own_call(norm_one_kernel, dims, "norm_one", order, (keep, recv, dattended), img, txt,
                    (vec,), (("img", BF16), ("txt", BF16), ("sums", F32)), 1)


def attend_back_kernel(dims, far, carry, order, lens, d_own, d_peer, normed, qkv, mixed, wo, wf, *refs):
    if not far:
        prior_keep, prior_send, *refs = refs
    if carry and far:
        fin_img, up_keep, up_send, z_sum, *refs = refs
    elif carry:
        fin_img, fin_txt, grad_f, z_sum, *refs = refs
    keep, send, grad, *refs = refs
    if far:
        grad_rest, *refs = refs
    col_sums, *refs = refs
    if carry:
        near_img, *refs = refs
        if not far:
            near_txt, *refs = refs
        x_sum, z_out, *refs, from_side, from_z, send_sem, recv_sem = refs
    dattn, dmixed, dqkv, acc, w, ow = refs
    i = pl.program_id(0)
    copies = []
    if carry:
        here = Place()
        last = dims.quarter - 1
        own_block = lambda j: pl.ds(pl.multiple_of((2 * j + here.x) * from_side.shape[1], 16), from_side.shape[1])
        side_block = lambda j: pl.ds(pl.multiple_of((2 * j + 1 - here.x) * from_side.shape[1], 16), from_side.shape[1])
        to_near = [(fin_img.at[pl.ds(0, last)], near_img)] if far else [
            (fin_img.at[pl.ds(last, 1)], near_img), (fin_txt, near_txt)]
        to_side = [(up_send.at[j] if far else grad_f.at[side_block(j)], from_side.at[j]) for j in range(4)]
        for (src, dst), device in ([(v, here.near) for v in to_near] + [(v, here.side) for v in to_side] + [
                ((z_sum.at[(here.z + k) % 4], from_z.at[k - 1]), here.along[k - 1]) for k in range(1, 4)]):
            copies.append(remote(src, dst, send_sem, recv_sem, len(copies), device))

        @pl.when(i == 0)
        def _():
            meet([here.near, here.side] + here.along)
            for copy in copies:
                copy.start()

    slab, quarter, local = dims.slab, dims.quarter, dims.local
    two, one_head = parts_of(dims)
    tiles = 2 if far else 1
    width = tiles * two
    count = quarter * slab
    model = normed.shape[-1]

    @pl.when(i == 0)
    def _():
        dattn[...] = d_own[...]
        acc[...] = jnp.zeros_like(acc)
        col_sums[...] = jnp.zeros_like(col_sums)
        for t in range(4):
            dst, at = (w, t * width) if t < 3 else (ow, 0)
            if far:
                copy_rows(dst, at, wf, t * local, two)
                copy_rows(dst, at + two, wo, t * local + two, one_head)
                copy_rows(dst, at + two + one_head, wf, t * local + two, one_head)
            else:
                copy_rows(dst, at, wo, t * local, two)

    @pl.when(i == 1)
    def _():
        dattn[...] = d_peer[...]

    d_rows = dattn[...].reshape(count, model)
    dmixed[...] = dot_t(d_rows, ow[...]).astype(BF16).reshape(quarter, slab, width)

    def one_pair(p, c):
        whose = here.quarter(0, i) if carry else order[2 * i]
        length = lens[whose * quarter + p]
        for lo, hi, start, limit in key_tail(dims, length):
            for g in range(tiles):
                at = [slice((t * tiles + g) * 128, (t * tiles + g + 1) * 128) for t in range(3)]
                q, k, v = [qkv[p, lo:hi, c] for c in at]
                q = scaled(q)
                qq = split_pair(q)
                dd = split_pair(dmixed[p, lo:hi, g * 128:(g + 1) * 128])
                w_ = softmax_keys(hide(dot_t(k, qq), start, limit))
                dw = dot_t(v, dd)
                dqkv[p, lo:hi, at[2]] = dot(w_.astype(BF16), dd).astype(BF16)
                ds = (w_ * (dw - jnp.sum(w_ * dw, axis=0, keepdims=True))).astype(BF16)
                dqkv[p, lo:hi, at[1]] = dot(ds, qq).astype(BF16)
                dqkv[p, lo:hi, at[0]] = (join_pair(t_dot(ds, k)) * HEAD_DIM ** -0.5).astype(BF16)
        return c

    lax.fori_loop(0, quarter, one_pair, 0)
    dp = dqkv[...].reshape(count, 3 * width)
    part = dot(dp, w[...])
    acc[:, 0:3 * width] += t_dot(normed[...].reshape(count, model), dp)
    acc[:, 3 * width:] += t_dot(d_rows, mixed[...].reshape(count, width))
    col_sums[...] += jnp.sum(dp.astype(F32), axis=0, keepdims=True)

    @pl.when(i == 0)
    def _():
        prior = 0.0 if far else prior_keep[...].reshape(count, model).astype(F32)
        keep[...] = (part + prior).astype(BF16).reshape(quarter, slab, model)

    @pl.when(i == 1)
    def _():
        prior = 0.0 if far else prior_send[...].reshape(count, model).astype(F32)
        send[...] = (part + prior).astype(BF16).reshape(quarter, slab, model)
        for t in range(4):
            grad[:, t * two:(t + 1) * two] = acc[:, t * width:t * width + two].astype(BF16)
            if far:
                at = t * width + two
                to = 4 * two + t * one_head
                grad[:, to:to + one_head] = acc[:, at + one_head:at + two].astype(BF16)
                grad_rest[:, t * one_head:(t + 1) * one_head] = acc[:, at:at + one_head].astype(BF16)
        for copy in copies:
            copy.wait()
        if carry:
            for j in range(4):
                own = up_keep[j] if far else grad_f[own_block(j), :]
                x_sum[j] = (own.astype(F32) + from_side[j].astype(F32)).astype(BF16)
            total = z_sum[here.z].astype(F32)
            for k in range(3):
                total = total + from_z[k].astype(F32)
            z_out[...] = total


def attend_back(dims, far, order, lens, d_own, d_peer, normed, qkv, mixed, wo, wf, prior=(), carry=()):
    model = normed.shape[-1]
    slab, quarter = dims.slab, dims.quarter
    width = 256 if far else 128
    one = pl.BlockSpec((quarter, slab, model), lambda i, o, n: (0, 0, 0))
    step = lambda cols: pl.BlockSpec((quarter, slab, cols), lambda i, o, n: (2 * i, 0, 0))
    held = pl.BlockSpec(memory_space=pltpu.VMEM)
    away = pl.BlockSpec(memory_space=pl.ANY)
    grads = (768, 256) if far else (512,)
    specs = [one, one] + [pl.BlockSpec((model, n), lambda i, o, n_: (0, 0)) for n in grads]
    specs += [pl.BlockSpec((1, 3 * width), lambda i, o, n: (0, 0))]
    shapes = [
        jax.ShapeDtypeStruct((quarter, slab, model), BF16),
        jax.ShapeDtypeStruct((quarter, slab, model), BF16),
    ] + [jax.ShapeDtypeStruct((model, n), BF16) for n in grads] + [jax.ShapeDtypeStruct((1, 3 * width), F32)]
    scratch = [
        pltpu.VMEM((quarter, slab, model), BF16),
        pltpu.VMEM((quarter, slab, width), BF16),
        pltpu.VMEM((quarter, slab, 3 * width), BF16),
        pltpu.VMEM((model, 4 * width), F32),
        pltpu.VMEM((3 * width, model), BF16),
        pltpu.VMEM((width, model), BF16),
    ]
    how = params()
    if carry:
        shapes.append(jax.ShapeDtypeStruct((quarter - 1 if far else 1, dims.patches, model), BF16))
        specs.append(away)
        if not far:
            shapes.append(jax.ShapeDtypeStruct((quarter, dims.caption, model), BF16))
            specs.append(away)
        hidden = carry[-1].shape[-1]
        piece = (2, model // 8, hidden)
        side = (4,) + piece if far else (4, model // 8, model)
        shapes += [jax.ShapeDtypeStruct(side, BF16), jax.ShapeDtypeStruct(piece, F32)]
        specs += [held, held]
        scratch += [pltpu.VMEM(side, BF16), pltpu.VMEM((3,) + piece, BF16),
                    pltpu.SemaphoreType.DMA((9,)), pltpu.SemaphoreType.DMA((9,))]
        how = params(collective_id=4 if far else 5, has_side_effects=True)
    return pl.pallas_call(
        functools.partial(attend_back_kernel, dims, far, bool(carry)),
        grid_spec=pltpu.PrefetchScalarGridSpec(
            num_scalar_prefetch=2,
            grid=(2,),
            in_specs=[one, one, step(model), step(3 * width), step(width), spec_whole(wo), spec_whole(wf)]
            + [one] * len(prior) + [held] * len(carry),
            out_specs=specs,
            scratch_shapes=scratch,
        ),
        out_shape=shapes,
        compiler_params=how,
        cost_estimate=pl.CostEstimate(
            flops=32 * quarter * slab * model * width, bytes_accessed=20_000_000, transcendentals=0),
        name="attend_back_far" if far else "attend_back_own",
    )(order, lens, d_own, d_peer, normed, qkv, mixed, wo, wf, *prior, *carry)


def swap(value, axis, bit):
    size = lax.axis_size(axis)
    return lax.ppermute(value, axis, [(j, j ^ bit) for j in range(size)])


def to_core(value):
    return swap(value, "mp", 1)


def to_y(value):
    return swap(value, "mp", 2)


def from_others(value, axis, first, count):
    return [value] + [swap(value, axis, k * first) for k in range(1, count)]


def add_tree(parts):
    while len(parts) > 1:
        parts = [a + b for a, b in zip(parts[::2], parts[1::2])]
    return parts[0]


def sum_over(value, axis):
    first = 1
    while first < lax.axis_size(axis):
        count = min(8, lax.axis_size(axis) // first)
        value = add_tree(from_others(value, axis, first, count))
        first *= count
    return value


def gather_batch(value):
    parts = [value]
    first = 1
    size = lax.axis_size("batch")
    while first < size:
        count = min(8, size // first)
        whole = jnp.concatenate(parts) if len(parts) > 1 else parts[0]
        parts = from_others(whole, "batch", first, count)
        first *= count
    return parts


def gather_rows(own, me):
    near = jnp.stack([own, to_y(own)])
    far = to_core(near)
    out = jnp.zeros((4,) + own.shape, own.dtype)
    for r, value in enumerate((near[0], near[1], far[0], far[1])):
        out = lax.dynamic_update_slice(out, value[None], (me ^ ORDER[r],) + (0,) * own.ndim)
    return out.reshape((4 * own.shape[0],) + own.shape[1:])


def add_low(a, b):
    return (a.astype(F32) + b.astype(F32)).astype(BF16)


MESH = pl.DeviceIdType.MESH


class Place:
    def __init__(self):
        self.b, self.m = lax.axis_index("batch"), lax.axis_index("mp")
        self.z, self.x = self.b // 2, self.b % 2
        self.y, self.c = self.m // 2, self.m % 2
        self.core = (self.b, 2 * self.y + 1 - self.c)
        self.near = (self.b, 2 * (1 - self.y) + self.c)
        self.across = (self.b, 2 * (1 - self.y) + 1 - self.c)
        self.side = (2 * self.z + 1 - self.x, self.m)
        self.along = [(2 * ((self.z + k) % 4) + self.x, self.m) for k in range(1, 4)]
        self.batch = [((self.b + k) % 8, self.m) for k in range(1, 8)]

    def quarter(self, far_y, far_core):
        return 2 * ((self.y + far_y) % 2) + (self.c + far_core) % 2


def meet(peers):
    barrier = pltpu.get_barrier_semaphore()
    for peer in peers:
        pl.semaphore_signal(barrier, inc=1, device_id=peer, device_id_type=MESH)
    pl.semaphore_wait(barrier, len(peers))


def remote(src, dst, send_sem, recv_sem, at, device):
    return pltpu.make_async_remote_copy(
        src_ref=src, dst_ref=dst, send_sem=send_sem.at[at], recv_sem=recv_sem.at[at],
        device_id=device, device_id_type=MESH)


def middle_kernel(dims, total, img, txt, own, peer, cls_own, cls_peer, vec, up, up_bias, down, weight, scale,
                  act, dup, ddn, dexp, d_own, d_near, bias_grad, class_e, c_act, c_dup, c_ddn, dcls,
                  head_in, dproj, gains, shifts, scalars,
                  bx, bd, rx, rd, x_near, x_far, ins, rows, part, parts, cls, back, cot, c_rows, extra, extras,
                  send_sem, recv_sem):
    here = Place()
    ip, slab, quarter = dims.ip, dims.slab, dims.quarter
    i = pl.program_id(0)
    model = own.shape[-1]
    mp_peers = [here.core, here.near, here.across]
    of = [here.quarter(0, 0), here.quarter(1, 0), here.quarter(0, 1), here.quarter(1, 1)]

    sent_x = [remote(bx.at[2 * j], rx.at[j], send_sem, recv_sem, j, here.core) for j in range(2)]
    sent_d = [remote(bd.at[2 * j], rd.at[j], send_sem, recv_sem, 2 + j, here.core) for j in range(2)]
    sent_near = remote(x_near, x_far, send_sem, recv_sem, 4, here.near)
    sent_part = [remote(part, parts.at[k], send_sem, recv_sem, 5 + k, mp_peers[k]) for k in range(3)]
    sent_extra = [remote(extra, extras.at[k], send_sem, recv_sem, 8 + k, mp_peers[k]) for k in range(3)]
    sent_cls = [remote(cls.at[here.b], cls.at[here.b], send_sem, recv_sem, 11 + k, here.batch[k]) for k in range(7)]

    @pl.when(i == 0)
    def _():
        rows[...] = jnp.zeros_like(rows)
        bias_grad[...] = jnp.zeros_like(bias_grad)
        for m in range(2):
            e = jnp.concatenate([cls_own[2 + m], cls_peer[2 + m]], axis=0).astype(BF16)
            class_e[m] = e
            u = dot(e, up[m]) + up_bias[m:m + 1]
            part[m] = dot(gelu_low(u), down[m])
        meet(mp_peers + here.batch)
        for copy in sent_part:
            copy.start()
        ins[...] = peer[quarter:, :, :]

    @pl.when(i == 1)
    def _():
        for copy in sent_part:
            copy.wait_recv()
        for m in range(2):
            cls[here.b, m] = jnp.zeros(cls.shape[2:], F32)
            for r in range(4):
                half, at = (cls_own, cls_peer)[r // 2], quarter * (r % 2)
                for p in range(quarter):
                    line = [d[m, own_row(dims, s, p):own_row(dims, s, p) + 1, :]
                            for d, s in ((part, r), (parts.at[0], r ^ 2), (parts.at[1], r ^ 1), (parts.at[2], r ^ 3))]
                    x = (line[0] + line[1]) + (line[2] + line[3]) + vector(vec, F_BIAS + m)
                    x = half[m, at + p:at + p + 1, :] + vector(vec, F_SCALE) * x
                    cls[here.b, m, pl.ds(4 * of[r] + p, 1), :] = x
        for copy in sent_cls:
            copy.start()
        ins[...] = own[quarter:, :, :]

    @pl.when(i == 2)
    def _():
        ins[...] = peer[:quarter, :, :]

    @pl.when(i == 3)
    def _():
        ins[...] = own[:quarter, :, :]
        for copy in sent_cls:
            copy.wait_recv()
        n_rows = 16 * cls.shape[0]
        sharp = jnp.exp(scale[...])
        col_at = lax.broadcasted_iota(jnp.int32, (1, n_rows), 1)
        row_at = lax.broadcasted_iota(jnp.int32, (n_rows, 1), 0)
        col_ok = (col_at % 4) < quarter
        row_ok = (row_at % 4) < quarter
        normal, inverse, proj, unit, embed = [], [], [], [], []
        for m in range(2):
            n, r = normalise(cls[:, m].reshape(n_rows, model))
            h = (n * vector(vec, H_GAIN + m) + vector(vec, H_SHIFT + m)).astype(BF16)
            head_in[m] = h
            y = dot(h, weight[m])
            u = lax.rsqrt(jnp.sum(y * y, axis=-1, keepdims=True) + 1e-6)
            normal.append(n)
            inverse.append(r)
            proj.append(y)
            unit.append(u)
            embed.append((y * u).astype(BF16))
        ok = row_ok & col_ok
        logits = sharp * dot_t(embed[0], embed[1])
        masked = jnp.where(ok, logits, -1e30)
        row_max = jnp.max(masked, axis=1, keepdims=True)
        row_lse = row_max + jnp.log(jnp.sum(jnp.exp(masked - row_max), axis=1, keepdims=True))
        col_max = jnp.max(masked, axis=0, keepdims=True)
        col_lse = col_max + jnp.log(jnp.sum(jnp.exp(masked - col_max), axis=0, keepdims=True))
        same = (row_at == col_at) & ok
        both = jnp.exp(masked - row_lse) + jnp.exp(masked - col_lse)
        dlogits = jnp.where(ok, jnp.where(same, both - 2.0, both) * (1.0 / (2 * total)), 0.0)
        diagonal = jnp.sum(jnp.where(same, logits, 0.0), axis=1, keepdims=True)
        lines = jnp.sum(jnp.where(row_ok, row_lse - 2.0 * diagonal, 0.0), axis=0, keepdims=True)
        lines = lines + jnp.sum(jnp.where(col_ok, col_lse, 0.0), axis=1, keepdims=True)
        slope = jnp.sum(jnp.sum(dlogits * logits, axis=1, keepdims=True), axis=0, keepdims=True)
        scalars[0:1, :] = jnp.broadcast_to(lines * (1.0 / (2 * total)), (1, 128))
        scalars[1:2, :] = jnp.broadcast_to(slope, (1, 128))
        high = lax.Precision.HIGHEST
        wide = [e.astype(F32) for e in embed]
        dembed = [
            sharp * jnp.dot(dlogits, wide[1], precision=high, preferred_element_type=F32),
            sharp * lax.dot_general(dlogits, wide[0], (((0,), (0,)), ((), ())), precision=high,
                                    preferred_element_type=F32),
        ]
        c_rows[...] = jnp.zeros_like(c_rows)
        dcls[...] = jnp.zeros_like(dcls)
        for m in range(2):
            for p in range(quarter):
                src = (img, txt)[m]
                cot[m, 8 * 3 + p:8 * 3 + p + 1, :] = src[p, 0:1, :].astype(F32)
        for m in range(2):
            u, y, d = unit[m], proj[m], dembed[m]
            dp = (u * d - u * u * u * y * jnp.sum(y * d, axis=-1, keepdims=True)).astype(BF16)
            dproj[m] = dp
            dh = dot_t(dp, weight[m])
            gains[m:m + 1, :] = jnp.sum(dh * normal[m], axis=0, keepdims=True)
            shifts[m:m + 1, :] = jnp.sum(dh, axis=0, keepdims=True)
            back[m] = norm_back(normal[m], inverse[m], dh * vector(vec, H_GAIN + m))
            for r in range(4):
                step = (3, 1, 2, 0)[r]
                for p in range(quarter):
                    g = back[m, pl.ds(16 * here.b + 4 * of[r] + p, 1), :]
                    at = own_row(dims, r, p)
                    c_rows[m, at:at + 1, :] = cot[m, 8 * step + p:8 * step + p + 1, :] + g
                    if r == 0:
                        dcls[p, m:m + 1, :] = g
            u = dot(class_e[m], up[m]) + up_bias[m:m + 1]
            big, small = gelu_parts(u)
            c_act[m] = (u * big).astype(BF16)
            g = (c_rows[m] * vector(vec, F_SCALE)).astype(BF16)
            c_ddn[m] = g
            du = dot_t(g, down[m]) * (big + u * small)
            bias_grad[m:m + 1, :] += jnp.sum(du, axis=0, keepdims=True)
            low = du.astype(BF16)
            c_dup[m] = low
            extra[m] = dot_t(low, up[m])
        for copy in sent_extra:
            copy.start()

    at = lax.broadcasted_iota(jnp.int32, (slab, 1), 0)
    inner = (at != 0) & (at != ip)

    def one(p, c):
        load_rows(dims, p, img, txt, rows)
        cot[0, pl.ds(8 * i + p, 1), :] = rows[0:1, :]
        cot[1, pl.ds(8 * i + p, 1), :] = rows[ip:ip + 1, :]
        ddn[p] = jnp.where(inner, rows[...] * vector(vec, F_SCALE), 0.0).astype(BF16)
        return c

    lax.fori_loop(0, quarter, one, 0)
    for m, lo, hi in ((0, 0, ip), (1, ip, slab)):
        count = quarter * (hi - lo)
        e = ins[:, lo:hi, :].reshape(count, model)
        u = dot(e, up[m]) + up_bias[m:m + 1]
        big, small = gelu_parts(u)
        a = (u * big).astype(BF16)
        act[:, lo:hi, :] = a.reshape(quarter, hi - lo, -1)
        slope = big + u * small
        bd[i, :, lo:hi, :] = dot(a, down[m]).astype(BF16).reshape(quarter, hi - lo, model)
        g = ddn[:, lo:hi, :].reshape(count, model)
        du = dot_t(g, down[m]) * slope
        bias_grad[m:m + 1, :] += jnp.sum(du, axis=0, keepdims=True)
        low = du.astype(BF16)
        dup[:, lo:hi, :] = low.reshape(quarter, hi - lo, -1)
        bx[i, :, lo:hi, :] = dot_t(low, up[m]).astype(BF16).reshape(quarter, hi - lo, model)

    for j in range(2):
        @pl.when(i == 2 * j)
        def _():
            sent_x[j].start()
            sent_d[j].start()

    @pl.when(i == 1)
    def _():
        sent_x[0].wait_recv()

        def add_x(p, c):
            x_near[p] = (bx[1, p].astype(F32) + rx[0, p].astype(F32)).astype(BF16)
            return c

        lax.fori_loop(0, quarter, add_x, 0)
        sent_near.start()
        sent_d[0].wait_recv()

        def add_d(p, c):
            d_near[p] = (bd[1, p].astype(F32) + rd[0, p].astype(F32)).astype(BF16)
            return c

        lax.fori_loop(0, quarter, add_d, 0)

    @pl.when(i == 3)
    def _():
        sent_d[1].wait_recv()

        def add_d(p, c):
            d_own[p] = bd[3, p].astype(F32) + rd[1, p].astype(F32)
            return c

        lax.fori_loop(0, quarter, add_d, 0)
        sent_x[1].wait_recv()
        sent_near.wait_recv()

        def add_x(p, c):
            dexp[p] = bx[3, p].astype(F32) + rx[1, p].astype(F32) + x_far[p].astype(F32)
            return c

        lax.fori_loop(0, quarter, add_x, 0)
        for copy in sent_extra:
            copy.wait_recv()
        for m in range(2):
            for p in range(quarter):
                line = [x[m, own_row(dims, r, p):own_row(dims, r, p) + 1, :]
                        for x, r in ((extra, 0), (extras.at[0], 2), (extras.at[1], 1), (extras.at[2], 3))]
                dexp[p, m * ip:m * ip + 1, :] += (line[0] + line[1]) + (line[2] + line[3])
        for copy in sent_x + sent_d + [sent_near] + sent_part + sent_extra + sent_cls:
            copy.wait_send()


def middle(dims, total, img, txt, own, peer, cls_own, cls_peer, vec, up, up_bias, down, weight, scale):
    model = own.shape[-1]
    hidden = up.shape[-1]
    slab, quarter = dims.slab, dims.quarter
    batch = 8

    def cot_at(i):
        here = Place()
        return here.quarter(1 - i // 2, 1 - i % 2), 0, 0

    held = pl.BlockSpec(memory_space=pltpu.VMEM)
    step = lambda cols: pl.BlockSpec((quarter, slab, cols), lambda i: (i, 0, 0))
    rows_of = lambda n, t: jax.ShapeDtypeStruct((n, slab, model), t)
    small = [((quarter, slab, model), F32), ((quarter, slab, model), F32), ((quarter, slab, model), BF16),
             ((2, hidden), F32), ((2, 16, model), BF16), ((2, 16, hidden), BF16), ((2, 16, hidden), BF16),
             ((2, 16, model), BF16), ((quarter, 8, model), F32), ((2, 16 * batch, model), BF16),
             ((2, 16 * batch, weight.shape[2]), BF16), ((2, model), F32), ((2, model), F32), ((2, 128), F32)]
    block = (quarter, slab, model)
    return pl.pallas_call(
        functools.partial(middle_kernel, dims, total),
        grid=(4,),
        in_specs=[pl.BlockSpec((quarter, dims.patches, model), cot_at),
                  pl.BlockSpec((quarter, dims.caption, model), cot_at)] + [held] * 10,
        out_specs=[step(hidden), step(hidden), step(model)] + [held] * len(small),
        out_shape=[rows_of(4 * quarter, BF16)] * 3 + [jax.ShapeDtypeStruct(v, t) for v, t in small],
        scratch_shapes=[
            pltpu.VMEM((4,) + block, BF16), pltpu.VMEM((4,) + block, BF16),
            pltpu.VMEM((2,) + block, BF16), pltpu.VMEM((2,) + block, BF16),
            pltpu.VMEM(block, BF16), pltpu.VMEM(block, BF16), pltpu.VMEM(block, BF16),
            pltpu.VMEM((slab, model), F32),
            pltpu.VMEM((2, 16, model), F32), pltpu.VMEM((3, 2, 16, model), F32),
            pltpu.VMEM((batch, 2, 16, model), F32), pltpu.VMEM((2, 16 * batch, model), F32),
            pltpu.VMEM((2, 32, model), F32), pltpu.VMEM((2, 16, model), F32),
            pltpu.VMEM((2, 16, model), F32), pltpu.VMEM((3, 2, 16, model), F32),
            pltpu.SemaphoreType.DMA((18,)), pltpu.SemaphoreType.DMA((18,)),
        ],
        compiler_params=params(collective_id=2, has_side_effects=True),
        cost_estimate=pl.CostEstimate(
            flops=32 * quarter * slab * model * hidden, bytes_accessed=40_000_000, transcendentals=0),
        name="middle",
    )(img, txt, own, peer, cls_own, cls_peer, vec, up, up_bias, down, weight, scale)


def turn_kernel(dims, img, txt, peer, own, act, dup, ddn, ce, ca, cu, cd, dexp, attended, attn, d_own, d_near, dcls, vec,
                down_sum, up_keep, up_send, dattended, dattn, dattn_peer, fin_img, fin_txt, sums,
                acc, d_far, n_peer, rows, side_send, side_recv, send_sem, recv_sem):
    here = Place()
    quarter, ip = dims.quarter, dims.ip
    i = pl.program_id(0)
    piece = side_send.shape[2]
    sent_near = remote(d_near, d_far, send_sem, recv_sem, 0, here.near)
    sent_core = [remote(dattn.at[p], n_peer.at[p], send_sem, recv_sem, 1 + p, here.core) for p in range(quarter)]
    sent_side = [remote(side_send.at[j], side_recv.at[j], send_sem, recv_sem, 1 + quarter + j, here.side)
                 for j in range(4)]
    spans = ((0, 0, ip), (1, ip, dims.slab))
    flat = lambda v: v.reshape(-1, v.shape[-1])
    block = lambda j: pl.ds(pl.multiple_of(j * piece, piece), piece)

    @pl.when(i == 0)
    def _():
        meet([here.core, here.near, here.side])
        sent_near.start()
        for m in range(2):
            acc[m] = t_dot(cd[m], ca[m])

    @pl.when(i < 4)
    def _():
        for m, lo, hi in spans:
            acc[m] += t_dot(flat(ddn[:, lo:hi, :]), flat(act[:, lo:hi, :]))

    @pl.when(i == 3)
    def _():
        for j in range(4):
            for m in range(2):
                side_send[j, m] = acc[m, block(2 * j + 1 - here.x), :].astype(BF16)
                down_sum[j, m] = acc[m, block(2 * j + here.x), :].astype(BF16)
            sent_side[j].start()

    @pl.when(i == 4)
    def _():
        for m in range(2):
            acc[m] = t_dot(ce[m], cu[m])

    for j, (e, at) in enumerate(((peer, quarter), (own, quarter), (peer, 0), (own, 0))):
        @pl.when(i == 4 + j)
        def _():
            for m, lo, hi in spans:
                acc[m] += t_dot(flat(e[at:at + quarter, lo:hi, :]), flat(dup[:, lo:hi, :]))

    @pl.when(i == 7)
    def _():
        for j in range(4):
            for m in range(2):
                up_keep[j, m] = acc[m, block(2 * j + here.x), :].astype(BF16)
                up_send[j, m] = acc[m, block(2 * j + 1 - here.x), :].astype(BF16)
        rows[...] = jnp.zeros_like(rows)
        sums[...] = jnp.zeros_like(sums)

        def load(p):
            load_rows(dims, p, img, txt, rows)
            rows[0:1, :] += dcls[p, 0:1, :]
            rows[ip:ip + 1, :] += dcls[p, 1:2, :]

        for p in range(quarter):
            load(p)
            for m, lo, hi in ((0, 0, ip), (1, ip, dims.slab)):
                n, r = normalise(attended[p, lo:hi, :])
                dy = dexp[p, lo:hi, :]
                sums[m:m + 1, :] += jnp.sum(dy * n, axis=0, keepdims=True)
                sums[2 + m:3 + m, :] += jnp.sum(dy, axis=0, keepdims=True)
                d = rows[lo:hi, :] + norm_back(n, r, dy * vector(vec, GAIN2 + m))
                dattended[p, lo:hi, :] = d
                sd = d * vector(vec, A_SCALE)
                dattn[p, lo:hi, :] = sd.astype(BF16)
                a = attn[p, lo:hi, :] + vector(vec, A_BIAS)
                sums[4:5, :] += jnp.sum(d * a, axis=0, keepdims=True)
                sums[5:6, :] += jnp.sum(sd, axis=0, keepdims=True)
            sent_core[p].start()
        sent_near.wait_recv()

        def final(p, c):
            load(p)
            for m, lo, hi in ((0, 0, ip), (1, ip, dims.slab)):
                b = d_own[p, lo:hi, :] + d_far[p, lo:hi, :].astype(F32) + vector(vec, F_BIAS + m)
                f = attended[p, lo:hi, :] + vector(vec, F_SCALE) * b
                if m == 0:
                    fin_img[p] = f[0:dims.patches].astype(BF16)
                else:
                    fin_txt[p] = f[0:dims.caption].astype(BF16)
                g = rows[lo:hi, :]
                sums[6:7, :] += jnp.sum(g * b, axis=0, keepdims=True)
                sums[7 + m:8 + m, :] += jnp.sum(g, axis=0, keepdims=True) * vector(vec, F_SCALE)
            return c

        lax.fori_loop(0, quarter, final, 0)
        for p in range(quarter):
            sent_core[p].wait()
            dattn_peer[p] = n_peer[p]
        for j in range(4):
            sent_side[j].wait()
            down_sum[j] = (down_sum[j].astype(F32) + side_recv[j].astype(F32)).astype(BF16)
        sent_near.wait_send()


def turn(dims, img, txt, peer, own, act, dup, ddn, ce, ca, cu, cd, dexp, attended, attn, d_own, d_near, dcls, vec):
    model = own.shape[-1]
    hidden = act.shape[-1]
    slab, quarter = dims.slab, dims.quarter
    held = pl.BlockSpec(memory_space=pltpu.VMEM)

    def own_at(i):
        return Place().quarter(0, 0), 0, 0

    first = pl.BlockSpec((quarter, slab, hidden), lambda i: (jnp.minimum(i, 3), 0, 0))
    last = pl.BlockSpec((quarter, slab, hidden), lambda i: (jnp.maximum(i - 4, 0), 0, 0))
    block = (quarter, slab, model)
    part = (4, 2, model // 8, hidden)
    outs = [(part, BF16), (part, BF16), (part, BF16), (block, F32), (block, BF16), (block, BF16),
            ((quarter, dims.patches, model), BF16), ((quarter, dims.caption, model), BF16), ((16, model), F32)]
    return pl.pallas_call(
        functools.partial(turn_kernel, dims),
        grid=(8,),
        in_specs=[pl.BlockSpec((quarter, dims.patches, model), own_at),
                  pl.BlockSpec((quarter, dims.caption, model), own_at)] + [held] * 2 + [first, last, first]
        + [held] * 11,
        out_specs=[held] * len(outs),
        out_shape=[jax.ShapeDtypeStruct(v, t) for v, t in outs],
        scratch_shapes=[
            pltpu.VMEM((2, model, hidden), F32), pltpu.VMEM(block, BF16), pltpu.VMEM(block, BF16),
            pltpu.VMEM((slab, model), F32), pltpu.VMEM(part, BF16), pltpu.VMEM(part, BF16),
            pltpu.SemaphoreType.DMA((5 + quarter,)), pltpu.SemaphoreType.DMA((5 + quarter,)),
        ],
        compiler_params=params(collective_id=3, has_side_effects=True),
        cost_estimate=pl.CostEstimate(
            flops=16 * quarter * slab * model * hidden, bytes_accessed=40_000_000, transcendentals=0),
        name="turn",
    )(img, txt, peer, own, act, dup, ddn, ce, ca, cu, cd, dexp, attended, attn, d_own, d_near, dcls, vec)


V_ROWS, V_MP, V_HEADS, V_FAR = 24, 11, 13, 15


def finish_kernel(dims, n_keep, n_send, dattended, states_img, states_txt, vec, fin_img, fin_txt,
                  near_a, near_b, near_txt, grad_pair, grad_single, grad_far, own_sums, up_sums, cols_own, cols_far,
                  out_img, out_txt, back_img, back_txt, grad_out, v_out,
                  n_recv, s_img, s_txt, d_img, d_txt, rows, xr, zs, zr, zr_far, far_sum, far_recv, vs, vr,
                  local_sem, send_sem, recv_sem):
    quarter = dims.quarter
    here = Place()
    z, x, m = here.z, here.x, here.m
    near_quarter = here.quarter(1, 0)
    used = [0]

    def send(src, dst, device):
        at = used[0]
        used[0] += 1
        return remote(src, dst, send_sem, recv_sem, at, device)

    loaded = [pltpu.make_async_copy(states_img.at[pl.ds(m * quarter, quarter)], s_img, local_sem.at[0]),
              pltpu.make_async_copy(states_txt.at[pl.ds(m * quarter, quarter)], s_txt, local_sem.at[1])]
    for copy in loaded:
        copy.start()
    meet([here.core, here.near, here.side] + here.along)

    n_copies = [send(n_send.at[p], n_recv.at[p], here.core) for p in range(quarter)]
    for copy in n_copies:
        copy.start()
    piece = xr.shape[1]
    wide = grad_pair.shape[1]
    spans = ((grad_pair, 0, wide), (grad_single, wide, xr.shape[2]))
    block = lambda j: pl.ds(pl.multiple_of(j * piece, piece), piece)
    x_copies = []
    for j in range(4):
        for src, lo, hi in spans:
            x_copies.append(send(src.at[block(2 * j + 1 - x)], xr.at[j, :, pl.ds(lo, hi - lo)], here.side))
            x_copies[-1].start()
    far_copies = [send(grad_far.at[(z + k) % 4], zr_far.at[k - 1], here.along[k - 1]) for k in range(1, 4)]
    for copy in far_copies:
        copy.start()

    last = quarter - 1
    fin_local, fin_remote = [], []
    for j, (src, dst, at, count) in enumerate((
        (fin_img, out_img, m * quarter, quarter), (fin_txt, out_txt, m * quarter, quarter),
        (near_a, out_img, near_quarter * quarter, last), (near_b, out_img, near_quarter * quarter + last, 1),
        (near_txt, out_txt, near_quarter * quarter, quarter),
    )):
        fin_local.append(pltpu.make_async_copy(src, dst.at[pl.ds(at, count)], local_sem.at[2 + j]))
        fin_remote.append(send(src, dst.at[pl.ds(at, count)], here.core))

    rows[...] = jnp.zeros_like(rows)
    for copy in loaded:
        copy.wait()
    total = [jnp.zeros((1, rows.shape[1]), F32)] * 2
    back_local, to_near, to_other = [], [], []
    for p in range(quarter):
        load_rows(dims, p, s_img, s_txt, rows)
        n, r = normalise(rows[...])
        n_copies[p].wait_recv()
        dy = n_keep[p].astype(F32) + n_recv[p].astype(F32)
        total[0] = total[0] + jnp.sum(dy * n, axis=0, keepdims=True)
        total[1] = total[1] + jnp.sum(dy, axis=0, keepdims=True)
        d = dattended[p] + norm_back(n, r, dy * vector(vec, GAIN1))
        d_img[p] = d[0:dims.patches].astype(BF16)
        d_txt[p] = d[dims.ip:dims.ip + dims.caption].astype(BF16)
        for j, (src, dst) in enumerate(((d_img, back_img), (d_txt, back_txt))):
            at = dst.at[m * quarter + p]
            to_near.append(send(src.at[p], at, here.near))
            to_near[-1].start()
            to_other.append(send(src.at[p], at, here.core))
            to_other[-1].start()
            back_local.append(pltpu.make_async_copy(src.at[p], at, local_sem.at[7 + 2 * p + j]))
            back_local[-1].start()
    for copy in fin_local + fin_remote:
        copy.start()

    def own_sum(j, k):
        src, lo, hi = spans[k]
        return src[block(2 * j + x), :].astype(F32) + xr[j, :, lo:hi].astype(F32)

    for copy in x_copies:
        copy.wait_recv()
    for j in range(4):
        for k, (src, lo, hi) in enumerate(spans):
            zs[j, :, lo:hi] = own_sum(j, k).astype(BF16)
    z_copies = [send(zs.at[(z + k) % 4], zr.at[k - 1], here.along[k - 1]) for k in range(1, 4)]
    for copy in z_copies:
        copy.start()

    at = lax.broadcasted_iota(jnp.int32, (V_ROWS, 1), 0)
    two, one_head = parts_of(dims)
    vs[0] = jnp.zeros(vs.shape[1:], F32)
    vs[0, 0:1, :] = total[0]
    vs[0, 1:2, :] = total[1]
    vs[0, 2:V_MP, :] = own_sums[0:V_MP - 2, :]
    vs[0, V_MP:V_HEADS, :] = up_sums[...]
    for j in range(2):
        own_at, far_at = 2 * j * two, 4 * j * two
        vs[0, V_HEADS + j:V_HEADS + j + 1, 0:two] = cols_own[0:1, own_at:own_at + two]
        vs[0, V_HEADS + j:V_HEADS + j + 1, two:two + one_head] = cols_far[0:1, far_at + two:far_at + two + one_head]
        vs[0, V_FAR + j:V_FAR + j + 1, 0:two] = cols_far[0:1, far_at:far_at + two]
        vs[0, V_FAR + j:V_FAR + j + 1, two:two + one_head] = cols_far[0:1, far_at + two + one_head:far_at + 2 * two]
    v = vs[0]
    v_copies = []

    def exchange(step, value, device):
        vs[step] = value
        copy = send(vs.at[step], vr.at[step], device)
        copy.start()
        copy.wait_recv()
        v_copies.append(copy)
        return vr[step]

    v = v + jnp.where(at < V_MP, exchange(0, v, here.core), 0.0)
    v = v + exchange(1, v, here.side)
    vs[2] = v
    vr[3 + z] = v
    around = [send(vs.at[2], vr.at[3 + z], here.along[k - 1]) for k in range(1, 4)]
    for copy in around:
        copy.start()
    for copy in around:
        copy.wait_recv()
    v = (vr[3] + vr[4]) + (vr[5] + vr[6])
    for copy in far_copies:
        copy.wait_recv()
    far = grad_far[z].astype(F32)
    for k in range(3):
        far = far + zr_far[k].astype(F32)
    far_sum[...] = far.astype(BF16)
    far_copy = send(far_sum, far_recv, here.near)
    far_copy.start()
    vs[3] = v
    v_near = send(vs.at[3], vr.at[2], here.near)
    v_near.start()
    for copy in z_copies:
        copy.wait_recv()
    for copy in fin_local + back_local:
        copy.wait()
    onward = []
    for p in range(quarter):
        for j, dst in enumerate((back_img, back_txt)):
            to_near[2 * p + j].wait_recv()
            at_near = dst.at[near_quarter * quarter + p]
            onward.append(send(at_near, at_near, here.core))
            onward[-1].start()
    far_copy.wait_recv()
    for k, (src, lo, hi) in enumerate(spans):
        g = own_sum(z, k) + far_recv[:, lo:hi].astype(F32)
        for j in range(3):
            g = g + zr[j, :, lo:hi].astype(F32)
        grad_out[:, lo:hi] = g
    v_near.wait_recv()
    there = vr[2]
    v_out[...] = v + jnp.where(at < V_MP, there, 0.0)
    v_out[V_HEADS:V_HEADS + 2, :] = v[V_HEADS:V_HEADS + 2, :] + there[V_FAR:V_FAR + 2, :]
    for copy in to_other + fin_remote + onward:
        copy.wait()
    for copy in n_copies + x_copies + far_copies + to_near + z_copies + v_copies + around + [far_copy, v_near]:
        copy.wait_send()


def finish(dims, n_keep, n_send, dattended, states_img, states_txt, vec, fin_img, fin_txt,
           near_a, near_b, near_txt, grad_pair, grad_single, grad_far, *tables):
    pairs, patches, model = states_img.shape
    caption = states_txt.shape[1]
    quarter, slab = dims.quarter, dims.slab
    piece, cols = grad_far.shape[1:]
    held = pl.BlockSpec(memory_space=pltpu.VMEM)
    away = pl.BlockSpec(memory_space=pl.ANY)
    n_remote = 7 * quarter + 27
    return pl.pallas_call(
        functools.partial(finish_kernel, dims),
        in_specs=[held] * 3 + [away] * 2 + [held] * 13,
        out_specs=[away] * 4 + [held] * 2,
        out_shape=[
            jax.ShapeDtypeStruct((pairs, patches, model), BF16),
            jax.ShapeDtypeStruct((pairs, caption, model), BF16),
            jax.ShapeDtypeStruct((pairs, patches, model), BF16),
            jax.ShapeDtypeStruct((pairs, caption, model), BF16),
            jax.ShapeDtypeStruct((piece, cols), F32),
            jax.ShapeDtypeStruct((V_ROWS, model), F32),
        ],
        scratch_shapes=[
            pltpu.VMEM((quarter, slab, model), BF16),
            pltpu.VMEM((quarter, patches, model), BF16),
            pltpu.VMEM((quarter, caption, model), BF16),
            pltpu.VMEM((quarter, patches, model), BF16),
            pltpu.VMEM((quarter, caption, model), BF16),
            pltpu.VMEM((slab, model), F32),
            pltpu.VMEM((4, piece, cols), BF16), pltpu.VMEM((4, piece, cols), BF16),
            pltpu.VMEM((3, piece, cols), BF16), pltpu.VMEM((3, piece, cols), BF16),
            pltpu.VMEM((piece, cols), BF16), pltpu.VMEM((piece, cols), BF16),
            pltpu.VMEM((4, V_ROWS, model), F32),
            pltpu.VMEM((7, V_ROWS, model), F32),
            pltpu.SemaphoreType.DMA((7 + 2 * quarter,)),
            pltpu.SemaphoreType.DMA((n_remote,)),
            pltpu.SemaphoreType.DMA((n_remote,)),
        ],
        compiler_params=params(collective_id=1, has_side_effects=True),
        name="finish",
    )(n_keep, n_send, dattended, states_img, states_txt, vec, fin_img, fin_txt,
      near_a, near_b, near_txt, grad_pair, grad_single, grad_far, *tables)


def spread_kernel(cols, at, sums, grad, gains, shifts, *refs):
    *outs, qkv, out_w, turned = refs
    back = sums.shape[1] - at[0] * cols

    def slice_of(value):
        return pltpu.roll(value, back, 1)[:, 0:cols]

    mine = slice_of(sums[...])
    for out, (lo, count) in zip(outs[:8], ((0, 1), (1, 1), (7, 1), (6, 1), (2, 2), (4, 2), (9, 2), (8, 1))):
        out[...] = mine[lo:lo + count, :]
    wide = jnp.concatenate([gains[...], shifts[...], jnp.zeros((4, sums.shape[1]), F32)], axis=0)
    heads = slice_of(wide)
    outs[8][...] = heads[0:2, :]
    outs[9][...] = heads[2:4, :]
    outs[10][...] = sums[V_MP:V_MP + 2, :]
    outs[11][...] = sums[V_HEADS:V_HEADS + 2, 0:outs[11].shape[1]]
    two, one = 2 * HEAD_DIM, HEAD_DIM
    for t in range(3):
        qkv[t, :, 0:two] = grad[:, t * two:(t + 1) * two]
        qkv[t, :, two:two + one] = grad[:, 4 * two + t * one:4 * two + (t + 1) * one]
    turned[...] = jnp.zeros_like(turned)
    turned[0:cols, 0:two] = grad[:, 3 * two:4 * two]
    turned[0:cols, two:two + one] = grad[:, 4 * two + 3 * one:4 * two + 4 * one]
    out_w[...] = turned[...].T[0:two + one, 0:cols]


def spread(local, at, sums, grad, gains, shifts):
    cols, model = grad.shape[0], sums.shape[1]
    assert cols <= 128
    shapes = [(1, cols)] * 4 + [(2, cols)] * 3 + [(1, cols)] + [(2, cols)] * 2 + [(2, model), (2, local)]
    shapes += [(3, cols, local), (local, cols)]
    args = (sums, grad, gains, shifts)
    return pl.pallas_call(
        functools.partial(spread_kernel, cols),
        grid_spec=pltpu.PrefetchScalarGridSpec(
            num_scalar_prefetch=1, grid=(1,),
            in_specs=[spec_whole(v) for v in args],
            out_specs=[pl.BlockSpec(v, lambda i, o, n=len(v): (0,) * n) for v in shapes],
            scratch_shapes=[pltpu.VMEM((128, 256), F32)],
        ),
        out_shape=[jax.ShapeDtypeStruct(v, F32) for v in shapes],
        compiler_params=params(),
        cost_estimate=pl.CostEstimate(flops=1_000_000, bytes_accessed=1_000_000, transcendentals=0),
        name="spread",
    )(at, *args)


def per_device(
    image_states, text_states, caption_lengths, image_cotangent, text_cotangent,
    first_gain, first_shift, query_key_value, query_value_bias, output_weight, output_bias,
    attention_scale, expert_gain, expert_shift, expert_up, expert_up_bias, expert_down,
    expert_down_bias, feedforward_scale, head_gain, head_shift, head_weight, logit_scale,
):
    pairs, patches, model = image_states.shape
    caption = text_states.shape[1]
    local = query_key_value.shape[2]
    quarter = pairs // 4
    batch_size = lax.axis_size("batch")
    assert lax.axis_size("mp") == 4 and pairs == 4 * quarter and quarter <= 3
    assert batch_size & (batch_size - 1) == 0
    assert local == 3 * HEAD_DIM
    ip, tp = up16(patches), up16(caption)
    dims = Dims(patches, caption, ip, tp, ip + tp, quarter, local)
    me = lax.axis_index("mp")
    batch_at = lax.axis_index("batch")
    order = me ^ jnp.asarray(ORDER, jnp.int32)
    vec = jnp.concatenate([
        first_gain[None], first_shift[None], attention_scale[None], output_bias[None], expert_gain, expert_shift,
        feedforward_scale[None], expert_down_bias, head_gain, head_shift, jnp.zeros((1, model), F32)])

    wo = jnp.concatenate([jnp.transpose(query_key_value, (1, 2, 0)).reshape(3 * local, model), output_weight])
    wf = to_y(wo)
    far_bias = to_y(query_value_bias)
    normed, qkv_own, rest, mixed_own = attend_own(
        dims, order, caption_lengths, image_states, text_states, vec, query_value_bias, wo)
    qkv_far, mixed_far, a_keep, a_send = attend_far(
        dims, order, caption_lengths, normed, rest, mixed_own, far_bias, wo, wf)
    a_recv = to_core(a_send)
    attended, attn, e_own, cls_own = residual(
        dims, order, a_keep, a_recv, image_states, text_states, vec)
    e_peer = to_core(e_own)
    cls_peer = to_core(cls_own)
    one_kernel = batch_size == 8 and model // batch_size % 32 == 0 and expert_up.shape[2] == model
    if one_kernel:
        (act, dup, ddn, dexp, d_own, d_near, up_sums, class_e, c_act, c_dup, c_ddn, dcls, head_in, dproj,
         grad_head_gain, grad_head_shift, scalars) = middle(
            dims, pairs * batch_size, image_cotangent, text_cotangent, e_own, e_peer, cls_own, cls_peer, vec,
            expert_up, expert_up_bias, expert_down, head_weight, logit_scale.reshape(1, 1))
        down_sum, up_keep, up_send, dattended, dattn, dattn_peer, fin_img, fin_txt, own_sums = turn(
            dims, image_cotangent, text_cotangent, e_peer, e_own, act, dup, ddn, class_e, c_act, c_dup, c_ddn,
            dexp, attended, attn, d_own, d_near, dcls, vec)
    else:
        class_part, class_e = class_forward(dims, cls_own, cls_peer, expert_up, expert_up_bias, expert_down)
        class_parts = from_others(class_part, "mp", 1, 4)

        act_a, dup_a, ddn_a, d_send3, d_keep1, x_send3, x_keep1, bias_a, cot_a = experts(
            dims, "experts_a", 1, order[jnp.asarray([3, 1])], e_peer, e_own, image_cotangent, text_cotangent,
            tie(vec, class_part), expert_up, expert_up_bias, expert_down)
        x_recv1 = to_core(x_send3)
        d_recv1 = to_core(d_send3)
        final_class = class_final(
            dims, order, cls_own, cls_peer, class_parts, tie(vec, bias_a))
        class_blocks = gather_batch(final_class[None])
        x_near = add_low(x_keep1, x_recv1)
        x_far = to_y(x_near)
        act_b, dup_b, ddn_b, d_send2, d_keep0, x_send2, x_keep0, bias_b, cot_b = experts(
            dims, "experts_b", 0, order[jnp.asarray([2, 0])], e_peer, e_own, image_cotangent, text_cotangent,
            tie(vec, final_class, x_near), expert_up, expert_up_bias, expert_down)
        x_recv0 = to_core(x_send2)
        d_recv0 = to_core(d_send2)

        head_in, dproj, dclass, grad_head_gain, grad_head_shift, scalars = (contrast if batch_size <= 8 else contrast_large)(
            dims, pairs * batch_size, batch_at.reshape(1), class_blocks, tie(vec, bias_b), head_weight,
             logit_scale.reshape(1, 1))
        c_act, c_dup, c_ddn, c_dexp, c_bias, dcls = class_back(
            dims, order, class_e, cot_a, cot_b, dclass, vec, expert_up, expert_up_bias, expert_down)
        extras = from_others(c_dexp, "mp", 1, 4)
        d_far = to_y(add_low(d_keep1, tie(d_recv1, c_dexp)))
        expert_grad = expert_grads(
            dims, e_peer, e_own, act_a, dup_a, ddn_a, act_b, dup_b, ddn_b, class_e, c_act, c_dup, c_ddn)
        expert_sum = lax.psum_scatter(expert_grad, "batch", scatter_dimension=1, tiled=True)

        dattended, dattn, sums_two = norm_two(
            dims, order, x_keep0, x_recv0, x_far, attended, a_keep, a_recv, image_cotangent, text_cotangent,
            dcls, extras, tie(vec, expert_grad))
        dattn_peer = to_core(dattn)
        fin_img, fin_txt, sums_fin = final_rows(
            dims, order, d_keep0, d_recv0, d_far, attended, image_cotangent, text_cotangent, dcls,
            tie(vec, sums_two))
        own_sums = jnp.concatenate([sums_two[:6], sums_fin[:3]])
        up_sums = bias_a + bias_b + c_bias
    contrast_loss = scalars[0, :1]
    grad_logit_scale = scalars[1, :1]
    carried = dict(carry=(fin_img, up_keep, up_send, down_sum)) if one_kernel else {}
    n_keep, n_send, grad_far, grad_o2, cols_far, *more_far = attend_back(
        dims, True, order, caption_lengths, dattn, dattn_peer, normed, qkv_far, mixed_far, wo, wf, **carried)
    carried = dict(carry=(fin_img, fin_txt, grad_far, more_far[1])) if one_kernel else {}
    n_keep, n_send, grad_o01, cols_own, *more_own = attend_back(
        dims, False, order, caption_lengths, dattn, dattn_peer, normed, qkv_own, mixed_own, wo, wf,
        prior=(n_keep, n_send), **carried)
    cols = model // batch_size
    mine = lambda v, axis: lax.dynamic_slice_in_dim(v, batch_at * cols, cols, axis=axis)
    grad_head_weight = jnp.einsum("mnc,mne->mce", mine(head_in, 2), dproj, preferred_element_type=F32)
    pair, single = 2 * HEAD_DIM, HEAD_DIM
    if one_kernel:
        near_a, _, grad_down = more_far
        near_b, near_txt, side_sum, grad_up = more_own
        image_output, text_output, image_grad, text_grad, attn_grad, sums = finish(
            dims, n_keep, n_send, dattended, image_states, text_states, vec, fin_img, fin_txt,
            near_a, near_b, near_txt, grad_o01, grad_o2, side_sum, own_sums, up_sums, cols_own, cols_far)
        *vectors, grad_qkv, grad_output_weight = spread(
            local, batch_at.reshape(1), sums, attn_grad, grad_head_gain, grad_head_shift)
        flat = lambda v: v.reshape(-1)
        return (
            image_output,
            text_output,
            contrast_loss,
            image_grad,
            text_grad,
            flat(vectors[0]),
            flat(vectors[1]),
            jnp.transpose(grad_qkv, (1, 0, 2)),
            vectors[11],
            grad_output_weight,
            flat(vectors[2]),
            flat(vectors[3]),
            vectors[4],
            vectors[5],
            grad_up,
            vectors[10],
            jnp.transpose(grad_down, (0, 2, 1)),
            vectors[6],
            flat(vectors[7]),
            vectors[8],
            vectors[9],
            grad_head_weight,
            grad_logit_scale,
        )
    else:
        grad_expert_up = expert_sum[:2].astype(F32)
        grad_expert_down = jnp.transpose(expert_sum[2:].astype(F32), (0, 2, 1))
        cols_own = cols_own.reshape(3, pair)[::2]
        cols_far = cols_far.reshape(3, 2 * pair)[::2]
        heads = jnp.concatenate([cols_own, cols_far[:, pair:pair + single]], axis=1)
        heads_far = jnp.concatenate([cols_far[:, :pair], cols_far[:, pair + single:]], axis=1)
        n_recv = to_core(n_send)
        d_img, d_txt, sums_one = norm_one(
            dims, order, n_keep, n_recv, dattended, image_states, text_states, vec)
        image_output = gather_rows(fin_img, me)
        text_output = gather_rows(fin_txt, me)
        image_grad = gather_rows(d_img, me)
        text_grad = gather_rows(d_txt, me)
        grad_own = jnp.concatenate([grad_o01, grad_o2], axis=1)
        grad_far = lax.psum_scatter(grad_far, "batch", scatter_dimension=0, tiled=True)
        grad_own = lax.psum_scatter(grad_own, "batch", scatter_dimension=0, tiled=True)
        attn_grad = grad_own.astype(F32) + to_y(grad_far).astype(F32)
        heads = heads + to_y(heads_far)
        own_sums = sum_over(jnp.concatenate([sums_one[:2], own_sums]), "mp")
        flat = jnp.concatenate([own_sums.reshape(-1), heads.reshape(-1), up_sums.reshape(-1)])
        count = flat.shape[0]
        flat = jnp.pad(flat, (0, -count % 1024)).reshape(-1, 128)
        flat = sum_over(flat, "batch").reshape(-1)[:count]
        done = own_sums.shape[0]
        own_sums = mine(flat[:done * model].reshape(done, model), 1)
        heads = flat[done * model:done * model + 2 * local].reshape(2, local)
        grad_expert_up_bias = flat[done * model + 2 * local:].reshape(up_sums.shape)
    attn_grad = jnp.concatenate(
        [attn_grad[:, :4 * pair].reshape(cols, 4, pair), attn_grad[:, 4 * pair:].reshape(cols, 4, single)], axis=2)
    grad_query_key_value = attn_grad[:, :3]
    grad_output_weight = jnp.transpose(attn_grad[:, 3])
    return (
        image_output,
        text_output,
        contrast_loss,
        image_grad,
        text_grad,
        own_sums[0],
        own_sums[1],
        grad_query_key_value,
        heads,
        grad_output_weight,
        own_sums[7],
        own_sums[6],
        own_sums[2:4],
        own_sums[4:6],
        grad_expert_up,
        grad_expert_up_bias,
        grad_expert_down,
        own_sums[9:11],
        own_sums[8],
        mine(grad_head_gain, 1),
        mine(grad_head_shift, 1),
        grad_head_weight,
        grad_logit_scale,
    )


def solution(mesh):
    return jax.shard_map(
        per_device,
        mesh=mesh,
        in_specs=(
            P("batch", None, None),
            P("batch", None, None),
            P("batch"),
            P("batch", None, None),
            P("batch", None, None),
            P(),
            P(),
            P(None, None, "mp"),
            P(None, "mp"),
            P("mp", None),
            P(),
            P(),
            P(),
            P(),
            P(None, None, "mp"),
            P(None, "mp"),
            P(None, "mp", None),
            P(),
            P(),
            P(),
            P(),
            P(),
            P(),
        ),
        out_specs=(
            P("batch", None, None),
            P("batch", None, None),
            P(),
            P("batch", None, None),
            P("batch", None, None),
            P("batch"),
            P("batch"),
            P("batch", None, "mp"),
            P(None, "mp"),
            P("mp", "batch"),
            P("batch"),
            P("batch"),
            P(None, "batch"),
            P(None, "batch"),
            P(None, "batch", "mp"),
            P(None, "mp"),
            P(None, "mp", "batch"),
            P(None, "batch"),
            P("batch"),
            P(None, "batch"),
            P(None, "batch"),
            P(None, "batch", None),
            P(),
        ),
        check_vma=False,
    )
```

```python
import functools
from typing import NamedTuple

import jax
import jax.numpy as jnp
from jax import lax
from jax.experimental import pallas as pl
from jax.experimental.pallas import tpu as pltpu
from jax.sharding import PartitionSpec as P

HEAD_DIM = 64
F32 = jnp.float32
BF16 = jnp.bfloat16
NEG = -1e9
EPS = 1e-5
ORDER = (0, 2, 1, 3)

VMEM_LIMIT = 60 * 1024 * 1024


def params(**kw):
    return pltpu.CompilerParams(vmem_limit_bytes=VMEM_LIMIT, **kw)


def up16(n):
    return -(-n // 16) * 16


def dot(a, b):
    return jnp.dot(a, b, preferred_element_type=F32)


def dot_t(a, b):
    return lax.dot_general(a, b, (((1,), (1,)), ((), ())), preferred_element_type=F32)


def t_dot(a, b):
    return lax.dot_general(a, b, (((0,), (0,)), ((), ())), preferred_element_type=F32)


def normalise(x):
    c = x - jnp.mean(x, axis=-1, keepdims=True)
    v = jnp.mean(c * c, axis=-1, keepdims=True)
    r = lax.rsqrt(v + EPS)
    return c * r, r


def norm_back(n, r, dn):
    a = jnp.mean(dn, axis=-1, keepdims=True)
    b = jnp.mean(dn * n, axis=-1, keepdims=True)
    return (dn - a - n * b) * r


def gelu_parts(u):
    big = 0.5 * (1.0 + lax.erf(u * 0.7071067811865476))
    small = 0.3989422804014327 * jnp.exp(-0.5 * u * u)
    return big, small


def gelu_low(u):
    return (u * (0.5 * (1.0 + lax.erf(u * 0.7071067811865476)))).astype(BF16)


def softmax_rows(scores):
    m = jnp.max(scores, axis=-1, keepdims=True)
    e = jnp.exp(scores - m)
    return e * (1.0 / jnp.sum(e, axis=-1, keepdims=True))


def tie(value, *after):
    return lax.optimization_barrier((value,) + after)[0]


def load_rows(dims, p, img, txt, rows):
    rows[0:dims.patches, :] = img[p].astype(F32)
    rows[dims.ip:dims.ip + dims.caption, :] = txt[p].astype(F32)


def spec_whole(a):
    return pl.BlockSpec(a.shape, lambda *_: (0,) * a.ndim)


class Dims(NamedTuple):
    patches: int
    caption: int
    ip: int
    tp: int
    slab: int
    quarter: int
    local: int


GAIN1, SHIFT1, A_SCALE, A_BIAS, GAIN2, SHIFT2, F_SCALE, F_BIAS, H_GAIN, H_SHIFT = 0, 1, 2, 3, 4, 6, 8, 9, 11, 13


def vector(table, at, count=1):
    return table[at:at + count, :]


def copy_rows(dst, at, src, start, count):
    dst[at:at + count, :] = src[start:start + count, :]


def parts_of(dims):
    return 2 * HEAD_DIM, HEAD_DIM


def key_tail(dims, length):
    at = dims.patches // 16 * 16
    return ((0, dims.ip, at, dims.patches), (dims.ip, dims.slab, 0, length))


def hide(scores, start, limit):
    if start >= scores.shape[0]:
        return scores
    tail = scores[start:]
    at = start + lax.broadcasted_iota(jnp.int32, (tail.shape[0], 1), 0)
    tail = jnp.where(at < limit, tail, NEG)
    return tail if start == 0 else jnp.concatenate([scores[:start], tail], axis=0)


def split_pair(value):
    low = lax.broadcasted_iota(jnp.int32, (1, 128), 1) < HEAD_DIM
    zero = jnp.zeros_like(value)
    return jnp.concatenate([jnp.where(low, value, zero), jnp.where(low, zero, value)], axis=0)


def join_pair(value):
    low = lax.broadcasted_iota(jnp.int32, (1, 128), 1) < HEAD_DIM
    half = value.shape[0] // 2
    return jnp.where(low, value[:half], value[half:])


def softmax_keys(scores):
    e = jnp.exp(scores - jnp.max(scores, axis=0, keepdims=True))
    return e * (1.0 / jnp.sum(e, axis=0, keepdims=True))


def pair_weights(q, k, start, limit):
    return softmax_keys(hide(dot_t(k, split_pair(q)), start, limit))


def scaled(q):
    return q * jnp.asarray(HEAD_DIM ** -0.5, BF16)


def attend_tiles(dims, lens, quarter_at, qkv, mixed):
    tiles = mixed.shape[-1] // 128

    def one_pair(p, c):
        length = lens[quarter_at * dims.quarter + p]
        for lo, hi, start, limit in key_tail(dims, length):
            for g in range(tiles):
                q, k, v = [qkv[p, lo:hi, (t * tiles + g) * 128:(t * tiles + g + 1) * 128] for t in range(3)]
                w = pair_weights(scaled(q), k, start, limit).astype(BF16)
                mixed[p, lo:hi, g * 128:(g + 1) * 128] = join_pair(t_dot(w, v)).astype(BF16)
        return c

    lax.fori_loop(0, dims.quarter, one_pair, 0)


def attend_own_kernel(dims, order, lens, img, txt, vec, bias, wo, normed, qkv, rest, mixed, rows, w, b):
    i = pl.program_id(0)
    local = dims.local
    two, one_head = parts_of(dims)

    @pl.when(i == 0)
    def _():
        rows[...] = jnp.zeros_like(rows)
        w[...] = jnp.zeros_like(w)
        b[...] = jnp.zeros_like(b)
        for t in range(3):
            copy_rows(w, t * 2 * two, wo, t * local, local)
        b[0:1, 0:local] = bias[0:1, :]
        b[0:1, 4 * two:4 * two + local] = bias[1:2, :]

    def one_norm(p, c):
        load_rows(dims, p, img, txt, rows)
        n, _ = normalise(rows[...])
        normed[p] = (n * vector(vec, GAIN1) + vector(vec, SHIFT1)).astype(BF16)
        return c

    lax.fori_loop(0, dims.quarter, one_norm, 0)
    model = normed.shape[-1]
    proj = (dot_t(normed[...].reshape(dims.quarter * dims.slab, model), w[...]) + b[0:1, :]).astype(BF16)
    proj = proj.reshape(dims.quarter, dims.slab, 6 * two)
    for t in range(3):
        qkv[:, :, t * two:(t + 1) * two] = proj[:, :, 2 * t * two:(2 * t + 1) * two]
        rest[:, :, t * two:(t + 1) * two] = proj[:, :, (2 * t + 1) * two:(2 * t + 2) * two]
    attend_tiles(dims, lens, order[i], qkv, mixed)


def attend_own(dims, order, lens, img, txt, vec, bias, wo):
    model = img.shape[-1]
    pairs = 4 * dims.quarter
    block = lambda cols: pl.BlockSpec((dims.quarter, dims.slab, cols), lambda i, o, n: (i, 0, 0))
    shape = lambda cols: jax.ShapeDtypeStruct((pairs, dims.slab, cols), BF16)
    return pl.pallas_call(
        functools.partial(attend_own_kernel, dims),
        grid_spec=pltpu.PrefetchScalarGridSpec(
            num_scalar_prefetch=2,
            grid=(4,),
            in_specs=[
                pl.BlockSpec((dims.quarter, dims.patches, model), lambda i, o, n: (o[i], 0, 0)),
                pl.BlockSpec((dims.quarter, dims.caption, model), lambda i, o, n: (o[i], 0, 0)),
                spec_whole(vec), spec_whole(bias), spec_whole(wo),
            ],
            out_specs=[block(model), block(384), block(384), block(128)],
            scratch_shapes=[pltpu.VMEM((dims.slab, model), F32), pltpu.VMEM((768, model), BF16),
                            pltpu.VMEM((8, 768), F32)],
        ),
        out_shape=[shape(model), shape(384), shape(384), shape(128)],
        compiler_params=params(),
        cost_estimate=pl.CostEstimate(
            flops=1536 * pairs * dims.slab * model, bytes_accessed=30_000_000, transcendentals=0),
        name="attend_own",
    )(order, lens, img, txt, vec, bias, wo)


def attend_far_kernel(dims, order, lens, normed, rest, own, bias, wo, wf, qkv, mixed, keep, send, w, ow, b):
    i = pl.program_id(0)
    local = dims.local
    two, one_head = parts_of(dims)
    count = dims.quarter * dims.slab
    model = normed.shape[-1]

    @pl.when(i == 0)
    def _():
        w[...] = jnp.zeros_like(w)
        b[...] = jnp.zeros_like(b)
        for t in range(3):
            copy_rows(w, t * 2 * two, wf, t * local, two)
            copy_rows(w, t * 2 * two + two + one_head, wf, t * local + two, one_head)
        for t, at in ((0, 0), (1, 4 * two)):
            b[0:1, at:at + two] = bias[t:t + 1, 0:two]
            b[0:1, at + two + one_head:at + 2 * two] = bias[t:t + 1, two:]
        copy_rows(ow, 0, wo, 3 * local, two)
        copy_rows(ow, two, wf, 3 * local, two)
        copy_rows(ow, 2 * two, wo, 3 * local + two, one_head)
        copy_rows(ow, 2 * two + one_head, wf, 3 * local + two, one_head)

    proj = (dot_t(normed[...].reshape(count, model), w[...]) + b[0:1, :]).astype(BF16)
    proj = proj.reshape(dims.quarter, dims.slab, 6 * two)
    for t in range(3):
        at = 2 * t * two
        qkv[:, :, at:at + two] = proj[:, :, at:at + two]
        qkv[:, :, at + two:at + 2 * two] = proj[:, :, at + two:at + 2 * two] + rest[:, :, t * two:(t + 1) * two]
    attend_tiles(dims, lens, order[(i + 2) % 4], qkv, mixed)
    part = dot(own[...].reshape(count, two), ow[0:two, :])
    part = part + dot(mixed[...].reshape(count, 2 * two), ow[two:, :])
    part = part.astype(BF16).reshape(dims.quarter, dims.slab, model)

    @pl.when(i < 2)
    def _():
        send[...] = part

    @pl.when(i >= 2)
    def _():
        keep[...] = part


def attend_far(dims, order, lens, normed, rest, own, bias, wo, wf):
    model = normed.shape[-1]
    pairs = 4 * dims.quarter
    at = lambda i: (i + 2) % 4
    block = lambda cols, f: pl.BlockSpec((dims.quarter, dims.slab, cols), lambda i, o, n: (f(i), 0, 0))
    shape = lambda count, cols: jax.ShapeDtypeStruct((count, dims.slab, cols), BF16)
    return pl.pallas_call(
        functools.partial(attend_far_kernel, dims),
        grid_spec=pltpu.PrefetchScalarGridSpec(
            num_scalar_prefetch=2,
            grid=(4,),
            in_specs=[
                block(model, at), block(384, at), block(128, at),
                spec_whole(bias), spec_whole(wo), spec_whole(wf),
            ],
            out_specs=[
                block(768, at), block(256, at),
                block(model, lambda i: jnp.maximum(i - 2, 0)), block(model, lambda i: jnp.minimum(i, 1)),
            ],
            scratch_shapes=[pltpu.VMEM((768, model), BF16), pltpu.VMEM((384, model), BF16),
                            pltpu.VMEM((8, 768), F32)],
        ),
        out_shape=[
            shape(pairs, 768), shape(pairs, 256),
            shape(2 * dims.quarter, model), shape(2 * dims.quarter, model),
        ],
        compiler_params=params(),
        cost_estimate=pl.CostEstimate(
            flops=2304 * pairs * dims.slab * model, bytes_accessed=30_000_000, transcendentals=0),
        name="attend_far",
    )(order, lens, normed, rest, own, bias, wo, wf)


def residual_kernel(dims, order, keep, recv, img, txt, vec, attended, attn, expert, cls, rows):
    i = pl.program_id(0)
    ip = dims.ip

    @pl.when(i == 0)
    def _():
        rows[...] = jnp.zeros_like(rows)
        cls[...] = jnp.zeros_like(cls)

    load_rows(dims, 0, img, txt, rows)
    a = keep[0].astype(F32) + recv[0].astype(F32)
    x = rows[...] + vector(vec, A_SCALE) * (a + vector(vec, A_BIAS))
    n, _ = normalise(x)
    e_img = n[0:ip] * vector(vec, GAIN2) + vector(vec, SHIFT2)
    e_txt = n[ip:] * vector(vec, GAIN2 + 1) + vector(vec, SHIFT2 + 1)
    expert[0, 0:ip, :] = e_img.astype(BF16)
    expert[0, ip:, :] = e_txt.astype(BF16)
    for j, v in enumerate((x[0:1], x[ip:ip + 1], e_img[0:1], e_txt[0:1])):
        cls[j, pl.ds(i, 1), :] = v

    @pl.when(i < dims.quarter)
    def _():
        attended[0] = x
        attn[0] = a


def residual(dims, order, keep, recv, img, txt, vec):
    model = img.shape[-1]
    quarter = dims.quarter
    block = pl.BlockSpec((1, dims.slab, model), lambda i, o: (i, 0, 0))
    pair = lambda i, o: (o[i // quarter] * quarter + i % quarter, 0, 0)
    return pl.pallas_call(
        functools.partial(residual_kernel, dims),
        grid_spec=pltpu.PrefetchScalarGridSpec(
            num_scalar_prefetch=1,
            grid=(2 * quarter,),
            in_specs=[
                block, block,
                pl.BlockSpec((1, dims.patches, model), pair),
                pl.BlockSpec((1, dims.caption, model), pair),
                spec_whole(vec),
            ],
            out_specs=[
                pl.BlockSpec((1, dims.slab, model), lambda i, o: (jnp.minimum(i, quarter - 1), 0, 0)),
                pl.BlockSpec((1, dims.slab, model), lambda i, o: (jnp.minimum(i, quarter - 1), 0, 0)),
                block,
                pl.BlockSpec((4, 8, model), lambda i, o: (0, 0, 0)),
            ],
            scratch_shapes=[pltpu.VMEM((dims.slab, model), F32)],
        ),
        out_shape=[
            jax.ShapeDtypeStruct((quarter, dims.slab, model), F32),
            jax.ShapeDtypeStruct((quarter, dims.slab, model), F32),
            jax.ShapeDtypeStruct((2 * quarter, dims.slab, model), BF16),
            jax.ShapeDtypeStruct((4, 8, model), F32),
        ],
        compiler_params=params(),
        cost_estimate=pl.CostEstimate(flops=40_000_000, bytes_accessed=20_000_000, transcendentals=0),
        name="residual",
    )(order, keep, recv, img, txt, vec)


def expert_kernel(dims, seq, peer, own, img, txt, vec, up, up_bias, down,
                  act, dup, ddown, d_send, d_keep, x_send, x_keep, bias_grad, cot, ins, rows):
    ip, slab, quarter = dims.ip, dims.slab, dims.quarter
    i = pl.program_id(0)
    model = own.shape[-1]

    @pl.when(i == 0)
    def _():
        rows[...] = jnp.zeros_like(rows)
        bias_grad[...] = jnp.zeros_like(bias_grad)
        cot[...] = jnp.zeros_like(cot)
        ins[...] = peer[...]

    @pl.when(i == 1)
    def _():
        ins[...] = own[...]

    at = lax.broadcasted_iota(jnp.int32, (slab, 1), 0)
    inner = (at != 0) & (at != ip)

    def one(p, c):
        load_rows(dims, p, img, txt, rows)
        cot[0, pl.ds(8 * i + p, 1), :] = rows[0:1, :]
        cot[1, pl.ds(8 * i + p, 1), :] = rows[ip:ip + 1, :]
        ddown[p] = jnp.where(inner, rows[...] * vector(vec, F_SCALE), 0.0).astype(BF16)
        return c

    lax.fori_loop(0, quarter, one, 0)
    for m, lo, hi in ((0, 0, ip), (1, ip, slab)):
        count = quarter * (hi - lo)
        e = ins[:, lo:hi, :].reshape(count, model)
        u = dot(e, up[m]) + up_bias[m:m + 1]
        big, small = gelu_parts(u)
        a = (u * big).astype(BF16)
        act[:, lo:hi, :] = a.reshape(quarter, hi - lo, -1)
        slope = big + u * small
        d = dot(a, down[m]).astype(BF16).reshape(quarter, hi - lo, model)
        g = ddown[:, lo:hi, :].reshape(count, model)
        du = dot_t(g, down[m]) * slope
        bias_grad[m:m + 1, :] += jnp.sum(du, axis=0, keepdims=True)
        low = du.astype(BF16)
        dup[:, lo:hi, :] = low.reshape(quarter, hi - lo, -1)
        x = dot_t(low, up[m]).astype(BF16).reshape(quarter, hi - lo, model)

        @pl.when(i == 0)
        def _():
            d_send[:, lo:hi, :] = d
            x_send[:, lo:hi, :] = x

        @pl.when(i == 1)
        def _():
            d_keep[:, lo:hi, :] = d
            x_keep[:, lo:hi, :] = x


def experts(dims, name, half, seq, peer, own, img, txt, vec, up, up_bias, down):
    model = own.shape[-1]
    hidden = up.shape[-1]
    slab, quarter = dims.slab, dims.quarter
    fixed = pl.BlockSpec((quarter, slab, model), lambda i, o: (half, 0, 0))
    first = pl.BlockSpec((quarter, slab, model), lambda i, o: (0, 0, 0))
    step = lambda cols: pl.BlockSpec((quarter, slab, cols), lambda i, o: (i, 0, 0))
    shape = lambda n, cols: jax.ShapeDtypeStruct((n * quarter, slab, cols), BF16)
    return pl.pallas_call(
        functools.partial(expert_kernel, dims),
        grid_spec=pltpu.PrefetchScalarGridSpec(
            num_scalar_prefetch=1,
            grid=(2,),
            in_specs=[
                fixed, fixed,
                pl.BlockSpec((quarter, dims.patches, model), lambda i, o: (o[i], 0, 0)),
                pl.BlockSpec((quarter, dims.caption, model), lambda i, o: (o[i], 0, 0)),
                spec_whole(vec), spec_whole(up), spec_whole(up_bias), spec_whole(down),
            ],
            out_specs=[
                step(hidden), step(hidden), step(model),
                first, first, first, first,
                pl.BlockSpec((2, hidden), lambda i, o: (0, 0)),
                pl.BlockSpec((2, 16, model), lambda i, o: (0, 0, 0)),
            ],
            scratch_shapes=[pltpu.VMEM((quarter, slab, model), BF16), pltpu.VMEM((slab, model), F32)],
        ),
        out_shape=[
            shape(2, hidden), shape(2, hidden), shape(2, model),
            shape(1, model), shape(1, model), shape(1, model), shape(1, model),
            jax.ShapeDtypeStruct((2, hidden), F32),
            jax.ShapeDtypeStruct((2, 16, model), F32),
        ],
        compiler_params=params(),
        cost_estimate=pl.CostEstimate(
            flops=16 * quarter * slab * model * hidden, bytes_accessed=20_000_000, transcendentals=0),
        name=name,
    )(seq, peer, own, img, txt, vec, up, up_bias, down)


def expert_grads_kernel(dims, peer, own, act_a, dup_a, ddn_a, act_b, dup_b, ddn_b, ce, ca, cu, cd, out, acc):
    i = pl.program_id(0)

    def add(e, dup, ddn, act):
        for m, lo, hi in ((0, 0, dims.ip), (1, dims.ip, dims.slab)):
            count = dims.quarter * (hi - lo)
            flat = lambda ref: ref[:, lo:hi, :].reshape(count, -1)
            acc[m] += t_dot(flat(e), flat(dup))
            acc[2 + m] += t_dot(flat(ddn), flat(act))

    @pl.when(i == 0)
    def _():
        for m in range(2):
            acc[m] = t_dot(ce[m], cu[m])
            acc[2 + m] = t_dot(cd[m], ca[m])

    for j, refs in enumerate((
        (peer, dup_a, ddn_a, act_a), (own, dup_a, ddn_a, act_a),
        (peer, dup_b, ddn_b, act_b), (own, dup_b, ddn_b, act_b),
    )):
        @pl.when(i == j)
        def _():
            add(*refs)

    @pl.when(i == 3)
    def _():
        out[...] = acc[...].astype(BF16)


def expert_grads(dims, peer, own, act_a, dup_a, ddn_a, act_b, dup_b, ddn_b, ce, ca, cu, cd):
    model = own.shape[-1]
    hidden = act_a.shape[-1]
    slab, quarter = dims.slab, dims.quarter
    assert hidden == model
    half = pl.BlockSpec((quarter, slab, model), lambda i: (jnp.where(i < 2, 1, 0), 0, 0))
    first = pl.BlockSpec((quarter, slab, hidden), lambda i: (jnp.minimum(i, 1), 0, 0))
    last = pl.BlockSpec((quarter, slab, hidden), lambda i: (jnp.maximum(i - 2, 0), 0, 0))
    return pl.pallas_call(
        functools.partial(expert_grads_kernel, dims),
        grid=(4,),
        in_specs=[half, half, first, first, first, last, last, last] + [spec_whole(v) for v in (ce, ca, cu, cd)],
        out_specs=pl.BlockSpec((4, model, hidden), lambda i: (0, 0, 0)),
        scratch_shapes=[pltpu.VMEM((4, model, hidden), F32)],
        out_shape=jax.ShapeDtypeStruct((4, model, hidden), BF16),
        compiler_params=params(),
        cost_estimate=pl.CostEstimate(
            flops=16 * quarter * slab * model * hidden, bytes_accessed=40_000_000, transcendentals=0),
        name="expert_grads",
    )(peer, own, act_a, dup_a, ddn_a, act_b, dup_b, ddn_b, ce, ca, cu, cd)


def own_row(dims, r, p):
    return 8 * (r // 2) + dims.quarter * (r % 2) + p


def class_forward_kernel(dims, near, far, up, up_bias, down, out, rows):
    for m in range(2):
        e = jnp.concatenate([near[2 + m], far[2 + m]], axis=0).astype(BF16)
        rows[m] = e
        u = dot(e, up[m]) + up_bias[m:m + 1]
        out[m] = dot(gelu_low(u), down[m])


def class_forward(dims, near, far, up, up_bias, down):
    shape = (2, 16, near.shape[-1])
    return pl.pallas_call(
        functools.partial(class_forward_kernel, dims),
        out_shape=[jax.ShapeDtypeStruct(shape, F32), jax.ShapeDtypeStruct(shape, BF16)],
        compiler_params=params(),
        cost_estimate=pl.CostEstimate(flops=200_000_000, bytes_accessed=5_000_000, transcendentals=0),
        name="class_forward",
    )(near, far, up, up_bias, down)


def class_final_kernel(dims, order, near, far, d0, d1, d2, d3, vec, out):
    q = dims.quarter
    for m in range(2):
        out[m] = jnp.zeros(out.shape[1:], F32)
        for r in range(4):
            half, at = (near, far)[r // 2], q * (r % 2)
            for p in range(q):
                rows = [d[m, own_row(dims, s, p):own_row(dims, s, p) + 1, :]
                        for d, s in ((d0, r), (d1, r ^ 2), (d2, r ^ 1), (d3, r ^ 3))]
                total = (rows[0] + rows[1]) + (rows[2] + rows[3])
                x = half[m, at + p:at + p + 1, :] + vector(vec, F_SCALE) * (total + vector(vec, F_BIAS + m))
                out[m, pl.ds(4 * order[r] + p, 1), :] = x


def class_final(dims, order, near, far, parts, vec):
    shape = (2, 16, near.shape[-1])
    args = (near, far) + tuple(parts) + (vec,)
    return pl.pallas_call(
        functools.partial(class_final_kernel, dims),
        grid_spec=pltpu.PrefetchScalarGridSpec(
            num_scalar_prefetch=1, grid=(1,),
            in_specs=[spec_whole(v) for v in args],
            out_specs=pl.BlockSpec(shape, lambda i, o: (0, 0, 0)),
        ),
        out_shape=jax.ShapeDtypeStruct(shape, F32),
        compiler_params=params(),
        cost_estimate=pl.CostEstimate(flops=1_000_000, bytes_accessed=1_000_000, transcendentals=0),
        name="class_final",
    )(order, *args)


def class_back_kernel(dims, order, e, cot_a, cot_b, dclass, vec, up, up_bias, down,
                      act, dup, ddown, dexp, bias_grad, dcls, rows):
    q = dims.quarter
    rows[...] = jnp.zeros_like(rows)
    dcls[...] = jnp.zeros_like(dcls)
    for m in range(2):
        for r in range(4):
            cot, base = (cot_b, cot_a)[r % 2], 8 * (1 - r // 2)
            for p in range(q):
                d = dclass[m, pl.ds(4 * order[r] + p, 1), :]
                at = own_row(dims, r, p)
                rows[m, at:at + 1, :] = cot[m, base + p:base + p + 1, :] + d
                if r == 0:
                    dcls[p, m:m + 1, :] = d
        u = dot(e[m], up[m]) + up_bias[m:m + 1]
        big, small = gelu_parts(u)
        act[m] = (u * big).astype(BF16)
        g = (rows[m] * vector(vec, F_SCALE)).astype(BF16)
        ddown[m] = g
        du = dot_t(g, down[m]) * (big + u * small)
        bias_grad[m:m + 1, :] = jnp.sum(du, axis=0, keepdims=True)
        low = du.astype(BF16)
        dup[m] = low
        dexp[m] = dot_t(low, up[m])


def class_back(dims, order, e, cot_a, cot_b, dclass, vec, up, up_bias, down):
    hidden, model = up.shape[-1], e.shape[-1]
    args = (e, cot_a, cot_b, dclass, vec, up, up_bias, down)
    shapes = [((2, 16, hidden), BF16), ((2, 16, hidden), BF16), ((2, 16, model), BF16), ((2, 16, model), F32),
              ((2, hidden), F32), ((dims.quarter, 8, model), F32)]
    return pl.pallas_call(
        functools.partial(class_back_kernel, dims),
        grid_spec=pltpu.PrefetchScalarGridSpec(
            num_scalar_prefetch=1, grid=(1,),
            in_specs=[spec_whole(v) for v in args],
            out_specs=[pl.BlockSpec(s, lambda i, o, n=len(s): (0,) * n) for s, _ in shapes],
            scratch_shapes=[pltpu.VMEM((2, 16, model), F32)],
        ),
        out_shape=[jax.ShapeDtypeStruct(s, t) for s, t in shapes],
        compiler_params=params(),
        cost_estimate=pl.CostEstimate(flops=300_000_000, bytes_accessed=5_000_000, transcendentals=0),
        name="class_back",
    )(order, *args)


def contrast_kernel(dims, total, at, blocks, vec, weight, scale,
                    head_in, dproj, dcls, gains, shifts, scalars, cls, back):
    me = at[0]
    span = blocks[0].shape[0]
    for k, block in enumerate(blocks):
        for j in range(span):
            for m in range(2):
                cls[m, pl.ds(pl.multiple_of(16 * (me ^ (k * span + j)), 16), 16), :] = block[j, m]
    n_rows = cls.shape[1]
    sharp = jnp.exp(scale[...])
    col_at = lax.broadcasted_iota(jnp.int32, (1, n_rows), 1)
    row_at = lax.broadcasted_iota(jnp.int32, (n_rows, 1), 0)
    col_ok = (col_at % 4) < dims.quarter
    row_ok = (row_at % 4) < dims.quarter
    normal, inverse, proj, unit, embed = [], [], [], [], []
    for m in range(2):
        n, r = normalise(cls[m])
        h = (n * vector(vec, H_GAIN + m) + vector(vec, H_SHIFT + m)).astype(BF16)
        head_in[m] = h
        y = dot(h, weight[m])
        u = lax.rsqrt(jnp.sum(y * y, axis=-1, keepdims=True) + 1e-6)
        normal.append(n)
        inverse.append(r)
        proj.append(y)
        unit.append(u)
        embed.append((y * u).astype(BF16))
    ok = row_ok & col_ok
    logits = sharp * dot_t(embed[0], embed[1])
    masked = jnp.where(ok, logits, -1e30)
    row_max = jnp.max(masked, axis=1, keepdims=True)
    row_lse = row_max + jnp.log(jnp.sum(jnp.exp(masked - row_max), axis=1, keepdims=True))
    col_max = jnp.max(masked, axis=0, keepdims=True)
    col_lse = col_max + jnp.log(jnp.sum(jnp.exp(masked - col_max), axis=0, keepdims=True))
    same = (row_at == col_at) & ok
    both = jnp.exp(masked - row_lse) + jnp.exp(masked - col_lse)
    dlogits = jnp.where(ok, jnp.where(same, both - 2.0, both) * (1.0 / (2 * total)), 0.0)
    diagonal = jnp.sum(jnp.where(same, logits, 0.0), axis=1, keepdims=True)
    rows = jnp.where(row_ok, row_lse - 2.0 * diagonal, 0.0)
    cols = jnp.where(col_ok, col_lse, 0.0)
    loss = (jnp.sum(rows, axis=0, keepdims=True) + jnp.sum(cols, axis=1, keepdims=True)) * (1.0 / (2 * total))
    slope = jnp.sum(jnp.sum(dlogits * logits, axis=1, keepdims=True), axis=0, keepdims=True)
    scalars[0:1, :] = jnp.broadcast_to(loss, (1, 128))
    scalars[1:2, :] = jnp.broadcast_to(slope, (1, 128))
    high = lax.Precision.HIGHEST
    wide = [e.astype(F32) for e in embed]
    dembed = [
        sharp * jnp.dot(dlogits, wide[1], precision=high, preferred_element_type=F32),
        sharp * lax.dot_general(dlogits, wide[0], (((0,), (0,)), ((), ())), precision=high,
                                preferred_element_type=F32),
    ]
    for m in range(2):
        u, y, d = unit[m], proj[m], dembed[m]
        dp = (u * d - u * u * u * y * jnp.sum(y * d, axis=-1, keepdims=True)).astype(BF16)
        dproj[m] = dp
        dh = dot_t(dp, weight[m])
        gains[m:m + 1, :] = jnp.sum(dh * normal[m], axis=0, keepdims=True)
        shifts[m:m + 1, :] = jnp.sum(dh, axis=0, keepdims=True)
        back[m] = norm_back(normal[m], inverse[m], dh * vector(vec, H_GAIN + m))
        dcls[m] = back[m, pl.ds(pl.multiple_of(16 * me, 16), 16), :]


def contrast(dims, total, at, blocks, vec, weight, scale):
    model = weight.shape[1]
    rows = 16 * len(blocks) * blocks[0].shape[0]
    args = tuple(blocks) + (vec, weight, scale)
    shapes = [((2, rows, model), BF16), ((2, rows, weight.shape[2]), BF16), ((2, 16, model), F32),
              ((2, model), F32), ((2, model), F32), ((2, 128), F32)]

    def kernel(at, *refs):
        contrast_kernel(dims, total, at, refs[:len(blocks)], *refs[len(blocks):])

    return pl.pallas_call(
        kernel,
        grid_spec=pltpu.PrefetchScalarGridSpec(
            num_scalar_prefetch=1, grid=(1,),
            in_specs=[spec_whole(v) for v in args],
            out_specs=[pl.BlockSpec(s, lambda i, o, n=len(s): (0,) * n) for s, _ in shapes],
            scratch_shapes=[pltpu.VMEM((2, rows, model), F32)] * 2,
        ),
        out_shape=[jax.ShapeDtypeStruct(s, t) for s, t in shapes],
        compiler_params=params(),
        cost_estimate=pl.CostEstimate(flops=1_000_000_000, bytes_accessed=5_000_000, transcendentals=0),
        name="contrast",
    )(at, *args)


def contrast_large(dims, total, at, blocks, vec, weight, scale):
    model = weight.shape[1]
    held = jnp.concatenate(blocks)
    held = held[jnp.arange(held.shape[0]) ^ at[0]]
    rows = jnp.asarray([r for r in range(16) if r % 4 < dims.quarter])
    cls = jnp.transpose(held[:, :, rows], (1, 0, 2, 3)).reshape(2, -1, model)
    gain, shift = vec[H_GAIN:H_GAIN + 2, None], vec[H_SHIFT:H_SHIFT + 2, None]
    n, r = normalise(cls)
    head_in = (n * gain + shift).astype(BF16)
    proj = jnp.einsum("mrc,mce->mre", head_in, weight, preferred_element_type=F32)
    unit = lax.rsqrt(jnp.sum(proj * proj, axis=-1, keepdims=True) + 1e-6)
    embed = (proj * unit).astype(BF16)
    sharp = jnp.exp(scale[0, 0])
    logits = sharp * dot_t(embed[0], embed[1])
    row_lse = jax.nn.logsumexp(logits, axis=1, keepdims=True)
    col_lse = jax.nn.logsumexp(logits, axis=0, keepdims=True)
    dlogits = jnp.exp(logits - row_lse) + jnp.exp(logits - col_lse) - 2.0 * jnp.eye(total, dtype=F32)
    dlogits = dlogits / (2 * total)
    loss = (jnp.sum(row_lse) + jnp.sum(col_lse) - 2.0 * jnp.trace(logits)) / (2 * total)
    slope = jnp.sum(dlogits * logits)
    high = lax.Precision.HIGHEST
    wide = embed.astype(F32)
    dembed = sharp * jnp.stack([
        jnp.dot(dlogits, wide[1], precision=high, preferred_element_type=F32),
        jnp.dot(dlogits.T, wide[0], precision=high, preferred_element_type=F32)])
    dproj = (unit * dembed - unit ** 3 * proj * jnp.sum(proj * dembed, axis=-1, keepdims=True)).astype(BF16)
    dh = jnp.einsum("mre,mce->mrc", dproj, weight, preferred_element_type=F32)
    back = norm_back(n, r, dh * gain)
    pairs = 4 * dims.quarter
    own = lax.dynamic_slice_in_dim(back, at[0] * pairs, pairs, axis=1)
    dcls = jnp.zeros((2, 16, model), F32).at[:, rows].set(own)
    scalars = jnp.broadcast_to(jnp.stack([loss, slope])[:, None], (2, 128))
    return head_in, dproj, dcls, jnp.sum(dh * n, axis=1), jnp.sum(dh, axis=1), scalars


def own_pair(rows_of):
    return lambda i, o: (o[0] * rows_of + i, 0, 0)


def own_call(kernel, dims, name, order, blocks, img, txt, others, outs, scratch):
    model = img.shape[-1]
    block = pl.BlockSpec((1, dims.slab, model), lambda i, o: (i, 0, 0))
    specs = {
        "slab": (block, (dims.quarter, dims.slab, model)),
        "img": (pl.BlockSpec((1, dims.patches, model), lambda i, o: (i, 0, 0)), (dims.quarter, dims.patches, model)),
        "txt": (pl.BlockSpec((1, dims.caption, model), lambda i, o: (i, 0, 0)), (dims.quarter, dims.caption, model)),
        "sums": (pl.BlockSpec((8, model), lambda i, o: (0, 0)), (8, model)),
    }
    return pl.pallas_call(
        functools.partial(kernel, dims),
        grid_spec=pltpu.PrefetchScalarGridSpec(
            num_scalar_prefetch=1,
            grid=(dims.quarter,),
            in_specs=[block] * len(blocks) + [
                pl.BlockSpec((1, dims.patches, model), own_pair(dims.quarter)),
                pl.BlockSpec((1, dims.caption, model), own_pair(dims.quarter)),
            ] + [spec_whole(v) for v in others],
            out_specs=[specs[kind][0] for kind, _ in outs],
            scratch_shapes=[pltpu.VMEM((dims.slab, model), F32)] * scratch,
        ),
        out_shape=[jax.ShapeDtypeStruct(specs[kind][1], dtype) for kind, dtype in outs],
        compiler_params=params(),
        cost_estimate=pl.CostEstimate(flops=40_000_000, bytes_accessed=15_000_000, transcendentals=0),
        name=name,
    )(order, *blocks, img, txt, *others)


def start_own(rows, sums):
    @pl.when(pl.program_id(0) == 0)
    def _():
        rows[...] = jnp.zeros_like(rows)
        sums[...] = jnp.zeros_like(sums)


def add_class(dims, dcls, rows):
    i = pl.program_id(0)
    rows[0:1, :] += dcls[i, 0:1, :]
    rows[dims.ip:dims.ip + 1, :] += dcls[i, 1:2, :]


def final_kernel(dims, order, keep, recv, far, attended, img, txt, dcls, vec, fin_img, fin_txt, sums, rows):
    start_own(rows, sums)
    load_rows(dims, 0, img, txt, rows)
    add_class(dims, dcls, rows)
    for m, lo, hi in ((0, 0, dims.ip), (1, dims.ip, dims.slab)):
        b = keep[0, lo:hi].astype(F32) + recv[0, lo:hi].astype(F32) + far[0, lo:hi].astype(F32)
        b = b + vector(vec, F_BIAS + m)
        f = attended[0, lo:hi, :] + vector(vec, F_SCALE) * b
        if m == 0:
            fin_img[0] = f[0:dims.patches].astype(BF16)
        else:
            fin_txt[0] = f[0:dims.caption].astype(BF16)
        g = rows[lo:hi, :]
        sums[0:1, :] += jnp.sum(g * b, axis=0, keepdims=True)
        sums[1 + m:2 + m, :] += jnp.sum(g, axis=0, keepdims=True) * vector(vec, F_SCALE)


def final_rows(dims, order, keep, recv, far, attended, img, txt, dcls, vec):
    return own_call(final_kernel, dims, "final_rows", order, (keep, recv, far, attended), img, txt,
                    (dcls, vec), (("img", BF16), ("txt", BF16), ("sums", F32)), 1)


def norm_two_kernel(dims, order, keep, recv, far, attended, a_keep, a_recv, img, txt, dcls, x0, x1, x2, x3,
                    vec, dattended, dattn, sums, rows, ups):
    i = pl.program_id(0)
    start_own(rows, sums)
    load_rows(dims, 0, img, txt, rows)
    add_class(dims, dcls, rows)
    ups[...] = keep[0].astype(F32) + recv[0].astype(F32) + far[0].astype(F32)
    for m, at in ((0, 0), (1, dims.ip)):
        extra = [x[m, pl.ds(own_row(dims, r, 0) + i, 1), :] for x, r in ((x0, 0), (x1, 2), (x2, 1), (x3, 3))]
        ups[at:at + 1, :] += (extra[0] + extra[1]) + (extra[2] + extra[3])
    for m, lo, hi in ((0, 0, dims.ip), (1, dims.ip, dims.slab)):
        n, r = normalise(attended[0, lo:hi, :])
        dy = ups[lo:hi, :]
        sums[m:m + 1, :] += jnp.sum(dy * n, axis=0, keepdims=True)
        sums[2 + m:3 + m, :] += jnp.sum(dy, axis=0, keepdims=True)
        d = rows[lo:hi, :] + norm_back(n, r, dy * vector(vec, GAIN2 + m))
        dattended[0, lo:hi, :] = d
        sd = d * vector(vec, A_SCALE)
        dattn[0, lo:hi, :] = sd.astype(BF16)
        a = a_keep[0, lo:hi, :].astype(F32) + a_recv[0, lo:hi, :].astype(F32) + vector(vec, A_BIAS)
        sums[4:5, :] += jnp.sum(d * a, axis=0, keepdims=True)
        sums[5:6, :] += jnp.sum(sd, axis=0, keepdims=True)


def norm_two(dims, order, keep, recv, far, attended, a_keep, a_recv, img, txt, dcls, parts, vec):
    return own_call(norm_two_kernel, dims, "norm_two", order, (keep, recv, far, attended, a_keep, a_recv), img, txt,
                    (dcls,) + tuple(parts) + (vec,), (("slab", F32), ("slab", BF16), ("sums", F32)), 2)


def norm_one_kernel(dims, order, keep, recv, dattended, img, txt, vec, d_img, d_txt, sums, rows):
    start_own(rows, sums)
    load_rows(dims, 0, img, txt, rows)
    n, r = normalise(rows[...])
    dy = keep[0].astype(F32) + recv[0].astype(F32)
    sums[0:1, :] += jnp.sum(dy * n, axis=0, keepdims=True)
    sums[1:2, :] += jnp.sum(dy, axis=0, keepdims=True)
    d = dattended[0] + norm_back(n, r, dy * vector(vec, GAIN1))
    d_img[0] = d[0:dims.patches].astype(BF16)
    d_txt[0] = d[dims.ip:dims.ip + dims.caption].astype(BF16)


def norm_one(dims, order, keep, recv, dattended, img, txt, vec):
    return own_call(norm_one_kernel, dims, "norm_one", order, (keep, recv, dattended), img, txt,
                    (vec,), (("img", BF16), ("txt", BF16), ("sums", F32)), 1)


def attend_back_kernel(dims, far, carry, order, lens, d_own, d_peer, normed, qkv, mixed, wq, wo, wf, *refs):
    if not far:
        prior_keep, prior_send, *refs = refs
    if carry and far:
        fin_img, up_keep, up_send, z_sum, *refs = refs
    elif carry:
        fin_img, fin_txt, grad_f, z_sum, *refs = refs
    keep, send, grad, *refs = refs
    if far:
        grad_rest, *refs = refs
    col_sums, *refs = refs
    if carry:
        near_img, *refs = refs
        if not far:
            near_txt, *refs = refs
        x_sum, z_out, *refs, from_side, from_z, send_sem, recv_sem = refs
    dattn, dmixed, dqkv, acc, w, ow = refs
    i = pl.program_id(0)
    copies = []
    if carry:
        here = Place()
        last = dims.quarter - 1
        own_block = lambda j: pl.ds(pl.multiple_of((2 * j + here.x) * from_side.shape[1], 16), from_side.shape[1])
        side_block = lambda j: pl.ds(pl.multiple_of((2 * j + 1 - here.x) * from_side.shape[1], 16), from_side.shape[1])
        to_near = [(fin_img.at[pl.ds(0, last)], near_img)] if far else [
            (fin_img.at[pl.ds(last, 1)], near_img), (fin_txt, near_txt)]
        to_side = [(up_send.at[j] if far else grad_f.at[side_block(j)], from_side.at[j]) for j in range(4)]
        for (src, dst), device in ([(v, here.near) for v in to_near] + [(v, here.side) for v in to_side] + [
                ((z_sum.at[(here.z + k) % 4], from_z.at[k - 1]), here.along[k - 1]) for k in range(1, 4)]):
            copies.append(remote(src, dst, send_sem, recv_sem, len(copies), device))

        @pl.when(i == 0)
        def _():
            meet([here.near, here.side] + here.along)
            for copy in copies:
                copy.start()

    slab, quarter, local = dims.slab, dims.quarter, dims.local
    two, one_head = parts_of(dims)
    tiles = 2 if far else 1
    width = tiles * two
    count = quarter * slab
    model = normed.shape[-1]

    @pl.when(i == 0)
    def _():
        dattn[...] = d_own[...]
        acc[...] = jnp.zeros_like(acc)
        col_sums[...] = jnp.zeros_like(col_sums)
        for t in range(4):
            dst, at = (w, t * width) if t < 3 else (ow, 0)
            own, start = (wq, t * local) if t < 3 else (wo, 0)
            if far:
                copy_rows(dst, at, wf, t * local, two)
                copy_rows(dst, at + two, own, start + two, one_head)
                copy_rows(dst, at + two + one_head, wf, t * local + two, one_head)
            else:
                copy_rows(dst, at, own, start, two)

    @pl.when(i == 1)
    def _():
        dattn[...] = d_peer[...]

    d_rows = dattn[...].reshape(count, model)
    dmixed[...] = dot_t(d_rows, ow[...]).astype(BF16).reshape(quarter, slab, width)

    def one_pair(p, c):
        whose = here.quarter(0, i) if carry else order[2 * i]
        length = lens[whose * quarter + p]
        for lo, hi, start, limit in key_tail(dims, length):
            for g in range(tiles):
                at = [slice((t * tiles + g) * 128, (t * tiles + g + 1) * 128) for t in range(3)]
                q, k, v = [qkv[p, lo:hi, c] for c in at]
                q = scaled(q)
                qq = split_pair(q)
                dd = split_pair(dmixed[p, lo:hi, g * 128:(g + 1) * 128])
                w_ = softmax_keys(hide(dot_t(k, qq), start, limit))
                dw = dot_t(v, dd)
                dqkv[p, lo:hi, at[2]] = dot(w_.astype(BF16), dd).astype(BF16)
                ds = (w_ * (dw - jnp.sum(w_ * dw, axis=0, keepdims=True))).astype(BF16)
                dqkv[p, lo:hi, at[1]] = dot(ds, qq).astype(BF16)
                dqkv[p, lo:hi, at[0]] = (join_pair(t_dot(ds, k)) * HEAD_DIM ** -0.5).astype(BF16)
        return c

    lax.fori_loop(0, quarter, one_pair, 0)
    dp = dqkv[...].reshape(count, 3 * width)
    part = dot(dp, w[...])
    acc[:, 0:3 * width] += t_dot(normed[...].reshape(count, model), dp)
    acc[:, 3 * width:] += t_dot(d_rows, mixed[...].reshape(count, width))
    col_sums[...] += jnp.sum(dp.astype(F32), axis=0, keepdims=True)

    @pl.when(i == 0)
    def _():
        prior = 0.0 if far else prior_keep[...].reshape(count, model).astype(F32)
        keep[...] = (part + prior).astype(BF16).reshape(quarter, slab, model)

    @pl.when(i == 1)
    def _():
        prior = 0.0 if far else prior_send[...].reshape(count, model).astype(F32)
        send[...] = (part + prior).astype(BF16).reshape(quarter, slab, model)
        for t in range(4):
            grad[:, t * two:(t + 1) * two] = acc[:, t * width:t * width + two].astype(BF16)
            if far:
                at = t * width + two
                to = 4 * two + t * one_head
                grad[:, to:to + one_head] = acc[:, at + one_head:at + two].astype(BF16)
                grad_rest[:, t * one_head:(t + 1) * one_head] = acc[:, at:at + one_head].astype(BF16)
        for copy in copies:
            copy.wait()
        if carry:
            for j in range(4):
                own = up_keep[j] if far else grad_f[own_block(j), :]
                x_sum[j] = (own.astype(F32) + from_side[j].astype(F32)).astype(BF16)
            total = z_sum[here.z].astype(F32)
            for k in range(3):
                total = total + from_z[k].astype(F32)
            z_out[...] = total


def attend_back(dims, far, order, lens, d_own, d_peer, normed, qkv, mixed, wq, wo, wf, prior=(), carry=()):
    model = normed.shape[-1]
    slab, quarter = dims.slab, dims.quarter
    width = 256 if far else 128
    one = pl.BlockSpec((quarter, slab, model), lambda i, o, n: (0, 0, 0))
    stride = normed.shape[0] // (2 * quarter)
    step = lambda cols: pl.BlockSpec((quarter, slab, cols), lambda i, o, n: (stride * i, 0, 0))
    held = pl.BlockSpec(memory_space=pltpu.VMEM)
    away = pl.BlockSpec(memory_space=pl.ANY)
    grads = (768, 256) if far else (512,)
    specs = [one, one] + [pl.BlockSpec((model, n), lambda i, o, n_: (0, 0)) for n in grads]
    specs += [pl.BlockSpec((1, 3 * width), lambda i, o, n: (0, 0))]
    shapes = [
        jax.ShapeDtypeStruct((quarter, slab, model), BF16),
        jax.ShapeDtypeStruct((quarter, slab, model), BF16),
    ] + [jax.ShapeDtypeStruct((model, n), BF16) for n in grads] + [jax.ShapeDtypeStruct((1, 3 * width), F32)]
    scratch = [
        pltpu.VMEM((quarter, slab, model), BF16),
        pltpu.VMEM((quarter, slab, width), BF16),
        pltpu.VMEM((quarter, slab, 3 * width), BF16),
        pltpu.VMEM((model, 4 * width), F32),
        pltpu.VMEM((3 * width, model), BF16),
        pltpu.VMEM((width, model), BF16),
    ]
    how = params()
    if carry:
        shapes.append(jax.ShapeDtypeStruct((quarter - 1 if far else 1, dims.patches, model), BF16))
        specs.append(away)
        if not far:
            shapes.append(jax.ShapeDtypeStruct((quarter, dims.caption, model), BF16))
            specs.append(away)
        hidden = carry[-1].shape[-1]
        piece = (2, model // 8, hidden)
        side = (4,) + piece if far else (4, model // 8, model)
        shapes += [jax.ShapeDtypeStruct(side, BF16), jax.ShapeDtypeStruct(piece, F32)]
        specs += [held, held]
        scratch += [pltpu.VMEM(side, BF16), pltpu.VMEM((3,) + piece, BF16),
                    pltpu.SemaphoreType.DMA((9,)), pltpu.SemaphoreType.DMA((9,))]
        how = params(collective_id=4 if far else 5, has_side_effects=True)
    return pl.pallas_call(
        functools.partial(attend_back_kernel, dims, far, bool(carry)),
        grid_spec=pltpu.PrefetchScalarGridSpec(
            num_scalar_prefetch=2,
            grid=(2,),
            in_specs=[one, one, step(model), step(3 * width), step(width), spec_whole(wq), spec_whole(wo),
                      spec_whole(wf)] + [one] * len(prior) + [held] * len(carry),
            out_specs=specs,
            scratch_shapes=scratch,
        ),
        out_shape=shapes,
        compiler_params=how,
        cost_estimate=pl.CostEstimate(
            flops=32 * quarter * slab * model * width, bytes_accessed=20_000_000, transcendentals=0),
        name="attend_back_far" if far else "attend_back_own",
    )(order, lens, d_own, d_peer, normed, qkv, mixed, wq, wo, wf, *prior, *carry)


def swap(value, axis, bit):
    size = lax.axis_size(axis)
    return lax.ppermute(value, axis, [(j, j ^ bit) for j in range(size)])


def to_core(value):
    return swap(value, "mp", 1)


def to_y(value):
    return swap(value, "mp", 2)


def from_others(value, axis, first, count):
    return [value] + [swap(value, axis, k * first) for k in range(1, count)]


def add_tree(parts):
    while len(parts) > 1:
        parts = [a + b for a, b in zip(parts[::2], parts[1::2])]
    return parts[0]


def sum_over(value, axis):
    first = 1
    while first < lax.axis_size(axis):
        count = min(8, lax.axis_size(axis) // first)
        value = add_tree(from_others(value, axis, first, count))
        first *= count
    return value


def gather_batch(value):
    parts = [value]
    first = 1
    size = lax.axis_size("batch")
    while first < size:
        count = min(8, size // first)
        whole = jnp.concatenate(parts) if len(parts) > 1 else parts[0]
        parts = from_others(whole, "batch", first, count)
        first *= count
    return parts


def gather_rows(own, me):
    near = jnp.stack([own, to_y(own)])
    far = to_core(near)
    out = jnp.zeros((4,) + own.shape, own.dtype)
    for r, value in enumerate((near[0], near[1], far[0], far[1])):
        out = lax.dynamic_update_slice(out, value[None], (me ^ ORDER[r],) + (0,) * own.ndim)
    return out.reshape((4 * own.shape[0],) + own.shape[1:])


def add_low(a, b):
    return (a.astype(F32) + b.astype(F32)).astype(BF16)


MESH = pl.DeviceIdType.MESH


class Place:
    def __init__(self):
        self.b, self.m = lax.axis_index("batch"), lax.axis_index("mp")
        self.z, self.x = self.b // 2, self.b % 2
        self.y, self.c = self.m // 2, self.m % 2
        self.core = (self.b, 2 * self.y + 1 - self.c)
        self.near = (self.b, 2 * (1 - self.y) + self.c)
        self.across = (self.b, 2 * (1 - self.y) + 1 - self.c)
        self.side = (2 * self.z + 1 - self.x, self.m)
        self.along = [(2 * ((self.z + k) % 4) + self.x, self.m) for k in range(1, 4)]
        self.batch = [((self.b + k) % 8, self.m) for k in range(1, 8)]

    def quarter(self, far_y, far_core):
        return 2 * ((self.y + far_y) % 2) + (self.c + far_core) % 2


def meet(peers):
    barrier = pltpu.get_barrier_semaphore()
    for peer in peers:
        pl.semaphore_signal(barrier, inc=1, device_id=peer, device_id_type=MESH)
    pl.semaphore_wait(barrier, len(peers))


def remote(src, dst, send_sem, recv_sem, at, device):
    return pltpu.make_async_remote_copy(
        src_ref=src, dst_ref=dst, send_sem=send_sem.at[at], recv_sem=recv_sem.at[at],
        device_id=device, device_id_type=MESH)


def front_kernel(dims, lens, img, txt, vec, bias, own_w, own_o,
                 normed, qkv, mixed, qkv_far, mixed_far, far_w, attended, attn, expert, expert_peer, cls, cls_peer,
                 rows, w, w2, ow, b, wf, far_bias, n_all, rest, m_all, m_far, q_own, q_far, a_send, a_recv, e_send, c_recv,
                 local_sem, send_sem, recv_sem):
    here = Place()
    i = pl.program_id(0)
    local, quarter, slab, ip = dims.local, dims.quarter, dims.slab, dims.ip
    two, one_head = parts_of(dims)
    count = quarter * slab
    model = img.shape[-1]
    at = i % 4
    whose = here.quarter(at % 2, 1 - at // 2)
    sent_w = [remote(own_w, wf.at[pl.ds(0, 3 * local)], send_sem, recv_sem, 0, here.near),
              remote(own_o, wf.at[pl.ds(3 * local, local)], send_sem, recv_sem, 1, here.near),
              remote(bias, far_bias, send_sem, recv_sem, 2, here.near)]
    sent_a = [remote(a_send.at[j], a_recv.at[j], send_sem, recv_sem, 3 + j, here.core) for j in range(2)]
    sent_e = [remote(e_send.at[j], expert_peer.at[j], send_sem, recv_sem, 5 + j, here.core) for j in range(2 * quarter)]
    sent_c = remote(cls, c_recv, send_sem, recv_sem, 5 + 2 * quarter, here.core)
    keep_w = pltpu.make_async_copy(wf, far_w, local_sem.at[0])
    keep_e = [pltpu.make_async_copy(e_send.at[j], expert.at[j], local_sem.at[1 + j]) for j in range(2 * quarter)]

    @pl.when(i == 0)
    def _():
        meet([here.core, here.near])
        for copy in sent_w:
            copy.start()
        rows[...] = jnp.zeros_like(rows)
        b[...] = jnp.zeros_like(b)
        w[...] = jnp.zeros_like(w)
        cls[...] = jnp.zeros_like(cls)
        for t in range(3):
            copy_rows(w, t * 2 * two, own_w, t * local, local)
        b[0:1, 0:local] = bias[0:1, :]
        b[0:1, 4 * two:4 * two + local] = bias[1:2, :]

    def project(weights):
        proj = dot_t(n_all[at].reshape(count, model), weights[...]) + b[0:1, :]
        return proj.astype(BF16).reshape(quarter, slab, 6 * two)

    @pl.when(i < 4)
    def _():
        def one_norm(p, c):
            load_rows(dims, p, img, txt, rows)
            n, _ = normalise(rows[...])
            n_all[at, p] = (n * vector(vec, GAIN1) + vector(vec, SHIFT1)).astype(BF16)
            return c

        lax.fori_loop(0, quarter, one_norm, 0)
        proj = project(w)
        for t in range(3):
            q_own[:, :, t * two:(t + 1) * two] = proj[:, :, 2 * t * two:(2 * t + 1) * two]
            rest[at, :, :, t * two:(t + 1) * two] = proj[:, :, (2 * t + 1) * two:(2 * t + 2) * two]
        attend_tiles(dims, lens, whose, q_own, m_all.at[at])

        @pl.when(i % 2 == 0)
        def _():
            normed[...] = n_all[at]
            qkv[...] = q_own[...]
            mixed[...] = m_all[at]

    @pl.when(i == 4)
    def _():
        for copy in sent_w:
            copy.wait_recv()
        keep_w.start()
        w2[...] = jnp.zeros_like(w2)
        b[...] = jnp.zeros_like(b)
        for t in range(3):
            copy_rows(w2, t * 2 * two, wf, t * local, two)
            copy_rows(w2, t * 2 * two + two + one_head, wf, t * local + two, one_head)
        for t, to in ((0, 0), (1, 4 * two)):
            b[0:1, to:to + two] = far_bias[t:t + 1, 0:two]
            b[0:1, to + two + one_head:to + 2 * two] = far_bias[t:t + 1, two:]
        copy_rows(ow, 0, own_o, 0, two)
        copy_rows(ow, two, wf, 3 * local, two)
        copy_rows(ow, 2 * two, own_o, two, one_head)
        copy_rows(ow, 2 * two + one_head, wf, 3 * local + two, one_head)

    @pl.when(i >= 4)
    def _():
        proj = project(w2)
        for t in range(3):
            to = 2 * t * two
            q_far[:, :, to:to + two] = proj[:, :, to:to + two]
            q_far[:, :, to + two:to + 2 * two] = (
                proj[:, :, to + two:to + 2 * two] + rest[at, :, :, t * two:(t + 1) * two])
        attend_tiles(dims, lens, whose, q_far, m_far)

        @pl.when(i % 2 == 0)
        def _():
            qkv_far[...] = q_far[...]
            mixed_far[...] = m_far[...]

        part = dot(m_all[at].reshape(count, two), ow[0:two, :])
        part = part + dot(m_far[...].reshape(count, 2 * two), ow[two:, :])
        part = part.reshape(quarter, slab, model)

        @pl.when(i < 6)
        def _():
            a_send[at] = part.astype(BF16)

        for j in range(2):
            @pl.when(i == 4 + j)
            def _():
                sent_a[j].start()

        for j in range(2):
            @pl.when(i == 6 + j)
            def _():
                sent_a[j].wait_recv()
                for p in range(quarter):
                    load_rows(dims, p, img, txt, rows)
                    a = part[p] + a_recv[j, p].astype(F32)
                    x = rows[...] + vector(vec, A_SCALE) * (a + vector(vec, A_BIAS))
                    n, _ = normalise(x)
                    e_img = n[0:ip] * vector(vec, GAIN2) + vector(vec, SHIFT2)
                    e_txt = n[ip:] * vector(vec, GAIN2 + 1) + vector(vec, SHIFT2 + 1)
                    r = j * quarter + p
                    e_send[r, 0:ip, :] = e_img.astype(BF16)
                    e_send[r, ip:, :] = e_txt.astype(BF16)
                    sent_e[r].start()
                    keep_e[r].start()
                    for k, v in enumerate((x[0:1], x[ip:ip + 1], e_img[0:1], e_txt[0:1])):
                        cls[k, r:r + 1, :] = v
                    if j == 0:
                        attended[p] = x
                        attn[p] = a

    @pl.when(i == 7)
    def _():
        sent_c.start()
        keep_w.wait()
        for copy in keep_e:
            copy.wait()
        sent_c.wait()
        cls_peer[...] = c_recv[...]
        for copy in sent_e:
            copy.wait()
        for copy in sent_w + sent_a:
            copy.wait_send()


def front(dims, lens, img, txt, vec, bias, own_w, own_o):
    model = img.shape[-1]
    quarter, slab, local = dims.quarter, dims.slab, dims.local
    held = pl.BlockSpec(memory_space=pltpu.VMEM)
    away = pl.BlockSpec(memory_space=pl.ANY)

    def states_at(i):
        return Place().quarter(i % 2, 1 - i % 4 // 2), 0, 0

    own_block = lambda cols: pl.BlockSpec((quarter, slab, cols), lambda i: (jnp.where(i < 2, 1, 0), 0, 0))
    far_block = lambda cols: pl.BlockSpec((quarter, slab, cols), lambda i: (jnp.where(i < 6, 1, 0), 0, 0))
    six = lambda cols: jax.ShapeDtypeStruct((2 * quarter, slab, cols), BF16)
    block = lambda cols: (quarter, slab, cols)
    n_remote = 6 + 2 * quarter
    return pl.pallas_call(
        functools.partial(front_kernel, dims),
        grid=(8,),
        in_specs=[pl.BlockSpec(memory_space=pltpu.SMEM),
                  pl.BlockSpec((quarter, dims.patches, model), states_at),
                  pl.BlockSpec((quarter, dims.caption, model), states_at)] + [held] * 4,
        out_specs=[own_block(model), own_block(384), own_block(128), far_block(768), far_block(256),
                   away, held, held, away, away, held, held],
        out_shape=[six(model), six(384), six(128), six(768), six(256),
                   jax.ShapeDtypeStruct((4 * local, model), BF16),
                   jax.ShapeDtypeStruct(block(model), F32), jax.ShapeDtypeStruct(block(model), F32),
                   six(model), six(model),
                   jax.ShapeDtypeStruct((4, 8, model), F32), jax.ShapeDtypeStruct((4, 8, model), F32)],
        scratch_shapes=[
            pltpu.VMEM((slab, model), F32), pltpu.VMEM((768, model), BF16), pltpu.VMEM((768, model), BF16),
            pltpu.VMEM((384, model), BF16), pltpu.VMEM((8, 768), F32), pltpu.VMEM((4 * local, model), BF16),
            pltpu.VMEM((2, local), F32),
            pltpu.VMEM((4,) + block(model), BF16), pltpu.VMEM((4,) + block(384), BF16),
            pltpu.VMEM((4,) + block(128), BF16), pltpu.VMEM(block(256), BF16),
            pltpu.VMEM(block(384), BF16), pltpu.VMEM(block(768), BF16),
            pltpu.VMEM((2,) + block(model), BF16), pltpu.VMEM((2,) + block(model), BF16),
            pltpu.VMEM((2 * quarter, slab, model), BF16), pltpu.VMEM((4, 8, model), F32),
            pltpu.SemaphoreType.DMA((1 + 2 * quarter,)),
            pltpu.SemaphoreType.DMA((n_remote,)), pltpu.SemaphoreType.DMA((n_remote,)),
        ],
        compiler_params=params(collective_id=6, has_side_effects=True),
        cost_estimate=pl.CostEstimate(
            flops=16 * quarter * slab * model * 1152, bytes_accessed=40_000_000, transcendentals=0),
        name="front",
    )(lens, img, txt, vec, bias, own_w, own_o)


def middle_kernel(dims, total, img, txt, own, peer, cls_own, cls_peer, vec, up, up_bias, down, weight, scale,
                  act, dup, ddn, dexp, d_own, d_near, bias_grad, class_e, c_act, c_dup, c_ddn, dcls,
                  head_in, dproj, gains, shifts, scalars,
                  bx, bd, rx, rd, x_near, x_far, ins, rows, part, parts, cls, back, cot, c_rows, extra, extras,
                  send_sem, recv_sem):
    here = Place()
    ip, slab, quarter = dims.ip, dims.slab, dims.quarter
    i = pl.program_id(0)
    model = own.shape[-1]
    mp_peers = [here.core, here.near, here.across]
    of = [here.quarter(0, 0), here.quarter(1, 0), here.quarter(0, 1), here.quarter(1, 1)]

    sent_x = [remote(bx.at[2 * j], rx.at[j], send_sem, recv_sem, j, here.core) for j in range(2)]
    sent_d = [remote(bd.at[2 * j], rd.at[j], send_sem, recv_sem, 2 + j, here.core) for j in range(2)]
    sent_near = remote(x_near, x_far, send_sem, recv_sem, 4, here.near)
    sent_part = [remote(part, parts.at[k], send_sem, recv_sem, 5 + k, mp_peers[k]) for k in range(3)]
    sent_extra = [remote(extra, extras.at[k], send_sem, recv_sem, 8 + k, mp_peers[k]) for k in range(3)]
    sent_cls = [remote(cls.at[here.b], cls.at[here.b], send_sem, recv_sem, 11 + k, here.batch[k]) for k in range(7)]

    @pl.when(i == 0)
    def _():
        rows[...] = jnp.zeros_like(rows)
        bias_grad[...] = jnp.zeros_like(bias_grad)
        for m in range(2):
            e = jnp.concatenate([cls_own[2 + m], cls_peer[2 + m]], axis=0).astype(BF16)
            class_e[m] = e
            u = dot(e, up[m]) + up_bias[m:m + 1]
            part[m] = dot(gelu_low(u), down[m])
        meet(mp_peers + here.batch)
        for copy in sent_part:
            copy.start()
        ins[...] = peer[quarter:, :, :]

    @pl.when(i == 1)
    def _():
        for copy in sent_part:
            copy.wait_recv()
        for m in range(2):
            cls[here.b, m] = jnp.zeros(cls.shape[2:], F32)
            for r in range(4):
                half, at = (cls_own, cls_peer)[r // 2], quarter * (r % 2)
                for p in range(quarter):
                    line = [d[m, own_row(dims, s, p):own_row(dims, s, p) + 1, :]
                            for d, s in ((part, r), (parts.at[0], r ^ 2), (parts.at[1], r ^ 1), (parts.at[2], r ^ 3))]
                    x = (line[0] + line[1]) + (line[2] + line[3]) + vector(vec, F_BIAS + m)
                    x = half[m, at + p:at + p + 1, :] + vector(vec, F_SCALE) * x
                    cls[here.b, m, pl.ds(4 * of[r] + p, 1), :] = x
        for copy in sent_cls:
            copy.start()
        ins[...] = own[quarter:, :, :]

    @pl.when(i == 2)
    def _():
        ins[...] = peer[:quarter, :, :]

    @pl.when(i == 3)
    def _():
        ins[...] = own[:quarter, :, :]
        for copy in sent_cls:
            copy.wait_recv()
        n_rows = 16 * cls.shape[0]
        sharp = jnp.exp(scale[...])
        col_at = lax.broadcasted_iota(jnp.int32, (1, n_rows), 1)
        row_at = lax.broadcasted_iota(jnp.int32, (n_rows, 1), 0)
        col_ok = (col_at % 4) < quarter
        row_ok = (row_at % 4) < quarter
        normal, inverse, proj, unit, embed = [], [], [], [], []
        for m in range(2):
            n, r = normalise(cls[:, m].reshape(n_rows, model))
            h = (n * vector(vec, H_GAIN + m) + vector(vec, H_SHIFT + m)).astype(BF16)
            head_in[m] = h
            y = dot(h, weight[m])
            u = lax.rsqrt(jnp.sum(y * y, axis=-1, keepdims=True) + 1e-6)
            normal.append(n)
            inverse.append(r)
            proj.append(y)
            unit.append(u)
            embed.append((y * u).astype(BF16))
        ok = row_ok & col_ok
        logits = sharp * dot_t(embed[0], embed[1])
        masked = jnp.where(ok, logits, -1e30)
        row_max = jnp.max(masked, axis=1, keepdims=True)
        row_lse = row_max + jnp.log(jnp.sum(jnp.exp(masked - row_max), axis=1, keepdims=True))
        col_max = jnp.max(masked, axis=0, keepdims=True)
        col_lse = col_max + jnp.log(jnp.sum(jnp.exp(masked - col_max), axis=0, keepdims=True))
        same = (row_at == col_at) & ok
        both = jnp.exp(masked - row_lse) + jnp.exp(masked - col_lse)
        dlogits = jnp.where(ok, jnp.where(same, both - 2.0, both) * (1.0 / (2 * total)), 0.0)
        diagonal = jnp.sum(jnp.where(same, logits, 0.0), axis=1, keepdims=True)
        lines = jnp.sum(jnp.where(row_ok, row_lse - 2.0 * diagonal, 0.0), axis=0, keepdims=True)
        lines = lines + jnp.sum(jnp.where(col_ok, col_lse, 0.0), axis=1, keepdims=True)
        slope = jnp.sum(jnp.sum(dlogits * logits, axis=1, keepdims=True), axis=0, keepdims=True)
        scalars[0:1, :] = jnp.broadcast_to(lines * (1.0 / (2 * total)), (1, 128))
        scalars[1:2, :] = jnp.broadcast_to(slope, (1, 128))
        high = lax.Precision.HIGHEST
        wide = [e.astype(F32) for e in embed]
        dembed = [
            sharp * jnp.dot(dlogits, wide[1], precision=high, preferred_element_type=F32),
            sharp * lax.dot_general(dlogits, wide[0], (((0,), (0,)), ((), ())), precision=high,
                                    preferred_element_type=F32),
        ]
        c_rows[...] = jnp.zeros_like(c_rows)
        dcls[...] = jnp.zeros_like(dcls)
        for m in range(2):
            for p in range(quarter):
                src = (img, txt)[m]
                cot[m, 8 * 3 + p:8 * 3 + p + 1, :] = src[p, 0:1, :].astype(F32)
        for m in range(2):
            u, y, d = unit[m], proj[m], dembed[m]
            dp = (u * d - u * u * u * y * jnp.sum(y * d, axis=-1, keepdims=True)).astype(BF16)
            dproj[m] = dp
            dh = dot_t(dp, weight[m])
            gains[m:m + 1, :] = jnp.sum(dh * normal[m], axis=0, keepdims=True)
            shifts[m:m + 1, :] = jnp.sum(dh, axis=0, keepdims=True)
            back[m] = norm_back(normal[m], inverse[m], dh * vector(vec, H_GAIN + m))
            for r in range(4):
                step = (3, 1, 2, 0)[r]
                for p in range(quarter):
                    g = back[m, pl.ds(16 * here.b + 4 * of[r] + p, 1), :]
                    at = own_row(dims, r, p)
                    c_rows[m, at:at + 1, :] = cot[m, 8 * step + p:8 * step + p + 1, :] + g
                    if r == 0:
                        dcls[p, m:m + 1, :] = g
            u = dot(class_e[m], up[m]) + up_bias[m:m + 1]
            big, small = gelu_parts(u)
            c_act[m] = (u * big).astype(BF16)
            g = (c_rows[m] * vector(vec, F_SCALE)).astype(BF16)
            c_ddn[m] = g
            du = dot_t(g, down[m]) * (big + u * small)
            bias_grad[m:m + 1, :] += jnp.sum(du, axis=0, keepdims=True)
            low = du.astype(BF16)
            c_dup[m] = low
            extra[m] = dot_t(low, up[m])
        for copy in sent_extra:
            copy.start()

    at = lax.broadcasted_iota(jnp.int32, (slab, 1), 0)
    inner = (at != 0) & (at != ip)

    def one(p, c):
        load_rows(dims, p, img, txt, rows)
        cot[0, pl.ds(8 * i + p, 1), :] = rows[0:1, :]
        cot[1, pl.ds(8 * i + p, 1), :] = rows[ip:ip + 1, :]
        ddn[p] = jnp.where(inner, rows[...] * vector(vec, F_SCALE), 0.0).astype(BF16)
        return c

    lax.fori_loop(0, quarter, one, 0)
    for m, lo, hi in ((0, 0, ip), (1, ip, slab)):
        count = quarter * (hi - lo)
        e = ins[:, lo:hi, :].reshape(count, model)
        u = dot(e, up[m]) + up_bias[m:m + 1]
        big, small = gelu_parts(u)
        a = (u * big).astype(BF16)
        act[:, lo:hi, :] = a.reshape(quarter, hi - lo, -1)
        slope = big + u * small
        bd[i, :, lo:hi, :] = dot(a, down[m]).astype(BF16).reshape(quarter, hi - lo, model)
        g = ddn[:, lo:hi, :].reshape(count, model)
        du = dot_t(g, down[m]) * slope
        bias_grad[m:m + 1, :] += jnp.sum(du, axis=0, keepdims=True)
        low = du.astype(BF16)
        dup[:, lo:hi, :] = low.reshape(quarter, hi - lo, -1)
        bx[i, :, lo:hi, :] = dot_t(low, up[m]).astype(BF16).reshape(quarter, hi - lo, model)

    for j in range(2):
        @pl.when(i == 2 * j)
        def _():
            sent_x[j].start()
            sent_d[j].start()

    @pl.when(i == 1)
    def _():
        sent_x[0].wait_recv()

        def add_x(p, c):
            x_near[p] = (bx[1, p].astype(F32) + rx[0, p].astype(F32)).astype(BF16)
            return c

        lax.fori_loop(0, quarter, add_x, 0)
        sent_near.start()
        sent_d[0].wait_recv()

        def add_d(p, c):
            d_near[p] = (bd[1, p].astype(F32) + rd[0, p].astype(F32)).astype(BF16)
            return c

        lax.fori_loop(0, quarter, add_d, 0)

    @pl.when(i == 3)
    def _():
        sent_d[1].wait_recv()

        def add_d(p, c):
            d_own[p] = bd[3, p].astype(F32) + rd[1, p].astype(F32)
            return c

        lax.fori_loop(0, quarter, add_d, 0)
        sent_x[1].wait_recv()
        sent_near.wait_recv()

        def add_x(p, c):
            dexp[p] = bx[3, p].astype(F32) + rx[1, p].astype(F32) + x_far[p].astype(F32)
            return c

        lax.fori_loop(0, quarter, add_x, 0)
        for copy in sent_extra:
            copy.wait_recv()
        for m in range(2):
            for p in range(quarter):
                line = [x[m, own_row(dims, r, p):own_row(dims, r, p) + 1, :]
                        for x, r in ((extra, 0), (extras.at[0], 2), (extras.at[1], 1), (extras.at[2], 3))]
                dexp[p, m * ip:m * ip + 1, :] += (line[0] + line[1]) + (line[2] + line[3])
        for copy in sent_x + sent_d + [sent_near] + sent_part + sent_extra + sent_cls:
            copy.wait_send()


def middle(dims, total, img, txt, own, peer, cls_own, cls_peer, vec, up, up_bias, down, weight, scale):
    model = own.shape[-1]
    hidden = up.shape[-1]
    slab, quarter = dims.slab, dims.quarter
    batch = 8

    def cot_at(i):
        here = Place()
        return here.quarter(1 - i // 2, 1 - i % 2), 0, 0

    held = pl.BlockSpec(memory_space=pltpu.VMEM)
    step = lambda cols: pl.BlockSpec((quarter, slab, cols), lambda i: (i, 0, 0))
    rows_of = lambda n, t: jax.ShapeDtypeStruct((n, slab, model), t)
    small = [((quarter, slab, model), F32), ((quarter, slab, model), F32), ((quarter, slab, model), BF16),
             ((2, hidden), F32), ((2, 16, model), BF16), ((2, 16, hidden), BF16), ((2, 16, hidden), BF16),
             ((2, 16, model), BF16), ((quarter, 8, model), F32), ((2, 16 * batch, model), BF16),
             ((2, 16 * batch, weight.shape[2]), BF16), ((2, model), F32), ((2, model), F32), ((2, 128), F32)]
    block = (quarter, slab, model)
    return pl.pallas_call(
        functools.partial(middle_kernel, dims, total),
        grid=(4,),
        in_specs=[pl.BlockSpec((quarter, dims.patches, model), cot_at),
                  pl.BlockSpec((quarter, dims.caption, model), cot_at)] + [held] * 10,
        out_specs=[step(hidden), step(hidden), step(model)] + [held] * len(small),
        out_shape=[rows_of(4 * quarter, BF16)] * 3 + [jax.ShapeDtypeStruct(v, t) for v, t in small],
        scratch_shapes=[
            pltpu.VMEM((4,) + block, BF16), pltpu.VMEM((4,) + block, BF16),
            pltpu.VMEM((2,) + block, BF16), pltpu.VMEM((2,) + block, BF16),
            pltpu.VMEM(block, BF16), pltpu.VMEM(block, BF16), pltpu.VMEM(block, BF16),
            pltpu.VMEM((slab, model), F32),
            pltpu.VMEM((2, 16, model), F32), pltpu.VMEM((3, 2, 16, model), F32),
            pltpu.VMEM((batch, 2, 16, model), F32), pltpu.VMEM((2, 16 * batch, model), F32),
            pltpu.VMEM((2, 32, model), F32), pltpu.VMEM((2, 16, model), F32),
            pltpu.VMEM((2, 16, model), F32), pltpu.VMEM((3, 2, 16, model), F32),
            pltpu.SemaphoreType.DMA((18,)), pltpu.SemaphoreType.DMA((18,)),
        ],
        compiler_params=params(collective_id=2, has_side_effects=True),
        cost_estimate=pl.CostEstimate(
            flops=32 * quarter * slab * model * hidden, bytes_accessed=40_000_000, transcendentals=0),
        name="middle",
    )(img, txt, own, peer, cls_own, cls_peer, vec, up, up_bias, down, weight, scale)


def turn_kernel(dims, img, txt, peer, own, act, dup, ddn, ce, ca, cu, cd, dexp, attended, attn, d_own, d_near, dcls, vec,
                down_sum, up_keep, up_send, dattended, dattn, dattn_peer, fin_img, fin_txt, sums,
                acc, d_far, n_peer, rows, side_send, side_recv, send_sem, recv_sem):
    here = Place()
    quarter, ip = dims.quarter, dims.ip
    i = pl.program_id(0)
    piece = side_send.shape[2]
    sent_near = remote(d_near, d_far, send_sem, recv_sem, 0, here.near)
    sent_core = [remote(dattn.at[p], n_peer.at[p], send_sem, recv_sem, 1 + p, here.core) for p in range(quarter)]
    sent_side = [remote(side_send.at[j], side_recv.at[j], send_sem, recv_sem, 1 + quarter + j, here.side)
                 for j in range(4)]
    spans = ((0, 0, ip), (1, ip, dims.slab))
    flat = lambda v: v.reshape(-1, v.shape[-1])
    block = lambda j: pl.ds(pl.multiple_of(j * piece, piece), piece)

    @pl.when(i == 0)
    def _():
        meet([here.core, here.near, here.side])
        sent_near.start()
        for m in range(2):
            acc[m] = t_dot(cd[m], ca[m])

    @pl.when(i < 4)
    def _():
        for m, lo, hi in spans:
            acc[m] += t_dot(flat(ddn[:, lo:hi, :]), flat(act[:, lo:hi, :]))

    @pl.when(i == 3)
    def _():
        for j in range(4):
            for m in range(2):
                side_send[j, m] = acc[m, block(2 * j + 1 - here.x), :].astype(BF16)
                down_sum[j, m] = acc[m, block(2 * j + here.x), :].astype(BF16)
            sent_side[j].start()

    @pl.when(i == 4)
    def _():
        for m in range(2):
            acc[m] = t_dot(ce[m], cu[m])

    for j, (e, at) in enumerate(((peer, quarter), (own, quarter), (peer, 0), (own, 0))):
        @pl.when(i == 4 + j)
        def _():
            for m, lo, hi in spans:
                acc[m] += t_dot(flat(e[at:at + quarter, lo:hi, :]), flat(dup[:, lo:hi, :]))

    @pl.when(i == 7)
    def _():
        for j in range(4):
            for m in range(2):
                up_keep[j, m] = acc[m, block(2 * j + here.x), :].astype(BF16)
                up_send[j, m] = acc[m, block(2 * j + 1 - here.x), :].astype(BF16)
        rows[...] = jnp.zeros_like(rows)
        sums[...] = jnp.zeros_like(sums)

        def load(p):
            load_rows(dims, p, img, txt, rows)
            rows[0:1, :] += dcls[p, 0:1, :]
            rows[ip:ip + 1, :] += dcls[p, 1:2, :]

        for p in range(quarter):
            load(p)
            for m, lo, hi in ((0, 0, ip), (1, ip, dims.slab)):
                n, r = normalise(attended[p, lo:hi, :])
                dy = dexp[p, lo:hi, :]
                sums[m:m + 1, :] += jnp.sum(dy * n, axis=0, keepdims=True)
                sums[2 + m:3 + m, :] += jnp.sum(dy, axis=0, keepdims=True)
                d = rows[lo:hi, :] + norm_back(n, r, dy * vector(vec, GAIN2 + m))
                dattended[p, lo:hi, :] = d
                sd = d * vector(vec, A_SCALE)
                dattn[p, lo:hi, :] = sd.astype(BF16)
                a = attn[p, lo:hi, :] + vector(vec, A_BIAS)
                sums[4:5, :] += jnp.sum(d * a, axis=0, keepdims=True)
                sums[5:6, :] += jnp.sum(sd, axis=0, keepdims=True)
            sent_core[p].start()
        sent_near.wait_recv()

        def final(p, c):
            load(p)
            for m, lo, hi in ((0, 0, ip), (1, ip, dims.slab)):
                b = d_own[p, lo:hi, :] + d_far[p, lo:hi, :].astype(F32) + vector(vec, F_BIAS + m)
                f = attended[p, lo:hi, :] + vector(vec, F_SCALE) * b
                if m == 0:
                    fin_img[p] = f[0:dims.patches].astype(BF16)
                else:
                    fin_txt[p] = f[0:dims.caption].astype(BF16)
                g = rows[lo:hi, :]
                sums[6:7, :] += jnp.sum(g * b, axis=0, keepdims=True)
                sums[7 + m:8 + m, :] += jnp.sum(g, axis=0, keepdims=True) * vector(vec, F_SCALE)
            return c

        lax.fori_loop(0, quarter, final, 0)
        for p in range(quarter):
            sent_core[p].wait()
            dattn_peer[p] = n_peer[p]
        for j in range(4):
            sent_side[j].wait()
            down_sum[j] = (down_sum[j].astype(F32) + side_recv[j].astype(F32)).astype(BF16)
        sent_near.wait_send()


def turn(dims, img, txt, peer, own, act, dup, ddn, ce, ca, cu, cd, dexp, attended, attn, d_own, d_near, dcls, vec):
    model = own.shape[-1]
    hidden = act.shape[-1]
    slab, quarter = dims.slab, dims.quarter
    held = pl.BlockSpec(memory_space=pltpu.VMEM)

    def own_at(i):
        return Place().quarter(0, 0), 0, 0

    first = pl.BlockSpec((quarter, slab, hidden), lambda i: (jnp.minimum(i, 3), 0, 0))
    last = pl.BlockSpec((quarter, slab, hidden), lambda i: (jnp.maximum(i - 4, 0), 0, 0))
    block = (quarter, slab, model)
    part = (4, 2, model // 8, hidden)
    outs = [(part, BF16), (part, BF16), (part, BF16), (block, F32), (block, BF16), (block, BF16),
            ((quarter, dims.patches, model), BF16), ((quarter, dims.caption, model), BF16), ((16, model), F32)]
    return pl.pallas_call(
        functools.partial(turn_kernel, dims),
        grid=(8,),
        in_specs=[pl.BlockSpec((quarter, dims.patches, model), own_at),
                  pl.BlockSpec((quarter, dims.caption, model), own_at)] + [held] * 2 + [first, last, first]
        + [held] * 11,
        out_specs=[held] * len(outs),
        out_shape=[jax.ShapeDtypeStruct(v, t) for v, t in outs],
        scratch_shapes=[
            pltpu.VMEM((2, model, hidden), F32), pltpu.VMEM(block, BF16), pltpu.VMEM(block, BF16),
            pltpu.VMEM((slab, model), F32), pltpu.VMEM(part, BF16), pltpu.VMEM(part, BF16),
            pltpu.SemaphoreType.DMA((5 + quarter,)), pltpu.SemaphoreType.DMA((5 + quarter,)),
        ],
        compiler_params=params(collective_id=3, has_side_effects=True),
        cost_estimate=pl.CostEstimate(
            flops=16 * quarter * slab * model * hidden, bytes_accessed=40_000_000, transcendentals=0),
        name="turn",
    )(img, txt, peer, own, act, dup, ddn, ce, ca, cu, cd, dexp, attended, attn, d_own, d_near, dcls, vec)


V_ROWS, V_MP, V_HEADS, V_FAR = 24, 11, 13, 15


def finish_kernel(dims, n_keep, n_send, dattended, states_img, states_txt, vec, fin_img, fin_txt,
                  near_a, near_b, near_txt, grad_pair, grad_single, grad_far, own_sums, up_sums, cols_own, cols_far,
                  out_img, out_txt, back_img, back_txt, grad_out, v_out,
                  n_recv, s_img, s_txt, d_img, d_txt, rows, xr, zs, zr, zr_far, far_sum, far_recv, vs, vr,
                  local_sem, send_sem, recv_sem):
    quarter = dims.quarter
    here = Place()
    z, x, m = here.z, here.x, here.m
    near_quarter = here.quarter(1, 0)
    used = [0]

    def send(src, dst, device):
        at = used[0]
        used[0] += 1
        return remote(src, dst, send_sem, recv_sem, at, device)

    loaded = [pltpu.make_async_copy(states_img.at[pl.ds(m * quarter, quarter)], s_img, local_sem.at[0]),
              pltpu.make_async_copy(states_txt.at[pl.ds(m * quarter, quarter)], s_txt, local_sem.at[1])]
    for copy in loaded:
        copy.start()
    meet([here.core, here.near, here.side] + here.along)

    n_copies = [send(n_send.at[p], n_recv.at[p], here.core) for p in range(quarter)]
    for copy in n_copies:
        copy.start()
    piece = xr.shape[1]
    wide = grad_pair.shape[1]
    spans = ((grad_pair, 0, wide), (grad_single, wide, xr.shape[2]))
    block = lambda j: pl.ds(pl.multiple_of(j * piece, piece), piece)
    x_copies = []
    for j in range(4):
        for src, lo, hi in spans:
            x_copies.append(send(src.at[block(2 * j + 1 - x)], xr.at[j, :, pl.ds(lo, hi - lo)], here.side))
            x_copies[-1].start()
    far_copies = [send(grad_far.at[(z + k) % 4], zr_far.at[k - 1], here.along[k - 1]) for k in range(1, 4)]
    for copy in far_copies:
        copy.start()

    last = quarter - 1
    fin_local, fin_remote = [], []
    for j, (src, dst, at, count) in enumerate((
        (fin_img, out_img, m * quarter, quarter), (fin_txt, out_txt, m * quarter, quarter),
        (near_a, out_img, near_quarter * quarter, last), (near_b, out_img, near_quarter * quarter + last, 1),
        (near_txt, out_txt, near_quarter * quarter, quarter),
    )):
        fin_local.append(pltpu.make_async_copy(src, dst.at[pl.ds(at, count)], local_sem.at[2 + j]))
        fin_remote.append(send(src, dst.at[pl.ds(at, count)], here.core))

    rows[...] = jnp.zeros_like(rows)
    for copy in loaded:
        copy.wait()
    total = [jnp.zeros((1, rows.shape[1]), F32)] * 2
    back_local, to_near, to_other = [], [], []
    for p in range(quarter):
        load_rows(dims, p, s_img, s_txt, rows)
        n, r = normalise(rows[...])
        n_copies[p].wait_recv()
        dy = n_keep[p].astype(F32) + n_recv[p].astype(F32)
        total[0] = total[0] + jnp.sum(dy * n, axis=0, keepdims=True)
        total[1] = total[1] + jnp.sum(dy, axis=0, keepdims=True)
        d = dattended[p] + norm_back(n, r, dy * vector(vec, GAIN1))
        d_img[p] = d[0:dims.patches].astype(BF16)
        d_txt[p] = d[dims.ip:dims.ip + dims.caption].astype(BF16)
        for j, (src, dst) in enumerate(((d_img, back_img), (d_txt, back_txt))):
            at = dst.at[m * quarter + p]
            to_near.append(send(src.at[p], at, here.near))
            to_near[-1].start()
            to_other.append(send(src.at[p], at, here.core))
            to_other[-1].start()
            back_local.append(pltpu.make_async_copy(src.at[p], at, local_sem.at[7 + 2 * p + j]))
            back_local[-1].start()
    for copy in fin_local + fin_remote:
        copy.start()

    at = lax.broadcasted_iota(jnp.int32, (V_ROWS, 1), 0)
    two, one_head = parts_of(dims)
    vs[0] = jnp.zeros(vs.shape[1:], F32)
    vs[0, 0:1, :] = total[0]
    vs[0, 1:2, :] = total[1]
    vs[0, 2:V_MP, :] = own_sums[0:V_MP - 2, :]
    vs[0, V_MP:V_HEADS, :] = up_sums[...]
    for j in range(2):
        own_at, far_at = 2 * j * two, 4 * j * two
        vs[0, V_HEADS + j:V_HEADS + j + 1, 0:two] = cols_own[0:1, own_at:own_at + two]
        vs[0, V_HEADS + j:V_HEADS + j + 1, two:two + one_head] = cols_far[0:1, far_at + two:far_at + two + one_head]
        vs[0, V_FAR + j:V_FAR + j + 1, 0:two] = cols_far[0:1, far_at:far_at + two]
        vs[0, V_FAR + j:V_FAR + j + 1, two:two + one_head] = cols_far[0:1, far_at + two + one_head:far_at + 2 * two]
    v = vs[0]
    v_copies = []

    def exchange(step, value, device):
        vs[step] = value
        copy = send(vs.at[step], vr.at[step], device)
        copy.start()
        copy.wait_recv()
        v_copies.append(copy)
        return vr[step]

    v = v + jnp.where(at < V_MP, exchange(0, v, here.core), 0.0)
    v = v + exchange(1, v, here.side)
    vs[2] = v
    vr[3 + z] = v
    around = [send(vs.at[2], vr.at[3 + z], here.along[k - 1]) for k in range(1, 4)]
    for copy in around:
        copy.start()
    def own_sum(j, k):
        src, lo, hi = spans[k]
        return src[block(2 * j + x), :].astype(F32) + xr[j, :, lo:hi].astype(F32)

    for copy in x_copies:
        copy.wait_recv()
    for j in range(4):
        for k, (src, lo, hi) in enumerate(spans):
            zs[j, :, lo:hi] = own_sum(j, k).astype(BF16)
    z_copies = [send(zs.at[(z + k) % 4], zr.at[k - 1], here.along[k - 1]) for k in range(1, 4)]
    for copy in z_copies:
        copy.start()

    for copy in around:
        copy.wait_recv()
    v = (vr[3] + vr[4]) + (vr[5] + vr[6])
    for copy in far_copies:
        copy.wait_recv()
    far = grad_far[z].astype(F32)
    for k in range(3):
        far = far + zr_far[k].astype(F32)
    far_sum[...] = far.astype(BF16)
    far_copy = send(far_sum, far_recv, here.near)
    far_copy.start()
    vs[3] = v
    v_near = send(vs.at[3], vr.at[2], here.near)
    v_near.start()
    for copy in z_copies:
        copy.wait_recv()
    for copy in fin_local + back_local:
        copy.wait()
    onward = []
    for p in range(quarter):
        for j, dst in enumerate((back_img, back_txt)):
            to_near[2 * p + j].wait_recv()
            at_near = dst.at[near_quarter * quarter + p]
            onward.append(send(at_near, at_near, here.core))
            onward[-1].start()
    far_copy.wait_recv()
    for k, (src, lo, hi) in enumerate(spans):
        g = own_sum(z, k) + far_recv[:, lo:hi].astype(F32)
        for j in range(3):
            g = g + zr[j, :, lo:hi].astype(F32)
        grad_out[:, lo:hi] = g
    v_near.wait_recv()
    there = vr[2]
    v_out[...] = v + jnp.where(at < V_MP, there, 0.0)
    v_out[V_HEADS:V_HEADS + 2, :] = v[V_HEADS:V_HEADS + 2, :] + there[V_FAR:V_FAR + 2, :]
    for copy in to_other + fin_remote + onward:
        copy.wait()
    for copy in n_copies + x_copies + far_copies + to_near + z_copies + v_copies + around + [far_copy, v_near]:
        copy.wait_send()


def finish(dims, n_keep, n_send, dattended, states_img, states_txt, vec, fin_img, fin_txt,
           near_a, near_b, near_txt, grad_pair, grad_single, grad_far, *tables):
    pairs, patches, model = states_img.shape
    caption = states_txt.shape[1]
    quarter, slab = dims.quarter, dims.slab
    piece, cols = grad_far.shape[1:]
    held = pl.BlockSpec(memory_space=pltpu.VMEM)
    away = pl.BlockSpec(memory_space=pl.ANY)
    n_remote = 7 * quarter + 27
    return pl.pallas_call(
        functools.partial(finish_kernel, dims),
        in_specs=[held] * 3 + [away] * 2 + [held] * 13,
        out_specs=[away] * 4 + [held] * 2,
        out_shape=[
            jax.ShapeDtypeStruct((pairs, patches, model), BF16),
            jax.ShapeDtypeStruct((pairs, caption, model), BF16),
            jax.ShapeDtypeStruct((pairs, patches, model), BF16),
            jax.ShapeDtypeStruct((pairs, caption, model), BF16),
            jax.ShapeDtypeStruct((piece, cols), F32),
            jax.ShapeDtypeStruct((V_ROWS, model), F32),
        ],
        scratch_shapes=[
            pltpu.VMEM((quarter, slab, model), BF16),
            pltpu.VMEM((quarter, patches, model), BF16),
            pltpu.VMEM((quarter, caption, model), BF16),
            pltpu.VMEM((quarter, patches, model), BF16),
            pltpu.VMEM((quarter, caption, model), BF16),
            pltpu.VMEM((slab, model), F32),
            pltpu.VMEM((4, piece, cols), BF16), pltpu.VMEM((4, piece, cols), BF16),
            pltpu.VMEM((3, piece, cols), BF16), pltpu.VMEM((3, piece, cols), BF16),
            pltpu.VMEM((piece, cols), BF16), pltpu.VMEM((piece, cols), BF16),
            pltpu.VMEM((4, V_ROWS, model), F32),
            pltpu.VMEM((7, V_ROWS, model), F32),
            pltpu.SemaphoreType.DMA((7 + 2 * quarter,)),
            pltpu.SemaphoreType.DMA((n_remote,)),
            pltpu.SemaphoreType.DMA((n_remote,)),
        ],
        compiler_params=params(collective_id=1, has_side_effects=True),
        name="finish",
    )(n_keep, n_send, dattended, states_img, states_txt, vec, fin_img, fin_txt,
      near_a, near_b, near_txt, grad_pair, grad_single, grad_far, *tables)


def spread_kernel(cols, at, sums, grad, gains, shifts, *refs):
    *outs, qkv, out_w, turned = refs
    back = sums.shape[1] - at[0] * cols

    def slice_of(value):
        return pltpu.roll(value, back, 1)[:, 0:cols]

    mine = slice_of(sums[...])
    for out, (lo, count) in zip(outs[:8], ((0, 1), (1, 1), (7, 1), (6, 1), (2, 2), (4, 2), (9, 2), (8, 1))):
        out[...] = mine[lo:lo + count, :]
    wide = jnp.concatenate([gains[...], shifts[...], jnp.zeros((4, sums.shape[1]), F32)], axis=0)
    heads = slice_of(wide)
    outs[8][...] = heads[0:2, :]
    outs[9][...] = heads[2:4, :]
    outs[10][...] = sums[V_MP:V_MP + 2, :]
    outs[11][...] = sums[V_HEADS:V_HEADS + 2, 0:outs[11].shape[1]]
    two, one = 2 * HEAD_DIM, HEAD_DIM
    for t in range(3):
        qkv[t, :, 0:two] = grad[:, t * two:(t + 1) * two]
        qkv[t, :, two:two + one] = grad[:, 4 * two + t * one:4 * two + (t + 1) * one]
    turned[...] = jnp.zeros_like(turned)
    turned[0:cols, 0:two] = grad[:, 3 * two:4 * two]
    turned[0:cols, two:two + one] = grad[:, 4 * two + 3 * one:4 * two + 4 * one]
    out_w[...] = turned[...].T[0:two + one, 0:cols]


def spread(local, at, sums, grad, gains, shifts):
    cols, model = grad.shape[0], sums.shape[1]
    assert cols <= 128
    shapes = [(1, cols)] * 4 + [(2, cols)] * 3 + [(1, cols)] + [(2, cols)] * 2 + [(2, model), (2, local)]
    shapes += [(3, cols, local), (local, cols)]
    args = (sums, grad, gains, shifts)
    return pl.pallas_call(
        functools.partial(spread_kernel, cols),
        grid_spec=pltpu.PrefetchScalarGridSpec(
            num_scalar_prefetch=1, grid=(1,),
            in_specs=[spec_whole(v) for v in args],
            out_specs=[pl.BlockSpec(v, lambda i, o, n=len(v): (0,) * n) for v in shapes],
            scratch_shapes=[pltpu.VMEM((128, 256), F32)],
        ),
        out_shape=[jax.ShapeDtypeStruct(v, F32) for v in shapes],
        compiler_params=params(),
        cost_estimate=pl.CostEstimate(flops=1_000_000, bytes_accessed=1_000_000, transcendentals=0),
        name="spread",
    )(at, *args)


def per_device(
    image_states, text_states, caption_lengths, image_cotangent, text_cotangent,
    first_gain, first_shift, query_key_value, query_value_bias, output_weight, output_bias,
    attention_scale, expert_gain, expert_shift, expert_up, expert_up_bias, expert_down,
    expert_down_bias, feedforward_scale, head_gain, head_shift, head_weight, logit_scale,
):
    pairs, patches, model = image_states.shape
    caption = text_states.shape[1]
    local = query_key_value.shape[2]
    quarter = pairs // 4
    batch_size = lax.axis_size("batch")
    assert lax.axis_size("mp") == 4 and pairs == 4 * quarter and quarter <= 3
    assert batch_size & (batch_size - 1) == 0
    assert local == 3 * HEAD_DIM
    ip, tp = up16(patches), up16(caption)
    dims = Dims(patches, caption, ip, tp, ip + tp, quarter, local)
    me = lax.axis_index("mp")
    batch_at = lax.axis_index("batch")
    order = me ^ jnp.asarray(ORDER, jnp.int32)
    vec = jnp.concatenate([
        first_gain[None], first_shift[None], attention_scale[None], output_bias[None], expert_gain, expert_shift,
        feedforward_scale[None], expert_down_bias, head_gain, head_shift, jnp.zeros((1, model), F32)])

    own_w = jnp.transpose(query_key_value, (1, 2, 0)).reshape(3 * local, model)
    one_kernel = batch_size == 8 and model // batch_size % 32 == 0 and expert_up.shape[2] == model
    if one_kernel:
        (normed, qkv_own, mixed_own, qkv_far, mixed_far, wf, attended, attn, e_own, e_peer, cls_own, cls_peer) = front(
            dims, caption_lengths, image_states, text_states, vec, query_value_bias, own_w, output_weight)
    else:
        wo = jnp.concatenate([own_w, output_weight])
        wf = to_y(wo)
        far_bias = to_y(query_value_bias)
        normed, qkv_own, rest, mixed_own = attend_own(
            dims, order, caption_lengths, image_states, text_states, vec, query_value_bias, wo)
        qkv_far, mixed_far, a_keep, a_send = attend_far(
            dims, order, caption_lengths, normed, rest, mixed_own, far_bias, wo, wf)
        a_recv = to_core(a_send)
        attended, attn, e_own, cls_own = residual(
            dims, order, a_keep, a_recv, image_states, text_states, vec)
        e_peer = to_core(e_own)
        cls_peer = to_core(cls_own)
    if one_kernel:
        (act, dup, ddn, dexp, d_own, d_near, up_sums, class_e, c_act, c_dup, c_ddn, dcls, head_in, dproj,
         grad_head_gain, grad_head_shift, scalars) = middle(
            dims, pairs * batch_size, image_cotangent, text_cotangent, e_own, e_peer, cls_own, cls_peer, vec,
            expert_up, expert_up_bias, expert_down, head_weight, logit_scale.reshape(1, 1))
        down_sum, up_keep, up_send, dattended, dattn, dattn_peer, fin_img, fin_txt, own_sums = turn(
            dims, image_cotangent, text_cotangent, e_peer, e_own, act, dup, ddn, class_e, c_act, c_dup, c_ddn,
            dexp, attended, attn, d_own, d_near, dcls, vec)
    else:
        class_part, class_e = class_forward(dims, cls_own, cls_peer, expert_up, expert_up_bias, expert_down)
        class_parts = from_others(class_part, "mp", 1, 4)

        act_a, dup_a, ddn_a, d_send3, d_keep1, x_send3, x_keep1, bias_a, cot_a = experts(
            dims, "experts_a", 1, order[jnp.asarray([3, 1])], e_peer, e_own, image_cotangent, text_cotangent,
            tie(vec, class_part), expert_up, expert_up_bias, expert_down)
        x_recv1 = to_core(x_send3)
        d_recv1 = to_core(d_send3)
        final_class = class_final(
            dims, order, cls_own, cls_peer, class_parts, tie(vec, bias_a))
        class_blocks = gather_batch(final_class[None])
        x_near = add_low(x_keep1, x_recv1)
        x_far = to_y(x_near)
        act_b, dup_b, ddn_b, d_send2, d_keep0, x_send2, x_keep0, bias_b, cot_b = experts(
            dims, "experts_b", 0, order[jnp.asarray([2, 0])], e_peer, e_own, image_cotangent, text_cotangent,
            tie(vec, final_class, x_near), expert_up, expert_up_bias, expert_down)
        x_recv0 = to_core(x_send2)
        d_recv0 = to_core(d_send2)

        head_in, dproj, dclass, grad_head_gain, grad_head_shift, scalars = (contrast if batch_size <= 8 else contrast_large)(
            dims, pairs * batch_size, batch_at.reshape(1), class_blocks, tie(vec, bias_b), head_weight,
             logit_scale.reshape(1, 1))
        c_act, c_dup, c_ddn, c_dexp, c_bias, dcls = class_back(
            dims, order, class_e, cot_a, cot_b, dclass, vec, expert_up, expert_up_bias, expert_down)
        extras = from_others(c_dexp, "mp", 1, 4)
        d_far = to_y(add_low(d_keep1, tie(d_recv1, c_dexp)))
        expert_grad = expert_grads(
            dims, e_peer, e_own, act_a, dup_a, ddn_a, act_b, dup_b, ddn_b, class_e, c_act, c_dup, c_ddn)
        expert_sum = lax.psum_scatter(expert_grad, "batch", scatter_dimension=1, tiled=True)

        dattended, dattn, sums_two = norm_two(
            dims, order, x_keep0, x_recv0, x_far, attended, a_keep, a_recv, image_cotangent, text_cotangent,
            dcls, extras, tie(vec, expert_grad))
        dattn_peer = to_core(dattn)
        fin_img, fin_txt, sums_fin = final_rows(
            dims, order, d_keep0, d_recv0, d_far, attended, image_cotangent, text_cotangent, dcls,
            tie(vec, sums_two))
        own_sums = jnp.concatenate([sums_two[:6], sums_fin[:3]])
        up_sums = bias_a + bias_b + c_bias
    contrast_loss = scalars[0, :1]
    grad_logit_scale = scalars[1, :1]
    carried = dict(carry=(fin_img, up_keep, up_send, down_sum)) if one_kernel else {}
    n_keep, n_send, grad_far, grad_o2, cols_far, *more_far = attend_back(
        dims, True, order, caption_lengths, dattn, dattn_peer, normed, qkv_far, mixed_far, own_w, output_weight, wf, **carried)
    carried = dict(carry=(fin_img, fin_txt, grad_far, more_far[1])) if one_kernel else {}
    n_keep, n_send, grad_o01, cols_own, *more_own = attend_back(
        dims, False, order, caption_lengths, dattn, dattn_peer, normed, qkv_own, mixed_own, own_w, output_weight, wf,
        prior=(n_keep, n_send), **carried)
    cols = model // batch_size
    mine = lambda v, axis: lax.dynamic_slice_in_dim(v, batch_at * cols, cols, axis=axis)
    grad_head_weight = jnp.einsum("mnc,mne->mce", mine(head_in, 2), dproj, preferred_element_type=F32)
    pair, single = 2 * HEAD_DIM, HEAD_DIM
    if one_kernel:
        near_a, _, grad_down = more_far
        near_b, near_txt, side_sum, grad_up = more_own
        image_output, text_output, image_grad, text_grad, attn_grad, sums = finish(
            dims, n_keep, n_send, dattended, image_states, text_states, vec, fin_img, fin_txt,
            near_a, near_b, near_txt, grad_o01, grad_o2, side_sum, own_sums, up_sums, cols_own, cols_far)
        *vectors, grad_qkv, grad_output_weight = spread(
            local, batch_at.reshape(1), sums, attn_grad, grad_head_gain, grad_head_shift)
        flat = lambda v: v.reshape(-1)
        return (
            image_output,
            text_output,
            contrast_loss,
            image_grad,
            text_grad,
            flat(vectors[0]),
            flat(vectors[1]),
            jnp.transpose(grad_qkv, (1, 0, 2)),
            vectors[11],
            grad_output_weight,
            flat(vectors[2]),
            flat(vectors[3]),
            vectors[4],
            vectors[5],
            grad_up,
            vectors[10],
            jnp.transpose(grad_down, (0, 2, 1)),
            vectors[6],
            flat(vectors[7]),
            vectors[8],
            vectors[9],
            grad_head_weight,
            grad_logit_scale,
        )
    else:
        grad_expert_up = expert_sum[:2].astype(F32)
        grad_expert_down = jnp.transpose(expert_sum[2:].astype(F32), (0, 2, 1))
        cols_own = cols_own.reshape(3, pair)[::2]
        cols_far = cols_far.reshape(3, 2 * pair)[::2]
        heads = jnp.concatenate([cols_own, cols_far[:, pair:pair + single]], axis=1)
        heads_far = jnp.concatenate([cols_far[:, :pair], cols_far[:, pair + single:]], axis=1)
        n_recv = to_core(n_send)
        d_img, d_txt, sums_one = norm_one(
            dims, order, n_keep, n_recv, dattended, image_states, text_states, vec)
        image_output = gather_rows(fin_img, me)
        text_output = gather_rows(fin_txt, me)
        image_grad = gather_rows(d_img, me)
        text_grad = gather_rows(d_txt, me)
        grad_own = jnp.concatenate([grad_o01, grad_o2], axis=1)
        grad_far = lax.psum_scatter(grad_far, "batch", scatter_dimension=0, tiled=True)
        grad_own = lax.psum_scatter(grad_own, "batch", scatter_dimension=0, tiled=True)
        attn_grad = grad_own.astype(F32) + to_y(grad_far).astype(F32)
        heads = heads + to_y(heads_far)
        own_sums = sum_over(jnp.concatenate([sums_one[:2], own_sums]), "mp")
        flat = jnp.concatenate([own_sums.reshape(-1), heads.reshape(-1), up_sums.reshape(-1)])
        count = flat.shape[0]
        flat = jnp.pad(flat, (0, -count % 1024)).reshape(-1, 128)
        flat = sum_over(flat, "batch").reshape(-1)[:count]
        done = own_sums.shape[0]
        own_sums = mine(flat[:done * model].reshape(done, model), 1)
        heads = flat[done * model:done * model + 2 * local].reshape(2, local)
        grad_expert_up_bias = flat[done * model + 2 * local:].reshape(up_sums.shape)
    attn_grad = jnp.concatenate(
        [attn_grad[:, :4 * pair].reshape(cols, 4, pair), attn_grad[:, 4 * pair:].reshape(cols, 4, single)], axis=2)
    grad_query_key_value = attn_grad[:, :3]
    grad_output_weight = jnp.transpose(attn_grad[:, 3])
    return (
        image_output,
        text_output,
        contrast_loss,
        image_grad,
        text_grad,
        own_sums[0],
        own_sums[1],
        grad_query_key_value,
        heads,
        grad_output_weight,
        own_sums[7],
        own_sums[6],
        own_sums[2:4],
        own_sums[4:6],
        grad_expert_up,
        grad_expert_up_bias,
        grad_expert_down,
        own_sums[9:11],
        own_sums[8],
        mine(grad_head_gain, 1),
        mine(grad_head_shift, 1),
        grad_head_weight,
        grad_logit_scale,
    )


def solution(mesh):
    return jax.shard_map(
        per_device,
        mesh=mesh,
        in_specs=(
            P("batch", None, None),
            P("batch", None, None),
            P("batch"),
            P("batch", None, None),
            P("batch", None, None),
            P(),
            P(),
            P(None, None, "mp"),
            P(None, "mp"),
            P("mp", None),
            P(),
            P(),
            P(),
            P(),
            P(None, None, "mp"),
            P(None, "mp"),
            P(None, "mp", None),
            P(),
            P(),
            P(),
            P(),
            P(),
            P(),
        ),
        out_specs=(
            P("batch", None, None),
            P("batch", None, None),
            P(),
            P("batch", None, None),
            P("batch", None, None),
            P("batch"),
            P("batch"),
            P("batch", None, "mp"),
            P(None, "mp"),
            P("mp", "batch"),
            P("batch"),
            P("batch"),
            P(None, "batch"),
            P(None, "batch"),
            P(None, "batch", "mp"),
            P(None, "mp"),
            P(None, "mp", "batch"),
            P(None, "batch"),
            P("batch"),
            P(None, "batch"),
            P(None, "batch"),
            P(None, "batch", None),
            P(),
        ),
        check_vma=False,
    )
```

```python
import functools
from typing import NamedTuple

import jax
import jax.numpy as jnp
from jax import lax
from jax.experimental import pallas as pl
from jax.experimental.pallas import tpu as pltpu
from jax.sharding import PartitionSpec as P

HEAD_DIM = 64
F32 = jnp.float32
BF16 = jnp.bfloat16
NEG = -1e9
EPS = 1e-5
ORDER = (0, 2, 1, 3)

VMEM_LIMIT = 60 * 1024 * 1024


def params(**kw):
    return pltpu.CompilerParams(vmem_limit_bytes=VMEM_LIMIT, **kw)


def up16(n):
    return -(-n // 16) * 16


def dot(a, b):
    return jnp.dot(a, b, preferred_element_type=F32)


def dot_t(a, b):
    return lax.dot_general(a, b, (((1,), (1,)), ((), ())), preferred_element_type=F32)


def t_dot(a, b):
    return lax.dot_general(a, b, (((0,), (0,)), ((), ())), preferred_element_type=F32)


def normalise(x):
    c = x - jnp.mean(x, axis=-1, keepdims=True)
    v = jnp.mean(c * c, axis=-1, keepdims=True)
    r = lax.rsqrt(v + EPS)
    return c * r, r


def norm_back(n, r, dn):
    a = jnp.mean(dn, axis=-1, keepdims=True)
    b = jnp.mean(dn * n, axis=-1, keepdims=True)
    return (dn - a - n * b) * r


def gelu_parts(u):
    big = 0.5 * (1.0 + lax.erf(u * 0.7071067811865476))
    small = 0.3989422804014327 * jnp.exp(-0.5 * u * u)
    return big, small


def gelu_low(u):
    return (u * (0.5 * (1.0 + lax.erf(u * 0.7071067811865476)))).astype(BF16)


def softmax_rows(scores):
    m = jnp.max(scores, axis=-1, keepdims=True)
    e = jnp.exp(scores - m)
    return e * (1.0 / jnp.sum(e, axis=-1, keepdims=True))


def tie(value, *after):
    return lax.optimization_barrier((value,) + after)[0]


def load_rows(dims, p, img, txt, rows):
    rows[0:dims.patches, :] = img[p].astype(F32)
    rows[dims.ip:dims.ip + dims.caption, :] = txt[p].astype(F32)


def spec_whole(a):
    return pl.BlockSpec(a.shape, lambda *_: (0,) * a.ndim)


class Dims(NamedTuple):
    patches: int
    caption: int
    ip: int
    tp: int
    slab: int
    quarter: int
    local: int


GAIN1, SHIFT1, A_SCALE, A_BIAS, GAIN2, SHIFT2, F_SCALE, F_BIAS, H_GAIN, H_SHIFT = 0, 1, 2, 3, 4, 6, 8, 9, 11, 13


def vector(table, at, count=1):
    return table[at:at + count, :]


def copy_rows(dst, at, src, start, count):
    dst[at:at + count, :] = src[start:start + count, :]


def parts_of(dims):
    return 2 * HEAD_DIM, HEAD_DIM


def key_tail(dims, length):
    at = dims.patches // 16 * 16
    return ((0, dims.ip, at, dims.patches), (dims.ip, dims.slab, 0, length))


def hide(scores, start, limit):
    if start >= scores.shape[0]:
        return scores
    tail = scores[start:]
    at = start + lax.broadcasted_iota(jnp.int32, (tail.shape[0], 1), 0)
    tail = jnp.where(at < limit, tail, NEG)
    return tail if start == 0 else jnp.concatenate([scores[:start], tail], axis=0)


def split_pair(value):
    low = lax.broadcasted_iota(jnp.int32, (1, 128), 1) < HEAD_DIM
    zero = jnp.zeros_like(value)
    return jnp.concatenate([jnp.where(low, value, zero), jnp.where(low, zero, value)], axis=0)


def join_pair(value):
    low = lax.broadcasted_iota(jnp.int32, (1, 128), 1) < HEAD_DIM
    half = value.shape[0] // 2
    return jnp.where(low, value[:half], value[half:])


def softmax_keys(scores):
    e = jnp.exp(scores - jnp.max(scores, axis=0, keepdims=True))
    return e * (1.0 / jnp.sum(e, axis=0, keepdims=True))


def pair_weights(q, k, start, limit):
    return softmax_keys(hide(dot_t(k, split_pair(q)), start, limit))


def scaled(q):
    return q * jnp.asarray(HEAD_DIM ** -0.5, BF16)


def attend_tiles(dims, lens, quarter_at, qkv, mixed):
    tiles = mixed.shape[-1] // 128

    def one_pair(p, c):
        length = lens[quarter_at * dims.quarter + p]
        for lo, hi, start, limit in key_tail(dims, length):
            for g in range(tiles):
                q, k, v = [qkv[p, lo:hi, (t * tiles + g) * 128:(t * tiles + g + 1) * 128] for t in range(3)]
                w = pair_weights(scaled(q), k, start, limit).astype(BF16)
                mixed[p, lo:hi, g * 128:(g + 1) * 128] = join_pair(t_dot(w, v)).astype(BF16)
        return c

    lax.fori_loop(0, dims.quarter, one_pair, 0)


def attend_own_kernel(dims, order, lens, img, txt, vec, bias, wo, normed, qkv, rest, mixed, rows, w, b):
    i = pl.program_id(0)
    local = dims.local
    two, one_head = parts_of(dims)

    @pl.when(i == 0)
    def _():
        rows[...] = jnp.zeros_like(rows)
        w[...] = jnp.zeros_like(w)
        b[...] = jnp.zeros_like(b)
        for t in range(3):
            copy_rows(w, t * 2 * two, wo, t * local, local)
        b[0:1, 0:local] = bias[0:1, :]
        b[0:1, 4 * two:4 * two + local] = bias[1:2, :]

    def one_norm(p, c):
        load_rows(dims, p, img, txt, rows)
        n, _ = normalise(rows[...])
        normed[p] = (n * vector(vec, GAIN1) + vector(vec, SHIFT1)).astype(BF16)
        return c

    lax.fori_loop(0, dims.quarter, one_norm, 0)
    model = normed.shape[-1]
    proj = (dot_t(normed[...].reshape(dims.quarter * dims.slab, model), w[...]) + b[0:1, :]).astype(BF16)
    proj = proj.reshape(dims.quarter, dims.slab, 6 * two)
    for t in range(3):
        qkv[:, :, t * two:(t + 1) * two] = proj[:, :, 2 * t * two:(2 * t + 1) * two]
        rest[:, :, t * two:(t + 1) * two] = proj[:, :, (2 * t + 1) * two:(2 * t + 2) * two]
    attend_tiles(dims, lens, order[i], qkv, mixed)


def attend_own(dims, order, lens, img, txt, vec, bias, wo):
    model = img.shape[-1]
    pairs = 4 * dims.quarter
    block = lambda cols: pl.BlockSpec((dims.quarter, dims.slab, cols), lambda i, o, n: (i, 0, 0))
    shape = lambda cols: jax.ShapeDtypeStruct((pairs, dims.slab, cols), BF16)
    return pl.pallas_call(
        functools.partial(attend_own_kernel, dims),
        grid_spec=pltpu.PrefetchScalarGridSpec(
            num_scalar_prefetch=2,
            grid=(4,),
            in_specs=[
                pl.BlockSpec((dims.quarter, dims.patches, model), lambda i, o, n: (o[i], 0, 0)),
                pl.BlockSpec((dims.quarter, dims.caption, model), lambda i, o, n: (o[i], 0, 0)),
                spec_whole(vec), spec_whole(bias), spec_whole(wo),
            ],
            out_specs=[block(model), block(384), block(384), block(128)],
            scratch_shapes=[pltpu.VMEM((dims.slab, model), F32), pltpu.VMEM((768, model), BF16),
                            pltpu.VMEM((8, 768), F32)],
        ),
        out_shape=[shape(model), shape(384), shape(384), shape(128)],
        compiler_params=params(),
        cost_estimate=pl.CostEstimate(
            flops=1536 * pairs * dims.slab * model, bytes_accessed=30_000_000, transcendentals=0),
        name="attend_own",
    )(order, lens, img, txt, vec, bias, wo)


def attend_far_kernel(dims, order, lens, normed, rest, own, bias, wo, wf, qkv, mixed, keep, send, w, ow, b):
    i = pl.program_id(0)
    local = dims.local
    two, one_head = parts_of(dims)
    count = dims.quarter * dims.slab
    model = normed.shape[-1]

    @pl.when(i == 0)
    def _():
        w[...] = jnp.zeros_like(w)
        b[...] = jnp.zeros_like(b)
        for t in range(3):
            copy_rows(w, t * 2 * two, wf, t * local, two)
            copy_rows(w, t * 2 * two + two + one_head, wf, t * local + two, one_head)
        for t, at in ((0, 0), (1, 4 * two)):
            b[0:1, at:at + two] = bias[t:t + 1, 0:two]
            b[0:1, at + two + one_head:at + 2 * two] = bias[t:t + 1, two:]
        copy_rows(ow, 0, wo, 3 * local, two)
        copy_rows(ow, two, wf, 3 * local, two)
        copy_rows(ow, 2 * two, wo, 3 * local + two, one_head)
        copy_rows(ow, 2 * two + one_head, wf, 3 * local + two, one_head)

    proj = (dot_t(normed[...].reshape(count, model), w[...]) + b[0:1, :]).astype(BF16)
    proj = proj.reshape(dims.quarter, dims.slab, 6 * two)
    for t in range(3):
        at = 2 * t * two
        qkv[:, :, at:at + two] = proj[:, :, at:at + two]
        qkv[:, :, at + two:at + 2 * two] = proj[:, :, at + two:at + 2 * two] + rest[:, :, t * two:(t + 1) * two]
    attend_tiles(dims, lens, order[(i + 2) % 4], qkv, mixed)
    part = dot(own[...].reshape(count, two), ow[0:two, :])
    part = part + dot(mixed[...].reshape(count, 2 * two), ow[two:, :])
    part = part.astype(BF16).reshape(dims.quarter, dims.slab, model)

    @pl.when(i < 2)
    def _():
        send[...] = part

    @pl.when(i >= 2)
    def _():
        keep[...] = part


def attend_far(dims, order, lens, normed, rest, own, bias, wo, wf):
    model = normed.shape[-1]
    pairs = 4 * dims.quarter
    at = lambda i: (i + 2) % 4
    block = lambda cols, f: pl.BlockSpec((dims.quarter, dims.slab, cols), lambda i, o, n: (f(i), 0, 0))
    shape = lambda count, cols: jax.ShapeDtypeStruct((count, dims.slab, cols), BF16)
    return pl.pallas_call(
        functools.partial(attend_far_kernel, dims),
        grid_spec=pltpu.PrefetchScalarGridSpec(
            num_scalar_prefetch=2,
            grid=(4,),
            in_specs=[
                block(model, at), block(384, at), block(128, at),
                spec_whole(bias), spec_whole(wo), spec_whole(wf),
            ],
            out_specs=[
                block(768, at), block(256, at),
                block(model, lambda i: jnp.maximum(i - 2, 0)), block(model, lambda i: jnp.minimum(i, 1)),
            ],
            scratch_shapes=[pltpu.VMEM((768, model), BF16), pltpu.VMEM((384, model), BF16),
                            pltpu.VMEM((8, 768), F32)],
        ),
        out_shape=[
            shape(pairs, 768), shape(pairs, 256),
            shape(2 * dims.quarter, model), shape(2 * dims.quarter, model),
        ],
        compiler_params=params(),
        cost_estimate=pl.CostEstimate(
            flops=2304 * pairs * dims.slab * model, bytes_accessed=30_000_000, transcendentals=0),
        name="attend_far",
    )(order, lens, normed, rest, own, bias, wo, wf)


def residual_kernel(dims, order, keep, recv, img, txt, vec, attended, attn, expert, cls, rows):
    i = pl.program_id(0)
    ip = dims.ip

    @pl.when(i == 0)
    def _():
        rows[...] = jnp.zeros_like(rows)
        cls[...] = jnp.zeros_like(cls)

    load_rows(dims, 0, img, txt, rows)
    a = keep[0].astype(F32) + recv[0].astype(F32)
    x = rows[...] + vector(vec, A_SCALE) * (a + vector(vec, A_BIAS))
    n, _ = normalise(x)
    e_img = n[0:ip] * vector(vec, GAIN2) + vector(vec, SHIFT2)
    e_txt = n[ip:] * vector(vec, GAIN2 + 1) + vector(vec, SHIFT2 + 1)
    expert[0, 0:ip, :] = e_img.astype(BF16)
    expert[0, ip:, :] = e_txt.astype(BF16)
    for j, v in enumerate((x[0:1], x[ip:ip + 1], e_img[0:1], e_txt[0:1])):
        cls[j, pl.ds(i, 1), :] = v

    @pl.when(i < dims.quarter)
    def _():
        attended[0] = x
        attn[0] = a


def residual(dims, order, keep, recv, img, txt, vec):
    model = img.shape[-1]
    quarter = dims.quarter
    block = pl.BlockSpec((1, dims.slab, model), lambda i, o: (i, 0, 0))
    pair = lambda i, o: (o[i // quarter] * quarter + i % quarter, 0, 0)
    return pl.pallas_call(
        functools.partial(residual_kernel, dims),
        grid_spec=pltpu.PrefetchScalarGridSpec(
            num_scalar_prefetch=1,
            grid=(2 * quarter,),
            in_specs=[
                block, block,
                pl.BlockSpec((1, dims.patches, model), pair),
                pl.BlockSpec((1, dims.caption, model), pair),
                spec_whole(vec),
            ],
            out_specs=[
                pl.BlockSpec((1, dims.slab, model), lambda i, o: (jnp.minimum(i, quarter - 1), 0, 0)),
                pl.BlockSpec((1, dims.slab, model), lambda i, o: (jnp.minimum(i, quarter - 1), 0, 0)),
                block,
                pl.BlockSpec((4, 8, model), lambda i, o: (0, 0, 0)),
            ],
            scratch_shapes=[pltpu.VMEM((dims.slab, model), F32)],
        ),
        out_shape=[
            jax.ShapeDtypeStruct((quarter, dims.slab, model), F32),
            jax.ShapeDtypeStruct((quarter, dims.slab, model), F32),
            jax.ShapeDtypeStruct((2 * quarter, dims.slab, model), BF16),
            jax.ShapeDtypeStruct((4, 8, model), F32),
        ],
        compiler_params=params(),
        cost_estimate=pl.CostEstimate(flops=40_000_000, bytes_accessed=20_000_000, transcendentals=0),
        name="residual",
    )(order, keep, recv, img, txt, vec)


def expert_kernel(dims, seq, peer, own, img, txt, vec, up, up_bias, down,
                  act, dup, ddown, d_send, d_keep, x_send, x_keep, bias_grad, cot, ins, rows):
    ip, slab, quarter = dims.ip, dims.slab, dims.quarter
    i = pl.program_id(0)
    model = own.shape[-1]

    @pl.when(i == 0)
    def _():
        rows[...] = jnp.zeros_like(rows)
        bias_grad[...] = jnp.zeros_like(bias_grad)
        cot[...] = jnp.zeros_like(cot)
        ins[...] = peer[...]

    @pl.when(i == 1)
    def _():
        ins[...] = own[...]

    at = lax.broadcasted_iota(jnp.int32, (slab, 1), 0)
    inner = (at != 0) & (at != ip)

    def one(p, c):
        load_rows(dims, p, img, txt, rows)
        cot[0, pl.ds(8 * i + p, 1), :] = rows[0:1, :]
        cot[1, pl.ds(8 * i + p, 1), :] = rows[ip:ip + 1, :]
        ddown[p] = jnp.where(inner, rows[...] * vector(vec, F_SCALE), 0.0).astype(BF16)
        return c

    lax.fori_loop(0, quarter, one, 0)
    for m, lo, hi in ((0, 0, ip), (1, ip, slab)):
        count = quarter * (hi - lo)
        e = ins[:, lo:hi, :].reshape(count, model)
        u = dot(e, up[m]) + up_bias[m:m + 1]
        big, small = gelu_parts(u)
        a = (u * big).astype(BF16)
        act[:, lo:hi, :] = a.reshape(quarter, hi - lo, -1)
        slope = big + u * small
        d = dot(a, down[m]).astype(BF16).reshape(quarter, hi - lo, model)
        g = ddown[:, lo:hi, :].reshape(count, model)
        du = dot_t(g, down[m]) * slope
        bias_grad[m:m + 1, :] += jnp.sum(du, axis=0, keepdims=True)
        low = du.astype(BF16)
        dup[:, lo:hi, :] = low.reshape(quarter, hi - lo, -1)
        x = dot_t(low, up[m]).astype(BF16).reshape(quarter, hi - lo, model)

        @pl.when(i == 0)
        def _():
            d_send[:, lo:hi, :] = d
            x_send[:, lo:hi, :] = x

        @pl.when(i == 1)
        def _():
            d_keep[:, lo:hi, :] = d
            x_keep[:, lo:hi, :] = x


def experts(dims, name, half, seq, peer, own, img, txt, vec, up, up_bias, down):
    model = own.shape[-1]
    hidden = up.shape[-1]
    slab, quarter = dims.slab, dims.quarter
    fixed = pl.BlockSpec((quarter, slab, model), lambda i, o: (half, 0, 0))
    first = pl.BlockSpec((quarter, slab, model), lambda i, o: (0, 0, 0))
    step = lambda cols: pl.BlockSpec((quarter, slab, cols), lambda i, o: (i, 0, 0))
    shape = lambda n, cols: jax.ShapeDtypeStruct((n * quarter, slab, cols), BF16)
    return pl.pallas_call(
        functools.partial(expert_kernel, dims),
        grid_spec=pltpu.PrefetchScalarGridSpec(
            num_scalar_prefetch=1,
            grid=(2,),
            in_specs=[
                fixed, fixed,
                pl.BlockSpec((quarter, dims.patches, model), lambda i, o: (o[i], 0, 0)),
                pl.BlockSpec((quarter, dims.caption, model), lambda i, o: (o[i], 0, 0)),
                spec_whole(vec), spec_whole(up), spec_whole(up_bias), spec_whole(down),
            ],
            out_specs=[
                step(hidden), step(hidden), step(model),
                first, first, first, first,
                pl.BlockSpec((2, hidden), lambda i, o: (0, 0)),
                pl.BlockSpec((2, 16, model), lambda i, o: (0, 0, 0)),
            ],
            scratch_shapes=[pltpu.VMEM((quarter, slab, model), BF16), pltpu.VMEM((slab, model), F32)],
        ),
        out_shape=[
            shape(2, hidden), shape(2, hidden), shape(2, model),
            shape(1, model), shape(1, model), shape(1, model), shape(1, model),
            jax.ShapeDtypeStruct((2, hidden), F32),
            jax.ShapeDtypeStruct((2, 16, model), F32),
        ],
        compiler_params=params(),
        cost_estimate=pl.CostEstimate(
            flops=16 * quarter * slab * model * hidden, bytes_accessed=20_000_000, transcendentals=0),
        name=name,
    )(seq, peer, own, img, txt, vec, up, up_bias, down)


def expert_grads_kernel(dims, peer, own, act_a, dup_a, ddn_a, act_b, dup_b, ddn_b, ce, ca, cu, cd, out, acc):
    i = pl.program_id(0)

    def add(e, dup, ddn, act):
        for m, lo, hi in ((0, 0, dims.ip), (1, dims.ip, dims.slab)):
            count = dims.quarter * (hi - lo)
            flat = lambda ref: ref[:, lo:hi, :].reshape(count, -1)
            acc[m] += t_dot(flat(e), flat(dup))
            acc[2 + m] += t_dot(flat(ddn), flat(act))

    @pl.when(i == 0)
    def _():
        for m in range(2):
            acc[m] = t_dot(ce[m], cu[m])
            acc[2 + m] = t_dot(cd[m], ca[m])

    for j, refs in enumerate((
        (peer, dup_a, ddn_a, act_a), (own, dup_a, ddn_a, act_a),
        (peer, dup_b, ddn_b, act_b), (own, dup_b, ddn_b, act_b),
    )):
        @pl.when(i == j)
        def _():
            add(*refs)

    @pl.when(i == 3)
    def _():
        out[...] = acc[...].astype(BF16)


def expert_grads(dims, peer, own, act_a, dup_a, ddn_a, act_b, dup_b, ddn_b, ce, ca, cu, cd):
    model = own.shape[-1]
    hidden = act_a.shape[-1]
    slab, quarter = dims.slab, dims.quarter
    assert hidden == model
    half = pl.BlockSpec((quarter, slab, model), lambda i: (jnp.where(i < 2, 1, 0), 0, 0))
    first = pl.BlockSpec((quarter, slab, hidden), lambda i: (jnp.minimum(i, 1), 0, 0))
    last = pl.BlockSpec((quarter, slab, hidden), lambda i: (jnp.maximum(i - 2, 0), 0, 0))
    return pl.pallas_call(
        functools.partial(expert_grads_kernel, dims),
        grid=(4,),
        in_specs=[half, half, first, first, first, last, last, last] + [spec_whole(v) for v in (ce, ca, cu, cd)],
        out_specs=pl.BlockSpec((4, model, hidden), lambda i: (0, 0, 0)),
        scratch_shapes=[pltpu.VMEM((4, model, hidden), F32)],
        out_shape=jax.ShapeDtypeStruct((4, model, hidden), BF16),
        compiler_params=params(),
        cost_estimate=pl.CostEstimate(
            flops=16 * quarter * slab * model * hidden, bytes_accessed=40_000_000, transcendentals=0),
        name="expert_grads",
    )(peer, own, act_a, dup_a, ddn_a, act_b, dup_b, ddn_b, ce, ca, cu, cd)


def own_row(dims, r, p):
    return 8 * (r // 2) + dims.quarter * (r % 2) + p


def class_forward_kernel(dims, near, far, up, up_bias, down, out, rows):
    for m in range(2):
        e = jnp.concatenate([near[2 + m], far[2 + m]], axis=0).astype(BF16)
        rows[m] = e
        u = dot(e, up[m]) + up_bias[m:m + 1]
        out[m] = dot(gelu_low(u), down[m])


def class_forward(dims, near, far, up, up_bias, down):
    shape = (2, 16, near.shape[-1])
    return pl.pallas_call(
        functools.partial(class_forward_kernel, dims),
        out_shape=[jax.ShapeDtypeStruct(shape, F32), jax.ShapeDtypeStruct(shape, BF16)],
        compiler_params=params(),
        cost_estimate=pl.CostEstimate(flops=200_000_000, bytes_accessed=5_000_000, transcendentals=0),
        name="class_forward",
    )(near, far, up, up_bias, down)


def class_final_kernel(dims, order, near, far, d0, d1, d2, d3, vec, out):
    q = dims.quarter
    for m in range(2):
        out[m] = jnp.zeros(out.shape[1:], F32)
        for r in range(4):
            half, at = (near, far)[r // 2], q * (r % 2)
            for p in range(q):
                rows = [d[m, own_row(dims, s, p):own_row(dims, s, p) + 1, :]
                        for d, s in ((d0, r), (d1, r ^ 2), (d2, r ^ 1), (d3, r ^ 3))]
                total = (rows[0] + rows[1]) + (rows[2] + rows[3])
                x = half[m, at + p:at + p + 1, :] + vector(vec, F_SCALE) * (total + vector(vec, F_BIAS + m))
                out[m, pl.ds(4 * order[r] + p, 1), :] = x


def class_final(dims, order, near, far, parts, vec):
    shape = (2, 16, near.shape[-1])
    args = (near, far) + tuple(parts) + (vec,)
    return pl.pallas_call(
        functools.partial(class_final_kernel, dims),
        grid_spec=pltpu.PrefetchScalarGridSpec(
            num_scalar_prefetch=1, grid=(1,),
            in_specs=[spec_whole(v) for v in args],
            out_specs=pl.BlockSpec(shape, lambda i, o: (0, 0, 0)),
        ),
        out_shape=jax.ShapeDtypeStruct(shape, F32),
        compiler_params=params(),
        cost_estimate=pl.CostEstimate(flops=1_000_000, bytes_accessed=1_000_000, transcendentals=0),
        name="class_final",
    )(order, *args)


def class_back_kernel(dims, order, e, cot_a, cot_b, dclass, vec, up, up_bias, down,
                      act, dup, ddown, dexp, bias_grad, dcls, rows):
    q = dims.quarter
    rows[...] = jnp.zeros_like(rows)
    dcls[...] = jnp.zeros_like(dcls)
    for m in range(2):
        for r in range(4):
            cot, base = (cot_b, cot_a)[r % 2], 8 * (1 - r // 2)
            for p in range(q):
                d = dclass[m, pl.ds(4 * order[r] + p, 1), :]
                at = own_row(dims, r, p)
                rows[m, at:at + 1, :] = cot[m, base + p:base + p + 1, :] + d
                if r == 0:
                    dcls[p, m:m + 1, :] = d
        u = dot(e[m], up[m]) + up_bias[m:m + 1]
        big, small = gelu_parts(u)
        act[m] = (u * big).astype(BF16)
        g = (rows[m] * vector(vec, F_SCALE)).astype(BF16)
        ddown[m] = g
        du = dot_t(g, down[m]) * (big + u * small)
        bias_grad[m:m + 1, :] = jnp.sum(du, axis=0, keepdims=True)
        low = du.astype(BF16)
        dup[m] = low
        dexp[m] = dot_t(low, up[m])


def class_back(dims, order, e, cot_a, cot_b, dclass, vec, up, up_bias, down):
    hidden, model = up.shape[-1], e.shape[-1]
    args = (e, cot_a, cot_b, dclass, vec, up, up_bias, down)
    shapes = [((2, 16, hidden), BF16), ((2, 16, hidden), BF16), ((2, 16, model), BF16), ((2, 16, model), F32),
              ((2, hidden), F32), ((dims.quarter, 8, model), F32)]
    return pl.pallas_call(
        functools.partial(class_back_kernel, dims),
        grid_spec=pltpu.PrefetchScalarGridSpec(
            num_scalar_prefetch=1, grid=(1,),
            in_specs=[spec_whole(v) for v in args],
            out_specs=[pl.BlockSpec(s, lambda i, o, n=len(s): (0,) * n) for s, _ in shapes],
            scratch_shapes=[pltpu.VMEM((2, 16, model), F32)],
        ),
        out_shape=[jax.ShapeDtypeStruct(s, t) for s, t in shapes],
        compiler_params=params(),
        cost_estimate=pl.CostEstimate(flops=300_000_000, bytes_accessed=5_000_000, transcendentals=0),
        name="class_back",
    )(order, *args)


def contrast_kernel(dims, total, at, blocks, vec, weight, scale,
                    head_in, dproj, dcls, gains, shifts, scalars, cls, back):
    me = at[0]
    span = blocks[0].shape[0]
    for k, block in enumerate(blocks):
        for j in range(span):
            for m in range(2):
                cls[m, pl.ds(pl.multiple_of(16 * (me ^ (k * span + j)), 16), 16), :] = block[j, m]
    n_rows = cls.shape[1]
    sharp = jnp.exp(scale[...])
    col_at = lax.broadcasted_iota(jnp.int32, (1, n_rows), 1)
    row_at = lax.broadcasted_iota(jnp.int32, (n_rows, 1), 0)
    col_ok = (col_at % 4) < dims.quarter
    row_ok = (row_at % 4) < dims.quarter
    normal, inverse, proj, unit, embed = [], [], [], [], []
    for m in range(2):
        n, r = normalise(cls[m])
        h = (n * vector(vec, H_GAIN + m) + vector(vec, H_SHIFT + m)).astype(BF16)
        head_in[m] = h
        y = dot(h, weight[m])
        u = lax.rsqrt(jnp.sum(y * y, axis=-1, keepdims=True) + 1e-6)
        normal.append(n)
        inverse.append(r)
        proj.append(y)
        unit.append(u)
        embed.append((y * u).astype(BF16))
    ok = row_ok & col_ok
    logits = sharp * dot_t(embed[0], embed[1])
    masked = jnp.where(ok, logits, -1e30)
    row_max = jnp.max(masked, axis=1, keepdims=True)
    row_lse = row_max + jnp.log(jnp.sum(jnp.exp(masked - row_max), axis=1, keepdims=True))
    col_max = jnp.max(masked, axis=0, keepdims=True)
    col_lse = col_max + jnp.log(jnp.sum(jnp.exp(masked - col_max), axis=0, keepdims=True))
    same = (row_at == col_at) & ok
    both = jnp.exp(masked - row_lse) + jnp.exp(masked - col_lse)
    dlogits = jnp.where(ok, jnp.where(same, both - 2.0, both) * (1.0 / (2 * total)), 0.0)
    diagonal = jnp.sum(jnp.where(same, logits, 0.0), axis=1, keepdims=True)
    rows = jnp.where(row_ok, row_lse - 2.0 * diagonal, 0.0)
    cols = jnp.where(col_ok, col_lse, 0.0)
    loss = (jnp.sum(rows, axis=0, keepdims=True) + jnp.sum(cols, axis=1, keepdims=True)) * (1.0 / (2 * total))
    slope = jnp.sum(jnp.sum(dlogits * logits, axis=1, keepdims=True), axis=0, keepdims=True)
    scalars[0:1, :] = jnp.broadcast_to(loss, (1, 128))
    scalars[1:2, :] = jnp.broadcast_to(slope, (1, 128))
    high = lax.Precision.HIGHEST
    wide = [e.astype(F32) for e in embed]
    dembed = [
        sharp * jnp.dot(dlogits, wide[1], precision=high, preferred_element_type=F32),
        sharp * lax.dot_general(dlogits, wide[0], (((0,), (0,)), ((), ())), precision=high,
                                preferred_element_type=F32),
    ]
    for m in range(2):
        u, y, d = unit[m], proj[m], dembed[m]
        dp = (u * d - u * u * u * y * jnp.sum(y * d, axis=-1, keepdims=True)).astype(BF16)
        dproj[m] = dp
        dh = dot_t(dp, weight[m])
        gains[m:m + 1, :] = jnp.sum(dh * normal[m], axis=0, keepdims=True)
        shifts[m:m + 1, :] = jnp.sum(dh, axis=0, keepdims=True)
        back[m] = norm_back(normal[m], inverse[m], dh * vector(vec, H_GAIN + m))
        dcls[m] = back[m, pl.ds(pl.multiple_of(16 * me, 16), 16), :]


def contrast(dims, total, at, blocks, vec, weight, scale):
    model = weight.shape[1]
    rows = 16 * len(blocks) * blocks[0].shape[0]
    args = tuple(blocks) + (vec, weight, scale)
    shapes = [((2, rows, model), BF16), ((2, rows, weight.shape[2]), BF16), ((2, 16, model), F32),
              ((2, model), F32), ((2, model), F32), ((2, 128), F32)]

    def kernel(at, *refs):
        contrast_kernel(dims, total, at, refs[:len(blocks)], *refs[len(blocks):])

    return pl.pallas_call(
        kernel,
        grid_spec=pltpu.PrefetchScalarGridSpec(
            num_scalar_prefetch=1, grid=(1,),
            in_specs=[spec_whole(v) for v in args],
            out_specs=[pl.BlockSpec(s, lambda i, o, n=len(s): (0,) * n) for s, _ in shapes],
            scratch_shapes=[pltpu.VMEM((2, rows, model), F32)] * 2,
        ),
        out_shape=[jax.ShapeDtypeStruct(s, t) for s, t in shapes],
        compiler_params=params(),
        cost_estimate=pl.CostEstimate(flops=1_000_000_000, bytes_accessed=5_000_000, transcendentals=0),
        name="contrast",
    )(at, *args)


def contrast_large(dims, total, at, blocks, vec, weight, scale):
    model = weight.shape[1]
    held = jnp.concatenate(blocks)
    held = held[jnp.arange(held.shape[0]) ^ at[0]]
    rows = jnp.asarray([r for r in range(16) if r % 4 < dims.quarter])
    cls = jnp.transpose(held[:, :, rows], (1, 0, 2, 3)).reshape(2, -1, model)
    gain, shift = vec[H_GAIN:H_GAIN + 2, None], vec[H_SHIFT:H_SHIFT + 2, None]
    n, r = normalise(cls)
    head_in = (n * gain + shift).astype(BF16)
    proj = jnp.einsum("mrc,mce->mre", head_in, weight, preferred_element_type=F32)
    unit = lax.rsqrt(jnp.sum(proj * proj, axis=-1, keepdims=True) + 1e-6)
    embed = (proj * unit).astype(BF16)
    sharp = jnp.exp(scale[0, 0])
    logits = sharp * dot_t(embed[0], embed[1])
    row_lse = jax.nn.logsumexp(logits, axis=1, keepdims=True)
    col_lse = jax.nn.logsumexp(logits, axis=0, keepdims=True)
    dlogits = jnp.exp(logits - row_lse) + jnp.exp(logits - col_lse) - 2.0 * jnp.eye(total, dtype=F32)
    dlogits = dlogits / (2 * total)
    loss = (jnp.sum(row_lse) + jnp.sum(col_lse) - 2.0 * jnp.trace(logits)) / (2 * total)
    slope = jnp.sum(dlogits * logits)
    high = lax.Precision.HIGHEST
    wide = embed.astype(F32)
    dembed = sharp * jnp.stack([
        jnp.dot(dlogits, wide[1], precision=high, preferred_element_type=F32),
        jnp.dot(dlogits.T, wide[0], precision=high, preferred_element_type=F32)])
    dproj = (unit * dembed - unit ** 3 * proj * jnp.sum(proj * dembed, axis=-1, keepdims=True)).astype(BF16)
    dh = jnp.einsum("mre,mce->mrc", dproj, weight, preferred_element_type=F32)
    back = norm_back(n, r, dh * gain)
    pairs = 4 * dims.quarter
    own = lax.dynamic_slice_in_dim(back, at[0] * pairs, pairs, axis=1)
    dcls = jnp.zeros((2, 16, model), F32).at[:, rows].set(own)
    scalars = jnp.broadcast_to(jnp.stack([loss, slope])[:, None], (2, 128))
    return head_in, dproj, dcls, jnp.sum(dh * n, axis=1), jnp.sum(dh, axis=1), scalars


def own_pair(rows_of):
    return lambda i, o: (o[0] * rows_of + i, 0, 0)


def own_call(kernel, dims, name, order, blocks, img, txt, others, outs, scratch):
    model = img.shape[-1]
    block = pl.BlockSpec((1, dims.slab, model), lambda i, o: (i, 0, 0))
    specs = {
        "slab": (block, (dims.quarter, dims.slab, model)),
        "img": (pl.BlockSpec((1, dims.patches, model), lambda i, o: (i, 0, 0)), (dims.quarter, dims.patches, model)),
        "txt": (pl.BlockSpec((1, dims.caption, model), lambda i, o: (i, 0, 0)), (dims.quarter, dims.caption, model)),
        "sums": (pl.BlockSpec((8, model), lambda i, o: (0, 0)), (8, model)),
    }
    return pl.pallas_call(
        functools.partial(kernel, dims),
        grid_spec=pltpu.PrefetchScalarGridSpec(
            num_scalar_prefetch=1,
            grid=(dims.quarter,),
            in_specs=[block] * len(blocks) + [
                pl.BlockSpec((1, dims.patches, model), own_pair(dims.quarter)),
                pl.BlockSpec((1, dims.caption, model), own_pair(dims.quarter)),
            ] + [spec_whole(v) for v in others],
            out_specs=[specs[kind][0] for kind, _ in outs],
            scratch_shapes=[pltpu.VMEM((dims.slab, model), F32)] * scratch,
        ),
        out_shape=[jax.ShapeDtypeStruct(specs[kind][1], dtype) for kind, dtype in outs],
        compiler_params=params(),
        cost_estimate=pl.CostEstimate(flops=40_000_000, bytes_accessed=15_000_000, transcendentals=0),
        name=name,
    )(order, *blocks, img, txt, *others)


def start_own(rows, sums):
    @pl.when(pl.program_id(0) == 0)
    def _():
        rows[...] = jnp.zeros_like(rows)
        sums[...] = jnp.zeros_like(sums)


def add_class(dims, dcls, rows):
    i = pl.program_id(0)
    rows[0:1, :] += dcls[i, 0:1, :]
    rows[dims.ip:dims.ip + 1, :] += dcls[i, 1:2, :]


def final_kernel(dims, order, keep, recv, far, attended, img, txt, dcls, vec, fin_img, fin_txt, sums, rows):
    start_own(rows, sums)
    load_rows(dims, 0, img, txt, rows)
    add_class(dims, dcls, rows)
    for m, lo, hi in ((0, 0, dims.ip), (1, dims.ip, dims.slab)):
        b = keep[0, lo:hi].astype(F32) + recv[0, lo:hi].astype(F32) + far[0, lo:hi].astype(F32)
        b = b + vector(vec, F_BIAS + m)
        f = attended[0, lo:hi, :] + vector(vec, F_SCALE) * b
        if m == 0:
            fin_img[0] = f[0:dims.patches].astype(BF16)
        else:
            fin_txt[0] = f[0:dims.caption].astype(BF16)
        g = rows[lo:hi, :]
        sums[0:1, :] += jnp.sum(g * b, axis=0, keepdims=True)
        sums[1 + m:2 + m, :] += jnp.sum(g, axis=0, keepdims=True) * vector(vec, F_SCALE)


def final_rows(dims, order, keep, recv, far, attended, img, txt, dcls, vec):
    return own_call(final_kernel, dims, "final_rows", order, (keep, recv, far, attended), img, txt,
                    (dcls, vec), (("img", BF16), ("txt", BF16), ("sums", F32)), 1)


def norm_two_kernel(dims, order, keep, recv, far, attended, a_keep, a_recv, img, txt, dcls, x0, x1, x2, x3,
                    vec, dattended, dattn, sums, rows, ups):
    i = pl.program_id(0)
    start_own(rows, sums)
    load_rows(dims, 0, img, txt, rows)
    add_class(dims, dcls, rows)
    ups[...] = keep[0].astype(F32) + recv[0].astype(F32) + far[0].astype(F32)
    for m, at in ((0, 0), (1, dims.ip)):
        extra = [x[m, pl.ds(own_row(dims, r, 0) + i, 1), :] for x, r in ((x0, 0), (x1, 2), (x2, 1), (x3, 3))]
        ups[at:at + 1, :] += (extra[0] + extra[1]) + (extra[2] + extra[3])
    for m, lo, hi in ((0, 0, dims.ip), (1, dims.ip, dims.slab)):
        n, r = normalise(attended[0, lo:hi, :])
        dy = ups[lo:hi, :]
        sums[m:m + 1, :] += jnp.sum(dy * n, axis=0, keepdims=True)
        sums[2 + m:3 + m, :] += jnp.sum(dy, axis=0, keepdims=True)
        d = rows[lo:hi, :] + norm_back(n, r, dy * vector(vec, GAIN2 + m))
        dattended[0, lo:hi, :] = d
        sd = d * vector(vec, A_SCALE)
        dattn[0, lo:hi, :] = sd.astype(BF16)
        a = a_keep[0, lo:hi, :].astype(F32) + a_recv[0, lo:hi, :].astype(F32) + vector(vec, A_BIAS)
        sums[4:5, :] += jnp.sum(d * a, axis=0, keepdims=True)
        sums[5:6, :] += jnp.sum(sd, axis=0, keepdims=True)


def norm_two(dims, order, keep, recv, far, attended, a_keep, a_recv, img, txt, dcls, parts, vec):
    return own_call(norm_two_kernel, dims, "norm_two", order, (keep, recv, far, attended, a_keep, a_recv), img, txt,
                    (dcls,) + tuple(parts) + (vec,), (("slab", F32), ("slab", BF16), ("sums", F32)), 2)


def norm_one_kernel(dims, order, keep, recv, dattended, img, txt, vec, d_img, d_txt, sums, rows):
    start_own(rows, sums)
    load_rows(dims, 0, img, txt, rows)
    n, r = normalise(rows[...])
    dy = keep[0].astype(F32) + recv[0].astype(F32)
    sums[0:1, :] += jnp.sum(dy * n, axis=0, keepdims=True)
    sums[1:2, :] += jnp.sum(dy, axis=0, keepdims=True)
    d = dattended[0] + norm_back(n, r, dy * vector(vec, GAIN1))
    d_img[0] = d[0:dims.patches].astype(BF16)
    d_txt[0] = d[dims.ip:dims.ip + dims.caption].astype(BF16)


def norm_one(dims, order, keep, recv, dattended, img, txt, vec):
    return own_call(norm_one_kernel, dims, "norm_one", order, (keep, recv, dattended), img, txt,
                    (vec,), (("img", BF16), ("txt", BF16), ("sums", F32)), 1)


def back_step(dims, tiles, lens, whose, dattn, normed, qkv, mixed, dmixed, dqkv, acc, col_sums, w, ow):
    quarter, slab = dims.quarter, dims.slab
    count, width = quarter * slab, tiles * 128
    model = normed.shape[-1]
    d_rows = dattn[...].reshape(count, model)
    dmixed[...] = dot_t(d_rows, ow[...]).astype(BF16).reshape(quarter, slab, width)

    def one_pair(p, c):
        length = lens[whose * quarter + p]
        for lo, hi, start, limit in key_tail(dims, length):
            for g in range(tiles):
                at = [slice((t * tiles + g) * 128, (t * tiles + g + 1) * 128) for t in range(3)]
                q, k, v = [qkv[p, lo:hi, c] for c in at]
                q = scaled(q)
                qq = split_pair(q)
                dd = split_pair(dmixed[p, lo:hi, g * 128:(g + 1) * 128])
                w_ = softmax_keys(hide(dot_t(k, qq), start, limit))
                dw = dot_t(v, dd)
                dqkv[p, lo:hi, at[2]] = dot(w_.astype(BF16), dd).astype(BF16)
                ds = (w_ * (dw - jnp.sum(w_ * dw, axis=0, keepdims=True))).astype(BF16)
                dqkv[p, lo:hi, at[1]] = dot(ds, qq).astype(BF16)
                dqkv[p, lo:hi, at[0]] = (join_pair(t_dot(ds, k)) * HEAD_DIM ** -0.5).astype(BF16)
        return c

    lax.fori_loop(0, quarter, one_pair, 0)
    dp = dqkv[...].reshape(count, 3 * width)
    part = dot(dp, w[...])
    acc[:, 0:3 * width] += t_dot(normed[...].reshape(count, model), dp)
    acc[:, 3 * width:] += t_dot(d_rows, mixed[...].reshape(count, width))
    col_sums[...] += jnp.sum(dp.astype(F32), axis=0, keepdims=True)
    return part


def attend_back_kernel(dims, far, order, lens, d_own, d_peer, normed, qkv, mixed, wq, wo, wf, *refs):
    if not far:
        prior_keep, prior_send, *refs = refs
    keep, send, grad, *refs = refs
    if far:
        grad_rest, *refs = refs
    col_sums, dattn, dmixed, dqkv, acc, w, ow = refs
    i = pl.program_id(0)
    slab, quarter, local = dims.slab, dims.quarter, dims.local
    two, one_head = parts_of(dims)
    tiles = 2 if far else 1
    width = tiles * two
    count = quarter * slab
    model = normed.shape[-1]

    @pl.when(i == 0)
    def _():
        dattn[...] = d_own[...]
        acc[...] = jnp.zeros_like(acc)
        col_sums[...] = jnp.zeros_like(col_sums)
        for t in range(4):
            dst, at = (w, t * width) if t < 3 else (ow, 0)
            own, start = (wq, t * local) if t < 3 else (wo, 0)
            if far:
                copy_rows(dst, at, wf, t * local, two)
                copy_rows(dst, at + two, own, start + two, one_head)
                copy_rows(dst, at + two + one_head, wf, t * local + two, one_head)
            else:
                copy_rows(dst, at, own, start, two)

    @pl.when(i == 1)
    def _():
        dattn[...] = d_peer[...]

    part = back_step(dims, tiles, lens, order[2 * i], dattn, normed, qkv, mixed,
                     dmixed, dqkv, acc, col_sums, w, ow)

    @pl.when(i == 0)
    def _():
        prior = 0.0 if far else prior_keep[...].reshape(count, model).astype(F32)
        keep[...] = (part + prior).astype(BF16).reshape(quarter, slab, model)

    @pl.when(i == 1)
    def _():
        prior = 0.0 if far else prior_send[...].reshape(count, model).astype(F32)
        send[...] = (part + prior).astype(BF16).reshape(quarter, slab, model)
        for t in range(4):
            grad[:, t * two:(t + 1) * two] = acc[:, t * width:t * width + two].astype(BF16)
            if far:
                at = t * width + two
                to = 4 * two + t * one_head
                grad[:, to:to + one_head] = acc[:, at + one_head:at + two].astype(BF16)
                grad_rest[:, t * one_head:(t + 1) * one_head] = acc[:, at:at + one_head].astype(BF16)


def attend_back(dims, far, order, lens, d_own, d_peer, normed, qkv, mixed, wq, wo, wf, prior=()):
    model = normed.shape[-1]
    slab, quarter = dims.slab, dims.quarter
    width = 256 if far else 128
    one = pl.BlockSpec((quarter, slab, model), lambda i, o, n: (0, 0, 0))
    stride = normed.shape[0] // (2 * quarter)
    step = lambda cols: pl.BlockSpec((quarter, slab, cols), lambda i, o, n: (stride * i, 0, 0))
    grads = (768, 256) if far else (512,)
    specs = [one, one] + [pl.BlockSpec((model, n), lambda i, o, n_: (0, 0)) for n in grads]
    specs += [pl.BlockSpec((1, 3 * width), lambda i, o, n: (0, 0))]
    shapes = [
        jax.ShapeDtypeStruct((quarter, slab, model), BF16),
        jax.ShapeDtypeStruct((quarter, slab, model), BF16),
    ] + [jax.ShapeDtypeStruct((model, n), BF16) for n in grads] + [jax.ShapeDtypeStruct((1, 3 * width), F32)]
    scratch = [
        pltpu.VMEM((quarter, slab, model), BF16),
        pltpu.VMEM((quarter, slab, width), BF16),
        pltpu.VMEM((quarter, slab, 3 * width), BF16),
        pltpu.VMEM((model, 4 * width), F32),
        pltpu.VMEM((3 * width, model), BF16),
        pltpu.VMEM((width, model), BF16),
    ]
    return pl.pallas_call(
        functools.partial(attend_back_kernel, dims, far),
        grid_spec=pltpu.PrefetchScalarGridSpec(
            num_scalar_prefetch=2,
            grid=(2,),
            in_specs=[one, one, step(model), step(3 * width), step(width), spec_whole(wq), spec_whole(wo),
                      spec_whole(wf)] + [one] * len(prior),
            out_specs=specs,
            scratch_shapes=scratch,
        ),
        out_shape=shapes,
        compiler_params=params(),
        cost_estimate=pl.CostEstimate(
            flops=32 * quarter * slab * model * width, bytes_accessed=20_000_000, transcendentals=0),
        name="attend_back_far" if far else "attend_back_own",
    )(order, lens, d_own, d_peer, normed, qkv, mixed, wq, wo, wf, *prior)


def swap(value, axis, bit):
    size = lax.axis_size(axis)
    return lax.ppermute(value, axis, [(j, j ^ bit) for j in range(size)])


def to_core(value):
    return swap(value, "mp", 1)


def to_y(value):
    return swap(value, "mp", 2)


def from_others(value, axis, first, count):
    return [value] + [swap(value, axis, k * first) for k in range(1, count)]


def add_tree(parts):
    while len(parts) > 1:
        parts = [a + b for a, b in zip(parts[::2], parts[1::2])]
    return parts[0]


def sum_over(value, axis):
    first = 1
    while first < lax.axis_size(axis):
        count = min(8, lax.axis_size(axis) // first)
        value = add_tree(from_others(value, axis, first, count))
        first *= count
    return value


def gather_batch(value):
    parts = [value]
    first = 1
    size = lax.axis_size("batch")
    while first < size:
        count = min(8, size // first)
        whole = jnp.concatenate(parts) if len(parts) > 1 else parts[0]
        parts = from_others(whole, "batch", first, count)
        first *= count
    return parts


def gather_rows(own, me):
    near = jnp.stack([own, to_y(own)])
    far = to_core(near)
    out = jnp.zeros((4,) + own.shape, own.dtype)
    for r, value in enumerate((near[0], near[1], far[0], far[1])):
        out = lax.dynamic_update_slice(out, value[None], (me ^ ORDER[r],) + (0,) * own.ndim)
    return out.reshape((4 * own.shape[0],) + own.shape[1:])


def add_low(a, b):
    return (a.astype(F32) + b.astype(F32)).astype(BF16)


MESH = pl.DeviceIdType.MESH


class Place:
    def __init__(self):
        self.b, self.m = lax.axis_index("batch"), lax.axis_index("mp")
        self.z, self.x = self.b // 2, self.b % 2
        self.y, self.c = self.m // 2, self.m % 2
        self.core = (self.b, 2 * self.y + 1 - self.c)
        self.near = (self.b, 2 * (1 - self.y) + self.c)
        self.across = (self.b, 2 * (1 - self.y) + 1 - self.c)
        self.side = (2 * self.z + 1 - self.x, self.m)
        self.along = [(2 * ((self.z + k) % 4) + self.x, self.m) for k in range(1, 4)]
        self.batch = [((self.b + k) % 8, self.m) for k in range(1, 8)]

    def quarter(self, far_y, far_core):
        return 2 * ((self.y + far_y) % 2) + (self.c + far_core) % 2


def meet(peers):
    barrier = pltpu.get_barrier_semaphore()
    for peer in peers:
        pl.semaphore_signal(barrier, inc=1, device_id=peer, device_id_type=MESH)
    pl.semaphore_wait(barrier, len(peers))


def remote(src, dst, send_sem, recv_sem, at, device):
    return pltpu.make_async_remote_copy(
        src_ref=src, dst_ref=dst, send_sem=send_sem.at[at], recv_sem=recv_sem.at[at],
        device_id=device, device_id_type=MESH)


def front_kernel(dims, lens, img, txt, vectors, bias, own_w, own_o,
                 vec, normed, qkv, mixed, qkv_far, mixed_far, far_w, attended, attn, expert, expert_peer, cls, cls_peer,
                 rows, w, w2, ow, b, wf, far_bias, n_all, rest, m_all, m_far, q_own, q_far, a_send, a_recv, e_send, c_recv,
                 local_sem, send_sem, recv_sem):
    here = Place()
    i = pl.program_id(0)
    local, quarter, slab, ip = dims.local, dims.quarter, dims.slab, dims.ip
    two, one_head = parts_of(dims)
    count = quarter * slab
    model = img.shape[-1]
    at = i % 4
    whose = here.quarter(at % 2, 1 - at // 2)
    sent_w = [remote(own_w, wf.at[pl.ds(0, 3 * local)], send_sem, recv_sem, 0, here.near),
              remote(own_o, wf.at[pl.ds(3 * local, local)], send_sem, recv_sem, 1, here.near),
              remote(bias, far_bias, send_sem, recv_sem, 2, here.near)]
    sent_a = [remote(a_send.at[j], a_recv.at[j], send_sem, recv_sem, 3 + j, here.core) for j in range(2)]

    def e_over(j):
        return remote(e_send.at[j], expert_peer.at[j], send_sem, recv_sem, 5 + j, here.core)

    def e_here(j):
        return pltpu.make_async_copy(e_send.at[j], expert.at[j], local_sem.at[1 + j])

    sent_c = remote(cls, c_recv, send_sem, recv_sem, 5 + 2 * quarter, here.core)
    keep_w = pltpu.make_async_copy(wf, far_w, local_sem.at[0])
    sent_e = [e_over(j) for j in range(2 * quarter)]
    keep_e = [e_here(j) for j in range(2 * quarter)]

    @pl.when(i == 0)
    def _():
        meet([here.core, here.near])
        for copy in sent_w:
            copy.start()
        fill(vec, vectors)
        rows[...] = jnp.zeros_like(rows)
        b[...] = jnp.zeros_like(b)
        w[...] = jnp.zeros_like(w)
        cls[...] = jnp.zeros_like(cls)
        for t in range(3):
            copy_rows(w, t * 2 * two, own_w, t * local, local)
        b[0:1, 0:local] = bias[0:1, :]
        b[0:1, 4 * two:4 * two + local] = bias[1:2, :]

    def project(weights):
        proj = dot_t(n_all[at].reshape(count, model), weights[...]) + b[0:1, :]
        return proj.astype(BF16).reshape(quarter, slab, 6 * two)

    @pl.when(i < 4)
    def _():
        def one_norm(p, c):
            load_rows(dims, p, img, txt, rows)
            n, _ = normalise(rows[...])
            n_all[at, p] = (n * vector(vec, GAIN1) + vector(vec, SHIFT1)).astype(BF16)
            return c

        lax.fori_loop(0, quarter, one_norm, 0)
        proj = project(w)
        for t in range(3):
            q_own[:, :, t * two:(t + 1) * two] = proj[:, :, 2 * t * two:(2 * t + 1) * two]
            rest[at, :, :, t * two:(t + 1) * two] = proj[:, :, (2 * t + 1) * two:(2 * t + 2) * two]
        attend_tiles(dims, lens, whose, q_own, m_all.at[at])

        @pl.when(i % 2 == 0)
        def _():
            normed[...] = n_all[at]
            qkv[...] = q_own[...]
            mixed[...] = m_all[at]

    @pl.when(i == 4)
    def _():
        for copy in sent_w:
            copy.wait_recv()
        keep_w.start()
        w2[...] = jnp.zeros_like(w2)
        b[...] = jnp.zeros_like(b)
        for t in range(3):
            copy_rows(w2, t * 2 * two, wf, t * local, two)
            copy_rows(w2, t * 2 * two + two + one_head, wf, t * local + two, one_head)
        for t, to in ((0, 0), (1, 4 * two)):
            b[0:1, to:to + two] = far_bias[t:t + 1, 0:two]
            b[0:1, to + two + one_head:to + 2 * two] = far_bias[t:t + 1, two:]
        copy_rows(ow, 0, own_o, 0, two)
        copy_rows(ow, two, wf, 3 * local, two)
        copy_rows(ow, 2 * two, own_o, two, one_head)
        copy_rows(ow, 2 * two + one_head, wf, 3 * local + two, one_head)

    @pl.when(i >= 4)
    def _():
        proj = project(w2)
        for t in range(3):
            to = 2 * t * two
            q_far[:, :, to:to + two] = proj[:, :, to:to + two]
            q_far[:, :, to + two:to + 2 * two] = (
                proj[:, :, to + two:to + 2 * two] + rest[at, :, :, t * two:(t + 1) * two])
        attend_tiles(dims, lens, whose, q_far, m_far)

        @pl.when(i % 2 == 0)
        def _():
            qkv_far[...] = q_far[...]
            mixed_far[...] = m_far[...]

        part = dot(m_all[at].reshape(count, two), ow[0:two, :])
        part = part + dot(m_far[...].reshape(count, 2 * two), ow[two:, :])
        part = part.reshape(quarter, slab, model)

        @pl.when(i < 6)
        def _():
            a_send[at] = part.astype(BF16)

        for j in range(2):
            @pl.when(i == 4 + j)
            def _():
                sent_a[j].start()

        for j in range(2):
            @pl.when(i == 6 + j)
            def _():
                sent_a[j].wait_recv()

        @pl.when(i >= 6)
        def _():
            j = i - 6
            for p in range(quarter):
                load_rows(dims, p, img, txt, rows)
                a = part[p] + a_recv[j, p].astype(F32)
                x = rows[...] + vector(vec, A_SCALE) * (a + vector(vec, A_BIAS))
                n, _ = normalise(x)
                e_img = n[0:ip] * vector(vec, GAIN2) + vector(vec, SHIFT2)
                e_txt = n[ip:] * vector(vec, GAIN2 + 1) + vector(vec, SHIFT2 + 1)
                r = j * quarter + p
                e_send[r, 0:ip, :] = e_img.astype(BF16)
                e_send[r, ip:, :] = e_txt.astype(BF16)
                e_over(r).start()
                e_here(r).start()
                for k, v in enumerate((x[0:1], x[ip:ip + 1], e_img[0:1], e_txt[0:1])):
                    cls[k, pl.ds(r, 1), :] = v

                @pl.when(j == 0)
                def _():
                    attended[p] = x
                    attn[p] = a


    @pl.when(i == 7)
    def _():
        sent_c.start()
        keep_w.wait()
        for copy in keep_e:
            copy.wait()
        sent_c.wait()
        cls_peer[...] = c_recv[...]
        for copy in sent_e:
            copy.wait()
        for copy in sent_w + sent_a:
            copy.wait_send()


def fill(table, vectors):
    table[...] = jnp.zeros_like(table)
    at = 0
    for v in vectors:
        n = v.shape[0] if len(v.shape) == 2 else 1
        table[at:at + n, :] = v[...].reshape(n, table.shape[1])
        at += n


def front(dims, lens, img, txt, vectors, bias, own_w, own_o):
    model = img.shape[-1]
    quarter, slab, local = dims.quarter, dims.slab, dims.local
    held = pl.BlockSpec(memory_space=pltpu.VMEM)
    away = pl.BlockSpec(memory_space=pl.ANY)

    def states_at(i):
        return Place().quarter(i % 2, 1 - i % 4 // 2), 0, 0

    own_block = lambda cols: pl.BlockSpec((quarter, slab, cols), lambda i: (jnp.where(i < 2, 1, 0), 0, 0))
    far_block = lambda cols: pl.BlockSpec((quarter, slab, cols), lambda i: (jnp.where(i < 6, 1, 0), 0, 0))
    six = lambda cols: jax.ShapeDtypeStruct((2 * quarter, slab, cols), BF16)
    block = lambda cols: (quarter, slab, cols)
    n_remote = 6 + 2 * quarter
    return pl.pallas_call(
        lambda lens, img, txt, *refs: front_kernel(
            dims, lens, img, txt, refs[:len(vectors)], *refs[len(vectors):]),
        grid=(8,),
        in_specs=[pl.BlockSpec(memory_space=pltpu.SMEM),
                  pl.BlockSpec((quarter, dims.patches, model), states_at),
                  pl.BlockSpec((quarter, dims.caption, model), states_at)] + [held] * (3 + len(vectors)),
        out_specs=[held, own_block(model), own_block(384), own_block(128), far_block(768), far_block(256),
                   away, held, held, away, away, held, held],
        out_shape=[jax.ShapeDtypeStruct((16, model), F32), six(model), six(384), six(128), six(768), six(256),
                   jax.ShapeDtypeStruct((4 * local, model), BF16),
                   jax.ShapeDtypeStruct(block(model), F32), jax.ShapeDtypeStruct(block(model), F32),
                   six(model), six(model),
                   jax.ShapeDtypeStruct((4, 8, model), F32), jax.ShapeDtypeStruct((4, 8, model), F32)],
        scratch_shapes=[
            pltpu.VMEM((slab, model), F32), pltpu.VMEM((768, model), BF16), pltpu.VMEM((768, model), BF16),
            pltpu.VMEM((384, model), BF16), pltpu.VMEM((8, 768), F32), pltpu.VMEM((4 * local, model), BF16),
            pltpu.VMEM((2, local), F32),
            pltpu.VMEM((4,) + block(model), BF16), pltpu.VMEM((4,) + block(384), BF16),
            pltpu.VMEM((4,) + block(128), BF16), pltpu.VMEM(block(256), BF16),
            pltpu.VMEM(block(384), BF16), pltpu.VMEM(block(768), BF16),
            pltpu.VMEM((2,) + block(model), BF16), pltpu.VMEM((2,) + block(model), BF16),
            pltpu.VMEM((2 * quarter, slab, model), BF16), pltpu.VMEM((4, 8, model), F32),
            pltpu.SemaphoreType.DMA((1 + 2 * quarter,)),
            pltpu.SemaphoreType.DMA((n_remote,)), pltpu.SemaphoreType.DMA((n_remote,)),
        ],
        compiler_params=params(collective_id=6, has_side_effects=True),
        cost_estimate=pl.CostEstimate(
            flops=16 * quarter * slab * model * 1152, bytes_accessed=40_000_000, transcendentals=0),
        name="front",
    )(lens, img, txt, *vectors, bias, own_w, own_o)


def middle_kernel(dims, total, img, txt, own, peer, cls_own, cls_peer, vec, up, up_bias, down, weight, scale,
                  act, dup, ddn, dexp, d_own, d_near, bias_grad, class_e, c_act, c_dup, c_ddn, dcls,
                  head_in, dproj, gains, shifts, scalars,
                  bx, bd, rx, rd, x_near, x_far, ins, rows, part, parts, cls, back, cot, c_rows, extra, extras,
                  send_sem, recv_sem):
    here = Place()
    ip, slab, quarter = dims.ip, dims.slab, dims.quarter
    i = pl.program_id(0)
    model = own.shape[-1]
    mp_peers = [here.core, here.near, here.across]
    of = [here.quarter(0, 0), here.quarter(1, 0), here.quarter(0, 1), here.quarter(1, 1)]

    sent_x = [remote(bx.at[2 * j], rx.at[j], send_sem, recv_sem, j, here.core) for j in range(2)]
    sent_d = [remote(bd.at[2 * j], rd.at[j], send_sem, recv_sem, 2 + j, here.core) for j in range(2)]
    sent_near = remote(x_near, x_far, send_sem, recv_sem, 4, here.near)
    sent_part = [remote(part, parts.at[k], send_sem, recv_sem, 5 + k, mp_peers[k]) for k in range(3)]
    sent_extra = [remote(extra, extras.at[k], send_sem, recv_sem, 8 + k, mp_peers[k]) for k in range(3)]
    sent_cls = [remote(cls.at[here.b], cls.at[here.b], send_sem, recv_sem, 11 + k, here.batch[k]) for k in range(7)]

    @pl.when(i == 0)
    def _():
        rows[...] = jnp.zeros_like(rows)
        bias_grad[...] = jnp.zeros_like(bias_grad)
        for m in range(2):
            e = jnp.concatenate([cls_own[2 + m], cls_peer[2 + m]], axis=0).astype(BF16)
            class_e[m] = e
            u = dot(e, up[m]) + up_bias[m:m + 1]
            part[m] = dot(gelu_low(u), down[m])
        meet(mp_peers + here.batch)
        for copy in sent_part:
            copy.start()
        ins[...] = peer[quarter:, :, :]

    @pl.when(i == 1)
    def _():
        for copy in sent_part:
            copy.wait_recv()
        for m in range(2):
            cls[here.b, m] = jnp.zeros(cls.shape[2:], F32)
            for r in range(4):
                half, at = (cls_own, cls_peer)[r // 2], quarter * (r % 2)
                for p in range(quarter):
                    line = [d[m, own_row(dims, s, p):own_row(dims, s, p) + 1, :]
                            for d, s in ((part, r), (parts.at[0], r ^ 2), (parts.at[1], r ^ 1), (parts.at[2], r ^ 3))]
                    x = (line[0] + line[1]) + (line[2] + line[3]) + vector(vec, F_BIAS + m)
                    x = half[m, at + p:at + p + 1, :] + vector(vec, F_SCALE) * x
                    cls[here.b, m, pl.ds(4 * of[r] + p, 1), :] = x
        for copy in sent_cls:
            copy.start()
        ins[...] = own[quarter:, :, :]

    @pl.when(i == 2)
    def _():
        ins[...] = peer[:quarter, :, :]

    @pl.when(i == 3)
    def _():
        ins[...] = own[:quarter, :, :]
        for copy in sent_cls:
            copy.wait_recv()
        n_rows = 16 * cls.shape[0]
        sharp = jnp.exp(scale[...])
        col_at = lax.broadcasted_iota(jnp.int32, (1, n_rows), 1)
        row_at = lax.broadcasted_iota(jnp.int32, (n_rows, 1), 0)
        col_ok = (col_at % 4) < quarter
        row_ok = (row_at % 4) < quarter
        normal, inverse, proj, unit, embed = [], [], [], [], []
        for m in range(2):
            n, r = normalise(cls[:, m].reshape(n_rows, model))
            h = (n * vector(vec, H_GAIN + m) + vector(vec, H_SHIFT + m)).astype(BF16)
            head_in[m] = h
            y = dot(h, weight[m])
            u = lax.rsqrt(jnp.sum(y * y, axis=-1, keepdims=True) + 1e-6)
            normal.append(n)
            inverse.append(r)
            proj.append(y)
            unit.append(u)
            embed.append((y * u).astype(BF16))
        ok = row_ok & col_ok
        logits = sharp * dot_t(embed[0], embed[1])
        masked = jnp.where(ok, logits, -1e30)
        row_max = jnp.max(masked, axis=1, keepdims=True)
        row_lse = row_max + jnp.log(jnp.sum(jnp.exp(masked - row_max), axis=1, keepdims=True))
        col_max = jnp.max(masked, axis=0, keepdims=True)
        col_lse = col_max + jnp.log(jnp.sum(jnp.exp(masked - col_max), axis=0, keepdims=True))
        same = (row_at == col_at) & ok
        both = jnp.exp(masked - row_lse) + jnp.exp(masked - col_lse)
        dlogits = jnp.where(ok, jnp.where(same, both - 2.0, both) * (1.0 / (2 * total)), 0.0)
        diagonal = jnp.sum(jnp.where(same, logits, 0.0), axis=1, keepdims=True)
        lines = jnp.sum(jnp.where(row_ok, row_lse - 2.0 * diagonal, 0.0), axis=0, keepdims=True)
        lines = lines + jnp.sum(jnp.where(col_ok, col_lse, 0.0), axis=1, keepdims=True)
        slope = jnp.sum(jnp.sum(dlogits * logits, axis=1, keepdims=True), axis=0, keepdims=True)
        scalars[0:1, :] = jnp.broadcast_to(lines * (1.0 / (2 * total)), (1, 128))
        scalars[1:2, :] = jnp.broadcast_to(slope, (1, 128))
        high = lax.Precision.HIGHEST
        wide = [e.astype(F32) for e in embed]
        dembed = [
            sharp * jnp.dot(dlogits, wide[1], precision=high, preferred_element_type=F32),
            sharp * lax.dot_general(dlogits, wide[0], (((0,), (0,)), ((), ())), precision=high,
                                    preferred_element_type=F32),
        ]
        c_rows[...] = jnp.zeros_like(c_rows)
        dcls[...] = jnp.zeros_like(dcls)
        for m in range(2):
            for p in range(quarter):
                src = (img, txt)[m]
                cot[m, 8 * 3 + p:8 * 3 + p + 1, :] = src[p, 0:1, :].astype(F32)
        for m in range(2):
            u, y, d = unit[m], proj[m], dembed[m]
            dp = (u * d - u * u * u * y * jnp.sum(y * d, axis=-1, keepdims=True)).astype(BF16)
            dproj[m] = dp
            dh = dot_t(dp, weight[m])
            gains[m:m + 1, :] = jnp.sum(dh * normal[m], axis=0, keepdims=True)
            shifts[m:m + 1, :] = jnp.sum(dh, axis=0, keepdims=True)
            back[m] = norm_back(normal[m], inverse[m], dh * vector(vec, H_GAIN + m))
            for r in range(4):
                step = (3, 1, 2, 0)[r]
                for p in range(quarter):
                    g = back[m, pl.ds(16 * here.b + 4 * of[r] + p, 1), :]
                    at = own_row(dims, r, p)
                    c_rows[m, at:at + 1, :] = cot[m, 8 * step + p:8 * step + p + 1, :] + g
                    if r == 0:
                        dcls[p, m:m + 1, :] = g
            u = dot(class_e[m], up[m]) + up_bias[m:m + 1]
            big, small = gelu_parts(u)
            c_act[m] = (u * big).astype(BF16)
            g = (c_rows[m] * vector(vec, F_SCALE)).astype(BF16)
            c_ddn[m] = g
            du = dot_t(g, down[m]) * (big + u * small)
            bias_grad[m:m + 1, :] += jnp.sum(du, axis=0, keepdims=True)
            low = du.astype(BF16)
            c_dup[m] = low
            extra[m] = dot_t(low, up[m])
        for copy in sent_extra:
            copy.start()

    at = lax.broadcasted_iota(jnp.int32, (slab, 1), 0)
    inner = (at != 0) & (at != ip)

    def one(p, c):
        load_rows(dims, p, img, txt, rows)
        cot[0, pl.ds(8 * i + p, 1), :] = rows[0:1, :]
        cot[1, pl.ds(8 * i + p, 1), :] = rows[ip:ip + 1, :]
        ddn[p] = jnp.where(inner, rows[...] * vector(vec, F_SCALE), 0.0).astype(BF16)
        return c

    lax.fori_loop(0, quarter, one, 0)
    for m, lo, hi in ((0, 0, ip), (1, ip, slab)):
        count = quarter * (hi - lo)
        e = ins[:, lo:hi, :].reshape(count, model)
        u = dot(e, up[m]) + up_bias[m:m + 1]
        big, small = gelu_parts(u)
        a = (u * big).astype(BF16)
        act[:, lo:hi, :] = a.reshape(quarter, hi - lo, -1)
        slope = big + u * small
        bd[i, :, lo:hi, :] = dot(a, down[m]).astype(BF16).reshape(quarter, hi - lo, model)
        g = ddn[:, lo:hi, :].reshape(count, model)
        du = dot_t(g, down[m]) * slope
        bias_grad[m:m + 1, :] += jnp.sum(du, axis=0, keepdims=True)
        low = du.astype(BF16)
        dup[:, lo:hi, :] = low.reshape(quarter, hi - lo, -1)
        bx[i, :, lo:hi, :] = dot_t(low, up[m]).astype(BF16).reshape(quarter, hi - lo, model)

    for j in range(2):
        @pl.when(i == 2 * j)
        def _():
            sent_x[j].start()
            sent_d[j].start()

    @pl.when(i == 1)
    def _():
        sent_x[0].wait_recv()

        def add_x(p, c):
            x_near[p] = (bx[1, p].astype(F32) + rx[0, p].astype(F32)).astype(BF16)
            return c

        lax.fori_loop(0, quarter, add_x, 0)
        sent_near.start()
        sent_d[0].wait_recv()

        def add_d(p, c):
            d_near[p] = (bd[1, p].astype(F32) + rd[0, p].astype(F32)).astype(BF16)
            return c

        lax.fori_loop(0, quarter, add_d, 0)

    @pl.when(i == 3)
    def _():
        sent_d[1].wait_recv()

        def add_d(p, c):
            d_own[p] = bd[3, p].astype(F32) + rd[1, p].astype(F32)
            return c

        lax.fori_loop(0, quarter, add_d, 0)
        sent_x[1].wait_recv()
        sent_near.wait_recv()

        def add_x(p, c):
            dexp[p] = bx[3, p].astype(F32) + rx[1, p].astype(F32) + x_far[p].astype(F32)
            return c

        lax.fori_loop(0, quarter, add_x, 0)
        for copy in sent_extra:
            copy.wait_recv()
        for m in range(2):
            for p in range(quarter):
                line = [x[m, own_row(dims, r, p):own_row(dims, r, p) + 1, :]
                        for x, r in ((extra, 0), (extras.at[0], 2), (extras.at[1], 1), (extras.at[2], 3))]
                dexp[p, m * ip:m * ip + 1, :] += (line[0] + line[1]) + (line[2] + line[3])
        for copy in sent_x + sent_d + [sent_near] + sent_part + sent_extra + sent_cls:
            copy.wait_send()


def middle(dims, total, img, txt, own, peer, cls_own, cls_peer, vec, up, up_bias, down, weight, scale):
    model = own.shape[-1]
    hidden = up.shape[-1]
    slab, quarter = dims.slab, dims.quarter
    batch = 8

    def cot_at(i):
        here = Place()
        return here.quarter(1 - i // 2, 1 - i % 2), 0, 0

    held = pl.BlockSpec(memory_space=pltpu.VMEM)
    step = lambda cols: pl.BlockSpec((quarter, slab, cols), lambda i: (i, 0, 0))
    rows_of = lambda n, t: jax.ShapeDtypeStruct((n, slab, model), t)
    small = [((quarter, slab, model), F32), ((quarter, slab, model), F32), ((quarter, slab, model), BF16),
             ((2, hidden), F32), ((2, 16, model), BF16), ((2, 16, hidden), BF16), ((2, 16, hidden), BF16),
             ((2, 16, model), BF16), ((quarter, 8, model), F32), ((2, 16 * batch, model), BF16),
             ((2, 16 * batch, weight.shape[2]), BF16), ((2, model), F32), ((2, model), F32), ((2, 128), F32)]
    block = (quarter, slab, model)
    return pl.pallas_call(
        functools.partial(middle_kernel, dims, total),
        grid=(4,),
        in_specs=[pl.BlockSpec((quarter, dims.patches, model), cot_at),
                  pl.BlockSpec((quarter, dims.caption, model), cot_at)] + [held] * 10,
        out_specs=[step(hidden), step(hidden), step(model)] + [held] * len(small),
        out_shape=[rows_of(4 * quarter, BF16)] * 3 + [jax.ShapeDtypeStruct(v, t) for v, t in small],
        scratch_shapes=[
            pltpu.VMEM((4,) + block, BF16), pltpu.VMEM((4,) + block, BF16),
            pltpu.VMEM((2,) + block, BF16), pltpu.VMEM((2,) + block, BF16),
            pltpu.VMEM(block, BF16), pltpu.VMEM(block, BF16), pltpu.VMEM(block, BF16),
            pltpu.VMEM((slab, model), F32),
            pltpu.VMEM((2, 16, model), F32), pltpu.VMEM((3, 2, 16, model), F32),
            pltpu.VMEM((batch, 2, 16, model), F32), pltpu.VMEM((2, 16 * batch, model), F32),
            pltpu.VMEM((2, 32, model), F32), pltpu.VMEM((2, 16, model), F32),
            pltpu.VMEM((2, 16, model), F32), pltpu.VMEM((3, 2, 16, model), F32),
            pltpu.SemaphoreType.DMA((18,)), pltpu.SemaphoreType.DMA((18,)),
        ],
        compiler_params=params(collective_id=2, has_side_effects=True),
        cost_estimate=pl.CostEstimate(
            flops=32 * quarter * slab * model * hidden, bytes_accessed=40_000_000, transcendentals=0),
        name="middle",
    )(img, txt, own, peer, cls_own, cls_peer, vec, up, up_bias, down, weight, scale)


def turn_kernel(dims, img, txt, peer, own, act, dup, ddn, ce, ca, cu, cd, dexp, attended, attn, d_own, d_near, dcls, vec,
                down_sum, up_keep, up_send, dattended, dattn, dattn_peer, fin_img, fin_txt, sums,
                acc, d_far, n_peer, rows, side_send, side_recv, e_in, dexp_in, attended_in, attn_in, d_own_in,
                local_sem, send_sem, recv_sem):
    here = Place()
    quarter, ip = dims.quarter, dims.ip
    i = pl.program_id(0)
    piece = side_send.shape[2]
    sent_near = remote(d_near, d_far, send_sem, recv_sem, 0, here.near)
    sent_core = [remote(dattn.at[p], n_peer.at[p], send_sem, recv_sem, 1 + p, here.core) for p in range(quarter)]
    sent_side = [remote(side_send.at[j], side_recv.at[j], send_sem, recv_sem, 1 + quarter + j, here.side)
                 for j in range(4)]
    loaded = [pltpu.make_async_copy(src, dst, local_sem.at[j]) for j, (src, dst) in enumerate((
        (dexp, dexp_in), (attended, attended_in), (attn, attn_in), (d_own, d_own_in)))]
    dexp, attended, attn, d_own = dexp_in, attended_in, attn_in, d_own_in
    spans = ((0, 0, ip), (1, ip, dims.slab))
    flat = lambda v: v.reshape(-1, v.shape[-1])
    block = lambda j: pl.ds(pl.multiple_of(j * piece, piece), piece)

    @pl.when(i == 0)
    def _():
        meet([here.core, here.near, here.side])
        sent_near.start()
        for copy in loaded:
            copy.start()
        for m in range(2):
            acc[m] = t_dot(cd[m], ca[m])

    @pl.when(i < 4)
    def _():
        for m, lo, hi in spans:
            acc[m] += t_dot(flat(ddn[:, lo:hi, :]), flat(act[:, lo:hi, :]))

    @pl.when(i == 3)
    def _():
        for j in range(4):
            for m in range(2):
                side_send[j, m] = acc[m, block(2 * j + 1 - here.x), :].astype(BF16)
                down_sum[j, m] = acc[m, block(2 * j + here.x), :].astype(BF16)
            sent_side[j].start()

    @pl.when(i == 4)
    def _():
        for m in range(2):
            acc[m] = t_dot(ce[m], cu[m])

    @pl.when((i >= 4) & (i % 2 == 0))
    def _():
        e_in[...] = peer[...]

    @pl.when((i >= 4) & (i % 2 == 1))
    def _():
        e_in[...] = own[...]

    @pl.when(i >= 4)
    def _():
        for m, lo, hi in spans:
            acc[m] += t_dot(flat(e_in[:, lo:hi, :]), flat(dup[:, lo:hi, :]))

    @pl.when(i == 7)
    def _():
        for j in range(4):
            for m in range(2):
                up_keep[j, m] = acc[m, block(2 * j + here.x), :].astype(BF16)
                up_send[j, m] = acc[m, block(2 * j + 1 - here.x), :].astype(BF16)
        for copy in loaded:
            copy.wait()
        rows[...] = jnp.zeros_like(rows)
        sums[...] = jnp.zeros_like(sums)

        def load(p):
            load_rows(dims, p, img, txt, rows)
            rows[0:1, :] += dcls[p, 0:1, :]
            rows[ip:ip + 1, :] += dcls[p, 1:2, :]

        for p in range(quarter):
            load(p)
            for m, lo, hi in ((0, 0, ip), (1, ip, dims.slab)):
                n, r = normalise(attended[p, lo:hi, :])
                dy = dexp[p, lo:hi, :]
                sums[m:m + 1, :] += jnp.sum(dy * n, axis=0, keepdims=True)
                sums[2 + m:3 + m, :] += jnp.sum(dy, axis=0, keepdims=True)
                d = rows[lo:hi, :] + norm_back(n, r, dy * vector(vec, GAIN2 + m))
                dattended[p, lo:hi, :] = d
                sd = d * vector(vec, A_SCALE)
                dattn[p, lo:hi, :] = sd.astype(BF16)
                a = attn[p, lo:hi, :] + vector(vec, A_BIAS)
                sums[4:5, :] += jnp.sum(d * a, axis=0, keepdims=True)
                sums[5:6, :] += jnp.sum(sd, axis=0, keepdims=True)
            sent_core[p].start()
        sent_near.wait_recv()

        def final(p, c):
            load(p)
            for m, lo, hi in ((0, 0, ip), (1, ip, dims.slab)):
                b = d_own[p, lo:hi, :] + d_far[p, lo:hi, :].astype(F32) + vector(vec, F_BIAS + m)
                f = attended[p, lo:hi, :] + vector(vec, F_SCALE) * b
                if m == 0:
                    fin_img[p] = f[0:dims.patches].astype(BF16)
                else:
                    fin_txt[p] = f[0:dims.caption].astype(BF16)
                g = rows[lo:hi, :]
                sums[6:7, :] += jnp.sum(g * b, axis=0, keepdims=True)
                sums[7 + m:8 + m, :] += jnp.sum(g, axis=0, keepdims=True) * vector(vec, F_SCALE)
            return c

        lax.fori_loop(0, quarter, final, 0)
        for p in range(quarter):
            sent_core[p].wait()
            dattn_peer[p] = n_peer[p]
        for j in range(4):
            sent_side[j].wait()
            down_sum[j] = (down_sum[j].astype(F32) + side_recv[j].astype(F32)).astype(BF16)
        sent_near.wait_send()


def turn(dims, img, txt, peer, own, act, dup, ddn, ce, ca, cu, cd, dexp, attended, attn, d_own, d_near, dcls, vec):
    model = own.shape[-1]
    hidden = act.shape[-1]
    slab, quarter = dims.slab, dims.quarter
    held = pl.BlockSpec(memory_space=pltpu.VMEM)

    def own_at(i):
        return Place().quarter(0, 0), 0, 0

    away = pl.BlockSpec(memory_space=pl.ANY)
    half = pl.BlockSpec((quarter, slab, model), lambda i: (jnp.where(i < 6, 1, 0), 0, 0))
    first = pl.BlockSpec((quarter, slab, hidden), lambda i: (jnp.minimum(i, 3), 0, 0))
    last = pl.BlockSpec((quarter, slab, hidden), lambda i: (jnp.maximum(i - 4, 0), 0, 0))
    block = (quarter, slab, model)
    part = (4, 2, model // 8, hidden)
    outs = [(part, BF16), (part, BF16), (part, BF16), (block, F32), (block, BF16), (block, BF16),
            ((quarter, dims.patches, model), BF16), ((quarter, dims.caption, model), BF16), ((16, model), F32)]
    return pl.pallas_call(
        functools.partial(turn_kernel, dims),
        grid=(8,),
        in_specs=[pl.BlockSpec((quarter, dims.patches, model), own_at),
                  pl.BlockSpec((quarter, dims.caption, model), own_at)] + [half] * 2 + [first, last, first]
        + [held] * 4 + [away] * 4 + [held] * 3,
        out_specs=[held] * len(outs),
        out_shape=[jax.ShapeDtypeStruct(v, t) for v, t in outs],
        scratch_shapes=[
            pltpu.VMEM((2, model, hidden), F32), pltpu.VMEM(block, BF16), pltpu.VMEM(block, BF16),
            pltpu.VMEM((slab, model), F32), pltpu.VMEM(part, BF16), pltpu.VMEM(part, BF16),
            pltpu.VMEM(block, BF16),
        ] + [pltpu.VMEM(block, F32)] * 4 + [
            pltpu.SemaphoreType.DMA((4,)),
            pltpu.SemaphoreType.DMA((5 + quarter,)), pltpu.SemaphoreType.DMA((5 + quarter,)),
        ],
        compiler_params=params(collective_id=3, has_side_effects=True),
        cost_estimate=pl.CostEstimate(
            flops=16 * quarter * slab * model * hidden, bytes_accessed=40_000_000, transcendentals=0),
        name="turn",
    )(img, txt, peer, own, act, dup, ddn, ce, ca, cu, cd, dexp, attended, attn, d_own, d_near, dcls, vec)


def back_kernel(dims, lens, d_own, d_peer, normed, qkv_far, mixed_far, qkv_own, mixed_own, wq, wo, wf,
                fin_img, fin_txt, up_keep, up_send, down_sum,
                keep, send, grad_pair, grad_single, cols_far, cols_own, near_img, near_txt, far_sum, up_one, down_out, up_out,
                dattn, dm_far, dm_own, dq_far, dq_own, acc_far, acc_own, w_far, w_own, o_far, o_own, dn, grad_f,
                up_mine, up_side, up_low, up_z, down_mine, down_z, from_side, local_sem, send_sem, recv_sem):
    here = Place()
    i = pl.program_id(0)
    slab, quarter, local = dims.slab, dims.quarter, dims.local
    two, one_head = parts_of(dims)
    count = quarter * slab
    model = normed.shape[-1]
    piece = from_side.shape[1]
    block = lambda j: pl.ds(pl.multiple_of(j * piece, piece), piece)
    used = [0]

    def make(src, dst, device):
        at = used[0]
        used[0] += 1
        return remote(src, dst, send_sem, recv_sem, at, device)

    sent_near = [make(fin_img, near_img, here.near), make(fin_txt, near_txt, here.near)]
    sent_up = [make(up_send.at[j, m], up_side.at[m, j], here.side) for m in range(2) for j in range(4)]
    sent_down = [make(down_sum.at[(here.z + k) % 4], down_z.at[k - 1], here.along[k - 1]) for k in range(1, 4)]
    sent_far = [make(grad_f.at[block(2 * j + 1 - here.x)], from_side.at[j], here.side) for j in range(4)]
    sent_low = [make(up_low.at[(here.z + k) % 4], up_z.at[k - 1], here.along[k - 1]) for k in range(1, 4)]
    loaded = [pltpu.make_async_copy(up_keep, up_mine, local_sem.at[0]),
              pltpu.make_async_copy(down_sum.at[here.z], down_mine, local_sem.at[1])]

    @pl.when(i == 0)
    def _():
        meet([here.near, here.side] + here.along)
        for copy in loaded + sent_near + sent_up + sent_down:
            copy.start()
        for acc, cols in ((acc_far, cols_far), (acc_own, cols_own)):
            acc[...] = jnp.zeros_like(acc)
            cols[...] = jnp.zeros_like(cols)
        for t in range(4):
            own, start = (wq, t * local) if t < 3 else (wo, 0)
            dst, at = (w_far, t * 2 * two) if t < 3 else (o_far, 0)
            copy_rows(dst, at, wf, t * local, two)
            copy_rows(dst, at + two, own, start + two, one_head)
            copy_rows(dst, at + two + one_head, wf, t * local + two, one_head)
            dst, at = (w_own, t * two) if t < 3 else (o_own, 0)
            copy_rows(dst, at, own, start, two)

    @pl.when(i % 2 == 0)
    def _():
        dattn[...] = d_own[...]

    @pl.when(i % 2 == 1)
    def _():
        dattn[...] = d_peer[...]

    whose = here.quarter(0, i % 2)

    @pl.when(i < 2)
    def _():
        part = back_step(dims, 2, lens, whose, dattn, normed, qkv_far, mixed_far, dm_far, dq_far, acc_far, cols_far,
                         w_far, o_far)
        dn[i] = part.reshape(quarter, slab, model)

    @pl.when(i == 1)
    def _():
        for t in range(4):
            at = t * 2 * two
            to = 4 * two + t * one_head
            grad_f[:, t * two:(t + 1) * two] = acc_far[:, at:at + two].astype(BF16)
            grad_f[:, to:to + one_head] = acc_far[:, at + two + one_head:at + 2 * two].astype(BF16)
            grad_single[:, t * one_head:(t + 1) * one_head] = acc_far[:, at + two:at + two + one_head].astype(BF16)
        for copy in sent_far:
            copy.start()
        loaded[0].wait()
        for j in range(4):
            sent_up[j].wait_recv()
            up_low[j] = (up_mine[j, 0].astype(F32) + up_side[0, j].astype(F32)).astype(BF16)
        for copy in sent_low:
            copy.start()

    @pl.when(i >= 2)
    def _():
        part = back_step(dims, 1, lens, whose, dattn, normed, qkv_own, mixed_own, dm_own, dq_own, acc_own, cols_own,
                         w_own, o_own)
        total = (part.reshape(quarter, slab, model) + dn[i - 2]).astype(BF16)

        @pl.when(i == 2)
        def _():
            keep[...] = total

        @pl.when(i == 3)
        def _():
            send[...] = total

    @pl.when(i == 3)
    def _():
        grad_pair[...] = acc_own[...].astype(BF16)
        for j in range(4):
            sent_up[4 + j].wait_recv()
            up_one[j] = (up_mine[j, 1].astype(F32) + up_side[1, j].astype(F32)).astype(BF16)
        loaded[1].wait()
        for copy in sent_down:
            copy.wait_recv()
        down_out[...] = (down_mine[...].astype(F32) + down_z[0].astype(F32)) + (
            down_z[1].astype(F32) + down_z[2].astype(F32))
        for j in range(4):
            sent_far[j].wait_recv()
            far_sum[j] = (grad_f[block(2 * j + here.x), :].astype(F32) + from_side[j].astype(F32)).astype(BF16)
        for copy in sent_low:
            copy.wait_recv()
        up_out[...] = (up_low[here.z].astype(F32) + up_z[0].astype(F32)) + (
            up_z[1].astype(F32) + up_z[2].astype(F32))
        for copy in sent_near:
            copy.wait_recv()
        for copy in sent_near + sent_up + sent_down + sent_far + sent_low:
            copy.wait_send()


def back(dims, lens, d_own, d_peer, normed, qkv_far, mixed_far, qkv_own, mixed_own, wq, wo, wf,
         fin_img, fin_txt, up_keep, up_send, down_sum):
    model = normed.shape[-1]
    slab, quarter = dims.slab, dims.quarter
    hidden = up_keep.shape[-1]
    piece = model // 8
    held = pl.BlockSpec(memory_space=pltpu.VMEM)
    away = pl.BlockSpec(memory_space=pl.ANY)
    spec = lambda cols, at: pl.BlockSpec((quarter, slab, cols), lambda i: (at(i), 0, 0))
    early, late = lambda i: jnp.minimum(i, 1), lambda i: jnp.maximum(i - 2, 0)
    rows = (quarter, slab, model)
    outs = [(held, rows, BF16), (held, rows, BF16), (held, (model, 512), BF16), (held, (model, 256), BF16),
            (held, (1, 768), F32), (held, (1, 384), F32),
            (away, fin_img.shape, BF16), (away, fin_txt.shape, BF16),
            (held, (4, piece, model), BF16), (held, (4, piece, hidden), BF16),
            (held, (2, piece, hidden), F32), (held, (piece, hidden), F32)]
    slabs = lambda cols: pltpu.VMEM((quarter, slab, cols), BF16)
    return pl.pallas_call(
        functools.partial(back_kernel, dims),
        grid=(4,),
        in_specs=[pl.BlockSpec(memory_space=pltpu.SMEM), held, held, spec(model, lambda i: i % 2),
                  spec(768, early), spec(256, early), spec(384, late), spec(128, late), held, held, held]
        + [away] * 5,
        out_specs=[v[0] for v in outs],
        out_shape=[jax.ShapeDtypeStruct(v[1], v[2]) for v in outs],
        scratch_shapes=[
            slabs(model), slabs(256), slabs(128), slabs(768), slabs(384),
            pltpu.VMEM((model, 1024), F32), pltpu.VMEM((model, 512), F32),
            pltpu.VMEM((768, model), BF16), pltpu.VMEM((384, model), BF16),
            pltpu.VMEM((256, model), BF16), pltpu.VMEM((128, model), BF16),
            pltpu.VMEM((2,) + rows, F32), pltpu.VMEM((model, model), BF16),
            pltpu.VMEM((4, 2, piece, hidden), BF16), pltpu.VMEM((2, 4, piece, hidden), BF16),
            pltpu.VMEM((4, piece, hidden), BF16), pltpu.VMEM((3, piece, hidden), BF16),
            pltpu.VMEM((2, piece, hidden), BF16), pltpu.VMEM((3, 2, piece, hidden), BF16),
            pltpu.VMEM((4, piece, model), BF16),
            pltpu.SemaphoreType.DMA((2,)), pltpu.SemaphoreType.DMA((20,)), pltpu.SemaphoreType.DMA((20,)),
        ],
        compiler_params=params(collective_id=4, has_side_effects=True),
        cost_estimate=pl.CostEstimate(
            flops=24 * quarter * slab * model * 1152, bytes_accessed=30_000_000, transcendentals=0),
        name="back",
    )(lens, d_own, d_peer, normed, qkv_far, mixed_far, qkv_own, mixed_own, wq, wo, wf,
      fin_img, fin_txt, up_keep, up_send, down_sum)


V_ROWS, V_MP, V_HEADS, V_FAR = 24, 11, 13, 15


def finish_kernel(dims, n_keep, n_send, dattended, states_img, states_txt, vec, fin_img, fin_txt,
                  near_img, near_txt, grad_pair, grad_single, grad_far, up_one, own_sums, up_sums, cols_own, cols_far,
                  out_img, out_txt, back_img, back_txt, grad_out, v_out, up_out,
                  n_recv, s_img, s_txt, d_img, d_txt, rows, xr, zs, zr, zr_far, zr_up, far_sum, far_recv, vs, vr,
                  local_sem, send_sem, recv_sem):
    quarter = dims.quarter
    here = Place()
    z, x, m = here.z, here.x, here.m
    near_quarter = here.quarter(1, 0)
    used = [0]

    def send(src, dst, device):
        at = used[0]
        used[0] += 1
        return remote(src, dst, send_sem, recv_sem, at, device)

    loaded = [pltpu.make_async_copy(states_img.at[pl.ds(m * quarter, quarter)], s_img, local_sem.at[0]),
              pltpu.make_async_copy(states_txt.at[pl.ds(m * quarter, quarter)], s_txt, local_sem.at[1])]
    for copy in loaded:
        copy.start()
    meet([here.core, here.near, here.side] + here.along)

    n_copies = [send(n_send.at[p], n_recv.at[p], here.core) for p in range(quarter)]
    for copy in n_copies:
        copy.start()
    piece = xr.shape[1]
    wide = grad_pair.shape[1]
    spans = ((grad_pair, 0, wide), (grad_single, wide, xr.shape[2]))
    block = lambda j: pl.ds(pl.multiple_of(j * piece, piece), piece)
    x_copies = []
    for j in range(4):
        for src, lo, hi in spans:
            x_copies.append(send(src.at[block(2 * j + 1 - x)], xr.at[j, :, pl.ds(lo, hi - lo)], here.side))
            x_copies[-1].start()
    far_copies = [send(grad_far.at[(z + k) % 4], zr_far.at[k - 1], here.along[k - 1]) for k in range(1, 4)]
    for copy in far_copies:
        copy.start()

    fin_local, fin_remote = [], []
    for j, (src, dst, q) in enumerate((
        (fin_img, out_img, m), (fin_txt, out_txt, m), (near_img, out_img, near_quarter), (near_txt, out_txt, near_quarter),
    )):
        at = pl.ds(q * quarter, quarter)
        fin_local.append(pltpu.make_async_copy(src, dst.at[at], local_sem.at[2 + j]))
        fin_remote.append(send(src, dst.at[at], here.core))

    rows[...] = jnp.zeros_like(rows)
    for copy in loaded:
        copy.wait()
    total = [jnp.zeros((1, rows.shape[1]), F32)] * 2
    back_local, to_near, to_other = [], [], []
    for p in range(quarter):
        load_rows(dims, p, s_img, s_txt, rows)
        n, r = normalise(rows[...])
        n_copies[p].wait_recv()
        dy = n_keep[p].astype(F32) + n_recv[p].astype(F32)
        total[0] = total[0] + jnp.sum(dy * n, axis=0, keepdims=True)
        total[1] = total[1] + jnp.sum(dy, axis=0, keepdims=True)
        d = dattended[p] + norm_back(n, r, dy * vector(vec, GAIN1))
        d_img[p] = d[0:dims.patches].astype(BF16)
        d_txt[p] = d[dims.ip:dims.ip + dims.caption].astype(BF16)
        for j, (src, dst) in enumerate(((d_img, back_img), (d_txt, back_txt))):
            at = dst.at[m * quarter + p]
            to_near.append(send(src.at[p], at, here.near))
            to_near[-1].start()
            to_other.append(send(src.at[p], at, here.core))
            to_other[-1].start()
            back_local.append(pltpu.make_async_copy(src.at[p], at, local_sem.at[6 + 2 * p + j]))
            back_local[-1].start()
    for copy in fin_local + fin_remote:
        copy.start()

    at = lax.broadcasted_iota(jnp.int32, (V_ROWS, 1), 0)
    two, one_head = parts_of(dims)
    vs[0] = jnp.zeros(vs.shape[1:], F32)
    vs[0, 0:1, :] = total[0]
    vs[0, 1:2, :] = total[1]
    vs[0, 2:V_MP, :] = own_sums[0:V_MP - 2, :]
    vs[0, V_MP:V_HEADS, :] = up_sums[...]
    for j in range(2):
        own_at, far_at = 2 * j * two, 4 * j * two
        vs[0, V_HEADS + j:V_HEADS + j + 1, 0:two] = cols_own[0:1, own_at:own_at + two]
        vs[0, V_HEADS + j:V_HEADS + j + 1, two:two + one_head] = cols_far[0:1, far_at + two:far_at + two + one_head]
        vs[0, V_FAR + j:V_FAR + j + 1, 0:two] = cols_far[0:1, far_at:far_at + two]
        vs[0, V_FAR + j:V_FAR + j + 1, two:two + one_head] = cols_far[0:1, far_at + two + one_head:far_at + 2 * two]
    v = vs[0]
    v_copies = []

    def exchange(step, value, device):
        vs[step] = value
        copy = send(vs.at[step], vr.at[step], device)
        copy.start()
        copy.wait_recv()
        v_copies.append(copy)
        return vr[step]

    v = v + jnp.where(at < V_MP, exchange(0, v, here.core), 0.0)
    v = v + exchange(1, v, here.side)
    vs[2] = v
    vr[3 + z] = v
    around = [send(vs.at[2], vr.at[3 + z], here.along[k - 1]) for k in range(1, 4)]
    for copy in around:
        copy.start()
    up_copies = [send(up_one.at[(z + k) % 4], zr_up.at[k - 1], here.along[k - 1]) for k in range(1, 4)]
    for copy in up_copies:
        copy.start()

    def own_sum(j, k):
        src, lo, hi = spans[k]
        return src[block(2 * j + x), :].astype(F32) + xr[j, :, lo:hi].astype(F32)

    for copy in x_copies:
        copy.wait_recv()
    for j in range(4):
        for k, (src, lo, hi) in enumerate(spans):
            zs[j, :, lo:hi] = own_sum(j, k).astype(BF16)
    z_copies = [send(zs.at[(z + k) % 4], zr.at[k - 1], here.along[k - 1]) for k in range(1, 4)]
    for copy in z_copies:
        copy.start()

    for copy in around:
        copy.wait_recv()
    v = (vr[3] + vr[4]) + (vr[5] + vr[6])
    for copy in far_copies:
        copy.wait_recv()
    far = grad_far[z].astype(F32)
    for k in range(3):
        far = far + zr_far[k].astype(F32)
    far_sum[...] = far.astype(BF16)
    far_copy = send(far_sum, far_recv, here.near)
    far_copy.start()
    vs[3] = v
    v_near = send(vs.at[3], vr.at[2], here.near)
    v_near.start()
    for copy in up_copies:
        copy.wait_recv()
    up_out[...] = (up_one[z].astype(F32) + zr_up[0].astype(F32)) + (zr_up[1].astype(F32) + zr_up[2].astype(F32))
    for copy in fin_local + back_local:
        copy.wait()
    onward = []
    for p in range(quarter):
        for j, dst in enumerate((back_img, back_txt)):
            to_near[2 * p + j].wait_recv()
            at_near = dst.at[near_quarter * quarter + p]
            onward.append(send(at_near, at_near, here.core))
            onward[-1].start()
    far_copy.wait_recv()
    for copy in z_copies:
        copy.wait_recv()
    for k, (src, lo, hi) in enumerate(spans):
        g = own_sum(z, k) + far_recv[:, lo:hi].astype(F32)
        for j in range(3):
            g = g + zr[j, :, lo:hi].astype(F32)
        grad_out[:, lo:hi] = g
    v_near.wait_recv()
    there = vr[2]
    v_out[...] = v + jnp.where(at < V_MP, there, 0.0)
    v_out[V_HEADS:V_HEADS + 2, :] = v[V_HEADS:V_HEADS + 2, :] + there[V_FAR:V_FAR + 2, :]
    for copy in to_other + fin_remote + onward:
        copy.wait()
    for copy in n_copies + x_copies + far_copies + to_near + z_copies + v_copies + around + up_copies + [far_copy, v_near]:
        copy.wait_send()


def finish(dims, n_keep, n_send, dattended, states_img, states_txt, vec, fin_img, fin_txt,
           near_img, near_txt, grad_pair, grad_single, grad_far, up_one, *tables):
    pairs, patches, model = states_img.shape
    caption = states_txt.shape[1]
    quarter, slab = dims.quarter, dims.slab
    piece, cols = grad_far.shape[1:]
    held = pl.BlockSpec(memory_space=pltpu.VMEM)
    away = pl.BlockSpec(memory_space=pl.ANY)
    n_remote = 7 * quarter + 28
    return pl.pallas_call(
        functools.partial(finish_kernel, dims),
        in_specs=[held] * 3 + [away] * 2 + [held] * 13,
        out_specs=[away] * 4 + [held] * 3,
        out_shape=[
            jax.ShapeDtypeStruct((pairs, patches, model), BF16),
            jax.ShapeDtypeStruct((pairs, caption, model), BF16),
            jax.ShapeDtypeStruct((pairs, patches, model), BF16),
            jax.ShapeDtypeStruct((pairs, caption, model), BF16),
            jax.ShapeDtypeStruct((piece, cols), F32),
            jax.ShapeDtypeStruct((V_ROWS, model), F32),
            jax.ShapeDtypeStruct(up_one.shape[1:], F32),
        ],
        scratch_shapes=[
            pltpu.VMEM((quarter, slab, model), BF16),
            pltpu.VMEM((quarter, patches, model), BF16),
            pltpu.VMEM((quarter, caption, model), BF16),
            pltpu.VMEM((quarter, patches, model), BF16),
            pltpu.VMEM((quarter, caption, model), BF16),
            pltpu.VMEM((slab, model), F32),
            pltpu.VMEM((4, piece, cols), BF16), pltpu.VMEM((4, piece, cols), BF16),
            pltpu.VMEM((3, piece, cols), BF16), pltpu.VMEM((3, piece, cols), BF16),
            pltpu.VMEM((3,) + up_one.shape[1:], BF16),
            pltpu.VMEM((piece, cols), BF16), pltpu.VMEM((piece, cols), BF16),
            pltpu.VMEM((4, V_ROWS, model), F32),
            pltpu.VMEM((7, V_ROWS, model), F32),
            pltpu.SemaphoreType.DMA((6 + 2 * quarter,)),
            pltpu.SemaphoreType.DMA((n_remote,)),
            pltpu.SemaphoreType.DMA((n_remote,)),
        ],
        compiler_params=params(collective_id=1, has_side_effects=True),
        name="finish",
    )(n_keep, n_send, dattended, states_img, states_txt, vec, fin_img, fin_txt,
      near_img, near_txt, grad_pair, grad_single, grad_far, up_one, *tables)


def spread_kernel(cols, at, sums, grad, gains, shifts, *refs):
    *outs, qkv, out_w, turned = refs
    back = sums.shape[1] - at[0] * cols

    def slice_of(value):
        return pltpu.roll(value, back, 1)[:, 0:cols]

    mine = slice_of(sums[...])
    for out, (lo, count) in zip(outs[:8], ((0, 1), (1, 1), (7, 1), (6, 1), (2, 2), (4, 2), (9, 2), (8, 1))):
        out[...] = mine[lo:lo + count, :]
    wide = jnp.concatenate([gains[...], shifts[...], jnp.zeros((4, sums.shape[1]), F32)], axis=0)
    heads = slice_of(wide)
    outs[8][...] = heads[0:2, :]
    outs[9][...] = heads[2:4, :]
    outs[10][...] = sums[V_MP:V_MP + 2, :]
    outs[11][...] = sums[V_HEADS:V_HEADS + 2, 0:outs[11].shape[1]]
    two, one = 2 * HEAD_DIM, HEAD_DIM
    for t in range(3):
        qkv[t, :, 0:two] = grad[:, t * two:(t + 1) * two]
        qkv[t, :, two:two + one] = grad[:, 4 * two + t * one:4 * two + (t + 1) * one]
    turned[...] = jnp.zeros_like(turned)
    turned[0:cols, 0:two] = grad[:, 3 * two:4 * two]
    turned[0:cols, two:two + one] = grad[:, 4 * two + 3 * one:4 * two + 4 * one]
    out_w[...] = turned[...].T[0:two + one, 0:cols]


def spread(local, at, sums, grad, gains, shifts):
    cols, model = grad.shape[0], sums.shape[1]
    assert cols <= 128
    shapes = [(1, cols)] * 4 + [(2, cols)] * 3 + [(1, cols)] + [(2, cols)] * 2 + [(2, model), (2, local)]
    shapes += [(3, cols, local), (local, cols)]
    args = (sums, grad, gains, shifts)
    return pl.pallas_call(
        functools.partial(spread_kernel, cols),
        grid_spec=pltpu.PrefetchScalarGridSpec(
            num_scalar_prefetch=1, grid=(1,),
            in_specs=[spec_whole(v) for v in args],
            out_specs=[pl.BlockSpec(v, lambda i, o, n=len(v): (0,) * n) for v in shapes],
            scratch_shapes=[pltpu.VMEM((128, 256), F32)],
        ),
        out_shape=[jax.ShapeDtypeStruct(v, F32) for v in shapes],
        compiler_params=params(),
        cost_estimate=pl.CostEstimate(flops=1_000_000, bytes_accessed=1_000_000, transcendentals=0),
        name="spread",
    )(at, *args)


def per_device(
    image_states, text_states, caption_lengths, image_cotangent, text_cotangent,
    first_gain, first_shift, query_key_value, query_value_bias, output_weight, output_bias,
    attention_scale, expert_gain, expert_shift, expert_up, expert_up_bias, expert_down,
    expert_down_bias, feedforward_scale, head_gain, head_shift, head_weight, logit_scale,
):
    pairs, patches, model = image_states.shape
    caption = text_states.shape[1]
    local = query_key_value.shape[2]
    quarter = pairs // 4
    batch_size = lax.axis_size("batch")
    assert lax.axis_size("mp") == 4 and pairs == 4 * quarter and quarter <= 3
    assert batch_size & (batch_size - 1) == 0
    assert local == 3 * HEAD_DIM
    ip, tp = up16(patches), up16(caption)
    dims = Dims(patches, caption, ip, tp, ip + tp, quarter, local)
    me = lax.axis_index("mp")
    batch_at = lax.axis_index("batch")
    order = me ^ jnp.asarray(ORDER, jnp.int32)
    vectors = (first_gain, first_shift, attention_scale, output_bias, expert_gain, expert_shift,
               feedforward_scale, expert_down_bias, head_gain, head_shift)
    own_w = jnp.transpose(query_key_value, (1, 2, 0)).reshape(3 * local, model)
    one_kernel = batch_size == 8 and model // batch_size % 32 == 0 and expert_up.shape[2] == model
    if one_kernel:
        (vec, normed, qkv_own, mixed_own, qkv_far, mixed_far, wf, attended, attn, e_own, e_peer, cls_own, cls_peer) = front(
            dims, caption_lengths, image_states, text_states, vectors, query_value_bias, own_w, output_weight)
    else:
        vec = jnp.concatenate([v.reshape(-1, model) for v in vectors] + [jnp.zeros((1, model), F32)])
        wo = jnp.concatenate([own_w, output_weight])
        wf = to_y(wo)
        far_bias = to_y(query_value_bias)
        normed, qkv_own, rest, mixed_own = attend_own(
            dims, order, caption_lengths, image_states, text_states, vec, query_value_bias, wo)
        qkv_far, mixed_far, a_keep, a_send = attend_far(
            dims, order, caption_lengths, normed, rest, mixed_own, far_bias, wo, wf)
        a_recv = to_core(a_send)
        attended, attn, e_own, cls_own = residual(
            dims, order, a_keep, a_recv, image_states, text_states, vec)
        e_peer = to_core(e_own)
        cls_peer = to_core(cls_own)
    if one_kernel:
        (act, dup, ddn, dexp, d_own, d_near, up_sums, class_e, c_act, c_dup, c_ddn, dcls, head_in, dproj,
         grad_head_gain, grad_head_shift, scalars) = middle(
            dims, pairs * batch_size, image_cotangent, text_cotangent, e_own, e_peer, cls_own, cls_peer, vec,
            expert_up, expert_up_bias, expert_down, head_weight, logit_scale.reshape(1, 1))
        down_sum, up_keep, up_send, dattended, dattn, dattn_peer, fin_img, fin_txt, own_sums = turn(
            dims, image_cotangent, text_cotangent, e_peer, e_own, act, dup, ddn, class_e, c_act, c_dup, c_ddn,
            dexp, attended, attn, d_own, d_near, dcls, vec)
    else:
        class_part, class_e = class_forward(dims, cls_own, cls_peer, expert_up, expert_up_bias, expert_down)
        class_parts = from_others(class_part, "mp", 1, 4)

        act_a, dup_a, ddn_a, d_send3, d_keep1, x_send3, x_keep1, bias_a, cot_a = experts(
            dims, "experts_a", 1, order[jnp.asarray([3, 1])], e_peer, e_own, image_cotangent, text_cotangent,
            tie(vec, class_part), expert_up, expert_up_bias, expert_down)
        x_recv1 = to_core(x_send3)
        d_recv1 = to_core(d_send3)
        final_class = class_final(
            dims, order, cls_own, cls_peer, class_parts, tie(vec, bias_a))
        class_blocks = gather_batch(final_class[None])
        x_near = add_low(x_keep1, x_recv1)
        x_far = to_y(x_near)
        act_b, dup_b, ddn_b, d_send2, d_keep0, x_send2, x_keep0, bias_b, cot_b = experts(
            dims, "experts_b", 0, order[jnp.asarray([2, 0])], e_peer, e_own, image_cotangent, text_cotangent,
            tie(vec, final_class, x_near), expert_up, expert_up_bias, expert_down)
        x_recv0 = to_core(x_send2)
        d_recv0 = to_core(d_send2)

        head_in, dproj, dclass, grad_head_gain, grad_head_shift, scalars = (contrast if batch_size <= 8 else contrast_large)(
            dims, pairs * batch_size, batch_at.reshape(1), class_blocks, tie(vec, bias_b), head_weight,
             logit_scale.reshape(1, 1))
        c_act, c_dup, c_ddn, c_dexp, c_bias, dcls = class_back(
            dims, order, class_e, cot_a, cot_b, dclass, vec, expert_up, expert_up_bias, expert_down)
        extras = from_others(c_dexp, "mp", 1, 4)
        d_far = to_y(add_low(d_keep1, tie(d_recv1, c_dexp)))
        expert_grad = expert_grads(
            dims, e_peer, e_own, act_a, dup_a, ddn_a, act_b, dup_b, ddn_b, class_e, c_act, c_dup, c_ddn)
        expert_sum = lax.psum_scatter(expert_grad, "batch", scatter_dimension=1, tiled=True)

        dattended, dattn, sums_two = norm_two(
            dims, order, x_keep0, x_recv0, x_far, attended, a_keep, a_recv, image_cotangent, text_cotangent,
            dcls, extras, tie(vec, expert_grad))
        dattn_peer = to_core(dattn)
        fin_img, fin_txt, sums_fin = final_rows(
            dims, order, d_keep0, d_recv0, d_far, attended, image_cotangent, text_cotangent, dcls,
            tie(vec, sums_two))
        own_sums = jnp.concatenate([sums_two[:6], sums_fin[:3]])
        up_sums = bias_a + bias_b + c_bias
    contrast_loss = scalars[0, :1]
    grad_logit_scale = scalars[1, :1]
    if one_kernel:
        (n_keep, n_send, grad_o01, grad_o2, cols_far, cols_own, near_img, near_txt, far_sum, up_one, grad_down,
         up_low) = back(
            dims, caption_lengths, dattn, dattn_peer, normed, qkv_far, mixed_far, qkv_own, mixed_own,
            own_w, output_weight, wf, fin_img, fin_txt, up_keep, up_send, down_sum)
    else:
        n_keep, n_send, grad_far, grad_o2, cols_far = attend_back(
            dims, True, order, caption_lengths, dattn, dattn_peer, normed, qkv_far, mixed_far, own_w, output_weight, wf)
        n_keep, n_send, grad_o01, cols_own = attend_back(
            dims, False, order, caption_lengths, dattn, dattn_peer, normed, qkv_own, mixed_own, own_w, output_weight, wf,
            prior=(n_keep, n_send))
    cols = model // batch_size
    mine = lambda v, axis: lax.dynamic_slice_in_dim(v, batch_at * cols, cols, axis=axis)
    grad_head_weight = jnp.einsum("mnc,mne->mce", mine(head_in, 2), dproj, preferred_element_type=F32)
    pair, single = 2 * HEAD_DIM, HEAD_DIM
    if one_kernel:
        image_output, text_output, image_grad, text_grad, attn_grad, sums, up_high = finish(
            dims, n_keep, n_send, dattended, image_states, text_states, vec, fin_img, fin_txt,
            near_img, near_txt, grad_o01, grad_o2, far_sum, up_one, own_sums, up_sums, cols_own, cols_far)
        *vectors, grad_qkv, grad_output_weight = spread(
            local, batch_at.reshape(1), sums, attn_grad, grad_head_gain, grad_head_shift)
        flat = lambda v: v.reshape(-1)
        return (
            image_output,
            text_output,
            contrast_loss,
            image_grad,
            text_grad,
            flat(vectors[0]),
            flat(vectors[1]),
            jnp.transpose(grad_qkv, (1, 0, 2)),
            vectors[11],
            grad_output_weight,
            flat(vectors[2]),
            flat(vectors[3]),
            vectors[4],
            vectors[5],
            jnp.stack([up_low, up_high]),
            vectors[10],
            jnp.transpose(grad_down, (0, 2, 1)),
            vectors[6],
            flat(vectors[7]),
            vectors[8],
            vectors[9],
            grad_head_weight,
            grad_logit_scale,
        )
    else:
        grad_expert_up = expert_sum[:2].astype(F32)
        grad_expert_down = jnp.transpose(expert_sum[2:].astype(F32), (0, 2, 1))
        cols_own = cols_own.reshape(3, pair)[::2]
        cols_far = cols_far.reshape(3, 2 * pair)[::2]
        heads = jnp.concatenate([cols_own, cols_far[:, pair:pair + single]], axis=1)
        heads_far = jnp.concatenate([cols_far[:, :pair], cols_far[:, pair + single:]], axis=1)
        n_recv = to_core(n_send)
        d_img, d_txt, sums_one = norm_one(
            dims, order, n_keep, n_recv, dattended, image_states, text_states, vec)
        image_output = gather_rows(fin_img, me)
        text_output = gather_rows(fin_txt, me)
        image_grad = gather_rows(d_img, me)
        text_grad = gather_rows(d_txt, me)
        grad_own = jnp.concatenate([grad_o01, grad_o2], axis=1)
        grad_far = lax.psum_scatter(grad_far, "batch", scatter_dimension=0, tiled=True)
        grad_own = lax.psum_scatter(grad_own, "batch", scatter_dimension=0, tiled=True)
        attn_grad = grad_own.astype(F32) + to_y(grad_far).astype(F32)
        heads = heads + to_y(heads_far)
        own_sums = sum_over(jnp.concatenate([sums_one[:2], own_sums]), "mp")
        flat = jnp.concatenate([own_sums.reshape(-1), heads.reshape(-1), up_sums.reshape(-1)])
        count = flat.shape[0]
        flat = jnp.pad(flat, (0, -count % 1024)).reshape(-1, 128)
        flat = sum_over(flat, "batch").reshape(-1)[:count]
        done = own_sums.shape[0]
        own_sums = mine(flat[:done * model].reshape(done, model), 1)
        heads = flat[done * model:done * model + 2 * local].reshape(2, local)
        grad_expert_up_bias = flat[done * model + 2 * local:].reshape(up_sums.shape)
    attn_grad = jnp.concatenate(
        [attn_grad[:, :4 * pair].reshape(cols, 4, pair), attn_grad[:, 4 * pair:].reshape(cols, 4, single)], axis=2)
    grad_query_key_value = attn_grad[:, :3]
    grad_output_weight = jnp.transpose(attn_grad[:, 3])
    return (
        image_output,
        text_output,
        contrast_loss,
        image_grad,
        text_grad,
        own_sums[0],
        own_sums[1],
        grad_query_key_value,
        heads,
        grad_output_weight,
        own_sums[7],
        own_sums[6],
        own_sums[2:4],
        own_sums[4:6],
        grad_expert_up,
        grad_expert_up_bias,
        grad_expert_down,
        own_sums[9:11],
        own_sums[8],
        mine(grad_head_gain, 1),
        mine(grad_head_shift, 1),
        grad_head_weight,
        grad_logit_scale,
    )


def solution(mesh):
    return jax.shard_map(
        per_device,
        mesh=mesh,
        in_specs=(
            P("batch", None, None),
            P("batch", None, None),
            P("batch"),
            P("batch", None, None),
            P("batch", None, None),
            P(),
            P(),
            P(None, None, "mp"),
            P(None, "mp"),
            P("mp", None),
            P(),
            P(),
            P(),
            P(),
            P(None, None, "mp"),
            P(None, "mp"),
            P(None, "mp", None),
            P(),
            P(),
            P(),
            P(),
            P(),
            P(),
        ),
        out_specs=(
            P("batch", None, None),
            P("batch", None, None),
            P(),
            P("batch", None, None),
            P("batch", None, None),
            P("batch"),
            P("batch"),
            P("batch", None, "mp"),
            P(None, "mp"),
            P("mp", "batch"),
            P("batch"),
            P("batch"),
            P(None, "batch"),
            P(None, "batch"),
            P(None, "batch", "mp"),
            P(None, "mp"),
            P(None, "mp", "batch"),
            P(None, "batch"),
            P("batch"),
            P(None, "batch"),
            P(None, "batch"),
            P(None, "batch", None),
            P(),
        ),
        check_vma=False,
    )
```

```python
import functools
from typing import NamedTuple

import jax
import jax.numpy as jnp
from jax import lax
from jax.experimental import pallas as pl
from jax.experimental.pallas import tpu as pltpu
from jax.sharding import PartitionSpec as P

HEAD_DIM = 64
F32 = jnp.float32
BF16 = jnp.bfloat16
NEG = -1e9
EPS = 1e-5
ORDER = (0, 2, 1, 3)

VMEM_LIMIT = 60 * 1024 * 1024


def params(**kw):
    return pltpu.CompilerParams(vmem_limit_bytes=VMEM_LIMIT, **kw)


def up16(n):
    return -(-n // 16) * 16


def dot(a, b):
    return jnp.dot(a, b, preferred_element_type=F32)


def dot_t(a, b):
    return lax.dot_general(a, b, (((1,), (1,)), ((), ())), preferred_element_type=F32)


def t_dot(a, b):
    return lax.dot_general(a, b, (((0,), (0,)), ((), ())), preferred_element_type=F32)


def normalise(x):
    c = x - jnp.mean(x, axis=-1, keepdims=True)
    v = jnp.mean(c * c, axis=-1, keepdims=True)
    r = lax.rsqrt(v + EPS)
    return c * r, r


def norm_back(n, r, dn):
    a = jnp.mean(dn, axis=-1, keepdims=True)
    b = jnp.mean(dn * n, axis=-1, keepdims=True)
    return (dn - a - n * b) * r


def gelu_parts(u):
    big = 0.5 * (1.0 + lax.erf(u * 0.7071067811865476))
    small = 0.3989422804014327 * jnp.exp(-0.5 * u * u)
    return big, small


def gelu_low(u):
    return (u * (0.5 * (1.0 + lax.erf(u * 0.7071067811865476)))).astype(BF16)


def softmax_rows(scores):
    m = jnp.max(scores, axis=-1, keepdims=True)
    e = jnp.exp(scores - m)
    return e * (1.0 / jnp.sum(e, axis=-1, keepdims=True))


def tie(value, *after):
    return lax.optimization_barrier((value,) + after)[0]


def load_rows(dims, p, img, txt, rows):
    rows[0:dims.patches, :] = img[p].astype(F32)
    rows[dims.ip:dims.ip + dims.caption, :] = txt[p].astype(F32)


def spec_whole(a):
    return pl.BlockSpec(a.shape, lambda *_: (0,) * a.ndim)


class Dims(NamedTuple):
    patches: int
    caption: int
    ip: int
    tp: int
    slab: int
    quarter: int
    local: int


GAIN1, SHIFT1, A_SCALE, A_BIAS, GAIN2, SHIFT2, F_SCALE, F_BIAS, H_GAIN, H_SHIFT = 0, 1, 2, 3, 4, 6, 8, 9, 11, 13


def vector(table, at, count=1):
    return table[at:at + count, :]


def copy_rows(dst, at, src, start, count):
    dst[at:at + count, :] = src[start:start + count, :]


def parts_of(dims):
    return 2 * HEAD_DIM, HEAD_DIM


def key_tail(dims, length):
    at = dims.patches // 16 * 16
    return ((0, dims.ip, at, dims.patches), (dims.ip, dims.slab, 0, length))


def hide(scores, start, limit):
    if start >= scores.shape[0]:
        return scores
    tail = scores[start:]
    at = start + lax.broadcasted_iota(jnp.int32, (tail.shape[0], 1), 0)
    tail = jnp.where(at < limit, tail, NEG)
    return tail if start == 0 else jnp.concatenate([scores[:start], tail], axis=0)


def split_pair(value):
    low = lax.broadcasted_iota(jnp.int32, (1, 128), 1) < HEAD_DIM
    zero = jnp.zeros_like(value)
    return jnp.concatenate([jnp.where(low, value, zero), jnp.where(low, zero, value)], axis=0)


def join_pair(value):
    low = lax.broadcasted_iota(jnp.int32, (1, 128), 1) < HEAD_DIM
    half = value.shape[0] // 2
    return jnp.where(low, value[:half], value[half:])


def softmax_keys(scores):
    e = jnp.exp(scores - jnp.max(scores, axis=0, keepdims=True))
    return e * (1.0 / jnp.sum(e, axis=0, keepdims=True))


def pair_weights(q, k, start, limit):
    return softmax_keys(hide(dot_t(k, split_pair(q)), start, limit))


def scaled(q):
    return q * jnp.asarray(HEAD_DIM ** -0.5, BF16)


def attend_tiles(dims, lens, quarter_at, qkv, mixed):
    tiles = mixed.shape[-1] // 128

    def one_pair(p, c):
        length = lens[quarter_at * dims.quarter + p]
        for lo, hi, start, limit in key_tail(dims, length):
            for g in range(tiles):
                q, k, v = [qkv[p, lo:hi, (t * tiles + g) * 128:(t * tiles + g + 1) * 128] for t in range(3)]
                w = pair_weights(scaled(q), k, start, limit).astype(BF16)
                mixed[p, lo:hi, g * 128:(g + 1) * 128] = join_pair(t_dot(w, v)).astype(BF16)
        return c

    lax.fori_loop(0, dims.quarter, one_pair, 0)


def attend_own_kernel(dims, order, lens, img, txt, vec, bias, wo, normed, qkv, rest, mixed, rows, w, b):
    i = pl.program_id(0)
    local = dims.local
    two, one_head = parts_of(dims)

    @pl.when(i == 0)
    def _():
        rows[...] = jnp.zeros_like(rows)
        w[...] = jnp.zeros_like(w)
        b[...] = jnp.zeros_like(b)
        for t in range(3):
            copy_rows(w, t * 2 * two, wo, t * local, local)
        b[0:1, 0:local] = bias[0:1, :]
        b[0:1, 4 * two:4 * two + local] = bias[1:2, :]

    def one_norm(p, c):
        load_rows(dims, p, img, txt, rows)
        n, _ = normalise(rows[...])
        normed[p] = (n * vector(vec, GAIN1) + vector(vec, SHIFT1)).astype(BF16)
        return c

    lax.fori_loop(0, dims.quarter, one_norm, 0)
    model = normed.shape[-1]
    proj = (dot_t(normed[...].reshape(dims.quarter * dims.slab, model), w[...]) + b[0:1, :]).astype(BF16)
    proj = proj.reshape(dims.quarter, dims.slab, 6 * two)
    for t in range(3):
        qkv[:, :, t * two:(t + 1) * two] = proj[:, :, 2 * t * two:(2 * t + 1) * two]
        rest[:, :, t * two:(t + 1) * two] = proj[:, :, (2 * t + 1) * two:(2 * t + 2) * two]
    attend_tiles(dims, lens, order[i], qkv, mixed)


def attend_own(dims, order, lens, img, txt, vec, bias, wo):
    model = img.shape[-1]
    pairs = 4 * dims.quarter
    block = lambda cols: pl.BlockSpec((dims.quarter, dims.slab, cols), lambda i, o, n: (i, 0, 0))
    shape = lambda cols: jax.ShapeDtypeStruct((pairs, dims.slab, cols), BF16)
    return pl.pallas_call(
        functools.partial(attend_own_kernel, dims),
        grid_spec=pltpu.PrefetchScalarGridSpec(
            num_scalar_prefetch=2,
            grid=(4,),
            in_specs=[
                pl.BlockSpec((dims.quarter, dims.patches, model), lambda i, o, n: (o[i], 0, 0)),
                pl.BlockSpec((dims.quarter, dims.caption, model), lambda i, o, n: (o[i], 0, 0)),
                spec_whole(vec), spec_whole(bias), spec_whole(wo),
            ],
            out_specs=[block(model), block(384), block(384), block(128)],
            scratch_shapes=[pltpu.VMEM((dims.slab, model), F32), pltpu.VMEM((768, model), BF16),
                            pltpu.VMEM((8, 768), F32)],
        ),
        out_shape=[shape(model), shape(384), shape(384), shape(128)],
        compiler_params=params(),
        cost_estimate=pl.CostEstimate(
            flops=1536 * pairs * dims.slab * model, bytes_accessed=30_000_000, transcendentals=0),
        name="attend_own",
    )(order, lens, img, txt, vec, bias, wo)


def attend_far_kernel(dims, order, lens, normed, rest, own, bias, wo, wf, qkv, mixed, keep, send, w, ow, b):
    i = pl.program_id(0)
    local = dims.local
    two, one_head = parts_of(dims)
    count = dims.quarter * dims.slab
    model = normed.shape[-1]

    @pl.when(i == 0)
    def _():
        w[...] = jnp.zeros_like(w)
        b[...] = jnp.zeros_like(b)
        for t in range(3):
            copy_rows(w, t * 2 * two, wf, t * local, two)
            copy_rows(w, t * 2 * two + two + one_head, wf, t * local + two, one_head)
        for t, at in ((0, 0), (1, 4 * two)):
            b[0:1, at:at + two] = bias[t:t + 1, 0:two]
            b[0:1, at + two + one_head:at + 2 * two] = bias[t:t + 1, two:]
        copy_rows(ow, 0, wo, 3 * local, two)
        copy_rows(ow, two, wf, 3 * local, two)
        copy_rows(ow, 2 * two, wo, 3 * local + two, one_head)
        copy_rows(ow, 2 * two + one_head, wf, 3 * local + two, one_head)

    proj = (dot_t(normed[...].reshape(count, model), w[...]) + b[0:1, :]).astype(BF16)
    proj = proj.reshape(dims.quarter, dims.slab, 6 * two)
    for t in range(3):
        at = 2 * t * two
        qkv[:, :, at:at + two] = proj[:, :, at:at + two]
        qkv[:, :, at + two:at + 2 * two] = proj[:, :, at + two:at + 2 * two] + rest[:, :, t * two:(t + 1) * two]
    attend_tiles(dims, lens, order[(i + 2) % 4], qkv, mixed)
    part = dot(own[...].reshape(count, two), ow[0:two, :])
    part = part + dot(mixed[...].reshape(count, 2 * two), ow[two:, :])
    part = part.astype(BF16).reshape(dims.quarter, dims.slab, model)

    @pl.when(i < 2)
    def _():
        send[...] = part

    @pl.when(i >= 2)
    def _():
        keep[...] = part


def attend_far(dims, order, lens, normed, rest, own, bias, wo, wf):
    model = normed.shape[-1]
    pairs = 4 * dims.quarter
    at = lambda i: (i + 2) % 4
    block = lambda cols, f: pl.BlockSpec((dims.quarter, dims.slab, cols), lambda i, o, n: (f(i), 0, 0))
    shape = lambda count, cols: jax.ShapeDtypeStruct((count, dims.slab, cols), BF16)
    return pl.pallas_call(
        functools.partial(attend_far_kernel, dims),
        grid_spec=pltpu.PrefetchScalarGridSpec(
            num_scalar_prefetch=2,
            grid=(4,),
            in_specs=[
                block(model, at), block(384, at), block(128, at),
                spec_whole(bias), spec_whole(wo), spec_whole(wf),
            ],
            out_specs=[
                block(768, at), block(256, at),
                block(model, lambda i: jnp.maximum(i - 2, 0)), block(model, lambda i: jnp.minimum(i, 1)),
            ],
            scratch_shapes=[pltpu.VMEM((768, model), BF16), pltpu.VMEM((384, model), BF16),
                            pltpu.VMEM((8, 768), F32)],
        ),
        out_shape=[
            shape(pairs, 768), shape(pairs, 256),
            shape(2 * dims.quarter, model), shape(2 * dims.quarter, model),
        ],
        compiler_params=params(),
        cost_estimate=pl.CostEstimate(
            flops=2304 * pairs * dims.slab * model, bytes_accessed=30_000_000, transcendentals=0),
        name="attend_far",
    )(order, lens, normed, rest, own, bias, wo, wf)


def residual_kernel(dims, order, keep, recv, img, txt, vec, attended, attn, expert, cls, rows):
    i = pl.program_id(0)
    ip = dims.ip

    @pl.when(i == 0)
    def _():
        rows[...] = jnp.zeros_like(rows)
        cls[...] = jnp.zeros_like(cls)

    load_rows(dims, 0, img, txt, rows)
    a = keep[0].astype(F32) + recv[0].astype(F32)
    x = rows[...] + vector(vec, A_SCALE) * (a + vector(vec, A_BIAS))
    n, _ = normalise(x)
    e_img = n[0:ip] * vector(vec, GAIN2) + vector(vec, SHIFT2)
    e_txt = n[ip:] * vector(vec, GAIN2 + 1) + vector(vec, SHIFT2 + 1)
    expert[0, 0:ip, :] = e_img.astype(BF16)
    expert[0, ip:, :] = e_txt.astype(BF16)
    for j, v in enumerate((x[0:1], x[ip:ip + 1], e_img[0:1], e_txt[0:1])):
        cls[j, pl.ds(i, 1), :] = v

    @pl.when(i < dims.quarter)
    def _():
        attended[0] = x
        attn[0] = a


def residual(dims, order, keep, recv, img, txt, vec):
    model = img.shape[-1]
    quarter = dims.quarter
    block = pl.BlockSpec((1, dims.slab, model), lambda i, o: (i, 0, 0))
    pair = lambda i, o: (o[i // quarter] * quarter + i % quarter, 0, 0)
    return pl.pallas_call(
        functools.partial(residual_kernel, dims),
        grid_spec=pltpu.PrefetchScalarGridSpec(
            num_scalar_prefetch=1,
            grid=(2 * quarter,),
            in_specs=[
                block, block,
                pl.BlockSpec((1, dims.patches, model), pair),
                pl.BlockSpec((1, dims.caption, model), pair),
                spec_whole(vec),
            ],
            out_specs=[
                pl.BlockSpec((1, dims.slab, model), lambda i, o: (jnp.minimum(i, quarter - 1), 0, 0)),
                pl.BlockSpec((1, dims.slab, model), lambda i, o: (jnp.minimum(i, quarter - 1), 0, 0)),
                block,
                pl.BlockSpec((4, 8, model), lambda i, o: (0, 0, 0)),
            ],
            scratch_shapes=[pltpu.VMEM((dims.slab, model), F32)],
        ),
        out_shape=[
            jax.ShapeDtypeStruct((quarter, dims.slab, model), F32),
            jax.ShapeDtypeStruct((quarter, dims.slab, model), F32),
            jax.ShapeDtypeStruct((2 * quarter, dims.slab, model), BF16),
            jax.ShapeDtypeStruct((4, 8, model), F32),
        ],
        compiler_params=params(),
        cost_estimate=pl.CostEstimate(flops=40_000_000, bytes_accessed=20_000_000, transcendentals=0),
        name="residual",
    )(order, keep, recv, img, txt, vec)


def expert_kernel(dims, seq, peer, own, img, txt, vec, up, up_bias, down,
                  act, dup, ddown, d_send, d_keep, x_send, x_keep, bias_grad, cot, ins, rows):
    ip, slab, quarter = dims.ip, dims.slab, dims.quarter
    i = pl.program_id(0)
    model = own.shape[-1]

    @pl.when(i == 0)
    def _():
        rows[...] = jnp.zeros_like(rows)
        bias_grad[...] = jnp.zeros_like(bias_grad)
        cot[...] = jnp.zeros_like(cot)
        ins[...] = peer[...]

    @pl.when(i == 1)
    def _():
        ins[...] = own[...]

    at = lax.broadcasted_iota(jnp.int32, (slab, 1), 0)
    inner = (at != 0) & (at != ip)

    def one(p, c):
        load_rows(dims, p, img, txt, rows)
        cot[0, pl.ds(8 * i + p, 1), :] = rows[0:1, :]
        cot[1, pl.ds(8 * i + p, 1), :] = rows[ip:ip + 1, :]
        ddown[p] = jnp.where(inner, rows[...] * vector(vec, F_SCALE), 0.0).astype(BF16)
        return c

    lax.fori_loop(0, quarter, one, 0)
    for m, lo, hi in ((0, 0, ip), (1, ip, slab)):
        count = quarter * (hi - lo)
        e = ins[:, lo:hi, :].reshape(count, model)
        u = dot(e, up[m]) + up_bias[m:m + 1]
        big, small = gelu_parts(u)
        a = (u * big).astype(BF16)
        act[:, lo:hi, :] = a.reshape(quarter, hi - lo, -1)
        slope = big + u * small
        d = dot(a, down[m]).astype(BF16).reshape(quarter, hi - lo, model)
        g = ddown[:, lo:hi, :].reshape(count, model)
        du = dot_t(g, down[m]) * slope
        bias_grad[m:m + 1, :] += jnp.sum(du, axis=0, keepdims=True)
        low = du.astype(BF16)
        dup[:, lo:hi, :] = low.reshape(quarter, hi - lo, -1)
        x = dot_t(low, up[m]).astype(BF16).reshape(quarter, hi - lo, model)

        @pl.when(i == 0)
        def _():
            d_send[:, lo:hi, :] = d
            x_send[:, lo:hi, :] = x

        @pl.when(i == 1)
        def _():
            d_keep[:, lo:hi, :] = d
            x_keep[:, lo:hi, :] = x


def experts(dims, name, half, seq, peer, own, img, txt, vec, up, up_bias, down):
    model = own.shape[-1]
    hidden = up.shape[-1]
    slab, quarter = dims.slab, dims.quarter
    fixed = pl.BlockSpec((quarter, slab, model), lambda i, o: (half, 0, 0))
    first = pl.BlockSpec((quarter, slab, model), lambda i, o: (0, 0, 0))
    step = lambda cols: pl.BlockSpec((quarter, slab, cols), lambda i, o: (i, 0, 0))
    shape = lambda n, cols: jax.ShapeDtypeStruct((n * quarter, slab, cols), BF16)
    return pl.pallas_call(
        functools.partial(expert_kernel, dims),
        grid_spec=pltpu.PrefetchScalarGridSpec(
            num_scalar_prefetch=1,
            grid=(2,),
            in_specs=[
                fixed, fixed,
                pl.BlockSpec((quarter, dims.patches, model), lambda i, o: (o[i], 0, 0)),
                pl.BlockSpec((quarter, dims.caption, model), lambda i, o: (o[i], 0, 0)),
                spec_whole(vec), spec_whole(up), spec_whole(up_bias), spec_whole(down),
            ],
            out_specs=[
                step(hidden), step(hidden), step(model),
                first, first, first, first,
                pl.BlockSpec((2, hidden), lambda i, o: (0, 0)),
                pl.BlockSpec((2, 16, model), lambda i, o: (0, 0, 0)),
            ],
            scratch_shapes=[pltpu.VMEM((quarter, slab, model), BF16), pltpu.VMEM((slab, model), F32)],
        ),
        out_shape=[
            shape(2, hidden), shape(2, hidden), shape(2, model),
            shape(1, model), shape(1, model), shape(1, model), shape(1, model),
            jax.ShapeDtypeStruct((2, hidden), F32),
            jax.ShapeDtypeStruct((2, 16, model), F32),
        ],
        compiler_params=params(),
        cost_estimate=pl.CostEstimate(
            flops=16 * quarter * slab * model * hidden, bytes_accessed=20_000_000, transcendentals=0),
        name=name,
    )(seq, peer, own, img, txt, vec, up, up_bias, down)


def expert_grads_kernel(dims, peer, own, act_a, dup_a, ddn_a, act_b, dup_b, ddn_b, ce, ca, cu, cd, out, acc):
    i = pl.program_id(0)

    def add(e, dup, ddn, act):
        for m, lo, hi in ((0, 0, dims.ip), (1, dims.ip, dims.slab)):
            count = dims.quarter * (hi - lo)
            flat = lambda ref: ref[:, lo:hi, :].reshape(count, -1)
            acc[m] += t_dot(flat(e), flat(dup))
            acc[2 + m] += t_dot(flat(ddn), flat(act))

    @pl.when(i == 0)
    def _():
        for m in range(2):
            acc[m] = t_dot(ce[m], cu[m])
            acc[2 + m] = t_dot(cd[m], ca[m])

    for j, refs in enumerate((
        (peer, dup_a, ddn_a, act_a), (own, dup_a, ddn_a, act_a),
        (peer, dup_b, ddn_b, act_b), (own, dup_b, ddn_b, act_b),
    )):
        @pl.when(i == j)
        def _():
            add(*refs)

    @pl.when(i == 3)
    def _():
        out[...] = acc[...].astype(BF16)


def expert_grads(dims, peer, own, act_a, dup_a, ddn_a, act_b, dup_b, ddn_b, ce, ca, cu, cd):
    model = own.shape[-1]
    hidden = act_a.shape[-1]
    slab, quarter = dims.slab, dims.quarter
    assert hidden == model
    half = pl.BlockSpec((quarter, slab, model), lambda i: (jnp.where(i < 2, 1, 0), 0, 0))
    first = pl.BlockSpec((quarter, slab, hidden), lambda i: (jnp.minimum(i, 1), 0, 0))
    last = pl.BlockSpec((quarter, slab, hidden), lambda i: (jnp.maximum(i - 2, 0), 0, 0))
    return pl.pallas_call(
        functools.partial(expert_grads_kernel, dims),
        grid=(4,),
        in_specs=[half, half, first, first, first, last, last, last] + [spec_whole(v) for v in (ce, ca, cu, cd)],
        out_specs=pl.BlockSpec((4, model, hidden), lambda i: (0, 0, 0)),
        scratch_shapes=[pltpu.VMEM((4, model, hidden), F32)],
        out_shape=jax.ShapeDtypeStruct((4, model, hidden), BF16),
        compiler_params=params(),
        cost_estimate=pl.CostEstimate(
            flops=16 * quarter * slab * model * hidden, bytes_accessed=40_000_000, transcendentals=0),
        name="expert_grads",
    )(peer, own, act_a, dup_a, ddn_a, act_b, dup_b, ddn_b, ce, ca, cu, cd)


def own_row(dims, r, p):
    return 8 * (r // 2) + dims.quarter * (r % 2) + p


def class_forward_kernel(dims, near, far, up, up_bias, down, out, rows):
    for m in range(2):
        e = jnp.concatenate([near[2 + m], far[2 + m]], axis=0).astype(BF16)
        rows[m] = e
        u = dot(e, up[m]) + up_bias[m:m + 1]
        out[m] = dot(gelu_low(u), down[m])


def class_forward(dims, near, far, up, up_bias, down):
    shape = (2, 16, near.shape[-1])
    return pl.pallas_call(
        functools.partial(class_forward_kernel, dims),
        out_shape=[jax.ShapeDtypeStruct(shape, F32), jax.ShapeDtypeStruct(shape, BF16)],
        compiler_params=params(),
        cost_estimate=pl.CostEstimate(flops=200_000_000, bytes_accessed=5_000_000, transcendentals=0),
        name="class_forward",
    )(near, far, up, up_bias, down)


def class_final_kernel(dims, order, near, far, d0, d1, d2, d3, vec, out):
    q = dims.quarter
    for m in range(2):
        out[m] = jnp.zeros(out.shape[1:], F32)
        for r in range(4):
            half, at = (near, far)[r // 2], q * (r % 2)
            for p in range(q):
                rows = [d[m, own_row(dims, s, p):own_row(dims, s, p) + 1, :]
                        for d, s in ((d0, r), (d1, r ^ 2), (d2, r ^ 1), (d3, r ^ 3))]
                total = (rows[0] + rows[1]) + (rows[2] + rows[3])
                x = half[m, at + p:at + p + 1, :] + vector(vec, F_SCALE) * (total + vector(vec, F_BIAS + m))
                out[m, pl.ds(4 * order[r] + p, 1), :] = x


def class_final(dims, order, near, far, parts, vec):
    shape = (2, 16, near.shape[-1])
    args = (near, far) + tuple(parts) + (vec,)
    return pl.pallas_call(
        functools.partial(class_final_kernel, dims),
        grid_spec=pltpu.PrefetchScalarGridSpec(
            num_scalar_prefetch=1, grid=(1,),
            in_specs=[spec_whole(v) for v in args],
            out_specs=pl.BlockSpec(shape, lambda i, o: (0, 0, 0)),
        ),
        out_shape=jax.ShapeDtypeStruct(shape, F32),
        compiler_params=params(),
        cost_estimate=pl.CostEstimate(flops=1_000_000, bytes_accessed=1_000_000, transcendentals=0),
        name="class_final",
    )(order, *args)


def class_back_kernel(dims, order, e, cot_a, cot_b, dclass, vec, up, up_bias, down,
                      act, dup, ddown, dexp, bias_grad, dcls, rows):
    q = dims.quarter
    rows[...] = jnp.zeros_like(rows)
    dcls[...] = jnp.zeros_like(dcls)
    for m in range(2):
        for r in range(4):
            cot, base = (cot_b, cot_a)[r % 2], 8 * (1 - r // 2)
            for p in range(q):
                d = dclass[m, pl.ds(4 * order[r] + p, 1), :]
                at = own_row(dims, r, p)
                rows[m, at:at + 1, :] = cot[m, base + p:base + p + 1, :] + d
                if r == 0:
                    dcls[p, m:m + 1, :] = d
        u = dot(e[m], up[m]) + up_bias[m:m + 1]
        big, small = gelu_parts(u)
        act[m] = (u * big).astype(BF16)
        g = (rows[m] * vector(vec, F_SCALE)).astype(BF16)
        ddown[m] = g
        du = dot_t(g, down[m]) * (big + u * small)
        bias_grad[m:m + 1, :] = jnp.sum(du, axis=0, keepdims=True)
        low = du.astype(BF16)
        dup[m] = low
        dexp[m] = dot_t(low, up[m])


def class_back(dims, order, e, cot_a, cot_b, dclass, vec, up, up_bias, down):
    hidden, model = up.shape[-1], e.shape[-1]
    args = (e, cot_a, cot_b, dclass, vec, up, up_bias, down)
    shapes = [((2, 16, hidden), BF16), ((2, 16, hidden), BF16), ((2, 16, model), BF16), ((2, 16, model), F32),
              ((2, hidden), F32), ((dims.quarter, 8, model), F32)]
    return pl.pallas_call(
        functools.partial(class_back_kernel, dims),
        grid_spec=pltpu.PrefetchScalarGridSpec(
            num_scalar_prefetch=1, grid=(1,),
            in_specs=[spec_whole(v) for v in args],
            out_specs=[pl.BlockSpec(s, lambda i, o, n=len(s): (0,) * n) for s, _ in shapes],
            scratch_shapes=[pltpu.VMEM((2, 16, model), F32)],
        ),
        out_shape=[jax.ShapeDtypeStruct(s, t) for s, t in shapes],
        compiler_params=params(),
        cost_estimate=pl.CostEstimate(flops=300_000_000, bytes_accessed=5_000_000, transcendentals=0),
        name="class_back",
    )(order, *args)


def contrast_kernel(dims, total, at, blocks, vec, weight, scale,
                    head_in, dproj, dcls, gains, shifts, scalars, cls, back):
    me = at[0]
    span = blocks[0].shape[0]
    for k, block in enumerate(blocks):
        for j in range(span):
            for m in range(2):
                cls[m, pl.ds(pl.multiple_of(16 * (me ^ (k * span + j)), 16), 16), :] = block[j, m]
    n_rows = cls.shape[1]
    sharp = jnp.exp(scale[...])
    col_at = lax.broadcasted_iota(jnp.int32, (1, n_rows), 1)
    row_at = lax.broadcasted_iota(jnp.int32, (n_rows, 1), 0)
    col_ok = (col_at % 4) < dims.quarter
    row_ok = (row_at % 4) < dims.quarter
    normal, inverse, proj, unit, embed = [], [], [], [], []
    for m in range(2):
        n, r = normalise(cls[m])
        h = (n * vector(vec, H_GAIN + m) + vector(vec, H_SHIFT + m)).astype(BF16)
        head_in[m] = h
        y = dot(h, weight[m])
        u = lax.rsqrt(jnp.sum(y * y, axis=-1, keepdims=True) + 1e-6)
        normal.append(n)
        inverse.append(r)
        proj.append(y)
        unit.append(u)
        embed.append((y * u).astype(BF16))
    ok = row_ok & col_ok
    logits = sharp * dot_t(embed[0], embed[1])
    masked = jnp.where(ok, logits, -1e30)
    row_max = jnp.max(masked, axis=1, keepdims=True)
    row_lse = row_max + jnp.log(jnp.sum(jnp.exp(masked - row_max), axis=1, keepdims=True))
    col_max = jnp.max(masked, axis=0, keepdims=True)
    col_lse = col_max + jnp.log(jnp.sum(jnp.exp(masked - col_max), axis=0, keepdims=True))
    same = (row_at == col_at) & ok
    both = jnp.exp(masked - row_lse) + jnp.exp(masked - col_lse)
    dlogits = jnp.where(ok, jnp.where(same, both - 2.0, both) * (1.0 / (2 * total)), 0.0)
    diagonal = jnp.sum(jnp.where(same, logits, 0.0), axis=1, keepdims=True)
    rows = jnp.where(row_ok, row_lse - 2.0 * diagonal, 0.0)
    cols = jnp.where(col_ok, col_lse, 0.0)
    loss = (jnp.sum(rows, axis=0, keepdims=True) + jnp.sum(cols, axis=1, keepdims=True)) * (1.0 / (2 * total))
    slope = jnp.sum(jnp.sum(dlogits * logits, axis=1, keepdims=True), axis=0, keepdims=True)
    scalars[0:1, :] = jnp.broadcast_to(loss, (1, 128))
    scalars[1:2, :] = jnp.broadcast_to(slope, (1, 128))
    high = lax.Precision.HIGHEST
    wide = [e.astype(F32) for e in embed]
    dembed = [
        sharp * jnp.dot(dlogits, wide[1], precision=high, preferred_element_type=F32),
        sharp * lax.dot_general(dlogits, wide[0], (((0,), (0,)), ((), ())), precision=high,
                                preferred_element_type=F32),
    ]
    for m in range(2):
        u, y, d = unit[m], proj[m], dembed[m]
        dp = (u * d - u * u * u * y * jnp.sum(y * d, axis=-1, keepdims=True)).astype(BF16)
        dproj[m] = dp
        dh = dot_t(dp, weight[m])
        gains[m:m + 1, :] = jnp.sum(dh * normal[m], axis=0, keepdims=True)
        shifts[m:m + 1, :] = jnp.sum(dh, axis=0, keepdims=True)
        back[m] = norm_back(normal[m], inverse[m], dh * vector(vec, H_GAIN + m))
        dcls[m] = back[m, pl.ds(pl.multiple_of(16 * me, 16), 16), :]


def contrast(dims, total, at, blocks, vec, weight, scale):
    model = weight.shape[1]
    rows = 16 * len(blocks) * blocks[0].shape[0]
    args = tuple(blocks) + (vec, weight, scale)
    shapes = [((2, rows, model), BF16), ((2, rows, weight.shape[2]), BF16), ((2, 16, model), F32),
              ((2, model), F32), ((2, model), F32), ((2, 128), F32)]

    def kernel(at, *refs):
        contrast_kernel(dims, total, at, refs[:len(blocks)], *refs[len(blocks):])

    return pl.pallas_call(
        kernel,
        grid_spec=pltpu.PrefetchScalarGridSpec(
            num_scalar_prefetch=1, grid=(1,),
            in_specs=[spec_whole(v) for v in args],
            out_specs=[pl.BlockSpec(s, lambda i, o, n=len(s): (0,) * n) for s, _ in shapes],
            scratch_shapes=[pltpu.VMEM((2, rows, model), F32)] * 2,
        ),
        out_shape=[jax.ShapeDtypeStruct(s, t) for s, t in shapes],
        compiler_params=params(),
        cost_estimate=pl.CostEstimate(flops=1_000_000_000, bytes_accessed=5_000_000, transcendentals=0),
        name="contrast",
    )(at, *args)


def contrast_large(dims, total, at, blocks, vec, weight, scale):
    model = weight.shape[1]
    held = jnp.concatenate(blocks)
    held = held[jnp.arange(held.shape[0]) ^ at[0]]
    rows = jnp.asarray([r for r in range(16) if r % 4 < dims.quarter])
    cls = jnp.transpose(held[:, :, rows], (1, 0, 2, 3)).reshape(2, -1, model)
    gain, shift = vec[H_GAIN:H_GAIN + 2, None], vec[H_SHIFT:H_SHIFT + 2, None]
    n, r = normalise(cls)
    head_in = (n * gain + shift).astype(BF16)
    proj = jnp.einsum("mrc,mce->mre", head_in, weight, preferred_element_type=F32)
    unit = lax.rsqrt(jnp.sum(proj * proj, axis=-1, keepdims=True) + 1e-6)
    embed = (proj * unit).astype(BF16)
    sharp = jnp.exp(scale[0, 0])
    logits = sharp * dot_t(embed[0], embed[1])
    row_lse = jax.nn.logsumexp(logits, axis=1, keepdims=True)
    col_lse = jax.nn.logsumexp(logits, axis=0, keepdims=True)
    dlogits = jnp.exp(logits - row_lse) + jnp.exp(logits - col_lse) - 2.0 * jnp.eye(total, dtype=F32)
    dlogits = dlogits / (2 * total)
    loss = (jnp.sum(row_lse) + jnp.sum(col_lse) - 2.0 * jnp.trace(logits)) / (2 * total)
    slope = jnp.sum(dlogits * logits)
    high = lax.Precision.HIGHEST
    wide = embed.astype(F32)
    dembed = sharp * jnp.stack([
        jnp.dot(dlogits, wide[1], precision=high, preferred_element_type=F32),
        jnp.dot(dlogits.T, wide[0], precision=high, preferred_element_type=F32)])
    dproj = (unit * dembed - unit ** 3 * proj * jnp.sum(proj * dembed, axis=-1, keepdims=True)).astype(BF16)
    dh = jnp.einsum("mre,mce->mrc", dproj, weight, preferred_element_type=F32)
    back = norm_back(n, r, dh * gain)
    pairs = 4 * dims.quarter
    own = lax.dynamic_slice_in_dim(back, at[0] * pairs, pairs, axis=1)
    dcls = jnp.zeros((2, 16, model), F32).at[:, rows].set(own)
    scalars = jnp.broadcast_to(jnp.stack([loss, slope])[:, None], (2, 128))
    return head_in, dproj, dcls, jnp.sum(dh * n, axis=1), jnp.sum(dh, axis=1), scalars


def own_pair(rows_of):
    return lambda i, o: (o[0] * rows_of + i, 0, 0)


def own_call(kernel, dims, name, order, blocks, img, txt, others, outs, scratch):
    model = img.shape[-1]
    block = pl.BlockSpec((1, dims.slab, model), lambda i, o: (i, 0, 0))
    specs = {
        "slab": (block, (dims.quarter, dims.slab, model)),
        "img": (pl.BlockSpec((1, dims.patches, model), lambda i, o: (i, 0, 0)), (dims.quarter, dims.patches, model)),
        "txt": (pl.BlockSpec((1, dims.caption, model), lambda i, o: (i, 0, 0)), (dims.quarter, dims.caption, model)),
        "sums": (pl.BlockSpec((8, model), lambda i, o: (0, 0)), (8, model)),
    }
    return pl.pallas_call(
        functools.partial(kernel, dims),
        grid_spec=pltpu.PrefetchScalarGridSpec(
            num_scalar_prefetch=1,
            grid=(dims.quarter,),
            in_specs=[block] * len(blocks) + [
                pl.BlockSpec((1, dims.patches, model), own_pair(dims.quarter)),
                pl.BlockSpec((1, dims.caption, model), own_pair(dims.quarter)),
            ] + [spec_whole(v) for v in others],
            out_specs=[specs[kind][0] for kind, _ in outs],
            scratch_shapes=[pltpu.VMEM((dims.slab, model), F32)] * scratch,
        ),
        out_shape=[jax.ShapeDtypeStruct(specs[kind][1], dtype) for kind, dtype in outs],
        compiler_params=params(),
        cost_estimate=pl.CostEstimate(flops=40_000_000, bytes_accessed=15_000_000, transcendentals=0),
        name=name,
    )(order, *blocks, img, txt, *others)


def start_own(rows, sums):
    @pl.when(pl.program_id(0) == 0)
    def _():
        rows[...] = jnp.zeros_like(rows)
        sums[...] = jnp.zeros_like(sums)


def add_class(dims, dcls, rows):
    i = pl.program_id(0)
    rows[0:1, :] += dcls[i, 0:1, :]
    rows[dims.ip:dims.ip + 1, :] += dcls[i, 1:2, :]


def final_kernel(dims, order, keep, recv, far, attended, img, txt, dcls, vec, fin_img, fin_txt, sums, rows):
    start_own(rows, sums)
    load_rows(dims, 0, img, txt, rows)
    add_class(dims, dcls, rows)
    for m, lo, hi in ((0, 0, dims.ip), (1, dims.ip, dims.slab)):
        b = keep[0, lo:hi].astype(F32) + recv[0, lo:hi].astype(F32) + far[0, lo:hi].astype(F32)
        b = b + vector(vec, F_BIAS + m)
        f = attended[0, lo:hi, :] + vector(vec, F_SCALE) * b
        if m == 0:
            fin_img[0] = f[0:dims.patches].astype(BF16)
        else:
            fin_txt[0] = f[0:dims.caption].astype(BF16)
        g = rows[lo:hi, :]
        sums[0:1, :] += jnp.sum(g * b, axis=0, keepdims=True)
        sums[1 + m:2 + m, :] += jnp.sum(g, axis=0, keepdims=True) * vector(vec, F_SCALE)


def final_rows(dims, order, keep, recv, far, attended, img, txt, dcls, vec):
    return own_call(final_kernel, dims, "final_rows", order, (keep, recv, far, attended), img, txt,
                    (dcls, vec), (("img", BF16), ("txt", BF16), ("sums", F32)), 1)


def norm_two_kernel(dims, order, keep, recv, far, attended, a_keep, a_recv, img, txt, dcls, x0, x1, x2, x3,
                    vec, dattended, dattn, sums, rows, ups):
    i = pl.program_id(0)
    start_own(rows, sums)
    load_rows(dims, 0, img, txt, rows)
    add_class(dims, dcls, rows)
    ups[...] = keep[0].astype(F32) + recv[0].astype(F32) + far[0].astype(F32)
    for m, at in ((0, 0), (1, dims.ip)):
        extra = [x[m, pl.ds(own_row(dims, r, 0) + i, 1), :] for x, r in ((x0, 0), (x1, 2), (x2, 1), (x3, 3))]
        ups[at:at + 1, :] += (extra[0] + extra[1]) + (extra[2] + extra[3])
    for m, lo, hi in ((0, 0, dims.ip), (1, dims.ip, dims.slab)):
        n, r = normalise(attended[0, lo:hi, :])
        dy = ups[lo:hi, :]
        sums[m:m + 1, :] += jnp.sum(dy * n, axis=0, keepdims=True)
        sums[2 + m:3 + m, :] += jnp.sum(dy, axis=0, keepdims=True)
        d = rows[lo:hi, :] + norm_back(n, r, dy * vector(vec, GAIN2 + m))
        dattended[0, lo:hi, :] = d
        sd = d * vector(vec, A_SCALE)
        dattn[0, lo:hi, :] = sd.astype(BF16)
        a = a_keep[0, lo:hi, :].astype(F32) + a_recv[0, lo:hi, :].astype(F32) + vector(vec, A_BIAS)
        sums[4:5, :] += jnp.sum(d * a, axis=0, keepdims=True)
        sums[5:6, :] += jnp.sum(sd, axis=0, keepdims=True)


def norm_two(dims, order, keep, recv, far, attended, a_keep, a_recv, img, txt, dcls, parts, vec):
    return own_call(norm_two_kernel, dims, "norm_two", order, (keep, recv, far, attended, a_keep, a_recv), img, txt,
                    (dcls,) + tuple(parts) + (vec,), (("slab", F32), ("slab", BF16), ("sums", F32)), 2)


def norm_one_kernel(dims, order, keep, recv, dattended, img, txt, vec, d_img, d_txt, sums, rows):
    start_own(rows, sums)
    load_rows(dims, 0, img, txt, rows)
    n, r = normalise(rows[...])
    dy = keep[0].astype(F32) + recv[0].astype(F32)
    sums[0:1, :] += jnp.sum(dy * n, axis=0, keepdims=True)
    sums[1:2, :] += jnp.sum(dy, axis=0, keepdims=True)
    d = dattended[0] + norm_back(n, r, dy * vector(vec, GAIN1))
    d_img[0] = d[0:dims.patches].astype(BF16)
    d_txt[0] = d[dims.ip:dims.ip + dims.caption].astype(BF16)


def norm_one(dims, order, keep, recv, dattended, img, txt, vec):
    return own_call(norm_one_kernel, dims, "norm_one", order, (keep, recv, dattended), img, txt,
                    (vec,), (("img", BF16), ("txt", BF16), ("sums", F32)), 1)


def back_step(dims, tiles, lens, whose, dattn, normed, qkv, mixed, dmixed, dqkv, acc, col_sums, w, ow):
    quarter, slab = dims.quarter, dims.slab
    count, width = quarter * slab, tiles * 128
    model = normed.shape[-1]
    d_rows = dattn[...].reshape(count, model)
    dmixed[...] = dot_t(d_rows, ow[...]).astype(BF16).reshape(quarter, slab, width)

    def one_pair(p, c):
        length = lens[whose * quarter + p]
        for lo, hi, start, limit in key_tail(dims, length):
            for g in range(tiles):
                at = [slice((t * tiles + g) * 128, (t * tiles + g + 1) * 128) for t in range(3)]
                q, k, v = [qkv[p, lo:hi, c] for c in at]
                q = scaled(q)
                qq = split_pair(q)
                dd = split_pair(dmixed[p, lo:hi, g * 128:(g + 1) * 128])
                w_ = softmax_keys(hide(dot_t(k, qq), start, limit))
                dw = dot_t(v, dd)
                dqkv[p, lo:hi, at[2]] = dot(w_.astype(BF16), dd).astype(BF16)
                ds = (w_ * (dw - jnp.sum(w_ * dw, axis=0, keepdims=True))).astype(BF16)
                dqkv[p, lo:hi, at[1]] = dot(ds, qq).astype(BF16)
                dqkv[p, lo:hi, at[0]] = (join_pair(t_dot(ds, k)) * HEAD_DIM ** -0.5).astype(BF16)
        return c

    lax.fori_loop(0, quarter, one_pair, 0)
    dp = dqkv[...].reshape(count, 3 * width)
    part = dot(dp, w[...])
    acc[:, 0:3 * width] += t_dot(normed[...].reshape(count, model), dp)
    acc[:, 3 * width:] += t_dot(d_rows, mixed[...].reshape(count, width))
    col_sums[...] += jnp.sum(dp.astype(F32), axis=0, keepdims=True)
    return part


def attend_back_kernel(dims, far, order, lens, d_own, d_peer, normed, qkv, mixed, wq, wo, wf, *refs):
    if not far:
        prior_keep, prior_send, *refs = refs
    keep, send, grad, *refs = refs
    if far:
        grad_rest, *refs = refs
    col_sums, dattn, dmixed, dqkv, acc, w, ow = refs
    i = pl.program_id(0)
    slab, quarter, local = dims.slab, dims.quarter, dims.local
    two, one_head = parts_of(dims)
    tiles = 2 if far else 1
    width = tiles * two
    count = quarter * slab
    model = normed.shape[-1]

    @pl.when(i == 0)
    def _():
        dattn[...] = d_own[...]
        acc[...] = jnp.zeros_like(acc)
        col_sums[...] = jnp.zeros_like(col_sums)
        for t in range(4):
            dst, at = (w, t * width) if t < 3 else (ow, 0)
            own, start = (wq, t * local) if t < 3 else (wo, 0)
            if far:
                copy_rows(dst, at, wf, t * local, two)
                copy_rows(dst, at + two, own, start + two, one_head)
                copy_rows(dst, at + two + one_head, wf, t * local + two, one_head)
            else:
                copy_rows(dst, at, own, start, two)

    @pl.when(i == 1)
    def _():
        dattn[...] = d_peer[...]

    part = back_step(dims, tiles, lens, order[2 * i], dattn, normed, qkv, mixed,
                     dmixed, dqkv, acc, col_sums, w, ow)

    @pl.when(i == 0)
    def _():
        prior = 0.0 if far else prior_keep[...].reshape(count, model).astype(F32)
        keep[...] = (part + prior).astype(BF16).reshape(quarter, slab, model)

    @pl.when(i == 1)
    def _():
        prior = 0.0 if far else prior_send[...].reshape(count, model).astype(F32)
        send[...] = (part + prior).astype(BF16).reshape(quarter, slab, model)
        for t in range(4):
            grad[:, t * two:(t + 1) * two] = acc[:, t * width:t * width + two].astype(BF16)
            if far:
                at = t * width + two
                to = 4 * two + t * one_head
                grad[:, to:to + one_head] = acc[:, at + one_head:at + two].astype(BF16)
                grad_rest[:, t * one_head:(t + 1) * one_head] = acc[:, at:at + one_head].astype(BF16)


def attend_back(dims, far, order, lens, d_own, d_peer, normed, qkv, mixed, wq, wo, wf, prior=()):
    model = normed.shape[-1]
    slab, quarter = dims.slab, dims.quarter
    width = 256 if far else 128
    one = pl.BlockSpec((quarter, slab, model), lambda i, o, n: (0, 0, 0))
    stride = normed.shape[0] // (2 * quarter)
    step = lambda cols: pl.BlockSpec((quarter, slab, cols), lambda i, o, n: (stride * i, 0, 0))
    grads = (768, 256) if far else (512,)
    specs = [one, one] + [pl.BlockSpec((model, n), lambda i, o, n_: (0, 0)) for n in grads]
    specs += [pl.BlockSpec((1, 3 * width), lambda i, o, n: (0, 0))]
    shapes = [
        jax.ShapeDtypeStruct((quarter, slab, model), BF16),
        jax.ShapeDtypeStruct((quarter, slab, model), BF16),
    ] + [jax.ShapeDtypeStruct((model, n), BF16) for n in grads] + [jax.ShapeDtypeStruct((1, 3 * width), F32)]
    scratch = [
        pltpu.VMEM((quarter, slab, model), BF16),
        pltpu.VMEM((quarter, slab, width), BF16),
        pltpu.VMEM((quarter, slab, 3 * width), BF16),
        pltpu.VMEM((model, 4 * width), F32),
        pltpu.VMEM((3 * width, model), BF16),
        pltpu.VMEM((width, model), BF16),
    ]
    return pl.pallas_call(
        functools.partial(attend_back_kernel, dims, far),
        grid_spec=pltpu.PrefetchScalarGridSpec(
            num_scalar_prefetch=2,
            grid=(2,),
            in_specs=[one, one, step(model), step(3 * width), step(width), spec_whole(wq), spec_whole(wo),
                      spec_whole(wf)] + [one] * len(prior),
            out_specs=specs,
            scratch_shapes=scratch,
        ),
        out_shape=shapes,
        compiler_params=params(),
        cost_estimate=pl.CostEstimate(
            flops=32 * quarter * slab * model * width, bytes_accessed=20_000_000, transcendentals=0),
        name="attend_back_far" if far else "attend_back_own",
    )(order, lens, d_own, d_peer, normed, qkv, mixed, wq, wo, wf, *prior)


def swap(value, axis, bit):
    size = lax.axis_size(axis)
    return lax.ppermute(value, axis, [(j, j ^ bit) for j in range(size)])


def to_core(value):
    return swap(value, "mp", 1)


def to_y(value):
    return swap(value, "mp", 2)


def from_others(value, axis, first, count):
    return [value] + [swap(value, axis, k * first) for k in range(1, count)]


def add_tree(parts):
    while len(parts) > 1:
        parts = [a + b for a, b in zip(parts[::2], parts[1::2])]
    return parts[0]


def sum_over(value, axis):
    first = 1
    while first < lax.axis_size(axis):
        count = min(8, lax.axis_size(axis) // first)
        value = add_tree(from_others(value, axis, first, count))
        first *= count
    return value


def gather_batch(value):
    parts = [value]
    first = 1
    size = lax.axis_size("batch")
    while first < size:
        count = min(8, size // first)
        whole = jnp.concatenate(parts) if len(parts) > 1 else parts[0]
        parts = from_others(whole, "batch", first, count)
        first *= count
    return parts


def gather_rows(own, me):
    near = jnp.stack([own, to_y(own)])
    far = to_core(near)
    out = jnp.zeros((4,) + own.shape, own.dtype)
    for r, value in enumerate((near[0], near[1], far[0], far[1])):
        out = lax.dynamic_update_slice(out, value[None], (me ^ ORDER[r],) + (0,) * own.ndim)
    return out.reshape((4 * own.shape[0],) + own.shape[1:])


def add_low(a, b):
    return (a.astype(F32) + b.astype(F32)).astype(BF16)


MESH = pl.DeviceIdType.MESH


class Place:
    def __init__(self):
        self.b, self.m = lax.axis_index("batch"), lax.axis_index("mp")
        self.z, self.x = self.b // 2, self.b % 2
        self.y, self.c = self.m // 2, self.m % 2
        self.core = (self.b, 2 * self.y + 1 - self.c)
        self.near = (self.b, 2 * (1 - self.y) + self.c)
        self.across = (self.b, 2 * (1 - self.y) + 1 - self.c)
        self.side = (2 * self.z + 1 - self.x, self.m)
        self.z_pair = self.z + 1 - 2 * (self.z % 2)
        self.z_far = (self.z + 2) % 4
        self.z_rest = (self.z_pair + 2) % 4
        self.paired = (2 * self.z_pair + self.x, self.m)
        self.opposite = (2 * self.z_far + self.x, self.m)
        self.batch = [((self.b + k) % 8, self.m) for k in range(1, 8)]

    def quarter(self, far_y, far_core):
        return 2 * ((self.y + far_y) % 2) + (self.c + far_core) % 2


def meet(peers):
    barrier = pltpu.get_barrier_semaphore()
    for peer in peers:
        pl.semaphore_signal(barrier, inc=1, device_id=peer, device_id_type=MESH)
    pl.semaphore_wait(barrier, len(peers))


def remote(src, dst, send_sem, recv_sem, at, device):
    return pltpu.make_async_remote_copy(
        src_ref=src, dst_ref=dst, send_sem=send_sem.at[at], recv_sem=recv_sem.at[at],
        device_id=device, device_id_type=MESH)


def front_kernel(dims, lens, img, txt, vectors, bias, own_w, own_o,
                 vec, normed, qkv, mixed, qkv_far, mixed_far, far_w, attended, attn, expert, expert_peer, cls, cls_peer,
                 rows, w, w2, ow, b, wf, far_bias, n_all, rest, m_all, m_far, q_own, q_far, a_send, a_recv, e_send, c_recv,
                 local_sem, send_sem, recv_sem):
    here = Place()
    i = pl.program_id(0)
    local, quarter, slab, ip = dims.local, dims.quarter, dims.slab, dims.ip
    two, one_head = parts_of(dims)
    count = quarter * slab
    model = img.shape[-1]
    at = i % 4
    whose = here.quarter(at % 2, 1 - at // 2)
    sent_w = [remote(own_w, wf.at[pl.ds(0, 3 * local)], send_sem, recv_sem, 0, here.near),
              remote(own_o, wf.at[pl.ds(3 * local, local)], send_sem, recv_sem, 1, here.near),
              remote(bias, far_bias, send_sem, recv_sem, 2, here.near)]
    sent_a = [remote(a_send.at[j], a_recv.at[j], send_sem, recv_sem, 3 + j, here.core) for j in range(2)]

    def e_over(j):
        return remote(e_send.at[j], expert_peer.at[j], send_sem, recv_sem, 5 + j, here.core)

    def e_here(j):
        return pltpu.make_async_copy(e_send.at[j], expert.at[j], local_sem.at[1 + j])

    sent_c = remote(cls, c_recv, send_sem, recv_sem, 5 + 2 * quarter, here.core)
    keep_w = pltpu.make_async_copy(wf, far_w, local_sem.at[0])
    sent_e = [e_over(j) for j in range(2 * quarter)]
    keep_e = [e_here(j) for j in range(2 * quarter)]

    @pl.when(i == 0)
    def _():
        meet([here.core, here.near])
        for copy in sent_w:
            copy.start()
        fill(vec, vectors)
        rows[...] = jnp.zeros_like(rows)
        b[...] = jnp.zeros_like(b)
        w[...] = jnp.zeros_like(w)
        cls[...] = jnp.zeros_like(cls)
        for t in range(3):
            copy_rows(w, t * 2 * two, own_w, t * local, local)
        b[0:1, 0:local] = bias[0:1, :]
        b[0:1, 4 * two:4 * two + local] = bias[1:2, :]

    def project(weights):
        proj = dot_t(n_all[at].reshape(count, model), weights[...]) + b[0:1, :]
        return proj.astype(BF16).reshape(quarter, slab, 6 * two)

    @pl.when(i < 4)
    def _():
        def one_norm(p, c):
            load_rows(dims, p, img, txt, rows)
            n, _ = normalise(rows[...])
            n_all[at, p] = (n * vector(vec, GAIN1) + vector(vec, SHIFT1)).astype(BF16)
            return c

        lax.fori_loop(0, quarter, one_norm, 0)
        proj = project(w)
        for t in range(3):
            q_own[:, :, t * two:(t + 1) * two] = proj[:, :, 2 * t * two:(2 * t + 1) * two]
            rest[at, :, :, t * two:(t + 1) * two] = proj[:, :, (2 * t + 1) * two:(2 * t + 2) * two]
        attend_tiles(dims, lens, whose, q_own, m_all.at[at])

        @pl.when(i % 2 == 0)
        def _():
            normed[...] = n_all[at]
            qkv[...] = q_own[...]
            mixed[...] = m_all[at]

    @pl.when(i == 4)
    def _():
        for copy in sent_w:
            copy.wait_recv()
        keep_w.start()
        w2[...] = jnp.zeros_like(w2)
        b[...] = jnp.zeros_like(b)
        for t in range(3):
            copy_rows(w2, t * 2 * two, wf, t * local, two)
            copy_rows(w2, t * 2 * two + two + one_head, wf, t * local + two, one_head)
        for t, to in ((0, 0), (1, 4 * two)):
            b[0:1, to:to + two] = far_bias[t:t + 1, 0:two]
            b[0:1, to + two + one_head:to + 2 * two] = far_bias[t:t + 1, two:]
        copy_rows(ow, 0, own_o, 0, two)
        copy_rows(ow, two, wf, 3 * local, two)
        copy_rows(ow, 2 * two, own_o, two, one_head)
        copy_rows(ow, 2 * two + one_head, wf, 3 * local + two, one_head)

    @pl.when(i >= 4)
    def _():
        proj = project(w2)
        for t in range(3):
            to = 2 * t * two
            q_far[:, :, to:to + two] = proj[:, :, to:to + two]
            q_far[:, :, to + two:to + 2 * two] = (
                proj[:, :, to + two:to + 2 * two] + rest[at, :, :, t * two:(t + 1) * two])
        attend_tiles(dims, lens, whose, q_far, m_far)

        @pl.when(i % 2 == 0)
        def _():
            qkv_far[...] = q_far[...]
            mixed_far[...] = m_far[...]

        part = dot(m_all[at].reshape(count, two), ow[0:two, :])
        part = part + dot(m_far[...].reshape(count, 2 * two), ow[two:, :])
        part = part.reshape(quarter, slab, model)

        @pl.when(i < 6)
        def _():
            a_send[at] = part.astype(BF16)

        for j in range(2):
            @pl.when(i == 4 + j)
            def _():
                sent_a[j].start()

        for j in range(2):
            @pl.when(i == 6 + j)
            def _():
                sent_a[j].wait_recv()

        @pl.when(i >= 6)
        def _():
            j = i - 6
            for p in range(quarter):
                load_rows(dims, p, img, txt, rows)
                a = part[p] + a_recv[j, p].astype(F32)
                x = rows[...] + vector(vec, A_SCALE) * (a + vector(vec, A_BIAS))
                n, _ = normalise(x)
                e_img = n[0:ip] * vector(vec, GAIN2) + vector(vec, SHIFT2)
                e_txt = n[ip:] * vector(vec, GAIN2 + 1) + vector(vec, SHIFT2 + 1)
                r = j * quarter + p
                e_send[r, 0:ip, :] = e_img.astype(BF16)
                e_send[r, ip:, :] = e_txt.astype(BF16)
                e_over(r).start()
                e_here(r).start()
                for k, v in enumerate((x[0:1], x[ip:ip + 1], e_img[0:1], e_txt[0:1])):
                    cls[k, pl.ds(r, 1), :] = v

                @pl.when(j == 0)
                def _():
                    attended[p] = x
                    attn[p] = a


    @pl.when(i == 7)
    def _():
        sent_c.start()
        keep_w.wait()
        for copy in keep_e:
            copy.wait()
        sent_c.wait()
        cls_peer[...] = c_recv[...]
        for copy in sent_e:
            copy.wait()
        for copy in sent_w + sent_a:
            copy.wait_send()


def fill(table, vectors):
    table[...] = jnp.zeros_like(table)
    at = 0
    for v in vectors:
        n = v.shape[0] if len(v.shape) == 2 else 1
        table[at:at + n, :] = v[...].reshape(n, table.shape[1])
        at += n


def front(dims, lens, img, txt, vectors, bias, own_w, own_o):
    model = img.shape[-1]
    quarter, slab, local = dims.quarter, dims.slab, dims.local
    held = pl.BlockSpec(memory_space=pltpu.VMEM)
    away = pl.BlockSpec(memory_space=pl.ANY)

    def states_at(i):
        return Place().quarter(i % 2, 1 - i % 4 // 2), 0, 0

    own_block = lambda cols: pl.BlockSpec((quarter, slab, cols), lambda i: (jnp.where(i < 2, 1, 0), 0, 0))
    far_block = lambda cols: pl.BlockSpec((quarter, slab, cols), lambda i: (jnp.where(i < 6, 1, 0), 0, 0))
    six = lambda cols: jax.ShapeDtypeStruct((2 * quarter, slab, cols), BF16)
    block = lambda cols: (quarter, slab, cols)
    n_remote = 6 + 2 * quarter
    return pl.pallas_call(
        lambda lens, img, txt, *refs: front_kernel(
            dims, lens, img, txt, refs[:len(vectors)], *refs[len(vectors):]),
        grid=(8,),
        in_specs=[pl.BlockSpec(memory_space=pltpu.SMEM),
                  pl.BlockSpec((quarter, dims.patches, model), states_at),
                  pl.BlockSpec((quarter, dims.caption, model), states_at)] + [held] * (3 + len(vectors)),
        out_specs=[held, own_block(model), own_block(384), own_block(128), far_block(768), far_block(256),
                   away, held, held, away, away, held, held],
        out_shape=[jax.ShapeDtypeStruct((16, model), F32), six(model), six(384), six(128), six(768), six(256),
                   jax.ShapeDtypeStruct((4 * local, model), BF16),
                   jax.ShapeDtypeStruct(block(model), F32), jax.ShapeDtypeStruct(block(model), F32),
                   six(model), six(model),
                   jax.ShapeDtypeStruct((4, 8, model), F32), jax.ShapeDtypeStruct((4, 8, model), F32)],
        scratch_shapes=[
            pltpu.VMEM((slab, model), F32), pltpu.VMEM((768, model), BF16), pltpu.VMEM((768, model), BF16),
            pltpu.VMEM((384, model), BF16), pltpu.VMEM((8, 768), F32), pltpu.VMEM((4 * local, model), BF16),
            pltpu.VMEM((2, local), F32),
            pltpu.VMEM((4,) + block(model), BF16), pltpu.VMEM((4,) + block(384), BF16),
            pltpu.VMEM((4,) + block(128), BF16), pltpu.VMEM(block(256), BF16),
            pltpu.VMEM(block(384), BF16), pltpu.VMEM(block(768), BF16),
            pltpu.VMEM((2,) + block(model), BF16), pltpu.VMEM((2,) + block(model), BF16),
            pltpu.VMEM((2 * quarter, slab, model), BF16), pltpu.VMEM((4, 8, model), F32),
            pltpu.SemaphoreType.DMA((1 + 2 * quarter,)),
            pltpu.SemaphoreType.DMA((n_remote,)), pltpu.SemaphoreType.DMA((n_remote,)),
        ],
        compiler_params=params(collective_id=6, has_side_effects=True),
        cost_estimate=pl.CostEstimate(
            flops=16 * quarter * slab * model * 1152, bytes_accessed=40_000_000, transcendentals=0),
        name="front",
    )(lens, img, txt, *vectors, bias, own_w, own_o)


def middle_kernel(dims, total, img, txt, own, peer, cls_own, cls_peer, vec, up, up_bias, down, weight, scale,
                  act, dup, ddn, dexp, d_own, d_near, bias_grad, class_e, c_act, c_dup, c_ddn, dcls,
                  head_in, dproj, gains, shifts, scalars,
                  bx, bd, rx, rd, x_near, x_far, ins, rows, part, parts, cls, back, cot, c_rows, extra, extras,
                  send_sem, recv_sem):
    here = Place()
    ip, slab, quarter = dims.ip, dims.slab, dims.quarter
    i = pl.program_id(0)
    model = own.shape[-1]
    mp_peers = [here.core, here.near, here.across]
    of = [here.quarter(0, 0), here.quarter(1, 0), here.quarter(0, 1), here.quarter(1, 1)]

    sent_x = [remote(bx.at[2 * j], rx.at[j], send_sem, recv_sem, j, here.core) for j in range(2)]
    sent_d = [remote(bd.at[2 * j], rd.at[j], send_sem, recv_sem, 2 + j, here.core) for j in range(2)]
    sent_near = remote(x_near, x_far, send_sem, recv_sem, 4, here.near)
    sent_part = [remote(part, parts.at[k], send_sem, recv_sem, 5 + k, mp_peers[k]) for k in range(3)]
    sent_extra = [remote(extra, extras.at[k], send_sem, recv_sem, 8 + k, mp_peers[k]) for k in range(3)]
    sent_cls = [remote(cls.at[here.b], cls.at[here.b], send_sem, recv_sem, 11 + k, here.batch[k]) for k in range(7)]

    @pl.when(i == 0)
    def _():
        rows[...] = jnp.zeros_like(rows)
        bias_grad[...] = jnp.zeros_like(bias_grad)
        for m in range(2):
            e = jnp.concatenate([cls_own[2 + m], cls_peer[2 + m]], axis=0).astype(BF16)
            class_e[m] = e
            u = dot(e, up[m]) + up_bias[m:m + 1]
            part[m] = dot(gelu_low(u), down[m])
        meet(mp_peers + here.batch)
        for copy in sent_part:
            copy.start()
        ins[...] = peer[quarter:, :, :]

    @pl.when(i == 1)
    def _():
        for copy in sent_part:
            copy.wait_recv()
        for m in range(2):
            cls[here.b, m] = jnp.zeros(cls.shape[2:], F32)
            for r in range(4):
                half, at = (cls_own, cls_peer)[r // 2], quarter * (r % 2)
                for p in range(quarter):
                    line = [d[m, own_row(dims, s, p):own_row(dims, s, p) + 1, :]
                            for d, s in ((part, r), (parts.at[0], r ^ 2), (parts.at[1], r ^ 1), (parts.at[2], r ^ 3))]
                    x = (line[0] + line[1]) + (line[2] + line[3]) + vector(vec, F_BIAS + m)
                    x = half[m, at + p:at + p + 1, :] + vector(vec, F_SCALE) * x
                    cls[here.b, m, pl.ds(4 * of[r] + p, 1), :] = x
        for copy in sent_cls:
            copy.start()
        ins[...] = own[quarter:, :, :]

    @pl.when(i == 2)
    def _():
        ins[...] = peer[:quarter, :, :]

    @pl.when(i == 3)
    def _():
        ins[...] = own[:quarter, :, :]
        for copy in sent_cls:
            copy.wait_recv()
        n_rows = 16 * cls.shape[0]
        sharp = jnp.exp(scale[...])
        col_at = lax.broadcasted_iota(jnp.int32, (1, n_rows), 1)
        row_at = lax.broadcasted_iota(jnp.int32, (n_rows, 1), 0)
        col_ok = (col_at % 4) < quarter
        row_ok = (row_at % 4) < quarter
        normal, inverse, proj, unit, embed = [], [], [], [], []
        for m in range(2):
            n, r = normalise(cls[:, m].reshape(n_rows, model))
            h = (n * vector(vec, H_GAIN + m) + vector(vec, H_SHIFT + m)).astype(BF16)
            head_in[m] = h
            y = dot(h, weight[m])
            u = lax.rsqrt(jnp.sum(y * y, axis=-1, keepdims=True) + 1e-6)
            normal.append(n)
            inverse.append(r)
            proj.append(y)
            unit.append(u)
            embed.append((y * u).astype(BF16))
        ok = row_ok & col_ok
        logits = sharp * dot_t(embed[0], embed[1])
        masked = jnp.where(ok, logits, -1e30)
        row_max = jnp.max(masked, axis=1, keepdims=True)
        row_lse = row_max + jnp.log(jnp.sum(jnp.exp(masked - row_max), axis=1, keepdims=True))
        col_max = jnp.max(masked, axis=0, keepdims=True)
        col_lse = col_max + jnp.log(jnp.sum(jnp.exp(masked - col_max), axis=0, keepdims=True))
        same = (row_at == col_at) & ok
        both = jnp.exp(masked - row_lse) + jnp.exp(masked - col_lse)
        dlogits = jnp.where(ok, jnp.where(same, both - 2.0, both) * (1.0 / (2 * total)), 0.0)
        diagonal = jnp.sum(jnp.where(same, logits, 0.0), axis=1, keepdims=True)
        lines = jnp.sum(jnp.where(row_ok, row_lse - 2.0 * diagonal, 0.0), axis=0, keepdims=True)
        lines = lines + jnp.sum(jnp.where(col_ok, col_lse, 0.0), axis=1, keepdims=True)
        slope = jnp.sum(jnp.sum(dlogits * logits, axis=1, keepdims=True), axis=0, keepdims=True)
        scalars[0:1, :] = jnp.broadcast_to(lines * (1.0 / (2 * total)), (1, 128))
        scalars[1:2, :] = jnp.broadcast_to(slope, (1, 128))
        high = lax.Precision.HIGHEST
        wide = [e.astype(F32) for e in embed]
        dembed = [
            sharp * jnp.dot(dlogits, wide[1], precision=high, preferred_element_type=F32),
            sharp * lax.dot_general(dlogits, wide[0], (((0,), (0,)), ((), ())), precision=high,
                                    preferred_element_type=F32),
        ]
        c_rows[...] = jnp.zeros_like(c_rows)
        dcls[...] = jnp.zeros_like(dcls)
        for m in range(2):
            for p in range(quarter):
                src = (img, txt)[m]
                cot[m, 8 * 3 + p:8 * 3 + p + 1, :] = src[p, 0:1, :].astype(F32)
        for m in range(2):
            u, y, d = unit[m], proj[m], dembed[m]
            dp = (u * d - u * u * u * y * jnp.sum(y * d, axis=-1, keepdims=True)).astype(BF16)
            dproj[m] = dp
            dh = dot_t(dp, weight[m])
            gains[m:m + 1, :] = jnp.sum(dh * normal[m], axis=0, keepdims=True)
            shifts[m:m + 1, :] = jnp.sum(dh, axis=0, keepdims=True)
            back[m] = norm_back(normal[m], inverse[m], dh * vector(vec, H_GAIN + m))
            for r in range(4):
                step = (3, 1, 2, 0)[r]
                for p in range(quarter):
                    g = back[m, pl.ds(16 * here.b + 4 * of[r] + p, 1), :]
                    at = own_row(dims, r, p)
                    c_rows[m, at:at + 1, :] = cot[m, 8 * step + p:8 * step + p + 1, :] + g
                    if r == 0:
                        dcls[p, m:m + 1, :] = g
            u = dot(class_e[m], up[m]) + up_bias[m:m + 1]
            big, small = gelu_parts(u)
            c_act[m] = (u * big).astype(BF16)
            g = (c_rows[m] * vector(vec, F_SCALE)).astype(BF16)
            c_ddn[m] = g
            du = dot_t(g, down[m]) * (big + u * small)
            bias_grad[m:m + 1, :] += jnp.sum(du, axis=0, keepdims=True)
            low = du.astype(BF16)
            c_dup[m] = low
            extra[m] = dot_t(low, up[m])
        for copy in sent_extra:
            copy.start()

    at = lax.broadcasted_iota(jnp.int32, (slab, 1), 0)
    inner = (at != 0) & (at != ip)

    def one(p, c):
        load_rows(dims, p, img, txt, rows)
        cot[0, pl.ds(8 * i + p, 1), :] = rows[0:1, :]
        cot[1, pl.ds(8 * i + p, 1), :] = rows[ip:ip + 1, :]
        ddn[p] = jnp.where(inner, rows[...] * vector(vec, F_SCALE), 0.0).astype(BF16)
        return c

    lax.fori_loop(0, quarter, one, 0)
    for m, lo, hi in ((0, 0, ip), (1, ip, slab)):
        count = quarter * (hi - lo)
        e = ins[:, lo:hi, :].reshape(count, model)
        u = dot(e, up[m]) + up_bias[m:m + 1]
        big, small = gelu_parts(u)
        a = (u * big).astype(BF16)
        act[:, lo:hi, :] = a.reshape(quarter, hi - lo, -1)
        slope = big + u * small
        bd[i, :, lo:hi, :] = dot(a, down[m]).astype(BF16).reshape(quarter, hi - lo, model)
        g = ddn[:, lo:hi, :].reshape(count, model)
        du = dot_t(g, down[m]) * slope
        bias_grad[m:m + 1, :] += jnp.sum(du, axis=0, keepdims=True)
        low = du.astype(BF16)
        dup[:, lo:hi, :] = low.reshape(quarter, hi - lo, -1)
        bx[i, :, lo:hi, :] = dot_t(low, up[m]).astype(BF16).reshape(quarter, hi - lo, model)

    for j in range(2):
        @pl.when(i == 2 * j)
        def _():
            sent_x[j].start()
            sent_d[j].start()

    @pl.when(i == 1)
    def _():
        sent_x[0].wait_recv()

        def add_x(p, c):
            x_near[p] = (bx[1, p].astype(F32) + rx[0, p].astype(F32)).astype(BF16)
            return c

        lax.fori_loop(0, quarter, add_x, 0)
        sent_near.start()
        sent_d[0].wait_recv()

        def add_d(p, c):
            d_near[p] = (bd[1, p].astype(F32) + rd[0, p].astype(F32)).astype(BF16)
            return c

        lax.fori_loop(0, quarter, add_d, 0)

    @pl.when(i == 3)
    def _():
        sent_d[1].wait_recv()

        def add_d(p, c):
            d_own[p] = bd[3, p].astype(F32) + rd[1, p].astype(F32)
            return c

        lax.fori_loop(0, quarter, add_d, 0)
        sent_x[1].wait_recv()
        sent_near.wait_recv()

        def add_x(p, c):
            dexp[p] = bx[3, p].astype(F32) + rx[1, p].astype(F32) + x_far[p].astype(F32)
            return c

        lax.fori_loop(0, quarter, add_x, 0)
        for copy in sent_extra:
            copy.wait_recv()
        for m in range(2):
            for p in range(quarter):
                line = [x[m, own_row(dims, r, p):own_row(dims, r, p) + 1, :]
                        for x, r in ((extra, 0), (extras.at[0], 2), (extras.at[1], 1), (extras.at[2], 3))]
                dexp[p, m * ip:m * ip + 1, :] += (line[0] + line[1]) + (line[2] + line[3])
        for copy in sent_x + sent_d + [sent_near] + sent_part + sent_extra + sent_cls:
            copy.wait_send()


def middle(dims, total, img, txt, own, peer, cls_own, cls_peer, vec, up, up_bias, down, weight, scale):
    model = own.shape[-1]
    hidden = up.shape[-1]
    slab, quarter = dims.slab, dims.quarter
    batch = 8

    def cot_at(i):
        here = Place()
        return here.quarter(1 - i // 2, 1 - i % 2), 0, 0

    held = pl.BlockSpec(memory_space=pltpu.VMEM)
    step = lambda cols: pl.BlockSpec((quarter, slab, cols), lambda i: (i, 0, 0))
    rows_of = lambda n, t: jax.ShapeDtypeStruct((n, slab, model), t)
    small = [((quarter, slab, model), F32), ((quarter, slab, model), F32), ((quarter, slab, model), BF16),
             ((2, hidden), F32), ((2, 16, model), BF16), ((2, 16, hidden), BF16), ((2, 16, hidden), BF16),
             ((2, 16, model), BF16), ((quarter, 8, model), F32), ((2, 16 * batch, model), BF16),
             ((2, 16 * batch, weight.shape[2]), BF16), ((2, model), F32), ((2, model), F32), ((2, 128), F32)]
    block = (quarter, slab, model)
    return pl.pallas_call(
        functools.partial(middle_kernel, dims, total),
        grid=(4,),
        in_specs=[pl.BlockSpec((quarter, dims.patches, model), cot_at),
                  pl.BlockSpec((quarter, dims.caption, model), cot_at)] + [held] * 10,
        out_specs=[step(hidden), step(hidden), step(model)] + [held] * len(small),
        out_shape=[rows_of(4 * quarter, BF16)] * 3 + [jax.ShapeDtypeStruct(v, t) for v, t in small],
        scratch_shapes=[
            pltpu.VMEM((4,) + block, BF16), pltpu.VMEM((4,) + block, BF16),
            pltpu.VMEM((2,) + block, BF16), pltpu.VMEM((2,) + block, BF16),
            pltpu.VMEM(block, BF16), pltpu.VMEM(block, BF16), pltpu.VMEM(block, BF16),
            pltpu.VMEM((slab, model), F32),
            pltpu.VMEM((2, 16, model), F32), pltpu.VMEM((3, 2, 16, model), F32),
            pltpu.VMEM((batch, 2, 16, model), F32), pltpu.VMEM((2, 16 * batch, model), F32),
            pltpu.VMEM((2, 32, model), F32), pltpu.VMEM((2, 16, model), F32),
            pltpu.VMEM((2, 16, model), F32), pltpu.VMEM((3, 2, 16, model), F32),
            pltpu.SemaphoreType.DMA((18,)), pltpu.SemaphoreType.DMA((18,)),
        ],
        compiler_params=params(collective_id=2, has_side_effects=True),
        cost_estimate=pl.CostEstimate(
            flops=32 * quarter * slab * model * hidden, bytes_accessed=40_000_000, transcendentals=0),
        name="middle",
    )(img, txt, own, peer, cls_own, cls_peer, vec, up, up_bias, down, weight, scale)


def turn_kernel(dims, img, txt, peer, own, act, dup, ddn, ce, ca, cu, cd, dexp, attended, attn, d_own, d_near, dcls, vec,
                down_sum, up_keep, up_send, dattended, dattn, dattn_peer, fin_img, fin_txt, sums,
                acc, d_far, n_peer, rows, side_send, side_recv, e_in, dexp_in, attended_in, attn_in, d_own_in,
                local_sem, send_sem, recv_sem):
    here = Place()
    quarter, ip = dims.quarter, dims.ip
    i = pl.program_id(0)
    piece = side_send.shape[2]
    sent_near = remote(d_near, d_far, send_sem, recv_sem, 0, here.near)
    sent_core = [remote(dattn.at[p], n_peer.at[p], send_sem, recv_sem, 1 + p, here.core) for p in range(quarter)]
    sent_side = [remote(side_send.at[j], side_recv.at[j], send_sem, recv_sem, 1 + quarter + j, here.side)
                 for j in range(4)]
    loaded = [pltpu.make_async_copy(src, dst, local_sem.at[j]) for j, (src, dst) in enumerate((
        (dexp, dexp_in), (attended, attended_in), (attn, attn_in), (d_own, d_own_in)))]
    dexp, attended, attn, d_own = dexp_in, attended_in, attn_in, d_own_in
    spans = ((0, 0, ip), (1, ip, dims.slab))
    flat = lambda v: v.reshape(-1, v.shape[-1])
    block = lambda j: pl.ds(pl.multiple_of(j * piece, piece), piece)

    @pl.when(i == 0)
    def _():
        meet([here.core, here.near, here.side])
        sent_near.start()
        for copy in loaded:
            copy.start()
        for m in range(2):
            acc[m] = t_dot(cd[m], ca[m])

    @pl.when(i < 4)
    def _():
        for m, lo, hi in spans:
            acc[m] += t_dot(flat(ddn[:, lo:hi, :]), flat(act[:, lo:hi, :]))

    @pl.when(i == 3)
    def _():
        for j in range(4):
            for m in range(2):
                side_send[j, m] = acc[m, block(2 * j + 1 - here.x), :].astype(BF16)
                down_sum[j, m] = acc[m, block(2 * j + here.x), :].astype(BF16)
            sent_side[j].start()

    @pl.when(i == 4)
    def _():
        for m in range(2):
            acc[m] = t_dot(ce[m], cu[m])

    @pl.when((i >= 4) & (i % 2 == 0))
    def _():
        e_in[...] = peer[...]

    @pl.when((i >= 4) & (i % 2 == 1))
    def _():
        e_in[...] = own[...]

    @pl.when(i >= 4)
    def _():
        for m, lo, hi in spans:
            acc[m] += t_dot(flat(e_in[:, lo:hi, :]), flat(dup[:, lo:hi, :]))

    @pl.when(i == 7)
    def _():
        for j in range(4):
            for m in range(2):
                up_keep[j, m] = acc[m, block(2 * j + here.x), :].astype(BF16)
                up_send[j, m] = acc[m, block(2 * j + 1 - here.x), :].astype(BF16)
        for copy in loaded:
            copy.wait()
        rows[...] = jnp.zeros_like(rows)
        sums[...] = jnp.zeros_like(sums)

        def load(p):
            load_rows(dims, p, img, txt, rows)
            rows[0:1, :] += dcls[p, 0:1, :]
            rows[ip:ip + 1, :] += dcls[p, 1:2, :]

        for p in range(quarter):
            load(p)
            for m, lo, hi in ((0, 0, ip), (1, ip, dims.slab)):
                n, r = normalise(attended[p, lo:hi, :])
                dy = dexp[p, lo:hi, :]
                sums[m:m + 1, :] += jnp.sum(dy * n, axis=0, keepdims=True)
                sums[2 + m:3 + m, :] += jnp.sum(dy, axis=0, keepdims=True)
                d = rows[lo:hi, :] + norm_back(n, r, dy * vector(vec, GAIN2 + m))
                dattended[p, lo:hi, :] = d
                sd = d * vector(vec, A_SCALE)
                dattn[p, lo:hi, :] = sd.astype(BF16)
                a = attn[p, lo:hi, :] + vector(vec, A_BIAS)
                sums[4:5, :] += jnp.sum(d * a, axis=0, keepdims=True)
                sums[5:6, :] += jnp.sum(sd, axis=0, keepdims=True)
            sent_core[p].start()
        sent_near.wait_recv()

        def final(p, c):
            load(p)
            for m, lo, hi in ((0, 0, ip), (1, ip, dims.slab)):
                b = d_own[p, lo:hi, :] + d_far[p, lo:hi, :].astype(F32) + vector(vec, F_BIAS + m)
                f = attended[p, lo:hi, :] + vector(vec, F_SCALE) * b
                if m == 0:
                    fin_img[p] = f[0:dims.patches].astype(BF16)
                else:
                    fin_txt[p] = f[0:dims.caption].astype(BF16)
                g = rows[lo:hi, :]
                sums[6:7, :] += jnp.sum(g * b, axis=0, keepdims=True)
                sums[7 + m:8 + m, :] += jnp.sum(g, axis=0, keepdims=True) * vector(vec, F_SCALE)
            return c

        lax.fori_loop(0, quarter, final, 0)
        for p in range(quarter):
            sent_core[p].wait()
            dattn_peer[p] = n_peer[p]
        for j in range(4):
            sent_side[j].wait()
            down_sum[j] = (down_sum[j].astype(F32) + side_recv[j].astype(F32)).astype(BF16)
        sent_near.wait_send()


def turn(dims, img, txt, peer, own, act, dup, ddn, ce, ca, cu, cd, dexp, attended, attn, d_own, d_near, dcls, vec):
    model = own.shape[-1]
    hidden = act.shape[-1]
    slab, quarter = dims.slab, dims.quarter
    held = pl.BlockSpec(memory_space=pltpu.VMEM)

    def own_at(i):
        return Place().quarter(0, 0), 0, 0

    away = pl.BlockSpec(memory_space=pl.ANY)
    half = pl.BlockSpec((quarter, slab, model), lambda i: (jnp.where(i < 6, 1, 0), 0, 0))
    first = pl.BlockSpec((quarter, slab, hidden), lambda i: (jnp.minimum(i, 3), 0, 0))
    last = pl.BlockSpec((quarter, slab, hidden), lambda i: (jnp.maximum(i - 4, 0), 0, 0))
    block = (quarter, slab, model)
    part = (4, 2, model // 8, hidden)
    outs = [(part, BF16), (part, BF16), (part, BF16), (block, F32), (block, BF16), (block, BF16),
            ((quarter, dims.patches, model), BF16), ((quarter, dims.caption, model), BF16), ((16, model), F32)]
    return pl.pallas_call(
        functools.partial(turn_kernel, dims),
        grid=(8,),
        in_specs=[pl.BlockSpec((quarter, dims.patches, model), own_at),
                  pl.BlockSpec((quarter, dims.caption, model), own_at)] + [half] * 2 + [first, last, first]
        + [held] * 4 + [away] * 4 + [held] * 3,
        out_specs=[held] * len(outs),
        out_shape=[jax.ShapeDtypeStruct(v, t) for v, t in outs],
        scratch_shapes=[
            pltpu.VMEM((2, model, hidden), F32), pltpu.VMEM(block, BF16), pltpu.VMEM(block, BF16),
            pltpu.VMEM((slab, model), F32), pltpu.VMEM(part, BF16), pltpu.VMEM(part, BF16),
            pltpu.VMEM(block, BF16),
        ] + [pltpu.VMEM(block, F32)] * 4 + [
            pltpu.SemaphoreType.DMA((4,)),
            pltpu.SemaphoreType.DMA((5 + quarter,)), pltpu.SemaphoreType.DMA((5 + quarter,)),
        ],
        compiler_params=params(collective_id=3, has_side_effects=True),
        cost_estimate=pl.CostEstimate(
            flops=16 * quarter * slab * model * hidden, bytes_accessed=40_000_000, transcendentals=0),
        name="turn",
    )(img, txt, peer, own, act, dup, ddn, ce, ca, cu, cd, dexp, attended, attn, d_own, d_near, dcls, vec)


def back_kernel(dims, lens, d_own, d_peer, normed, qkv_far, mixed_far, qkv_own, mixed_own, wq, wo, wf,
                fin_img, fin_txt, up_keep, up_send, down_sum,
                keep, send, grad_pair, grad_single, cols_far, cols_own, near_img, near_txt, far_sum, up_half, down_out, up_out,
                dattn, dm_far, dm_own, dq_far, dq_own, acc_far, acc_own, w_far, w_own, o_far, o_own, dn, grad_f,
                up_mine, up_side, up_low, up_one, up_in, one_in, up_pass, up_last, down_mine, down_in, down_pass, down_last,
                from_side, local_sem, send_sem, recv_sem):
    here = Place()
    i = pl.program_id(0)
    slab, quarter, local = dims.slab, dims.quarter, dims.local
    two, one_head = parts_of(dims)
    count = quarter * slab
    model = normed.shape[-1]
    piece = from_side.shape[1]
    block = lambda j: pl.ds(pl.multiple_of(j * piece, piece), piece)
    used = [0]

    def make(src, dst, device):
        at = used[0]
        used[0] += 1
        return remote(src, dst, send_sem, recv_sem, at, device)

    sent_near = [make(fin_img, near_img, here.near), make(fin_txt, near_txt, here.near)]
    sent_up = [make(up_send.at[j, m], up_side.at[m, j], here.side) for m in range(2) for j in range(4)]
    in_pair = lambda src, dst: [make(src.at[here.z_pair], dst.at[0], here.paired), make(src.at[here.z_rest], dst.at[1], here.paired)]
    sent_down = in_pair(down_sum, down_in)
    pass_down = make(down_pass, down_last, here.opposite)
    sent_far = [make(grad_f.at[block(2 * j + 1 - here.x)], from_side.at[j], here.side) for j in range(4)]
    sent_low = in_pair(up_low, up_in)
    pass_low = make(up_pass, up_last, here.opposite)
    sent_one = in_pair(up_one, one_in)
    loaded = [pltpu.make_async_copy(up_keep, up_mine, local_sem.at[0]),
              pltpu.make_async_copy(down_sum.at[here.z], down_mine.at[0], local_sem.at[1]),
              pltpu.make_async_copy(down_sum.at[here.z_far], down_mine.at[1], local_sem.at[2])]
    add = lambda *parts: functools.reduce(lambda p, q: p + q, [v.astype(F32) for v in parts])

    @pl.when(i == 0)
    def _():
        meet([here.near, here.side, here.paired, here.opposite])
        for copy in loaded + sent_near + sent_up + sent_down:
            copy.start()
        for acc, cols in ((acc_far, cols_far), (acc_own, cols_own)):
            acc[...] = jnp.zeros_like(acc)
            cols[...] = jnp.zeros_like(cols)
        for t in range(4):
            own, start = (wq, t * local) if t < 3 else (wo, 0)
            dst, at = (w_far, t * 2 * two) if t < 3 else (o_far, 0)
            copy_rows(dst, at, wf, t * local, two)
            copy_rows(dst, at + two, own, start + two, one_head)
            copy_rows(dst, at + two + one_head, wf, t * local + two, one_head)
            dst, at = (w_own, t * two) if t < 3 else (o_own, 0)
            copy_rows(dst, at, own, start, two)

    @pl.when(i % 2 == 0)
    def _():
        dattn[...] = d_own[...]

    @pl.when(i % 2 == 1)
    def _():
        dattn[...] = d_peer[...]

    whose = here.quarter(0, i % 2)

    @pl.when(i < 2)
    def _():
        part = back_step(dims, 2, lens, whose, dattn, normed, qkv_far, mixed_far, dm_far, dq_far, acc_far, cols_far,
                         w_far, o_far)
        dn[i] = part.reshape(quarter, slab, model)

    @pl.when(i == 0)
    def _():
        for copy in loaded[1:]:
            copy.wait()
        for copy in sent_down:
            copy.wait_recv()
        down_pass[...] = add(down_mine[1], down_in[1]).astype(BF16)
        pass_down.start()

    @pl.when(i == 1)
    def _():
        for t in range(4):
            at = t * 2 * two
            to = 4 * two + t * one_head
            grad_f[:, t * two:(t + 1) * two] = acc_far[:, at:at + two].astype(BF16)
            grad_f[:, to:to + one_head] = acc_far[:, at + two + one_head:at + 2 * two].astype(BF16)
            grad_single[:, t * one_head:(t + 1) * one_head] = acc_far[:, at + two:at + two + one_head].astype(BF16)
        for copy in sent_far:
            copy.start()
        loaded[0].wait()
        for j in range(4):
            sent_up[j].wait_recv()
            up_low[j] = add(up_mine[j, 0], up_side[0, j]).astype(BF16)
        for copy in sent_low:
            copy.start()

    @pl.when(i >= 2)
    def _():
        part = back_step(dims, 1, lens, whose, dattn, normed, qkv_own, mixed_own, dm_own, dq_own, acc_own, cols_own,
                         w_own, o_own)
        total = (part.reshape(quarter, slab, model) + dn[i - 2]).astype(BF16)

        @pl.when(i == 2)
        def _():
            keep[...] = total
            for copy in sent_low:
                copy.wait_recv()
            up_pass[...] = add(up_low[here.z_far], up_in[1]).astype(BF16)
            pass_low.start()
            for j in range(4):
                sent_up[4 + j].wait_recv()
                up_one[j] = add(up_mine[j, 1], up_side[1, j]).astype(BF16)
            for copy in sent_one:
                copy.start()

        @pl.when(i == 3)
        def _():
            send[...] = total

    @pl.when(i == 3)
    def _():
        grad_pair[...] = acc_own[...].astype(BF16)
        down_out[...] = add(down_mine[0], down_in[0])
        for j in range(4):
            sent_far[j].wait_recv()
            far_sum[j] = add(grad_f[block(2 * j + here.x), :], from_side[j]).astype(BF16)
        pass_down.wait_recv()
        down_out[...] += down_last[...].astype(F32)
        for copy in sent_one:
            copy.wait_recv()
        up_half[0] = add(up_one[here.z], one_in[0]).astype(BF16)
        up_half[1] = add(up_one[here.z_far], one_in[1]).astype(BF16)
        pass_low.wait_recv()
        up_out[...] = add(up_low[here.z], up_in[0], up_last[...])
        for copy in sent_near:
            copy.wait_recv()
        for copy in sent_near + sent_up + sent_down + sent_far + sent_low + sent_one + [pass_down, pass_low]:
            copy.wait_send()


def back(dims, lens, d_own, d_peer, normed, qkv_far, mixed_far, qkv_own, mixed_own, wq, wo, wf,
         fin_img, fin_txt, up_keep, up_send, down_sum):
    model = normed.shape[-1]
    slab, quarter = dims.slab, dims.quarter
    hidden = up_keep.shape[-1]
    piece = model // 8
    held = pl.BlockSpec(memory_space=pltpu.VMEM)
    away = pl.BlockSpec(memory_space=pl.ANY)
    spec = lambda cols, at: pl.BlockSpec((quarter, slab, cols), lambda i: (at(i), 0, 0))
    early, late = lambda i: jnp.minimum(i, 1), lambda i: jnp.maximum(i - 2, 0)
    rows = (quarter, slab, model)
    outs = [(held, rows, BF16), (held, rows, BF16), (held, (model, 512), BF16), (held, (model, 256), BF16),
            (held, (1, 768), F32), (held, (1, 384), F32),
            (away, fin_img.shape, BF16), (away, fin_txt.shape, BF16),
            (held, (4, piece, model), BF16), (held, (2, piece, hidden), BF16),
            (held, (2, piece, hidden), F32), (held, (piece, hidden), F32)]
    slabs = lambda cols: pltpu.VMEM((quarter, slab, cols), BF16)
    return pl.pallas_call(
        functools.partial(back_kernel, dims),
        grid=(4,),
        in_specs=[pl.BlockSpec(memory_space=pltpu.SMEM), held, held, spec(model, lambda i: i % 2),
                  spec(768, early), spec(256, early), spec(384, late), spec(128, late), held, held, held]
        + [away] * 5,
        out_specs=[v[0] for v in outs],
        out_shape=[jax.ShapeDtypeStruct(v[1], v[2]) for v in outs],
        scratch_shapes=[
            slabs(model), slabs(256), slabs(128), slabs(768), slabs(384),
            pltpu.VMEM((model, 1024), F32), pltpu.VMEM((model, 512), F32),
            pltpu.VMEM((768, model), BF16), pltpu.VMEM((384, model), BF16),
            pltpu.VMEM((256, model), BF16), pltpu.VMEM((128, model), BF16),
            pltpu.VMEM((2,) + rows, F32), pltpu.VMEM((model, model), BF16),
            pltpu.VMEM((4, 2, piece, hidden), BF16), pltpu.VMEM((2, 4, piece, hidden), BF16),
            pltpu.VMEM((4, piece, hidden), BF16), pltpu.VMEM((4, piece, hidden), BF16),
            pltpu.VMEM((2, piece, hidden), BF16), pltpu.VMEM((2, piece, hidden), BF16),
            pltpu.VMEM((piece, hidden), BF16), pltpu.VMEM((piece, hidden), BF16),
            pltpu.VMEM((2, 2, piece, hidden), BF16), pltpu.VMEM((2, 2, piece, hidden), BF16),
            pltpu.VMEM((2, piece, hidden), BF16), pltpu.VMEM((2, piece, hidden), BF16),
            pltpu.VMEM((4, piece, model), BF16),
            pltpu.SemaphoreType.DMA((3,)), pltpu.SemaphoreType.DMA((22,)), pltpu.SemaphoreType.DMA((22,)),
        ],
        compiler_params=params(collective_id=4, has_side_effects=True),
        cost_estimate=pl.CostEstimate(
            flops=24 * quarter * slab * model * 1152, bytes_accessed=30_000_000, transcendentals=0),
        name="back",
    )(lens, d_own, d_peer, normed, qkv_far, mixed_far, qkv_own, mixed_own, wq, wo, wf,
      fin_img, fin_txt, up_keep, up_send, down_sum)


V_ROWS, V_MP, V_HEADS, V_FAR = 24, 11, 13, 15


def finish_kernel(dims, n_keep, n_send, dattended, states_img, states_txt, vec, fin_img, fin_txt,
                  near_img, near_txt, grad_pair, grad_single, grad_far, up_half, own_sums, up_sums, cols_own, cols_far,
                  out_img, out_txt, back_img, back_txt, grad_out, v_out, up_out,
                  n_recv, s_img, s_txt, d_img, d_txt, rows, xr, zs, z_in, z_pass, z_last, f_in, f_pass, f_last, up_last, far_sum, far_recv, vs, vr,
                  local_sem, send_sem, recv_sem):
    quarter = dims.quarter
    here = Place()
    z, x, m = here.z, here.x, here.m
    near_quarter = here.quarter(1, 0)
    used = [0]

    def send(src, dst, device):
        at = used[0]
        used[0] += 1
        return remote(src, dst, send_sem, recv_sem, at, device)

    loaded = [pltpu.make_async_copy(states_img.at[pl.ds(m * quarter, quarter)], s_img, local_sem.at[0]),
              pltpu.make_async_copy(states_txt.at[pl.ds(m * quarter, quarter)], s_txt, local_sem.at[1])]
    for copy in loaded:
        copy.start()
    meet([here.core, here.near, here.side, here.paired, here.opposite])

    n_copies = [send(n_send.at[p], n_recv.at[p], here.core) for p in range(quarter)]
    for copy in n_copies:
        copy.start()
    piece = xr.shape[1]
    wide = grad_pair.shape[1]
    spans = ((grad_pair, 0, wide), (grad_single, wide, xr.shape[2]))
    block = lambda j: pl.ds(pl.multiple_of(j * piece, piece), piece)
    x_copies = []
    for j in range(4):
        for src, lo, hi in spans:
            x_copies.append(send(src.at[block(2 * j + 1 - x)], xr.at[j, :, pl.ds(lo, hi - lo)], here.side))
            x_copies[-1].start()
    add = lambda *parts: functools.reduce(lambda p, q: p + q, [v.astype(F32) for v in parts])
    in_pair = lambda src, dst: [send(src.at[here.z_pair], dst.at[0], here.paired),
                                send(src.at[here.z_rest], dst.at[1], here.paired)]
    up_copy = send(up_half.at[1], up_last, here.opposite)
    far_copies = in_pair(grad_far, f_in)
    for copy in [up_copy] + far_copies:
        copy.start()

    fin_local, fin_remote = [], []
    for j, (src, dst, q) in enumerate((
        (fin_img, out_img, m), (fin_txt, out_txt, m), (near_img, out_img, near_quarter), (near_txt, out_txt, near_quarter),
    )):
        at = pl.ds(q * quarter, quarter)
        fin_local.append(pltpu.make_async_copy(src, dst.at[at], local_sem.at[2 + j]))
        fin_remote.append(send(src, dst.at[at], here.core))

    rows[...] = jnp.zeros_like(rows)
    for copy in loaded:
        copy.wait()
    total = [jnp.zeros((1, rows.shape[1]), F32)] * 2
    back_local, to_near, to_other = [], [], []
    for p in range(quarter):
        load_rows(dims, p, s_img, s_txt, rows)
        n, r = normalise(rows[...])
        n_copies[p].wait_recv()
        dy = n_keep[p].astype(F32) + n_recv[p].astype(F32)
        total[0] = total[0] + jnp.sum(dy * n, axis=0, keepdims=True)
        total[1] = total[1] + jnp.sum(dy, axis=0, keepdims=True)
        d = dattended[p] + norm_back(n, r, dy * vector(vec, GAIN1))
        d_img[p] = d[0:dims.patches].astype(BF16)
        d_txt[p] = d[dims.ip:dims.ip + dims.caption].astype(BF16)
        for j, (src, dst) in enumerate(((d_img, back_img), (d_txt, back_txt))):
            at = dst.at[m * quarter + p]
            to_near.append(send(src.at[p], at, here.near))
            to_near[-1].start()
            to_other.append(send(src.at[p], at, here.core))
            to_other[-1].start()
            back_local.append(pltpu.make_async_copy(src.at[p], at, local_sem.at[6 + 2 * p + j]))
            back_local[-1].start()
    for copy in fin_local + fin_remote:
        copy.start()

    at = lax.broadcasted_iota(jnp.int32, (V_ROWS, 1), 0)
    two, one_head = parts_of(dims)
    vs[0] = jnp.zeros(vs.shape[1:], F32)
    vs[0, 0:1, :] = total[0]
    vs[0, 1:2, :] = total[1]
    vs[0, 2:V_MP, :] = own_sums[0:V_MP - 2, :]
    vs[0, V_MP:V_HEADS, :] = up_sums[...]
    for j in range(2):
        own_at, far_at = 2 * j * two, 4 * j * two
        vs[0, V_HEADS + j:V_HEADS + j + 1, 0:two] = cols_own[0:1, own_at:own_at + two]
        vs[0, V_HEADS + j:V_HEADS + j + 1, two:two + one_head] = cols_far[0:1, far_at + two:far_at + two + one_head]
        vs[0, V_FAR + j:V_FAR + j + 1, 0:two] = cols_far[0:1, far_at:far_at + two]
        vs[0, V_FAR + j:V_FAR + j + 1, two:two + one_head] = cols_far[0:1, far_at + two + one_head:far_at + 2 * two]
    v = vs[0]
    v_copies = []

    def exchange(step, value, device):
        vs[step] = value
        copy = send(vs.at[step], vr.at[step], device)
        copy.start()
        copy.wait_recv()
        v_copies.append(copy)
        return vr[step]

    v = v + jnp.where(at < V_MP, exchange(0, v, here.core), 0.0)
    for copy in far_copies:
        copy.wait_recv()
    f_pass[...] = add(grad_far[here.z_far], f_in[1]).astype(BF16)
    far_copies.append(send(f_pass, f_last, here.opposite))
    far_copies[-1].start()
    v = v + exchange(1, v, here.side)
    v = v + exchange(2, v, here.paired)
    vs[3] = v
    v_far = send(vs.at[3], vr.at[3], here.opposite)
    v_far.start()

    def own_sum(j, k):
        src, lo, hi = spans[k]
        return src[block(2 * j + x), :].astype(F32) + xr[j, :, lo:hi].astype(F32)

    for copy in x_copies:
        copy.wait_recv()
    for j in range(4):
        for k, (src, lo, hi) in enumerate(spans):
            zs[j, :, lo:hi] = own_sum(j, k).astype(BF16)
    z_copies = in_pair(zs, z_in)
    for copy in z_copies:
        copy.start()

    far_copies[-1].wait_recv()
    far_sum[...] = add(grad_far[z], f_in[0], f_last[...]).astype(BF16)
    far_copy = send(far_sum, far_recv, here.near)
    far_copy.start()
    v_far.wait_recv()
    v = v + vr[3]
    up_copy.wait_recv()
    up_out[...] = add(up_half[0], up_last[...])
    for copy in z_copies:
        copy.wait_recv()
    z_pass[...] = add(zs[here.z_far], z_in[1]).astype(BF16)
    z_copies.append(send(z_pass, z_last, here.opposite))
    z_copies[-1].start()
    vs[4] = v
    v_near = send(vs.at[4], vr.at[4], here.near)
    v_near.start()
    for copy in fin_local + back_local:
        copy.wait()
    onward = []
    for p in range(quarter):
        for j, dst in enumerate((back_img, back_txt)):
            to_near[2 * p + j].wait_recv()
            at_near = dst.at[near_quarter * quarter + p]
            onward.append(send(at_near, at_near, here.core))
            onward[-1].start()
    far_copy.wait_recv()
    z_copies[-1].wait_recv()
    for k, (src, lo, hi) in enumerate(spans):
        grad_out[:, lo:hi] = own_sum(z, k) + add(
            far_recv[:, lo:hi], z_in[0, :, lo:hi], z_last[:, lo:hi])
    v_near.wait_recv()
    there = vr[4]
    v_out[...] = v + jnp.where(at < V_MP, there, 0.0)
    v_out[V_HEADS:V_HEADS + 2, :] = v[V_HEADS:V_HEADS + 2, :] + there[V_FAR:V_FAR + 2, :]
    for copy in to_other + fin_remote + onward:
        copy.wait()
    for copy in n_copies + x_copies + far_copies + to_near + z_copies + v_copies + [far_copy, v_near, v_far, up_copy]:
        copy.wait_send()


def finish(dims, n_keep, n_send, dattended, states_img, states_txt, vec, fin_img, fin_txt,
           near_img, near_txt, grad_pair, grad_single, grad_far, up_half, *tables):
    pairs, patches, model = states_img.shape
    caption = states_txt.shape[1]
    quarter, slab = dims.quarter, dims.slab
    piece, cols = grad_far.shape[1:]
    held = pl.BlockSpec(memory_space=pltpu.VMEM)
    away = pl.BlockSpec(memory_space=pl.ANY)
    n_remote = 7 * quarter + 28
    return pl.pallas_call(
        functools.partial(finish_kernel, dims),
        in_specs=[held] * 3 + [away] * 2 + [held] * 13,
        out_specs=[away] * 4 + [held] * 3,
        out_shape=[
            jax.ShapeDtypeStruct((pairs, patches, model), BF16),
            jax.ShapeDtypeStruct((pairs, caption, model), BF16),
            jax.ShapeDtypeStruct((pairs, patches, model), BF16),
            jax.ShapeDtypeStruct((pairs, caption, model), BF16),
            jax.ShapeDtypeStruct((piece, cols), F32),
            jax.ShapeDtypeStruct((V_ROWS, model), F32),
            jax.ShapeDtypeStruct(up_half.shape[1:], F32),
        ],
        scratch_shapes=[
            pltpu.VMEM((quarter, slab, model), BF16),
            pltpu.VMEM((quarter, patches, model), BF16),
            pltpu.VMEM((quarter, caption, model), BF16),
            pltpu.VMEM((quarter, patches, model), BF16),
            pltpu.VMEM((quarter, caption, model), BF16),
            pltpu.VMEM((slab, model), F32),
            pltpu.VMEM((4, piece, cols), BF16), pltpu.VMEM((4, piece, cols), BF16),
        ] + [pltpu.VMEM((2, piece, cols), BF16), pltpu.VMEM((piece, cols), BF16), pltpu.VMEM((piece, cols), BF16)] * 2 + [
            pltpu.VMEM(up_half.shape[1:], BF16),
            pltpu.VMEM((piece, cols), BF16), pltpu.VMEM((piece, cols), BF16),
            pltpu.VMEM((5, V_ROWS, model), F32),
            pltpu.VMEM((5, V_ROWS, model), F32),
            pltpu.SemaphoreType.DMA((6 + 2 * quarter,)),
            pltpu.SemaphoreType.DMA((n_remote,)),
            pltpu.SemaphoreType.DMA((n_remote,)),
        ],
        compiler_params=params(collective_id=1, has_side_effects=True),
        name="finish",
    )(n_keep, n_send, dattended, states_img, states_txt, vec, fin_img, fin_txt,
      near_img, near_txt, grad_pair, grad_single, grad_far, up_half, *tables)


def spread_kernel(cols, at, sums, grad, gains, shifts, *refs):
    *outs, qkv, out_w, turned = refs
    back = sums.shape[1] - at[0] * cols

    def slice_of(value):
        return pltpu.roll(value, back, 1)[:, 0:cols]

    mine = slice_of(sums[...])
    for out, (lo, count) in zip(outs[:8], ((0, 1), (1, 1), (7, 1), (6, 1), (2, 2), (4, 2), (9, 2), (8, 1))):
        out[...] = mine[lo:lo + count, :]
    wide = jnp.concatenate([gains[...], shifts[...], jnp.zeros((4, sums.shape[1]), F32)], axis=0)
    heads = slice_of(wide)
    outs[8][...] = heads[0:2, :]
    outs[9][...] = heads[2:4, :]
    outs[10][...] = sums[V_MP:V_MP + 2, :]
    outs[11][...] = sums[V_HEADS:V_HEADS + 2, 0:outs[11].shape[1]]
    two, one = 2 * HEAD_DIM, HEAD_DIM
    for t in range(3):
        qkv[t, :, 0:two] = grad[:, t * two:(t + 1) * two]
        qkv[t, :, two:two + one] = grad[:, 4 * two + t * one:4 * two + (t + 1) * one]
    turned[...] = jnp.zeros_like(turned)
    turned[0:cols, 0:two] = grad[:, 3 * two:4 * two]
    turned[0:cols, two:two + one] = grad[:, 4 * two + 3 * one:4 * two + 4 * one]
    out_w[...] = turned[...].T[0:two + one, 0:cols]


def spread(local, at, sums, grad, gains, shifts):
    cols, model = grad.shape[0], sums.shape[1]
    assert cols <= 128
    shapes = [(1, cols)] * 4 + [(2, cols)] * 3 + [(1, cols)] + [(2, cols)] * 2 + [(2, model), (2, local)]
    shapes += [(3, cols, local), (local, cols)]
    args = (sums, grad, gains, shifts)
    return pl.pallas_call(
        functools.partial(spread_kernel, cols),
        grid_spec=pltpu.PrefetchScalarGridSpec(
            num_scalar_prefetch=1, grid=(1,),
            in_specs=[spec_whole(v) for v in args],
            out_specs=[pl.BlockSpec(v, lambda i, o, n=len(v): (0,) * n) for v in shapes],
            scratch_shapes=[pltpu.VMEM((128, 256), F32)],
        ),
        out_shape=[jax.ShapeDtypeStruct(v, F32) for v in shapes],
        compiler_params=params(),
        cost_estimate=pl.CostEstimate(flops=1_000_000, bytes_accessed=1_000_000, transcendentals=0),
        name="spread",
    )(at, *args)


def per_device(
    image_states, text_states, caption_lengths, image_cotangent, text_cotangent,
    first_gain, first_shift, query_key_value, query_value_bias, output_weight, output_bias,
    attention_scale, expert_gain, expert_shift, expert_up, expert_up_bias, expert_down,
    expert_down_bias, feedforward_scale, head_gain, head_shift, head_weight, logit_scale,
):
    pairs, patches, model = image_states.shape
    caption = text_states.shape[1]
    local = query_key_value.shape[2]
    quarter = pairs // 4
    batch_size = lax.axis_size("batch")
    assert lax.axis_size("mp") == 4 and pairs == 4 * quarter and quarter <= 3
    assert batch_size & (batch_size - 1) == 0
    assert local == 3 * HEAD_DIM
    ip, tp = up16(patches), up16(caption)
    dims = Dims(patches, caption, ip, tp, ip + tp, quarter, local)
    me = lax.axis_index("mp")
    batch_at = lax.axis_index("batch")
    order = me ^ jnp.asarray(ORDER, jnp.int32)
    vectors = (first_gain, first_shift, attention_scale, output_bias, expert_gain, expert_shift,
               feedforward_scale, expert_down_bias, head_gain, head_shift)
    own_w = jnp.transpose(query_key_value, (1, 2, 0)).reshape(3 * local, model)
    one_kernel = batch_size == 8 and model // batch_size % 32 == 0 and expert_up.shape[2] == model
    if one_kernel:
        (vec, normed, qkv_own, mixed_own, qkv_far, mixed_far, wf, attended, attn, e_own, e_peer, cls_own, cls_peer) = front(
            dims, caption_lengths, image_states, text_states, vectors, query_value_bias, own_w, output_weight)
    else:
        vec = jnp.concatenate([v.reshape(-1, model) for v in vectors] + [jnp.zeros((1, model), F32)])
        wo = jnp.concatenate([own_w, output_weight])
        wf = to_y(wo)
        far_bias = to_y(query_value_bias)
        normed, qkv_own, rest, mixed_own = attend_own(
            dims, order, caption_lengths, image_states, text_states, vec, query_value_bias, wo)
        qkv_far, mixed_far, a_keep, a_send = attend_far(
            dims, order, caption_lengths, normed, rest, mixed_own, far_bias, wo, wf)
        a_recv = to_core(a_send)
        attended, attn, e_own, cls_own = residual(
            dims, order, a_keep, a_recv, image_states, text_states, vec)
        e_peer = to_core(e_own)
        cls_peer = to_core(cls_own)
    if one_kernel:
        (act, dup, ddn, dexp, d_own, d_near, up_sums, class_e, c_act, c_dup, c_ddn, dcls, head_in, dproj,
         grad_head_gain, grad_head_shift, scalars) = middle(
            dims, pairs * batch_size, image_cotangent, text_cotangent, e_own, e_peer, cls_own, cls_peer, vec,
            expert_up, expert_up_bias, expert_down, head_weight, logit_scale.reshape(1, 1))
        down_sum, up_keep, up_send, dattended, dattn, dattn_peer, fin_img, fin_txt, own_sums = turn(
            dims, image_cotangent, text_cotangent, e_peer, e_own, act, dup, ddn, class_e, c_act, c_dup, c_ddn,
            dexp, attended, attn, d_own, d_near, dcls, vec)
    else:
        class_part, class_e = class_forward(dims, cls_own, cls_peer, expert_up, expert_up_bias, expert_down)
        class_parts = from_others(class_part, "mp", 1, 4)

        act_a, dup_a, ddn_a, d_send3, d_keep1, x_send3, x_keep1, bias_a, cot_a = experts(
            dims, "experts_a", 1, order[jnp.asarray([3, 1])], e_peer, e_own, image_cotangent, text_cotangent,
            tie(vec, class_part), expert_up, expert_up_bias, expert_down)
        x_recv1 = to_core(x_send3)
        d_recv1 = to_core(d_send3)
        final_class = class_final(
            dims, order, cls_own, cls_peer, class_parts, tie(vec, bias_a))
        class_blocks = gather_batch(final_class[None])
        x_near = add_low(x_keep1, x_recv1)
        x_far = to_y(x_near)
        act_b, dup_b, ddn_b, d_send2, d_keep0, x_send2, x_keep0, bias_b, cot_b = experts(
            dims, "experts_b", 0, order[jnp.asarray([2, 0])], e_peer, e_own, image_cotangent, text_cotangent,
            tie(vec, final_class, x_near), expert_up, expert_up_bias, expert_down)
        x_recv0 = to_core(x_send2)
        d_recv0 = to_core(d_send2)

        head_in, dproj, dclass, grad_head_gain, grad_head_shift, scalars = (contrast if batch_size <= 8 else contrast_large)(
            dims, pairs * batch_size, batch_at.reshape(1), class_blocks, tie(vec, bias_b), head_weight,
             logit_scale.reshape(1, 1))
        c_act, c_dup, c_ddn, c_dexp, c_bias, dcls = class_back(
            dims, order, class_e, cot_a, cot_b, dclass, vec, expert_up, expert_up_bias, expert_down)
        extras = from_others(c_dexp, "mp", 1, 4)
        d_far = to_y(add_low(d_keep1, tie(d_recv1, c_dexp)))
        expert_grad = expert_grads(
            dims, e_peer, e_own, act_a, dup_a, ddn_a, act_b, dup_b, ddn_b, class_e, c_act, c_dup, c_ddn)
        expert_sum = lax.psum_scatter(expert_grad, "batch", scatter_dimension=1, tiled=True)

        dattended, dattn, sums_two = norm_two(
            dims, order, x_keep0, x_recv0, x_far, attended, a_keep, a_recv, image_cotangent, text_cotangent,
            dcls, extras, tie(vec, expert_grad))
        dattn_peer = to_core(dattn)
        fin_img, fin_txt, sums_fin = final_rows(
            dims, order, d_keep0, d_recv0, d_far, attended, image_cotangent, text_cotangent, dcls,
            tie(vec, sums_two))
        own_sums = jnp.concatenate([sums_two[:6], sums_fin[:3]])
        up_sums = bias_a + bias_b + c_bias
    contrast_loss = scalars[0, :1]
    grad_logit_scale = scalars[1, :1]
    if one_kernel:
        (n_keep, n_send, grad_o01, grad_o2, cols_far, cols_own, near_img, near_txt, far_sum, up_half, grad_down,
         up_low) = back(
            dims, caption_lengths, dattn, dattn_peer, normed, qkv_far, mixed_far, qkv_own, mixed_own,
            own_w, output_weight, wf, fin_img, fin_txt, up_keep, up_send, down_sum)
    else:
        n_keep, n_send, grad_far, grad_o2, cols_far = attend_back(
            dims, True, order, caption_lengths, dattn, dattn_peer, normed, qkv_far, mixed_far, own_w, output_weight, wf)
        n_keep, n_send, grad_o01, cols_own = attend_back(
            dims, False, order, caption_lengths, dattn, dattn_peer, normed, qkv_own, mixed_own, own_w, output_weight, wf,
            prior=(n_keep, n_send))
    cols = model // batch_size
    mine = lambda v, axis: lax.dynamic_slice_in_dim(v, batch_at * cols, cols, axis=axis)
    grad_head_weight = jnp.einsum("mnc,mne->mce", mine(head_in, 2), dproj, preferred_element_type=F32)
    pair, single = 2 * HEAD_DIM, HEAD_DIM
    if one_kernel:
        image_output, text_output, image_grad, text_grad, attn_grad, sums, up_high = finish(
            dims, n_keep, n_send, dattended, image_states, text_states, vec, fin_img, fin_txt,
            near_img, near_txt, grad_o01, grad_o2, far_sum, up_half, own_sums, up_sums, cols_own, cols_far)
        *vectors, grad_qkv, grad_output_weight = spread(
            local, batch_at.reshape(1), sums, attn_grad, grad_head_gain, grad_head_shift)
        flat = lambda v: v.reshape(-1)
        return (
            image_output,
            text_output,
            contrast_loss,
            image_grad,
            text_grad,
            flat(vectors[0]),
            flat(vectors[1]),
            jnp.transpose(grad_qkv, (1, 0, 2)),
            vectors[11],
            grad_output_weight,
            flat(vectors[2]),
            flat(vectors[3]),
            vectors[4],
            vectors[5],
            jnp.stack([up_low, up_high]),
            vectors[10],
            jnp.transpose(grad_down, (0, 2, 1)),
            vectors[6],
            flat(vectors[7]),
            vectors[8],
            vectors[9],
            grad_head_weight,
            grad_logit_scale,
        )
    else:
        grad_expert_up = expert_sum[:2].astype(F32)
        grad_expert_down = jnp.transpose(expert_sum[2:].astype(F32), (0, 2, 1))
        cols_own = cols_own.reshape(3, pair)[::2]
        cols_far = cols_far.reshape(3, 2 * pair)[::2]
        heads = jnp.concatenate([cols_own, cols_far[:, pair:pair + single]], axis=1)
        heads_far = jnp.concatenate([cols_far[:, :pair], cols_far[:, pair + single:]], axis=1)
        n_recv = to_core(n_send)
        d_img, d_txt, sums_one = norm_one(
            dims, order, n_keep, n_recv, dattended, image_states, text_states, vec)
        image_output = gather_rows(fin_img, me)
        text_output = gather_rows(fin_txt, me)
        image_grad = gather_rows(d_img, me)
        text_grad = gather_rows(d_txt, me)
        grad_own = jnp.concatenate([grad_o01, grad_o2], axis=1)
        grad_far = lax.psum_scatter(grad_far, "batch", scatter_dimension=0, tiled=True)
        grad_own = lax.psum_scatter(grad_own, "batch", scatter_dimension=0, tiled=True)
        attn_grad = grad_own.astype(F32) + to_y(grad_far).astype(F32)
        heads = heads + to_y(heads_far)
        own_sums = sum_over(jnp.concatenate([sums_one[:2], own_sums]), "mp")
        flat = jnp.concatenate([own_sums.reshape(-1), heads.reshape(-1), up_sums.reshape(-1)])
        count = flat.shape[0]
        flat = jnp.pad(flat, (0, -count % 1024)).reshape(-1, 128)
        flat = sum_over(flat, "batch").reshape(-1)[:count]
        done = own_sums.shape[0]
        own_sums = mine(flat[:done * model].reshape(done, model), 1)
        heads = flat[done * model:done * model + 2 * local].reshape(2, local)
        grad_expert_up_bias = flat[done * model + 2 * local:].reshape(up_sums.shape)
    attn_grad = jnp.concatenate(
        [attn_grad[:, :4 * pair].reshape(cols, 4, pair), attn_grad[:, 4 * pair:].reshape(cols, 4, single)], axis=2)
    grad_query_key_value = attn_grad[:, :3]
    grad_output_weight = jnp.transpose(attn_grad[:, 3])
    return (
        image_output,
        text_output,
        contrast_loss,
        image_grad,
        text_grad,
        own_sums[0],
        own_sums[1],
        grad_query_key_value,
        heads,
        grad_output_weight,
        own_sums[7],
        own_sums[6],
        own_sums[2:4],
        own_sums[4:6],
        grad_expert_up,
        grad_expert_up_bias,
        grad_expert_down,
        own_sums[9:11],
        own_sums[8],
        mine(grad_head_gain, 1),
        mine(grad_head_shift, 1),
        grad_head_weight,
        grad_logit_scale,
    )


def solution(mesh):
    return jax.shard_map(
        per_device,
        mesh=mesh,
        in_specs=(
            P("batch", None, None),
            P("batch", None, None),
            P("batch"),
            P("batch", None, None),
            P("batch", None, None),
            P(),
            P(),
            P(None, None, "mp"),
            P(None, "mp"),
            P("mp", None),
            P(),
            P(),
            P(),
            P(),
            P(None, None, "mp"),
            P(None, "mp"),
            P(None, "mp", None),
            P(),
            P(),
            P(),
            P(),
            P(),
            P(),
        ),
        out_specs=(
            P("batch", None, None),
            P("batch", None, None),
            P(),
            P("batch", None, None),
            P("batch", None, None),
            P("batch"),
            P("batch"),
            P("batch", None, "mp"),
            P(None, "mp"),
            P("mp", "batch"),
            P("batch"),
            P("batch"),
            P(None, "batch"),
            P(None, "batch"),
            P(None, "batch", "mp"),
            P(None, "mp"),
            P(None, "mp", "batch"),
            P(None, "batch"),
            P("batch"),
            P(None, "batch"),
            P(None, "batch"),
            P(None, "batch", None),
            P(),
        ),
        check_vma=False,
    )
```

```python
import functools
from typing import NamedTuple

import jax
import jax.numpy as jnp
from jax import lax
from jax.experimental import pallas as pl
from jax.experimental.pallas import tpu as pltpu
from jax.sharding import PartitionSpec as P

HEAD_DIM = 64
F32 = jnp.float32
BF16 = jnp.bfloat16
NEG = -1e9
EPS = 1e-5
ORDER = (0, 2, 1, 3)

VMEM_LIMIT = 60 * 1024 * 1024


def params(**kw):
    return pltpu.CompilerParams(vmem_limit_bytes=VMEM_LIMIT, **kw)


def up16(n):
    return -(-n // 16) * 16


def dot(a, b):
    return jnp.dot(a, b, preferred_element_type=F32)


def dot_t(a, b):
    return lax.dot_general(a, b, (((1,), (1,)), ((), ())), preferred_element_type=F32)


def t_dot(a, b):
    return lax.dot_general(a, b, (((0,), (0,)), ((), ())), preferred_element_type=F32)


def normalise(x):
    c = x - jnp.mean(x, axis=-1, keepdims=True)
    v = jnp.mean(c * c, axis=-1, keepdims=True)
    r = lax.rsqrt(v + EPS)
    return c * r, r


def norm_back(n, r, dn):
    a = jnp.mean(dn, axis=-1, keepdims=True)
    b = jnp.mean(dn * n, axis=-1, keepdims=True)
    return (dn - a - n * b) * r


def gelu_parts(u):
    big = 0.5 * (1.0 + lax.erf(u * 0.7071067811865476))
    small = 0.3989422804014327 * jnp.exp(-0.5 * u * u)
    return big, small


def gelu_low(u):
    return (u * (0.5 * (1.0 + lax.erf(u * 0.7071067811865476)))).astype(BF16)


def softmax_rows(scores):
    m = jnp.max(scores, axis=-1, keepdims=True)
    e = jnp.exp(scores - m)
    return e * (1.0 / jnp.sum(e, axis=-1, keepdims=True))


def tie(value, *after):
    return lax.optimization_barrier((value,) + after)[0]


def load_rows(dims, p, img, txt, rows):
    rows[0:dims.patches, :] = img[p].astype(F32)
    rows[dims.ip:dims.ip + dims.caption, :] = txt[p].astype(F32)


def spec_whole(a):
    return pl.BlockSpec(a.shape, lambda *_: (0,) * a.ndim)


class Dims(NamedTuple):
    patches: int
    caption: int
    ip: int
    tp: int
    slab: int
    quarter: int
    local: int


GAIN1, SHIFT1, A_SCALE, A_BIAS, GAIN2, SHIFT2, F_SCALE, F_BIAS, H_GAIN, H_SHIFT = 0, 1, 2, 3, 4, 6, 8, 9, 11, 13


def vector(table, at, count=1):
    return table[at:at + count, :]


def copy_rows(dst, at, src, start, count):
    dst[at:at + count, :] = src[start:start + count, :]


def parts_of(dims):
    return 2 * HEAD_DIM, HEAD_DIM


def key_tail(dims, length):
    at = dims.patches // 16 * 16
    return ((0, dims.ip, at, dims.patches), (dims.ip, dims.slab, 0, length))


def hide(scores, start, limit):
    if start >= scores.shape[0]:
        return scores
    tail = scores[start:]
    at = start + lax.broadcasted_iota(jnp.int32, (tail.shape[0], 1), 0)
    tail = jnp.where(at < limit, tail, NEG)
    return tail if start == 0 else jnp.concatenate([scores[:start], tail], axis=0)


def split_pair(value):
    low = lax.broadcasted_iota(jnp.int32, (1, 128), 1) < HEAD_DIM
    zero = jnp.zeros_like(value)
    return jnp.concatenate([jnp.where(low, value, zero), jnp.where(low, zero, value)], axis=0)


def join_pair(value):
    low = lax.broadcasted_iota(jnp.int32, (1, 128), 1) < HEAD_DIM
    half = value.shape[0] // 2
    return jnp.where(low, value[:half], value[half:])


def softmax_keys(scores):
    e = jnp.exp(scores - jnp.max(scores, axis=0, keepdims=True))
    return e * (1.0 / jnp.sum(e, axis=0, keepdims=True))


def pair_weights(q, k, start, limit):
    return softmax_keys(hide(dot_t(k, split_pair(q)), start, limit))


def scaled(q):
    return q * jnp.asarray(HEAD_DIM ** -0.5, BF16)


def attend_tiles(dims, lens, quarter_at, qkv, mixed):
    tiles = mixed.shape[-1] // 128

    def one_pair(p, c):
        length = lens[quarter_at * dims.quarter + p]
        for lo, hi, start, limit in key_tail(dims, length):
            for g in range(tiles):
                q, k, v = [qkv[p, lo:hi, (t * tiles + g) * 128:(t * tiles + g + 1) * 128] for t in range(3)]
                w = pair_weights(scaled(q), k, start, limit).astype(BF16)
                mixed[p, lo:hi, g * 128:(g + 1) * 128] = join_pair(t_dot(w, v)).astype(BF16)
        return c

    lax.fori_loop(0, dims.quarter, one_pair, 0)


def attend_own_kernel(dims, order, lens, img, txt, vec, bias, wo, normed, qkv, rest, mixed, rows, w, b):
    i = pl.program_id(0)
    local = dims.local
    two, one_head = parts_of(dims)

    @pl.when(i == 0)
    def _():
        rows[...] = jnp.zeros_like(rows)
        w[...] = jnp.zeros_like(w)
        b[...] = jnp.zeros_like(b)
        for t in range(3):
            copy_rows(w, t * 2 * two, wo, t * local, local)
        b[0:1, 0:local] = bias[0:1, :]
        b[0:1, 4 * two:4 * two + local] = bias[1:2, :]

    def one_norm(p, c):
        load_rows(dims, p, img, txt, rows)
        n, _ = normalise(rows[...])
        normed[p] = (n * vector(vec, GAIN1) + vector(vec, SHIFT1)).astype(BF16)
        return c

    lax.fori_loop(0, dims.quarter, one_norm, 0)
    model = normed.shape[-1]
    proj = (dot_t(normed[...].reshape(dims.quarter * dims.slab, model), w[...]) + b[0:1, :]).astype(BF16)
    proj = proj.reshape(dims.quarter, dims.slab, 6 * two)
    for t in range(3):
        qkv[:, :, t * two:(t + 1) * two] = proj[:, :, 2 * t * two:(2 * t + 1) * two]
        rest[:, :, t * two:(t + 1) * two] = proj[:, :, (2 * t + 1) * two:(2 * t + 2) * two]
    attend_tiles(dims, lens, order[i], qkv, mixed)


def attend_own(dims, order, lens, img, txt, vec, bias, wo):
    model = img.shape[-1]
    pairs = 4 * dims.quarter
    block = lambda cols: pl.BlockSpec((dims.quarter, dims.slab, cols), lambda i, o, n: (i, 0, 0))
    shape = lambda cols: jax.ShapeDtypeStruct((pairs, dims.slab, cols), BF16)
    return pl.pallas_call(
        functools.partial(attend_own_kernel, dims),
        grid_spec=pltpu.PrefetchScalarGridSpec(
            num_scalar_prefetch=2,
            grid=(4,),
            in_specs=[
                pl.BlockSpec((dims.quarter, dims.patches, model), lambda i, o, n: (o[i], 0, 0)),
                pl.BlockSpec((dims.quarter, dims.caption, model), lambda i, o, n: (o[i], 0, 0)),
                spec_whole(vec), spec_whole(bias), spec_whole(wo),
            ],
            out_specs=[block(model), block(384), block(384), block(128)],
            scratch_shapes=[pltpu.VMEM((dims.slab, model), F32), pltpu.VMEM((768, model), BF16),
                            pltpu.VMEM((8, 768), F32)],
        ),
        out_shape=[shape(model), shape(384), shape(384), shape(128)],
        compiler_params=params(),
        cost_estimate=pl.CostEstimate(
            flops=1536 * pairs * dims.slab * model, bytes_accessed=30_000_000, transcendentals=0),
        name="attend_own",
    )(order, lens, img, txt, vec, bias, wo)


def attend_far_kernel(dims, order, lens, normed, rest, own, bias, wo, wf, qkv, mixed, keep, send, w, ow, b):
    i = pl.program_id(0)
    local = dims.local
    two, one_head = parts_of(dims)
    count = dims.quarter * dims.slab
    model = normed.shape[-1]

    @pl.when(i == 0)
    def _():
        w[...] = jnp.zeros_like(w)
        b[...] = jnp.zeros_like(b)
        for t in range(3):
            copy_rows(w, t * 2 * two, wf, t * local, two)
            copy_rows(w, t * 2 * two + two + one_head, wf, t * local + two, one_head)
        for t, at in ((0, 0), (1, 4 * two)):
            b[0:1, at:at + two] = bias[t:t + 1, 0:two]
            b[0:1, at + two + one_head:at + 2 * two] = bias[t:t + 1, two:]
        copy_rows(ow, 0, wo, 3 * local, two)
        copy_rows(ow, two, wf, 3 * local, two)
        copy_rows(ow, 2 * two, wo, 3 * local + two, one_head)
        copy_rows(ow, 2 * two + one_head, wf, 3 * local + two, one_head)

    proj = (dot_t(normed[...].reshape(count, model), w[...]) + b[0:1, :]).astype(BF16)
    proj = proj.reshape(dims.quarter, dims.slab, 6 * two)
    for t in range(3):
        at = 2 * t * two
        qkv[:, :, at:at + two] = proj[:, :, at:at + two]
        qkv[:, :, at + two:at + 2 * two] = proj[:, :, at + two:at + 2 * two] + rest[:, :, t * two:(t + 1) * two]
    attend_tiles(dims, lens, order[(i + 2) % 4], qkv, mixed)
    part = dot(own[...].reshape(count, two), ow[0:two, :])
    part = part + dot(mixed[...].reshape(count, 2 * two), ow[two:, :])
    part = part.astype(BF16).reshape(dims.quarter, dims.slab, model)

    @pl.when(i < 2)
    def _():
        send[...] = part

    @pl.when(i >= 2)
    def _():
        keep[...] = part


def attend_far(dims, order, lens, normed, rest, own, bias, wo, wf):
    model = normed.shape[-1]
    pairs = 4 * dims.quarter
    at = lambda i: (i + 2) % 4
    block = lambda cols, f: pl.BlockSpec((dims.quarter, dims.slab, cols), lambda i, o, n: (f(i), 0, 0))
    shape = lambda count, cols: jax.ShapeDtypeStruct((count, dims.slab, cols), BF16)
    return pl.pallas_call(
        functools.partial(attend_far_kernel, dims),
        grid_spec=pltpu.PrefetchScalarGridSpec(
            num_scalar_prefetch=2,
            grid=(4,),
            in_specs=[
                block(model, at), block(384, at), block(128, at),
                spec_whole(bias), spec_whole(wo), spec_whole(wf),
            ],
            out_specs=[
                block(768, at), block(256, at),
                block(model, lambda i: jnp.maximum(i - 2, 0)), block(model, lambda i: jnp.minimum(i, 1)),
            ],
            scratch_shapes=[pltpu.VMEM((768, model), BF16), pltpu.VMEM((384, model), BF16),
                            pltpu.VMEM((8, 768), F32)],
        ),
        out_shape=[
            shape(pairs, 768), shape(pairs, 256),
            shape(2 * dims.quarter, model), shape(2 * dims.quarter, model),
        ],
        compiler_params=params(),
        cost_estimate=pl.CostEstimate(
            flops=2304 * pairs * dims.slab * model, bytes_accessed=30_000_000, transcendentals=0),
        name="attend_far",
    )(order, lens, normed, rest, own, bias, wo, wf)


def residual_kernel(dims, order, keep, recv, img, txt, vec, attended, attn, expert, cls, rows):
    i = pl.program_id(0)
    ip = dims.ip

    @pl.when(i == 0)
    def _():
        rows[...] = jnp.zeros_like(rows)
        cls[...] = jnp.zeros_like(cls)

    load_rows(dims, 0, img, txt, rows)
    a = keep[0].astype(F32) + recv[0].astype(F32)
    x = rows[...] + vector(vec, A_SCALE) * (a + vector(vec, A_BIAS))
    n, _ = normalise(x)
    e_img = n[0:ip] * vector(vec, GAIN2) + vector(vec, SHIFT2)
    e_txt = n[ip:] * vector(vec, GAIN2 + 1) + vector(vec, SHIFT2 + 1)
    expert[0, 0:ip, :] = e_img.astype(BF16)
    expert[0, ip:, :] = e_txt.astype(BF16)
    for j, v in enumerate((x[0:1], x[ip:ip + 1], e_img[0:1], e_txt[0:1])):
        cls[j, pl.ds(i, 1), :] = v

    @pl.when(i < dims.quarter)
    def _():
        attended[0] = x
        attn[0] = a


def residual(dims, order, keep, recv, img, txt, vec):
    model = img.shape[-1]
    quarter = dims.quarter
    block = pl.BlockSpec((1, dims.slab, model), lambda i, o: (i, 0, 0))
    pair = lambda i, o: (o[i // quarter] * quarter + i % quarter, 0, 0)
    return pl.pallas_call(
        functools.partial(residual_kernel, dims),
        grid_spec=pltpu.PrefetchScalarGridSpec(
            num_scalar_prefetch=1,
            grid=(2 * quarter,),
            in_specs=[
                block, block,
                pl.BlockSpec((1, dims.patches, model), pair),
                pl.BlockSpec((1, dims.caption, model), pair),
                spec_whole(vec),
            ],
            out_specs=[
                pl.BlockSpec((1, dims.slab, model), lambda i, o: (jnp.minimum(i, quarter - 1), 0, 0)),
                pl.BlockSpec((1, dims.slab, model), lambda i, o: (jnp.minimum(i, quarter - 1), 0, 0)),
                block,
                pl.BlockSpec((4, 8, model), lambda i, o: (0, 0, 0)),
            ],
            scratch_shapes=[pltpu.VMEM((dims.slab, model), F32)],
        ),
        out_shape=[
            jax.ShapeDtypeStruct((quarter, dims.slab, model), F32),
            jax.ShapeDtypeStruct((quarter, dims.slab, model), F32),
            jax.ShapeDtypeStruct((2 * quarter, dims.slab, model), BF16),
            jax.ShapeDtypeStruct((4, 8, model), F32),
        ],
        compiler_params=params(),
        cost_estimate=pl.CostEstimate(flops=40_000_000, bytes_accessed=20_000_000, transcendentals=0),
        name="residual",
    )(order, keep, recv, img, txt, vec)


def expert_kernel(dims, seq, peer, own, img, txt, vec, up, up_bias, down,
                  act, dup, ddown, d_send, d_keep, x_send, x_keep, bias_grad, cot, ins, rows):
    ip, slab, quarter = dims.ip, dims.slab, dims.quarter
    i = pl.program_id(0)
    model = own.shape[-1]

    @pl.when(i == 0)
    def _():
        rows[...] = jnp.zeros_like(rows)
        bias_grad[...] = jnp.zeros_like(bias_grad)
        cot[...] = jnp.zeros_like(cot)
        ins[...] = peer[...]

    @pl.when(i == 1)
    def _():
        ins[...] = own[...]

    at = lax.broadcasted_iota(jnp.int32, (slab, 1), 0)
    inner = (at != 0) & (at != ip)

    def one(p, c):
        load_rows(dims, p, img, txt, rows)
        cot[0, pl.ds(8 * i + p, 1), :] = rows[0:1, :]
        cot[1, pl.ds(8 * i + p, 1), :] = rows[ip:ip + 1, :]
        ddown[p] = jnp.where(inner, rows[...] * vector(vec, F_SCALE), 0.0).astype(BF16)
        return c

    lax.fori_loop(0, quarter, one, 0)
    for m, lo, hi in ((0, 0, ip), (1, ip, slab)):
        count = quarter * (hi - lo)
        e = ins[:, lo:hi, :].reshape(count, model)
        u = dot(e, up[m]) + up_bias[m:m + 1]
        big, small = gelu_parts(u)
        a = (u * big).astype(BF16)
        act[:, lo:hi, :] = a.reshape(quarter, hi - lo, -1)
        slope = big + u * small
        d = dot(a, down[m]).astype(BF16).reshape(quarter, hi - lo, model)
        g = ddown[:, lo:hi, :].reshape(count, model)
        du = dot_t(g, down[m]) * slope
        bias_grad[m:m + 1, :] += jnp.sum(du, axis=0, keepdims=True)
        low = du.astype(BF16)
        dup[:, lo:hi, :] = low.reshape(quarter, hi - lo, -1)
        x = dot_t(low, up[m]).astype(BF16).reshape(quarter, hi - lo, model)

        @pl.when(i == 0)
        def _():
            d_send[:, lo:hi, :] = d
            x_send[:, lo:hi, :] = x

        @pl.when(i == 1)
        def _():
            d_keep[:, lo:hi, :] = d
            x_keep[:, lo:hi, :] = x


def experts(dims, name, half, seq, peer, own, img, txt, vec, up, up_bias, down):
    model = own.shape[-1]
    hidden = up.shape[-1]
    slab, quarter = dims.slab, dims.quarter
    fixed = pl.BlockSpec((quarter, slab, model), lambda i, o: (half, 0, 0))
    first = pl.BlockSpec((quarter, slab, model), lambda i, o: (0, 0, 0))
    step = lambda cols: pl.BlockSpec((quarter, slab, cols), lambda i, o: (i, 0, 0))
    shape = lambda n, cols: jax.ShapeDtypeStruct((n * quarter, slab, cols), BF16)
    return pl.pallas_call(
        functools.partial(expert_kernel, dims),
        grid_spec=pltpu.PrefetchScalarGridSpec(
            num_scalar_prefetch=1,
            grid=(2,),
            in_specs=[
                fixed, fixed,
                pl.BlockSpec((quarter, dims.patches, model), lambda i, o: (o[i], 0, 0)),
                pl.BlockSpec((quarter, dims.caption, model), lambda i, o: (o[i], 0, 0)),
                spec_whole(vec), spec_whole(up), spec_whole(up_bias), spec_whole(down),
            ],
            out_specs=[
                step(hidden), step(hidden), step(model),
                first, first, first, first,
                pl.BlockSpec((2, hidden), lambda i, o: (0, 0)),
                pl.BlockSpec((2, 16, model), lambda i, o: (0, 0, 0)),
            ],
            scratch_shapes=[pltpu.VMEM((quarter, slab, model), BF16), pltpu.VMEM((slab, model), F32)],
        ),
        out_shape=[
            shape(2, hidden), shape(2, hidden), shape(2, model),
            shape(1, model), shape(1, model), shape(1, model), shape(1, model),
            jax.ShapeDtypeStruct((2, hidden), F32),
            jax.ShapeDtypeStruct((2, 16, model), F32),
        ],
        compiler_params=params(),
        cost_estimate=pl.CostEstimate(
            flops=16 * quarter * slab * model * hidden, bytes_accessed=20_000_000, transcendentals=0),
        name=name,
    )(seq, peer, own, img, txt, vec, up, up_bias, down)


def expert_grads_kernel(dims, peer, own, act_a, dup_a, ddn_a, act_b, dup_b, ddn_b, ce, ca, cu, cd, out, acc):
    i = pl.program_id(0)

    def add(e, dup, ddn, act):
        for m, lo, hi in ((0, 0, dims.ip), (1, dims.ip, dims.slab)):
            count = dims.quarter * (hi - lo)
            flat = lambda ref: ref[:, lo:hi, :].reshape(count, -1)
            acc[m] += t_dot(flat(e), flat(dup))
            acc[2 + m] += t_dot(flat(ddn), flat(act))

    @pl.when(i == 0)
    def _():
        for m in range(2):
            acc[m] = t_dot(ce[m], cu[m])
            acc[2 + m] = t_dot(cd[m], ca[m])

    for j, refs in enumerate((
        (peer, dup_a, ddn_a, act_a), (own, dup_a, ddn_a, act_a),
        (peer, dup_b, ddn_b, act_b), (own, dup_b, ddn_b, act_b),
    )):
        @pl.when(i == j)
        def _():
            add(*refs)

    @pl.when(i == 3)
    def _():
        out[...] = acc[...].astype(BF16)


def expert_grads(dims, peer, own, act_a, dup_a, ddn_a, act_b, dup_b, ddn_b, ce, ca, cu, cd):
    model = own.shape[-1]
    hidden = act_a.shape[-1]
    slab, quarter = dims.slab, dims.quarter
    assert hidden == model
    half = pl.BlockSpec((quarter, slab, model), lambda i: (jnp.where(i < 2, 1, 0), 0, 0))
    first = pl.BlockSpec((quarter, slab, hidden), lambda i: (jnp.minimum(i, 1), 0, 0))
    last = pl.BlockSpec((quarter, slab, hidden), lambda i: (jnp.maximum(i - 2, 0), 0, 0))
    return pl.pallas_call(
        functools.partial(expert_grads_kernel, dims),
        grid=(4,),
        in_specs=[half, half, first, first, first, last, last, last] + [spec_whole(v) for v in (ce, ca, cu, cd)],
        out_specs=pl.BlockSpec((4, model, hidden), lambda i: (0, 0, 0)),
        scratch_shapes=[pltpu.VMEM((4, model, hidden), F32)],
        out_shape=jax.ShapeDtypeStruct((4, model, hidden), BF16),
        compiler_params=params(),
        cost_estimate=pl.CostEstimate(
            flops=16 * quarter * slab * model * hidden, bytes_accessed=40_000_000, transcendentals=0),
        name="expert_grads",
    )(peer, own, act_a, dup_a, ddn_a, act_b, dup_b, ddn_b, ce, ca, cu, cd)


def own_row(dims, r, p):
    return 8 * (r // 2) + dims.quarter * (r % 2) + p


def class_forward_kernel(dims, near, far, up, up_bias, down, out, rows):
    for m in range(2):
        e = jnp.concatenate([near[2 + m], far[2 + m]], axis=0).astype(BF16)
        rows[m] = e
        u = dot(e, up[m]) + up_bias[m:m + 1]
        out[m] = dot(gelu_low(u), down[m])


def class_forward(dims, near, far, up, up_bias, down):
    shape = (2, 16, near.shape[-1])
    return pl.pallas_call(
        functools.partial(class_forward_kernel, dims),
        out_shape=[jax.ShapeDtypeStruct(shape, F32), jax.ShapeDtypeStruct(shape, BF16)],
        compiler_params=params(),
        cost_estimate=pl.CostEstimate(flops=200_000_000, bytes_accessed=5_000_000, transcendentals=0),
        name="class_forward",
    )(near, far, up, up_bias, down)


def class_final_kernel(dims, order, near, far, d0, d1, d2, d3, vec, out):
    q = dims.quarter
    for m in range(2):
        out[m] = jnp.zeros(out.shape[1:], F32)
        for r in range(4):
            half, at = (near, far)[r // 2], q * (r % 2)
            for p in range(q):
                rows = [d[m, own_row(dims, s, p):own_row(dims, s, p) + 1, :]
                        for d, s in ((d0, r), (d1, r ^ 2), (d2, r ^ 1), (d3, r ^ 3))]
                total = (rows[0] + rows[1]) + (rows[2] + rows[3])
                x = half[m, at + p:at + p + 1, :] + vector(vec, F_SCALE) * (total + vector(vec, F_BIAS + m))
                out[m, pl.ds(4 * order[r] + p, 1), :] = x


def class_final(dims, order, near, far, parts, vec):
    shape = (2, 16, near.shape[-1])
    args = (near, far) + tuple(parts) + (vec,)
    return pl.pallas_call(
        functools.partial(class_final_kernel, dims),
        grid_spec=pltpu.PrefetchScalarGridSpec(
            num_scalar_prefetch=1, grid=(1,),
            in_specs=[spec_whole(v) for v in args],
            out_specs=pl.BlockSpec(shape, lambda i, o: (0, 0, 0)),
        ),
        out_shape=jax.ShapeDtypeStruct(shape, F32),
        compiler_params=params(),
        cost_estimate=pl.CostEstimate(flops=1_000_000, bytes_accessed=1_000_000, transcendentals=0),
        name="class_final",
    )(order, *args)


def class_back_kernel(dims, order, e, cot_a, cot_b, dclass, vec, up, up_bias, down,
                      act, dup, ddown, dexp, bias_grad, dcls, rows):
    q = dims.quarter
    rows[...] = jnp.zeros_like(rows)
    dcls[...] = jnp.zeros_like(dcls)
    for m in range(2):
        for r in range(4):
            cot, base = (cot_b, cot_a)[r % 2], 8 * (1 - r // 2)
            for p in range(q):
                d = dclass[m, pl.ds(4 * order[r] + p, 1), :]
                at = own_row(dims, r, p)
                rows[m, at:at + 1, :] = cot[m, base + p:base + p + 1, :] + d
                if r == 0:
                    dcls[p, m:m + 1, :] = d
        u = dot(e[m], up[m]) + up_bias[m:m + 1]
        big, small = gelu_parts(u)
        act[m] = (u * big).astype(BF16)
        g = (rows[m] * vector(vec, F_SCALE)).astype(BF16)
        ddown[m] = g
        du = dot_t(g, down[m]) * (big + u * small)
        bias_grad[m:m + 1, :] = jnp.sum(du, axis=0, keepdims=True)
        low = du.astype(BF16)
        dup[m] = low
        dexp[m] = dot_t(low, up[m])


def class_back(dims, order, e, cot_a, cot_b, dclass, vec, up, up_bias, down):
    hidden, model = up.shape[-1], e.shape[-1]
    args = (e, cot_a, cot_b, dclass, vec, up, up_bias, down)
    shapes = [((2, 16, hidden), BF16), ((2, 16, hidden), BF16), ((2, 16, model), BF16), ((2, 16, model), F32),
              ((2, hidden), F32), ((dims.quarter, 8, model), F32)]
    return pl.pallas_call(
        functools.partial(class_back_kernel, dims),
        grid_spec=pltpu.PrefetchScalarGridSpec(
            num_scalar_prefetch=1, grid=(1,),
            in_specs=[spec_whole(v) for v in args],
            out_specs=[pl.BlockSpec(s, lambda i, o, n=len(s): (0,) * n) for s, _ in shapes],
            scratch_shapes=[pltpu.VMEM((2, 16, model), F32)],
        ),
        out_shape=[jax.ShapeDtypeStruct(s, t) for s, t in shapes],
        compiler_params=params(),
        cost_estimate=pl.CostEstimate(flops=300_000_000, bytes_accessed=5_000_000, transcendentals=0),
        name="class_back",
    )(order, *args)


def contrast_kernel(dims, total, at, blocks, vec, weight, scale,
                    head_in, dproj, dcls, gains, shifts, scalars, cls, back):
    me = at[0]
    span = blocks[0].shape[0]
    for k, block in enumerate(blocks):
        for j in range(span):
            for m in range(2):
                cls[m, pl.ds(pl.multiple_of(16 * (me ^ (k * span + j)), 16), 16), :] = block[j, m]
    n_rows = cls.shape[1]
    sharp = jnp.exp(scale[...])
    col_at = lax.broadcasted_iota(jnp.int32, (1, n_rows), 1)
    row_at = lax.broadcasted_iota(jnp.int32, (n_rows, 1), 0)
    col_ok = (col_at % 4) < dims.quarter
    row_ok = (row_at % 4) < dims.quarter
    normal, inverse, proj, unit, embed = [], [], [], [], []
    for m in range(2):
        n, r = normalise(cls[m])
        h = (n * vector(vec, H_GAIN + m) + vector(vec, H_SHIFT + m)).astype(BF16)
        head_in[m] = h
        y = dot(h, weight[m])
        u = lax.rsqrt(jnp.sum(y * y, axis=-1, keepdims=True) + 1e-6)
        normal.append(n)
        inverse.append(r)
        proj.append(y)
        unit.append(u)
        embed.append((y * u).astype(BF16))
    ok = row_ok & col_ok
    logits = sharp * dot_t(embed[0], embed[1])
    masked = jnp.where(ok, logits, -1e30)
    row_max = jnp.max(masked, axis=1, keepdims=True)
    row_lse = row_max + jnp.log(jnp.sum(jnp.exp(masked - row_max), axis=1, keepdims=True))
    col_max = jnp.max(masked, axis=0, keepdims=True)
    col_lse = col_max + jnp.log(jnp.sum(jnp.exp(masked - col_max), axis=0, keepdims=True))
    same = (row_at == col_at) & ok
    both = jnp.exp(masked - row_lse) + jnp.exp(masked - col_lse)
    dlogits = jnp.where(ok, jnp.where(same, both - 2.0, both) * (1.0 / (2 * total)), 0.0)
    diagonal = jnp.sum(jnp.where(same, logits, 0.0), axis=1, keepdims=True)
    rows = jnp.where(row_ok, row_lse - 2.0 * diagonal, 0.0)
    cols = jnp.where(col_ok, col_lse, 0.0)
    loss = (jnp.sum(rows, axis=0, keepdims=True) + jnp.sum(cols, axis=1, keepdims=True)) * (1.0 / (2 * total))
    slope = jnp.sum(jnp.sum(dlogits * logits, axis=1, keepdims=True), axis=0, keepdims=True)
    scalars[0:1, :] = jnp.broadcast_to(loss, (1, 128))
    scalars[1:2, :] = jnp.broadcast_to(slope, (1, 128))
    high = lax.Precision.HIGHEST
    wide = [e.astype(F32) for e in embed]
    dembed = [
        sharp * jnp.dot(dlogits, wide[1], precision=high, preferred_element_type=F32),
        sharp * lax.dot_general(dlogits, wide[0], (((0,), (0,)), ((), ())), precision=high,
                                preferred_element_type=F32),
    ]
    for m in range(2):
        u, y, d = unit[m], proj[m], dembed[m]
        dp = (u * d - u * u * u * y * jnp.sum(y * d, axis=-1, keepdims=True)).astype(BF16)
        dproj[m] = dp
        dh = dot_t(dp, weight[m])
        gains[m:m + 1, :] = jnp.sum(dh * normal[m], axis=0, keepdims=True)
        shifts[m:m + 1, :] = jnp.sum(dh, axis=0, keepdims=True)
        back[m] = norm_back(normal[m], inverse[m], dh * vector(vec, H_GAIN + m))
        dcls[m] = back[m, pl.ds(pl.multiple_of(16 * me, 16), 16), :]


def contrast(dims, total, at, blocks, vec, weight, scale):
    model = weight.shape[1]
    rows = 16 * len(blocks) * blocks[0].shape[0]
    args = tuple(blocks) + (vec, weight, scale)
    shapes = [((2, rows, model), BF16), ((2, rows, weight.shape[2]), BF16), ((2, 16, model), F32),
              ((2, model), F32), ((2, model), F32), ((2, 128), F32)]

    def kernel(at, *refs):
        contrast_kernel(dims, total, at, refs[:len(blocks)], *refs[len(blocks):])

    return pl.pallas_call(
        kernel,
        grid_spec=pltpu.PrefetchScalarGridSpec(
            num_scalar_prefetch=1, grid=(1,),
            in_specs=[spec_whole(v) for v in args],
            out_specs=[pl.BlockSpec(s, lambda i, o, n=len(s): (0,) * n) for s, _ in shapes],
            scratch_shapes=[pltpu.VMEM((2, rows, model), F32)] * 2,
        ),
        out_shape=[jax.ShapeDtypeStruct(s, t) for s, t in shapes],
        compiler_params=params(),
        cost_estimate=pl.CostEstimate(flops=1_000_000_000, bytes_accessed=5_000_000, transcendentals=0),
        name="contrast",
    )(at, *args)


def contrast_large(dims, total, at, blocks, vec, weight, scale):
    model = weight.shape[1]
    held = jnp.concatenate(blocks)
    held = held[jnp.arange(held.shape[0]) ^ at[0]]
    rows = jnp.asarray([r for r in range(16) if r % 4 < dims.quarter])
    cls = jnp.transpose(held[:, :, rows], (1, 0, 2, 3)).reshape(2, -1, model)
    gain, shift = vec[H_GAIN:H_GAIN + 2, None], vec[H_SHIFT:H_SHIFT + 2, None]
    n, r = normalise(cls)
    head_in = (n * gain + shift).astype(BF16)
    proj = jnp.einsum("mrc,mce->mre", head_in, weight, preferred_element_type=F32)
    unit = lax.rsqrt(jnp.sum(proj * proj, axis=-1, keepdims=True) + 1e-6)
    embed = (proj * unit).astype(BF16)
    sharp = jnp.exp(scale[0, 0])
    logits = sharp * dot_t(embed[0], embed[1])
    row_lse = jax.nn.logsumexp(logits, axis=1, keepdims=True)
    col_lse = jax.nn.logsumexp(logits, axis=0, keepdims=True)
    dlogits = jnp.exp(logits - row_lse) + jnp.exp(logits - col_lse) - 2.0 * jnp.eye(total, dtype=F32)
    dlogits = dlogits / (2 * total)
    loss = (jnp.sum(row_lse) + jnp.sum(col_lse) - 2.0 * jnp.trace(logits)) / (2 * total)
    slope = jnp.sum(dlogits * logits)
    high = lax.Precision.HIGHEST
    wide = embed.astype(F32)
    dembed = sharp * jnp.stack([
        jnp.dot(dlogits, wide[1], precision=high, preferred_element_type=F32),
        jnp.dot(dlogits.T, wide[0], precision=high, preferred_element_type=F32)])
    dproj = (unit * dembed - unit ** 3 * proj * jnp.sum(proj * dembed, axis=-1, keepdims=True)).astype(BF16)
    dh = jnp.einsum("mre,mce->mrc", dproj, weight, preferred_element_type=F32)
    back = norm_back(n, r, dh * gain)
    pairs = 4 * dims.quarter
    own = lax.dynamic_slice_in_dim(back, at[0] * pairs, pairs, axis=1)
    dcls = jnp.zeros((2, 16, model), F32).at[:, rows].set(own)
    scalars = jnp.broadcast_to(jnp.stack([loss, slope])[:, None], (2, 128))
    return head_in, dproj, dcls, jnp.sum(dh * n, axis=1), jnp.sum(dh, axis=1), scalars


def own_pair(rows_of):
    return lambda i, o: (o[0] * rows_of + i, 0, 0)


def own_call(kernel, dims, name, order, blocks, img, txt, others, outs, scratch):
    model = img.shape[-1]
    block = pl.BlockSpec((1, dims.slab, model), lambda i, o: (i, 0, 0))
    specs = {
        "slab": (block, (dims.quarter, dims.slab, model)),
        "img": (pl.BlockSpec((1, dims.patches, model), lambda i, o: (i, 0, 0)), (dims.quarter, dims.patches, model)),
        "txt": (pl.BlockSpec((1, dims.caption, model), lambda i, o: (i, 0, 0)), (dims.quarter, dims.caption, model)),
        "sums": (pl.BlockSpec((8, model), lambda i, o: (0, 0)), (8, model)),
    }
    return pl.pallas_call(
        functools.partial(kernel, dims),
        grid_spec=pltpu.PrefetchScalarGridSpec(
            num_scalar_prefetch=1,
            grid=(dims.quarter,),
            in_specs=[block] * len(blocks) + [
                pl.BlockSpec((1, dims.patches, model), own_pair(dims.quarter)),
                pl.BlockSpec((1, dims.caption, model), own_pair(dims.quarter)),
            ] + [spec_whole(v) for v in others],
            out_specs=[specs[kind][0] for kind, _ in outs],
            scratch_shapes=[pltpu.VMEM((dims.slab, model), F32)] * scratch,
        ),
        out_shape=[jax.ShapeDtypeStruct(specs[kind][1], dtype) for kind, dtype in outs],
        compiler_params=params(),
        cost_estimate=pl.CostEstimate(flops=40_000_000, bytes_accessed=15_000_000, transcendentals=0),
        name=name,
    )(order, *blocks, img, txt, *others)


def start_own(rows, sums):
    @pl.when(pl.program_id(0) == 0)
    def _():
        rows[...] = jnp.zeros_like(rows)
        sums[...] = jnp.zeros_like(sums)


def add_class(dims, dcls, rows):
    i = pl.program_id(0)
    rows[0:1, :] += dcls[i, 0:1, :]
    rows[dims.ip:dims.ip + 1, :] += dcls[i, 1:2, :]


def final_kernel(dims, order, keep, recv, far, attended, img, txt, dcls, vec, fin_img, fin_txt, sums, rows):
    start_own(rows, sums)
    load_rows(dims, 0, img, txt, rows)
    add_class(dims, dcls, rows)
    for m, lo, hi in ((0, 0, dims.ip), (1, dims.ip, dims.slab)):
        b = keep[0, lo:hi].astype(F32) + recv[0, lo:hi].astype(F32) + far[0, lo:hi].astype(F32)
        b = b + vector(vec, F_BIAS + m)
        f = attended[0, lo:hi, :] + vector(vec, F_SCALE) * b
        if m == 0:
            fin_img[0] = f[0:dims.patches].astype(BF16)
        else:
            fin_txt[0] = f[0:dims.caption].astype(BF16)
        g = rows[lo:hi, :]
        sums[0:1, :] += jnp.sum(g * b, axis=0, keepdims=True)
        sums[1 + m:2 + m, :] += jnp.sum(g, axis=0, keepdims=True) * vector(vec, F_SCALE)


def final_rows(dims, order, keep, recv, far, attended, img, txt, dcls, vec):
    return own_call(final_kernel, dims, "final_rows", order, (keep, recv, far, attended), img, txt,
                    (dcls, vec), (("img", BF16), ("txt", BF16), ("sums", F32)), 1)


def norm_two_kernel(dims, order, keep, recv, far, attended, a_keep, a_recv, img, txt, dcls, x0, x1, x2, x3,
                    vec, dattended, dattn, sums, rows, ups):
    i = pl.program_id(0)
    start_own(rows, sums)
    load_rows(dims, 0, img, txt, rows)
    add_class(dims, dcls, rows)
    ups[...] = keep[0].astype(F32) + recv[0].astype(F32) + far[0].astype(F32)
    for m, at in ((0, 0), (1, dims.ip)):
        extra = [x[m, pl.ds(own_row(dims, r, 0) + i, 1), :] for x, r in ((x0, 0), (x1, 2), (x2, 1), (x3, 3))]
        ups[at:at + 1, :] += (extra[0] + extra[1]) + (extra[2] + extra[3])
    for m, lo, hi in ((0, 0, dims.ip), (1, dims.ip, dims.slab)):
        n, r = normalise(attended[0, lo:hi, :])
        dy = ups[lo:hi, :]
        sums[m:m + 1, :] += jnp.sum(dy * n, axis=0, keepdims=True)
        sums[2 + m:3 + m, :] += jnp.sum(dy, axis=0, keepdims=True)
        d = rows[lo:hi, :] + norm_back(n, r, dy * vector(vec, GAIN2 + m))
        dattended[0, lo:hi, :] = d
        sd = d * vector(vec, A_SCALE)
        dattn[0, lo:hi, :] = sd.astype(BF16)
        a = a_keep[0, lo:hi, :].astype(F32) + a_recv[0, lo:hi, :].astype(F32) + vector(vec, A_BIAS)
        sums[4:5, :] += jnp.sum(d * a, axis=0, keepdims=True)
        sums[5:6, :] += jnp.sum(sd, axis=0, keepdims=True)


def norm_two(dims, order, keep, recv, far, attended, a_keep, a_recv, img, txt, dcls, parts, vec):
    return own_call(norm_two_kernel, dims, "norm_two", order, (keep, recv, far, attended, a_keep, a_recv), img, txt,
                    (dcls,) + tuple(parts) + (vec,), (("slab", F32), ("slab", BF16), ("sums", F32)), 2)


def norm_one_kernel(dims, order, keep, recv, dattended, img, txt, vec, d_img, d_txt, sums, rows):
    start_own(rows, sums)
    load_rows(dims, 0, img, txt, rows)
    n, r = normalise(rows[...])
    dy = keep[0].astype(F32) + recv[0].astype(F32)
    sums[0:1, :] += jnp.sum(dy * n, axis=0, keepdims=True)
    sums[1:2, :] += jnp.sum(dy, axis=0, keepdims=True)
    d = dattended[0] + norm_back(n, r, dy * vector(vec, GAIN1))
    d_img[0] = d[0:dims.patches].astype(BF16)
    d_txt[0] = d[dims.ip:dims.ip + dims.caption].astype(BF16)


def norm_one(dims, order, keep, recv, dattended, img, txt, vec):
    return own_call(norm_one_kernel, dims, "norm_one", order, (keep, recv, dattended), img, txt,
                    (vec,), (("img", BF16), ("txt", BF16), ("sums", F32)), 1)


def back_step(dims, tiles, lens, whose, dattn, normed, qkv, mixed, dmixed, dqkv, acc, col_sums, w, ow):
    quarter, slab = dims.quarter, dims.slab
    count, width = quarter * slab, tiles * 128
    model = normed.shape[-1]
    d_rows = dattn[...].reshape(count, model)
    dmixed[...] = dot_t(d_rows, ow[...]).astype(BF16).reshape(quarter, slab, width)

    def one_pair(p, c):
        length = lens[whose * quarter + p]
        for lo, hi, start, limit in key_tail(dims, length):
            for g in range(tiles):
                at = [slice((t * tiles + g) * 128, (t * tiles + g + 1) * 128) for t in range(3)]
                q, k, v = [qkv[p, lo:hi, c] for c in at]
                q = scaled(q)
                qq = split_pair(q)
                dd = split_pair(dmixed[p, lo:hi, g * 128:(g + 1) * 128])
                w_ = softmax_keys(hide(dot_t(k, qq), start, limit))
                dw = dot_t(v, dd)
                dqkv[p, lo:hi, at[2]] = dot(w_.astype(BF16), dd).astype(BF16)
                ds = (w_ * (dw - jnp.sum(w_ * dw, axis=0, keepdims=True))).astype(BF16)
                dqkv[p, lo:hi, at[1]] = dot(ds, qq).astype(BF16)
                dqkv[p, lo:hi, at[0]] = (join_pair(t_dot(ds, k)) * HEAD_DIM ** -0.5).astype(BF16)
        return c

    lax.fori_loop(0, quarter, one_pair, 0)
    dp = dqkv[...].reshape(count, 3 * width)
    part = dot(dp, w[...])
    acc[:, 0:3 * width] += t_dot(normed[...].reshape(count, model), dp)
    acc[:, 3 * width:] += t_dot(d_rows, mixed[...].reshape(count, width))
    col_sums[...] += jnp.sum(dp.astype(F32), axis=0, keepdims=True)
    return part


def attend_back_kernel(dims, far, order, lens, d_own, d_peer, normed, qkv, mixed, wq, wo, wf, *refs):
    if not far:
        prior_keep, prior_send, *refs = refs
    keep, send, grad, *refs = refs
    if far:
        grad_rest, *refs = refs
    col_sums, dattn, dmixed, dqkv, acc, w, ow = refs
    i = pl.program_id(0)
    slab, quarter, local = dims.slab, dims.quarter, dims.local
    two, one_head = parts_of(dims)
    tiles = 2 if far else 1
    width = tiles * two
    count = quarter * slab
    model = normed.shape[-1]

    @pl.when(i == 0)
    def _():
        dattn[...] = d_own[...]
        acc[...] = jnp.zeros_like(acc)
        col_sums[...] = jnp.zeros_like(col_sums)
        for t in range(4):
            dst, at = (w, t * width) if t < 3 else (ow, 0)
            own, start = (wq, t * local) if t < 3 else (wo, 0)
            if far:
                copy_rows(dst, at, wf, t * local, two)
                copy_rows(dst, at + two, own, start + two, one_head)
                copy_rows(dst, at + two + one_head, wf, t * local + two, one_head)
            else:
                copy_rows(dst, at, own, start, two)

    @pl.when(i == 1)
    def _():
        dattn[...] = d_peer[...]

    part = back_step(dims, tiles, lens, order[2 * i], dattn, normed, qkv, mixed,
                     dmixed, dqkv, acc, col_sums, w, ow)

    @pl.when(i == 0)
    def _():
        prior = 0.0 if far else prior_keep[...].reshape(count, model).astype(F32)
        keep[...] = (part + prior).astype(BF16).reshape(quarter, slab, model)

    @pl.when(i == 1)
    def _():
        prior = 0.0 if far else prior_send[...].reshape(count, model).astype(F32)
        send[...] = (part + prior).astype(BF16).reshape(quarter, slab, model)
        for t in range(4):
            grad[:, t * two:(t + 1) * two] = acc[:, t * width:t * width + two].astype(BF16)
            if far:
                at = t * width + two
                to = 4 * two + t * one_head
                grad[:, to:to + one_head] = acc[:, at + one_head:at + two].astype(BF16)
                grad_rest[:, t * one_head:(t + 1) * one_head] = acc[:, at:at + one_head].astype(BF16)


def attend_back(dims, far, order, lens, d_own, d_peer, normed, qkv, mixed, wq, wo, wf, prior=()):
    model = normed.shape[-1]
    slab, quarter = dims.slab, dims.quarter
    width = 256 if far else 128
    one = pl.BlockSpec((quarter, slab, model), lambda i, o, n: (0, 0, 0))
    stride = normed.shape[0] // (2 * quarter)
    step = lambda cols: pl.BlockSpec((quarter, slab, cols), lambda i, o, n: (stride * i, 0, 0))
    grads = (768, 256) if far else (512,)
    specs = [one, one] + [pl.BlockSpec((model, n), lambda i, o, n_: (0, 0)) for n in grads]
    specs += [pl.BlockSpec((1, 3 * width), lambda i, o, n: (0, 0))]
    shapes = [
        jax.ShapeDtypeStruct((quarter, slab, model), BF16),
        jax.ShapeDtypeStruct((quarter, slab, model), BF16),
    ] + [jax.ShapeDtypeStruct((model, n), BF16) for n in grads] + [jax.ShapeDtypeStruct((1, 3 * width), F32)]
    scratch = [
        pltpu.VMEM((quarter, slab, model), BF16),
        pltpu.VMEM((quarter, slab, width), BF16),
        pltpu.VMEM((quarter, slab, 3 * width), BF16),
        pltpu.VMEM((model, 4 * width), F32),
        pltpu.VMEM((3 * width, model), BF16),
        pltpu.VMEM((width, model), BF16),
    ]
    return pl.pallas_call(
        functools.partial(attend_back_kernel, dims, far),
        grid_spec=pltpu.PrefetchScalarGridSpec(
            num_scalar_prefetch=2,
            grid=(2,),
            in_specs=[one, one, step(model), step(3 * width), step(width), spec_whole(wq), spec_whole(wo),
                      spec_whole(wf)] + [one] * len(prior),
            out_specs=specs,
            scratch_shapes=scratch,
        ),
        out_shape=shapes,
        compiler_params=params(),
        cost_estimate=pl.CostEstimate(
            flops=32 * quarter * slab * model * width, bytes_accessed=20_000_000, transcendentals=0),
        name="attend_back_far" if far else "attend_back_own",
    )(order, lens, d_own, d_peer, normed, qkv, mixed, wq, wo, wf, *prior)


def swap(value, axis, bit):
    size = lax.axis_size(axis)
    return lax.ppermute(value, axis, [(j, j ^ bit) for j in range(size)])


def to_core(value):
    return swap(value, "mp", 1)


def to_y(value):
    return swap(value, "mp", 2)


def from_others(value, axis, first, count):
    return [value] + [swap(value, axis, k * first) for k in range(1, count)]


def add_tree(parts):
    while len(parts) > 1:
        parts = [a + b for a, b in zip(parts[::2], parts[1::2])]
    return parts[0]


def sum_over(value, axis):
    first = 1
    while first < lax.axis_size(axis):
        count = min(8, lax.axis_size(axis) // first)
        value = add_tree(from_others(value, axis, first, count))
        first *= count
    return value


def gather_batch(value):
    parts = [value]
    first = 1
    size = lax.axis_size("batch")
    while first < size:
        count = min(8, size // first)
        whole = jnp.concatenate(parts) if len(parts) > 1 else parts[0]
        parts = from_others(whole, "batch", first, count)
        first *= count
    return parts


def gather_rows(own, me):
    near = jnp.stack([own, to_y(own)])
    far = to_core(near)
    out = jnp.zeros((4,) + own.shape, own.dtype)
    for r, value in enumerate((near[0], near[1], far[0], far[1])):
        out = lax.dynamic_update_slice(out, value[None], (me ^ ORDER[r],) + (0,) * own.ndim)
    return out.reshape((4 * own.shape[0],) + own.shape[1:])


def add_low(a, b):
    return (a.astype(F32) + b.astype(F32)).astype(BF16)


MESH = pl.DeviceIdType.MESH


class Place:
    def __init__(self):
        self.b, self.m = lax.axis_index("batch"), lax.axis_index("mp")
        self.z, self.x = self.b // 2, self.b % 2
        self.y, self.c = self.m // 2, self.m % 2
        self.core = (self.b, 2 * self.y + 1 - self.c)
        self.near = (self.b, 2 * (1 - self.y) + self.c)
        self.across = (self.b, 2 * (1 - self.y) + 1 - self.c)
        self.side = (2 * self.z + 1 - self.x, self.m)
        self.z_pair = self.z + 1 - 2 * (self.z % 2)
        self.z_far = (self.z + 2) % 4
        self.z_rest = (self.z_pair + 2) % 4
        self.paired = (2 * self.z_pair + self.x, self.m)
        self.opposite = (2 * self.z_far + self.x, self.m)
        self.batch = [((self.b + k) % 8, self.m) for k in range(1, 8)]

    def quarter(self, far_y, far_core):
        return 2 * ((self.y + far_y) % 2) + (self.c + far_core) % 2


def meet(peers):
    barrier = pltpu.get_barrier_semaphore()
    for peer in peers:
        pl.semaphore_signal(barrier, inc=1, device_id=peer, device_id_type=MESH)
    pl.semaphore_wait(barrier, len(peers))


def remote(src, dst, send_sem, recv_sem, at, device):
    return pltpu.make_async_remote_copy(
        src_ref=src, dst_ref=dst, send_sem=send_sem.at[at], recv_sem=recv_sem.at[at],
        device_id=device, device_id_type=MESH)


def front_kernel(dims, lens, img, txt, vectors, bias, own_w, own_o,
                 vec, normed, qkv, mixed, qkv_far, mixed_far, far_w, attended, attn, expert, expert_peer, cls, cls_peer,
                 rows, w, w2, ow, b, wf, far_bias, n_all, rest, m_all, m_far, q_own, q_far, a_send, a_recv, e_send, c_recv, held,
                 local_sem, send_sem, recv_sem):
    here = Place()
    i = pl.program_id(0)
    local, quarter, slab, ip = dims.local, dims.quarter, dims.slab, dims.ip
    two, one_head = parts_of(dims)
    count = quarter * slab
    model = img.shape[-1]
    at = i % 4
    whose = here.quarter(at % 2, 1 - at // 2)
    sent_w = [remote(own_w, wf.at[pl.ds(0, 3 * local)], send_sem, recv_sem, 0, here.near),
              remote(own_o, wf.at[pl.ds(3 * local, local)], send_sem, recv_sem, 1, here.near),
              remote(bias, far_bias, send_sem, recv_sem, 2, here.near)]
    sent_a = [remote(a_send.at[j], a_recv.at[j], send_sem, recv_sem, 3 + j, here.core) for j in range(2)]

    def e_over(j):
        return remote(e_send.at[j], expert_peer.at[j], send_sem, recv_sem, 5 + j, here.core)

    def e_here(j):
        return pltpu.make_async_copy(e_send.at[j], expert.at[j], local_sem.at[1 + j])

    sent_c = remote(cls, c_recv, send_sem, recv_sem, 5 + 2 * quarter, here.core)
    keep_w = pltpu.make_async_copy(wf, far_w, local_sem.at[0])
    sent_e = [e_over(j) for j in range(2 * quarter)]
    keep_e = [e_here(j) for j in range(2 * quarter)]

    @pl.when(i == 0)
    def _():
        meet([here.core, here.near])
        for copy in sent_w:
            copy.start()
        fill(vec, vectors)
        rows[...] = jnp.zeros_like(rows)
        b[...] = jnp.zeros_like(b)
        w[...] = jnp.zeros_like(w)
        cls[...] = jnp.zeros_like(cls)
        for t in range(3):
            copy_rows(w, t * 2 * two, own_w, t * local, local)
        b[0:1, 0:local] = bias[0:1, :]
        b[0:1, 4 * two:4 * two + local] = bias[1:2, :]

    def project(weights):
        proj = dot_t(n_all[at].reshape(count, model), weights[...]) + b[0:1, :]
        return proj.astype(BF16).reshape(quarter, slab, 6 * two)

    @pl.when(i < 4)
    def _():
        def one_norm(p, c):
            load_rows(dims, p, img, txt, rows)
            n, _ = normalise(rows[...])
            n_all[at, p] = (n * vector(vec, GAIN1) + vector(vec, SHIFT1)).astype(BF16)
            return c

        lax.fori_loop(0, quarter, one_norm, 0)
        proj = project(w)
        for t in range(3):
            q_own[:, :, t * two:(t + 1) * two] = proj[:, :, 2 * t * two:(2 * t + 1) * two]
            rest[at, :, :, t * two:(t + 1) * two] = proj[:, :, (2 * t + 1) * two:(2 * t + 2) * two]
        attend_tiles(dims, lens, whose, q_own, m_all.at[at])

        @pl.when(i % 2 == 0)
        def _():
            normed[...] = n_all[at]
            qkv[...] = q_own[...]
            mixed[...] = m_all[at]

    @pl.when(i == 4)
    def _():
        for copy in sent_w:
            copy.wait_recv()
        keep_w.start()
        w2[...] = jnp.zeros_like(w2)
        b[...] = jnp.zeros_like(b)
        for t in range(3):
            copy_rows(w2, t * 2 * two, wf, t * local, two)
            copy_rows(w2, t * 2 * two + two + one_head, wf, t * local + two, one_head)
        for t, to in ((0, 0), (1, 4 * two)):
            b[0:1, to:to + two] = far_bias[t:t + 1, 0:two]
            b[0:1, to + two + one_head:to + 2 * two] = far_bias[t:t + 1, two:]
        copy_rows(ow, 0, own_o, 0, two)
        copy_rows(ow, two, wf, 3 * local, two)
        copy_rows(ow, 2 * two, own_o, two, one_head)
        copy_rows(ow, 2 * two + one_head, wf, 3 * local + two, one_head)

    @pl.when(i >= 4)
    def _():
        proj = project(w2)
        for t in range(3):
            to = 2 * t * two
            q_far[:, :, to:to + two] = proj[:, :, to:to + two]
            q_far[:, :, to + two:to + 2 * two] = (
                proj[:, :, to + two:to + 2 * two] + rest[at, :, :, t * two:(t + 1) * two])
        attend_tiles(dims, lens, whose, q_far, m_far)

        @pl.when(i % 2 == 0)
        def _():
            qkv_far[...] = q_far[...]
            mixed_far[...] = m_far[...]

        part = dot(m_all[at].reshape(count, two), ow[0:two, :])
        part = part + dot(m_far[...].reshape(count, 2 * two), ow[two:, :])
        part = part.reshape(quarter, slab, model)

        @pl.when(i < 6)
        def _():
            a_send[at] = part.astype(BF16)

        for j in range(2):
            @pl.when(i == 4 + j)
            def _():
                sent_a[j].start()

        for j in range(2):
            @pl.when(i == 6 + j)
            def _():
                sent_a[j].wait_recv()

        @pl.when(i >= 6)
        def _():
            j = i - 6
            held[...] = part

            def one_residual(p, c):
                load_rows(dims, p, img, txt, rows)
                a = held[p] + a_recv[j, p].astype(F32)
                x = rows[...] + vector(vec, A_SCALE) * (a + vector(vec, A_BIAS))
                n, _ = normalise(x)
                e_img = n[0:ip] * vector(vec, GAIN2) + vector(vec, SHIFT2)
                e_txt = n[ip:] * vector(vec, GAIN2 + 1) + vector(vec, SHIFT2 + 1)
                r = j * quarter + p
                e_send[r, 0:ip, :] = e_img.astype(BF16)
                e_send[r, ip:, :] = e_txt.astype(BF16)
                e_over(r).start()
                e_here(r).start()
                for k, v in enumerate((x[0:1], x[ip:ip + 1], e_img[0:1], e_txt[0:1])):
                    cls[k, pl.ds(r, 1), :] = v

                @pl.when(j == 0)
                def _():
                    attended[p] = x
                    attn[p] = a

                return c

            lax.fori_loop(0, quarter, one_residual, 0)

    @pl.when(i == 7)
    def _():
        sent_c.start()
        keep_w.wait()
        for copy in keep_e:
            copy.wait()
        sent_c.wait()
        cls_peer[...] = c_recv[...]
        for copy in sent_e:
            copy.wait()
        for copy in sent_w + sent_a:
            copy.wait_send()


def fill(table, vectors):
    table[...] = jnp.zeros_like(table)
    at = 0
    for v in vectors:
        n = v.shape[0] if len(v.shape) == 2 else 1
        table[at:at + n, :] = v[...].reshape(n, table.shape[1])
        at += n


def front(dims, lens, img, txt, vectors, bias, own_w, own_o):
    model = img.shape[-1]
    quarter, slab, local = dims.quarter, dims.slab, dims.local
    held = pl.BlockSpec(memory_space=pltpu.VMEM)
    away = pl.BlockSpec(memory_space=pl.ANY)

    def states_at(i):
        return Place().quarter(i % 2, 1 - i % 4 // 2), 0, 0

    own_block = lambda cols: pl.BlockSpec((quarter, slab, cols), lambda i: (jnp.where(i < 2, 1, 0), 0, 0))
    far_block = lambda cols: pl.BlockSpec((quarter, slab, cols), lambda i: (jnp.where(i < 6, 1, 0), 0, 0))
    six = lambda cols: jax.ShapeDtypeStruct((2 * quarter, slab, cols), BF16)
    block = lambda cols: (quarter, slab, cols)
    n_remote = 6 + 2 * quarter
    return pl.pallas_call(
        lambda lens, img, txt, *refs: front_kernel(
            dims, lens, img, txt, refs[:len(vectors)], *refs[len(vectors):]),
        grid=(8,),
        in_specs=[pl.BlockSpec(memory_space=pltpu.SMEM),
                  pl.BlockSpec((quarter, dims.patches, model), states_at),
                  pl.BlockSpec((quarter, dims.caption, model), states_at)] + [held] * (3 + len(vectors)),
        out_specs=[held, own_block(model), own_block(384), own_block(128), far_block(768), far_block(256),
                   away, held, held, away, away, held, held],
        out_shape=[jax.ShapeDtypeStruct((16, model), F32), six(model), six(384), six(128), six(768), six(256),
                   jax.ShapeDtypeStruct((4 * local, model), BF16),
                   jax.ShapeDtypeStruct(block(model), F32), jax.ShapeDtypeStruct(block(model), F32),
                   six(model), six(model),
                   jax.ShapeDtypeStruct((4, 8, model), F32), jax.ShapeDtypeStruct((4, 8, model), F32)],
        scratch_shapes=[
            pltpu.VMEM((slab, model), F32), pltpu.VMEM((768, model), BF16), pltpu.VMEM((768, model), BF16),
            pltpu.VMEM((384, model), BF16), pltpu.VMEM((8, 768), F32), pltpu.VMEM((4 * local, model), BF16),
            pltpu.VMEM((2, local), F32),
            pltpu.VMEM((4,) + block(model), BF16), pltpu.VMEM((4,) + block(384), BF16),
            pltpu.VMEM((4,) + block(128), BF16), pltpu.VMEM(block(256), BF16),
            pltpu.VMEM(block(384), BF16), pltpu.VMEM(block(768), BF16),
            pltpu.VMEM((2,) + block(model), BF16), pltpu.VMEM((2,) + block(model), BF16),
            pltpu.VMEM((2 * quarter, slab, model), BF16), pltpu.VMEM((4, 8, model), F32),
            pltpu.VMEM(block(model), F32),
            pltpu.SemaphoreType.DMA((1 + 2 * quarter,)),
            pltpu.SemaphoreType.DMA((n_remote,)), pltpu.SemaphoreType.DMA((n_remote,)),
        ],
        compiler_params=params(collective_id=6, has_side_effects=True),
        cost_estimate=pl.CostEstimate(
            flops=16 * quarter * slab * model * 1152, bytes_accessed=40_000_000, transcendentals=0),
        name="front",
    )(lens, img, txt, *vectors, bias, own_w, own_o)


def middle_kernel(dims, total, img, txt, own, peer, cls_own, cls_peer, vec, up, up_bias, down, weight, scale,
                  act, dup, ddn, dexp, d_own, d_near, bias_grad, class_e, c_act, c_dup, c_ddn, dcls,
                  head_in, dproj, gains, shifts, scalars,
                  bx, bd, rx, rd, x_near, x_far, ins, rows, part, parts, cls, back, cot, c_rows, extra, extras,
                  send_sem, recv_sem):
    here = Place()
    ip, slab, quarter = dims.ip, dims.slab, dims.quarter
    i = pl.program_id(0)
    model = own.shape[-1]
    mp_peers = [here.core, here.near, here.across]
    of = [here.quarter(0, 0), here.quarter(1, 0), here.quarter(0, 1), here.quarter(1, 1)]

    sent_x = [remote(bx.at[2 * j], rx.at[j], send_sem, recv_sem, j, here.core) for j in range(2)]
    sent_d = [remote(bd.at[2 * j], rd.at[j], send_sem, recv_sem, 2 + j, here.core) for j in range(2)]
    sent_near = remote(x_near, x_far, send_sem, recv_sem, 4, here.near)
    sent_part = [remote(part, parts.at[k], send_sem, recv_sem, 5 + k, mp_peers[k]) for k in range(3)]
    sent_extra = [remote(extra, extras.at[k], send_sem, recv_sem, 8 + k, mp_peers[k]) for k in range(3)]
    sent_cls = [remote(cls.at[here.b], cls.at[here.b], send_sem, recv_sem, 11 + k, here.batch[k]) for k in range(7)]

    @pl.when(i == 0)
    def _():
        rows[...] = jnp.zeros_like(rows)
        bias_grad[...] = jnp.zeros_like(bias_grad)
        for m in range(2):
            e = jnp.concatenate([cls_own[2 + m], cls_peer[2 + m]], axis=0).astype(BF16)
            class_e[m] = e
            u = dot(e, up[m]) + up_bias[m:m + 1]
            part[m] = dot(gelu_low(u), down[m])
        meet(mp_peers + here.batch)
        for copy in sent_part:
            copy.start()
        ins[...] = peer[quarter:, :, :]

    @pl.when(i == 1)
    def _():
        for copy in sent_part:
            copy.wait_recv()
        for m in range(2):
            cls[here.b, m] = jnp.zeros(cls.shape[2:], F32)
            for r in range(4):
                half, at = (cls_own, cls_peer)[r // 2], quarter * (r % 2)
                for p in range(quarter):
                    line = [d[m, own_row(dims, s, p):own_row(dims, s, p) + 1, :]
                            for d, s in ((part, r), (parts.at[0], r ^ 2), (parts.at[1], r ^ 1), (parts.at[2], r ^ 3))]
                    x = (line[0] + line[1]) + (line[2] + line[3]) + vector(vec, F_BIAS + m)
                    x = half[m, at + p:at + p + 1, :] + vector(vec, F_SCALE) * x
                    cls[here.b, m, pl.ds(4 * of[r] + p, 1), :] = x
        for copy in sent_cls:
            copy.start()
        ins[...] = own[quarter:, :, :]

    @pl.when(i == 2)
    def _():
        ins[...] = peer[:quarter, :, :]

    @pl.when(i == 3)
    def _():
        ins[...] = own[:quarter, :, :]
        for copy in sent_cls:
            copy.wait_recv()
        n_rows = 16 * cls.shape[0]
        sharp = jnp.exp(scale[...])
        col_at = lax.broadcasted_iota(jnp.int32, (1, n_rows), 1)
        row_at = lax.broadcasted_iota(jnp.int32, (n_rows, 1), 0)
        col_ok = (col_at % 4) < quarter
        row_ok = (row_at % 4) < quarter
        normal, inverse, proj, unit, embed = [], [], [], [], []
        for m in range(2):
            n, r = normalise(cls[:, m].reshape(n_rows, model))
            h = (n * vector(vec, H_GAIN + m) + vector(vec, H_SHIFT + m)).astype(BF16)
            head_in[m] = h
            y = dot(h, weight[m])
            u = lax.rsqrt(jnp.sum(y * y, axis=-1, keepdims=True) + 1e-6)
            normal.append(n)
            inverse.append(r)
            proj.append(y)
            unit.append(u)
            embed.append((y * u).astype(BF16))
        ok = row_ok & col_ok
        logits = sharp * dot_t(embed[0], embed[1])
        masked = jnp.where(ok, logits, -1e30)
        row_max = jnp.max(masked, axis=1, keepdims=True)
        row_lse = row_max + jnp.log(jnp.sum(jnp.exp(masked - row_max), axis=1, keepdims=True))
        col_max = jnp.max(masked, axis=0, keepdims=True)
        col_lse = col_max + jnp.log(jnp.sum(jnp.exp(masked - col_max), axis=0, keepdims=True))
        same = (row_at == col_at) & ok
        both = jnp.exp(masked - row_lse) + jnp.exp(masked - col_lse)
        dlogits = jnp.where(ok, jnp.where(same, both - 2.0, both) * (1.0 / (2 * total)), 0.0)
        diagonal = jnp.sum(jnp.where(same, logits, 0.0), axis=1, keepdims=True)
        lines = jnp.sum(jnp.where(row_ok, row_lse - 2.0 * diagonal, 0.0), axis=0, keepdims=True)
        lines = lines + jnp.sum(jnp.where(col_ok, col_lse, 0.0), axis=1, keepdims=True)
        slope = jnp.sum(jnp.sum(dlogits * logits, axis=1, keepdims=True), axis=0, keepdims=True)
        scalars[0:1, :] = jnp.broadcast_to(lines * (1.0 / (2 * total)), (1, 128))
        scalars[1:2, :] = jnp.broadcast_to(slope, (1, 128))
        high = lax.Precision.HIGHEST
        wide = [e.astype(F32) for e in embed]
        dembed = [
            sharp * jnp.dot(dlogits, wide[1], precision=high, preferred_element_type=F32),
            sharp * lax.dot_general(dlogits, wide[0], (((0,), (0,)), ((), ())), precision=high,
                                    preferred_element_type=F32),
        ]
        c_rows[...] = jnp.zeros_like(c_rows)
        dcls[...] = jnp.zeros_like(dcls)
        for m in range(2):
            for p in range(quarter):
                src = (img, txt)[m]
                cot[m, 8 * 3 + p:8 * 3 + p + 1, :] = src[p, 0:1, :].astype(F32)
        for m in range(2):
            u, y, d = unit[m], proj[m], dembed[m]
            dp = (u * d - u * u * u * y * jnp.sum(y * d, axis=-1, keepdims=True)).astype(BF16)
            dproj[m] = dp
            dh = dot_t(dp, weight[m])
            gains[m:m + 1, :] = jnp.sum(dh * normal[m], axis=0, keepdims=True)
            shifts[m:m + 1, :] = jnp.sum(dh, axis=0, keepdims=True)
            back[m] = norm_back(normal[m], inverse[m], dh * vector(vec, H_GAIN + m))
            for r in range(4):
                step = (3, 1, 2, 0)[r]
                for p in range(quarter):
                    g = back[m, pl.ds(16 * here.b + 4 * of[r] + p, 1), :]
                    at = own_row(dims, r, p)
                    c_rows[m, at:at + 1, :] = cot[m, 8 * step + p:8 * step + p + 1, :] + g
                    if r == 0:
                        dcls[p, m:m + 1, :] = g
            u = dot(class_e[m], up[m]) + up_bias[m:m + 1]
            big, small = gelu_parts(u)
            c_act[m] = (u * big).astype(BF16)
            g = (c_rows[m] * vector(vec, F_SCALE)).astype(BF16)
            c_ddn[m] = g
            du = dot_t(g, down[m]) * (big + u * small)
            bias_grad[m:m + 1, :] += jnp.sum(du, axis=0, keepdims=True)
            low = du.astype(BF16)
            c_dup[m] = low
            extra[m] = dot_t(low, up[m])
        for copy in sent_extra:
            copy.start()

    at = lax.broadcasted_iota(jnp.int32, (slab, 1), 0)
    inner = (at != 0) & (at != ip)

    def one(p, c):
        load_rows(dims, p, img, txt, rows)
        cot[0, pl.ds(8 * i + p, 1), :] = rows[0:1, :]
        cot[1, pl.ds(8 * i + p, 1), :] = rows[ip:ip + 1, :]
        ddn[p] = jnp.where(inner, rows[...] * vector(vec, F_SCALE), 0.0).astype(BF16)
        return c

    lax.fori_loop(0, quarter, one, 0)
    for m, lo, hi in ((0, 0, ip), (1, ip, slab)):
        count = quarter * (hi - lo)
        e = ins[:, lo:hi, :].reshape(count, model)
        u = dot(e, up[m]) + up_bias[m:m + 1]
        big, small = gelu_parts(u)
        a = (u * big).astype(BF16)
        act[:, lo:hi, :] = a.reshape(quarter, hi - lo, -1)
        slope = big + u * small
        bd[i, :, lo:hi, :] = dot(a, down[m]).astype(BF16).reshape(quarter, hi - lo, model)
        g = ddn[:, lo:hi, :].reshape(count, model)
        du = dot_t(g, down[m]) * slope
        bias_grad[m:m + 1, :] += jnp.sum(du, axis=0, keepdims=True)
        low = du.astype(BF16)
        dup[:, lo:hi, :] = low.reshape(quarter, hi - lo, -1)
        bx[i, :, lo:hi, :] = dot_t(low, up[m]).astype(BF16).reshape(quarter, hi - lo, model)

    for j in range(2):
        @pl.when(i == 2 * j)
        def _():
            sent_x[j].start()
            sent_d[j].start()

    @pl.when(i == 1)
    def _():
        sent_x[0].wait_recv()

        def add_x(p, c):
            x_near[p] = (bx[1, p].astype(F32) + rx[0, p].astype(F32)).astype(BF16)
            return c

        lax.fori_loop(0, quarter, add_x, 0)
        sent_near.start()
        sent_d[0].wait_recv()

        def add_d(p, c):
            d_near[p] = (bd[1, p].astype(F32) + rd[0, p].astype(F32)).astype(BF16)
            return c

        lax.fori_loop(0, quarter, add_d, 0)

    @pl.when(i == 3)
    def _():
        sent_d[1].wait_recv()

        def add_d(p, c):
            d_own[p] = bd[3, p].astype(F32) + rd[1, p].astype(F32)
            return c

        lax.fori_loop(0, quarter, add_d, 0)
        sent_x[1].wait_recv()
        sent_near.wait_recv()

        def add_x(p, c):
            dexp[p] = bx[3, p].astype(F32) + rx[1, p].astype(F32) + x_far[p].astype(F32)
            return c

        lax.fori_loop(0, quarter, add_x, 0)
        for copy in sent_extra:
            copy.wait_recv()
        for m in range(2):
            for p in range(quarter):
                line = [x[m, own_row(dims, r, p):own_row(dims, r, p) + 1, :]
                        for x, r in ((extra, 0), (extras.at[0], 2), (extras.at[1], 1), (extras.at[2], 3))]
                dexp[p, m * ip:m * ip + 1, :] += (line[0] + line[1]) + (line[2] + line[3])
        for copy in sent_x + sent_d + [sent_near] + sent_part + sent_extra + sent_cls:
            copy.wait_send()


def middle(dims, total, img, txt, own, peer, cls_own, cls_peer, vec, up, up_bias, down, weight, scale):
    model = own.shape[-1]
    hidden = up.shape[-1]
    slab, quarter = dims.slab, dims.quarter
    batch = 8

    def cot_at(i):
        here = Place()
        return here.quarter(1 - i // 2, 1 - i % 2), 0, 0

    held = pl.BlockSpec(memory_space=pltpu.VMEM)
    step = lambda cols: pl.BlockSpec((quarter, slab, cols), lambda i: (i, 0, 0))
    rows_of = lambda n, t: jax.ShapeDtypeStruct((n, slab, model), t)
    small = [((quarter, slab, model), F32), ((quarter, slab, model), F32), ((quarter, slab, model), BF16),
             ((2, hidden), F32), ((2, 16, model), BF16), ((2, 16, hidden), BF16), ((2, 16, hidden), BF16),
             ((2, 16, model), BF16), ((quarter, 8, model), F32), ((2, 16 * batch, model), BF16),
             ((2, 16 * batch, weight.shape[2]), BF16), ((2, model), F32), ((2, model), F32), ((2, 128), F32)]
    block = (quarter, slab, model)
    return pl.pallas_call(
        functools.partial(middle_kernel, dims, total),
        grid=(4,),
        in_specs=[pl.BlockSpec((quarter, dims.patches, model), cot_at),
                  pl.BlockSpec((quarter, dims.caption, model), cot_at)] + [held] * 10,
        out_specs=[step(hidden), step(hidden), step(model)] + [held] * len(small),
        out_shape=[rows_of(4 * quarter, BF16)] * 3 + [jax.ShapeDtypeStruct(v, t) for v, t in small],
        scratch_shapes=[
            pltpu.VMEM((4,) + block, BF16), pltpu.VMEM((4,) + block, BF16),
            pltpu.VMEM((2,) + block, BF16), pltpu.VMEM((2,) + block, BF16),
            pltpu.VMEM(block, BF16), pltpu.VMEM(block, BF16), pltpu.VMEM(block, BF16),
            pltpu.VMEM((slab, model), F32),
            pltpu.VMEM((2, 16, model), F32), pltpu.VMEM((3, 2, 16, model), F32),
            pltpu.VMEM((batch, 2, 16, model), F32), pltpu.VMEM((2, 16 * batch, model), F32),
            pltpu.VMEM((2, 32, model), F32), pltpu.VMEM((2, 16, model), F32),
            pltpu.VMEM((2, 16, model), F32), pltpu.VMEM((3, 2, 16, model), F32),
            pltpu.SemaphoreType.DMA((18,)), pltpu.SemaphoreType.DMA((18,)),
        ],
        compiler_params=params(collective_id=2, has_side_effects=True),
        cost_estimate=pl.CostEstimate(
            flops=32 * quarter * slab * model * hidden, bytes_accessed=40_000_000, transcendentals=0),
        name="middle",
    )(img, txt, own, peer, cls_own, cls_peer, vec, up, up_bias, down, weight, scale)


def turn_kernel(dims, img, txt, peer, own, act, dup, ddn, ce, ca, cu, cd, dexp, attended, attn, d_own, d_near, dcls, vec,
                down_sum, up_keep, up_send, dattended, dattn, dattn_peer, fin_img, fin_txt, sums,
                acc, d_far, n_peer, rows, side_send, side_recv, e_in, dexp_in, attended_in, attn_in, d_own_in,
                local_sem, send_sem, recv_sem):
    here = Place()
    quarter, ip = dims.quarter, dims.ip
    i = pl.program_id(0)
    piece = side_send.shape[2]
    sent_near = remote(d_near, d_far, send_sem, recv_sem, 0, here.near)

    def over(p):
        return remote(dattn.at[p], n_peer.at[p], send_sem, recv_sem, 1 + p, here.core)

    sent_core = [over(p) for p in range(quarter)]
    sent_side = [remote(side_send.at[j], side_recv.at[j], send_sem, recv_sem, 1 + quarter + j, here.side)
                 for j in range(4)]
    loaded = [pltpu.make_async_copy(src, dst, local_sem.at[j]) for j, (src, dst) in enumerate((
        (dexp, dexp_in), (attended, attended_in), (attn, attn_in), (d_own, d_own_in)))]
    dexp, attended, attn, d_own = dexp_in, attended_in, attn_in, d_own_in
    spans = ((0, 0, ip), (1, ip, dims.slab))
    flat = lambda v: v.reshape(-1, v.shape[-1])
    block = lambda j: pl.ds(pl.multiple_of(j * piece, piece), piece)

    @pl.when(i == 0)
    def _():
        meet([here.core, here.near, here.side])
        sent_near.start()
        for copy in loaded:
            copy.start()
        for m in range(2):
            acc[m] = t_dot(cd[m], ca[m])

    @pl.when(i < 4)
    def _():
        for m, lo, hi in spans:
            acc[m] += t_dot(flat(ddn[:, lo:hi, :]), flat(act[:, lo:hi, :]))

    @pl.when(i == 3)
    def _():
        for j in range(4):
            for m in range(2):
                side_send[j, m] = acc[m, block(2 * j + 1 - here.x), :].astype(BF16)
                down_sum[j, m] = acc[m, block(2 * j + here.x), :].astype(BF16)
            sent_side[j].start()

    @pl.when(i == 4)
    def _():
        for m in range(2):
            acc[m] = t_dot(ce[m], cu[m])

    @pl.when((i >= 4) & (i % 2 == 0))
    def _():
        e_in[...] = peer[...]

    @pl.when((i >= 4) & (i % 2 == 1))
    def _():
        e_in[...] = own[...]

    @pl.when(i >= 4)
    def _():
        for m, lo, hi in spans:
            acc[m] += t_dot(flat(e_in[:, lo:hi, :]), flat(dup[:, lo:hi, :]))

    @pl.when(i == 7)
    def _():
        for j in range(4):
            for m in range(2):
                up_keep[j, m] = acc[m, block(2 * j + here.x), :].astype(BF16)
                up_send[j, m] = acc[m, block(2 * j + 1 - here.x), :].astype(BF16)
        for copy in loaded:
            copy.wait()
        rows[...] = jnp.zeros_like(rows)
        sums[...] = jnp.zeros_like(sums)

        def load(p):
            load_rows(dims, p, img, txt, rows)
            rows[0:1, :] += dcls[p, 0:1, :]
            rows[ip:ip + 1, :] += dcls[p, 1:2, :]

        def norm(p, c):
            load(p)
            for m, lo, hi in ((0, 0, ip), (1, ip, dims.slab)):
                n, r = normalise(attended[p, lo:hi, :])
                dy = dexp[p, lo:hi, :]
                sums[m:m + 1, :] += jnp.sum(dy * n, axis=0, keepdims=True)
                sums[2 + m:3 + m, :] += jnp.sum(dy, axis=0, keepdims=True)
                d = rows[lo:hi, :] + norm_back(n, r, dy * vector(vec, GAIN2 + m))
                dattended[p, lo:hi, :] = d
                sd = d * vector(vec, A_SCALE)
                dattn[p, lo:hi, :] = sd.astype(BF16)
                a = attn[p, lo:hi, :] + vector(vec, A_BIAS)
                sums[4:5, :] += jnp.sum(d * a, axis=0, keepdims=True)
                sums[5:6, :] += jnp.sum(sd, axis=0, keepdims=True)
            over(p).start()
            return c

        lax.fori_loop(0, quarter, norm, 0)
        sent_near.wait_recv()

        def final(p, c):
            load(p)
            for m, lo, hi in ((0, 0, ip), (1, ip, dims.slab)):
                b = d_own[p, lo:hi, :] + d_far[p, lo:hi, :].astype(F32) + vector(vec, F_BIAS + m)
                f = attended[p, lo:hi, :] + vector(vec, F_SCALE) * b
                if m == 0:
                    fin_img[p] = f[0:dims.patches].astype(BF16)
                else:
                    fin_txt[p] = f[0:dims.caption].astype(BF16)
                g = rows[lo:hi, :]
                sums[6:7, :] += jnp.sum(g * b, axis=0, keepdims=True)
                sums[7 + m:8 + m, :] += jnp.sum(g, axis=0, keepdims=True) * vector(vec, F_SCALE)
            return c

        lax.fori_loop(0, quarter, final, 0)
        for p in range(quarter):
            sent_core[p].wait()
            dattn_peer[p] = n_peer[p]
        for j in range(4):
            sent_side[j].wait()
            down_sum[j] = (down_sum[j].astype(F32) + side_recv[j].astype(F32)).astype(BF16)
        sent_near.wait_send()


def turn(dims, img, txt, peer, own, act, dup, ddn, ce, ca, cu, cd, dexp, attended, attn, d_own, d_near, dcls, vec):
    model = own.shape[-1]
    hidden = act.shape[-1]
    slab, quarter = dims.slab, dims.quarter
    held = pl.BlockSpec(memory_space=pltpu.VMEM)

    def own_at(i):
        return Place().quarter(0, 0), 0, 0

    away = pl.BlockSpec(memory_space=pl.ANY)
    half = pl.BlockSpec((quarter, slab, model), lambda i: (jnp.where(i < 6, 1, 0), 0, 0))
    first = pl.BlockSpec((quarter, slab, hidden), lambda i: (jnp.minimum(i, 3), 0, 0))
    last = pl.BlockSpec((quarter, slab, hidden), lambda i: (jnp.maximum(i - 4, 0), 0, 0))
    block = (quarter, slab, model)
    part = (4, 2, model // 8, hidden)
    outs = [(part, BF16), (part, BF16), (part, BF16), (block, F32), (block, BF16), (block, BF16),
            ((quarter, dims.patches, model), BF16), ((quarter, dims.caption, model), BF16), ((16, model), F32)]
    return pl.pallas_call(
        functools.partial(turn_kernel, dims),
        grid=(8,),
        in_specs=[pl.BlockSpec((quarter, dims.patches, model), own_at),
                  pl.BlockSpec((quarter, dims.caption, model), own_at)] + [half] * 2 + [first, last, first]
        + [held] * 4 + [away] * 4 + [held] * 3,
        out_specs=[held] * len(outs),
        out_shape=[jax.ShapeDtypeStruct(v, t) for v, t in outs],
        scratch_shapes=[
            pltpu.VMEM((2, model, hidden), F32), pltpu.VMEM(block, BF16), pltpu.VMEM(block, BF16),
            pltpu.VMEM((slab, model), F32), pltpu.VMEM(part, BF16), pltpu.VMEM(part, BF16),
            pltpu.VMEM(block, BF16),
        ] + [pltpu.VMEM(block, F32)] * 4 + [
            pltpu.SemaphoreType.DMA((4,)),
            pltpu.SemaphoreType.DMA((5 + quarter,)), pltpu.SemaphoreType.DMA((5 + quarter,)),
        ],
        compiler_params=params(collective_id=3, has_side_effects=True),
        cost_estimate=pl.CostEstimate(
            flops=16 * quarter * slab * model * hidden, bytes_accessed=40_000_000, transcendentals=0),
        name="turn",
    )(img, txt, peer, own, act, dup, ddn, ce, ca, cu, cd, dexp, attended, attn, d_own, d_near, dcls, vec)


def back_kernel(dims, lens, d_own, d_peer, normed, qkv_far, mixed_far, qkv_own, mixed_own, wq, wo, wf,
                fin_img, fin_txt, up_keep, up_send, down_sum,
                keep, send, grad_pair, grad_single, cols_far, cols_own, near_img, near_txt, far_sum, up_one, down_out, up_out,
                dattn, dm_far, dm_own, dq_far, dq_own, acc_far, acc_own, w_far, w_own, o_far, o_own, dn, grad_f,
                up_mine, up_side, up_low, up_in, up_pass, up_last, down_mine, down_in, down_pass, down_last,
                from_side, local_sem, send_sem, recv_sem):
    here = Place()
    i = pl.program_id(0)
    slab, quarter, local = dims.slab, dims.quarter, dims.local
    two, one_head = parts_of(dims)
    count = quarter * slab
    model = normed.shape[-1]
    piece = from_side.shape[1]
    block = lambda j: pl.ds(pl.multiple_of(j * piece, piece), piece)
    used = [0]

    def make(src, dst, device):
        at = used[0]
        used[0] += 1
        return remote(src, dst, send_sem, recv_sem, at, device)

    sent_near = [make(fin_img, near_img, here.near), make(fin_txt, near_txt, here.near)]
    sent_up = [make(up_send.at[j, m], up_side.at[m, j], here.side) for m in range(2) for j in range(4)]
    in_pair = lambda src, dst: [make(src.at[here.z_pair], dst.at[0], here.paired), make(src.at[here.z_rest], dst.at[1], here.paired)]
    sent_down = in_pair(down_sum, down_in)
    pass_down = make(down_pass, down_last, here.opposite)
    sent_far = [make(grad_f.at[block(2 * j + 1 - here.x)], from_side.at[j], here.side) for j in range(4)]
    sent_low = in_pair(up_low, up_in)
    pass_low = make(up_pass, up_last, here.opposite)
    loaded = [pltpu.make_async_copy(up_keep, up_mine, local_sem.at[0]),
              pltpu.make_async_copy(down_sum.at[here.z], down_mine.at[0], local_sem.at[1]),
              pltpu.make_async_copy(down_sum.at[here.z_far], down_mine.at[1], local_sem.at[2])]
    add = lambda *parts: functools.reduce(lambda p, q: p + q, [v.astype(F32) for v in parts])

    @pl.when(i == 0)
    def _():
        meet([here.near, here.side, here.paired, here.opposite])
        for copy in loaded + sent_near + sent_up + sent_down:
            copy.start()
        for acc, cols in ((acc_far, cols_far), (acc_own, cols_own)):
            acc[...] = jnp.zeros_like(acc)
            cols[...] = jnp.zeros_like(cols)
        for t in range(4):
            own, start = (wq, t * local) if t < 3 else (wo, 0)
            dst, at = (w_far, t * 2 * two) if t < 3 else (o_far, 0)
            copy_rows(dst, at, wf, t * local, two)
            copy_rows(dst, at + two, own, start + two, one_head)
            copy_rows(dst, at + two + one_head, wf, t * local + two, one_head)
            dst, at = (w_own, t * two) if t < 3 else (o_own, 0)
            copy_rows(dst, at, own, start, two)

    @pl.when(i % 2 == 0)
    def _():
        dattn[...] = d_own[...]

    @pl.when(i % 2 == 1)
    def _():
        dattn[...] = d_peer[...]

    whose = here.quarter(0, i % 2)

    @pl.when(i < 2)
    def _():
        part = back_step(dims, 2, lens, whose, dattn, normed, qkv_far, mixed_far, dm_far, dq_far, acc_far, cols_far,
                         w_far, o_far)
        dn[i] = part.reshape(quarter, slab, model)

    @pl.when(i == 0)
    def _():
        for copy in loaded[1:]:
            copy.wait()
        for copy in sent_down:
            copy.wait_recv()
        down_pass[...] = add(down_mine[1], down_in[1]).astype(BF16)
        pass_down.start()

    @pl.when(i == 1)
    def _():
        for t in range(4):
            at = t * 2 * two
            to = 4 * two + t * one_head
            grad_f[:, t * two:(t + 1) * two] = acc_far[:, at:at + two].astype(BF16)
            grad_f[:, to:to + one_head] = acc_far[:, at + two + one_head:at + 2 * two].astype(BF16)
            grad_single[:, t * one_head:(t + 1) * one_head] = acc_far[:, at + two:at + two + one_head].astype(BF16)
        for copy in sent_far:
            copy.start()
        loaded[0].wait()
        for j in range(4):
            sent_up[j].wait_recv()
            up_low[j] = add(up_mine[j, 0], up_side[0, j]).astype(BF16)
        for copy in sent_low:
            copy.start()

    @pl.when(i >= 2)
    def _():
        part = back_step(dims, 1, lens, whose, dattn, normed, qkv_own, mixed_own, dm_own, dq_own, acc_own, cols_own,
                         w_own, o_own)
        total = (part.reshape(quarter, slab, model) + dn[i - 2]).astype(BF16)

        @pl.when(i == 2)
        def _():
            keep[...] = total
            for copy in sent_low:
                copy.wait_recv()
            up_pass[...] = add(up_low[here.z_far], up_in[1]).astype(BF16)
            pass_low.start()

        @pl.when(i == 3)
        def _():
            send[...] = total

    @pl.when(i == 3)
    def _():
        grad_pair[...] = acc_own[...].astype(BF16)
        down_out[...] = add(down_mine[0], down_in[0])
        for j in range(4):
            sent_far[j].wait_recv()
            far_sum[j] = add(grad_f[block(2 * j + here.x), :], from_side[j]).astype(BF16)
        pass_down.wait_recv()
        down_out[...] += down_last[...].astype(F32)
        for j in range(4):
            sent_up[4 + j].wait_recv()
            up_one[j] = add(up_mine[j, 1], up_side[1, j]).astype(BF16)
        pass_low.wait_recv()
        up_out[...] = add(up_low[here.z], up_in[0], up_last[...])
        for copy in sent_near:
            copy.wait_recv()
        for copy in sent_near + sent_up + sent_down + sent_far + sent_low + [pass_down, pass_low]:
            copy.wait_send()


def back(dims, lens, d_own, d_peer, normed, qkv_far, mixed_far, qkv_own, mixed_own, wq, wo, wf,
         fin_img, fin_txt, up_keep, up_send, down_sum):
    model = normed.shape[-1]
    slab, quarter = dims.slab, dims.quarter
    hidden = up_keep.shape[-1]
    piece = model // 8
    held = pl.BlockSpec(memory_space=pltpu.VMEM)
    away = pl.BlockSpec(memory_space=pl.ANY)
    spec = lambda cols, at: pl.BlockSpec((quarter, slab, cols), lambda i: (at(i), 0, 0))
    early, late = lambda i: jnp.minimum(i, 1), lambda i: jnp.maximum(i - 2, 0)
    rows = (quarter, slab, model)
    outs = [(held, rows, BF16), (held, rows, BF16), (held, (model, 512), BF16), (held, (model, 256), BF16),
            (held, (1, 768), F32), (held, (1, 384), F32),
            (away, fin_img.shape, BF16), (away, fin_txt.shape, BF16),
            (held, (4, piece, model), BF16), (held, (4, piece, hidden), BF16),
            (held, (2, piece, hidden), F32), (held, (piece, hidden), F32)]
    slabs = lambda cols: pltpu.VMEM((quarter, slab, cols), BF16)
    return pl.pallas_call(
        functools.partial(back_kernel, dims),
        grid=(4,),
        in_specs=[pl.BlockSpec(memory_space=pltpu.SMEM), held, held, spec(model, lambda i: i % 2),
                  spec(768, early), spec(256, early), spec(384, late), spec(128, late), held, held, held]
        + [away] * 5,
        out_specs=[v[0] for v in outs],
        out_shape=[jax.ShapeDtypeStruct(v[1], v[2]) for v in outs],
        scratch_shapes=[
            slabs(model), slabs(256), slabs(128), slabs(768), slabs(384),
            pltpu.VMEM((model, 1024), F32), pltpu.VMEM((model, 512), F32),
            pltpu.VMEM((768, model), BF16), pltpu.VMEM((384, model), BF16),
            pltpu.VMEM((256, model), BF16), pltpu.VMEM((128, model), BF16),
            pltpu.VMEM((2,) + rows, F32), pltpu.VMEM((model, model), BF16),
            pltpu.VMEM((4, 2, piece, hidden), BF16), pltpu.VMEM((2, 4, piece, hidden), BF16),
            pltpu.VMEM((4, piece, hidden), BF16), pltpu.VMEM((2, piece, hidden), BF16),
            pltpu.VMEM((piece, hidden), BF16), pltpu.VMEM((piece, hidden), BF16),
            pltpu.VMEM((2, 2, piece, hidden), BF16), pltpu.VMEM((2, 2, piece, hidden), BF16),
            pltpu.VMEM((2, piece, hidden), BF16), pltpu.VMEM((2, piece, hidden), BF16),
            pltpu.VMEM((4, piece, model), BF16),
            pltpu.SemaphoreType.DMA((3,)), pltpu.SemaphoreType.DMA((20,)), pltpu.SemaphoreType.DMA((20,)),
        ],
        compiler_params=params(collective_id=4, has_side_effects=True),
        cost_estimate=pl.CostEstimate(
            flops=24 * quarter * slab * model * 1152, bytes_accessed=30_000_000, transcendentals=0),
        name="back",
    )(lens, d_own, d_peer, normed, qkv_far, mixed_far, qkv_own, mixed_own, wq, wo, wf,
      fin_img, fin_txt, up_keep, up_send, down_sum)


V_ROWS, V_MP, V_HEADS, V_FAR = 24, 11, 13, 15


def finish_kernel(dims, n_keep, n_send, dattended, states_img, states_txt, vec, fin_img, fin_txt,
                  near_img, near_txt, grad_pair, grad_single, grad_far, up_one, own_sums, up_sums, cols_own, cols_far,
                  core_img, core_txt, across_img, across_txt, back_img, back_txt, grad_out, v_out, up_out,
                  n_recv, s_img, s_txt, d_img, d_txt, rows, xr, zs, z_in, z_pass, z_last, f_in, f_pass, f_last, u_in, u_pass, u_last, far_sum, far_recv, vs, vr,
                  local_sem, send_sem, recv_sem):
    quarter = dims.quarter
    here = Place()
    z, x, m = here.z, here.x, here.m
    near_quarter = here.quarter(1, 0)
    used = [0]

    def send(src, dst, device):
        at = used[0]
        used[0] += 1
        return remote(src, dst, send_sem, recv_sem, at, device)

    loaded = [pltpu.make_async_copy(states_img.at[pl.ds(m * quarter, quarter)], s_img, local_sem.at[0]),
              pltpu.make_async_copy(states_txt.at[pl.ds(m * quarter, quarter)], s_txt, local_sem.at[1])]
    for copy in loaded:
        copy.start()
    meet([here.core, here.near, here.side, here.paired, here.opposite])

    n_copies = [send(n_send.at[p], n_recv.at[p], here.core) for p in range(quarter)]
    for copy in n_copies:
        copy.start()
    piece = xr.shape[1]
    wide = grad_pair.shape[1]
    spans = ((grad_pair, 0, wide), (grad_single, wide, xr.shape[2]))
    block = lambda j: pl.ds(pl.multiple_of(j * piece, piece), piece)
    x_copies = []
    for j in range(4):
        for src, lo, hi in spans:
            x_copies.append(send(src.at[block(2 * j + 1 - x)], xr.at[j, :, pl.ds(lo, hi - lo)], here.side))
            x_copies[-1].start()
    add = lambda *parts: functools.reduce(lambda p, q: p + q, [v.astype(F32) for v in parts])
    in_pair = lambda src, dst: [send(src.at[here.z_pair], dst.at[0], here.paired),
                                send(src.at[here.z_rest], dst.at[1], here.paired)]
    far_copies = in_pair(grad_far, f_in)
    up_copies = in_pair(up_one, u_in)
    for copy in far_copies + up_copies:
        copy.start()

    fin_remote = [send(src, dst, here.core) for src, dst in (
        (fin_img, core_img), (fin_txt, core_txt), (near_img, across_img), (near_txt, across_txt))]

    rows[...] = jnp.zeros_like(rows)
    for copy in loaded:
        copy.wait()
    total = [jnp.zeros((1, rows.shape[1]), F32)] * 2
    back_local, to_near, to_other = [], [], []
    for p in range(quarter):
        load_rows(dims, p, s_img, s_txt, rows)
        n, r = normalise(rows[...])
        n_copies[p].wait_recv()
        dy = n_keep[p].astype(F32) + n_recv[p].astype(F32)
        total[0] = total[0] + jnp.sum(dy * n, axis=0, keepdims=True)
        total[1] = total[1] + jnp.sum(dy, axis=0, keepdims=True)
        d = dattended[p] + norm_back(n, r, dy * vector(vec, GAIN1))
        d_img[p] = d[0:dims.patches].astype(BF16)
        d_txt[p] = d[dims.ip:dims.ip + dims.caption].astype(BF16)
        for j, (src, dst) in enumerate(((d_img, back_img), (d_txt, back_txt))):
            at = dst.at[m * quarter + p]
            to_near.append(send(src.at[p], at, here.near))
            to_near[-1].start()
            to_other.append(send(src.at[p], at, here.core))
            to_other[-1].start()
            back_local.append(pltpu.make_async_copy(src.at[p], at, local_sem.at[2 + 2 * p + j]))
            back_local[-1].start()
    for copy in fin_remote:
        copy.start()

    at = lax.broadcasted_iota(jnp.int32, (V_ROWS, 1), 0)
    two, one_head = parts_of(dims)
    vs[0] = jnp.zeros(vs.shape[1:], F32)
    vs[0, 0:1, :] = total[0]
    vs[0, 1:2, :] = total[1]
    vs[0, 2:V_MP, :] = own_sums[0:V_MP - 2, :]
    vs[0, V_MP:V_HEADS, :] = up_sums[...]
    for j in range(2):
        own_at, far_at = 2 * j * two, 4 * j * two
        vs[0, V_HEADS + j:V_HEADS + j + 1, 0:two] = cols_own[0:1, own_at:own_at + two]
        vs[0, V_HEADS + j:V_HEADS + j + 1, two:two + one_head] = cols_far[0:1, far_at + two:far_at + two + one_head]
        vs[0, V_FAR + j:V_FAR + j + 1, 0:two] = cols_far[0:1, far_at:far_at + two]
        vs[0, V_FAR + j:V_FAR + j + 1, two:two + one_head] = cols_far[0:1, far_at + two + one_head:far_at + 2 * two]
    v = vs[0]
    v_copies = []

    def exchange(step, value, device):
        vs[step] = value
        copy = send(vs.at[step], vr.at[step], device)
        copy.start()
        copy.wait_recv()
        v_copies.append(copy)
        return vr[step]

    v = v + jnp.where(at < V_MP, exchange(0, v, here.core), 0.0)
    for copy in far_copies:
        copy.wait_recv()
    f_pass[...] = add(grad_far[here.z_far], f_in[1]).astype(BF16)
    far_copies.append(send(f_pass, f_last, here.opposite))
    far_copies[-1].start()
    v = v + exchange(1, v, here.side)
    for copy in up_copies:
        copy.wait_recv()
    u_pass[...] = add(up_one[here.z_far], u_in[1]).astype(BF16)
    v = v + exchange(2, v, here.paired)
    vs[3] = v
    v_far = send(vs.at[3], vr.at[3], here.opposite)
    v_far.start()
    up_copies.append(send(u_pass, u_last, here.opposite))
    up_copies[-1].start()

    def own_sum(j, k):
        src, lo, hi = spans[k]
        return src[block(2 * j + x), :].astype(F32) + xr[j, :, lo:hi].astype(F32)

    for copy in x_copies:
        copy.wait_recv()
    for j in range(4):
        for k, (src, lo, hi) in enumerate(spans):
            zs[j, :, lo:hi] = own_sum(j, k).astype(BF16)
    z_copies = in_pair(zs, z_in)
    for copy in z_copies:
        copy.start()

    far_copies[-1].wait_recv()
    far_sum[...] = add(grad_far[z], f_in[0], f_last[...]).astype(BF16)
    far_copy = send(far_sum, far_recv, here.near)
    far_copy.start()
    v_far.wait_recv()
    v = v + vr[3]
    up_copies[-1].wait_recv()
    up_out[...] = add(up_one[z], u_in[0], u_last[...])
    for copy in z_copies:
        copy.wait_recv()
    z_pass[...] = add(zs[here.z_far], z_in[1]).astype(BF16)
    z_copies.append(send(z_pass, z_last, here.opposite))
    z_copies[-1].start()
    vs[4] = v
    v_near = send(vs.at[4], vr.at[4], here.near)
    v_near.start()
    for copy in back_local:
        copy.wait()
    onward = []
    for p in range(quarter):
        for j, dst in enumerate((back_img, back_txt)):
            to_near[2 * p + j].wait_recv()
            at_near = dst.at[near_quarter * quarter + p]
            onward.append(send(at_near, at_near, here.core))
            onward[-1].start()
    far_copy.wait_recv()
    z_copies[-1].wait_recv()
    for k, (src, lo, hi) in enumerate(spans):
        grad_out[:, lo:hi] = own_sum(z, k) + add(
            far_recv[:, lo:hi], z_in[0, :, lo:hi], z_last[:, lo:hi])
    v_near.wait_recv()
    there = vr[4]
    v_out[...] = v + jnp.where(at < V_MP, there, 0.0)
    v_out[V_HEADS:V_HEADS + 2, :] = v[V_HEADS:V_HEADS + 2, :] + there[V_FAR:V_FAR + 2, :]
    for copy in to_other + fin_remote + onward:
        copy.wait()
    for copy in n_copies + x_copies + far_copies + to_near + z_copies + v_copies + up_copies + [far_copy, v_near, v_far]:
        copy.wait_send()


def finish(dims, n_keep, n_send, dattended, states_img, states_txt, vec, fin_img, fin_txt,
           near_img, near_txt, grad_pair, grad_single, grad_far, up_one, *tables):
    pairs, patches, model = states_img.shape
    caption = states_txt.shape[1]
    quarter, slab = dims.quarter, dims.slab
    piece, cols = grad_far.shape[1:]
    held = pl.BlockSpec(memory_space=pltpu.VMEM)
    away = pl.BlockSpec(memory_space=pl.ANY)
    n_remote = 7 * quarter + 28
    return pl.pallas_call(
        functools.partial(finish_kernel, dims),
        in_specs=[held, away, held] + [away] * 2 + [held] + [away] * 4 + [held] * 8,
        out_specs=[away] * 6 + [held] * 3,
        out_shape=[jax.ShapeDtypeStruct(v.shape, BF16) for v in (fin_img, fin_txt) * 2] + [
            jax.ShapeDtypeStruct((pairs, patches, model), BF16),
            jax.ShapeDtypeStruct((pairs, caption, model), BF16),
            jax.ShapeDtypeStruct((piece, cols), F32),
            jax.ShapeDtypeStruct((V_ROWS, model), F32),
            jax.ShapeDtypeStruct(up_one.shape[1:], F32),
        ],
        scratch_shapes=[
            pltpu.VMEM((quarter, slab, model), BF16),
            pltpu.VMEM((quarter, patches, model), BF16),
            pltpu.VMEM((quarter, caption, model), BF16),
            pltpu.VMEM((quarter, patches, model), BF16),
            pltpu.VMEM((quarter, caption, model), BF16),
            pltpu.VMEM((slab, model), F32),
            pltpu.VMEM((4, piece, cols), BF16), pltpu.VMEM((4, piece, cols), BF16),
        ] + [pltpu.VMEM((2, piece, cols), BF16), pltpu.VMEM((piece, cols), BF16), pltpu.VMEM((piece, cols), BF16)] * 2 + [
            pltpu.VMEM((2,) + up_one.shape[1:], BF16), pltpu.VMEM(up_one.shape[1:], BF16), pltpu.VMEM(up_one.shape[1:], BF16),
            pltpu.VMEM((piece, cols), BF16), pltpu.VMEM((piece, cols), BF16),
            pltpu.VMEM((5, V_ROWS, model), F32),
            pltpu.VMEM((5, V_ROWS, model), F32),
            pltpu.SemaphoreType.DMA((2 + 2 * quarter,)),
            pltpu.SemaphoreType.DMA((n_remote,)),
            pltpu.SemaphoreType.DMA((n_remote,)),
        ],
        compiler_params=params(collective_id=1, has_side_effects=True),
        name="finish",
    )(n_keep, n_send, dattended, states_img, states_txt, vec, fin_img, fin_txt,
      near_img, near_txt, grad_pair, grad_single, grad_far, up_one, *tables)


def spread_kernel(dims, cols, sums, grad, gains, shifts, up_low, up_high, down, head_in, dproj, *refs):
    forward, refs = refs[:8], refs[8:]
    back_img, back_txt, *refs = refs
    outs, refs = refs[:12], refs[12:]
    (qkv, out_w, up_out, down_out, head_out, out_img, out_txt, grad_img, grad_txt,
     turned, held_img, held_txt, in_sem, out_sem) = refs
    here = Place()
    quarter = dims.quarter
    whose = [here.quarter(0, 0), here.quarter(1, 0), here.quarter(0, 1), here.quarter(1, 1)]
    place = lambda q: pl.ds(q * quarter, quarter)
    comes, goes = [], []
    for r in range(4):
        for j, (held, src, dst, back, to) in enumerate((
            (held_img, forward[2 * r], out_img, back_img, grad_img), (held_txt, forward[2 * r + 1], out_txt, back_txt, grad_txt),
        )):
            for k, (source, target, q) in enumerate(((src, dst, whose[r]), (back.at[place(r)], to, r))):
                at = 4 * r + 2 * j + k
                comes.append(pltpu.make_async_copy(source, held.at[2 * r + k], in_sem.at[at]))
                goes.append(pltpu.make_async_copy(held.at[2 * r + k], target.at[place(q)], out_sem.at[at]))
    for copy in comes:
        copy.start()
    turn_by = sums.shape[1] - here.b * cols

    def slice_of(value):
        return pltpu.roll(value, turn_by, 1)[:, 0:cols]

    mine = slice_of(sums[...])
    for out, (lo, count) in zip(outs[:8], ((0, 1), (1, 1), (7, 1), (6, 1), (2, 2), (4, 2), (9, 2), (8, 1))):
        out[...] = mine[lo:lo + count, :]
    wide = jnp.concatenate([gains[...], shifts[...], jnp.zeros((4, sums.shape[1]), F32)], axis=0)
    heads = slice_of(wide)
    outs[8][...] = heads[0:2, :]
    outs[9][...] = heads[2:4, :]
    outs[10][...] = sums[V_MP:V_MP + 2, :]
    outs[11][...] = sums[V_HEADS:V_HEADS + 2, 0:outs[11].shape[1]]
    two, one = 2 * HEAD_DIM, HEAD_DIM
    for t in range(3):
        qkv[t, :, 0:two] = grad[:, t * two:(t + 1) * two]
        qkv[t, :, two:two + one] = grad[:, 4 * two + t * one:4 * two + (t + 1) * one]
    turned[...] = jnp.zeros_like(turned)
    turned[0:cols, 0:two] = grad[:, 3 * two:4 * two]
    turned[0:cols, two:two + one] = grad[:, 4 * two + 3 * one:4 * two + 4 * one]
    out_w[...] = turned[...].T[0:two + one, 0:cols]
    up_out[0] = up_low[...]
    up_out[1] = up_high[...]
    down_out[...] = down[...]
    for come, go in zip(comes, goes):
        come.wait()
        go.start()
    for m in range(2):
        part = pltpu.roll(head_in[m].astype(F32), turn_by, 1)[:, 0:128].astype(BF16)
        head_out[m] = t_dot(part, dproj[m])[0:cols]
    for go in goes:
        go.wait()


def spread(dims, sums, grad, gains, shifts, up_low, up_high, down, head_in, dproj, forward, back_img, back_txt):
    cols, model = grad.shape[0], sums.shape[1]
    local, quarter = dims.local, dims.quarter
    assert cols <= 128
    shapes = [(1, cols)] * 4 + [(2, cols)] * 3 + [(1, cols)] + [(2, cols)] * 2 + [(2, model), (2, local)]
    shapes += [(3, cols, local), (local, cols), (2,) + up_low.shape, down.shape, (2, cols, dproj.shape[2])]
    held = pl.BlockSpec(memory_space=pltpu.VMEM)
    away = pl.BlockSpec(memory_space=pl.ANY)
    args = (sums, grad, gains, shifts, up_low, up_high, down, head_in, dproj)
    return pl.pallas_call(
        functools.partial(spread_kernel, dims, cols),
        in_specs=[held] * len(args) + [away] * 10,
        out_specs=[held] * len(shapes) + [away] * 4,
        out_shape=[jax.ShapeDtypeStruct(v, F32) for v in shapes]
        + [jax.ShapeDtypeStruct(v.shape, BF16) for v in (back_img, back_txt) * 2],
        scratch_shapes=[
            pltpu.VMEM((128, 256), F32),
            pltpu.VMEM((8, quarter, dims.patches, model), BF16), pltpu.VMEM((8, quarter, dims.caption, model), BF16),
            pltpu.SemaphoreType.DMA((16,)), pltpu.SemaphoreType.DMA((16,)),
        ],
        compiler_params=params(),
        cost_estimate=pl.CostEstimate(flops=1_000_000, bytes_accessed=20_000_000, transcendentals=0),
        name="spread",
    )(*args, *forward, back_img, back_txt)


def per_device(
    image_states, text_states, caption_lengths, image_cotangent, text_cotangent,
    first_gain, first_shift, query_key_value, query_value_bias, output_weight, output_bias,
    attention_scale, expert_gain, expert_shift, expert_up, expert_up_bias, expert_down,
    expert_down_bias, feedforward_scale, head_gain, head_shift, head_weight, logit_scale,
):
    pairs, patches, model = image_states.shape
    caption = text_states.shape[1]
    local = query_key_value.shape[2]
    quarter = pairs // 4
    batch_size = lax.axis_size("batch")
    assert lax.axis_size("mp") == 4 and pairs == 4 * quarter and quarter <= 3
    assert batch_size & (batch_size - 1) == 0
    assert local == 3 * HEAD_DIM
    ip, tp = up16(patches), up16(caption)
    dims = Dims(patches, caption, ip, tp, ip + tp, quarter, local)
    me = lax.axis_index("mp")
    batch_at = lax.axis_index("batch")
    order = me ^ jnp.asarray(ORDER, jnp.int32)
    vectors = (first_gain, first_shift, attention_scale, output_bias, expert_gain, expert_shift,
               feedforward_scale, expert_down_bias, head_gain, head_shift)
    own_w = jnp.transpose(query_key_value, (1, 2, 0)).reshape(3 * local, model)
    one_kernel = batch_size == 8 and model // batch_size % 32 == 0 and expert_up.shape[2] == model
    if one_kernel:
        (vec, normed, qkv_own, mixed_own, qkv_far, mixed_far, wf, attended, attn, e_own, e_peer, cls_own, cls_peer) = front(
            dims, caption_lengths, image_states, text_states, vectors, query_value_bias, own_w, output_weight)
    else:
        vec = jnp.concatenate([v.reshape(-1, model) for v in vectors] + [jnp.zeros((1, model), F32)])
        wo = jnp.concatenate([own_w, output_weight])
        wf = to_y(wo)
        far_bias = to_y(query_value_bias)
        normed, qkv_own, rest, mixed_own = attend_own(
            dims, order, caption_lengths, image_states, text_states, vec, query_value_bias, wo)
        qkv_far, mixed_far, a_keep, a_send = attend_far(
            dims, order, caption_lengths, normed, rest, mixed_own, far_bias, wo, wf)
        a_recv = to_core(a_send)
        attended, attn, e_own, cls_own = residual(
            dims, order, a_keep, a_recv, image_states, text_states, vec)
        e_peer = to_core(e_own)
        cls_peer = to_core(cls_own)
    if one_kernel:
        (act, dup, ddn, dexp, d_own, d_near, up_sums, class_e, c_act, c_dup, c_ddn, dcls, head_in, dproj,
         grad_head_gain, grad_head_shift, scalars) = middle(
            dims, pairs * batch_size, image_cotangent, text_cotangent, e_own, e_peer, cls_own, cls_peer, vec,
            expert_up, expert_up_bias, expert_down, head_weight, logit_scale.reshape(1, 1))
        down_sum, up_keep, up_send, dattended, dattn, dattn_peer, fin_img, fin_txt, own_sums = turn(
            dims, image_cotangent, text_cotangent, e_peer, e_own, act, dup, ddn, class_e, c_act, c_dup, c_ddn,
            dexp, attended, attn, d_own, d_near, dcls, vec)
    else:
        class_part, class_e = class_forward(dims, cls_own, cls_peer, expert_up, expert_up_bias, expert_down)
        class_parts = from_others(class_part, "mp", 1, 4)

        act_a, dup_a, ddn_a, d_send3, d_keep1, x_send3, x_keep1, bias_a, cot_a = experts(
            dims, "experts_a", 1, order[jnp.asarray([3, 1])], e_peer, e_own, image_cotangent, text_cotangent,
            tie(vec, class_part), expert_up, expert_up_bias, expert_down)
        x_recv1 = to_core(x_send3)
        d_recv1 = to_core(d_send3)
        final_class = class_final(
            dims, order, cls_own, cls_peer, class_parts, tie(vec, bias_a))
        class_blocks = gather_batch(final_class[None])
        x_near = add_low(x_keep1, x_recv1)
        x_far = to_y(x_near)
        act_b, dup_b, ddn_b, d_send2, d_keep0, x_send2, x_keep0, bias_b, cot_b = experts(
            dims, "experts_b", 0, order[jnp.asarray([2, 0])], e_peer, e_own, image_cotangent, text_cotangent,
            tie(vec, final_class, x_near), expert_up, expert_up_bias, expert_down)
        x_recv0 = to_core(x_send2)
        d_recv0 = to_core(d_send2)

        head_in, dproj, dclass, grad_head_gain, grad_head_shift, scalars = (contrast if batch_size <= 8 else contrast_large)(
            dims, pairs * batch_size, batch_at.reshape(1), class_blocks, tie(vec, bias_b), head_weight,
             logit_scale.reshape(1, 1))
        c_act, c_dup, c_ddn, c_dexp, c_bias, dcls = class_back(
            dims, order, class_e, cot_a, cot_b, dclass, vec, expert_up, expert_up_bias, expert_down)
        extras = from_others(c_dexp, "mp", 1, 4)
        d_far = to_y(add_low(d_keep1, tie(d_recv1, c_dexp)))
        expert_grad = expert_grads(
            dims, e_peer, e_own, act_a, dup_a, ddn_a, act_b, dup_b, ddn_b, class_e, c_act, c_dup, c_ddn)
        expert_sum = lax.psum_scatter(expert_grad, "batch", scatter_dimension=1, tiled=True)

        dattended, dattn, sums_two = norm_two(
            dims, order, x_keep0, x_recv0, x_far, attended, a_keep, a_recv, image_cotangent, text_cotangent,
            dcls, extras, tie(vec, expert_grad))
        dattn_peer = to_core(dattn)
        fin_img, fin_txt, sums_fin = final_rows(
            dims, order, d_keep0, d_recv0, d_far, attended, image_cotangent, text_cotangent, dcls,
            tie(vec, sums_two))
        own_sums = jnp.concatenate([sums_two[:6], sums_fin[:3]])
        up_sums = bias_a + bias_b + c_bias
    contrast_loss = scalars[0, :1]
    grad_logit_scale = scalars[1, :1]
    if one_kernel:
        (n_keep, n_send, grad_o01, grad_o2, cols_far, cols_own, near_img, near_txt, far_sum, up_one, grad_down,
         up_low) = back(
            dims, caption_lengths, dattn, dattn_peer, normed, qkv_far, mixed_far, qkv_own, mixed_own,
            own_w, output_weight, wf, fin_img, fin_txt, up_keep, up_send, down_sum)
    else:
        n_keep, n_send, grad_far, grad_o2, cols_far = attend_back(
            dims, True, order, caption_lengths, dattn, dattn_peer, normed, qkv_far, mixed_far, own_w, output_weight, wf)
        n_keep, n_send, grad_o01, cols_own = attend_back(
            dims, False, order, caption_lengths, dattn, dattn_peer, normed, qkv_own, mixed_own, own_w, output_weight, wf,
            prior=(n_keep, n_send))
    cols = model // batch_size
    mine = lambda v, axis: lax.dynamic_slice_in_dim(v, batch_at * cols, cols, axis=axis)
    pair, single = 2 * HEAD_DIM, HEAD_DIM
    if one_kernel:
        core_img, core_txt, across_img, across_txt, back_img, back_txt, attn_grad, sums, up_high = finish(
            dims, n_keep, n_send, dattended, image_states, text_states, vec, fin_img, fin_txt,
            near_img, near_txt, grad_o01, grad_o2, far_sum, up_one, own_sums, up_sums, cols_own, cols_far)
        forward = (fin_img, fin_txt, near_img, near_txt, core_img, core_txt, across_img, across_txt)
        (*vectors, grad_qkv, grad_output_weight, grad_up, grad_down, grad_head_weight,
         image_output, text_output, image_grad, text_grad) = spread(
            dims, sums, attn_grad, grad_head_gain, grad_head_shift, up_low, up_high, grad_down, head_in, dproj,
            forward, back_img, back_txt)
        flat = lambda v: v.reshape(-1)
        return (
            image_output,
            text_output,
            contrast_loss,
            image_grad,
            text_grad,
            flat(vectors[0]),
            flat(vectors[1]),
            jnp.transpose(grad_qkv, (1, 0, 2)),
            vectors[11],
            grad_output_weight,
            flat(vectors[2]),
            flat(vectors[3]),
            vectors[4],
            vectors[5],
            grad_up,
            vectors[10],
            jnp.transpose(grad_down, (0, 2, 1)),
            vectors[6],
            flat(vectors[7]),
            vectors[8],
            vectors[9],
            grad_head_weight,
            grad_logit_scale,
        )
    else:
        grad_head_weight = jnp.einsum("mnc,mne->mce", mine(head_in, 2), dproj, preferred_element_type=F32)
        grad_expert_up = expert_sum[:2].astype(F32)
        grad_expert_down = jnp.transpose(expert_sum[2:].astype(F32), (0, 2, 1))
        cols_own = cols_own.reshape(3, pair)[::2]
        cols_far = cols_far.reshape(3, 2 * pair)[::2]
        heads = jnp.concatenate([cols_own, cols_far[:, pair:pair + single]], axis=1)
        heads_far = jnp.concatenate([cols_far[:, :pair], cols_far[:, pair + single:]], axis=1)
        n_recv = to_core(n_send)
        d_img, d_txt, sums_one = norm_one(
            dims, order, n_keep, n_recv, dattended, image_states, text_states, vec)
        image_output = gather_rows(fin_img, me)
        text_output = gather_rows(fin_txt, me)
        image_grad = gather_rows(d_img, me)
        text_grad = gather_rows(d_txt, me)
        grad_own = jnp.concatenate([grad_o01, grad_o2], axis=1)
        grad_far = lax.psum_scatter(grad_far, "batch", scatter_dimension=0, tiled=True)
        grad_own = lax.psum_scatter(grad_own, "batch", scatter_dimension=0, tiled=True)
        attn_grad = grad_own.astype(F32) + to_y(grad_far).astype(F32)
        heads = heads + to_y(heads_far)
        own_sums = sum_over(jnp.concatenate([sums_one[:2], own_sums]), "mp")
        flat = jnp.concatenate([own_sums.reshape(-1), heads.reshape(-1), up_sums.reshape(-1)])
        count = flat.shape[0]
        flat = jnp.pad(flat, (0, -count % 1024)).reshape(-1, 128)
        flat = sum_over(flat, "batch").reshape(-1)[:count]
        done = own_sums.shape[0]
        own_sums = mine(flat[:done * model].reshape(done, model), 1)
        heads = flat[done * model:done * model + 2 * local].reshape(2, local)
        grad_expert_up_bias = flat[done * model + 2 * local:].reshape(up_sums.shape)
    attn_grad = jnp.concatenate(
        [attn_grad[:, :4 * pair].reshape(cols, 4, pair), attn_grad[:, 4 * pair:].reshape(cols, 4, single)], axis=2)
    grad_query_key_value = attn_grad[:, :3]
    grad_output_weight = jnp.transpose(attn_grad[:, 3])
    return (
        image_output,
        text_output,
        contrast_loss,
        image_grad,
        text_grad,
        own_sums[0],
        own_sums[1],
        grad_query_key_value,
        heads,
        grad_output_weight,
        own_sums[7],
        own_sums[6],
        own_sums[2:4],
        own_sums[4:6],
        grad_expert_up,
        grad_expert_up_bias,
        grad_expert_down,
        own_sums[9:11],
        own_sums[8],
        mine(grad_head_gain, 1),
        mine(grad_head_shift, 1),
        grad_head_weight,
        grad_logit_scale,
    )


def solution(mesh):
    return jax.shard_map(
        per_device,
        mesh=mesh,
        in_specs=(
            P("batch", None, None),
            P("batch", None, None),
            P("batch"),
            P("batch", None, None),
            P("batch", None, None),
            P(),
            P(),
            P(None, None, "mp"),
            P(None, "mp"),
            P("mp", None),
            P(),
            P(),
            P(),
            P(),
            P(None, None, "mp"),
            P(None, "mp"),
            P(None, "mp", None),
            P(),
            P(),
            P(),
            P(),
            P(),
            P(),
        ),
        out_specs=(
            P("batch", None, None),
            P("batch", None, None),
            P(),
            P("batch", None, None),
            P("batch", None, None),
            P("batch"),
            P("batch"),
            P("batch", None, "mp"),
            P(None, "mp"),
            P("mp", "batch"),
            P("batch"),
            P("batch"),
            P(None, "batch"),
            P(None, "batch"),
            P(None, "batch", "mp"),
            P(None, "mp"),
            P(None, "mp", "batch"),
            P(None, "batch"),
            P("batch"),
            P(None, "batch"),
            P(None, "batch"),
            P(None, "batch", None),
            P(),
        ),
        check_vma=False,
    )
```

```python
import functools
from typing import NamedTuple

import jax
import jax.numpy as jnp
from jax import lax
from jax.experimental import pallas as pl
from jax.experimental.pallas import tpu as pltpu
from jax.sharding import PartitionSpec as P

HEAD_DIM = 64
F32 = jnp.float32
BF16 = jnp.bfloat16
NEG = -1e9
EPS = 1e-5
ORDER = (0, 2, 1, 3)

VMEM_LIMIT = 60 * 1024 * 1024


def params(**kw):
    return pltpu.CompilerParams(vmem_limit_bytes=VMEM_LIMIT, **kw)


def up16(n):
    return -(-n // 16) * 16


def dot(a, b):
    return jnp.dot(a, b, preferred_element_type=F32)


def dot_t(a, b):
    return lax.dot_general(a, b, (((1,), (1,)), ((), ())), preferred_element_type=F32)


def t_dot(a, b):
    return lax.dot_general(a, b, (((0,), (0,)), ((), ())), preferred_element_type=F32)


def normalise(x):
    c = x - jnp.mean(x, axis=-1, keepdims=True)
    v = jnp.mean(c * c, axis=-1, keepdims=True)
    r = lax.rsqrt(v + EPS)
    return c * r, r


def norm_back(n, r, dn):
    a = jnp.mean(dn, axis=-1, keepdims=True)
    b = jnp.mean(dn * n, axis=-1, keepdims=True)
    return (dn - a - n * b) * r


def gelu_parts(u):
    big = 0.5 * (1.0 + lax.erf(u * 0.7071067811865476))
    small = 0.3989422804014327 * jnp.exp(-0.5 * u * u)
    return big, small


def gelu_low(u):
    return (u * (0.5 * (1.0 + lax.erf(u * 0.7071067811865476)))).astype(BF16)


def softmax_rows(scores):
    m = jnp.max(scores, axis=-1, keepdims=True)
    e = jnp.exp(scores - m)
    return e * (1.0 / jnp.sum(e, axis=-1, keepdims=True))


def tie(value, *after):
    return lax.optimization_barrier((value,) + after)[0]


def load_rows(dims, p, img, txt, rows):
    rows[0:dims.patches, :] = img[p].astype(F32)
    rows[dims.ip:dims.ip + dims.caption, :] = txt[p].astype(F32)


def spec_whole(a):
    return pl.BlockSpec(a.shape, lambda *_: (0,) * a.ndim)


class Dims(NamedTuple):
    patches: int
    caption: int
    ip: int
    tp: int
    slab: int
    quarter: int
    local: int


GAIN1, SHIFT1, A_SCALE, A_BIAS, GAIN2, SHIFT2, F_SCALE, F_BIAS, H_GAIN, H_SHIFT = 0, 1, 2, 3, 4, 6, 8, 9, 11, 13


def vector(table, at, count=1):
    return table[at:at + count, :]


def copy_rows(dst, at, src, start, count):
    dst[at:at + count, :] = src[start:start + count, :]


def parts_of(dims):
    return 2 * HEAD_DIM, HEAD_DIM


def key_tail(dims, length):
    at = dims.patches // 16 * 16
    return ((0, dims.ip, at, dims.patches), (dims.ip, dims.slab, 0, length))


def hide(scores, start, limit):
    if start >= scores.shape[0]:
        return scores
    tail = scores[start:]
    at = start + lax.broadcasted_iota(jnp.int32, (tail.shape[0], 1), 0)
    tail = jnp.where(at < limit, tail, NEG)
    return tail if start == 0 else jnp.concatenate([scores[:start], tail], axis=0)


def split_pair(value):
    low = lax.broadcasted_iota(jnp.int32, (1, 128), 1) < HEAD_DIM
    zero = jnp.zeros_like(value)
    return jnp.concatenate([jnp.where(low, value, zero), jnp.where(low, zero, value)], axis=0)


def join_pair(value):
    low = lax.broadcasted_iota(jnp.int32, (1, 128), 1) < HEAD_DIM
    half = value.shape[0] // 2
    return jnp.where(low, value[:half], value[half:])


def softmax_keys(scores):
    e = jnp.exp(scores - jnp.max(scores, axis=0, keepdims=True))
    return e * (1.0 / jnp.sum(e, axis=0, keepdims=True))


def pair_weights(q, k, start, limit):
    return softmax_keys(hide(dot_t(k, split_pair(q)), start, limit))


def scaled(q):
    return q * jnp.asarray(HEAD_DIM ** -0.5, BF16)


def attend_tiles(dims, lens, quarter_at, qkv, mixed):
    tiles = mixed.shape[-1] // 128

    def one_pair(p, c):
        length = lens[quarter_at * dims.quarter + p]
        for lo, hi, start, limit in key_tail(dims, length):
            for g in range(tiles):
                q, k, v = [qkv[p, lo:hi, (t * tiles + g) * 128:(t * tiles + g + 1) * 128] for t in range(3)]
                w = pair_weights(scaled(q), k, start, limit).astype(BF16)
                mixed[p, lo:hi, g * 128:(g + 1) * 128] = join_pair(t_dot(w, v)).astype(BF16)
        return c

    lax.fori_loop(0, dims.quarter, one_pair, 0)


def attend_own_kernel(dims, order, lens, img, txt, vec, bias, wo, normed, qkv, rest, mixed, rows, w, b):
    i = pl.program_id(0)
    local = dims.local
    two, one_head = parts_of(dims)

    @pl.when(i == 0)
    def _():
        rows[...] = jnp.zeros_like(rows)
        w[...] = jnp.zeros_like(w)
        b[...] = jnp.zeros_like(b)
        for t in range(3):
            copy_rows(w, t * 2 * two, wo, t * local, local)
        b[0:1, 0:local] = bias[0:1, :]
        b[0:1, 4 * two:4 * two + local] = bias[1:2, :]

    def one_norm(p, c):
        load_rows(dims, p, img, txt, rows)
        n, _ = normalise(rows[...])
        normed[p] = (n * vector(vec, GAIN1) + vector(vec, SHIFT1)).astype(BF16)
        return c

    lax.fori_loop(0, dims.quarter, one_norm, 0)
    model = normed.shape[-1]
    proj = (dot_t(normed[...].reshape(dims.quarter * dims.slab, model), w[...]) + b[0:1, :]).astype(BF16)
    proj = proj.reshape(dims.quarter, dims.slab, 6 * two)
    for t in range(3):
        qkv[:, :, t * two:(t + 1) * two] = proj[:, :, 2 * t * two:(2 * t + 1) * two]
        rest[:, :, t * two:(t + 1) * two] = proj[:, :, (2 * t + 1) * two:(2 * t + 2) * two]
    attend_tiles(dims, lens, order[i], qkv, mixed)


def attend_own(dims, order, lens, img, txt, vec, bias, wo):
    model = img.shape[-1]
    pairs = 4 * dims.quarter
    block = lambda cols: pl.BlockSpec((dims.quarter, dims.slab, cols), lambda i, o, n: (i, 0, 0))
    shape = lambda cols: jax.ShapeDtypeStruct((pairs, dims.slab, cols), BF16)
    return pl.pallas_call(
        functools.partial(attend_own_kernel, dims),
        grid_spec=pltpu.PrefetchScalarGridSpec(
            num_scalar_prefetch=2,
            grid=(4,),
            in_specs=[
                pl.BlockSpec((dims.quarter, dims.patches, model), lambda i, o, n: (o[i], 0, 0)),
                pl.BlockSpec((dims.quarter, dims.caption, model), lambda i, o, n: (o[i], 0, 0)),
                spec_whole(vec), spec_whole(bias), spec_whole(wo),
            ],
            out_specs=[block(model), block(384), block(384), block(128)],
            scratch_shapes=[pltpu.VMEM((dims.slab, model), F32), pltpu.VMEM((768, model), BF16),
                            pltpu.VMEM((8, 768), F32)],
        ),
        out_shape=[shape(model), shape(384), shape(384), shape(128)],
        compiler_params=params(),
        cost_estimate=pl.CostEstimate(
            flops=1536 * pairs * dims.slab * model, bytes_accessed=30_000_000, transcendentals=0),
        name="attend_own",
    )(order, lens, img, txt, vec, bias, wo)


def attend_far_kernel(dims, order, lens, normed, rest, own, bias, wo, wf, qkv, mixed, keep, send, w, ow, b):
    i = pl.program_id(0)
    local = dims.local
    two, one_head = parts_of(dims)
    count = dims.quarter * dims.slab
    model = normed.shape[-1]

    @pl.when(i == 0)
    def _():
        w[...] = jnp.zeros_like(w)
        b[...] = jnp.zeros_like(b)
        for t in range(3):
            copy_rows(w, t * 2 * two, wf, t * local, two)
            copy_rows(w, t * 2 * two + two + one_head, wf, t * local + two, one_head)
        for t, at in ((0, 0), (1, 4 * two)):
            b[0:1, at:at + two] = bias[t:t + 1, 0:two]
            b[0:1, at + two + one_head:at + 2 * two] = bias[t:t + 1, two:]
        copy_rows(ow, 0, wo, 3 * local, two)
        copy_rows(ow, two, wf, 3 * local, two)
        copy_rows(ow, 2 * two, wo, 3 * local + two, one_head)
        copy_rows(ow, 2 * two + one_head, wf, 3 * local + two, one_head)

    proj = (dot_t(normed[...].reshape(count, model), w[...]) + b[0:1, :]).astype(BF16)
    proj = proj.reshape(dims.quarter, dims.slab, 6 * two)
    for t in range(3):
        at = 2 * t * two
        qkv[:, :, at:at + two] = proj[:, :, at:at + two]
        qkv[:, :, at + two:at + 2 * two] = proj[:, :, at + two:at + 2 * two] + rest[:, :, t * two:(t + 1) * two]
    attend_tiles(dims, lens, order[(i + 2) % 4], qkv, mixed)
    part = dot(own[...].reshape(count, two), ow[0:two, :])
    part = part + dot(mixed[...].reshape(count, 2 * two), ow[two:, :])
    part = part.astype(BF16).reshape(dims.quarter, dims.slab, model)

    @pl.when(i < 2)
    def _():
        send[...] = part

    @pl.when(i >= 2)
    def _():
        keep[...] = part


def attend_far(dims, order, lens, normed, rest, own, bias, wo, wf):
    model = normed.shape[-1]
    pairs = 4 * dims.quarter
    at = lambda i: (i + 2) % 4
    block = lambda cols, f: pl.BlockSpec((dims.quarter, dims.slab, cols), lambda i, o, n: (f(i), 0, 0))
    shape = lambda count, cols: jax.ShapeDtypeStruct((count, dims.slab, cols), BF16)
    return pl.pallas_call(
        functools.partial(attend_far_kernel, dims),
        grid_spec=pltpu.PrefetchScalarGridSpec(
            num_scalar_prefetch=2,
            grid=(4,),
            in_specs=[
                block(model, at), block(384, at), block(128, at),
                spec_whole(bias), spec_whole(wo), spec_whole(wf),
            ],
            out_specs=[
                block(768, at), block(256, at),
                block(model, lambda i: jnp.maximum(i - 2, 0)), block(model, lambda i: jnp.minimum(i, 1)),
            ],
            scratch_shapes=[pltpu.VMEM((768, model), BF16), pltpu.VMEM((384, model), BF16),
                            pltpu.VMEM((8, 768), F32)],
        ),
        out_shape=[
            shape(pairs, 768), shape(pairs, 256),
            shape(2 * dims.quarter, model), shape(2 * dims.quarter, model),
        ],
        compiler_params=params(),
        cost_estimate=pl.CostEstimate(
            flops=2304 * pairs * dims.slab * model, bytes_accessed=30_000_000, transcendentals=0),
        name="attend_far",
    )(order, lens, normed, rest, own, bias, wo, wf)


def residual_kernel(dims, order, keep, recv, img, txt, vec, attended, attn, expert, cls, rows):
    i = pl.program_id(0)
    ip = dims.ip

    @pl.when(i == 0)
    def _():
        rows[...] = jnp.zeros_like(rows)
        cls[...] = jnp.zeros_like(cls)

    load_rows(dims, 0, img, txt, rows)
    a = keep[0].astype(F32) + recv[0].astype(F32)
    x = rows[...] + vector(vec, A_SCALE) * (a + vector(vec, A_BIAS))
    n, _ = normalise(x)
    e_img = n[0:ip] * vector(vec, GAIN2) + vector(vec, SHIFT2)
    e_txt = n[ip:] * vector(vec, GAIN2 + 1) + vector(vec, SHIFT2 + 1)
    expert[0, 0:ip, :] = e_img.astype(BF16)
    expert[0, ip:, :] = e_txt.astype(BF16)
    for j, v in enumerate((x[0:1], x[ip:ip + 1], e_img[0:1], e_txt[0:1])):
        cls[j, pl.ds(i, 1), :] = v

    @pl.when(i < dims.quarter)
    def _():
        attended[0] = x
        attn[0] = a


def residual(dims, order, keep, recv, img, txt, vec):
    model = img.shape[-1]
    quarter = dims.quarter
    block = pl.BlockSpec((1, dims.slab, model), lambda i, o: (i, 0, 0))
    pair = lambda i, o: (o[i // quarter] * quarter + i % quarter, 0, 0)
    return pl.pallas_call(
        functools.partial(residual_kernel, dims),
        grid_spec=pltpu.PrefetchScalarGridSpec(
            num_scalar_prefetch=1,
            grid=(2 * quarter,),
            in_specs=[
                block, block,
                pl.BlockSpec((1, dims.patches, model), pair),
                pl.BlockSpec((1, dims.caption, model), pair),
                spec_whole(vec),
            ],
            out_specs=[
                pl.BlockSpec((1, dims.slab, model), lambda i, o: (jnp.minimum(i, quarter - 1), 0, 0)),
                pl.BlockSpec((1, dims.slab, model), lambda i, o: (jnp.minimum(i, quarter - 1), 0, 0)),
                block,
                pl.BlockSpec((4, 8, model), lambda i, o: (0, 0, 0)),
            ],
            scratch_shapes=[pltpu.VMEM((dims.slab, model), F32)],
        ),
        out_shape=[
            jax.ShapeDtypeStruct((quarter, dims.slab, model), F32),
            jax.ShapeDtypeStruct((quarter, dims.slab, model), F32),
            jax.ShapeDtypeStruct((2 * quarter, dims.slab, model), BF16),
            jax.ShapeDtypeStruct((4, 8, model), F32),
        ],
        compiler_params=params(),
        cost_estimate=pl.CostEstimate(flops=40_000_000, bytes_accessed=20_000_000, transcendentals=0),
        name="residual",
    )(order, keep, recv, img, txt, vec)


def expert_kernel(dims, seq, peer, own, img, txt, vec, up, up_bias, down,
                  act, dup, ddown, d_send, d_keep, x_send, x_keep, bias_grad, cot, ins, rows):
    ip, slab, quarter = dims.ip, dims.slab, dims.quarter
    i = pl.program_id(0)
    model = own.shape[-1]

    @pl.when(i == 0)
    def _():
        rows[...] = jnp.zeros_like(rows)
        bias_grad[...] = jnp.zeros_like(bias_grad)
        cot[...] = jnp.zeros_like(cot)
        ins[...] = peer[...]

    @pl.when(i == 1)
    def _():
        ins[...] = own[...]

    at = lax.broadcasted_iota(jnp.int32, (slab, 1), 0)
    inner = (at != 0) & (at != ip)

    def one(p, c):
        load_rows(dims, p, img, txt, rows)
        cot[0, pl.ds(8 * i + p, 1), :] = rows[0:1, :]
        cot[1, pl.ds(8 * i + p, 1), :] = rows[ip:ip + 1, :]
        ddown[p] = jnp.where(inner, rows[...] * vector(vec, F_SCALE), 0.0).astype(BF16)
        return c

    lax.fori_loop(0, quarter, one, 0)
    for m, lo, hi in ((0, 0, ip), (1, ip, slab)):
        count = quarter * (hi - lo)
        e = ins[:, lo:hi, :].reshape(count, model)
        u = dot(e, up[m]) + up_bias[m:m + 1]
        big, small = gelu_parts(u)
        a = (u * big).astype(BF16)
        act[:, lo:hi, :] = a.reshape(quarter, hi - lo, -1)
        slope = big + u * small
        d = dot(a, down[m]).astype(BF16).reshape(quarter, hi - lo, model)
        g = ddown[:, lo:hi, :].reshape(count, model)
        du = dot_t(g, down[m]) * slope
        bias_grad[m:m + 1, :] += jnp.sum(du, axis=0, keepdims=True)
        low = du.astype(BF16)
        dup[:, lo:hi, :] = low.reshape(quarter, hi - lo, -1)
        x = dot_t(low, up[m]).astype(BF16).reshape(quarter, hi - lo, model)

        @pl.when(i == 0)
        def _():
            d_send[:, lo:hi, :] = d
            x_send[:, lo:hi, :] = x

        @pl.when(i == 1)
        def _():
            d_keep[:, lo:hi, :] = d
            x_keep[:, lo:hi, :] = x


def experts(dims, name, half, seq, peer, own, img, txt, vec, up, up_bias, down):
    model = own.shape[-1]
    hidden = up.shape[-1]
    slab, quarter = dims.slab, dims.quarter
    fixed = pl.BlockSpec((quarter, slab, model), lambda i, o: (half, 0, 0))
    first = pl.BlockSpec((quarter, slab, model), lambda i, o: (0, 0, 0))
    step = lambda cols: pl.BlockSpec((quarter, slab, cols), lambda i, o: (i, 0, 0))
    shape = lambda n, cols: jax.ShapeDtypeStruct((n * quarter, slab, cols), BF16)
    return pl.pallas_call(
        functools.partial(expert_kernel, dims),
        grid_spec=pltpu.PrefetchScalarGridSpec(
            num_scalar_prefetch=1,
            grid=(2,),
            in_specs=[
                fixed, fixed,
                pl.BlockSpec((quarter, dims.patches, model), lambda i, o: (o[i], 0, 0)),
                pl.BlockSpec((quarter, dims.caption, model), lambda i, o: (o[i], 0, 0)),
                spec_whole(vec), spec_whole(up), spec_whole(up_bias), spec_whole(down),
            ],
            out_specs=[
                step(hidden), step(hidden), step(model),
                first, first, first, first,
                pl.BlockSpec((2, hidden), lambda i, o: (0, 0)),
                pl.BlockSpec((2, 16, model), lambda i, o: (0, 0, 0)),
            ],
            scratch_shapes=[pltpu.VMEM((quarter, slab, model), BF16), pltpu.VMEM((slab, model), F32)],
        ),
        out_shape=[
            shape(2, hidden), shape(2, hidden), shape(2, model),
            shape(1, model), shape(1, model), shape(1, model), shape(1, model),
            jax.ShapeDtypeStruct((2, hidden), F32),
            jax.ShapeDtypeStruct((2, 16, model), F32),
        ],
        compiler_params=params(),
        cost_estimate=pl.CostEstimate(
            flops=16 * quarter * slab * model * hidden, bytes_accessed=20_000_000, transcendentals=0),
        name=name,
    )(seq, peer, own, img, txt, vec, up, up_bias, down)


def expert_grads_kernel(dims, peer, own, act_a, dup_a, ddn_a, act_b, dup_b, ddn_b, ce, ca, cu, cd, out, acc):
    i = pl.program_id(0)

    def add(e, dup, ddn, act):
        for m, lo, hi in ((0, 0, dims.ip), (1, dims.ip, dims.slab)):
            count = dims.quarter * (hi - lo)
            flat = lambda ref: ref[:, lo:hi, :].reshape(count, -1)
            acc[m] += t_dot(flat(e), flat(dup))
            acc[2 + m] += t_dot(flat(ddn), flat(act))

    @pl.when(i == 0)
    def _():
        for m in range(2):
            acc[m] = t_dot(ce[m], cu[m])
            acc[2 + m] = t_dot(cd[m], ca[m])

    for j, refs in enumerate((
        (peer, dup_a, ddn_a, act_a), (own, dup_a, ddn_a, act_a),
        (peer, dup_b, ddn_b, act_b), (own, dup_b, ddn_b, act_b),
    )):
        @pl.when(i == j)
        def _():
            add(*refs)

    @pl.when(i == 3)
    def _():
        out[...] = acc[...].astype(BF16)


def expert_grads(dims, peer, own, act_a, dup_a, ddn_a, act_b, dup_b, ddn_b, ce, ca, cu, cd):
    model = own.shape[-1]
    hidden = act_a.shape[-1]
    slab, quarter = dims.slab, dims.quarter
    assert hidden == model
    half = pl.BlockSpec((quarter, slab, model), lambda i: (jnp.where(i < 2, 1, 0), 0, 0))
    first = pl.BlockSpec((quarter, slab, hidden), lambda i: (jnp.minimum(i, 1), 0, 0))
    last = pl.BlockSpec((quarter, slab, hidden), lambda i: (jnp.maximum(i - 2, 0), 0, 0))
    return pl.pallas_call(
        functools.partial(expert_grads_kernel, dims),
        grid=(4,),
        in_specs=[half, half, first, first, first, last, last, last] + [spec_whole(v) for v in (ce, ca, cu, cd)],
        out_specs=pl.BlockSpec((4, model, hidden), lambda i: (0, 0, 0)),
        scratch_shapes=[pltpu.VMEM((4, model, hidden), F32)],
        out_shape=jax.ShapeDtypeStruct((4, model, hidden), BF16),
        compiler_params=params(),
        cost_estimate=pl.CostEstimate(
            flops=16 * quarter * slab * model * hidden, bytes_accessed=40_000_000, transcendentals=0),
        name="expert_grads",
    )(peer, own, act_a, dup_a, ddn_a, act_b, dup_b, ddn_b, ce, ca, cu, cd)


def own_row(dims, r, p):
    return 8 * (r // 2) + dims.quarter * (r % 2) + p


def class_forward_kernel(dims, near, far, up, up_bias, down, out, rows):
    for m in range(2):
        e = jnp.concatenate([near[2 + m], far[2 + m]], axis=0).astype(BF16)
        rows[m] = e
        u = dot(e, up[m]) + up_bias[m:m + 1]
        out[m] = dot(gelu_low(u), down[m])


def class_forward(dims, near, far, up, up_bias, down):
    shape = (2, 16, near.shape[-1])
    return pl.pallas_call(
        functools.partial(class_forward_kernel, dims),
        out_shape=[jax.ShapeDtypeStruct(shape, F32), jax.ShapeDtypeStruct(shape, BF16)],
        compiler_params=params(),
        cost_estimate=pl.CostEstimate(flops=200_000_000, bytes_accessed=5_000_000, transcendentals=0),
        name="class_forward",
    )(near, far, up, up_bias, down)


def class_final_kernel(dims, order, near, far, d0, d1, d2, d3, vec, out):
    q = dims.quarter
    for m in range(2):
        out[m] = jnp.zeros(out.shape[1:], F32)
        for r in range(4):
            half, at = (near, far)[r // 2], q * (r % 2)
            for p in range(q):
                rows = [d[m, own_row(dims, s, p):own_row(dims, s, p) + 1, :]
                        for d, s in ((d0, r), (d1, r ^ 2), (d2, r ^ 1), (d3, r ^ 3))]
                total = (rows[0] + rows[1]) + (rows[2] + rows[3])
                x = half[m, at + p:at + p + 1, :] + vector(vec, F_SCALE) * (total + vector(vec, F_BIAS + m))
                out[m, pl.ds(4 * order[r] + p, 1), :] = x


def class_final(dims, order, near, far, parts, vec):
    shape = (2, 16, near.shape[-1])
    args = (near, far) + tuple(parts) + (vec,)
    return pl.pallas_call(
        functools.partial(class_final_kernel, dims),
        grid_spec=pltpu.PrefetchScalarGridSpec(
            num_scalar_prefetch=1, grid=(1,),
            in_specs=[spec_whole(v) for v in args],
            out_specs=pl.BlockSpec(shape, lambda i, o: (0, 0, 0)),
        ),
        out_shape=jax.ShapeDtypeStruct(shape, F32),
        compiler_params=params(),
        cost_estimate=pl.CostEstimate(flops=1_000_000, bytes_accessed=1_000_000, transcendentals=0),
        name="class_final",
    )(order, *args)


def class_back_kernel(dims, order, e, cot_a, cot_b, dclass, vec, up, up_bias, down,
                      act, dup, ddown, dexp, bias_grad, dcls, rows):
    q = dims.quarter
    rows[...] = jnp.zeros_like(rows)
    dcls[...] = jnp.zeros_like(dcls)
    for m in range(2):
        for r in range(4):
            cot, base = (cot_b, cot_a)[r % 2], 8 * (1 - r // 2)
            for p in range(q):
                d = dclass[m, pl.ds(4 * order[r] + p, 1), :]
                at = own_row(dims, r, p)
                rows[m, at:at + 1, :] = cot[m, base + p:base + p + 1, :] + d
                if r == 0:
                    dcls[p, m:m + 1, :] = d
        u = dot(e[m], up[m]) + up_bias[m:m + 1]
        big, small = gelu_parts(u)
        act[m] = (u * big).astype(BF16)
        g = (rows[m] * vector(vec, F_SCALE)).astype(BF16)
        ddown[m] = g
        du = dot_t(g, down[m]) * (big + u * small)
        bias_grad[m:m + 1, :] = jnp.sum(du, axis=0, keepdims=True)
        low = du.astype(BF16)
        dup[m] = low
        dexp[m] = dot_t(low, up[m])


def class_back(dims, order, e, cot_a, cot_b, dclass, vec, up, up_bias, down):
    hidden, model = up.shape[-1], e.shape[-1]
    args = (e, cot_a, cot_b, dclass, vec, up, up_bias, down)
    shapes = [((2, 16, hidden), BF16), ((2, 16, hidden), BF16), ((2, 16, model), BF16), ((2, 16, model), F32),
              ((2, hidden), F32), ((dims.quarter, 8, model), F32)]
    return pl.pallas_call(
        functools.partial(class_back_kernel, dims),
        grid_spec=pltpu.PrefetchScalarGridSpec(
            num_scalar_prefetch=1, grid=(1,),
            in_specs=[spec_whole(v) for v in args],
            out_specs=[pl.BlockSpec(s, lambda i, o, n=len(s): (0,) * n) for s, _ in shapes],
            scratch_shapes=[pltpu.VMEM((2, 16, model), F32)],
        ),
        out_shape=[jax.ShapeDtypeStruct(s, t) for s, t in shapes],
        compiler_params=params(),
        cost_estimate=pl.CostEstimate(flops=300_000_000, bytes_accessed=5_000_000, transcendentals=0),
        name="class_back",
    )(order, *args)


def contrast_kernel(dims, total, at, blocks, vec, weight, scale,
                    head_in, dproj, dcls, gains, shifts, scalars, cls, back):
    me = at[0]
    span = blocks[0].shape[0]
    for k, block in enumerate(blocks):
        for j in range(span):
            for m in range(2):
                cls[m, pl.ds(pl.multiple_of(16 * (me ^ (k * span + j)), 16), 16), :] = block[j, m]
    n_rows = cls.shape[1]
    sharp = jnp.exp(scale[...])
    col_at = lax.broadcasted_iota(jnp.int32, (1, n_rows), 1)
    row_at = lax.broadcasted_iota(jnp.int32, (n_rows, 1), 0)
    col_ok = (col_at % 4) < dims.quarter
    row_ok = (row_at % 4) < dims.quarter
    normal, inverse, proj, unit, embed = [], [], [], [], []
    for m in range(2):
        n, r = normalise(cls[m])
        h = (n * vector(vec, H_GAIN + m) + vector(vec, H_SHIFT + m)).astype(BF16)
        head_in[m] = h
        y = dot(h, weight[m])
        u = lax.rsqrt(jnp.sum(y * y, axis=-1, keepdims=True) + 1e-6)
        normal.append(n)
        inverse.append(r)
        proj.append(y)
        unit.append(u)
        embed.append((y * u).astype(BF16))
    ok = row_ok & col_ok
    logits = sharp * dot_t(embed[0], embed[1])
    masked = jnp.where(ok, logits, -1e30)
    row_max = jnp.max(masked, axis=1, keepdims=True)
    row_lse = row_max + jnp.log(jnp.sum(jnp.exp(masked - row_max), axis=1, keepdims=True))
    col_max = jnp.max(masked, axis=0, keepdims=True)
    col_lse = col_max + jnp.log(jnp.sum(jnp.exp(masked - col_max), axis=0, keepdims=True))
    same = (row_at == col_at) & ok
    both = jnp.exp(masked - row_lse) + jnp.exp(masked - col_lse)
    dlogits = jnp.where(ok, jnp.where(same, both - 2.0, both) * (1.0 / (2 * total)), 0.0)
    diagonal = jnp.sum(jnp.where(same, logits, 0.0), axis=1, keepdims=True)
    rows = jnp.where(row_ok, row_lse - 2.0 * diagonal, 0.0)
    cols = jnp.where(col_ok, col_lse, 0.0)
    loss = (jnp.sum(rows, axis=0, keepdims=True) + jnp.sum(cols, axis=1, keepdims=True)) * (1.0 / (2 * total))
    slope = jnp.sum(jnp.sum(dlogits * logits, axis=1, keepdims=True), axis=0, keepdims=True)
    scalars[0:1, :] = jnp.broadcast_to(loss, (1, 128))
    scalars[1:2, :] = jnp.broadcast_to(slope, (1, 128))
    high = lax.Precision.HIGHEST
    wide = [e.astype(F32) for e in embed]
    dembed = [
        sharp * jnp.dot(dlogits, wide[1], precision=high, preferred_element_type=F32),
        sharp * lax.dot_general(dlogits, wide[0], (((0,), (0,)), ((), ())), precision=high,
                                preferred_element_type=F32),
    ]
    for m in range(2):
        u, y, d = unit[m], proj[m], dembed[m]
        dp = (u * d - u * u * u * y * jnp.sum(y * d, axis=-1, keepdims=True)).astype(BF16)
        dproj[m] = dp
        dh = dot_t(dp, weight[m])
        gains[m:m + 1, :] = jnp.sum(dh * normal[m], axis=0, keepdims=True)
        shifts[m:m + 1, :] = jnp.sum(dh, axis=0, keepdims=True)
        back[m] = norm_back(normal[m], inverse[m], dh * vector(vec, H_GAIN + m))
        dcls[m] = back[m, pl.ds(pl.multiple_of(16 * me, 16), 16), :]


def contrast(dims, total, at, blocks, vec, weight, scale):
    model = weight.shape[1]
    rows = 16 * len(blocks) * blocks[0].shape[0]
    args = tuple(blocks) + (vec, weight, scale)
    shapes = [((2, rows, model), BF16), ((2, rows, weight.shape[2]), BF16), ((2, 16, model), F32),
              ((2, model), F32), ((2, model), F32), ((2, 128), F32)]

    def kernel(at, *refs):
        contrast_kernel(dims, total, at, refs[:len(blocks)], *refs[len(blocks):])

    return pl.pallas_call(
        kernel,
        grid_spec=pltpu.PrefetchScalarGridSpec(
            num_scalar_prefetch=1, grid=(1,),
            in_specs=[spec_whole(v) for v in args],
            out_specs=[pl.BlockSpec(s, lambda i, o, n=len(s): (0,) * n) for s, _ in shapes],
            scratch_shapes=[pltpu.VMEM((2, rows, model), F32)] * 2,
        ),
        out_shape=[jax.ShapeDtypeStruct(s, t) for s, t in shapes],
        compiler_params=params(),
        cost_estimate=pl.CostEstimate(flops=1_000_000_000, bytes_accessed=5_000_000, transcendentals=0),
        name="contrast",
    )(at, *args)


def contrast_large(dims, total, at, blocks, vec, weight, scale):
    model = weight.shape[1]
    held = jnp.concatenate(blocks)
    held = held[jnp.arange(held.shape[0]) ^ at[0]]
    rows = jnp.asarray([r for r in range(16) if r % 4 < dims.quarter])
    cls = jnp.transpose(held[:, :, rows], (1, 0, 2, 3)).reshape(2, -1, model)
    gain, shift = vec[H_GAIN:H_GAIN + 2, None], vec[H_SHIFT:H_SHIFT + 2, None]
    n, r = normalise(cls)
    head_in = (n * gain + shift).astype(BF16)
    proj = jnp.einsum("mrc,mce->mre", head_in, weight, preferred_element_type=F32)
    unit = lax.rsqrt(jnp.sum(proj * proj, axis=-1, keepdims=True) + 1e-6)
    embed = (proj * unit).astype(BF16)
    sharp = jnp.exp(scale[0, 0])
    logits = sharp * dot_t(embed[0], embed[1])
    row_lse = jax.nn.logsumexp(logits, axis=1, keepdims=True)
    col_lse = jax.nn.logsumexp(logits, axis=0, keepdims=True)
    dlogits = jnp.exp(logits - row_lse) + jnp.exp(logits - col_lse) - 2.0 * jnp.eye(total, dtype=F32)
    dlogits = dlogits / (2 * total)
    loss = (jnp.sum(row_lse) + jnp.sum(col_lse) - 2.0 * jnp.trace(logits)) / (2 * total)
    slope = jnp.sum(dlogits * logits)
    high = lax.Precision.HIGHEST
    wide = embed.astype(F32)
    dembed = sharp * jnp.stack([
        jnp.dot(dlogits, wide[1], precision=high, preferred_element_type=F32),
        jnp.dot(dlogits.T, wide[0], precision=high, preferred_element_type=F32)])
    dproj = (unit * dembed - unit ** 3 * proj * jnp.sum(proj * dembed, axis=-1, keepdims=True)).astype(BF16)
    dh = jnp.einsum("mre,mce->mrc", dproj, weight, preferred_element_type=F32)
    back = norm_back(n, r, dh * gain)
    pairs = 4 * dims.quarter
    own = lax.dynamic_slice_in_dim(back, at[0] * pairs, pairs, axis=1)
    dcls = jnp.zeros((2, 16, model), F32).at[:, rows].set(own)
    scalars = jnp.broadcast_to(jnp.stack([loss, slope])[:, None], (2, 128))
    return head_in, dproj, dcls, jnp.sum(dh * n, axis=1), jnp.sum(dh, axis=1), scalars


def own_pair(rows_of):
    return lambda i, o: (o[0] * rows_of + i, 0, 0)


def own_call(kernel, dims, name, order, blocks, img, txt, others, outs, scratch):
    model = img.shape[-1]
    block = pl.BlockSpec((1, dims.slab, model), lambda i, o: (i, 0, 0))
    specs = {
        "slab": (block, (dims.quarter, dims.slab, model)),
        "img": (pl.BlockSpec((1, dims.patches, model), lambda i, o: (i, 0, 0)), (dims.quarter, dims.patches, model)),
        "txt": (pl.BlockSpec((1, dims.caption, model), lambda i, o: (i, 0, 0)), (dims.quarter, dims.caption, model)),
        "sums": (pl.BlockSpec((8, model), lambda i, o: (0, 0)), (8, model)),
    }
    return pl.pallas_call(
        functools.partial(kernel, dims),
        grid_spec=pltpu.PrefetchScalarGridSpec(
            num_scalar_prefetch=1,
            grid=(dims.quarter,),
            in_specs=[block] * len(blocks) + [
                pl.BlockSpec((1, dims.patches, model), own_pair(dims.quarter)),
                pl.BlockSpec((1, dims.caption, model), own_pair(dims.quarter)),
            ] + [spec_whole(v) for v in others],
            out_specs=[specs[kind][0] for kind, _ in outs],
            scratch_shapes=[pltpu.VMEM((dims.slab, model), F32)] * scratch,
        ),
        out_shape=[jax.ShapeDtypeStruct(specs[kind][1], dtype) for kind, dtype in outs],
        compiler_params=params(),
        cost_estimate=pl.CostEstimate(flops=40_000_000, bytes_accessed=15_000_000, transcendentals=0),
        name=name,
    )(order, *blocks, img, txt, *others)


def start_own(rows, sums):
    @pl.when(pl.program_id(0) == 0)
    def _():
        rows[...] = jnp.zeros_like(rows)
        sums[...] = jnp.zeros_like(sums)


def add_class(dims, dcls, rows):
    i = pl.program_id(0)
    rows[0:1, :] += dcls[i, 0:1, :]
    rows[dims.ip:dims.ip + 1, :] += dcls[i, 1:2, :]


def final_kernel(dims, order, keep, recv, far, attended, img, txt, dcls, vec, fin_img, fin_txt, sums, rows):
    start_own(rows, sums)
    load_rows(dims, 0, img, txt, rows)
    add_class(dims, dcls, rows)
    for m, lo, hi in ((0, 0, dims.ip), (1, dims.ip, dims.slab)):
        b = keep[0, lo:hi].astype(F32) + recv[0, lo:hi].astype(F32) + far[0, lo:hi].astype(F32)
        b = b + vector(vec, F_BIAS + m)
        f = attended[0, lo:hi, :] + vector(vec, F_SCALE) * b
        if m == 0:
            fin_img[0] = f[0:dims.patches].astype(BF16)
        else:
            fin_txt[0] = f[0:dims.caption].astype(BF16)
        g = rows[lo:hi, :]
        sums[0:1, :] += jnp.sum(g * b, axis=0, keepdims=True)
        sums[1 + m:2 + m, :] += jnp.sum(g, axis=0, keepdims=True) * vector(vec, F_SCALE)


def final_rows(dims, order, keep, recv, far, attended, img, txt, dcls, vec):
    return own_call(final_kernel, dims, "final_rows", order, (keep, recv, far, attended), img, txt,
                    (dcls, vec), (("img", BF16), ("txt", BF16), ("sums", F32)), 1)


def norm_two_kernel(dims, order, keep, recv, far, attended, a_keep, a_recv, img, txt, dcls, x0, x1, x2, x3,
                    vec, dattended, dattn, sums, rows, ups):
    i = pl.program_id(0)
    start_own(rows, sums)
    load_rows(dims, 0, img, txt, rows)
    add_class(dims, dcls, rows)
    ups[...] = keep[0].astype(F32) + recv[0].astype(F32) + far[0].astype(F32)
    for m, at in ((0, 0), (1, dims.ip)):
        extra = [x[m, pl.ds(own_row(dims, r, 0) + i, 1), :] for x, r in ((x0, 0), (x1, 2), (x2, 1), (x3, 3))]
        ups[at:at + 1, :] += (extra[0] + extra[1]) + (extra[2] + extra[3])
    for m, lo, hi in ((0, 0, dims.ip), (1, dims.ip, dims.slab)):
        n, r = normalise(attended[0, lo:hi, :])
        dy = ups[lo:hi, :]
        sums[m:m + 1, :] += jnp.sum(dy * n, axis=0, keepdims=True)
        sums[2 + m:3 + m, :] += jnp.sum(dy, axis=0, keepdims=True)
        d = rows[lo:hi, :] + norm_back(n, r, dy * vector(vec, GAIN2 + m))
        dattended[0, lo:hi, :] = d
        sd = d * vector(vec, A_SCALE)
        dattn[0, lo:hi, :] = sd.astype(BF16)
        a = a_keep[0, lo:hi, :].astype(F32) + a_recv[0, lo:hi, :].astype(F32) + vector(vec, A_BIAS)
        sums[4:5, :] += jnp.sum(d * a, axis=0, keepdims=True)
        sums[5:6, :] += jnp.sum(sd, axis=0, keepdims=True)


def norm_two(dims, order, keep, recv, far, attended, a_keep, a_recv, img, txt, dcls, parts, vec):
    return own_call(norm_two_kernel, dims, "norm_two", order, (keep, recv, far, attended, a_keep, a_recv), img, txt,
                    (dcls,) + tuple(parts) + (vec,), (("slab", F32), ("slab", BF16), ("sums", F32)), 2)


def norm_one_kernel(dims, order, keep, recv, dattended, img, txt, vec, d_img, d_txt, sums, rows):
    start_own(rows, sums)
    load_rows(dims, 0, img, txt, rows)
    n, r = normalise(rows[...])
    dy = keep[0].astype(F32) + recv[0].astype(F32)
    sums[0:1, :] += jnp.sum(dy * n, axis=0, keepdims=True)
    sums[1:2, :] += jnp.sum(dy, axis=0, keepdims=True)
    d = dattended[0] + norm_back(n, r, dy * vector(vec, GAIN1))
    d_img[0] = d[0:dims.patches].astype(BF16)
    d_txt[0] = d[dims.ip:dims.ip + dims.caption].astype(BF16)


def norm_one(dims, order, keep, recv, dattended, img, txt, vec):
    return own_call(norm_one_kernel, dims, "norm_one", order, (keep, recv, dattended), img, txt,
                    (vec,), (("img", BF16), ("txt", BF16), ("sums", F32)), 1)


def back_step(dims, tiles, lens, whose, dattn, normed, qkv, mixed, dmixed, dqkv, acc, col_sums, w, ow):
    quarter, slab = dims.quarter, dims.slab
    count, width = quarter * slab, tiles * 128
    model = normed.shape[-1]
    d_rows = dattn[...].reshape(count, model)
    dmixed[...] = dot_t(d_rows, ow[...]).astype(BF16).reshape(quarter, slab, width)

    def one_pair(p, c):
        length = lens[whose * quarter + p]
        for lo, hi, start, limit in key_tail(dims, length):
            for g in range(tiles):
                at = [slice((t * tiles + g) * 128, (t * tiles + g + 1) * 128) for t in range(3)]
                q, k, v = [qkv[p, lo:hi, c] for c in at]
                q = scaled(q)
                qq = split_pair(q)
                dd = split_pair(dmixed[p, lo:hi, g * 128:(g + 1) * 128])
                w_ = softmax_keys(hide(dot_t(k, qq), start, limit))
                dw = dot_t(v, dd)
                dqkv[p, lo:hi, at[2]] = dot(w_.astype(BF16), dd).astype(BF16)
                ds = (w_ * (dw - jnp.sum(w_ * dw, axis=0, keepdims=True))).astype(BF16)
                dqkv[p, lo:hi, at[1]] = dot(ds, qq).astype(BF16)
                dqkv[p, lo:hi, at[0]] = (join_pair(t_dot(ds, k)) * HEAD_DIM ** -0.5).astype(BF16)
        return c

    lax.fori_loop(0, quarter, one_pair, 0)
    dp = dqkv[...].reshape(count, 3 * width)
    part = dot(dp, w[...])
    acc[:, 0:3 * width] += t_dot(normed[...].reshape(count, model), dp)
    acc[:, 3 * width:] += t_dot(d_rows, mixed[...].reshape(count, width))
    col_sums[...] += jnp.sum(dp.astype(F32), axis=0, keepdims=True)
    return part


def attend_back_kernel(dims, far, order, lens, d_own, d_peer, normed, qkv, mixed, wq, wo, wf, *refs):
    if not far:
        prior_keep, prior_send, *refs = refs
    keep, send, grad, *refs = refs
    if far:
        grad_rest, *refs = refs
    col_sums, dattn, dmixed, dqkv, acc, w, ow = refs
    i = pl.program_id(0)
    slab, quarter, local = dims.slab, dims.quarter, dims.local
    two, one_head = parts_of(dims)
    tiles = 2 if far else 1
    width = tiles * two
    count = quarter * slab
    model = normed.shape[-1]

    @pl.when(i == 0)
    def _():
        dattn[...] = d_own[...]
        acc[...] = jnp.zeros_like(acc)
        col_sums[...] = jnp.zeros_like(col_sums)
        for t in range(4):
            dst, at = (w, t * width) if t < 3 else (ow, 0)
            own, start = (wq, t * local) if t < 3 else (wo, 0)
            if far:
                copy_rows(dst, at, wf, t * local, two)
                copy_rows(dst, at + two, own, start + two, one_head)
                copy_rows(dst, at + two + one_head, wf, t * local + two, one_head)
            else:
                copy_rows(dst, at, own, start, two)

    @pl.when(i == 1)
    def _():
        dattn[...] = d_peer[...]

    part = back_step(dims, tiles, lens, order[2 * i], dattn, normed, qkv, mixed,
                     dmixed, dqkv, acc, col_sums, w, ow)

    @pl.when(i == 0)
    def _():
        prior = 0.0 if far else prior_keep[...].reshape(count, model).astype(F32)
        keep[...] = (part + prior).astype(BF16).reshape(quarter, slab, model)

    @pl.when(i == 1)
    def _():
        prior = 0.0 if far else prior_send[...].reshape(count, model).astype(F32)
        send[...] = (part + prior).astype(BF16).reshape(quarter, slab, model)
        for t in range(4):
            grad[:, t * two:(t + 1) * two] = acc[:, t * width:t * width + two].astype(BF16)
            if far:
                at = t * width + two
                to = 4 * two + t * one_head
                grad[:, to:to + one_head] = acc[:, at + one_head:at + two].astype(BF16)
                grad_rest[:, t * one_head:(t + 1) * one_head] = acc[:, at:at + one_head].astype(BF16)


def attend_back(dims, far, order, lens, d_own, d_peer, normed, qkv, mixed, wq, wo, wf, prior=()):
    model = normed.shape[-1]
    slab, quarter = dims.slab, dims.quarter
    width = 256 if far else 128
    one = pl.BlockSpec((quarter, slab, model), lambda i, o, n: (0, 0, 0))
    stride = normed.shape[0] // (2 * quarter)
    step = lambda cols: pl.BlockSpec((quarter, slab, cols), lambda i, o, n: (stride * i, 0, 0))
    grads = (768, 256) if far else (512,)
    specs = [one, one] + [pl.BlockSpec((model, n), lambda i, o, n_: (0, 0)) for n in grads]
    specs += [pl.BlockSpec((1, 3 * width), lambda i, o, n: (0, 0))]
    shapes = [
        jax.ShapeDtypeStruct((quarter, slab, model), BF16),
        jax.ShapeDtypeStruct((quarter, slab, model), BF16),
    ] + [jax.ShapeDtypeStruct((model, n), BF16) for n in grads] + [jax.ShapeDtypeStruct((1, 3 * width), F32)]
    scratch = [
        pltpu.VMEM((quarter, slab, model), BF16),
        pltpu.VMEM((quarter, slab, width), BF16),
        pltpu.VMEM((quarter, slab, 3 * width), BF16),
        pltpu.VMEM((model, 4 * width), F32),
        pltpu.VMEM((3 * width, model), BF16),
        pltpu.VMEM((width, model), BF16),
    ]
    return pl.pallas_call(
        functools.partial(attend_back_kernel, dims, far),
        grid_spec=pltpu.PrefetchScalarGridSpec(
            num_scalar_prefetch=2,
            grid=(2,),
            in_specs=[one, one, step(model), step(3 * width), step(width), spec_whole(wq), spec_whole(wo),
                      spec_whole(wf)] + [one] * len(prior),
            out_specs=specs,
            scratch_shapes=scratch,
        ),
        out_shape=shapes,
        compiler_params=params(),
        cost_estimate=pl.CostEstimate(
            flops=32 * quarter * slab * model * width, bytes_accessed=20_000_000, transcendentals=0),
        name="attend_back_far" if far else "attend_back_own",
    )(order, lens, d_own, d_peer, normed, qkv, mixed, wq, wo, wf, *prior)


def swap(value, axis, bit):
    size = lax.axis_size(axis)
    return lax.ppermute(value, axis, [(j, j ^ bit) for j in range(size)])


def to_core(value):
    return swap(value, "mp", 1)


def to_y(value):
    return swap(value, "mp", 2)


def from_others(value, axis, first, count):
    return [value] + [swap(value, axis, k * first) for k in range(1, count)]


def add_tree(parts):
    while len(parts) > 1:
        parts = [a + b for a, b in zip(parts[::2], parts[1::2])]
    return parts[0]


def sum_over(value, axis):
    first = 1
    while first < lax.axis_size(axis):
        count = min(8, lax.axis_size(axis) // first)
        value = add_tree(from_others(value, axis, first, count))
        first *= count
    return value


def gather_batch(value):
    parts = [value]
    first = 1
    size = lax.axis_size("batch")
    while first < size:
        count = min(8, size // first)
        whole = jnp.concatenate(parts) if len(parts) > 1 else parts[0]
        parts = from_others(whole, "batch", first, count)
        first *= count
    return parts


def gather_rows(own, me):
    near = jnp.stack([own, to_y(own)])
    far = to_core(near)
    out = jnp.zeros((4,) + own.shape, own.dtype)
    for r, value in enumerate((near[0], near[1], far[0], far[1])):
        out = lax.dynamic_update_slice(out, value[None], (me ^ ORDER[r],) + (0,) * own.ndim)
    return out.reshape((4 * own.shape[0],) + own.shape[1:])


def add_low(a, b):
    return (a.astype(F32) + b.astype(F32)).astype(BF16)


MESH = pl.DeviceIdType.MESH


class Place:
    def __init__(self):
        self.b, self.m = lax.axis_index("batch"), lax.axis_index("mp")
        self.z, self.x = self.b // 2, self.b % 2
        self.y, self.c = self.m // 2, self.m % 2
        self.core = (self.b, 2 * self.y + 1 - self.c)
        self.near = (self.b, 2 * (1 - self.y) + self.c)
        self.across = (self.b, 2 * (1 - self.y) + 1 - self.c)
        self.side = (2 * self.z + 1 - self.x, self.m)
        self.z_pair = self.z + 1 - 2 * (self.z % 2)
        self.z_far = (self.z + 2) % 4
        self.z_rest = (self.z_pair + 2) % 4
        self.paired = (2 * self.z_pair + self.x, self.m)
        self.opposite = (2 * self.z_far + self.x, self.m)
        self.batch = [((self.b + k) % 8, self.m) for k in range(1, 8)]

    def quarter(self, far_y, far_core):
        return 2 * ((self.y + far_y) % 2) + (self.c + far_core) % 2


def meet(peers):
    barrier = pltpu.get_barrier_semaphore()
    for peer in peers:
        pl.semaphore_signal(barrier, inc=1, device_id=peer, device_id_type=MESH)
    pl.semaphore_wait(barrier, len(peers))


def remote(src, dst, send_sem, recv_sem, at, device):
    return pltpu.make_async_remote_copy(
        src_ref=src, dst_ref=dst, send_sem=send_sem.at[at], recv_sem=recv_sem.at[at],
        device_id=device, device_id_type=MESH)


def front_kernel(dims, lens, img, txt, vectors, bias, own_w, own_o,
                 vec, normed, qkv, mixed, qkv_far, mixed_far, far_w, attended, attn, expert, expert_peer, cls, cls_peer,
                 rows, w, w2, ow, b, wf, far_bias, n_all, rest, m_all, m_far, q_own, q_far, a_send, a_recv, e_send, c_recv, held,
                 local_sem, send_sem, recv_sem):
    here = Place()
    i = pl.program_id(0)
    local, quarter, slab, ip = dims.local, dims.quarter, dims.slab, dims.ip
    two, one_head = parts_of(dims)
    count = quarter * slab
    model = img.shape[-1]
    at = i % 4
    whose = here.quarter(at % 2, 1 - at // 2)
    sent_w = [remote(own_w, wf.at[pl.ds(0, 3 * local)], send_sem, recv_sem, 0, here.near),
              remote(own_o, wf.at[pl.ds(3 * local, local)], send_sem, recv_sem, 1, here.near),
              remote(bias, far_bias, send_sem, recv_sem, 2, here.near)]
    sent_a = [remote(a_send.at[j], a_recv.at[j], send_sem, recv_sem, 3 + j, here.core) for j in range(2)]

    def e_over(j):
        return remote(e_send.at[j], expert_peer.at[j], send_sem, recv_sem, 5 + j, here.core)

    def e_here(j):
        return pltpu.make_async_copy(e_send.at[j], expert.at[j], local_sem.at[1 + j])

    sent_c = remote(cls, c_recv, send_sem, recv_sem, 5 + 2 * quarter, here.core)
    keep_w = pltpu.make_async_copy(wf, far_w, local_sem.at[0])
    sent_e = [e_over(j) for j in range(2 * quarter)]
    keep_e = [e_here(j) for j in range(2 * quarter)]

    @pl.when(i == 0)
    def _():
        meet([here.core, here.near])
        for copy in sent_w:
            copy.start()
        fill(vec, vectors)
        rows[...] = jnp.zeros_like(rows)
        b[...] = jnp.zeros_like(b)
        w[...] = jnp.zeros_like(w)
        cls[...] = jnp.zeros_like(cls)
        for t in range(3):
            copy_rows(w, t * 2 * two, own_w, t * local, local)
        b[0:1, 0:local] = bias[0:1, :]
        b[0:1, 4 * two:4 * two + local] = bias[1:2, :]

    def project(weights):
        proj = dot_t(n_all[at].reshape(count, model), weights[...]) + b[0:1, :]
        return proj.astype(BF16).reshape(quarter, slab, 6 * two)

    @pl.when(i < 4)
    def _():
        def one_norm(p, c):
            load_rows(dims, p, img, txt, rows)
            n, _ = normalise(rows[...])
            n_all[at, p] = (n * vector(vec, GAIN1) + vector(vec, SHIFT1)).astype(BF16)
            return c

        lax.fori_loop(0, quarter, one_norm, 0)
        proj = project(w)
        for t in range(3):
            q_own[:, :, t * two:(t + 1) * two] = proj[:, :, 2 * t * two:(2 * t + 1) * two]
            rest[at, :, :, t * two:(t + 1) * two] = proj[:, :, (2 * t + 1) * two:(2 * t + 2) * two]
        attend_tiles(dims, lens, whose, q_own, m_all.at[at])

        @pl.when(i % 2 == 0)
        def _():
            normed[...] = n_all[at]
            qkv[...] = q_own[...]
            mixed[...] = m_all[at]

    @pl.when(i == 4)
    def _():
        for copy in sent_w:
            copy.wait_recv()
        keep_w.start()
        w2[...] = jnp.zeros_like(w2)
        b[...] = jnp.zeros_like(b)
        for t in range(3):
            copy_rows(w2, t * 2 * two, wf, t * local, two)
            copy_rows(w2, t * 2 * two + two + one_head, wf, t * local + two, one_head)
        for t, to in ((0, 0), (1, 4 * two)):
            b[0:1, to:to + two] = far_bias[t:t + 1, 0:two]
            b[0:1, to + two + one_head:to + 2 * two] = far_bias[t:t + 1, two:]
        copy_rows(ow, 0, own_o, 0, two)
        copy_rows(ow, two, wf, 3 * local, two)
        copy_rows(ow, 2 * two, own_o, two, one_head)
        copy_rows(ow, 2 * two + one_head, wf, 3 * local + two, one_head)

    @pl.when(i >= 4)
    def _():
        proj = project(w2)
        for t in range(3):
            to = 2 * t * two
            q_far[:, :, to:to + two] = proj[:, :, to:to + two]
            q_far[:, :, to + two:to + 2 * two] = (
                proj[:, :, to + two:to + 2 * two] + rest[at, :, :, t * two:(t + 1) * two])
        attend_tiles(dims, lens, whose, q_far, m_far)

        @pl.when(i % 2 == 0)
        def _():
            qkv_far[...] = q_far[...]
            mixed_far[...] = m_far[...]

        part = dot(m_all[at].reshape(count, two), ow[0:two, :])
        part = part + dot(m_far[...].reshape(count, 2 * two), ow[two:, :])
        part = part.reshape(quarter, slab, model)

        @pl.when(i < 6)
        def _():
            a_send[at] = part.astype(BF16)

        for j in range(2):
            @pl.when(i == 4 + j)
            def _():
                sent_a[j].start()

        for j in range(2):
            @pl.when(i == 6 + j)
            def _():
                sent_a[j].wait_recv()

        @pl.when(i >= 6)
        def _():
            j = i - 6
            held[...] = part

            def one_residual(p, c):
                load_rows(dims, p, img, txt, rows)
                a = held[p] + a_recv[j, p].astype(F32)
                x = rows[...] + vector(vec, A_SCALE) * (a + vector(vec, A_BIAS))
                n, _ = normalise(x)
                e_img = n[0:ip] * vector(vec, GAIN2) + vector(vec, SHIFT2)
                e_txt = n[ip:] * vector(vec, GAIN2 + 1) + vector(vec, SHIFT2 + 1)
                r = j * quarter + p
                e_send[r, 0:ip, :] = e_img.astype(BF16)
                e_send[r, ip:, :] = e_txt.astype(BF16)
                e_over(r).start()
                e_here(r).start()
                for k, v in enumerate((x[0:1], x[ip:ip + 1], e_img[0:1], e_txt[0:1])):
                    cls[k, pl.ds(r, 1), :] = v

                @pl.when(j == 0)
                def _():
                    attended[p] = x
                    attn[p] = a

                return c

            lax.fori_loop(0, quarter, one_residual, 0)

    @pl.when(i == 7)
    def _():
        sent_c.start()
        keep_w.wait()
        for copy in keep_e:
            copy.wait()
        sent_c.wait()
        cls_peer[...] = c_recv[...]
        for copy in sent_e:
            copy.wait()
        for copy in sent_w + sent_a:
            copy.wait_send()


def fill(table, vectors):
    table[...] = jnp.zeros_like(table)
    at = 0
    for v in vectors:
        n = v.shape[0] if len(v.shape) == 2 else 1
        table[at:at + n, :] = v[...].reshape(n, table.shape[1])
        at += n


def front(dims, lens, img, txt, vectors, bias, own_w, own_o):
    model = img.shape[-1]
    quarter, slab, local = dims.quarter, dims.slab, dims.local
    held = pl.BlockSpec(memory_space=pltpu.VMEM)
    away = pl.BlockSpec(memory_space=pl.ANY)

    def states_at(i):
        return Place().quarter(i % 2, 1 - i % 4 // 2), 0, 0

    own_block = lambda cols: pl.BlockSpec((quarter, slab, cols), lambda i: (jnp.where(i < 2, 1, 0), 0, 0))
    far_block = lambda cols: pl.BlockSpec((quarter, slab, cols), lambda i: (jnp.where(i < 6, 1, 0), 0, 0))
    six = lambda cols: jax.ShapeDtypeStruct((2 * quarter, slab, cols), BF16)
    block = lambda cols: (quarter, slab, cols)
    n_remote = 6 + 2 * quarter
    return pl.pallas_call(
        lambda lens, img, txt, *refs: front_kernel(
            dims, lens, img, txt, refs[:len(vectors)], *refs[len(vectors):]),
        grid=(8,),
        in_specs=[pl.BlockSpec(memory_space=pltpu.SMEM),
                  pl.BlockSpec((quarter, dims.patches, model), states_at),
                  pl.BlockSpec((quarter, dims.caption, model), states_at)] + [held] * (3 + len(vectors)),
        out_specs=[held, own_block(model), own_block(384), own_block(128), far_block(768), far_block(256),
                   away, held, held, away, away, held, held],
        out_shape=[jax.ShapeDtypeStruct((16, model), F32), six(model), six(384), six(128), six(768), six(256),
                   jax.ShapeDtypeStruct((4 * local, model), BF16),
                   jax.ShapeDtypeStruct(block(model), F32), jax.ShapeDtypeStruct(block(model), F32),
                   six(model), six(model),
                   jax.ShapeDtypeStruct((4, 8, model), F32), jax.ShapeDtypeStruct((4, 8, model), F32)],
        scratch_shapes=[
            pltpu.VMEM((slab, model), F32), pltpu.VMEM((768, model), BF16), pltpu.VMEM((768, model), BF16),
            pltpu.VMEM((384, model), BF16), pltpu.VMEM((8, 768), F32), pltpu.VMEM((4 * local, model), BF16),
            pltpu.VMEM((2, local), F32),
            pltpu.VMEM((4,) + block(model), BF16), pltpu.VMEM((4,) + block(384), BF16),
            pltpu.VMEM((4,) + block(128), BF16), pltpu.VMEM(block(256), BF16),
            pltpu.VMEM(block(384), BF16), pltpu.VMEM(block(768), BF16),
            pltpu.VMEM((2,) + block(model), BF16), pltpu.VMEM((2,) + block(model), BF16),
            pltpu.VMEM((2 * quarter, slab, model), BF16), pltpu.VMEM((4, 8, model), F32),
            pltpu.VMEM(block(model), F32),
            pltpu.SemaphoreType.DMA((1 + 2 * quarter,)),
            pltpu.SemaphoreType.DMA((n_remote,)), pltpu.SemaphoreType.DMA((n_remote,)),
        ],
        compiler_params=params(collective_id=6, has_side_effects=True),
        cost_estimate=pl.CostEstimate(
            flops=16 * quarter * slab * model * 1152, bytes_accessed=40_000_000, transcendentals=0),
        name="front",
    )(lens, img, txt, *vectors, bias, own_w, own_o)


def middle_kernel(dims, total, img, txt, own, peer, cls_own, cls_peer, vec, up, up_bias, down, head_weight, scale,
                  act, dup, ddn, dexp, d_own, d_near, bias_grad, class_e, c_act, c_dup, c_ddn, dcls,
                  head_in, dproj, gains, shifts, scalars,
                  bx, bd, rx, rd, x_near, x_far, ins, rows, part, parts, cls, back, cot, c_rows, extra, extras, hidden_in, weight,
                  local_sem, send_sem, recv_sem):
    here = Place()
    ip, slab, quarter = dims.ip, dims.slab, dims.quarter
    i = pl.program_id(0)
    model = own.shape[-1]
    mp_peers = [here.core, here.near, here.across]
    fetch = pltpu.make_async_copy(head_weight, weight, local_sem.at[0])
    of = [here.quarter(0, 0), here.quarter(1, 0), here.quarter(0, 1), here.quarter(1, 1)]

    sent_x = [remote(bx.at[2 * j], rx.at[j], send_sem, recv_sem, j, here.core) for j in range(2)]
    sent_d = [remote(bd.at[2 * j], rd.at[j], send_sem, recv_sem, 2 + j, here.core) for j in range(2)]
    sent_near = remote(x_near, x_far, send_sem, recv_sem, 4, here.near)
    sent_part = [remote(part, parts.at[k], send_sem, recv_sem, 5 + k, mp_peers[k]) for k in range(3)]
    sent_extra = [remote(extra, extras.at[k], send_sem, recv_sem, 8 + k, mp_peers[k]) for k in range(3)]
    sent_cls = [remote(cls.at[here.b], cls.at[here.b], send_sem, recv_sem, 11 + k, here.batch[k]) for k in range(7)]

    @pl.when(i == 0)
    def _():
        fetch.start()
        rows[...] = jnp.zeros_like(rows)
        bias_grad[...] = jnp.zeros_like(bias_grad)
        for m in range(2):
            e = jnp.concatenate([cls_own[2 + m], cls_peer[2 + m]], axis=0).astype(BF16)
            class_e[m] = e
            u = dot(e, up[m]) + up_bias[m:m + 1]
            hidden_in[m] = u
            part[m] = dot(gelu_low(u), down[m])
        meet(mp_peers + here.batch)
        for copy in sent_part:
            copy.start()
        ins[...] = peer[...]

    @pl.when(i == 1)
    def _():
        for copy in sent_part:
            copy.wait_recv()
        for m in range(2):
            cls[here.b, m] = jnp.zeros(cls.shape[2:], F32)
            for r in range(4):
                half, at = (cls_own, cls_peer)[r // 2], quarter * (r % 2)
                for p in range(quarter):
                    line = [d[m, own_row(dims, s, p):own_row(dims, s, p) + 1, :]
                            for d, s in ((part, r), (parts.at[0], r ^ 2), (parts.at[1], r ^ 1), (parts.at[2], r ^ 3))]
                    x = (line[0] + line[1]) + (line[2] + line[3]) + vector(vec, F_BIAS + m)
                    x = half[m, at + p:at + p + 1, :] + vector(vec, F_SCALE) * x
                    cls[here.b, m, pl.ds(4 * of[r] + p, 1), :] = x
        for copy in sent_cls:
            copy.start()
        ins[...] = own[...]

    @pl.when(i == 2)
    def _():
        ins[...] = peer[...]

    @pl.when(i == 3)
    def _():
        ins[...] = own[...]
        fetch.wait()
        for copy in sent_cls:
            copy.wait_recv()
        n_rows = 16 * cls.shape[0]
        sharp = jnp.exp(scale[...])
        col_at = lax.broadcasted_iota(jnp.int32, (1, n_rows), 1)
        row_at = lax.broadcasted_iota(jnp.int32, (n_rows, 1), 0)
        col_ok = (col_at % 4) < quarter
        row_ok = (row_at % 4) < quarter
        normal, inverse, proj, unit, embed = [], [], [], [], []
        for m in range(2):
            n, r = normalise(cls[:, m].reshape(n_rows, model))
            h = (n * vector(vec, H_GAIN + m) + vector(vec, H_SHIFT + m)).astype(BF16)
            head_in[m] = h
            y = dot(h, weight[m])
            u = lax.rsqrt(jnp.sum(y * y, axis=-1, keepdims=True) + 1e-6)
            normal.append(n)
            inverse.append(r)
            proj.append(y)
            unit.append(u)
            embed.append((y * u).astype(BF16))
        ok = row_ok & col_ok
        logits = sharp * dot_t(embed[0], embed[1])
        masked = jnp.where(ok, logits, -1e30)
        row_max = jnp.max(masked, axis=1, keepdims=True)
        row_lse = row_max + jnp.log(jnp.sum(jnp.exp(masked - row_max), axis=1, keepdims=True))
        col_max = jnp.max(masked, axis=0, keepdims=True)
        col_lse = col_max + jnp.log(jnp.sum(jnp.exp(masked - col_max), axis=0, keepdims=True))
        same = (row_at == col_at) & ok
        both = jnp.exp(masked - row_lse) + jnp.exp(masked - col_lse)
        dlogits = jnp.where(ok, jnp.where(same, both - 2.0, both) * (1.0 / (2 * total)), 0.0)
        diagonal = jnp.sum(jnp.where(same, logits, 0.0), axis=1, keepdims=True)
        lines = jnp.sum(jnp.where(row_ok, row_lse - 2.0 * diagonal, 0.0), axis=0, keepdims=True)
        lines = lines + jnp.sum(jnp.where(col_ok, col_lse, 0.0), axis=1, keepdims=True)
        slope = jnp.sum(jnp.sum(dlogits * logits, axis=1, keepdims=True), axis=0, keepdims=True)
        scalars[0:1, :] = jnp.broadcast_to(lines * (1.0 / (2 * total)), (1, 128))
        scalars[1:2, :] = jnp.broadcast_to(slope, (1, 128))
        pieces, left = [], dlogits
        for _ in range(3):
            pieces.append(left.astype(BF16))
            left = left - pieces[-1].astype(F32)
        dembed = [
            sharp * (dot(pieces[0], embed[1]) + (dot(pieces[1], embed[1]) + dot(pieces[2], embed[1]))),
            sharp * (t_dot(pieces[0], embed[0]) + (t_dot(pieces[1], embed[0]) + t_dot(pieces[2], embed[0]))),
        ]
        c_rows[...] = jnp.zeros_like(c_rows)
        dcls[...] = jnp.zeros_like(dcls)
        for m in range(2):
            for p in range(quarter):
                src = (img, txt)[m]
                cot[m, 8 * 3 + p:8 * 3 + p + 1, :] = src[p, 0:1, :].astype(F32)
        for m in range(2):
            u, y, d = unit[m], proj[m], dembed[m]
            dp = (u * d - u * u * u * y * jnp.sum(y * d, axis=-1, keepdims=True)).astype(BF16)
            dproj[m] = dp
            dh = dot_t(dp, weight[m])
            gains[m:m + 1, :] = jnp.sum(dh * normal[m], axis=0, keepdims=True)
            shifts[m:m + 1, :] = jnp.sum(dh, axis=0, keepdims=True)
            back[m] = norm_back(normal[m], inverse[m], dh * vector(vec, H_GAIN + m))
            for r in range(4):
                step = (3, 1, 2, 0)[r]
                for p in range(quarter):
                    g = back[m, pl.ds(16 * here.b + 4 * of[r] + p, 1), :]
                    at = own_row(dims, r, p)
                    c_rows[m, at:at + 1, :] = cot[m, 8 * step + p:8 * step + p + 1, :] + g
                    if r == 0:
                        dcls[p, m:m + 1, :] = g
            u = hidden_in[m]
            big, small = gelu_parts(u)
            c_act[m] = (u * big).astype(BF16)
            g = (c_rows[m] * vector(vec, F_SCALE)).astype(BF16)
            c_ddn[m] = g
            du = dot_t(g, down[m]) * (big + u * small)
            bias_grad[m:m + 1, :] += jnp.sum(du, axis=0, keepdims=True)
            low = du.astype(BF16)
            c_dup[m] = low
            extra[m] = dot_t(low, up[m])
        for copy in sent_extra:
            copy.start()

    at = lax.broadcasted_iota(jnp.int32, (slab, 1), 0)
    inner = (at != 0) & (at != ip)

    def one(p, c):
        load_rows(dims, p, img, txt, rows)
        cot[0, pl.ds(8 * i + p, 1), :] = rows[0:1, :]
        cot[1, pl.ds(8 * i + p, 1), :] = rows[ip:ip + 1, :]
        ddn[p] = jnp.where(inner, rows[...] * vector(vec, F_SCALE), 0.0).astype(BF16)
        return c

    lax.fori_loop(0, quarter, one, 0)
    for m, lo, hi in ((0, 0, ip), (1, ip, slab)):
        count = quarter * (hi - lo)
        e = ins[:, lo:hi, :].reshape(count, model)
        u = dot(e, up[m]) + up_bias[m:m + 1]
        big, small = gelu_parts(u)
        a = (u * big).astype(BF16)
        act[:, lo:hi, :] = a.reshape(quarter, hi - lo, -1)
        slope = big + u * small
        bd[i, :, lo:hi, :] = dot(a, down[m]).astype(BF16).reshape(quarter, hi - lo, model)
        g = ddn[:, lo:hi, :].reshape(count, model)
        du = dot_t(g, down[m]) * slope
        bias_grad[m:m + 1, :] += jnp.sum(du, axis=0, keepdims=True)
        low = du.astype(BF16)
        dup[:, lo:hi, :] = low.reshape(quarter, hi - lo, -1)
        bx[i, :, lo:hi, :] = dot_t(low, up[m]).astype(BF16).reshape(quarter, hi - lo, model)

    for j in range(2):
        @pl.when(i == 2 * j)
        def _():
            sent_x[j].start()
            sent_d[j].start()

    @pl.when(i == 1)
    def _():
        sent_x[0].wait_recv()

        def add_x(p, c):
            x_near[p] = (bx[1, p].astype(F32) + rx[0, p].astype(F32)).astype(BF16)
            return c

        lax.fori_loop(0, quarter, add_x, 0)
        sent_near.start()
        sent_d[0].wait_recv()

        def add_d(p, c):
            d_near[p] = (bd[1, p].astype(F32) + rd[0, p].astype(F32)).astype(BF16)
            return c

        lax.fori_loop(0, quarter, add_d, 0)

    @pl.when(i == 3)
    def _():
        sent_d[1].wait_recv()

        def add_d(p, c):
            d_own[p] = bd[3, p].astype(F32) + rd[1, p].astype(F32)
            return c

        lax.fori_loop(0, quarter, add_d, 0)
        sent_x[1].wait_recv()
        sent_near.wait_recv()

        def add_x(p, c):
            dexp[p] = bx[3, p].astype(F32) + rx[1, p].astype(F32) + x_far[p].astype(F32)
            return c

        lax.fori_loop(0, quarter, add_x, 0)
        for copy in sent_extra:
            copy.wait_recv()
        for m in range(2):
            for p in range(quarter):
                line = [x[m, own_row(dims, r, p):own_row(dims, r, p) + 1, :]
                        for x, r in ((extra, 0), (extras.at[0], 2), (extras.at[1], 1), (extras.at[2], 3))]
                dexp[p, m * ip:m * ip + 1, :] += (line[0] + line[1]) + (line[2] + line[3])
        for copy in sent_x + sent_d + [sent_near] + sent_part + sent_extra + sent_cls:
            copy.wait_send()


def middle(dims, total, img, txt, own, peer, cls_own, cls_peer, vec, up, up_bias, down, weight, scale):
    model = own.shape[-1]
    hidden = up.shape[-1]
    slab, quarter = dims.slab, dims.quarter
    batch = 8

    def cot_at(i):
        here = Place()
        return here.quarter(1 - i // 2, 1 - i % 2), 0, 0

    held = pl.BlockSpec(memory_space=pltpu.VMEM)
    half = pl.BlockSpec((quarter, slab, model), lambda i: (jnp.where(i < 2, 1, 0), 0, 0))
    step = lambda cols: pl.BlockSpec((quarter, slab, cols), lambda i: (i, 0, 0))
    rows_of = lambda n, t: jax.ShapeDtypeStruct((n, slab, model), t)
    small = [((quarter, slab, model), F32), ((quarter, slab, model), F32), ((quarter, slab, model), BF16),
             ((2, hidden), F32), ((2, 16, model), BF16), ((2, 16, hidden), BF16), ((2, 16, hidden), BF16),
             ((2, 16, model), BF16), ((quarter, 8, model), F32), ((2, 16 * batch, model), BF16),
             ((2, 16 * batch, weight.shape[2]), BF16), ((2, model), F32), ((2, model), F32), ((2, 128), F32)]
    block = (quarter, slab, model)
    return pl.pallas_call(
        functools.partial(middle_kernel, dims, total),
        grid=(4,),
        in_specs=[pl.BlockSpec((quarter, dims.patches, model), cot_at),
                  pl.BlockSpec((quarter, dims.caption, model), cot_at)] + [half] * 2 + [held] * 6
        + [pl.BlockSpec(memory_space=pl.ANY), held],
        out_specs=[step(hidden), step(hidden), step(model)] + [held] * len(small),
        out_shape=[rows_of(4 * quarter, BF16)] * 3 + [jax.ShapeDtypeStruct(v, t) for v, t in small],
        scratch_shapes=[
            pltpu.VMEM((4,) + block, BF16), pltpu.VMEM((4,) + block, BF16),
            pltpu.VMEM((2,) + block, BF16), pltpu.VMEM((2,) + block, BF16),
            pltpu.VMEM(block, BF16), pltpu.VMEM(block, BF16), pltpu.VMEM(block, BF16),
            pltpu.VMEM((slab, model), F32),
            pltpu.VMEM((2, 16, model), F32), pltpu.VMEM((3, 2, 16, model), F32),
            pltpu.VMEM((batch, 2, 16, model), F32), pltpu.VMEM((2, 16 * batch, model), F32),
            pltpu.VMEM((2, 32, model), F32), pltpu.VMEM((2, 16, model), F32),
            pltpu.VMEM((2, 16, model), F32), pltpu.VMEM((3, 2, 16, model), F32),
            pltpu.VMEM((2, 16, hidden), F32), pltpu.VMEM(weight.shape, BF16), pltpu.SemaphoreType.DMA((1,)),
            pltpu.SemaphoreType.DMA((18,)), pltpu.SemaphoreType.DMA((18,)),
        ],
        compiler_params=params(collective_id=2, has_side_effects=True),
        cost_estimate=pl.CostEstimate(
            flops=32 * quarter * slab * model * hidden, bytes_accessed=40_000_000, transcendentals=0),
        name="middle",
    )(img, txt, own, peer, cls_own, cls_peer, vec, up, up_bias, down, weight, scale)


def turn_kernel(dims, img, txt, peer, own, act, dup, ddn, ce, ca, cu, cd, dexp, attended, attn, d_own, d_near, dcls, vec,
                down_sum, up_keep, up_send, dattended, dattn, dattn_peer, fin_img, fin_txt, sums,
                acc, d_far, n_peer, rows, side_send, side_recv, e_in, dexp_in, attended_in, attn_in, d_own_in,
                local_sem, send_sem, recv_sem):
    here = Place()
    quarter, ip = dims.quarter, dims.ip
    i = pl.program_id(0)
    piece = side_send.shape[3]
    sent_near = remote(d_near, d_far, send_sem, recv_sem, 0, here.near)

    def over(p):
        return remote(dattn.at[p], n_peer.at[p], send_sem, recv_sem, 1 + p, here.core)

    sent_core = [over(p) for p in range(quarter)]
    sent_side = [remote(side_send.at[h], side_recv.at[h], send_sem, recv_sem, 1 + quarter + h, here.side)
                 for h in range(2)]
    part = acc.shape[2] // 2
    loaded = [pltpu.make_async_copy(src, dst, local_sem.at[j]) for j, (src, dst) in enumerate((
        (dexp, dexp_in), (attended, attended_in), (attn, attn_in), (d_own, d_own_in)))]
    dexp, attended, attn, d_own = dexp_in, attended_in, attn_in, d_own_in
    spans = ((0, 0, ip), (1, ip, dims.slab))
    flat = lambda v: v.reshape(-1, v.shape[-1])
    block = lambda j: pl.ds(pl.multiple_of(j * piece, piece), piece)

    @pl.when(i == 0)
    def _():
        meet([here.core, here.near, here.side])
        sent_near.start()
        for copy in loaded:
            copy.start()
        for m in range(2):
            acc[m] = t_dot(cd[m], ca[m])

    for h in range(2):
        @pl.when(i // 4 == h)
        def _():
            for m, lo, hi in spans:
                acc[m, :, h * part:(h + 1) * part] += t_dot(flat(ddn[:, lo:hi, :]), flat(act[:, lo:hi, :]))

        @pl.when(i == 4 * h + 3)
        def _():
            cols = slice(h * part, (h + 1) * part)
            for j in range(4):
                for m in range(2):
                    side_send[h, j, m] = acc[m, block(2 * j + 1 - here.x), cols].astype(BF16)
                    down_sum[j, m, :, cols] = acc[m, block(2 * j + here.x), cols].astype(BF16)
            sent_side[h].start()

    @pl.when(i == 8)
    def _():
        for m in range(2):
            acc[m] = t_dot(ce[m], cu[m])

    @pl.when((i >= 8) & (i % 2 == 0))
    def _():
        e_in[...] = peer[...]

    @pl.when((i >= 8) & (i % 2 == 1))
    def _():
        e_in[...] = own[...]

    @pl.when(i >= 8)
    def _():
        for m, lo, hi in spans:
            acc[m] += t_dot(flat(e_in[:, lo:hi, :]), flat(dup[:, lo:hi, :]))

    @pl.when(i == 11)
    def _():
        for j in range(4):
            for m in range(2):
                up_keep[j, m] = acc[m, block(2 * j + here.x), :].astype(BF16)
                up_send[j, m] = acc[m, block(2 * j + 1 - here.x), :].astype(BF16)
        for copy in loaded:
            copy.wait()
        rows[...] = jnp.zeros_like(rows)
        sums[...] = jnp.zeros_like(sums)

        def load(p):
            load_rows(dims, p, img, txt, rows)
            rows[0:1, :] += dcls[p, 0:1, :]
            rows[ip:ip + 1, :] += dcls[p, 1:2, :]

        def norm(p, c):
            load(p)
            for m, lo, hi in ((0, 0, ip), (1, ip, dims.slab)):
                n, r = normalise(attended[p, lo:hi, :])
                dy = dexp[p, lo:hi, :]
                sums[m:m + 1, :] += jnp.sum(dy * n, axis=0, keepdims=True)
                sums[2 + m:3 + m, :] += jnp.sum(dy, axis=0, keepdims=True)
                d = rows[lo:hi, :] + norm_back(n, r, dy * vector(vec, GAIN2 + m))
                dattended[p, lo:hi, :] = d
                sd = d * vector(vec, A_SCALE)
                dattn[p, lo:hi, :] = sd.astype(BF16)
                a = attn[p, lo:hi, :] + vector(vec, A_BIAS)
                sums[4:5, :] += jnp.sum(d * a, axis=0, keepdims=True)
                sums[5:6, :] += jnp.sum(sd, axis=0, keepdims=True)
            over(p).start()
            return c

        lax.fori_loop(0, quarter, norm, 0)
        sent_near.wait_recv()

        def final(p, c):
            load(p)
            for m, lo, hi in ((0, 0, ip), (1, ip, dims.slab)):
                b = d_own[p, lo:hi, :] + d_far[p, lo:hi, :].astype(F32) + vector(vec, F_BIAS + m)
                f = attended[p, lo:hi, :] + vector(vec, F_SCALE) * b
                if m == 0:
                    fin_img[p] = f[0:dims.patches].astype(BF16)
                else:
                    fin_txt[p] = f[0:dims.caption].astype(BF16)
                g = rows[lo:hi, :]
                sums[6:7, :] += jnp.sum(g * b, axis=0, keepdims=True)
                sums[7 + m:8 + m, :] += jnp.sum(g, axis=0, keepdims=True) * vector(vec, F_SCALE)
            return c

        lax.fori_loop(0, quarter, final, 0)
        for p in range(quarter):
            sent_core[p].wait()
            dattn_peer[p] = n_peer[p]
        for h in range(2):
            sent_side[h].wait()
            cols = slice(h * part, (h + 1) * part)
            for j in range(4):
                down_sum[j, :, :, cols] = (
                    down_sum[j, :, :, cols].astype(F32) + side_recv[h, j].astype(F32)).astype(BF16)
        sent_near.wait_send()


def turn(dims, img, txt, peer, own, act, dup, ddn, ce, ca, cu, cd, dexp, attended, attn, d_own, d_near, dcls, vec):
    model = own.shape[-1]
    hidden = act.shape[-1]
    slab, quarter = dims.slab, dims.quarter
    held = pl.BlockSpec(memory_space=pltpu.VMEM)

    def own_at(i):
        return Place().quarter(0, 0), 0, 0

    away = pl.BlockSpec(memory_space=pl.ANY)
    half = pl.BlockSpec((quarter, slab, model), lambda i: (jnp.where(i < 10, 1, 0), 0, 0))
    row = lambda i: jnp.where(i < 8, i % 4, 3)
    first = pl.BlockSpec((quarter, slab, model), lambda i: (row(i), 0, 0))
    piece = pl.BlockSpec((quarter, slab, hidden // 2), lambda i: (row(i), 0, jnp.minimum(i // 4, 1)))
    last = pl.BlockSpec((quarter, slab, hidden), lambda i: (jnp.maximum(i - 8, 0), 0, 0))
    block = (quarter, slab, model)
    part = (4, 2, model // 8, hidden)
    split = (2, 4, 2, model // 8, hidden // 2)
    outs = [(part, BF16), (part, BF16), (part, BF16), (block, F32), (block, BF16), (block, BF16),
            ((quarter, dims.patches, model), BF16), ((quarter, dims.caption, model), BF16), ((16, model), F32)]
    return pl.pallas_call(
        functools.partial(turn_kernel, dims),
        grid=(12,),
        in_specs=[pl.BlockSpec((quarter, dims.patches, model), own_at),
                  pl.BlockSpec((quarter, dims.caption, model), own_at)] + [half] * 2 + [piece, last, first]
        + [held] * 4 + [away] * 4 + [held] * 3,
        out_specs=[held] * len(outs),
        out_shape=[jax.ShapeDtypeStruct(v, t) for v, t in outs],
        scratch_shapes=[
            pltpu.VMEM((2, model, hidden), F32), pltpu.VMEM(block, BF16), pltpu.VMEM(block, BF16),
            pltpu.VMEM((slab, model), F32), pltpu.VMEM(split, BF16), pltpu.VMEM(split, BF16),
            pltpu.VMEM(block, BF16),
        ] + [pltpu.VMEM(block, F32)] * 4 + [
            pltpu.SemaphoreType.DMA((4,)),
            pltpu.SemaphoreType.DMA((3 + quarter,)), pltpu.SemaphoreType.DMA((3 + quarter,)),
        ],
        compiler_params=params(collective_id=3, has_side_effects=True),
        cost_estimate=pl.CostEstimate(
            flops=16 * quarter * slab * model * hidden, bytes_accessed=40_000_000, transcendentals=0),
        name="turn",
    )(img, txt, peer, own, act, dup, ddn, ce, ca, cu, cd, dexp, attended, attn, d_own, d_near, dcls, vec)


def back_kernel(dims, lens, d_own, d_peer, normed, qkv_far, mixed_far, qkv_own, mixed_own, wq, wo, wf,
                fin_img, fin_txt, up_keep, up_send, down_sum,
                whole, grad_pair, grad_single, cols_far, cols_own, near_img, near_txt, far_sum, up_one, down_out, up_out,
                dattn, dm_far, dm_own, dq_far, dq_own, acc_far, acc_own, w_far, w_own, o_far, o_own, dn, grad_f,
                up_mine, up_side, up_low, up_in, up_pass, up_last, down_mine, down_in, down_pass, down_last,
                n_send, n_recv, from_side, local_sem, send_sem, recv_sem):
    here = Place()
    i = pl.program_id(0)
    slab, quarter, local = dims.slab, dims.quarter, dims.local
    two, one_head = parts_of(dims)
    count = quarter * slab
    model = normed.shape[-1]
    piece = from_side.shape[1]
    block = lambda j: pl.ds(pl.multiple_of(j * piece, piece), piece)
    used = [0]

    def make(src, dst, device):
        at = used[0]
        used[0] += 1
        return remote(src, dst, send_sem, recv_sem, at, device)

    sent_near = [make(fin_img, near_img, here.near), make(fin_txt, near_txt, here.near)]
    sent_up = [make(up_send.at[j, m], up_side.at[m, j], here.side) for m in range(2) for j in range(4)]
    in_pair = lambda src, dst: [make(src.at[here.z_pair], dst.at[0], here.paired), make(src.at[here.z_rest], dst.at[1], here.paired)]
    sent_down = in_pair(down_sum, down_in)
    pass_down = make(down_pass, down_last, here.opposite)
    sent_far = [make(grad_f.at[block(2 * j + 1 - here.x)], from_side.at[j], here.side) for j in range(4)]
    sent_low = in_pair(up_low, up_in)
    pass_low = make(up_pass, up_last, here.opposite)
    sent_n = make(n_send, n_recv, here.core)
    loaded = [pltpu.make_async_copy(up_keep, up_mine, local_sem.at[0]),
              pltpu.make_async_copy(down_sum.at[here.z], down_mine.at[0], local_sem.at[1]),
              pltpu.make_async_copy(down_sum.at[here.z_far], down_mine.at[1], local_sem.at[2])]
    add = lambda *parts: functools.reduce(lambda p, q: p + q, [v.astype(F32) for v in parts])

    @pl.when(i == 0)
    def _():
        meet([here.core, here.near, here.side, here.paired, here.opposite])
        for copy in loaded + sent_near + sent_up + sent_down:
            copy.start()
        for acc, cols in ((acc_far, cols_far), (acc_own, cols_own)):
            acc[...] = jnp.zeros_like(acc)
            cols[...] = jnp.zeros_like(cols)
        for t in range(4):
            own, start = (wq, t * local) if t < 3 else (wo, 0)
            dst, at = (w_far, t * 2 * two) if t < 3 else (o_far, 0)
            copy_rows(dst, at, wf, t * local, two)
            copy_rows(dst, at + two, own, start + two, one_head)
            copy_rows(dst, at + two + one_head, wf, t * local + two, one_head)
            dst, at = (w_own, t * two) if t < 3 else (o_own, 0)
            copy_rows(dst, at, own, start, two)

    @pl.when(i % 2 == 0)
    def _():
        dattn[...] = d_peer[...]

    @pl.when(i % 2 == 1)
    def _():
        dattn[...] = d_own[...]

    whose = here.quarter(0, 1 - i % 2)

    @pl.when(i < 2)
    def _():
        part = back_step(dims, 2, lens, whose, dattn, normed, qkv_far, mixed_far, dm_far, dq_far, acc_far, cols_far,
                         w_far, o_far)
        dn[i] = part.reshape(quarter, slab, model)

    @pl.when(i == 0)
    def _():
        for copy in loaded[1:]:
            copy.wait()
        for copy in sent_down:
            copy.wait_recv()
        down_pass[...] = add(down_mine[1], down_in[1]).astype(BF16)
        pass_down.start()

    @pl.when(i == 1)
    def _():
        for t in range(4):
            at = t * 2 * two
            to = 4 * two + t * one_head
            grad_f[:, t * two:(t + 1) * two] = acc_far[:, at:at + two].astype(BF16)
            grad_f[:, to:to + one_head] = acc_far[:, at + two + one_head:at + 2 * two].astype(BF16)
            grad_single[:, t * one_head:(t + 1) * one_head] = acc_far[:, at + two:at + two + one_head].astype(BF16)
        for copy in sent_far:
            copy.start()
        loaded[0].wait()
        for j in range(4):
            sent_up[j].wait_recv()
            up_low[j] = add(up_mine[j, 0], up_side[0, j]).astype(BF16)
        for copy in sent_low:
            copy.start()

    @pl.when(i >= 2)
    def _():
        part = back_step(dims, 1, lens, whose, dattn, normed, qkv_own, mixed_own, dm_own, dq_own, acc_own, cols_own,
                         w_own, o_own)
        total = part.reshape(quarter, slab, model) + dn[i - 2]

        @pl.when(i == 2)
        def _():
            n_send[...] = total.astype(BF16)
            sent_n.start()
            for copy in sent_low:
                copy.wait_recv()
            up_pass[...] = add(up_low[here.z_far], up_in[1]).astype(BF16)
            pass_low.start()

        @pl.when(i == 3)
        def _():
            whole[...] = total

    @pl.when(i == 3)
    def _():
        grad_pair[...] = acc_own[...].astype(BF16)
        sent_n.wait_recv()
        whole[...] += n_recv[...].astype(F32)
        down_out[...] = add(down_mine[0], down_in[0])
        for j in range(4):
            sent_far[j].wait_recv()
            far_sum[j] = add(grad_f[block(2 * j + here.x), :], from_side[j]).astype(BF16)
        pass_down.wait_recv()
        down_out[...] += down_last[...].astype(F32)
        for j in range(4):
            sent_up[4 + j].wait_recv()
            up_one[j] = add(up_mine[j, 1], up_side[1, j]).astype(BF16)
        pass_low.wait_recv()
        up_out[...] = add(up_low[here.z], up_in[0], up_last[...])
        for copy in sent_near:
            copy.wait_recv()
        for copy in sent_near + sent_up + sent_down + sent_far + sent_low + [pass_down, pass_low, sent_n]:
            copy.wait_send()


def back(dims, lens, d_own, d_peer, normed, qkv_far, mixed_far, qkv_own, mixed_own, wq, wo, wf,
         fin_img, fin_txt, up_keep, up_send, down_sum):
    model = normed.shape[-1]
    slab, quarter = dims.slab, dims.quarter
    hidden = up_keep.shape[-1]
    piece = model // 8
    held = pl.BlockSpec(memory_space=pltpu.VMEM)
    away = pl.BlockSpec(memory_space=pl.ANY)
    spec = lambda cols, at: pl.BlockSpec((quarter, slab, cols), lambda i: (at(i), 0, 0))
    early, late = lambda i: jnp.maximum(1 - i, 0), lambda i: jnp.where(i < 3, 1, 0)
    rows = (quarter, slab, model)
    outs = [(held, rows, F32), (held, (model, 512), BF16), (held, (model, 256), BF16),
            (held, (1, 768), F32), (held, (1, 384), F32),
            (away, fin_img.shape, BF16), (away, fin_txt.shape, BF16),
            (held, (4, piece, model), BF16), (held, (4, piece, hidden), BF16),
            (held, (2, piece, hidden), F32), (held, (piece, hidden), F32)]
    slabs = lambda cols: pltpu.VMEM((quarter, slab, cols), BF16)
    return pl.pallas_call(
        functools.partial(back_kernel, dims),
        grid=(4,),
        in_specs=[pl.BlockSpec(memory_space=pltpu.SMEM), held, held, spec(model, lambda i: 1 - i % 2),
                  spec(768, early), spec(256, early), spec(384, late), spec(128, late), held, held, held]
        + [away] * 5,
        out_specs=[v[0] for v in outs],
        out_shape=[jax.ShapeDtypeStruct(v[1], v[2]) for v in outs],
        scratch_shapes=[
            slabs(model), slabs(256), slabs(128), slabs(768), slabs(384),
            pltpu.VMEM((model, 1024), F32), pltpu.VMEM((model, 512), F32),
            pltpu.VMEM((768, model), BF16), pltpu.VMEM((384, model), BF16),
            pltpu.VMEM((256, model), BF16), pltpu.VMEM((128, model), BF16),
            pltpu.VMEM((2,) + rows, F32), pltpu.VMEM((model, model), BF16),
            pltpu.VMEM((4, 2, piece, hidden), BF16), pltpu.VMEM((2, 4, piece, hidden), BF16),
            pltpu.VMEM((4, piece, hidden), BF16), pltpu.VMEM((2, piece, hidden), BF16),
            pltpu.VMEM((piece, hidden), BF16), pltpu.VMEM((piece, hidden), BF16),
            pltpu.VMEM((2, 2, piece, hidden), BF16), pltpu.VMEM((2, 2, piece, hidden), BF16),
            pltpu.VMEM((2, piece, hidden), BF16), pltpu.VMEM((2, piece, hidden), BF16),
            pltpu.VMEM(rows, BF16), pltpu.VMEM(rows, BF16), pltpu.VMEM((4, piece, model), BF16),
            pltpu.SemaphoreType.DMA((3,)), pltpu.SemaphoreType.DMA((21,)), pltpu.SemaphoreType.DMA((21,)),
        ],
        compiler_params=params(collective_id=4, has_side_effects=True),
        cost_estimate=pl.CostEstimate(
            flops=24 * quarter * slab * model * 1152, bytes_accessed=30_000_000, transcendentals=0),
        name="back",
    )(lens, d_own, d_peer, normed, qkv_far, mixed_far, qkv_own, mixed_own, wq, wo, wf,
      fin_img, fin_txt, up_keep, up_send, down_sum)


V_ROWS, V_MP, V_HEADS, V_FAR = 24, 11, 13, 15


def finish_kernel(dims, dnormed, dattended, states_img, states_txt, vec, fin_img, fin_txt,
                  near_img, near_txt, grad_pair, grad_single, grad_far, up_one, own_sums, up_sums, cols_own, cols_far,
                  core_img, core_txt, across_img, across_txt, back_img, back_txt, grad_out, v_out, up_out,
                  s_img, s_txt, d_img, d_txt, rows, xr, zs, z_in, z_pass, z_last, f_in, f_pass, f_last, u_in, u_pass, u_last, far_sum, far_recv, vs, vr,
                  local_sem, send_sem, recv_sem):
    quarter = dims.quarter
    here = Place()
    z, x, m = here.z, here.x, here.m
    near_quarter = here.quarter(1, 0)
    used = [0]

    def send(src, dst, device):
        at = used[0]
        used[0] += 1
        return remote(src, dst, send_sem, recv_sem, at, device)

    loaded = [pltpu.make_async_copy(states_img.at[pl.ds(m * quarter, quarter)], s_img, local_sem.at[0]),
              pltpu.make_async_copy(states_txt.at[pl.ds(m * quarter, quarter)], s_txt, local_sem.at[1])]
    for copy in loaded:
        copy.start()
    meet([here.core, here.near, here.side, here.paired, here.opposite])

    piece = xr.shape[1]
    wide = grad_pair.shape[1]
    spans = ((grad_pair, 0, wide), (grad_single, wide, xr.shape[2]))
    block = lambda j: pl.ds(pl.multiple_of(j * piece, piece), piece)
    x_copies = []
    for j in range(4):
        for src, lo, hi in spans:
            x_copies.append(send(src.at[block(2 * j + 1 - x)], xr.at[j, :, pl.ds(lo, hi - lo)], here.side))
            x_copies[-1].start()
    add = lambda *parts: functools.reduce(lambda p, q: p + q, [v.astype(F32) for v in parts])
    in_pair = lambda src, dst: [send(src.at[here.z_pair], dst.at[0], here.paired),
                                send(src.at[here.z_rest], dst.at[1], here.paired)]
    far_copies = in_pair(grad_far, f_in)
    up_copies = in_pair(up_one, u_in)
    for copy in far_copies + up_copies:
        copy.start()

    fin_remote = [send(src, dst, here.core) for src, dst in (
        (fin_img, core_img), (fin_txt, core_txt), (near_img, across_img), (near_txt, across_txt))]

    rows[...] = jnp.zeros_like(rows)
    for copy in loaded:
        copy.wait()
    total = [jnp.zeros((1, rows.shape[1]), F32)] * 2
    back_local, to_near, to_other = [], [], []
    for p in range(quarter):
        load_rows(dims, p, s_img, s_txt, rows)
        n, r = normalise(rows[...])
        dy = dnormed[p]
        total[0] = total[0] + jnp.sum(dy * n, axis=0, keepdims=True)
        total[1] = total[1] + jnp.sum(dy, axis=0, keepdims=True)
        d = dattended[p] + norm_back(n, r, dy * vector(vec, GAIN1))
        d_img[p] = d[0:dims.patches].astype(BF16)
        d_txt[p] = d[dims.ip:dims.ip + dims.caption].astype(BF16)
        for j, (src, dst) in enumerate(((d_img, back_img), (d_txt, back_txt))):
            at = dst.at[m * quarter + p]
            to_near.append(send(src.at[p], at, here.near))
            to_near[-1].start()
            to_other.append(send(src.at[p], at, here.core))
            to_other[-1].start()
            back_local.append(pltpu.make_async_copy(src.at[p], at, local_sem.at[2 + 2 * p + j]))
            back_local[-1].start()
    for copy in fin_remote:
        copy.start()

    at = lax.broadcasted_iota(jnp.int32, (V_ROWS, 1), 0)
    two, one_head = parts_of(dims)
    vs[0] = jnp.zeros(vs.shape[1:], F32)
    vs[0, 0:1, :] = total[0]
    vs[0, 1:2, :] = total[1]
    vs[0, 2:V_MP, :] = own_sums[0:V_MP - 2, :]
    vs[0, V_MP:V_HEADS, :] = up_sums[...]
    for j in range(2):
        own_at, far_at = 2 * j * two, 4 * j * two
        vs[0, V_HEADS + j:V_HEADS + j + 1, 0:two] = cols_own[0:1, own_at:own_at + two]
        vs[0, V_HEADS + j:V_HEADS + j + 1, two:two + one_head] = cols_far[0:1, far_at + two:far_at + two + one_head]
        vs[0, V_FAR + j:V_FAR + j + 1, 0:two] = cols_far[0:1, far_at:far_at + two]
        vs[0, V_FAR + j:V_FAR + j + 1, two:two + one_head] = cols_far[0:1, far_at + two + one_head:far_at + 2 * two]
    v = vs[0]
    v_copies = []

    def exchange(step, value, device):
        vs[step] = value
        copy = send(vs.at[step], vr.at[step], device)
        copy.start()
        copy.wait_recv()
        v_copies.append(copy)
        return vr[step]

    v = v + jnp.where(at < V_MP, exchange(0, v, here.core), 0.0)
    for copy in far_copies:
        copy.wait_recv()
    f_pass[...] = add(grad_far[here.z_far], f_in[1]).astype(BF16)
    far_copies.append(send(f_pass, f_last, here.opposite))
    far_copies[-1].start()
    v = v + exchange(1, v, here.side)
    for copy in up_copies:
        copy.wait_recv()
    u_pass[...] = add(up_one[here.z_far], u_in[1]).astype(BF16)
    v = v + exchange(2, v, here.paired)
    vs[3] = v
    v_far = send(vs.at[3], vr.at[3], here.opposite)
    v_far.start()
    up_copies.append(send(u_pass, u_last, here.opposite))
    up_copies[-1].start()

    def own_sum(j, k):
        src, lo, hi = spans[k]
        return src[block(2 * j + x), :].astype(F32) + xr[j, :, lo:hi].astype(F32)

    for copy in x_copies:
        copy.wait_recv()
    for j in range(4):
        for k, (src, lo, hi) in enumerate(spans):
            zs[j, :, lo:hi] = own_sum(j, k).astype(BF16)
    z_copies = in_pair(zs, z_in)
    for copy in z_copies:
        copy.start()

    far_copies[-1].wait_recv()
    far_sum[...] = add(grad_far[z], f_in[0], f_last[...]).astype(BF16)
    far_copy = send(far_sum, far_recv, here.near)
    far_copy.start()
    v_far.wait_recv()
    v = v + vr[3]
    up_copies[-1].wait_recv()
    up_out[...] = add(up_one[z], u_in[0], u_last[...])
    for copy in z_copies:
        copy.wait_recv()
    z_pass[...] = add(zs[here.z_far], z_in[1]).astype(BF16)
    z_copies.append(send(z_pass, z_last, here.opposite))
    z_copies[-1].start()
    vs[4] = v
    v_near = send(vs.at[4], vr.at[4], here.near)
    v_near.start()
    for copy in back_local:
        copy.wait()
    onward = []
    for p in range(quarter):
        for j, dst in enumerate((back_img, back_txt)):
            to_near[2 * p + j].wait_recv()
            at_near = dst.at[near_quarter * quarter + p]
            onward.append(send(at_near, at_near, here.core))
            onward[-1].start()
    far_copy.wait_recv()
    z_copies[-1].wait_recv()
    for k, (src, lo, hi) in enumerate(spans):
        grad_out[:, lo:hi] = own_sum(z, k) + add(
            far_recv[:, lo:hi], z_in[0, :, lo:hi], z_last[:, lo:hi])
    v_near.wait_recv()
    there = vr[4]
    v_out[...] = v + jnp.where(at < V_MP, there, 0.0)
    v_out[V_HEADS:V_HEADS + 2, :] = v[V_HEADS:V_HEADS + 2, :] + there[V_FAR:V_FAR + 2, :]
    for copy in to_other + fin_remote + onward:
        copy.wait()
    for copy in x_copies + far_copies + to_near + z_copies + v_copies + up_copies + [far_copy, v_near, v_far]:
        copy.wait_send()


def finish(dims, dnormed, dattended, states_img, states_txt, vec, fin_img, fin_txt,
           near_img, near_txt, grad_pair, grad_single, grad_far, up_one, *tables):
    pairs, patches, model = states_img.shape
    caption = states_txt.shape[1]
    quarter, slab = dims.quarter, dims.slab
    piece, cols = grad_far.shape[1:]
    held = pl.BlockSpec(memory_space=pltpu.VMEM)
    away = pl.BlockSpec(memory_space=pl.ANY)
    n_remote = 7 * quarter + 28
    return pl.pallas_call(
        functools.partial(finish_kernel, dims),
        in_specs=[held, held] + [away] * 2 + [held] + [away] * 4 + [held] * 8,
        out_specs=[away] * 6 + [held] * 3,
        out_shape=[jax.ShapeDtypeStruct(v.shape, BF16) for v in (fin_img, fin_txt) * 2] + [
            jax.ShapeDtypeStruct((pairs, patches, model), BF16),
            jax.ShapeDtypeStruct((pairs, caption, model), BF16),
            jax.ShapeDtypeStruct((piece, cols), F32),
            jax.ShapeDtypeStruct((V_ROWS, model), F32),
            jax.ShapeDtypeStruct(up_one.shape[1:], F32),
        ],
        scratch_shapes=[
            pltpu.VMEM((quarter, patches, model), BF16),
            pltpu.VMEM((quarter, caption, model), BF16),
            pltpu.VMEM((quarter, patches, model), BF16),
            pltpu.VMEM((quarter, caption, model), BF16),
            pltpu.VMEM((slab, model), F32),
            pltpu.VMEM((4, piece, cols), BF16), pltpu.VMEM((4, piece, cols), BF16),
        ] + [pltpu.VMEM((2, piece, cols), BF16), pltpu.VMEM((piece, cols), BF16), pltpu.VMEM((piece, cols), BF16)] * 2 + [
            pltpu.VMEM((2,) + up_one.shape[1:], BF16), pltpu.VMEM(up_one.shape[1:], BF16), pltpu.VMEM(up_one.shape[1:], BF16),
            pltpu.VMEM((piece, cols), BF16), pltpu.VMEM((piece, cols), BF16),
            pltpu.VMEM((5, V_ROWS, model), F32),
            pltpu.VMEM((5, V_ROWS, model), F32),
            pltpu.SemaphoreType.DMA((2 + 2 * quarter,)),
            pltpu.SemaphoreType.DMA((n_remote,)),
            pltpu.SemaphoreType.DMA((n_remote,)),
        ],
        compiler_params=params(collective_id=1, has_side_effects=True),
        name="finish",
    )(dnormed, dattended, states_img, states_txt, vec, fin_img, fin_txt,
      near_img, near_txt, grad_pair, grad_single, grad_far, up_one, *tables)


def spread_kernel(dims, cols, sums, grad, gains, shifts, up_low, up_high, down, head_in, dproj, *refs):
    forward, refs = refs[:8], refs[8:]
    back_img, back_txt, *refs = refs
    outs, refs = refs[:12], refs[12:]
    (qkv, out_w, up_out, down_out, head_out, out_img, out_txt, grad_img, grad_txt,
     turned, held_img, held_txt, in_sem, out_sem) = refs
    here = Place()
    quarter = dims.quarter
    whose = [here.quarter(0, 0), here.quarter(1, 0), here.quarter(0, 1), here.quarter(1, 1)]
    place = lambda q: pl.ds(q * quarter, quarter)
    comes, goes = [], []
    for r in range(4):
        for j, (held, src, dst, back, to) in enumerate((
            (held_img, forward[2 * r], out_img, back_img, grad_img), (held_txt, forward[2 * r + 1], out_txt, back_txt, grad_txt),
        )):
            for k, (source, target, q) in enumerate(((src, dst, whose[r]), (back.at[place(r)], to, r))):
                at = 4 * r + 2 * j + k
                comes.append(pltpu.make_async_copy(source, held.at[2 * r + k], in_sem.at[at]))
                goes.append(pltpu.make_async_copy(held.at[2 * r + k], target.at[place(q)], out_sem.at[at]))
    for copy in comes:
        copy.start()
    turn_by = sums.shape[1] - here.b * cols

    def slice_of(value):
        return pltpu.roll(value, turn_by, 1)[:, 0:cols]

    mine = slice_of(sums[...])
    for out, (lo, count) in zip(outs[:8], ((0, 1), (1, 1), (7, 1), (6, 1), (2, 2), (4, 2), (9, 2), (8, 1))):
        out[...] = mine[lo:lo + count, :]
    wide = jnp.concatenate([gains[...], shifts[...], jnp.zeros((4, sums.shape[1]), F32)], axis=0)
    heads = slice_of(wide)
    outs[8][...] = heads[0:2, :]
    outs[9][...] = heads[2:4, :]
    outs[10][...] = sums[V_MP:V_MP + 2, :]
    outs[11][...] = sums[V_HEADS:V_HEADS + 2, 0:outs[11].shape[1]]
    two, one = 2 * HEAD_DIM, HEAD_DIM
    for t in range(3):
        qkv[t, :, 0:two] = grad[:, t * two:(t + 1) * two]
        qkv[t, :, two:two + one] = grad[:, 4 * two + t * one:4 * two + (t + 1) * one]
    turned[...] = jnp.zeros_like(turned)
    turned[0:cols, 0:two] = grad[:, 3 * two:4 * two]
    turned[0:cols, two:two + one] = grad[:, 4 * two + 3 * one:4 * two + 4 * one]
    out_w[...] = turned[...].T[0:two + one, 0:cols]
    up_out[0] = up_low[...]
    up_out[1] = up_high[...]
    down_out[...] = down[...]
    for come, go in zip(comes, goes):
        come.wait()
        go.start()
    for m in range(2):
        part = pltpu.roll(head_in[m].astype(F32), turn_by, 1)[:, 0:128].astype(BF16)
        head_out[m] = t_dot(part, dproj[m])[0:cols]
    for go in goes:
        go.wait()


def spread(dims, sums, grad, gains, shifts, up_low, up_high, down, head_in, dproj, forward, back_img, back_txt):
    cols, model = grad.shape[0], sums.shape[1]
    local, quarter = dims.local, dims.quarter
    assert cols <= 128
    shapes = [(1, cols)] * 4 + [(2, cols)] * 3 + [(1, cols)] + [(2, cols)] * 2 + [(2, model), (2, local)]
    shapes += [(3, cols, local), (local, cols), (2,) + up_low.shape, down.shape, (2, cols, dproj.shape[2])]
    held = pl.BlockSpec(memory_space=pltpu.VMEM)
    away = pl.BlockSpec(memory_space=pl.ANY)
    args = (sums, grad, gains, shifts, up_low, up_high, down, head_in, dproj)
    return pl.pallas_call(
        functools.partial(spread_kernel, dims, cols),
        in_specs=[held] * len(args) + [away] * 10,
        out_specs=[held] * len(shapes) + [away] * 4,
        out_shape=[jax.ShapeDtypeStruct(v, F32) for v in shapes]
        + [jax.ShapeDtypeStruct(v.shape, BF16) for v in (back_img, back_txt) * 2],
        scratch_shapes=[
            pltpu.VMEM((128, 256), F32),
            pltpu.VMEM((8, quarter, dims.patches, model), BF16), pltpu.VMEM((8, quarter, dims.caption, model), BF16),
            pltpu.SemaphoreType.DMA((16,)), pltpu.SemaphoreType.DMA((16,)),
        ],
        compiler_params=params(),
        cost_estimate=pl.CostEstimate(flops=1_000_000, bytes_accessed=20_000_000, transcendentals=0),
        name="spread",
    )(*args, *forward, back_img, back_txt)


def per_device(
    image_states, text_states, caption_lengths, image_cotangent, text_cotangent,
    first_gain, first_shift, query_key_value, query_value_bias, output_weight, output_bias,
    attention_scale, expert_gain, expert_shift, expert_up, expert_up_bias, expert_down,
    expert_down_bias, feedforward_scale, head_gain, head_shift, head_weight, logit_scale,
):
    pairs, patches, model = image_states.shape
    caption = text_states.shape[1]
    local = query_key_value.shape[2]
    quarter = pairs // 4
    batch_size = lax.axis_size("batch")
    assert lax.axis_size("mp") == 4 and pairs == 4 * quarter and quarter <= 3
    assert batch_size & (batch_size - 1) == 0
    assert local == 3 * HEAD_DIM
    ip, tp = up16(patches), up16(caption)
    dims = Dims(patches, caption, ip, tp, ip + tp, quarter, local)
    me = lax.axis_index("mp")
    batch_at = lax.axis_index("batch")
    order = me ^ jnp.asarray(ORDER, jnp.int32)
    vectors = (first_gain, first_shift, attention_scale, output_bias, expert_gain, expert_shift,
               feedforward_scale, expert_down_bias, head_gain, head_shift)
    own_w = jnp.transpose(query_key_value, (1, 2, 0)).reshape(3 * local, model)
    one_kernel = batch_size == 8 and model // batch_size % 32 == 0 and expert_up.shape[2] == model
    if one_kernel:
        (vec, normed, qkv_own, mixed_own, qkv_far, mixed_far, wf, attended, attn, e_own, e_peer, cls_own, cls_peer) = front(
            dims, caption_lengths, image_states, text_states, vectors, query_value_bias, own_w, output_weight)
    else:
        vec = jnp.concatenate([v.reshape(-1, model) for v in vectors] + [jnp.zeros((1, model), F32)])
        wo = jnp.concatenate([own_w, output_weight])
        wf = to_y(wo)
        far_bias = to_y(query_value_bias)
        normed, qkv_own, rest, mixed_own = attend_own(
            dims, order, caption_lengths, image_states, text_states, vec, query_value_bias, wo)
        qkv_far, mixed_far, a_keep, a_send = attend_far(
            dims, order, caption_lengths, normed, rest, mixed_own, far_bias, wo, wf)
        a_recv = to_core(a_send)
        attended, attn, e_own, cls_own = residual(
            dims, order, a_keep, a_recv, image_states, text_states, vec)
        e_peer = to_core(e_own)
        cls_peer = to_core(cls_own)
    if one_kernel:
        (act, dup, ddn, dexp, d_own, d_near, up_sums, class_e, c_act, c_dup, c_ddn, dcls, head_in, dproj,
         grad_head_gain, grad_head_shift, scalars) = middle(
            dims, pairs * batch_size, image_cotangent, text_cotangent, e_own, e_peer, cls_own, cls_peer, vec,
            expert_up, expert_up_bias, expert_down, head_weight, logit_scale.reshape(1, 1))
        down_sum, up_keep, up_send, dattended, dattn, dattn_peer, fin_img, fin_txt, own_sums = turn(
            dims, image_cotangent, text_cotangent, e_peer, e_own, act, dup, ddn, class_e, c_act, c_dup, c_ddn,
            dexp, attended, attn, d_own, d_near, dcls, vec)
    else:
        class_part, class_e = class_forward(dims, cls_own, cls_peer, expert_up, expert_up_bias, expert_down)
        class_parts = from_others(class_part, "mp", 1, 4)

        act_a, dup_a, ddn_a, d_send3, d_keep1, x_send3, x_keep1, bias_a, cot_a = experts(
            dims, "experts_a", 1, order[jnp.asarray([3, 1])], e_peer, e_own, image_cotangent, text_cotangent,
            tie(vec, class_part), expert_up, expert_up_bias, expert_down)
        x_recv1 = to_core(x_send3)
        d_recv1 = to_core(d_send3)
        final_class = class_final(
            dims, order, cls_own, cls_peer, class_parts, tie(vec, bias_a))
        class_blocks = gather_batch(final_class[None])
        x_near = add_low(x_keep1, x_recv1)
        x_far = to_y(x_near)
        act_b, dup_b, ddn_b, d_send2, d_keep0, x_send2, x_keep0, bias_b, cot_b = experts(
            dims, "experts_b", 0, order[jnp.asarray([2, 0])], e_peer, e_own, image_cotangent, text_cotangent,
            tie(vec, final_class, x_near), expert_up, expert_up_bias, expert_down)
        x_recv0 = to_core(x_send2)
        d_recv0 = to_core(d_send2)

        head_in, dproj, dclass, grad_head_gain, grad_head_shift, scalars = (contrast if batch_size <= 8 else contrast_large)(
            dims, pairs * batch_size, batch_at.reshape(1), class_blocks, tie(vec, bias_b), head_weight,
             logit_scale.reshape(1, 1))
        c_act, c_dup, c_ddn, c_dexp, c_bias, dcls = class_back(
            dims, order, class_e, cot_a, cot_b, dclass, vec, expert_up, expert_up_bias, expert_down)
        extras = from_others(c_dexp, "mp", 1, 4)
        d_far = to_y(add_low(d_keep1, tie(d_recv1, c_dexp)))
        expert_grad = expert_grads(
            dims, e_peer, e_own, act_a, dup_a, ddn_a, act_b, dup_b, ddn_b, class_e, c_act, c_dup, c_ddn)
        expert_sum = lax.psum_scatter(expert_grad, "batch", scatter_dimension=1, tiled=True)

        dattended, dattn, sums_two = norm_two(
            dims, order, x_keep0, x_recv0, x_far, attended, a_keep, a_recv, image_cotangent, text_cotangent,
            dcls, extras, tie(vec, expert_grad))
        dattn_peer = to_core(dattn)
        fin_img, fin_txt, sums_fin = final_rows(
            dims, order, d_keep0, d_recv0, d_far, attended, image_cotangent, text_cotangent, dcls,
            tie(vec, sums_two))
        own_sums = jnp.concatenate([sums_two[:6], sums_fin[:3]])
        up_sums = bias_a + bias_b + c_bias
    contrast_loss = scalars[0, :1]
    grad_logit_scale = scalars[1, :1]
    if one_kernel:
        (dnormed, grad_o01, grad_o2, cols_far, cols_own, near_img, near_txt, far_sum, up_one, grad_down,
         up_low) = back(
            dims, caption_lengths, dattn, dattn_peer, normed, qkv_far, mixed_far, qkv_own, mixed_own,
            own_w, output_weight, wf, fin_img, fin_txt, up_keep, up_send, down_sum)
    else:
        n_keep, n_send, grad_far, grad_o2, cols_far = attend_back(
            dims, True, order, caption_lengths, dattn, dattn_peer, normed, qkv_far, mixed_far, own_w, output_weight, wf)
        n_keep, n_send, grad_o01, cols_own = attend_back(
            dims, False, order, caption_lengths, dattn, dattn_peer, normed, qkv_own, mixed_own, own_w, output_weight, wf,
            prior=(n_keep, n_send))
    cols = model // batch_size
    mine = lambda v, axis: lax.dynamic_slice_in_dim(v, batch_at * cols, cols, axis=axis)
    pair, single = 2 * HEAD_DIM, HEAD_DIM
    if one_kernel:
        core_img, core_txt, across_img, across_txt, back_img, back_txt, attn_grad, sums, up_high = finish(
            dims, dnormed, dattended, image_states, text_states, vec, fin_img, fin_txt,
            near_img, near_txt, grad_o01, grad_o2, far_sum, up_one, own_sums, up_sums, cols_own, cols_far)
        forward = (fin_img, fin_txt, near_img, near_txt, core_img, core_txt, across_img, across_txt)
        (*vectors, grad_qkv, grad_output_weight, grad_up, grad_down, grad_head_weight,
         image_output, text_output, image_grad, text_grad) = spread(
            dims, sums, attn_grad, grad_head_gain, grad_head_shift, up_low, up_high, grad_down, head_in, dproj,
            forward, back_img, back_txt)
        flat = lambda v: v.reshape(-1)
        return (
            image_output,
            text_output,
            contrast_loss,
            image_grad,
            text_grad,
            flat(vectors[0]),
            flat(vectors[1]),
            jnp.transpose(grad_qkv, (1, 0, 2)),
            vectors[11],
            grad_output_weight,
            flat(vectors[2]),
            flat(vectors[3]),
            vectors[4],
            vectors[5],
            grad_up,
            vectors[10],
            jnp.transpose(grad_down, (0, 2, 1)),
            vectors[6],
            flat(vectors[7]),
            vectors[8],
            vectors[9],
            grad_head_weight,
            grad_logit_scale,
        )
    else:
        grad_head_weight = jnp.einsum("mnc,mne->mce", mine(head_in, 2), dproj, preferred_element_type=F32)
        grad_expert_up = expert_sum[:2].astype(F32)
        grad_expert_down = jnp.transpose(expert_sum[2:].astype(F32), (0, 2, 1))
        cols_own = cols_own.reshape(3, pair)[::2]
        cols_far = cols_far.reshape(3, 2 * pair)[::2]
        heads = jnp.concatenate([cols_own, cols_far[:, pair:pair + single]], axis=1)
        heads_far = jnp.concatenate([cols_far[:, :pair], cols_far[:, pair + single:]], axis=1)
        n_recv = to_core(n_send)
        d_img, d_txt, sums_one = norm_one(
            dims, order, n_keep, n_recv, dattended, image_states, text_states, vec)
        image_output = gather_rows(fin_img, me)
        text_output = gather_rows(fin_txt, me)
        image_grad = gather_rows(d_img, me)
        text_grad = gather_rows(d_txt, me)
        grad_own = jnp.concatenate([grad_o01, grad_o2], axis=1)
        grad_far = lax.psum_scatter(grad_far, "batch", scatter_dimension=0, tiled=True)
        grad_own = lax.psum_scatter(grad_own, "batch", scatter_dimension=0, tiled=True)
        attn_grad = grad_own.astype(F32) + to_y(grad_far).astype(F32)
        heads = heads + to_y(heads_far)
        own_sums = sum_over(jnp.concatenate([sums_one[:2], own_sums]), "mp")
        flat = jnp.concatenate([own_sums.reshape(-1), heads.reshape(-1), up_sums.reshape(-1)])
        count = flat.shape[0]
        flat = jnp.pad(flat, (0, -count % 1024)).reshape(-1, 128)
        flat = sum_over(flat, "batch").reshape(-1)[:count]
        done = own_sums.shape[0]
        own_sums = mine(flat[:done * model].reshape(done, model), 1)
        heads = flat[done * model:done * model + 2 * local].reshape(2, local)
        grad_expert_up_bias = flat[done * model + 2 * local:].reshape(up_sums.shape)
    attn_grad = jnp.concatenate(
        [attn_grad[:, :4 * pair].reshape(cols, 4, pair), attn_grad[:, 4 * pair:].reshape(cols, 4, single)], axis=2)
    grad_query_key_value = attn_grad[:, :3]
    grad_output_weight = jnp.transpose(attn_grad[:, 3])
    return (
        image_output,
        text_output,
        contrast_loss,
        image_grad,
        text_grad,
        own_sums[0],
        own_sums[1],
        grad_query_key_value,
        heads,
        grad_output_weight,
        own_sums[7],
        own_sums[6],
        own_sums[2:4],
        own_sums[4:6],
        grad_expert_up,
        grad_expert_up_bias,
        grad_expert_down,
        own_sums[9:11],
        own_sums[8],
        mine(grad_head_gain, 1),
        mine(grad_head_shift, 1),
        grad_head_weight,
        grad_logit_scale,
    )


def solution(mesh):
    return jax.shard_map(
        per_device,
        mesh=mesh,
        in_specs=(
            P("batch", None, None),
            P("batch", None, None),
            P("batch"),
            P("batch", None, None),
            P("batch", None, None),
            P(),
            P(),
            P(None, None, "mp"),
            P(None, "mp"),
            P("mp", None),
            P(),
            P(),
            P(),
            P(),
            P(None, None, "mp"),
            P(None, "mp"),
            P(None, "mp", None),
            P(),
            P(),
            P(),
            P(),
            P(),
            P(),
        ),
        out_specs=(
            P("batch", None, None),
            P("batch", None, None),
            P(),
            P("batch", None, None),
            P("batch", None, None),
            P("batch"),
            P("batch"),
            P("batch", None, "mp"),
            P(None, "mp"),
            P("mp", "batch"),
            P("batch"),
            P("batch"),
            P(None, "batch"),
            P(None, "batch"),
            P(None, "batch", "mp"),
            P(None, "mp"),
            P(None, "mp", "batch"),
            P(None, "batch"),
            P("batch"),
            P(None, "batch"),
            P(None, "batch"),
            P(None, "batch", None),
            P(),
        ),
        check_vma=False,
    )
```

```python
import functools
from typing import NamedTuple

import jax
import jax.numpy as jnp
from jax import lax
from jax.experimental import pallas as pl
from jax.experimental.pallas import tpu as pltpu
from jax.sharding import PartitionSpec as P

HEAD_DIM = 64
F32 = jnp.float32
BF16 = jnp.bfloat16
NEG = -1e9
EPS = 1e-5
ORDER = (0, 2, 1, 3)

VMEM_LIMIT = 60 * 1024 * 1024


def params(**kw):
    return pltpu.CompilerParams(vmem_limit_bytes=VMEM_LIMIT, **kw)


def up16(n):
    return -(-n // 16) * 16


def dot(a, b):
    return jnp.dot(a, b, preferred_element_type=F32)


def dot_t(a, b):
    return lax.dot_general(a, b, (((1,), (1,)), ((), ())), preferred_element_type=F32)


def t_dot(a, b):
    return lax.dot_general(a, b, (((0,), (0,)), ((), ())), preferred_element_type=F32)


def normalise(x):
    c = x - jnp.mean(x, axis=-1, keepdims=True)
    v = jnp.mean(c * c, axis=-1, keepdims=True)
    r = lax.rsqrt(v + EPS)
    return c * r, r


def norm_back(n, r, dn):
    a = jnp.mean(dn, axis=-1, keepdims=True)
    b = jnp.mean(dn * n, axis=-1, keepdims=True)
    return (dn - a - n * b) * r


def gelu_parts(u):
    big = 0.5 * (1.0 + lax.erf(u * 0.7071067811865476))
    small = 0.3989422804014327 * jnp.exp(-0.5 * u * u)
    return big, small


def gelu_low(u):
    return (u * (0.5 * (1.0 + lax.erf(u * 0.7071067811865476)))).astype(BF16)


def softmax_rows(scores):
    m = jnp.max(scores, axis=-1, keepdims=True)
    e = jnp.exp(scores - m)
    return e * (1.0 / jnp.sum(e, axis=-1, keepdims=True))


def tie(value, *after):
    return lax.optimization_barrier((value,) + after)[0]


def load_rows(dims, p, img, txt, rows):
    rows[0:dims.patches, :] = img[p].astype(F32)
    rows[dims.ip:dims.ip + dims.caption, :] = txt[p].astype(F32)


def spec_whole(a):
    return pl.BlockSpec(a.shape, lambda *_: (0,) * a.ndim)


class Dims(NamedTuple):
    patches: int
    caption: int
    ip: int
    tp: int
    slab: int
    quarter: int
    local: int


GAIN1, SHIFT1, A_SCALE, A_BIAS, GAIN2, SHIFT2, F_SCALE, F_BIAS, H_GAIN, H_SHIFT = 0, 1, 2, 3, 4, 6, 8, 9, 11, 13


def vector(table, at, count=1):
    return table[at:at + count, :]


def copy_rows(dst, at, src, start, count):
    dst[at:at + count, :] = src[start:start + count, :]


def parts_of(dims):
    return 2 * HEAD_DIM, HEAD_DIM


def key_tail(dims, length):
    at = dims.patches // 16 * 16
    return ((0, dims.ip, at, dims.patches), (dims.ip, dims.slab, 0, length))


def hide(scores, start, limit):
    if start >= scores.shape[0]:
        return scores
    tail = scores[start:]
    at = start + lax.broadcasted_iota(jnp.int32, (tail.shape[0], 1), 0)
    tail = jnp.where(at < limit, tail, NEG)
    return tail if start == 0 else jnp.concatenate([scores[:start], tail], axis=0)


def split_pair(value):
    low = lax.broadcasted_iota(jnp.int32, (1, 128), 1) < HEAD_DIM
    zero = jnp.zeros_like(value)
    return jnp.concatenate([jnp.where(low, value, zero), jnp.where(low, zero, value)], axis=0)


def join_pair(value):
    low = lax.broadcasted_iota(jnp.int32, (1, 128), 1) < HEAD_DIM
    half = value.shape[0] // 2
    return jnp.where(low, value[:half], value[half:])


def softmax_keys(scores):
    e = jnp.exp(scores - jnp.max(scores, axis=0, keepdims=True))
    return e * (1.0 / jnp.sum(e, axis=0, keepdims=True))


def pair_weights(q, k, start, limit):
    return softmax_keys(hide(dot_t(k, split_pair(q)), start, limit))


def scaled(q):
    return q * jnp.asarray(HEAD_DIM ** -0.5, BF16)


def attend_tiles(dims, lens, quarter_at, qkv, mixed):
    tiles = mixed.shape[-1] // 128

    def one_pair(p, c):
        length = lens[quarter_at * dims.quarter + p]
        for lo, hi, start, limit in key_tail(dims, length):
            for g in range(tiles):
                q, k, v = [qkv[p, lo:hi, (t * tiles + g) * 128:(t * tiles + g + 1) * 128] for t in range(3)]
                w = pair_weights(scaled(q), k, start, limit).astype(BF16)
                mixed[p, lo:hi, g * 128:(g + 1) * 128] = join_pair(t_dot(w, v)).astype(BF16)
        return c

    lax.fori_loop(0, dims.quarter, one_pair, 0)


def attend_own_kernel(dims, order, lens, img, txt, vec, bias, wo, normed, qkv, rest, mixed, rows, w, b):
    i = pl.program_id(0)
    local = dims.local
    two, one_head = parts_of(dims)

    @pl.when(i == 0)
    def _():
        rows[...] = jnp.zeros_like(rows)
        w[...] = jnp.zeros_like(w)
        b[...] = jnp.zeros_like(b)
        for t in range(3):
            copy_rows(w, t * 2 * two, wo, t * local, local)
        b[0:1, 0:local] = bias[0:1, :]
        b[0:1, 4 * two:4 * two + local] = bias[1:2, :]

    def one_norm(p, c):
        load_rows(dims, p, img, txt, rows)
        n, _ = normalise(rows[...])
        normed[p] = (n * vector(vec, GAIN1) + vector(vec, SHIFT1)).astype(BF16)
        return c

    lax.fori_loop(0, dims.quarter, one_norm, 0)
    model = normed.shape[-1]
    proj = (dot_t(normed[...].reshape(dims.quarter * dims.slab, model), w[...]) + b[0:1, :]).astype(BF16)
    proj = proj.reshape(dims.quarter, dims.slab, 6 * two)
    for t in range(3):
        qkv[:, :, t * two:(t + 1) * two] = proj[:, :, 2 * t * two:(2 * t + 1) * two]
        rest[:, :, t * two:(t + 1) * two] = proj[:, :, (2 * t + 1) * two:(2 * t + 2) * two]
    attend_tiles(dims, lens, order[i], qkv, mixed)


def attend_own(dims, order, lens, img, txt, vec, bias, wo):
    model = img.shape[-1]
    pairs = 4 * dims.quarter
    block = lambda cols: pl.BlockSpec((dims.quarter, dims.slab, cols), lambda i, o, n: (i, 0, 0))
    shape = lambda cols: jax.ShapeDtypeStruct((pairs, dims.slab, cols), BF16)
    return pl.pallas_call(
        functools.partial(attend_own_kernel, dims),
        grid_spec=pltpu.PrefetchScalarGridSpec(
            num_scalar_prefetch=2,
            grid=(4,),
            in_specs=[
                pl.BlockSpec((dims.quarter, dims.patches, model), lambda i, o, n: (o[i], 0, 0)),
                pl.BlockSpec((dims.quarter, dims.caption, model), lambda i, o, n: (o[i], 0, 0)),
                spec_whole(vec), spec_whole(bias), spec_whole(wo),
            ],
            out_specs=[block(model), block(384), block(384), block(128)],
            scratch_shapes=[pltpu.VMEM((dims.slab, model), F32), pltpu.VMEM((768, model), BF16),
                            pltpu.VMEM((8, 768), F32)],
        ),
        out_shape=[shape(model), shape(384), shape(384), shape(128)],
        compiler_params=params(),
        cost_estimate=pl.CostEstimate(
            flops=1536 * pairs * dims.slab * model, bytes_accessed=30_000_000, transcendentals=0),
        name="attend_own",
    )(order, lens, img, txt, vec, bias, wo)


def attend_far_kernel(dims, order, lens, normed, rest, own, bias, wo, wf, qkv, mixed, keep, send, w, ow, b):
    i = pl.program_id(0)
    local = dims.local
    two, one_head = parts_of(dims)
    count = dims.quarter * dims.slab
    model = normed.shape[-1]

    @pl.when(i == 0)
    def _():
        w[...] = jnp.zeros_like(w)
        b[...] = jnp.zeros_like(b)
        for t in range(3):
            copy_rows(w, t * 2 * two, wf, t * local, two)
            copy_rows(w, t * 2 * two + two + one_head, wf, t * local + two, one_head)
        for t, at in ((0, 0), (1, 4 * two)):
            b[0:1, at:at + two] = bias[t:t + 1, 0:two]
            b[0:1, at + two + one_head:at + 2 * two] = bias[t:t + 1, two:]
        copy_rows(ow, 0, wo, 3 * local, two)
        copy_rows(ow, two, wf, 3 * local, two)
        copy_rows(ow, 2 * two, wo, 3 * local + two, one_head)
        copy_rows(ow, 2 * two + one_head, wf, 3 * local + two, one_head)

    proj = (dot_t(normed[...].reshape(count, model), w[...]) + b[0:1, :]).astype(BF16)
    proj = proj.reshape(dims.quarter, dims.slab, 6 * two)
    for t in range(3):
        at = 2 * t * two
        qkv[:, :, at:at + two] = proj[:, :, at:at + two]
        qkv[:, :, at + two:at + 2 * two] = proj[:, :, at + two:at + 2 * two] + rest[:, :, t * two:(t + 1) * two]
    attend_tiles(dims, lens, order[(i + 2) % 4], qkv, mixed)
    part = dot(own[...].reshape(count, two), ow[0:two, :])
    part = part + dot(mixed[...].reshape(count, 2 * two), ow[two:, :])
    part = part.astype(BF16).reshape(dims.quarter, dims.slab, model)

    @pl.when(i < 2)
    def _():
        send[...] = part

    @pl.when(i >= 2)
    def _():
        keep[...] = part


def attend_far(dims, order, lens, normed, rest, own, bias, wo, wf):
    model = normed.shape[-1]
    pairs = 4 * dims.quarter
    at = lambda i: (i + 2) % 4
    block = lambda cols, f: pl.BlockSpec((dims.quarter, dims.slab, cols), lambda i, o, n: (f(i), 0, 0))
    shape = lambda count, cols: jax.ShapeDtypeStruct((count, dims.slab, cols), BF16)
    return pl.pallas_call(
        functools.partial(attend_far_kernel, dims),
        grid_spec=pltpu.PrefetchScalarGridSpec(
            num_scalar_prefetch=2,
            grid=(4,),
            in_specs=[
                block(model, at), block(384, at), block(128, at),
                spec_whole(bias), spec_whole(wo), spec_whole(wf),
            ],
            out_specs=[
                block(768, at), block(256, at),
                block(model, lambda i: jnp.maximum(i - 2, 0)), block(model, lambda i: jnp.minimum(i, 1)),
            ],
            scratch_shapes=[pltpu.VMEM((768, model), BF16), pltpu.VMEM((384, model), BF16),
                            pltpu.VMEM((8, 768), F32)],
        ),
        out_shape=[
            shape(pairs, 768), shape(pairs, 256),
            shape(2 * dims.quarter, model), shape(2 * dims.quarter, model),
        ],
        compiler_params=params(),
        cost_estimate=pl.CostEstimate(
            flops=2304 * pairs * dims.slab * model, bytes_accessed=30_000_000, transcendentals=0),
        name="attend_far",
    )(order, lens, normed, rest, own, bias, wo, wf)


def residual_kernel(dims, order, keep, recv, img, txt, vec, attended, attn, expert, cls, rows):
    i = pl.program_id(0)
    ip = dims.ip

    @pl.when(i == 0)
    def _():
        rows[...] = jnp.zeros_like(rows)
        cls[...] = jnp.zeros_like(cls)

    load_rows(dims, 0, img, txt, rows)
    a = keep[0].astype(F32) + recv[0].astype(F32)
    x = rows[...] + vector(vec, A_SCALE) * (a + vector(vec, A_BIAS))
    n, _ = normalise(x)
    e_img = n[0:ip] * vector(vec, GAIN2) + vector(vec, SHIFT2)
    e_txt = n[ip:] * vector(vec, GAIN2 + 1) + vector(vec, SHIFT2 + 1)
    expert[0, 0:ip, :] = e_img.astype(BF16)
    expert[0, ip:, :] = e_txt.astype(BF16)
    for j, v in enumerate((x[0:1], x[ip:ip + 1], e_img[0:1], e_txt[0:1])):
        cls[j, pl.ds(i, 1), :] = v

    @pl.when(i < dims.quarter)
    def _():
        attended[0] = x
        attn[0] = a


def residual(dims, order, keep, recv, img, txt, vec):
    model = img.shape[-1]
    quarter = dims.quarter
    block = pl.BlockSpec((1, dims.slab, model), lambda i, o: (i, 0, 0))
    pair = lambda i, o: (o[i // quarter] * quarter + i % quarter, 0, 0)
    return pl.pallas_call(
        functools.partial(residual_kernel, dims),
        grid_spec=pltpu.PrefetchScalarGridSpec(
            num_scalar_prefetch=1,
            grid=(2 * quarter,),
            in_specs=[
                block, block,
                pl.BlockSpec((1, dims.patches, model), pair),
                pl.BlockSpec((1, dims.caption, model), pair),
                spec_whole(vec),
            ],
            out_specs=[
                pl.BlockSpec((1, dims.slab, model), lambda i, o: (jnp.minimum(i, quarter - 1), 0, 0)),
                pl.BlockSpec((1, dims.slab, model), lambda i, o: (jnp.minimum(i, quarter - 1), 0, 0)),
                block,
                pl.BlockSpec((4, 8, model), lambda i, o: (0, 0, 0)),
            ],
            scratch_shapes=[pltpu.VMEM((dims.slab, model), F32)],
        ),
        out_shape=[
            jax.ShapeDtypeStruct((quarter, dims.slab, model), F32),
            jax.ShapeDtypeStruct((quarter, dims.slab, model), F32),
            jax.ShapeDtypeStruct((2 * quarter, dims.slab, model), BF16),
            jax.ShapeDtypeStruct((4, 8, model), F32),
        ],
        compiler_params=params(),
        cost_estimate=pl.CostEstimate(flops=40_000_000, bytes_accessed=20_000_000, transcendentals=0),
        name="residual",
    )(order, keep, recv, img, txt, vec)


def expert_kernel(dims, seq, peer, own, img, txt, vec, up, up_bias, down,
                  act, dup, ddown, d_send, d_keep, x_send, x_keep, bias_grad, cot, ins, rows):
    ip, slab, quarter = dims.ip, dims.slab, dims.quarter
    i = pl.program_id(0)
    model = own.shape[-1]

    @pl.when(i == 0)
    def _():
        rows[...] = jnp.zeros_like(rows)
        bias_grad[...] = jnp.zeros_like(bias_grad)
        cot[...] = jnp.zeros_like(cot)
        ins[...] = peer[...]

    @pl.when(i == 1)
    def _():
        ins[...] = own[...]

    at = lax.broadcasted_iota(jnp.int32, (slab, 1), 0)
    inner = (at != 0) & (at != ip)

    def one(p, c):
        load_rows(dims, p, img, txt, rows)
        cot[0, pl.ds(8 * i + p, 1), :] = rows[0:1, :]
        cot[1, pl.ds(8 * i + p, 1), :] = rows[ip:ip + 1, :]
        ddown[p] = jnp.where(inner, rows[...] * vector(vec, F_SCALE), 0.0).astype(BF16)
        return c

    lax.fori_loop(0, quarter, one, 0)
    for m, lo, hi in ((0, 0, ip), (1, ip, slab)):
        count = quarter * (hi - lo)
        e = ins[:, lo:hi, :].reshape(count, model)
        u = dot(e, up[m]) + up_bias[m:m + 1]
        big, small = gelu_parts(u)
        a = (u * big).astype(BF16)
        act[:, lo:hi, :] = a.reshape(quarter, hi - lo, -1)
        slope = big + u * small
        d = dot(a, down[m]).astype(BF16).reshape(quarter, hi - lo, model)
        g = ddown[:, lo:hi, :].reshape(count, model)
        du = dot_t(g, down[m]) * slope
        bias_grad[m:m + 1, :] += jnp.sum(du, axis=0, keepdims=True)
        low = du.astype(BF16)
        dup[:, lo:hi, :] = low.reshape(quarter, hi - lo, -1)
        x = dot_t(low, up[m]).astype(BF16).reshape(quarter, hi - lo, model)

        @pl.when(i == 0)
        def _():
            d_send[:, lo:hi, :] = d
            x_send[:, lo:hi, :] = x

        @pl.when(i == 1)
        def _():
            d_keep[:, lo:hi, :] = d
            x_keep[:, lo:hi, :] = x


def experts(dims, name, half, seq, peer, own, img, txt, vec, up, up_bias, down):
    model = own.shape[-1]
    hidden = up.shape[-1]
    slab, quarter = dims.slab, dims.quarter
    fixed = pl.BlockSpec((quarter, slab, model), lambda i, o: (half, 0, 0))
    first = pl.BlockSpec((quarter, slab, model), lambda i, o: (0, 0, 0))
    step = lambda cols: pl.BlockSpec((quarter, slab, cols), lambda i, o: (i, 0, 0))
    shape = lambda n, cols: jax.ShapeDtypeStruct((n * quarter, slab, cols), BF16)
    return pl.pallas_call(
        functools.partial(expert_kernel, dims),
        grid_spec=pltpu.PrefetchScalarGridSpec(
            num_scalar_prefetch=1,
            grid=(2,),
            in_specs=[
                fixed, fixed,
                pl.BlockSpec((quarter, dims.patches, model), lambda i, o: (o[i], 0, 0)),
                pl.BlockSpec((quarter, dims.caption, model), lambda i, o: (o[i], 0, 0)),
                spec_whole(vec), spec_whole(up), spec_whole(up_bias), spec_whole(down),
            ],
            out_specs=[
                step(hidden), step(hidden), step(model),
                first, first, first, first,
                pl.BlockSpec((2, hidden), lambda i, o: (0, 0)),
                pl.BlockSpec((2, 16, model), lambda i, o: (0, 0, 0)),
            ],
            scratch_shapes=[pltpu.VMEM((quarter, slab, model), BF16), pltpu.VMEM((slab, model), F32)],
        ),
        out_shape=[
            shape(2, hidden), shape(2, hidden), shape(2, model),
            shape(1, model), shape(1, model), shape(1, model), shape(1, model),
            jax.ShapeDtypeStruct((2, hidden), F32),
            jax.ShapeDtypeStruct((2, 16, model), F32),
        ],
        compiler_params=params(),
        cost_estimate=pl.CostEstimate(
            flops=16 * quarter * slab * model * hidden, bytes_accessed=20_000_000, transcendentals=0),
        name=name,
    )(seq, peer, own, img, txt, vec, up, up_bias, down)


def expert_grads_kernel(dims, peer, own, act_a, dup_a, ddn_a, act_b, dup_b, ddn_b, ce, ca, cu, cd, out, acc):
    i = pl.program_id(0)

    def add(e, dup, ddn, act):
        for m, lo, hi in ((0, 0, dims.ip), (1, dims.ip, dims.slab)):
            count = dims.quarter * (hi - lo)
            flat = lambda ref: ref[:, lo:hi, :].reshape(count, -1)
            acc[m] += t_dot(flat(e), flat(dup))
            acc[2 + m] += t_dot(flat(ddn), flat(act))

    @pl.when(i == 0)
    def _():
        for m in range(2):
            acc[m] = t_dot(ce[m], cu[m])
            acc[2 + m] = t_dot(cd[m], ca[m])

    for j, refs in enumerate((
        (peer, dup_a, ddn_a, act_a), (own, dup_a, ddn_a, act_a),
        (peer, dup_b, ddn_b, act_b), (own, dup_b, ddn_b, act_b),
    )):
        @pl.when(i == j)
        def _():
            add(*refs)

    @pl.when(i == 3)
    def _():
        out[...] = acc[...].astype(BF16)


def expert_grads(dims, peer, own, act_a, dup_a, ddn_a, act_b, dup_b, ddn_b, ce, ca, cu, cd):
    model = own.shape[-1]
    hidden = act_a.shape[-1]
    slab, quarter = dims.slab, dims.quarter
    assert hidden == model
    half = pl.BlockSpec((quarter, slab, model), lambda i: (jnp.where(i < 2, 1, 0), 0, 0))
    first = pl.BlockSpec((quarter, slab, hidden), lambda i: (jnp.minimum(i, 1), 0, 0))
    last = pl.BlockSpec((quarter, slab, hidden), lambda i: (jnp.maximum(i - 2, 0), 0, 0))
    return pl.pallas_call(
        functools.partial(expert_grads_kernel, dims),
        grid=(4,),
        in_specs=[half, half, first, first, first, last, last, last] + [spec_whole(v) for v in (ce, ca, cu, cd)],
        out_specs=pl.BlockSpec((4, model, hidden), lambda i: (0, 0, 0)),
        scratch_shapes=[pltpu.VMEM((4, model, hidden), F32)],
        out_shape=jax.ShapeDtypeStruct((4, model, hidden), BF16),
        compiler_params=params(),
        cost_estimate=pl.CostEstimate(
            flops=16 * quarter * slab * model * hidden, bytes_accessed=40_000_000, transcendentals=0),
        name="expert_grads",
    )(peer, own, act_a, dup_a, ddn_a, act_b, dup_b, ddn_b, ce, ca, cu, cd)


def own_row(dims, r, p):
    return 8 * (r // 2) + dims.quarter * (r % 2) + p


def class_forward_kernel(dims, near, far, up, up_bias, down, out, rows):
    for m in range(2):
        e = jnp.concatenate([near[2 + m], far[2 + m]], axis=0).astype(BF16)
        rows[m] = e
        u = dot(e, up[m]) + up_bias[m:m + 1]
        out[m] = dot(gelu_low(u), down[m])


def class_forward(dims, near, far, up, up_bias, down):
    shape = (2, 16, near.shape[-1])
    return pl.pallas_call(
        functools.partial(class_forward_kernel, dims),
        out_shape=[jax.ShapeDtypeStruct(shape, F32), jax.ShapeDtypeStruct(shape, BF16)],
        compiler_params=params(),
        cost_estimate=pl.CostEstimate(flops=200_000_000, bytes_accessed=5_000_000, transcendentals=0),
        name="class_forward",
    )(near, far, up, up_bias, down)


def class_final_kernel(dims, order, near, far, d0, d1, d2, d3, vec, out):
    q = dims.quarter
    for m in range(2):
        out[m] = jnp.zeros(out.shape[1:], F32)
        for r in range(4):
            half, at = (near, far)[r // 2], q * (r % 2)
            for p in range(q):
                rows = [d[m, own_row(dims, s, p):own_row(dims, s, p) + 1, :]
                        for d, s in ((d0, r), (d1, r ^ 2), (d2, r ^ 1), (d3, r ^ 3))]
                total = (rows[0] + rows[1]) + (rows[2] + rows[3])
                x = half[m, at + p:at + p + 1, :] + vector(vec, F_SCALE) * (total + vector(vec, F_BIAS + m))
                out[m, pl.ds(4 * order[r] + p, 1), :] = x


def class_final(dims, order, near, far, parts, vec):
    shape = (2, 16, near.shape[-1])
    args = (near, far) + tuple(parts) + (vec,)
    return pl.pallas_call(
        functools.partial(class_final_kernel, dims),
        grid_spec=pltpu.PrefetchScalarGridSpec(
            num_scalar_prefetch=1, grid=(1,),
            in_specs=[spec_whole(v) for v in args],
            out_specs=pl.BlockSpec(shape, lambda i, o: (0, 0, 0)),
        ),
        out_shape=jax.ShapeDtypeStruct(shape, F32),
        compiler_params=params(),
        cost_estimate=pl.CostEstimate(flops=1_000_000, bytes_accessed=1_000_000, transcendentals=0),
        name="class_final",
    )(order, *args)


def class_back_kernel(dims, order, e, cot_a, cot_b, dclass, vec, up, up_bias, down,
                      act, dup, ddown, dexp, bias_grad, dcls, rows):
    q = dims.quarter
    rows[...] = jnp.zeros_like(rows)
    dcls[...] = jnp.zeros_like(dcls)
    for m in range(2):
        for r in range(4):
            cot, base = (cot_b, cot_a)[r % 2], 8 * (1 - r // 2)
            for p in range(q):
                d = dclass[m, pl.ds(4 * order[r] + p, 1), :]
                at = own_row(dims, r, p)
                rows[m, at:at + 1, :] = cot[m, base + p:base + p + 1, :] + d
                if r == 0:
                    dcls[p, m:m + 1, :] = d
        u = dot(e[m], up[m]) + up_bias[m:m + 1]
        big, small = gelu_parts(u)
        act[m] = (u * big).astype(BF16)
        g = (rows[m] * vector(vec, F_SCALE)).astype(BF16)
        ddown[m] = g
        du = dot_t(g, down[m]) * (big + u * small)
        bias_grad[m:m + 1, :] = jnp.sum(du, axis=0, keepdims=True)
        low = du.astype(BF16)
        dup[m] = low
        dexp[m] = dot_t(low, up[m])


def class_back(dims, order, e, cot_a, cot_b, dclass, vec, up, up_bias, down):
    hidden, model = up.shape[-1], e.shape[-1]
    args = (e, cot_a, cot_b, dclass, vec, up, up_bias, down)
    shapes = [((2, 16, hidden), BF16), ((2, 16, hidden), BF16), ((2, 16, model), BF16), ((2, 16, model), F32),
              ((2, hidden), F32), ((dims.quarter, 8, model), F32)]
    return pl.pallas_call(
        functools.partial(class_back_kernel, dims),
        grid_spec=pltpu.PrefetchScalarGridSpec(
            num_scalar_prefetch=1, grid=(1,),
            in_specs=[spec_whole(v) for v in args],
            out_specs=[pl.BlockSpec(s, lambda i, o, n=len(s): (0,) * n) for s, _ in shapes],
            scratch_shapes=[pltpu.VMEM((2, 16, model), F32)],
        ),
        out_shape=[jax.ShapeDtypeStruct(s, t) for s, t in shapes],
        compiler_params=params(),
        cost_estimate=pl.CostEstimate(flops=300_000_000, bytes_accessed=5_000_000, transcendentals=0),
        name="class_back",
    )(order, *args)


def contrast_kernel(dims, total, at, blocks, vec, weight, scale,
                    head_in, dproj, dcls, gains, shifts, scalars, cls, back):
    me = at[0]
    span = blocks[0].shape[0]
    for k, block in enumerate(blocks):
        for j in range(span):
            for m in range(2):
                cls[m, pl.ds(pl.multiple_of(16 * (me ^ (k * span + j)), 16), 16), :] = block[j, m]
    n_rows = cls.shape[1]
    sharp = jnp.exp(scale[...])
    col_at = lax.broadcasted_iota(jnp.int32, (1, n_rows), 1)
    row_at = lax.broadcasted_iota(jnp.int32, (n_rows, 1), 0)
    col_ok = (col_at % 4) < dims.quarter
    row_ok = (row_at % 4) < dims.quarter
    normal, inverse, proj, unit, embed = [], [], [], [], []
    for m in range(2):
        n, r = normalise(cls[m])
        h = (n * vector(vec, H_GAIN + m) + vector(vec, H_SHIFT + m)).astype(BF16)
        head_in[m] = h
        y = dot(h, weight[m])
        u = lax.rsqrt(jnp.sum(y * y, axis=-1, keepdims=True) + 1e-6)
        normal.append(n)
        inverse.append(r)
        proj.append(y)
        unit.append(u)
        embed.append((y * u).astype(BF16))
    ok = row_ok & col_ok
    logits = sharp * dot_t(embed[0], embed[1])
    masked = jnp.where(ok, logits, -1e30)
    row_max = jnp.max(masked, axis=1, keepdims=True)
    row_lse = row_max + jnp.log(jnp.sum(jnp.exp(masked - row_max), axis=1, keepdims=True))
    col_max = jnp.max(masked, axis=0, keepdims=True)
    col_lse = col_max + jnp.log(jnp.sum(jnp.exp(masked - col_max), axis=0, keepdims=True))
    same = (row_at == col_at) & ok
    both = jnp.exp(masked - row_lse) + jnp.exp(masked - col_lse)
    dlogits = jnp.where(ok, jnp.where(same, both - 2.0, both) * (1.0 / (2 * total)), 0.0)
    diagonal = jnp.sum(jnp.where(same, logits, 0.0), axis=1, keepdims=True)
    rows = jnp.where(row_ok, row_lse - 2.0 * diagonal, 0.0)
    cols = jnp.where(col_ok, col_lse, 0.0)
    loss = (jnp.sum(rows, axis=0, keepdims=True) + jnp.sum(cols, axis=1, keepdims=True)) * (1.0 / (2 * total))
    slope = jnp.sum(jnp.sum(dlogits * logits, axis=1, keepdims=True), axis=0, keepdims=True)
    scalars[0:1, :] = jnp.broadcast_to(loss, (1, 128))
    scalars[1:2, :] = jnp.broadcast_to(slope, (1, 128))
    high = lax.Precision.HIGHEST
    wide = [e.astype(F32) for e in embed]
    dembed = [
        sharp * jnp.dot(dlogits, wide[1], precision=high, preferred_element_type=F32),
        sharp * lax.dot_general(dlogits, wide[0], (((0,), (0,)), ((), ())), precision=high,
                                preferred_element_type=F32),
    ]
    for m in range(2):
        u, y, d = unit[m], proj[m], dembed[m]
        dp = (u * d - u * u * u * y * jnp.sum(y * d, axis=-1, keepdims=True)).astype(BF16)
        dproj[m] = dp
        dh = dot_t(dp, weight[m])
        gains[m:m + 1, :] = jnp.sum(dh * normal[m], axis=0, keepdims=True)
        shifts[m:m + 1, :] = jnp.sum(dh, axis=0, keepdims=True)
        back[m] = norm_back(normal[m], inverse[m], dh * vector(vec, H_GAIN + m))
        dcls[m] = back[m, pl.ds(pl.multiple_of(16 * me, 16), 16), :]


def contrast(dims, total, at, blocks, vec, weight, scale):
    model = weight.shape[1]
    rows = 16 * len(blocks) * blocks[0].shape[0]
    args = tuple(blocks) + (vec, weight, scale)
    shapes = [((2, rows, model), BF16), ((2, rows, weight.shape[2]), BF16), ((2, 16, model), F32),
              ((2, model), F32), ((2, model), F32), ((2, 128), F32)]

    def kernel(at, *refs):
        contrast_kernel(dims, total, at, refs[:len(blocks)], *refs[len(blocks):])

    return pl.pallas_call(
        kernel,
        grid_spec=pltpu.PrefetchScalarGridSpec(
            num_scalar_prefetch=1, grid=(1,),
            in_specs=[spec_whole(v) for v in args],
            out_specs=[pl.BlockSpec(s, lambda i, o, n=len(s): (0,) * n) for s, _ in shapes],
            scratch_shapes=[pltpu.VMEM((2, rows, model), F32)] * 2,
        ),
        out_shape=[jax.ShapeDtypeStruct(s, t) for s, t in shapes],
        compiler_params=params(),
        cost_estimate=pl.CostEstimate(flops=1_000_000_000, bytes_accessed=5_000_000, transcendentals=0),
        name="contrast",
    )(at, *args)


def contrast_large(dims, total, at, blocks, vec, weight, scale):
    model = weight.shape[1]
    held = jnp.concatenate(blocks)
    held = held[jnp.arange(held.shape[0]) ^ at[0]]
    rows = jnp.asarray([r for r in range(16) if r % 4 < dims.quarter])
    cls = jnp.transpose(held[:, :, rows], (1, 0, 2, 3)).reshape(2, -1, model)
    gain, shift = vec[H_GAIN:H_GAIN + 2, None], vec[H_SHIFT:H_SHIFT + 2, None]
    n, r = normalise(cls)
    head_in = (n * gain + shift).astype(BF16)
    proj = jnp.einsum("mrc,mce->mre", head_in, weight, preferred_element_type=F32)
    unit = lax.rsqrt(jnp.sum(proj * proj, axis=-1, keepdims=True) + 1e-6)
    embed = (proj * unit).astype(BF16)
    sharp = jnp.exp(scale[0, 0])
    logits = sharp * dot_t(embed[0], embed[1])
    row_lse = jax.nn.logsumexp(logits, axis=1, keepdims=True)
    col_lse = jax.nn.logsumexp(logits, axis=0, keepdims=True)
    dlogits = jnp.exp(logits - row_lse) + jnp.exp(logits - col_lse) - 2.0 * jnp.eye(total, dtype=F32)
    dlogits = dlogits / (2 * total)
    loss = (jnp.sum(row_lse) + jnp.sum(col_lse) - 2.0 * jnp.trace(logits)) / (2 * total)
    slope = jnp.sum(dlogits * logits)
    high = lax.Precision.HIGHEST
    wide = embed.astype(F32)
    dembed = sharp * jnp.stack([
        jnp.dot(dlogits, wide[1], precision=high, preferred_element_type=F32),
        jnp.dot(dlogits.T, wide[0], precision=high, preferred_element_type=F32)])
    dproj = (unit * dembed - unit ** 3 * proj * jnp.sum(proj * dembed, axis=-1, keepdims=True)).astype(BF16)
    dh = jnp.einsum("mre,mce->mrc", dproj, weight, preferred_element_type=F32)
    back = norm_back(n, r, dh * gain)
    pairs = 4 * dims.quarter
    own = lax.dynamic_slice_in_dim(back, at[0] * pairs, pairs, axis=1)
    dcls = jnp.zeros((2, 16, model), F32).at[:, rows].set(own)
    scalars = jnp.broadcast_to(jnp.stack([loss, slope])[:, None], (2, 128))
    return head_in, dproj, dcls, jnp.sum(dh * n, axis=1), jnp.sum(dh, axis=1), scalars


def own_pair(rows_of):
    return lambda i, o: (o[0] * rows_of + i, 0, 0)


def own_call(kernel, dims, name, order, blocks, img, txt, others, outs, scratch):
    model = img.shape[-1]
    block = pl.BlockSpec((1, dims.slab, model), lambda i, o: (i, 0, 0))
    specs = {
        "slab": (block, (dims.quarter, dims.slab, model)),
        "img": (pl.BlockSpec((1, dims.patches, model), lambda i, o: (i, 0, 0)), (dims.quarter, dims.patches, model)),
        "txt": (pl.BlockSpec((1, dims.caption, model), lambda i, o: (i, 0, 0)), (dims.quarter, dims.caption, model)),
        "sums": (pl.BlockSpec((8, model), lambda i, o: (0, 0)), (8, model)),
    }
    return pl.pallas_call(
        functools.partial(kernel, dims),
        grid_spec=pltpu.PrefetchScalarGridSpec(
            num_scalar_prefetch=1,
            grid=(dims.quarter,),
            in_specs=[block] * len(blocks) + [
                pl.BlockSpec((1, dims.patches, model), own_pair(dims.quarter)),
                pl.BlockSpec((1, dims.caption, model), own_pair(dims.quarter)),
            ] + [spec_whole(v) for v in others],
            out_specs=[specs[kind][0] for kind, _ in outs],
            scratch_shapes=[pltpu.VMEM((dims.slab, model), F32)] * scratch,
        ),
        out_shape=[jax.ShapeDtypeStruct(specs[kind][1], dtype) for kind, dtype in outs],
        compiler_params=params(),
        cost_estimate=pl.CostEstimate(flops=40_000_000, bytes_accessed=15_000_000, transcendentals=0),
        name=name,
    )(order, *blocks, img, txt, *others)


def start_own(rows, sums):
    @pl.when(pl.program_id(0) == 0)
    def _():
        rows[...] = jnp.zeros_like(rows)
        sums[...] = jnp.zeros_like(sums)


def add_class(dims, dcls, rows):
    i = pl.program_id(0)
    rows[0:1, :] += dcls[i, 0:1, :]
    rows[dims.ip:dims.ip + 1, :] += dcls[i, 1:2, :]


def final_kernel(dims, order, keep, recv, far, attended, img, txt, dcls, vec, fin_img, fin_txt, sums, rows):
    start_own(rows, sums)
    load_rows(dims, 0, img, txt, rows)
    add_class(dims, dcls, rows)
    for m, lo, hi in ((0, 0, dims.ip), (1, dims.ip, dims.slab)):
        b = keep[0, lo:hi].astype(F32) + recv[0, lo:hi].astype(F32) + far[0, lo:hi].astype(F32)
        b = b + vector(vec, F_BIAS + m)
        f = attended[0, lo:hi, :] + vector(vec, F_SCALE) * b
        if m == 0:
            fin_img[0] = f[0:dims.patches].astype(BF16)
        else:
            fin_txt[0] = f[0:dims.caption].astype(BF16)
        g = rows[lo:hi, :]
        sums[0:1, :] += jnp.sum(g * b, axis=0, keepdims=True)
        sums[1 + m:2 + m, :] += jnp.sum(g, axis=0, keepdims=True) * vector(vec, F_SCALE)


def final_rows(dims, order, keep, recv, far, attended, img, txt, dcls, vec):
    return own_call(final_kernel, dims, "final_rows", order, (keep, recv, far, attended), img, txt,
                    (dcls, vec), (("img", BF16), ("txt", BF16), ("sums", F32)), 1)


def norm_two_kernel(dims, order, keep, recv, far, attended, a_keep, a_recv, img, txt, dcls, x0, x1, x2, x3,
                    vec, dattended, dattn, sums, rows, ups):
    i = pl.program_id(0)
    start_own(rows, sums)
    load_rows(dims, 0, img, txt, rows)
    add_class(dims, dcls, rows)
    ups[...] = keep[0].astype(F32) + recv[0].astype(F32) + far[0].astype(F32)
    for m, at in ((0, 0), (1, dims.ip)):
        extra = [x[m, pl.ds(own_row(dims, r, 0) + i, 1), :] for x, r in ((x0, 0), (x1, 2), (x2, 1), (x3, 3))]
        ups[at:at + 1, :] += (extra[0] + extra[1]) + (extra[2] + extra[3])
    for m, lo, hi in ((0, 0, dims.ip), (1, dims.ip, dims.slab)):
        n, r = normalise(attended[0, lo:hi, :])
        dy = ups[lo:hi, :]
        sums[m:m + 1, :] += jnp.sum(dy * n, axis=0, keepdims=True)
        sums[2 + m:3 + m, :] += jnp.sum(dy, axis=0, keepdims=True)
        d = rows[lo:hi, :] + norm_back(n, r, dy * vector(vec, GAIN2 + m))
        dattended[0, lo:hi, :] = d
        sd = d * vector(vec, A_SCALE)
        dattn[0, lo:hi, :] = sd.astype(BF16)
        a = a_keep[0, lo:hi, :].astype(F32) + a_recv[0, lo:hi, :].astype(F32) + vector(vec, A_BIAS)
        sums[4:5, :] += jnp.sum(d * a, axis=0, keepdims=True)
        sums[5:6, :] += jnp.sum(sd, axis=0, keepdims=True)


def norm_two(dims, order, keep, recv, far, attended, a_keep, a_recv, img, txt, dcls, parts, vec):
    return own_call(norm_two_kernel, dims, "norm_two", order, (keep, recv, far, attended, a_keep, a_recv), img, txt,
                    (dcls,) + tuple(parts) + (vec,), (("slab", F32), ("slab", BF16), ("sums", F32)), 2)


def norm_one_kernel(dims, order, keep, recv, dattended, img, txt, vec, d_img, d_txt, sums, rows):
    start_own(rows, sums)
    load_rows(dims, 0, img, txt, rows)
    n, r = normalise(rows[...])
    dy = keep[0].astype(F32) + recv[0].astype(F32)
    sums[0:1, :] += jnp.sum(dy * n, axis=0, keepdims=True)
    sums[1:2, :] += jnp.sum(dy, axis=0, keepdims=True)
    d = dattended[0] + norm_back(n, r, dy * vector(vec, GAIN1))
    d_img[0] = d[0:dims.patches].astype(BF16)
    d_txt[0] = d[dims.ip:dims.ip + dims.caption].astype(BF16)


def norm_one(dims, order, keep, recv, dattended, img, txt, vec):
    return own_call(norm_one_kernel, dims, "norm_one", order, (keep, recv, dattended), img, txt,
                    (vec,), (("img", BF16), ("txt", BF16), ("sums", F32)), 1)


def back_step(dims, tiles, lens, whose, dattn, normed, qkv, mixed, dmixed, dqkv, acc, col_sums, w, ow):
    quarter, slab = dims.quarter, dims.slab
    count, width = quarter * slab, tiles * 128
    model = normed.shape[-1]
    d_rows = dattn[...].reshape(count, model)
    dmixed[...] = dot_t(d_rows, ow[...]).astype(BF16).reshape(quarter, slab, width)

    def one_pair(p, c):
        length = lens[whose * quarter + p]
        for lo, hi, start, limit in key_tail(dims, length):
            for g in range(tiles):
                at = [slice((t * tiles + g) * 128, (t * tiles + g + 1) * 128) for t in range(3)]
                q, k, v = [qkv[p, lo:hi, c] for c in at]
                q = scaled(q)
                qq = split_pair(q)
                dd = split_pair(dmixed[p, lo:hi, g * 128:(g + 1) * 128])
                w_ = softmax_keys(hide(dot_t(k, qq), start, limit))
                dw = dot_t(v, dd)
                dqkv[p, lo:hi, at[2]] = dot(w_.astype(BF16), dd).astype(BF16)
                ds = (w_ * (dw - jnp.sum(w_ * dw, axis=0, keepdims=True))).astype(BF16)
                dqkv[p, lo:hi, at[1]] = dot(ds, qq).astype(BF16)
                dqkv[p, lo:hi, at[0]] = (join_pair(t_dot(ds, k)) * HEAD_DIM ** -0.5).astype(BF16)
        return c

    lax.fori_loop(0, quarter, one_pair, 0)
    dp = dqkv[...].reshape(count, 3 * width)
    part = dot(dp, w[...])
    acc[:, 0:3 * width] += t_dot(normed[...].reshape(count, model), dp)
    acc[:, 3 * width:] += t_dot(d_rows, mixed[...].reshape(count, width))
    col_sums[...] += jnp.sum(dp.astype(F32), axis=0, keepdims=True)
    return part


def attend_back_kernel(dims, far, order, lens, d_own, d_peer, normed, qkv, mixed, wq, wo, wf, *refs):
    if not far:
        prior_keep, prior_send, *refs = refs
    keep, send, grad, *refs = refs
    if far:
        grad_rest, *refs = refs
    col_sums, dattn, dmixed, dqkv, acc, w, ow = refs
    i = pl.program_id(0)
    slab, quarter, local = dims.slab, dims.quarter, dims.local
    two, one_head = parts_of(dims)
    tiles = 2 if far else 1
    width = tiles * two
    count = quarter * slab
    model = normed.shape[-1]

    @pl.when(i == 0)
    def _():
        dattn[...] = d_own[...]
        acc[...] = jnp.zeros_like(acc)
        col_sums[...] = jnp.zeros_like(col_sums)
        for t in range(4):
            dst, at = (w, t * width) if t < 3 else (ow, 0)
            own, start = (wq, t * local) if t < 3 else (wo, 0)
            if far:
                copy_rows(dst, at, wf, t * local, two)
                copy_rows(dst, at + two, own, start + two, one_head)
                copy_rows(dst, at + two + one_head, wf, t * local + two, one_head)
            else:
                copy_rows(dst, at, own, start, two)

    @pl.when(i == 1)
    def _():
        dattn[...] = d_peer[...]

    part = back_step(dims, tiles, lens, order[2 * i], dattn, normed, qkv, mixed,
                     dmixed, dqkv, acc, col_sums, w, ow)

    @pl.when(i == 0)
    def _():
        prior = 0.0 if far else prior_keep[...].reshape(count, model).astype(F32)
        keep[...] = (part + prior).astype(BF16).reshape(quarter, slab, model)

    @pl.when(i == 1)
    def _():
        prior = 0.0 if far else prior_send[...].reshape(count, model).astype(F32)
        send[...] = (part + prior).astype(BF16).reshape(quarter, slab, model)
        for t in range(4):
            grad[:, t * two:(t + 1) * two] = acc[:, t * width:t * width + two].astype(BF16)
            if far:
                at = t * width + two
                to = 4 * two + t * one_head
                grad[:, to:to + one_head] = acc[:, at + one_head:at + two].astype(BF16)
                grad_rest[:, t * one_head:(t + 1) * one_head] = acc[:, at:at + one_head].astype(BF16)


def attend_back(dims, far, order, lens, d_own, d_peer, normed, qkv, mixed, wq, wo, wf, prior=()):
    model = normed.shape[-1]
    slab, quarter = dims.slab, dims.quarter
    width = 256 if far else 128
    one = pl.BlockSpec((quarter, slab, model), lambda i, o, n: (0, 0, 0))
    stride = normed.shape[0] // (2 * quarter)
    step = lambda cols: pl.BlockSpec((quarter, slab, cols), lambda i, o, n: (stride * i, 0, 0))
    grads = (768, 256) if far else (512,)
    specs = [one, one] + [pl.BlockSpec((model, n), lambda i, o, n_: (0, 0)) for n in grads]
    specs += [pl.BlockSpec((1, 3 * width), lambda i, o, n: (0, 0))]
    shapes = [
        jax.ShapeDtypeStruct((quarter, slab, model), BF16),
        jax.ShapeDtypeStruct((quarter, slab, model), BF16),
    ] + [jax.ShapeDtypeStruct((model, n), BF16) for n in grads] + [jax.ShapeDtypeStruct((1, 3 * width), F32)]
    scratch = [
        pltpu.VMEM((quarter, slab, model), BF16),
        pltpu.VMEM((quarter, slab, width), BF16),
        pltpu.VMEM((quarter, slab, 3 * width), BF16),
        pltpu.VMEM((model, 4 * width), F32),
        pltpu.VMEM((3 * width, model), BF16),
        pltpu.VMEM((width, model), BF16),
    ]
    return pl.pallas_call(
        functools.partial(attend_back_kernel, dims, far),
        grid_spec=pltpu.PrefetchScalarGridSpec(
            num_scalar_prefetch=2,
            grid=(2,),
            in_specs=[one, one, step(model), step(3 * width), step(width), spec_whole(wq), spec_whole(wo),
                      spec_whole(wf)] + [one] * len(prior),
            out_specs=specs,
            scratch_shapes=scratch,
        ),
        out_shape=shapes,
        compiler_params=params(),
        cost_estimate=pl.CostEstimate(
            flops=32 * quarter * slab * model * width, bytes_accessed=20_000_000, transcendentals=0),
        name="attend_back_far" if far else "attend_back_own",
    )(order, lens, d_own, d_peer, normed, qkv, mixed, wq, wo, wf, *prior)


def swap(value, axis, bit):
    size = lax.axis_size(axis)
    return lax.ppermute(value, axis, [(j, j ^ bit) for j in range(size)])


def to_core(value):
    return swap(value, "mp", 1)


def to_y(value):
    return swap(value, "mp", 2)


def from_others(value, axis, first, count):
    return [value] + [swap(value, axis, k * first) for k in range(1, count)]


def add_tree(parts):
    while len(parts) > 1:
        parts = [a + b for a, b in zip(parts[::2], parts[1::2])]
    return parts[0]


def sum_over(value, axis):
    first = 1
    while first < lax.axis_size(axis):
        count = min(8, lax.axis_size(axis) // first)
        value = add_tree(from_others(value, axis, first, count))
        first *= count
    return value


def gather_batch(value):
    parts = [value]
    first = 1
    size = lax.axis_size("batch")
    while first < size:
        count = min(8, size // first)
        whole = jnp.concatenate(parts) if len(parts) > 1 else parts[0]
        parts = from_others(whole, "batch", first, count)
        first *= count
    return parts


def gather_rows(own, me):
    near = jnp.stack([own, to_y(own)])
    far = to_core(near)
    out = jnp.zeros((4,) + own.shape, own.dtype)
    for r, value in enumerate((near[0], near[1], far[0], far[1])):
        out = lax.dynamic_update_slice(out, value[None], (me ^ ORDER[r],) + (0,) * own.ndim)
    return out.reshape((4 * own.shape[0],) + own.shape[1:])


def add_low(a, b):
    return (a.astype(F32) + b.astype(F32)).astype(BF16)


MESH = pl.DeviceIdType.MESH


class Place:
    def __init__(self):
        self.b, self.m = lax.axis_index("batch"), lax.axis_index("mp")
        self.z, self.x = self.b // 2, self.b % 2
        self.y, self.c = self.m // 2, self.m % 2
        self.core = (self.b, 2 * self.y + 1 - self.c)
        self.near = (self.b, 2 * (1 - self.y) + self.c)
        self.across = (self.b, 2 * (1 - self.y) + 1 - self.c)
        self.side = (2 * self.z + 1 - self.x, self.m)
        self.z_pair = self.z + 1 - 2 * (self.z % 2)
        self.z_far = (self.z + 2) % 4
        self.z_rest = (self.z_pair + 2) % 4
        self.paired = (2 * self.z_pair + self.x, self.m)
        self.opposite = (2 * self.z_far + self.x, self.m)
        self.batch = [((self.b + k) % 8, self.m) for k in range(1, 8)]

    def quarter(self, far_y, far_core):
        return 2 * ((self.y + far_y) % 2) + (self.c + far_core) % 2


def meet(peers):
    barrier = pltpu.get_barrier_semaphore()
    for peer in peers:
        pl.semaphore_signal(barrier, inc=1, device_id=peer, device_id_type=MESH)
    pl.semaphore_wait(barrier, len(peers))


def remote(src, dst, send_sem, recv_sem, at, device):
    return pltpu.make_async_remote_copy(
        src_ref=src, dst_ref=dst, send_sem=send_sem.at[at], recv_sem=recv_sem.at[at],
        device_id=device, device_id_type=MESH)


def front_kernel(dims, lens, img, txt, vectors, bias, own_w, own_o,
                 vec, normed, qkv, mixed, qkv_far, mixed_far, far_w, attended, attn, expert, expert_peer, cls, cls_peer,
                 rows, w, w2, ow, b, wf, far_bias, n_all, rest, m_all, m_far, q_own, q_far, a_send, a_recv, e_send, c_recv, held,
                 local_sem, send_sem, recv_sem):
    here = Place()
    i = pl.program_id(0)
    local, quarter, slab, ip = dims.local, dims.quarter, dims.slab, dims.ip
    two, one_head = parts_of(dims)
    count = quarter * slab
    model = img.shape[-1]
    at = i % 4
    whose = here.quarter(at % 2, 1 - at // 2)
    sent_w = [remote(own_w, wf.at[pl.ds(0, 3 * local)], send_sem, recv_sem, 0, here.near),
              remote(own_o, wf.at[pl.ds(3 * local, local)], send_sem, recv_sem, 1, here.near),
              remote(bias, far_bias, send_sem, recv_sem, 2, here.near)]
    sent_a = [remote(a_send.at[j], a_recv.at[j], send_sem, recv_sem, 3 + j, here.core) for j in range(2)]

    def e_over(j):
        return remote(e_send.at[j], expert_peer.at[j], send_sem, recv_sem, 5 + j, here.core)

    def e_here(j):
        return pltpu.make_async_copy(e_send.at[j], expert.at[j], local_sem.at[1 + j])

    sent_c = remote(cls, c_recv, send_sem, recv_sem, 5 + 2 * quarter, here.core)
    keep_w = pltpu.make_async_copy(wf, far_w, local_sem.at[0])
    sent_e = [e_over(j) for j in range(2 * quarter)]
    keep_e = [e_here(j) for j in range(2 * quarter)]

    @pl.when(i == 0)
    def _():
        meet([here.core, here.near])
        for copy in sent_w:
            copy.start()
        fill(vec, vectors)
        rows[...] = jnp.zeros_like(rows)
        b[...] = jnp.zeros_like(b)
        w[...] = jnp.zeros_like(w)
        cls[...] = jnp.zeros_like(cls)
        for t in range(3):
            copy_rows(w, t * 2 * two, own_w, t * local, local)
        b[0:1, 0:local] = bias[0:1, :]
        b[0:1, 4 * two:4 * two + local] = bias[1:2, :]

    def project(weights):
        proj = dot_t(n_all[at].reshape(count, model), weights[...]) + b[0:1, :]
        return proj.astype(BF16).reshape(quarter, slab, 6 * two)

    @pl.when(i < 4)
    def _():
        def one_norm(p, c):
            load_rows(dims, p, img, txt, rows)
            n, _ = normalise(rows[...])
            n_all[at, p] = (n * vector(vec, GAIN1) + vector(vec, SHIFT1)).astype(BF16)
            return c

        lax.fori_loop(0, quarter, one_norm, 0)
        proj = project(w)
        for t in range(3):
            q_own[:, :, t * two:(t + 1) * two] = proj[:, :, 2 * t * two:(2 * t + 1) * two]
            rest[at, :, :, t * two:(t + 1) * two] = proj[:, :, (2 * t + 1) * two:(2 * t + 2) * two]
        attend_tiles(dims, lens, whose, q_own, m_all.at[at])

        @pl.when(i % 2 == 0)
        def _():
            normed[...] = n_all[at]
            qkv[...] = q_own[...]
            mixed[...] = m_all[at]

    @pl.when(i == 4)
    def _():
        for copy in sent_w:
            copy.wait_recv()
        keep_w.start()
        w2[...] = jnp.zeros_like(w2)
        b[...] = jnp.zeros_like(b)
        for t in range(3):
            copy_rows(w2, t * 2 * two, wf, t * local, two)
            copy_rows(w2, t * 2 * two + two + one_head, wf, t * local + two, one_head)
        for t, to in ((0, 0), (1, 4 * two)):
            b[0:1, to:to + two] = far_bias[t:t + 1, 0:two]
            b[0:1, to + two + one_head:to + 2 * two] = far_bias[t:t + 1, two:]
        copy_rows(ow, 0, own_o, 0, two)
        copy_rows(ow, two, wf, 3 * local, two)
        copy_rows(ow, 2 * two, own_o, two, one_head)
        copy_rows(ow, 2 * two + one_head, wf, 3 * local + two, one_head)

    @pl.when(i >= 4)
    def _():
        proj = project(w2)
        for t in range(3):
            to = 2 * t * two
            q_far[:, :, to:to + two] = proj[:, :, to:to + two]
            q_far[:, :, to + two:to + 2 * two] = (
                proj[:, :, to + two:to + 2 * two] + rest[at, :, :, t * two:(t + 1) * two])
        attend_tiles(dims, lens, whose, q_far, m_far)

        @pl.when(i % 2 == 0)
        def _():
            qkv_far[...] = q_far[...]
            mixed_far[...] = m_far[...]

        part = dot(m_all[at].reshape(count, two), ow[0:two, :])
        part = part + dot(m_far[...].reshape(count, 2 * two), ow[two:, :])
        part = part.reshape(quarter, slab, model)

        @pl.when(i < 6)
        def _():
            a_send[at] = part.astype(BF16)

        for j in range(2):
            @pl.when(i == 4 + j)
            def _():
                sent_a[j].start()

        for j in range(2):
            @pl.when(i == 6 + j)
            def _():
                sent_a[j].wait_recv()

        @pl.when(i >= 6)
        def _():
            j = i - 6
            held[...] = part

            def one_residual(p, c):
                load_rows(dims, p, img, txt, rows)
                a = held[p] + a_recv[j, p].astype(F32)
                x = rows[...] + vector(vec, A_SCALE) * (a + vector(vec, A_BIAS))
                n, _ = normalise(x)
                e_img = n[0:ip] * vector(vec, GAIN2) + vector(vec, SHIFT2)
                e_txt = n[ip:] * vector(vec, GAIN2 + 1) + vector(vec, SHIFT2 + 1)
                r = j * quarter + p
                e_send[r, 0:ip, :] = e_img.astype(BF16)
                e_send[r, ip:, :] = e_txt.astype(BF16)
                e_over(r).start()
                e_here(r).start()
                for k, v in enumerate((x[0:1], x[ip:ip + 1], e_img[0:1], e_txt[0:1])):
                    cls[k, pl.ds(r, 1), :] = v

                @pl.when(j == 0)
                def _():
                    attended[p] = x
                    attn[p] = a

                return c

            lax.fori_loop(0, quarter, one_residual, 0)

    @pl.when(i == 7)
    def _():
        sent_c.start()
        keep_w.wait()
        for copy in keep_e:
            copy.wait()
        sent_c.wait()
        cls_peer[...] = c_recv[...]
        for copy in sent_e:
            copy.wait()
        for copy in sent_w + sent_a:
            copy.wait_send()


def fill(table, vectors):
    table[...] = jnp.zeros_like(table)
    at = 0
    for v in vectors:
        n = v.shape[0] if len(v.shape) == 2 else 1
        table[at:at + n, :] = v[...].reshape(n, table.shape[1])
        at += n


def front(dims, lens, img, txt, vectors, bias, own_w, own_o):
    model = img.shape[-1]
    quarter, slab, local = dims.quarter, dims.slab, dims.local
    held = pl.BlockSpec(memory_space=pltpu.VMEM)
    away = pl.BlockSpec(memory_space=pl.ANY)

    def states_at(i):
        return Place().quarter(i % 2, 1 - i % 4 // 2), 0, 0

    own_block = lambda cols: pl.BlockSpec((quarter, slab, cols), lambda i: (jnp.where(i < 2, 1, 0), 0, 0))
    far_block = lambda cols: pl.BlockSpec((quarter, slab, cols), lambda i: (jnp.where(i < 6, 1, 0), 0, 0))
    six = lambda cols: jax.ShapeDtypeStruct((2 * quarter, slab, cols), BF16)
    block = lambda cols: (quarter, slab, cols)
    n_remote = 6 + 2 * quarter
    return pl.pallas_call(
        lambda lens, img, txt, *refs: front_kernel(
            dims, lens, img, txt, refs[:len(vectors)], *refs[len(vectors):]),
        grid=(8,),
        in_specs=[pl.BlockSpec(memory_space=pltpu.SMEM),
                  pl.BlockSpec((quarter, dims.patches, model), states_at),
                  pl.BlockSpec((quarter, dims.caption, model), states_at)] + [held] * (3 + len(vectors)),
        out_specs=[held, own_block(model), own_block(384), own_block(128), far_block(768), far_block(256),
                   away, held, held, away, away, held, held],
        out_shape=[jax.ShapeDtypeStruct((16, model), F32), six(model), six(384), six(128), six(768), six(256),
                   jax.ShapeDtypeStruct((4 * local, model), BF16),
                   jax.ShapeDtypeStruct(block(model), F32), jax.ShapeDtypeStruct(block(model), F32),
                   six(model), six(model),
                   jax.ShapeDtypeStruct((4, 8, model), F32), jax.ShapeDtypeStruct((4, 8, model), F32)],
        scratch_shapes=[
            pltpu.VMEM((slab, model), F32), pltpu.VMEM((768, model), BF16), pltpu.VMEM((768, model), BF16),
            pltpu.VMEM((384, model), BF16), pltpu.VMEM((8, 768), F32), pltpu.VMEM((4 * local, model), BF16),
            pltpu.VMEM((2, local), F32),
            pltpu.VMEM((4,) + block(model), BF16), pltpu.VMEM((4,) + block(384), BF16),
            pltpu.VMEM((4,) + block(128), BF16), pltpu.VMEM(block(256), BF16),
            pltpu.VMEM(block(384), BF16), pltpu.VMEM(block(768), BF16),
            pltpu.VMEM((2,) + block(model), BF16), pltpu.VMEM((2,) + block(model), BF16),
            pltpu.VMEM((2 * quarter, slab, model), BF16), pltpu.VMEM((4, 8, model), F32),
            pltpu.VMEM(block(model), F32),
            pltpu.SemaphoreType.DMA((1 + 2 * quarter,)),
            pltpu.SemaphoreType.DMA((n_remote,)), pltpu.SemaphoreType.DMA((n_remote,)),
        ],
        compiler_params=params(collective_id=6, has_side_effects=True),
        cost_estimate=pl.CostEstimate(
            flops=16 * quarter * slab * model * 1152, bytes_accessed=40_000_000, transcendentals=0),
        name="front",
    )(lens, img, txt, *vectors, bias, own_w, own_o)


def middle_kernel(dims, total, img, txt, own, peer, cls_own, cls_peer, vec, up, up_bias, down, head_weight, scale,
                  act, dup, ddn, dexp, d_own, d_near, bias_grad, class_e, c_act, c_dup, c_ddn, dcls,
                  head_in, dproj, gains, shifts, scalars,
                  bx, bd, rx, rd, x_near, x_far, ins, rows, part, parts, cls, back, cot, c_rows, extra, extras, hidden_in, weight,
                  local_sem, send_sem, recv_sem):
    here = Place()
    ip, slab, quarter = dims.ip, dims.slab, dims.quarter
    i = pl.program_id(0)
    model = own.shape[-1]
    mp_peers = [here.core, here.near, here.across]
    fetch = pltpu.make_async_copy(head_weight, weight, local_sem.at[0])
    of = [here.quarter(0, 0), here.quarter(1, 0), here.quarter(0, 1), here.quarter(1, 1)]

    sent_x = [remote(bx.at[2 * j], rx.at[j], send_sem, recv_sem, j, here.core) for j in range(2)]
    sent_d = [remote(bd.at[2 * j], rd.at[j], send_sem, recv_sem, 2 + j, here.core) for j in range(2)]
    sent_near = remote(x_near, x_far, send_sem, recv_sem, 4, here.near)
    sent_part = [remote(part, parts.at[k], send_sem, recv_sem, 5 + k, mp_peers[k]) for k in range(3)]
    sent_extra = [remote(extra, extras.at[k], send_sem, recv_sem, 8 + k, mp_peers[k]) for k in range(3)]
    sent_cls = [remote(cls.at[here.b], cls.at[here.b], send_sem, recv_sem, 11 + k, here.batch[k]) for k in range(7)]

    @pl.when(i == 0)
    def _():
        fetch.start()
        rows[...] = jnp.zeros_like(rows)
        bias_grad[...] = jnp.zeros_like(bias_grad)
        for m in range(2):
            e = jnp.concatenate([cls_own[2 + m], cls_peer[2 + m]], axis=0).astype(BF16)
            class_e[m] = e
            u = dot(e, up[m]) + up_bias[m:m + 1]
            hidden_in[m] = u
            part[m] = dot(gelu_low(u), down[m])
        meet(mp_peers + here.batch)
        for copy in sent_part:
            copy.start()
        ins[...] = peer[...]

    @pl.when(i == 1)
    def _():
        for copy in sent_part:
            copy.wait_recv()
        for m in range(2):
            cls[here.b, m] = jnp.zeros(cls.shape[2:], F32)
            for r in range(4):
                half, at = (cls_own, cls_peer)[r // 2], quarter * (r % 2)
                for p in range(quarter):
                    line = [d[m, own_row(dims, s, p):own_row(dims, s, p) + 1, :]
                            for d, s in ((part, r), (parts.at[0], r ^ 2), (parts.at[1], r ^ 1), (parts.at[2], r ^ 3))]
                    x = (line[0] + line[1]) + (line[2] + line[3]) + vector(vec, F_BIAS + m)
                    x = half[m, at + p:at + p + 1, :] + vector(vec, F_SCALE) * x
                    cls[here.b, m, pl.ds(4 * of[r] + p, 1), :] = x
        for copy in sent_cls:
            copy.start()
        ins[...] = own[...]

    @pl.when(i == 2)
    def _():
        ins[...] = peer[...]

    @pl.when(i == 3)
    def _():
        ins[...] = own[...]
        fetch.wait()
        for copy in sent_cls:
            copy.wait_recv()
        n_rows = 16 * cls.shape[0]
        sharp = jnp.exp(scale[...])
        col_at = lax.broadcasted_iota(jnp.int32, (1, n_rows), 1)
        row_at = lax.broadcasted_iota(jnp.int32, (n_rows, 1), 0)
        col_ok = (col_at % 4) < quarter
        row_ok = (row_at % 4) < quarter
        normal, inverse, proj, unit, embed = [], [], [], [], []
        for m in range(2):
            n, r = normalise(cls[:, m].reshape(n_rows, model))
            h = (n * vector(vec, H_GAIN + m) + vector(vec, H_SHIFT + m)).astype(BF16)
            head_in[m] = h
            y = dot(h, weight[m])
            u = lax.rsqrt(jnp.sum(y * y, axis=-1, keepdims=True) + 1e-6)
            normal.append(n)
            inverse.append(r)
            proj.append(y)
            unit.append(u)
            embed.append((y * u).astype(BF16))
        ok = row_ok & col_ok
        logits = sharp * dot_t(embed[0], embed[1])
        masked = jnp.where(ok, logits, -1e30)
        row_max = jnp.max(masked, axis=1, keepdims=True)
        row_lse = row_max + jnp.log(jnp.sum(jnp.exp(masked - row_max), axis=1, keepdims=True))
        col_max = jnp.max(masked, axis=0, keepdims=True)
        col_lse = col_max + jnp.log(jnp.sum(jnp.exp(masked - col_max), axis=0, keepdims=True))
        same = (row_at == col_at) & ok
        both = jnp.exp(masked - row_lse) + jnp.exp(masked - col_lse)
        dlogits = jnp.where(ok, jnp.where(same, both - 2.0, both) * (1.0 / (2 * total)), 0.0)
        diagonal = jnp.sum(jnp.where(same, logits, 0.0), axis=1, keepdims=True)
        lines = jnp.sum(jnp.where(row_ok, row_lse - 2.0 * diagonal, 0.0), axis=0, keepdims=True)
        lines = lines + jnp.sum(jnp.where(col_ok, col_lse, 0.0), axis=1, keepdims=True)
        slope = jnp.sum(jnp.sum(dlogits * logits, axis=1, keepdims=True), axis=0, keepdims=True)
        scalars[0:1, :] = jnp.broadcast_to(lines * (1.0 / (2 * total)), (1, 128))
        scalars[1:2, :] = jnp.broadcast_to(slope, (1, 128))
        pieces, left = [], dlogits
        for _ in range(3):
            pieces.append(left.astype(BF16))
            left = left - pieces[-1].astype(F32)
        dembed = [
            sharp * (dot(pieces[0], embed[1]) + (dot(pieces[1], embed[1]) + dot(pieces[2], embed[1]))),
            sharp * (t_dot(pieces[0], embed[0]) + (t_dot(pieces[1], embed[0]) + t_dot(pieces[2], embed[0]))),
        ]
        c_rows[...] = jnp.zeros_like(c_rows)
        dcls[...] = jnp.zeros_like(dcls)
        for m in range(2):
            for p in range(quarter):
                src = (img, txt)[m]
                cot[m, 8 * 3 + p:8 * 3 + p + 1, :] = src[p, 0:1, :].astype(F32)
        for m in range(2):
            u, y, d = unit[m], proj[m], dembed[m]
            dp = (u * d - u * u * u * y * jnp.sum(y * d, axis=-1, keepdims=True)).astype(BF16)
            dproj[m] = dp
            dh = dot_t(dp, weight[m])
            gains[m:m + 1, :] = jnp.sum(dh * normal[m], axis=0, keepdims=True)
            shifts[m:m + 1, :] = jnp.sum(dh, axis=0, keepdims=True)
            back[m] = norm_back(normal[m], inverse[m], dh * vector(vec, H_GAIN + m))
            for r in range(4):
                step = (3, 1, 2, 0)[r]
                for p in range(quarter):
                    g = back[m, pl.ds(16 * here.b + 4 * of[r] + p, 1), :]
                    at = own_row(dims, r, p)
                    c_rows[m, at:at + 1, :] = cot[m, 8 * step + p:8 * step + p + 1, :] + g
                    if r == 0:
                        dcls[p, m:m + 1, :] = g
            u = hidden_in[m]
            big, small = gelu_parts(u)
            c_act[m] = (u * big).astype(BF16)
            g = (c_rows[m] * vector(vec, F_SCALE)).astype(BF16)
            c_ddn[m] = g
            du = dot_t(g, down[m]) * (big + u * small)
            bias_grad[m:m + 1, :] += jnp.sum(du, axis=0, keepdims=True)
            low = du.astype(BF16)
            c_dup[m] = low
            extra[m] = dot_t(low, up[m])
        for copy in sent_extra:
            copy.start()

    at = lax.broadcasted_iota(jnp.int32, (slab, 1), 0)
    inner = (at != 0) & (at != ip)

    def one(p, c):
        load_rows(dims, p, img, txt, rows)
        cot[0, pl.ds(8 * i + p, 1), :] = rows[0:1, :]
        cot[1, pl.ds(8 * i + p, 1), :] = rows[ip:ip + 1, :]
        ddn[p] = jnp.where(inner, rows[...] * vector(vec, F_SCALE), 0.0).astype(BF16)
        return c

    lax.fori_loop(0, quarter, one, 0)
    for m, lo, hi in ((0, 0, ip), (1, ip, slab)):
        count = quarter * (hi - lo)
        e = ins[:, lo:hi, :].reshape(count, model)
        u = dot(e, up[m]) + up_bias[m:m + 1]
        big, small = gelu_parts(u)
        a = (u * big).astype(BF16)
        act[:, lo:hi, :] = a.reshape(quarter, hi - lo, -1)
        slope = big + u * small
        bd[i, :, lo:hi, :] = dot(a, down[m]).astype(BF16).reshape(quarter, hi - lo, model)
        g = ddn[:, lo:hi, :].reshape(count, model)
        du = dot_t(g, down[m]) * slope
        bias_grad[m:m + 1, :] += jnp.sum(du, axis=0, keepdims=True)
        low = du.astype(BF16)
        dup[:, lo:hi, :] = low.reshape(quarter, hi - lo, -1)
        bx[i, :, lo:hi, :] = dot_t(low, up[m]).astype(BF16).reshape(quarter, hi - lo, model)

    for j in range(2):
        @pl.when(i == 2 * j)
        def _():
            sent_x[j].start()
            sent_d[j].start()

    @pl.when(i == 1)
    def _():
        sent_x[0].wait_recv()

        def add_x(p, c):
            x_near[p] = (bx[1, p].astype(F32) + rx[0, p].astype(F32)).astype(BF16)
            return c

        lax.fori_loop(0, quarter, add_x, 0)
        sent_near.start()
        sent_d[0].wait_recv()

        def add_d(p, c):
            d_near[p] = (bd[1, p].astype(F32) + rd[0, p].astype(F32)).astype(BF16)
            return c

        lax.fori_loop(0, quarter, add_d, 0)

    @pl.when(i == 3)
    def _():
        sent_d[1].wait_recv()

        def add_d(p, c):
            d_own[p] = bd[3, p].astype(F32) + rd[1, p].astype(F32)
            return c

        lax.fori_loop(0, quarter, add_d, 0)
        sent_x[1].wait_recv()
        sent_near.wait_recv()

        def add_x(p, c):
            dexp[p] = bx[3, p].astype(F32) + rx[1, p].astype(F32) + x_far[p].astype(F32)
            return c

        lax.fori_loop(0, quarter, add_x, 0)
        for copy in sent_extra:
            copy.wait_recv()
        for m in range(2):
            for p in range(quarter):
                line = [x[m, own_row(dims, r, p):own_row(dims, r, p) + 1, :]
                        for x, r in ((extra, 0), (extras.at[0], 2), (extras.at[1], 1), (extras.at[2], 3))]
                dexp[p, m * ip:m * ip + 1, :] += (line[0] + line[1]) + (line[2] + line[3])
        for copy in sent_x + sent_d + [sent_near] + sent_part + sent_extra + sent_cls:
            copy.wait_send()


def middle(dims, total, img, txt, own, peer, cls_own, cls_peer, vec, up, up_bias, down, weight, scale):
    model = own.shape[-1]
    hidden = up.shape[-1]
    slab, quarter = dims.slab, dims.quarter
    batch = 8

    def cot_at(i):
        here = Place()
        return here.quarter(1 - i // 2, 1 - i % 2), 0, 0

    held = pl.BlockSpec(memory_space=pltpu.VMEM)
    half = pl.BlockSpec((quarter, slab, model), lambda i: (jnp.where(i < 2, 1, 0), 0, 0))
    step = lambda cols: pl.BlockSpec((quarter, slab, cols), lambda i: (i, 0, 0))
    rows_of = lambda n, t: jax.ShapeDtypeStruct((n, slab, model), t)
    small = [((quarter, slab, model), F32), ((quarter, slab, model), F32), ((quarter, slab, model), BF16),
             ((2, hidden), F32), ((2, 16, model), BF16), ((2, 16, hidden), BF16), ((2, 16, hidden), BF16),
             ((2, 16, model), BF16), ((quarter, 8, model), F32), ((2, 16 * batch, model), BF16),
             ((2, 16 * batch, weight.shape[2]), BF16), ((2, model), F32), ((2, model), F32), ((2, 128), F32)]
    block = (quarter, slab, model)
    return pl.pallas_call(
        functools.partial(middle_kernel, dims, total),
        grid=(4,),
        in_specs=[pl.BlockSpec((quarter, dims.patches, model), cot_at),
                  pl.BlockSpec((quarter, dims.caption, model), cot_at)] + [half] * 2 + [held] * 6
        + [pl.BlockSpec(memory_space=pl.ANY), held],
        out_specs=[step(hidden), step(hidden), step(model)] + [held] * len(small),
        out_shape=[rows_of(4 * quarter, BF16)] * 3 + [jax.ShapeDtypeStruct(v, t) for v, t in small],
        scratch_shapes=[
            pltpu.VMEM((4,) + block, BF16), pltpu.VMEM((4,) + block, BF16),
            pltpu.VMEM((2,) + block, BF16), pltpu.VMEM((2,) + block, BF16),
            pltpu.VMEM(block, BF16), pltpu.VMEM(block, BF16), pltpu.VMEM(block, BF16),
            pltpu.VMEM((slab, model), F32),
            pltpu.VMEM((2, 16, model), F32), pltpu.VMEM((3, 2, 16, model), F32),
            pltpu.VMEM((batch, 2, 16, model), F32), pltpu.VMEM((2, 16 * batch, model), F32),
            pltpu.VMEM((2, 32, model), F32), pltpu.VMEM((2, 16, model), F32),
            pltpu.VMEM((2, 16, model), F32), pltpu.VMEM((3, 2, 16, model), F32),
            pltpu.VMEM((2, 16, hidden), F32), pltpu.VMEM(weight.shape, BF16), pltpu.SemaphoreType.DMA((1,)),
            pltpu.SemaphoreType.DMA((18,)), pltpu.SemaphoreType.DMA((18,)),
        ],
        compiler_params=params(collective_id=2, has_side_effects=True),
        cost_estimate=pl.CostEstimate(
            flops=32 * quarter * slab * model * hidden, bytes_accessed=40_000_000, transcendentals=0),
        name="middle",
    )(img, txt, own, peer, cls_own, cls_peer, vec, up, up_bias, down, weight, scale)


def turn_kernel(dims, img, txt, peer, own, act, dup, ddn, ce, ca, cu, cd, dexp, attended, attn, d_own, d_near, dcls, vec,
                down_sum, up_keep, up_send, dattended, dattn, dattn_peer, fin_img, fin_txt, sums,
                acc, d_far, n_peer, rows, side_send, side_recv, e_in, dexp_in, attended_in, attn_in, d_own_in,
                local_sem, send_sem, recv_sem):
    here = Place()
    quarter, ip = dims.quarter, dims.ip
    i = pl.program_id(0)
    piece = side_send.shape[3]
    sent_near = remote(d_near, d_far, send_sem, recv_sem, 0, here.near)

    def over(p):
        return remote(dattn.at[p], n_peer.at[p], send_sem, recv_sem, 1 + p, here.core)

    sent_core = [over(p) for p in range(quarter)]
    sent_side = [remote(side_send.at[h], side_recv.at[h], send_sem, recv_sem, 1 + quarter + h, here.side)
                 for h in range(2)]
    part = acc.shape[2] // 2
    loaded = [pltpu.make_async_copy(src, dst, local_sem.at[j]) for j, (src, dst) in enumerate((
        (dexp, dexp_in), (attended, attended_in), (attn, attn_in), (d_own, d_own_in)))]
    dexp, attended, attn, d_own = dexp_in, attended_in, attn_in, d_own_in
    spans = ((0, 0, ip), (1, ip, dims.slab))
    flat = lambda v: v.reshape(-1, v.shape[-1])
    block = lambda j: pl.ds(pl.multiple_of(j * piece, piece), piece)

    @pl.when(i == 0)
    def _():
        meet([here.core, here.near, here.side])
        sent_near.start()
        for copy in loaded:
            copy.start()
        for m in range(2):
            acc[m] = t_dot(cd[m], ca[m])

    for h in range(2):
        @pl.when(i // 4 == h)
        def _():
            for m, lo, hi in spans:
                acc[m, :, h * part:(h + 1) * part] += t_dot(flat(ddn[:, lo:hi, :]), flat(act[:, lo:hi, :]))

        @pl.when(i == 4 * h + 3)
        def _():
            cols = slice(h * part, (h + 1) * part)
            for j in range(4):
                for m in range(2):
                    side_send[h, j, m] = acc[m, block(2 * j + 1 - here.x), cols].astype(BF16)
                    down_sum[j, m, :, cols] = acc[m, block(2 * j + here.x), cols].astype(BF16)
            sent_side[h].start()

    @pl.when(i == 8)
    def _():
        for m in range(2):
            acc[m] = t_dot(ce[m], cu[m])

    @pl.when((i >= 8) & (i % 2 == 0))
    def _():
        e_in[...] = peer[...]

    @pl.when((i >= 8) & (i % 2 == 1))
    def _():
        e_in[...] = own[...]

    @pl.when(i >= 8)
    def _():
        for m, lo, hi in spans:
            acc[m] += t_dot(flat(e_in[:, lo:hi, :]), flat(dup[:, lo:hi, :]))

    @pl.when(i == 11)
    def _():
        for j in range(4):
            for m in range(2):
                up_keep[j, m] = acc[m, block(2 * j + here.x), :].astype(BF16)
                up_send[j, m] = acc[m, block(2 * j + 1 - here.x), :].astype(BF16)
        for copy in loaded:
            copy.wait()
        rows[...] = jnp.zeros_like(rows)
        sums[...] = jnp.zeros_like(sums)

        def load(p):
            load_rows(dims, p, img, txt, rows)
            rows[0:1, :] += dcls[p, 0:1, :]
            rows[ip:ip + 1, :] += dcls[p, 1:2, :]

        def norm(p, c):
            load(p)
            for m, lo, hi in ((0, 0, ip), (1, ip, dims.slab)):
                n, r = normalise(attended[p, lo:hi, :])
                dy = dexp[p, lo:hi, :]
                sums[m:m + 1, :] += jnp.sum(dy * n, axis=0, keepdims=True)
                sums[2 + m:3 + m, :] += jnp.sum(dy, axis=0, keepdims=True)
                d = rows[lo:hi, :] + norm_back(n, r, dy * vector(vec, GAIN2 + m))
                dattended[p, lo:hi, :] = d
                sd = d * vector(vec, A_SCALE)
                dattn[p, lo:hi, :] = sd.astype(BF16)
                a = attn[p, lo:hi, :] + vector(vec, A_BIAS)
                sums[4:5, :] += jnp.sum(d * a, axis=0, keepdims=True)
                sums[5:6, :] += jnp.sum(sd, axis=0, keepdims=True)
            over(p).start()
            return c

        lax.fori_loop(0, quarter, norm, 0)
        sent_near.wait_recv()

        def final(p, c):
            load(p)
            for m, lo, hi in ((0, 0, ip), (1, ip, dims.slab)):
                b = d_own[p, lo:hi, :] + d_far[p, lo:hi, :].astype(F32) + vector(vec, F_BIAS + m)
                f = attended[p, lo:hi, :] + vector(vec, F_SCALE) * b
                if m == 0:
                    fin_img[p] = f[0:dims.patches].astype(BF16)
                else:
                    fin_txt[p] = f[0:dims.caption].astype(BF16)
                g = rows[lo:hi, :]
                sums[6:7, :] += jnp.sum(g * b, axis=0, keepdims=True)
                sums[7 + m:8 + m, :] += jnp.sum(g, axis=0, keepdims=True) * vector(vec, F_SCALE)
            return c

        lax.fori_loop(0, quarter, final, 0)
        for p in range(quarter):
            sent_core[p].wait()
            dattn_peer[p] = n_peer[p]
        for h in range(2):
            sent_side[h].wait()
            cols = slice(h * part, (h + 1) * part)
            for j in range(4):
                down_sum[j, :, :, cols] = (
                    down_sum[j, :, :, cols].astype(F32) + side_recv[h, j].astype(F32)).astype(BF16)
        sent_near.wait_send()


def turn(dims, img, txt, peer, own, act, dup, ddn, ce, ca, cu, cd, dexp, attended, attn, d_own, d_near, dcls, vec):
    model = own.shape[-1]
    hidden = act.shape[-1]
    slab, quarter = dims.slab, dims.quarter
    held = pl.BlockSpec(memory_space=pltpu.VMEM)

    def own_at(i):
        return Place().quarter(0, 0), 0, 0

    away = pl.BlockSpec(memory_space=pl.ANY)
    half = pl.BlockSpec((quarter, slab, model), lambda i: (jnp.where(i < 10, 1, 0), 0, 0))
    row = lambda i: jnp.where(i < 8, i % 4, 3)
    first = pl.BlockSpec((quarter, slab, model), lambda i: (row(i), 0, 0))
    piece = pl.BlockSpec((quarter, slab, hidden // 2), lambda i: (row(i), 0, jnp.minimum(i // 4, 1)))
    last = pl.BlockSpec((quarter, slab, hidden), lambda i: (jnp.maximum(i - 8, 0), 0, 0))
    block = (quarter, slab, model)
    part = (4, 2, model // 8, hidden)
    split = (2, 4, 2, model // 8, hidden // 2)
    outs = [(part, BF16), (part, BF16), (part, BF16), (block, F32), (block, BF16), (block, BF16),
            ((quarter, dims.patches, model), BF16), ((quarter, dims.caption, model), BF16), ((16, model), F32)]
    return pl.pallas_call(
        functools.partial(turn_kernel, dims),
        grid=(12,),
        in_specs=[pl.BlockSpec((quarter, dims.patches, model), own_at),
                  pl.BlockSpec((quarter, dims.caption, model), own_at)] + [half] * 2 + [piece, last, first]
        + [held] * 4 + [away] * 4 + [held] * 3,
        out_specs=[held] * len(outs),
        out_shape=[jax.ShapeDtypeStruct(v, t) for v, t in outs],
        scratch_shapes=[
            pltpu.VMEM((2, model, hidden), F32), pltpu.VMEM(block, BF16), pltpu.VMEM(block, BF16),
            pltpu.VMEM((slab, model), F32), pltpu.VMEM(split, BF16), pltpu.VMEM(split, BF16),
            pltpu.VMEM(block, BF16),
        ] + [pltpu.VMEM(block, F32)] * 4 + [
            pltpu.SemaphoreType.DMA((4,)),
            pltpu.SemaphoreType.DMA((3 + quarter,)), pltpu.SemaphoreType.DMA((3 + quarter,)),
        ],
        compiler_params=params(collective_id=3, has_side_effects=True),
        cost_estimate=pl.CostEstimate(
            flops=16 * quarter * slab * model * hidden, bytes_accessed=40_000_000, transcendentals=0),
        name="turn",
    )(img, txt, peer, own, act, dup, ddn, ce, ca, cu, cd, dexp, attended, attn, d_own, d_near, dcls, vec)


def back_kernel(dims, lens, d_own, d_peer, normed, qkv_far, mixed_far, qkv_own, mixed_own, wq, wo, wf,
                fin_img, fin_txt, up_keep, up_send, down_sum,
                whole, grad_pair, grad_single, cols_far, cols_own, near_img, near_txt, far_sum, down_out, up_out,
                dattn, dm_far, dm_own, dq_far, dq_own, acc_far, acc_own, w_far, w_own, o_far, o_own, dn, grad_f,
                up_mine, up_side, up_sum, up_in, up_pass, up_last, down_mine, down_in, down_pass, down_last,
                n_send, n_recv, from_side, local_sem, send_sem, recv_sem):
    here = Place()
    i = pl.program_id(0)
    slab, quarter, local = dims.slab, dims.quarter, dims.local
    two, one_head = parts_of(dims)
    count = quarter * slab
    model = normed.shape[-1]
    piece = from_side.shape[1]
    block = lambda j: pl.ds(pl.multiple_of(j * piece, piece), piece)
    used = [0]

    def make(src, dst, device):
        at = used[0]
        used[0] += 1
        return remote(src, dst, send_sem, recv_sem, at, device)

    sent_near = [make(fin_img, near_img, here.near), make(fin_txt, near_txt, here.near)]
    sent_up = [make(up_send.at[j, m], up_side.at[m, j], here.side) for m in range(2) for j in range(4)]
    in_pair = lambda src, dst: [make(src.at[here.z_pair], dst.at[0], here.paired), make(src.at[here.z_rest], dst.at[1], here.paired)]
    sent_down = in_pair(down_sum, down_in)
    pass_down = make(down_pass, down_last, here.opposite)
    wide = grad_f.shape[1]
    sent_far = [make(grad_f.at[block(2 * j + 1 - here.x)], from_side.at[j, :, pl.ds(0, wide)], here.side) for j in range(4)]
    sent_far += [make(grad_single.at[block(2 * j + 1 - here.x)], from_side.at[j, :, pl.ds(wide, grad_single.shape[1])],
                      here.side) for j in range(4)]
    sent_pair = [in_pair(up_sum.at[m], up_in.at[m]) for m in range(2)]
    pass_up = [make(up_pass.at[m], up_last.at[m], here.opposite) for m in range(2)]
    sent_n = make(n_send, n_recv, here.core)
    loaded = [pltpu.make_async_copy(up_keep, up_mine, local_sem.at[0]),
              pltpu.make_async_copy(down_sum.at[here.z], down_mine.at[0], local_sem.at[1]),
              pltpu.make_async_copy(down_sum.at[here.z_far], down_mine.at[1], local_sem.at[2])]
    add = lambda *parts: functools.reduce(lambda p, q: p + q, [v.astype(F32) for v in parts])

    @pl.when(i == 0)
    def _():
        meet([here.core, here.near, here.side, here.paired, here.opposite])
        for copy in loaded + sent_near + sent_up + sent_down:
            copy.start()
        for acc, cols in ((acc_far, cols_far), (acc_own, cols_own)):
            acc[...] = jnp.zeros_like(acc)
            cols[...] = jnp.zeros_like(cols)
        for t in range(4):
            own, start = (wq, t * local) if t < 3 else (wo, 0)
            dst, at = (w_far, t * 2 * two) if t < 3 else (o_far, 0)
            copy_rows(dst, at, wf, t * local, two)
            copy_rows(dst, at + two, own, start + two, one_head)
            copy_rows(dst, at + two + one_head, wf, t * local + two, one_head)
            dst, at = (w_own, t * two) if t < 3 else (o_own, 0)
            copy_rows(dst, at, own, start, two)

    @pl.when(i % 2 == 0)
    def _():
        dattn[...] = d_peer[...]

    @pl.when(i % 2 == 1)
    def _():
        dattn[...] = d_own[...]

    whose = here.quarter(0, 1 - i % 2)

    @pl.when(i < 2)
    def _():
        part = back_step(dims, 2, lens, whose, dattn, normed, qkv_far, mixed_far, dm_far, dq_far, acc_far, cols_far,
                         w_far, o_far)
        dn[i] = part.reshape(quarter, slab, model)

    def sum_up(m):
        for j in range(4):
            sent_up[4 * m + j].wait_recv()
            up_sum[m, j] = add(up_mine[j, m], up_side[m, j]).astype(BF16)
        for copy in sent_pair[m]:
            copy.start()

    def pass_on(m):
        for copy in sent_pair[m]:
            copy.wait_recv()
        up_pass[m] = add(up_sum[m, here.z_far], up_in[m, 1]).astype(BF16)
        pass_up[m].start()

    @pl.when(i == 0)
    def _():
        for copy in loaded[1:]:
            copy.wait()
        for copy in sent_down:
            copy.wait_recv()
        down_pass[...] = add(down_mine[1], down_in[1]).astype(BF16)
        pass_down.start()
        loaded[0].wait()
        sum_up(0)

    @pl.when(i == 1)
    def _():
        for t in range(4):
            at = t * 2 * two
            to = 4 * two + t * one_head
            grad_f[:, t * two:(t + 1) * two] = acc_far[:, at:at + two].astype(BF16)
            grad_f[:, to:to + one_head] = acc_far[:, at + two + one_head:at + 2 * two].astype(BF16)
            grad_single[:, t * one_head:(t + 1) * one_head] = acc_far[:, at + two:at + two + one_head].astype(BF16)
        for copy in sent_far:
            copy.start()
        pass_on(0)
        sum_up(1)

    @pl.when(i >= 2)
    def _():
        part = back_step(dims, 1, lens, whose, dattn, normed, qkv_own, mixed_own, dm_own, dq_own, acc_own, cols_own,
                         w_own, o_own)
        total = part.reshape(quarter, slab, model) + dn[i - 2]

        @pl.when(i == 2)
        def _():
            n_send[...] = total.astype(BF16)
            sent_n.start()
            pass_on(1)

        @pl.when(i == 3)
        def _():
            whole[...] = total

    @pl.when(i == 3)
    def _():
        grad_pair[...] = acc_own[...].astype(BF16)
        sent_n.wait_recv()
        whole[...] += n_recv[...].astype(F32)
        down_out[...] = add(down_mine[0], down_in[0])
        for copy in sent_far:
            copy.wait_recv()
        for j in range(4):
            far_sum[j, :, 0:wide] = add(grad_f[block(2 * j + here.x), :], from_side[j, :, 0:wide]).astype(BF16)
            far_sum[j, :, wide:] = add(grad_single[block(2 * j + here.x), :], from_side[j, :, wide:]).astype(BF16)
        pass_down.wait_recv()
        down_out[...] += down_last[...].astype(F32)
        for m in range(2):
            pass_up[m].wait_recv()
            up_out[m] = add(up_sum[m, here.z], up_in[m, 0], up_last[m])
        for copy in sent_near:
            copy.wait_recv()
        for copy in sent_near + sent_up + sent_down + sent_far + sent_pair[0] + sent_pair[1] + pass_up + [pass_down, sent_n]:
            copy.wait_send()


def back(dims, lens, d_own, d_peer, normed, qkv_far, mixed_far, qkv_own, mixed_own, wq, wo, wf,
         fin_img, fin_txt, up_keep, up_send, down_sum):
    model = normed.shape[-1]
    slab, quarter = dims.slab, dims.quarter
    hidden = up_keep.shape[-1]
    piece = model // 8
    held = pl.BlockSpec(memory_space=pltpu.VMEM)
    away = pl.BlockSpec(memory_space=pl.ANY)
    spec = lambda cols, at: pl.BlockSpec((quarter, slab, cols), lambda i: (at(i), 0, 0))
    early, late = lambda i: jnp.maximum(1 - i, 0), lambda i: jnp.where(i < 3, 1, 0)
    rows = (quarter, slab, model)
    outs = [(held, rows, F32), (held, (model, 512), BF16), (held, (model, 256), BF16),
            (held, (1, 768), F32), (held, (1, 384), F32),
            (away, fin_img.shape, BF16), (away, fin_txt.shape, BF16),
            (held, (4, piece, model + 256), BF16), (held, (2, piece, hidden), F32), (held, (2, piece, hidden), F32)]
    slabs = lambda cols: pltpu.VMEM((quarter, slab, cols), BF16)
    return pl.pallas_call(
        functools.partial(back_kernel, dims),
        grid=(4,),
        in_specs=[pl.BlockSpec(memory_space=pltpu.SMEM), held, held, spec(model, lambda i: 1 - i % 2),
                  spec(768, early), spec(256, early), spec(384, late), spec(128, late), held, held, held]
        + [away] * 5,
        out_specs=[v[0] for v in outs],
        out_shape=[jax.ShapeDtypeStruct(v[1], v[2]) for v in outs],
        scratch_shapes=[
            slabs(model), slabs(256), slabs(128), slabs(768), slabs(384),
            pltpu.VMEM((model, 1024), F32), pltpu.VMEM((model, 512), F32),
            pltpu.VMEM((768, model), BF16), pltpu.VMEM((384, model), BF16),
            pltpu.VMEM((256, model), BF16), pltpu.VMEM((128, model), BF16),
            pltpu.VMEM((2,) + rows, F32), pltpu.VMEM((model, model), BF16),
            pltpu.VMEM((4, 2, piece, hidden), BF16), pltpu.VMEM((2, 4, piece, hidden), BF16),
            pltpu.VMEM((2, 4, piece, hidden), BF16), pltpu.VMEM((2, 2, piece, hidden), BF16),
            pltpu.VMEM((2, piece, hidden), BF16), pltpu.VMEM((2, piece, hidden), BF16),
            pltpu.VMEM((2, 2, piece, hidden), BF16), pltpu.VMEM((2, 2, piece, hidden), BF16),
            pltpu.VMEM((2, piece, hidden), BF16), pltpu.VMEM((2, piece, hidden), BF16),
            pltpu.VMEM(rows, BF16), pltpu.VMEM(rows, BF16), pltpu.VMEM((4, piece, model + 256), BF16),
            pltpu.SemaphoreType.DMA((3,)), pltpu.SemaphoreType.DMA((28,)), pltpu.SemaphoreType.DMA((28,)),
        ],
        compiler_params=params(collective_id=4, has_side_effects=True),
        cost_estimate=pl.CostEstimate(
            flops=24 * quarter * slab * model * 1152, bytes_accessed=30_000_000, transcendentals=0),
        name="back",
    )(lens, d_own, d_peer, normed, qkv_far, mixed_far, qkv_own, mixed_own, wq, wo, wf,
      fin_img, fin_txt, up_keep, up_send, down_sum)


V_ROWS, V_MP, V_HEADS, V_FAR = 16, 11, 13, 256


def finish_kernel(dims, dnormed, dattended, states_img, states_txt, vec, fin_img, fin_txt,
                  near_img, near_txt, grad_pair, grad_far, own_sums, up_sums, cols_own, cols_far,
                  core_img, core_txt, across_img, across_txt, back_img, back_txt, grad_out, v_out,
                  s_img, s_txt, d_img, d_txt, rows, xr, zs, z_in, z_pass, z_last, f_in, f_pass, f_last, far_sum, far_recv, vs, vr,
                  local_sem, send_sem, recv_sem):
    quarter = dims.quarter
    here = Place()
    z, x, m = here.z, here.x, here.m
    near_quarter = here.quarter(1, 0)
    used = [0]

    def send(src, dst, device):
        at = used[0]
        used[0] += 1
        return remote(src, dst, send_sem, recv_sem, at, device)

    loaded = [pltpu.make_async_copy(states_img.at[pl.ds(m * quarter, quarter)], s_img, local_sem.at[0]),
              pltpu.make_async_copy(states_txt.at[pl.ds(m * quarter, quarter)], s_txt, local_sem.at[1])]
    for copy in loaded:
        copy.start()
    meet([here.core, here.near, here.side, here.paired, here.opposite])

    piece = xr.shape[1]
    wide = grad_pair.shape[1]
    block = lambda j: pl.ds(pl.multiple_of(j * piece, piece), piece)
    x_copies = []
    for j in range(4):
        x_copies.append(send(grad_pair.at[block(2 * j + 1 - x)], xr.at[j], here.side))
        x_copies[-1].start()
    add = lambda *parts: functools.reduce(lambda p, q: p + q, [v.astype(F32) for v in parts])
    in_pair = lambda src, dst: [send(src.at[here.z_pair], dst.at[0], here.paired),
                                send(src.at[here.z_rest], dst.at[1], here.paired)]
    far_copies = in_pair(grad_far, f_in)
    for copy in far_copies:
        copy.start()

    fin_remote = [send(src, dst, here.core) for src, dst in (
        (fin_img, core_img), (fin_txt, core_txt), (near_img, across_img), (near_txt, across_txt))]

    rows[...] = jnp.zeros_like(rows)
    for copy in loaded:
        copy.wait()
    total = [jnp.zeros((1, rows.shape[1]), F32)] * 2
    back_local, to_near, to_other = [], [], []
    for p in range(quarter):
        load_rows(dims, p, s_img, s_txt, rows)
        n, r = normalise(rows[...])
        dy = dnormed[p]
        total[0] = total[0] + jnp.sum(dy * n, axis=0, keepdims=True)
        total[1] = total[1] + jnp.sum(dy, axis=0, keepdims=True)
        d = dattended[p] + norm_back(n, r, dy * vector(vec, GAIN1))
        d_img[p] = d[0:dims.patches].astype(BF16)
        d_txt[p] = d[dims.ip:dims.ip + dims.caption].astype(BF16)
        for j, (src, dst) in enumerate(((d_img, back_img), (d_txt, back_txt))):
            at = dst.at[m * quarter + p]
            to_near.append(send(src.at[p], at, here.near))
            to_near[-1].start()
            to_other.append(send(src.at[p], at, here.core))
            to_other[-1].start()
            back_local.append(pltpu.make_async_copy(src.at[p], at, local_sem.at[2 + 2 * p + j]))
            back_local[-1].start()
    for copy in fin_remote:
        copy.start()

    at = lax.broadcasted_iota(jnp.int32, (V_ROWS, 1), 0)
    two, one_head = parts_of(dims)
    vs[0] = jnp.zeros(vs.shape[1:], F32)
    vs[0, 0:1, :] = total[0]
    vs[0, 1:2, :] = total[1]
    vs[0, 2:V_MP, :] = own_sums[0:V_MP - 2, :]
    vs[0, V_MP:V_HEADS, :] = up_sums[...]
    for j in range(2):
        own_at, far_at = 2 * j * two, 4 * j * two
        vs[0, V_HEADS + j:V_HEADS + j + 1, 0:two] = cols_own[0:1, own_at:own_at + two]
        vs[0, V_HEADS + j:V_HEADS + j + 1, two:two + one_head] = cols_far[0:1, far_at + two:far_at + two + one_head]
        vs[0, V_HEADS + j:V_HEADS + j + 1, V_FAR:V_FAR + two] = cols_far[0:1, far_at:far_at + two]
        vs[0, V_HEADS + j:V_HEADS + j + 1, V_FAR + two:V_FAR + two + one_head] = cols_far[0:1, far_at + two + one_head:far_at + 2 * two]
    v = vs[0]
    v_copies = []

    def exchange(step, value, device):
        vs[step] = value
        copy = send(vs.at[step], vr.at[step], device)
        copy.start()
        copy.wait_recv()
        v_copies.append(copy)
        return vr[step]

    v = v + jnp.where(at < V_MP, exchange(0, v, here.core), 0.0)
    for copy in far_copies:
        copy.wait_recv()
    f_pass[...] = add(grad_far[here.z_far], f_in[1]).astype(BF16)
    far_copies.append(send(f_pass, f_last, here.opposite))
    far_copies[-1].start()
    v = v + exchange(1, v, here.side)
    v = v + exchange(2, v, here.paired)
    vs[3] = v
    v_far = send(vs.at[3], vr.at[3], here.opposite)
    v_far.start()

    def own_sum(j):
        return add(grad_pair[block(2 * j + x), :], xr[j])

    for copy in x_copies:
        copy.wait_recv()
    for j in range(4):
        zs[j] = own_sum(j).astype(BF16)
    z_copies = in_pair(zs, z_in)
    for copy in z_copies:
        copy.start()

    far_copies[-1].wait_recv()
    narrow = far_sum.shape[1]
    far_sum[...] = add(grad_far[z, :, 0:narrow], f_in[0, :, 0:narrow], f_last[:, 0:narrow]).astype(BF16)
    far_copy = send(far_sum, far_recv, here.near)
    far_copy.start()
    v_far.wait_recv()
    v = v + vr[3]
    for copy in z_copies:
        copy.wait_recv()
    z_pass[...] = add(zs[here.z_far], z_in[1]).astype(BF16)
    z_copies.append(send(z_pass, z_last, here.opposite))
    z_copies[-1].start()
    vs[4] = v
    v_near = send(vs.at[4], vr.at[4], here.near)
    v_near.start()
    for copy in back_local:
        copy.wait()
    onward = []
    for p in range(quarter):
        for j, dst in enumerate((back_img, back_txt)):
            to_near[2 * p + j].wait_recv()
            at_near = dst.at[near_quarter * quarter + p]
            onward.append(send(at_near, at_near, here.core))
            onward[-1].start()
    far_copy.wait_recv()
    z_copies[-1].wait_recv()
    grad_out[:, 0:wide] = own_sum(z) + add(far_recv[:, 0:wide], z_in[0], z_last[...])
    grad_out[:, wide:] = add(
        far_recv[:, wide:], grad_far[z, :, narrow:], f_in[0, :, narrow:], f_last[:, narrow:])
    v_near.wait_recv()
    there = vr[4]
    v_out[...] = v + jnp.where(at < V_MP, there, 0.0)
    width = two + one_head
    v_out[V_HEADS:V_HEADS + 2, 0:width] = v[V_HEADS:V_HEADS + 2, 0:width] + there[V_HEADS:V_HEADS + 2, V_FAR:V_FAR + width]
    for copy in to_other + fin_remote + onward:
        copy.wait()
    for copy in x_copies + far_copies + to_near + z_copies + v_copies + [far_copy, v_near, v_far]:
        copy.wait_send()


def finish(dims, dnormed, dattended, states_img, states_txt, vec, fin_img, fin_txt,
           near_img, near_txt, grad_pair, grad_far, *tables):
    pairs, patches, model = states_img.shape
    caption = states_txt.shape[1]
    quarter, slab = dims.quarter, dims.slab
    piece, cols = grad_far.shape[1], model
    wide, all_cols = grad_pair.shape[1], grad_far.shape[2]
    held = pl.BlockSpec(memory_space=pltpu.VMEM)
    away = pl.BlockSpec(memory_space=pl.ANY)
    n_remote = 7 * quarter + 28
    return pl.pallas_call(
        functools.partial(finish_kernel, dims),
        in_specs=[held, held] + [away] * 2 + [held] + [away] * 4 + [held] * 6,
        out_specs=[away] * 6 + [held] * 2,
        out_shape=[jax.ShapeDtypeStruct(v.shape, BF16) for v in (fin_img, fin_txt) * 2] + [
            jax.ShapeDtypeStruct((pairs, patches, model), BF16),
            jax.ShapeDtypeStruct((pairs, caption, model), BF16),
            jax.ShapeDtypeStruct((piece, cols), F32),
            jax.ShapeDtypeStruct((V_ROWS, model), F32),
        ],
        scratch_shapes=[
            pltpu.VMEM((quarter, patches, model), BF16),
            pltpu.VMEM((quarter, caption, model), BF16),
            pltpu.VMEM((quarter, patches, model), BF16),
            pltpu.VMEM((quarter, caption, model), BF16),
            pltpu.VMEM((slab, model), F32),
            pltpu.VMEM((4, piece, wide), BF16), pltpu.VMEM((4, piece, wide), BF16),
            pltpu.VMEM((2, piece, wide), BF16), pltpu.VMEM((piece, wide), BF16), pltpu.VMEM((piece, wide), BF16),
            pltpu.VMEM((2, piece, all_cols), BF16), pltpu.VMEM((piece, all_cols), BF16), pltpu.VMEM((piece, all_cols), BF16),
            pltpu.VMEM((piece, cols), BF16), pltpu.VMEM((piece, cols), BF16),
            pltpu.VMEM((5, V_ROWS, model), F32),
            pltpu.VMEM((5, V_ROWS, model), F32),
            pltpu.SemaphoreType.DMA((2 + 2 * quarter,)),
            pltpu.SemaphoreType.DMA((n_remote,)),
            pltpu.SemaphoreType.DMA((n_remote,)),
        ],
        compiler_params=params(collective_id=1, has_side_effects=True),
        name="finish",
    )(dnormed, dattended, states_img, states_txt, vec, fin_img, fin_txt,
      near_img, near_txt, grad_pair, grad_far, *tables)


def spread_kernel(dims, cols, sums, grad, gains, shifts, up, down, head_in, dproj, *refs):
    forward, refs = refs[:8], refs[8:]
    back_img, back_txt, *refs = refs
    outs, refs = refs[:12], refs[12:]
    (qkv, out_w, up_out, down_out, head_out, out_img, out_txt, grad_img, grad_txt,
     turned, held_img, held_txt, in_sem, out_sem) = refs
    here = Place()
    quarter = dims.quarter
    whose = [here.quarter(0, 0), here.quarter(1, 0), here.quarter(0, 1), here.quarter(1, 1)]
    place = lambda q: pl.ds(q * quarter, quarter)
    comes, goes = [], []
    for r in range(4):
        for j, (held, src, dst, back, to) in enumerate((
            (held_img, forward[2 * r], out_img, back_img, grad_img), (held_txt, forward[2 * r + 1], out_txt, back_txt, grad_txt),
        )):
            for k, (source, target, q) in enumerate(((src, dst, whose[r]), (back.at[place(r)], to, r))):
                at = 4 * r + 2 * j + k
                comes.append(pltpu.make_async_copy(source, held.at[2 * r + k], in_sem.at[at]))
                goes.append(pltpu.make_async_copy(held.at[2 * r + k], target.at[place(q)], out_sem.at[at]))
    for copy in comes:
        copy.start()
    turn_by = sums.shape[1] - here.b * cols

    def slice_of(value):
        return pltpu.roll(value, turn_by, 1)[:, 0:cols]

    mine = slice_of(sums[...])
    for out, (lo, count) in zip(outs[:8], ((0, 1), (1, 1), (7, 1), (6, 1), (2, 2), (4, 2), (9, 2), (8, 1))):
        out[...] = mine[lo:lo + count, :]
    wide = jnp.concatenate([gains[...], shifts[...], jnp.zeros((4, sums.shape[1]), F32)], axis=0)
    heads = slice_of(wide)
    outs[8][...] = heads[0:2, :]
    outs[9][...] = heads[2:4, :]
    outs[10][...] = sums[V_MP:V_MP + 2, :]
    outs[11][...] = sums[V_HEADS:V_HEADS + 2, 0:outs[11].shape[1]]
    two, one = 2 * HEAD_DIM, HEAD_DIM
    for t in range(3):
        qkv[t, :, 0:two] = grad[:, t * two:(t + 1) * two]
        qkv[t, :, two:two + one] = grad[:, 4 * two + t * one:4 * two + (t + 1) * one]
    turned[...] = jnp.zeros_like(turned)
    turned[0:cols, 0:two] = grad[:, 3 * two:4 * two]
    turned[0:cols, two:two + one] = grad[:, 4 * two + 3 * one:4 * two + 4 * one]
    out_w[...] = turned[...].T[0:two + one, 0:cols]
    up_out[...] = up[...]
    down_out[...] = down[...]
    for come, go in zip(comes, goes):
        come.wait()
        go.start()
    for m in range(2):
        part = pltpu.roll(head_in[m].astype(F32), turn_by, 1)[:, 0:128].astype(BF16)
        head_out[m] = t_dot(part, dproj[m])[0:cols]
    for go in goes:
        go.wait()


def spread(dims, sums, grad, gains, shifts, up, down, head_in, dproj, forward, back_img, back_txt):
    cols, model = grad.shape[0], sums.shape[1]
    local, quarter = dims.local, dims.quarter
    assert cols <= 128
    shapes = [(1, cols)] * 4 + [(2, cols)] * 3 + [(1, cols)] + [(2, cols)] * 2 + [(2, model), (2, local)]
    shapes += [(3, cols, local), (local, cols), up.shape, down.shape, (2, cols, dproj.shape[2])]
    held = pl.BlockSpec(memory_space=pltpu.VMEM)
    away = pl.BlockSpec(memory_space=pl.ANY)
    args = (sums, grad, gains, shifts, up, down, head_in, dproj)
    return pl.pallas_call(
        functools.partial(spread_kernel, dims, cols),
        in_specs=[held] * len(args) + [away] * 10,
        out_specs=[held] * len(shapes) + [away] * 4,
        out_shape=[jax.ShapeDtypeStruct(v, F32) for v in shapes]
        + [jax.ShapeDtypeStruct(v.shape, BF16) for v in (back_img, back_txt) * 2],
        scratch_shapes=[
            pltpu.VMEM((128, 256), F32),
            pltpu.VMEM((8, quarter, dims.patches, model), BF16), pltpu.VMEM((8, quarter, dims.caption, model), BF16),
            pltpu.SemaphoreType.DMA((16,)), pltpu.SemaphoreType.DMA((16,)),
        ],
        compiler_params=params(),
        cost_estimate=pl.CostEstimate(flops=1_000_000, bytes_accessed=20_000_000, transcendentals=0),
        name="spread",
    )(*args, *forward, back_img, back_txt)


def per_device(
    image_states, text_states, caption_lengths, image_cotangent, text_cotangent,
    first_gain, first_shift, query_key_value, query_value_bias, output_weight, output_bias,
    attention_scale, expert_gain, expert_shift, expert_up, expert_up_bias, expert_down,
    expert_down_bias, feedforward_scale, head_gain, head_shift, head_weight, logit_scale,
):
    pairs, patches, model = image_states.shape
    caption = text_states.shape[1]
    local = query_key_value.shape[2]
    quarter = pairs // 4
    batch_size = lax.axis_size("batch")
    assert lax.axis_size("mp") == 4 and pairs == 4 * quarter and quarter <= 3
    assert batch_size & (batch_size - 1) == 0
    assert local == 3 * HEAD_DIM
    ip, tp = up16(patches), up16(caption)
    dims = Dims(patches, caption, ip, tp, ip + tp, quarter, local)
    me = lax.axis_index("mp")
    batch_at = lax.axis_index("batch")
    order = me ^ jnp.asarray(ORDER, jnp.int32)
    vectors = (first_gain, first_shift, attention_scale, output_bias, expert_gain, expert_shift,
               feedforward_scale, expert_down_bias, head_gain, head_shift)
    own_w = jnp.transpose(query_key_value, (1, 2, 0)).reshape(3 * local, model)
    one_kernel = batch_size == 8 and model // batch_size % 32 == 0 and expert_up.shape[2] == model
    if one_kernel:
        (vec, normed, qkv_own, mixed_own, qkv_far, mixed_far, wf, attended, attn, e_own, e_peer, cls_own, cls_peer) = front(
            dims, caption_lengths, image_states, text_states, vectors, query_value_bias, own_w, output_weight)
    else:
        vec = jnp.concatenate([v.reshape(-1, model) for v in vectors] + [jnp.zeros((1, model), F32)])
        wo = jnp.concatenate([own_w, output_weight])
        wf = to_y(wo)
        far_bias = to_y(query_value_bias)
        normed, qkv_own, rest, mixed_own = attend_own(
            dims, order, caption_lengths, image_states, text_states, vec, query_value_bias, wo)
        qkv_far, mixed_far, a_keep, a_send = attend_far(
            dims, order, caption_lengths, normed, rest, mixed_own, far_bias, wo, wf)
        a_recv = to_core(a_send)
        attended, attn, e_own, cls_own = residual(
            dims, order, a_keep, a_recv, image_states, text_states, vec)
        e_peer = to_core(e_own)
        cls_peer = to_core(cls_own)
    if one_kernel:
        (act, dup, ddn, dexp, d_own, d_near, up_sums, class_e, c_act, c_dup, c_ddn, dcls, head_in, dproj,
         grad_head_gain, grad_head_shift, scalars) = middle(
            dims, pairs * batch_size, image_cotangent, text_cotangent, e_own, e_peer, cls_own, cls_peer, vec,
            expert_up, expert_up_bias, expert_down, head_weight, logit_scale.reshape(1, 1))
        down_sum, up_keep, up_send, dattended, dattn, dattn_peer, fin_img, fin_txt, own_sums = turn(
            dims, image_cotangent, text_cotangent, e_peer, e_own, act, dup, ddn, class_e, c_act, c_dup, c_ddn,
            dexp, attended, attn, d_own, d_near, dcls, vec)
    else:
        class_part, class_e = class_forward(dims, cls_own, cls_peer, expert_up, expert_up_bias, expert_down)
        class_parts = from_others(class_part, "mp", 1, 4)

        act_a, dup_a, ddn_a, d_send3, d_keep1, x_send3, x_keep1, bias_a, cot_a = experts(
            dims, "experts_a", 1, order[jnp.asarray([3, 1])], e_peer, e_own, image_cotangent, text_cotangent,
            tie(vec, class_part), expert_up, expert_up_bias, expert_down)
        x_recv1 = to_core(x_send3)
        d_recv1 = to_core(d_send3)
        final_class = class_final(
            dims, order, cls_own, cls_peer, class_parts, tie(vec, bias_a))
        class_blocks = gather_batch(final_class[None])
        x_near = add_low(x_keep1, x_recv1)
        x_far = to_y(x_near)
        act_b, dup_b, ddn_b, d_send2, d_keep0, x_send2, x_keep0, bias_b, cot_b = experts(
            dims, "experts_b", 0, order[jnp.asarray([2, 0])], e_peer, e_own, image_cotangent, text_cotangent,
            tie(vec, final_class, x_near), expert_up, expert_up_bias, expert_down)
        x_recv0 = to_core(x_send2)
        d_recv0 = to_core(d_send2)

        head_in, dproj, dclass, grad_head_gain, grad_head_shift, scalars = (contrast if batch_size <= 8 else contrast_large)(
            dims, pairs * batch_size, batch_at.reshape(1), class_blocks, tie(vec, bias_b), head_weight,
             logit_scale.reshape(1, 1))
        c_act, c_dup, c_ddn, c_dexp, c_bias, dcls = class_back(
            dims, order, class_e, cot_a, cot_b, dclass, vec, expert_up, expert_up_bias, expert_down)
        extras = from_others(c_dexp, "mp", 1, 4)
        d_far = to_y(add_low(d_keep1, tie(d_recv1, c_dexp)))
        expert_grad = expert_grads(
            dims, e_peer, e_own, act_a, dup_a, ddn_a, act_b, dup_b, ddn_b, class_e, c_act, c_dup, c_ddn)
        expert_sum = lax.psum_scatter(expert_grad, "batch", scatter_dimension=1, tiled=True)

        dattended, dattn, sums_two = norm_two(
            dims, order, x_keep0, x_recv0, x_far, attended, a_keep, a_recv, image_cotangent, text_cotangent,
            dcls, extras, tie(vec, expert_grad))
        dattn_peer = to_core(dattn)
        fin_img, fin_txt, sums_fin = final_rows(
            dims, order, d_keep0, d_recv0, d_far, attended, image_cotangent, text_cotangent, dcls,
            tie(vec, sums_two))
        own_sums = jnp.concatenate([sums_two[:6], sums_fin[:3]])
        up_sums = bias_a + bias_b + c_bias
    contrast_loss = scalars[0, :1]
    grad_logit_scale = scalars[1, :1]
    if one_kernel:
        (dnormed, grad_o01, grad_o2, cols_far, cols_own, near_img, near_txt, far_sum, grad_down,
         grad_up) = back(
            dims, caption_lengths, dattn, dattn_peer, normed, qkv_far, mixed_far, qkv_own, mixed_own,
            own_w, output_weight, wf, fin_img, fin_txt, up_keep, up_send, down_sum)
    else:
        n_keep, n_send, grad_far, grad_o2, cols_far = attend_back(
            dims, True, order, caption_lengths, dattn, dattn_peer, normed, qkv_far, mixed_far, own_w, output_weight, wf)
        n_keep, n_send, grad_o01, cols_own = attend_back(
            dims, False, order, caption_lengths, dattn, dattn_peer, normed, qkv_own, mixed_own, own_w, output_weight, wf,
            prior=(n_keep, n_send))
    cols = model // batch_size
    mine = lambda v, axis: lax.dynamic_slice_in_dim(v, batch_at * cols, cols, axis=axis)
    pair, single = 2 * HEAD_DIM, HEAD_DIM
    if one_kernel:
        core_img, core_txt, across_img, across_txt, back_img, back_txt, attn_grad, sums = finish(
            dims, dnormed, dattended, image_states, text_states, vec, fin_img, fin_txt,
            near_img, near_txt, grad_o01, far_sum, own_sums, up_sums, cols_own, cols_far)
        forward = (fin_img, fin_txt, near_img, near_txt, core_img, core_txt, across_img, across_txt)
        (*vectors, grad_qkv, grad_output_weight, grad_up, grad_down, grad_head_weight,
         image_output, text_output, image_grad, text_grad) = spread(
            dims, sums, attn_grad, grad_head_gain, grad_head_shift, grad_up, grad_down, head_in, dproj,
            forward, back_img, back_txt)
        flat = lambda v: v.reshape(-1)
        return (
            image_output,
            text_output,
            contrast_loss,
            image_grad,
            text_grad,
            flat(vectors[0]),
            flat(vectors[1]),
            jnp.transpose(grad_qkv, (1, 0, 2)),
            vectors[11],
            grad_output_weight,
            flat(vectors[2]),
            flat(vectors[3]),
            vectors[4],
            vectors[5],
            grad_up,
            vectors[10],
            jnp.transpose(grad_down, (0, 2, 1)),
            vectors[6],
            flat(vectors[7]),
            vectors[8],
            vectors[9],
            grad_head_weight,
            grad_logit_scale,
        )
    else:
        grad_head_weight = jnp.einsum("mnc,mne->mce", mine(head_in, 2), dproj, preferred_element_type=F32)
        grad_expert_up = expert_sum[:2].astype(F32)
        grad_expert_down = jnp.transpose(expert_sum[2:].astype(F32), (0, 2, 1))
        cols_own = cols_own.reshape(3, pair)[::2]
        cols_far = cols_far.reshape(3, 2 * pair)[::2]
        heads = jnp.concatenate([cols_own, cols_far[:, pair:pair + single]], axis=1)
        heads_far = jnp.concatenate([cols_far[:, :pair], cols_far[:, pair + single:]], axis=1)
        n_recv = to_core(n_send)
        d_img, d_txt, sums_one = norm_one(
            dims, order, n_keep, n_recv, dattended, image_states, text_states, vec)
        image_output = gather_rows(fin_img, me)
        text_output = gather_rows(fin_txt, me)
        image_grad = gather_rows(d_img, me)
        text_grad = gather_rows(d_txt, me)
        grad_own = jnp.concatenate([grad_o01, grad_o2], axis=1)
        grad_far = lax.psum_scatter(grad_far, "batch", scatter_dimension=0, tiled=True)
        grad_own = lax.psum_scatter(grad_own, "batch", scatter_dimension=0, tiled=True)
        attn_grad = grad_own.astype(F32) + to_y(grad_far).astype(F32)
        heads = heads + to_y(heads_far)
        own_sums = sum_over(jnp.concatenate([sums_one[:2], own_sums]), "mp")
        flat = jnp.concatenate([own_sums.reshape(-1), heads.reshape(-1), up_sums.reshape(-1)])
        count = flat.shape[0]
        flat = jnp.pad(flat, (0, -count % 1024)).reshape(-1, 128)
        flat = sum_over(flat, "batch").reshape(-1)[:count]
        done = own_sums.shape[0]
        own_sums = mine(flat[:done * model].reshape(done, model), 1)
        heads = flat[done * model:done * model + 2 * local].reshape(2, local)
        grad_expert_up_bias = flat[done * model + 2 * local:].reshape(up_sums.shape)
    attn_grad = jnp.concatenate(
        [attn_grad[:, :4 * pair].reshape(cols, 4, pair), attn_grad[:, 4 * pair:].reshape(cols, 4, single)], axis=2)
    grad_query_key_value = attn_grad[:, :3]
    grad_output_weight = jnp.transpose(attn_grad[:, 3])
    return (
        image_output,
        text_output,
        contrast_loss,
        image_grad,
        text_grad,
        own_sums[0],
        own_sums[1],
        grad_query_key_value,
        heads,
        grad_output_weight,
        own_sums[7],
        own_sums[6],
        own_sums[2:4],
        own_sums[4:6],
        grad_expert_up,
        grad_expert_up_bias,
        grad_expert_down,
        own_sums[9:11],
        own_sums[8],
        mine(grad_head_gain, 1),
        mine(grad_head_shift, 1),
        grad_head_weight,
        grad_logit_scale,
    )


def solution(mesh):
    return jax.shard_map(
        per_device,
        mesh=mesh,
        in_specs=(
            P("batch", None, None),
            P("batch", None, None),
            P("batch"),
            P("batch", None, None),
            P("batch", None, None),
            P(),
            P(),
            P(None, None, "mp"),
            P(None, "mp"),
            P("mp", None),
            P(),
            P(),
            P(),
            P(),
            P(None, None, "mp"),
            P(None, "mp"),
            P(None, "mp", None),
            P(),
            P(),
            P(),
            P(),
            P(),
            P(),
        ),
        out_specs=(
            P("batch", None, None),
            P("batch", None, None),
            P(),
            P("batch", None, None),
            P("batch", None, None),
            P("batch"),
            P("batch"),
            P("batch", None, "mp"),
            P(None, "mp"),
            P("mp", "batch"),
            P("batch"),
            P("batch"),
            P(None, "batch"),
            P(None, "batch"),
            P(None, "batch", "mp"),
            P(None, "mp"),
            P(None, "mp", "batch"),
            P(None, "batch"),
            P("batch"),
            P(None, "batch"),
            P(None, "batch"),
            P(None, "batch", None),
            P(),
        ),
        check_vma=False,
    )
```

```python
import functools
from typing import NamedTuple

import jax
import jax.numpy as jnp
from jax import lax
from jax.experimental import pallas as pl
from jax.experimental.pallas import tpu as pltpu
from jax.sharding import PartitionSpec as P

HEAD_DIM = 64
F32 = jnp.float32
BF16 = jnp.bfloat16
NEG = -1e9
EPS = 1e-5
ORDER = (0, 2, 1, 3)

VMEM_LIMIT = 60 * 1024 * 1024


def params(**kw):
    return pltpu.CompilerParams(vmem_limit_bytes=VMEM_LIMIT, **kw)


def up16(n):
    return -(-n // 16) * 16


def dot(a, b):
    return jnp.dot(a, b, preferred_element_type=F32)


def dot_t(a, b):
    return lax.dot_general(a, b, (((1,), (1,)), ((), ())), preferred_element_type=F32)


def t_dot(a, b):
    return lax.dot_general(a, b, (((0,), (0,)), ((), ())), preferred_element_type=F32)


def normalise(x):
    c = x - jnp.mean(x, axis=-1, keepdims=True)
    v = jnp.mean(c * c, axis=-1, keepdims=True)
    r = lax.rsqrt(v + EPS)
    return c * r, r


def norm_back(n, r, dn):
    a = jnp.mean(dn, axis=-1, keepdims=True)
    b = jnp.mean(dn * n, axis=-1, keepdims=True)
    return (dn - a - n * b) * r


def gelu_parts(u):
    big = 0.5 * (1.0 + lax.erf(u * 0.7071067811865476))
    small = 0.3989422804014327 * jnp.exp(-0.5 * u * u)
    return big, small


def gelu_low(u):
    return (u * (0.5 * (1.0 + lax.erf(u * 0.7071067811865476)))).astype(BF16)


def softmax_rows(scores):
    m = jnp.max(scores, axis=-1, keepdims=True)
    e = jnp.exp(scores - m)
    return e * (1.0 / jnp.sum(e, axis=-1, keepdims=True))


def tie(value, *after):
    return lax.optimization_barrier((value,) + after)[0]


def load_rows(dims, p, img, txt, rows):
    rows[0:dims.patches, :] = img[p].astype(F32)
    rows[dims.ip:dims.ip + dims.caption, :] = txt[p].astype(F32)


def spec_whole(a):
    return pl.BlockSpec(a.shape, lambda *_: (0,) * a.ndim)


class Dims(NamedTuple):
    patches: int
    caption: int
    ip: int
    tp: int
    slab: int
    quarter: int
    local: int


GAIN1, SHIFT1, A_SCALE, A_BIAS, GAIN2, SHIFT2, F_SCALE, F_BIAS, H_GAIN, H_SHIFT = 0, 1, 2, 3, 4, 6, 8, 9, 11, 13


def vector(table, at, count=1):
    return table[at:at + count, :]


def copy_rows(dst, at, src, start, count):
    dst[at:at + count, :] = src[start:start + count, :]


def parts_of(dims):
    return 2 * HEAD_DIM, HEAD_DIM


def key_tail(dims, length):
    at = dims.patches // 16 * 16
    return ((0, dims.ip, at, dims.patches), (dims.ip, dims.slab, 0, length))


def hide(scores, start, limit):
    if start >= scores.shape[0]:
        return scores
    tail = scores[start:]
    at = start + lax.broadcasted_iota(jnp.int32, (tail.shape[0], 1), 0)
    tail = jnp.where(at < limit, tail, NEG)
    return tail if start == 0 else jnp.concatenate([scores[:start], tail], axis=0)


def split_pair(value):
    low = lax.broadcasted_iota(jnp.int32, (1, 128), 1) < HEAD_DIM
    zero = jnp.zeros_like(value)
    return jnp.concatenate([jnp.where(low, value, zero), jnp.where(low, zero, value)], axis=0)


def join_pair(value):
    low = lax.broadcasted_iota(jnp.int32, (1, 128), 1) < HEAD_DIM
    half = value.shape[0] // 2
    return jnp.where(low, value[:half], value[half:])


def softmax_keys(scores):
    e = jnp.exp(scores - jnp.max(scores, axis=0, keepdims=True))
    return e * (1.0 / jnp.sum(e, axis=0, keepdims=True))


def pair_weights(q, k, start, limit):
    return softmax_keys(hide(dot_t(k, split_pair(q)), start, limit))


def scaled(q):
    return q * jnp.asarray(HEAD_DIM ** -0.5, BF16)


def attend_tiles(dims, lens, quarter_at, qkv, mixed):
    tiles = mixed.shape[-1] // 128

    def one_pair(p, c):
        length = lens[quarter_at * dims.quarter + p]
        for lo, hi, start, limit in key_tail(dims, length):
            for g in range(tiles):
                q, k, v = [qkv[p, lo:hi, (t * tiles + g) * 128:(t * tiles + g + 1) * 128] for t in range(3)]
                w = pair_weights(scaled(q), k, start, limit).astype(BF16)
                mixed[p, lo:hi, g * 128:(g + 1) * 128] = join_pair(t_dot(w, v)).astype(BF16)
        return c

    lax.fori_loop(0, dims.quarter, one_pair, 0)


def attend_own_kernel(dims, order, lens, img, txt, vec, bias, wo, normed, qkv, rest, mixed, rows, w, b):
    i = pl.program_id(0)
    local = dims.local
    two, one_head = parts_of(dims)

    @pl.when(i == 0)
    def _():
        rows[...] = jnp.zeros_like(rows)
        w[...] = jnp.zeros_like(w)
        b[...] = jnp.zeros_like(b)
        for t in range(3):
            copy_rows(w, t * 2 * two, wo, t * local, local)
        b[0:1, 0:local] = bias[0:1, :]
        b[0:1, 4 * two:4 * two + local] = bias[1:2, :]

    def one_norm(p, c):
        load_rows(dims, p, img, txt, rows)
        n, _ = normalise(rows[...])
        normed[p] = (n * vector(vec, GAIN1) + vector(vec, SHIFT1)).astype(BF16)
        return c

    lax.fori_loop(0, dims.quarter, one_norm, 0)
    model = normed.shape[-1]
    proj = (dot_t(normed[...].reshape(dims.quarter * dims.slab, model), w[...]) + b[0:1, :]).astype(BF16)
    proj = proj.reshape(dims.quarter, dims.slab, 6 * two)
    for t in range(3):
        qkv[:, :, t * two:(t + 1) * two] = proj[:, :, 2 * t * two:(2 * t + 1) * two]
        rest[:, :, t * two:(t + 1) * two] = proj[:, :, (2 * t + 1) * two:(2 * t + 2) * two]
    attend_tiles(dims, lens, order[i], qkv, mixed)


def attend_own(dims, order, lens, img, txt, vec, bias, wo):
    model = img.shape[-1]
    pairs = 4 * dims.quarter
    block = lambda cols: pl.BlockSpec((dims.quarter, dims.slab, cols), lambda i, o, n: (i, 0, 0))
    shape = lambda cols: jax.ShapeDtypeStruct((pairs, dims.slab, cols), BF16)
    return pl.pallas_call(
        functools.partial(attend_own_kernel, dims),
        grid_spec=pltpu.PrefetchScalarGridSpec(
            num_scalar_prefetch=2,
            grid=(4,),
            in_specs=[
                pl.BlockSpec((dims.quarter, dims.patches, model), lambda i, o, n: (o[i], 0, 0)),
                pl.BlockSpec((dims.quarter, dims.caption, model), lambda i, o, n: (o[i], 0, 0)),
                spec_whole(vec), spec_whole(bias), spec_whole(wo),
            ],
            out_specs=[block(model), block(384), block(384), block(128)],
            scratch_shapes=[pltpu.VMEM((dims.slab, model), F32), pltpu.VMEM((768, model), BF16),
                            pltpu.VMEM((8, 768), F32)],
        ),
        out_shape=[shape(model), shape(384), shape(384), shape(128)],
        compiler_params=params(),
        cost_estimate=pl.CostEstimate(
            flops=1536 * pairs * dims.slab * model, bytes_accessed=30_000_000, transcendentals=0),
        name="attend_own",
    )(order, lens, img, txt, vec, bias, wo)


def attend_far_kernel(dims, order, lens, normed, rest, own, bias, wo, wf, qkv, mixed, keep, send, w, ow, b):
    i = pl.program_id(0)
    local = dims.local
    two, one_head = parts_of(dims)
    count = dims.quarter * dims.slab
    model = normed.shape[-1]

    @pl.when(i == 0)
    def _():
        w[...] = jnp.zeros_like(w)
        b[...] = jnp.zeros_like(b)
        for t in range(3):
            copy_rows(w, t * 2 * two, wf, t * local, two)
            copy_rows(w, t * 2 * two + two + one_head, wf, t * local + two, one_head)
        for t, at in ((0, 0), (1, 4 * two)):
            b[0:1, at:at + two] = bias[t:t + 1, 0:two]
            b[0:1, at + two + one_head:at + 2 * two] = bias[t:t + 1, two:]
        copy_rows(ow, 0, wo, 3 * local, two)
        copy_rows(ow, two, wf, 3 * local, two)
        copy_rows(ow, 2 * two, wo, 3 * local + two, one_head)
        copy_rows(ow, 2 * two + one_head, wf, 3 * local + two, one_head)

    proj = (dot_t(normed[...].reshape(count, model), w[...]) + b[0:1, :]).astype(BF16)
    proj = proj.reshape(dims.quarter, dims.slab, 6 * two)
    for t in range(3):
        at = 2 * t * two
        qkv[:, :, at:at + two] = proj[:, :, at:at + two]
        qkv[:, :, at + two:at + 2 * two] = proj[:, :, at + two:at + 2 * two] + rest[:, :, t * two:(t + 1) * two]
    attend_tiles(dims, lens, order[(i + 2) % 4], qkv, mixed)
    part = dot(own[...].reshape(count, two), ow[0:two, :])
    part = part + dot(mixed[...].reshape(count, 2 * two), ow[two:, :])
    part = part.astype(BF16).reshape(dims.quarter, dims.slab, model)

    @pl.when(i < 2)
    def _():
        send[...] = part

    @pl.when(i >= 2)
    def _():
        keep[...] = part


def attend_far(dims, order, lens, normed, rest, own, bias, wo, wf):
    model = normed.shape[-1]
    pairs = 4 * dims.quarter
    at = lambda i: (i + 2) % 4
    block = lambda cols, f: pl.BlockSpec((dims.quarter, dims.slab, cols), lambda i, o, n: (f(i), 0, 0))
    shape = lambda count, cols: jax.ShapeDtypeStruct((count, dims.slab, cols), BF16)
    return pl.pallas_call(
        functools.partial(attend_far_kernel, dims),
        grid_spec=pltpu.PrefetchScalarGridSpec(
            num_scalar_prefetch=2,
            grid=(4,),
            in_specs=[
                block(model, at), block(384, at), block(128, at),
                spec_whole(bias), spec_whole(wo), spec_whole(wf),
            ],
            out_specs=[
                block(768, at), block(256, at),
                block(model, lambda i: jnp.maximum(i - 2, 0)), block(model, lambda i: jnp.minimum(i, 1)),
            ],
            scratch_shapes=[pltpu.VMEM((768, model), BF16), pltpu.VMEM((384, model), BF16),
                            pltpu.VMEM((8, 768), F32)],
        ),
        out_shape=[
            shape(pairs, 768), shape(pairs, 256),
            shape(2 * dims.quarter, model), shape(2 * dims.quarter, model),
        ],
        compiler_params=params(),
        cost_estimate=pl.CostEstimate(
            flops=2304 * pairs * dims.slab * model, bytes_accessed=30_000_000, transcendentals=0),
        name="attend_far",
    )(order, lens, normed, rest, own, bias, wo, wf)


def residual_kernel(dims, order, keep, recv, img, txt, vec, attended, attn, expert, cls, rows):
    i = pl.program_id(0)
    ip = dims.ip

    @pl.when(i == 0)
    def _():
        rows[...] = jnp.zeros_like(rows)
        cls[...] = jnp.zeros_like(cls)

    load_rows(dims, 0, img, txt, rows)
    a = keep[0].astype(F32) + recv[0].astype(F32)
    x = rows[...] + vector(vec, A_SCALE) * (a + vector(vec, A_BIAS))
    n, _ = normalise(x)
    e_img = n[0:ip] * vector(vec, GAIN2) + vector(vec, SHIFT2)
    e_txt = n[ip:] * vector(vec, GAIN2 + 1) + vector(vec, SHIFT2 + 1)
    expert[0, 0:ip, :] = e_img.astype(BF16)
    expert[0, ip:, :] = e_txt.astype(BF16)
    for j, v in enumerate((x[0:1], x[ip:ip + 1], e_img[0:1], e_txt[0:1])):
        cls[j, pl.ds(i, 1), :] = v

    @pl.when(i < dims.quarter)
    def _():
        attended[0] = x
        attn[0] = a


def residual(dims, order, keep, recv, img, txt, vec):
    model = img.shape[-1]
    quarter = dims.quarter
    block = pl.BlockSpec((1, dims.slab, model), lambda i, o: (i, 0, 0))
    pair = lambda i, o: (o[i // quarter] * quarter + i % quarter, 0, 0)
    return pl.pallas_call(
        functools.partial(residual_kernel, dims),
        grid_spec=pltpu.PrefetchScalarGridSpec(
            num_scalar_prefetch=1,
            grid=(2 * quarter,),
            in_specs=[
                block, block,
                pl.BlockSpec((1, dims.patches, model), pair),
                pl.BlockSpec((1, dims.caption, model), pair),
                spec_whole(vec),
            ],
            out_specs=[
                pl.BlockSpec((1, dims.slab, model), lambda i, o: (jnp.minimum(i, quarter - 1), 0, 0)),
                pl.BlockSpec((1, dims.slab, model), lambda i, o: (jnp.minimum(i, quarter - 1), 0, 0)),
                block,
                pl.BlockSpec((4, 8, model), lambda i, o: (0, 0, 0)),
            ],
            scratch_shapes=[pltpu.VMEM((dims.slab, model), F32)],
        ),
        out_shape=[
            jax.ShapeDtypeStruct((quarter, dims.slab, model), F32),
            jax.ShapeDtypeStruct((quarter, dims.slab, model), F32),
            jax.ShapeDtypeStruct((2 * quarter, dims.slab, model), BF16),
            jax.ShapeDtypeStruct((4, 8, model), F32),
        ],
        compiler_params=params(),
        cost_estimate=pl.CostEstimate(flops=40_000_000, bytes_accessed=20_000_000, transcendentals=0),
        name="residual",
    )(order, keep, recv, img, txt, vec)


def expert_kernel(dims, seq, peer, own, img, txt, vec, up, up_bias, down,
                  act, dup, ddown, d_send, d_keep, x_send, x_keep, bias_grad, cot, ins, rows):
    ip, slab, quarter = dims.ip, dims.slab, dims.quarter
    i = pl.program_id(0)
    model = own.shape[-1]

    @pl.when(i == 0)
    def _():
        rows[...] = jnp.zeros_like(rows)
        bias_grad[...] = jnp.zeros_like(bias_grad)
        cot[...] = jnp.zeros_like(cot)
        ins[...] = peer[...]

    @pl.when(i == 1)
    def _():
        ins[...] = own[...]

    at = lax.broadcasted_iota(jnp.int32, (slab, 1), 0)
    inner = (at != 0) & (at != ip)

    def one(p, c):
        load_rows(dims, p, img, txt, rows)
        cot[0, pl.ds(8 * i + p, 1), :] = rows[0:1, :]
        cot[1, pl.ds(8 * i + p, 1), :] = rows[ip:ip + 1, :]
        ddown[p] = jnp.where(inner, rows[...] * vector(vec, F_SCALE), 0.0).astype(BF16)
        return c

    lax.fori_loop(0, quarter, one, 0)
    for m, lo, hi in ((0, 0, ip), (1, ip, slab)):
        count = quarter * (hi - lo)
        e = ins[:, lo:hi, :].reshape(count, model)
        u = dot(e, up[m]) + up_bias[m:m + 1]
        big, small = gelu_parts(u)
        a = (u * big).astype(BF16)
        act[:, lo:hi, :] = a.reshape(quarter, hi - lo, -1)
        slope = big + u * small
        d = dot(a, down[m]).astype(BF16).reshape(quarter, hi - lo, model)
        g = ddown[:, lo:hi, :].reshape(count, model)
        du = dot_t(g, down[m]) * slope
        bias_grad[m:m + 1, :] += jnp.sum(du, axis=0, keepdims=True)
        low = du.astype(BF16)
        dup[:, lo:hi, :] = low.reshape(quarter, hi - lo, -1)
        x = dot_t(low, up[m]).astype(BF16).reshape(quarter, hi - lo, model)

        @pl.when(i == 0)
        def _():
            d_send[:, lo:hi, :] = d
            x_send[:, lo:hi, :] = x

        @pl.when(i == 1)
        def _():
            d_keep[:, lo:hi, :] = d
            x_keep[:, lo:hi, :] = x


def experts(dims, name, half, seq, peer, own, img, txt, vec, up, up_bias, down):
    model = own.shape[-1]
    hidden = up.shape[-1]
    slab, quarter = dims.slab, dims.quarter
    fixed = pl.BlockSpec((quarter, slab, model), lambda i, o: (half, 0, 0))
    first = pl.BlockSpec((quarter, slab, model), lambda i, o: (0, 0, 0))
    step = lambda cols: pl.BlockSpec((quarter, slab, cols), lambda i, o: (i, 0, 0))
    shape = lambda n, cols: jax.ShapeDtypeStruct((n * quarter, slab, cols), BF16)
    return pl.pallas_call(
        functools.partial(expert_kernel, dims),
        grid_spec=pltpu.PrefetchScalarGridSpec(
            num_scalar_prefetch=1,
            grid=(2,),
            in_specs=[
                fixed, fixed,
                pl.BlockSpec((quarter, dims.patches, model), lambda i, o: (o[i], 0, 0)),
                pl.BlockSpec((quarter, dims.caption, model), lambda i, o: (o[i], 0, 0)),
                spec_whole(vec), spec_whole(up), spec_whole(up_bias), spec_whole(down),
            ],
            out_specs=[
                step(hidden), step(hidden), step(model),
                first, first, first, first,
                pl.BlockSpec((2, hidden), lambda i, o: (0, 0)),
                pl.BlockSpec((2, 16, model), lambda i, o: (0, 0, 0)),
            ],
            scratch_shapes=[pltpu.VMEM((quarter, slab, model), BF16), pltpu.VMEM((slab, model), F32)],
        ),
        out_shape=[
            shape(2, hidden), shape(2, hidden), shape(2, model),
            shape(1, model), shape(1, model), shape(1, model), shape(1, model),
            jax.ShapeDtypeStruct((2, hidden), F32),
            jax.ShapeDtypeStruct((2, 16, model), F32),
        ],
        compiler_params=params(),
        cost_estimate=pl.CostEstimate(
            flops=16 * quarter * slab * model * hidden, bytes_accessed=20_000_000, transcendentals=0),
        name=name,
    )(seq, peer, own, img, txt, vec, up, up_bias, down)


def expert_grads_kernel(dims, peer, own, act_a, dup_a, ddn_a, act_b, dup_b, ddn_b, ce, ca, cu, cd, out, acc):
    i = pl.program_id(0)

    def add(e, dup, ddn, act):
        for m, lo, hi in ((0, 0, dims.ip), (1, dims.ip, dims.slab)):
            count = dims.quarter * (hi - lo)
            flat = lambda ref: ref[:, lo:hi, :].reshape(count, -1)
            acc[m] += t_dot(flat(e), flat(dup))
            acc[2 + m] += t_dot(flat(ddn), flat(act))

    @pl.when(i == 0)
    def _():
        for m in range(2):
            acc[m] = t_dot(ce[m], cu[m])
            acc[2 + m] = t_dot(cd[m], ca[m])

    for j, refs in enumerate((
        (peer, dup_a, ddn_a, act_a), (own, dup_a, ddn_a, act_a),
        (peer, dup_b, ddn_b, act_b), (own, dup_b, ddn_b, act_b),
    )):
        @pl.when(i == j)
        def _():
            add(*refs)

    @pl.when(i == 3)
    def _():
        out[...] = acc[...].astype(BF16)


def expert_grads(dims, peer, own, act_a, dup_a, ddn_a, act_b, dup_b, ddn_b, ce, ca, cu, cd):
    model = own.shape[-1]
    hidden = act_a.shape[-1]
    slab, quarter = dims.slab, dims.quarter
    assert hidden == model
    half = pl.BlockSpec((quarter, slab, model), lambda i: (jnp.where(i < 2, 1, 0), 0, 0))
    first = pl.BlockSpec((quarter, slab, hidden), lambda i: (jnp.minimum(i, 1), 0, 0))
    last = pl.BlockSpec((quarter, slab, hidden), lambda i: (jnp.maximum(i - 2, 0), 0, 0))
    return pl.pallas_call(
        functools.partial(expert_grads_kernel, dims),
        grid=(4,),
        in_specs=[half, half, first, first, first, last, last, last] + [spec_whole(v) for v in (ce, ca, cu, cd)],
        out_specs=pl.BlockSpec((4, model, hidden), lambda i: (0, 0, 0)),
        scratch_shapes=[pltpu.VMEM((4, model, hidden), F32)],
        out_shape=jax.ShapeDtypeStruct((4, model, hidden), BF16),
        compiler_params=params(),
        cost_estimate=pl.CostEstimate(
            flops=16 * quarter * slab * model * hidden, bytes_accessed=40_000_000, transcendentals=0),
        name="expert_grads",
    )(peer, own, act_a, dup_a, ddn_a, act_b, dup_b, ddn_b, ce, ca, cu, cd)


def own_row(dims, r, p):
    return 8 * (r // 2) + dims.quarter * (r % 2) + p


def class_forward_kernel(dims, near, far, up, up_bias, down, out, rows):
    for m in range(2):
        e = jnp.concatenate([near[2 + m], far[2 + m]], axis=0).astype(BF16)
        rows[m] = e
        u = dot(e, up[m]) + up_bias[m:m + 1]
        out[m] = dot(gelu_low(u), down[m])


def class_forward(dims, near, far, up, up_bias, down):
    shape = (2, 16, near.shape[-1])
    return pl.pallas_call(
        functools.partial(class_forward_kernel, dims),
        out_shape=[jax.ShapeDtypeStruct(shape, F32), jax.ShapeDtypeStruct(shape, BF16)],
        compiler_params=params(),
        cost_estimate=pl.CostEstimate(flops=200_000_000, bytes_accessed=5_000_000, transcendentals=0),
        name="class_forward",
    )(near, far, up, up_bias, down)


def class_final_kernel(dims, order, near, far, d0, d1, d2, d3, vec, out):
    q = dims.quarter
    for m in range(2):
        out[m] = jnp.zeros(out.shape[1:], F32)
        for r in range(4):
            half, at = (near, far)[r // 2], q * (r % 2)
            for p in range(q):
                rows = [d[m, own_row(dims, s, p):own_row(dims, s, p) + 1, :]
                        for d, s in ((d0, r), (d1, r ^ 2), (d2, r ^ 1), (d3, r ^ 3))]
                total = (rows[0] + rows[1]) + (rows[2] + rows[3])
                x = half[m, at + p:at + p + 1, :] + vector(vec, F_SCALE) * (total + vector(vec, F_BIAS + m))
                out[m, pl.ds(4 * order[r] + p, 1), :] = x


def class_final(dims, order, near, far, parts, vec):
    shape = (2, 16, near.shape[-1])
    args = (near, far) + tuple(parts) + (vec,)
    return pl.pallas_call(
        functools.partial(class_final_kernel, dims),
        grid_spec=pltpu.PrefetchScalarGridSpec(
            num_scalar_prefetch=1, grid=(1,),
            in_specs=[spec_whole(v) for v in args],
            out_specs=pl.BlockSpec(shape, lambda i, o: (0, 0, 0)),
        ),
        out_shape=jax.ShapeDtypeStruct(shape, F32),
        compiler_params=params(),
        cost_estimate=pl.CostEstimate(flops=1_000_000, bytes_accessed=1_000_000, transcendentals=0),
        name="class_final",
    )(order, *args)


def class_back_kernel(dims, order, e, cot_a, cot_b, dclass, vec, up, up_bias, down,
                      act, dup, ddown, dexp, bias_grad, dcls, rows):
    q = dims.quarter
    rows[...] = jnp.zeros_like(rows)
    dcls[...] = jnp.zeros_like(dcls)
    for m in range(2):
        for r in range(4):
            cot, base = (cot_b, cot_a)[r % 2], 8 * (1 - r // 2)
            for p in range(q):
                d = dclass[m, pl.ds(4 * order[r] + p, 1), :]
                at = own_row(dims, r, p)
                rows[m, at:at + 1, :] = cot[m, base + p:base + p + 1, :] + d
                if r == 0:
                    dcls[p, m:m + 1, :] = d
        u = dot(e[m], up[m]) + up_bias[m:m + 1]
        big, small = gelu_parts(u)
        act[m] = (u * big).astype(BF16)
        g = (rows[m] * vector(vec, F_SCALE)).astype(BF16)
        ddown[m] = g
        du = dot_t(g, down[m]) * (big + u * small)
        bias_grad[m:m + 1, :] = jnp.sum(du, axis=0, keepdims=True)
        low = du.astype(BF16)
        dup[m] = low
        dexp[m] = dot_t(low, up[m])


def class_back(dims, order, e, cot_a, cot_b, dclass, vec, up, up_bias, down):
    hidden, model = up.shape[-1], e.shape[-1]
    args = (e, cot_a, cot_b, dclass, vec, up, up_bias, down)
    shapes = [((2, 16, hidden), BF16), ((2, 16, hidden), BF16), ((2, 16, model), BF16), ((2, 16, model), F32),
              ((2, hidden), F32), ((dims.quarter, 8, model), F32)]
    return pl.pallas_call(
        functools.partial(class_back_kernel, dims),
        grid_spec=pltpu.PrefetchScalarGridSpec(
            num_scalar_prefetch=1, grid=(1,),
            in_specs=[spec_whole(v) for v in args],
            out_specs=[pl.BlockSpec(s, lambda i, o, n=len(s): (0,) * n) for s, _ in shapes],
            scratch_shapes=[pltpu.VMEM((2, 16, model), F32)],
        ),
        out_shape=[jax.ShapeDtypeStruct(s, t) for s, t in shapes],
        compiler_params=params(),
        cost_estimate=pl.CostEstimate(flops=300_000_000, bytes_accessed=5_000_000, transcendentals=0),
        name="class_back",
    )(order, *args)


def contrast_kernel(dims, total, at, blocks, vec, weight, scale,
                    head_in, dproj, dcls, gains, shifts, scalars, cls, back):
    me = at[0]
    span = blocks[0].shape[0]
    for k, block in enumerate(blocks):
        for j in range(span):
            for m in range(2):
                cls[m, pl.ds(pl.multiple_of(16 * (me ^ (k * span + j)), 16), 16), :] = block[j, m]
    n_rows = cls.shape[1]
    sharp = jnp.exp(scale[...])
    col_at = lax.broadcasted_iota(jnp.int32, (1, n_rows), 1)
    row_at = lax.broadcasted_iota(jnp.int32, (n_rows, 1), 0)
    col_ok = (col_at % 4) < dims.quarter
    row_ok = (row_at % 4) < dims.quarter
    normal, inverse, proj, unit, embed = [], [], [], [], []
    for m in range(2):
        n, r = normalise(cls[m])
        h = (n * vector(vec, H_GAIN + m) + vector(vec, H_SHIFT + m)).astype(BF16)
        head_in[m] = h
        y = dot(h, weight[m])
        u = lax.rsqrt(jnp.sum(y * y, axis=-1, keepdims=True) + 1e-6)
        normal.append(n)
        inverse.append(r)
        proj.append(y)
        unit.append(u)
        embed.append((y * u).astype(BF16))
    ok = row_ok & col_ok
    logits = sharp * dot_t(embed[0], embed[1])
    masked = jnp.where(ok, logits, -1e30)
    row_max = jnp.max(masked, axis=1, keepdims=True)
    row_lse = row_max + jnp.log(jnp.sum(jnp.exp(masked - row_max), axis=1, keepdims=True))
    col_max = jnp.max(masked, axis=0, keepdims=True)
    col_lse = col_max + jnp.log(jnp.sum(jnp.exp(masked - col_max), axis=0, keepdims=True))
    same = (row_at == col_at) & ok
    both = jnp.exp(masked - row_lse) + jnp.exp(masked - col_lse)
    dlogits = jnp.where(ok, jnp.where(same, both - 2.0, both) * (1.0 / (2 * total)), 0.0)
    diagonal = jnp.sum(jnp.where(same, logits, 0.0), axis=1, keepdims=True)
    rows = jnp.where(row_ok, row_lse - 2.0 * diagonal, 0.0)
    cols = jnp.where(col_ok, col_lse, 0.0)
    loss = (jnp.sum(rows, axis=0, keepdims=True) + jnp.sum(cols, axis=1, keepdims=True)) * (1.0 / (2 * total))
    slope = jnp.sum(jnp.sum(dlogits * logits, axis=1, keepdims=True), axis=0, keepdims=True)
    scalars[0:1, :] = jnp.broadcast_to(loss, (1, 128))
    scalars[1:2, :] = jnp.broadcast_to(slope, (1, 128))
    high = lax.Precision.HIGHEST
    wide = [e.astype(F32) for e in embed]
    dembed = [
        sharp * jnp.dot(dlogits, wide[1], precision=high, preferred_element_type=F32),
        sharp * lax.dot_general(dlogits, wide[0], (((0,), (0,)), ((), ())), precision=high,
                                preferred_element_type=F32),
    ]
    for m in range(2):
        u, y, d = unit[m], proj[m], dembed[m]
        dp = (u * d - u * u * u * y * jnp.sum(y * d, axis=-1, keepdims=True)).astype(BF16)
        dproj[m] = dp
        dh = dot_t(dp, weight[m])
        gains[m:m + 1, :] = jnp.sum(dh * normal[m], axis=0, keepdims=True)
        shifts[m:m + 1, :] = jnp.sum(dh, axis=0, keepdims=True)
        back[m] = norm_back(normal[m], inverse[m], dh * vector(vec, H_GAIN + m))
        dcls[m] = back[m, pl.ds(pl.multiple_of(16 * me, 16), 16), :]


def contrast(dims, total, at, blocks, vec, weight, scale):
    model = weight.shape[1]
    rows = 16 * len(blocks) * blocks[0].shape[0]
    args = tuple(blocks) + (vec, weight, scale)
    shapes = [((2, rows, model), BF16), ((2, rows, weight.shape[2]), BF16), ((2, 16, model), F32),
              ((2, model), F32), ((2, model), F32), ((2, 128), F32)]

    def kernel(at, *refs):
        contrast_kernel(dims, total, at, refs[:len(blocks)], *refs[len(blocks):])

    return pl.pallas_call(
        kernel,
        grid_spec=pltpu.PrefetchScalarGridSpec(
            num_scalar_prefetch=1, grid=(1,),
            in_specs=[spec_whole(v) for v in args],
            out_specs=[pl.BlockSpec(s, lambda i, o, n=len(s): (0,) * n) for s, _ in shapes],
            scratch_shapes=[pltpu.VMEM((2, rows, model), F32)] * 2,
        ),
        out_shape=[jax.ShapeDtypeStruct(s, t) for s, t in shapes],
        compiler_params=params(),
        cost_estimate=pl.CostEstimate(flops=1_000_000_000, bytes_accessed=5_000_000, transcendentals=0),
        name="contrast",
    )(at, *args)


def contrast_large(dims, total, at, blocks, vec, weight, scale):
    model = weight.shape[1]
    held = jnp.concatenate(blocks)
    held = held[jnp.arange(held.shape[0]) ^ at[0]]
    rows = jnp.asarray([r for r in range(16) if r % 4 < dims.quarter])
    cls = jnp.transpose(held[:, :, rows], (1, 0, 2, 3)).reshape(2, -1, model)
    gain, shift = vec[H_GAIN:H_GAIN + 2, None], vec[H_SHIFT:H_SHIFT + 2, None]
    n, r = normalise(cls)
    head_in = (n * gain + shift).astype(BF16)
    proj = jnp.einsum("mrc,mce->mre", head_in, weight, preferred_element_type=F32)
    unit = lax.rsqrt(jnp.sum(proj * proj, axis=-1, keepdims=True) + 1e-6)
    embed = (proj * unit).astype(BF16)
    sharp = jnp.exp(scale[0, 0])
    logits = sharp * dot_t(embed[0], embed[1])
    row_lse = jax.nn.logsumexp(logits, axis=1, keepdims=True)
    col_lse = jax.nn.logsumexp(logits, axis=0, keepdims=True)
    dlogits = jnp.exp(logits - row_lse) + jnp.exp(logits - col_lse) - 2.0 * jnp.eye(total, dtype=F32)
    dlogits = dlogits / (2 * total)
    loss = (jnp.sum(row_lse) + jnp.sum(col_lse) - 2.0 * jnp.trace(logits)) / (2 * total)
    slope = jnp.sum(dlogits * logits)
    high = lax.Precision.HIGHEST
    wide = embed.astype(F32)
    dembed = sharp * jnp.stack([
        jnp.dot(dlogits, wide[1], precision=high, preferred_element_type=F32),
        jnp.dot(dlogits.T, wide[0], precision=high, preferred_element_type=F32)])
    dproj = (unit * dembed - unit ** 3 * proj * jnp.sum(proj * dembed, axis=-1, keepdims=True)).astype(BF16)
    dh = jnp.einsum("mre,mce->mrc", dproj, weight, preferred_element_type=F32)
    back = norm_back(n, r, dh * gain)
    pairs = 4 * dims.quarter
    own = lax.dynamic_slice_in_dim(back, at[0] * pairs, pairs, axis=1)
    dcls = jnp.zeros((2, 16, model), F32).at[:, rows].set(own)
    scalars = jnp.broadcast_to(jnp.stack([loss, slope])[:, None], (2, 128))
    return head_in, dproj, dcls, jnp.sum(dh * n, axis=1), jnp.sum(dh, axis=1), scalars


def own_pair(rows_of):
    return lambda i, o: (o[0] * rows_of + i, 0, 0)


def own_call(kernel, dims, name, order, blocks, img, txt, others, outs, scratch):
    model = img.shape[-1]
    block = pl.BlockSpec((1, dims.slab, model), lambda i, o: (i, 0, 0))
    specs = {
        "slab": (block, (dims.quarter, dims.slab, model)),
        "img": (pl.BlockSpec((1, dims.patches, model), lambda i, o: (i, 0, 0)), (dims.quarter, dims.patches, model)),
        "txt": (pl.BlockSpec((1, dims.caption, model), lambda i, o: (i, 0, 0)), (dims.quarter, dims.caption, model)),
        "sums": (pl.BlockSpec((8, model), lambda i, o: (0, 0)), (8, model)),
    }
    return pl.pallas_call(
        functools.partial(kernel, dims),
        grid_spec=pltpu.PrefetchScalarGridSpec(
            num_scalar_prefetch=1,
            grid=(dims.quarter,),
            in_specs=[block] * len(blocks) + [
                pl.BlockSpec((1, dims.patches, model), own_pair(dims.quarter)),
                pl.BlockSpec((1, dims.caption, model), own_pair(dims.quarter)),
            ] + [spec_whole(v) for v in others],
            out_specs=[specs[kind][0] for kind, _ in outs],
            scratch_shapes=[pltpu.VMEM((dims.slab, model), F32)] * scratch,
        ),
        out_shape=[jax.ShapeDtypeStruct(specs[kind][1], dtype) for kind, dtype in outs],
        compiler_params=params(),
        cost_estimate=pl.CostEstimate(flops=40_000_000, bytes_accessed=15_000_000, transcendentals=0),
        name=name,
    )(order, *blocks, img, txt, *others)


def start_own(rows, sums):
    @pl.when(pl.program_id(0) == 0)
    def _():
        rows[...] = jnp.zeros_like(rows)
        sums[...] = jnp.zeros_like(sums)


def add_class(dims, dcls, rows):
    i = pl.program_id(0)
    rows[0:1, :] += dcls[i, 0:1, :]
    rows[dims.ip:dims.ip + 1, :] += dcls[i, 1:2, :]


def final_kernel(dims, order, keep, recv, far, attended, img, txt, dcls, vec, fin_img, fin_txt, sums, rows):
    start_own(rows, sums)
    load_rows(dims, 0, img, txt, rows)
    add_class(dims, dcls, rows)
    for m, lo, hi in ((0, 0, dims.ip), (1, dims.ip, dims.slab)):
        b = keep[0, lo:hi].astype(F32) + recv[0, lo:hi].astype(F32) + far[0, lo:hi].astype(F32)
        b = b + vector(vec, F_BIAS + m)
        f = attended[0, lo:hi, :] + vector(vec, F_SCALE) * b
        if m == 0:
            fin_img[0] = f[0:dims.patches].astype(BF16)
        else:
            fin_txt[0] = f[0:dims.caption].astype(BF16)
        g = rows[lo:hi, :]
        sums[0:1, :] += jnp.sum(g * b, axis=0, keepdims=True)
        sums[1 + m:2 + m, :] += jnp.sum(g, axis=0, keepdims=True) * vector(vec, F_SCALE)


def final_rows(dims, order, keep, recv, far, attended, img, txt, dcls, vec):
    return own_call(final_kernel, dims, "final_rows", order, (keep, recv, far, attended), img, txt,
                    (dcls, vec), (("img", BF16), ("txt", BF16), ("sums", F32)), 1)


def norm_two_kernel(dims, order, keep, recv, far, attended, a_keep, a_recv, img, txt, dcls, x0, x1, x2, x3,
                    vec, dattended, dattn, sums, rows, ups):
    i = pl.program_id(0)
    start_own(rows, sums)
    load_rows(dims, 0, img, txt, rows)
    add_class(dims, dcls, rows)
    ups[...] = keep[0].astype(F32) + recv[0].astype(F32) + far[0].astype(F32)
    for m, at in ((0, 0), (1, dims.ip)):
        extra = [x[m, pl.ds(own_row(dims, r, 0) + i, 1), :] for x, r in ((x0, 0), (x1, 2), (x2, 1), (x3, 3))]
        ups[at:at + 1, :] += (extra[0] + extra[1]) + (extra[2] + extra[3])
    for m, lo, hi in ((0, 0, dims.ip), (1, dims.ip, dims.slab)):
        n, r = normalise(attended[0, lo:hi, :])
        dy = ups[lo:hi, :]
        sums[m:m + 1, :] += jnp.sum(dy * n, axis=0, keepdims=True)
        sums[2 + m:3 + m, :] += jnp.sum(dy, axis=0, keepdims=True)
        d = rows[lo:hi, :] + norm_back(n, r, dy * vector(vec, GAIN2 + m))
        dattended[0, lo:hi, :] = d
        sd = d * vector(vec, A_SCALE)
        dattn[0, lo:hi, :] = sd.astype(BF16)
        a = a_keep[0, lo:hi, :].astype(F32) + a_recv[0, lo:hi, :].astype(F32) + vector(vec, A_BIAS)
        sums[4:5, :] += jnp.sum(d * a, axis=0, keepdims=True)
        sums[5:6, :] += jnp.sum(sd, axis=0, keepdims=True)


def norm_two(dims, order, keep, recv, far, attended, a_keep, a_recv, img, txt, dcls, parts, vec):
    return own_call(norm_two_kernel, dims, "norm_two", order, (keep, recv, far, attended, a_keep, a_recv), img, txt,
                    (dcls,) + tuple(parts) + (vec,), (("slab", F32), ("slab", BF16), ("sums", F32)), 2)


def norm_one_kernel(dims, order, keep, recv, dattended, img, txt, vec, d_img, d_txt, sums, rows):
    start_own(rows, sums)
    load_rows(dims, 0, img, txt, rows)
    n, r = normalise(rows[...])
    dy = keep[0].astype(F32) + recv[0].astype(F32)
    sums[0:1, :] += jnp.sum(dy * n, axis=0, keepdims=True)
    sums[1:2, :] += jnp.sum(dy, axis=0, keepdims=True)
    d = dattended[0] + norm_back(n, r, dy * vector(vec, GAIN1))
    d_img[0] = d[0:dims.patches].astype(BF16)
    d_txt[0] = d[dims.ip:dims.ip + dims.caption].astype(BF16)


def norm_one(dims, order, keep, recv, dattended, img, txt, vec):
    return own_call(norm_one_kernel, dims, "norm_one", order, (keep, recv, dattended), img, txt,
                    (vec,), (("img", BF16), ("txt", BF16), ("sums", F32)), 1)


def back_step(dims, tiles, lens, whose, dattn, normed, qkv, mixed, dmixed, dqkv, acc, col_sums, w, ow):
    quarter, slab = dims.quarter, dims.slab
    count, width = quarter * slab, tiles * 128
    model = normed.shape[-1]
    d_rows = dattn[...].reshape(count, model)
    dmixed[...] = dot_t(d_rows, ow[...]).astype(BF16).reshape(quarter, slab, width)

    def one_pair(p, c):
        length = lens[whose * quarter + p]
        for lo, hi, start, limit in key_tail(dims, length):
            for g in range(tiles):
                at = [slice((t * tiles + g) * 128, (t * tiles + g + 1) * 128) for t in range(3)]
                q, k, v = [qkv[p, lo:hi, c] for c in at]
                q = scaled(q)
                qq = split_pair(q)
                dd = split_pair(dmixed[p, lo:hi, g * 128:(g + 1) * 128])
                w_ = softmax_keys(hide(dot_t(k, qq), start, limit))
                dw = dot_t(v, dd)
                dqkv[p, lo:hi, at[2]] = dot(w_.astype(BF16), dd).astype(BF16)
                ds = (w_ * (dw - jnp.sum(w_ * dw, axis=0, keepdims=True))).astype(BF16)
                dqkv[p, lo:hi, at[1]] = dot(ds, qq).astype(BF16)
                dqkv[p, lo:hi, at[0]] = (join_pair(t_dot(ds, k)) * HEAD_DIM ** -0.5).astype(BF16)
        return c

    lax.fori_loop(0, quarter, one_pair, 0)
    dp = dqkv[...].reshape(count, 3 * width)
    part = dot(dp, w[...])
    acc[:, 0:3 * width] += t_dot(normed[...].reshape(count, model), dp)
    acc[:, 3 * width:] += t_dot(d_rows, mixed[...].reshape(count, width))
    col_sums[...] += jnp.sum(dp.astype(F32), axis=0, keepdims=True)
    return part


def attend_back_kernel(dims, far, order, lens, d_own, d_peer, normed, qkv, mixed, wq, wo, wf, *refs):
    if not far:
        prior_keep, prior_send, *refs = refs
    keep, send, grad, *refs = refs
    if far:
        grad_rest, *refs = refs
    col_sums, dattn, dmixed, dqkv, acc, w, ow = refs
    i = pl.program_id(0)
    slab, quarter, local = dims.slab, dims.quarter, dims.local
    two, one_head = parts_of(dims)
    tiles = 2 if far else 1
    width = tiles * two
    count = quarter * slab
    model = normed.shape[-1]

    @pl.when(i == 0)
    def _():
        dattn[...] = d_own[...]
        acc[...] = jnp.zeros_like(acc)
        col_sums[...] = jnp.zeros_like(col_sums)
        for t in range(4):
            dst, at = (w, t * width) if t < 3 else (ow, 0)
            own, start = (wq, t * local) if t < 3 else (wo, 0)
            if far:
                copy_rows(dst, at, wf, t * local, two)
                copy_rows(dst, at + two, own, start + two, one_head)
                copy_rows(dst, at + two + one_head, wf, t * local + two, one_head)
            else:
                copy_rows(dst, at, own, start, two)

    @pl.when(i == 1)
    def _():
        dattn[...] = d_peer[...]

    part = back_step(dims, tiles, lens, order[2 * i], dattn, normed, qkv, mixed,
                     dmixed, dqkv, acc, col_sums, w, ow)

    @pl.when(i == 0)
    def _():
        prior = 0.0 if far else prior_keep[...].reshape(count, model).astype(F32)
        keep[...] = (part + prior).astype(BF16).reshape(quarter, slab, model)

    @pl.when(i == 1)
    def _():
        prior = 0.0 if far else prior_send[...].reshape(count, model).astype(F32)
        send[...] = (part + prior).astype(BF16).reshape(quarter, slab, model)
        for t in range(4):
            grad[:, t * two:(t + 1) * two] = acc[:, t * width:t * width + two].astype(BF16)
            if far:
                at = t * width + two
                to = 4 * two + t * one_head
                grad[:, to:to + one_head] = acc[:, at + one_head:at + two].astype(BF16)
                grad_rest[:, t * one_head:(t + 1) * one_head] = acc[:, at:at + one_head].astype(BF16)


def attend_back(dims, far, order, lens, d_own, d_peer, normed, qkv, mixed, wq, wo, wf, prior=()):
    model = normed.shape[-1]
    slab, quarter = dims.slab, dims.quarter
    width = 256 if far else 128
    one = pl.BlockSpec((quarter, slab, model), lambda i, o, n: (0, 0, 0))
    stride = normed.shape[0] // (2 * quarter)
    step = lambda cols: pl.BlockSpec((quarter, slab, cols), lambda i, o, n: (stride * i, 0, 0))
    grads = (768, 256) if far else (512,)
    specs = [one, one] + [pl.BlockSpec((model, n), lambda i, o, n_: (0, 0)) for n in grads]
    specs += [pl.BlockSpec((1, 3 * width), lambda i, o, n: (0, 0))]
    shapes = [
        jax.ShapeDtypeStruct((quarter, slab, model), BF16),
        jax.ShapeDtypeStruct((quarter, slab, model), BF16),
    ] + [jax.ShapeDtypeStruct((model, n), BF16) for n in grads] + [jax.ShapeDtypeStruct((1, 3 * width), F32)]
    scratch = [
        pltpu.VMEM((quarter, slab, model), BF16),
        pltpu.VMEM((quarter, slab, width), BF16),
        pltpu.VMEM((quarter, slab, 3 * width), BF16),
        pltpu.VMEM((model, 4 * width), F32),
        pltpu.VMEM((3 * width, model), BF16),
        pltpu.VMEM((width, model), BF16),
    ]
    return pl.pallas_call(
        functools.partial(attend_back_kernel, dims, far),
        grid_spec=pltpu.PrefetchScalarGridSpec(
            num_scalar_prefetch=2,
            grid=(2,),
            in_specs=[one, one, step(model), step(3 * width), step(width), spec_whole(wq), spec_whole(wo),
                      spec_whole(wf)] + [one] * len(prior),
            out_specs=specs,
            scratch_shapes=scratch,
        ),
        out_shape=shapes,
        compiler_params=params(),
        cost_estimate=pl.CostEstimate(
            flops=32 * quarter * slab * model * width, bytes_accessed=20_000_000, transcendentals=0),
        name="attend_back_far" if far else "attend_back_own",
    )(order, lens, d_own, d_peer, normed, qkv, mixed, wq, wo, wf, *prior)


def swap(value, axis, bit):
    size = lax.axis_size(axis)
    return lax.ppermute(value, axis, [(j, j ^ bit) for j in range(size)])


def to_core(value):
    return swap(value, "mp", 1)


def to_y(value):
    return swap(value, "mp", 2)


def from_others(value, axis, first, count):
    return [value] + [swap(value, axis, k * first) for k in range(1, count)]


def add_tree(parts):
    while len(parts) > 1:
        parts = [a + b for a, b in zip(parts[::2], parts[1::2])]
    return parts[0]


def sum_over(value, axis):
    first = 1
    while first < lax.axis_size(axis):
        count = min(8, lax.axis_size(axis) // first)
        value = add_tree(from_others(value, axis, first, count))
        first *= count
    return value


def gather_batch(value):
    parts = [value]
    first = 1
    size = lax.axis_size("batch")
    while first < size:
        count = min(8, size // first)
        whole = jnp.concatenate(parts) if len(parts) > 1 else parts[0]
        parts = from_others(whole, "batch", first, count)
        first *= count
    return parts


def gather_rows(own, me):
    near = jnp.stack([own, to_y(own)])
    far = to_core(near)
    out = jnp.zeros((4,) + own.shape, own.dtype)
    for r, value in enumerate((near[0], near[1], far[0], far[1])):
        out = lax.dynamic_update_slice(out, value[None], (me ^ ORDER[r],) + (0,) * own.ndim)
    return out.reshape((4 * own.shape[0],) + own.shape[1:])


def add_low(a, b):
    return (a.astype(F32) + b.astype(F32)).astype(BF16)


MESH = pl.DeviceIdType.MESH


class Place:
    def __init__(self):
        self.b, self.m = lax.axis_index("batch"), lax.axis_index("mp")
        self.z, self.x = self.b // 2, self.b % 2
        self.y, self.c = self.m // 2, self.m % 2
        self.core = (self.b, 2 * self.y + 1 - self.c)
        self.near = (self.b, 2 * (1 - self.y) + self.c)
        self.across = (self.b, 2 * (1 - self.y) + 1 - self.c)
        self.side = (2 * self.z + 1 - self.x, self.m)
        self.z_pair = self.z + 1 - 2 * (self.z % 2)
        self.z_far = (self.z + 2) % 4
        self.z_rest = (self.z_pair + 2) % 4
        self.paired = (2 * self.z_pair + self.x, self.m)
        self.opposite = (2 * self.z_far + self.x, self.m)
        self.batch = [((self.b + k) % 8, self.m) for k in range(1, 8)]

    def quarter(self, far_y, far_core):
        return 2 * ((self.y + far_y) % 2) + (self.c + far_core) % 2


def meet(peers):
    barrier = pltpu.get_barrier_semaphore()
    for peer in peers:
        pl.semaphore_signal(barrier, inc=1, device_id=peer, device_id_type=MESH)
    pl.semaphore_wait(barrier, len(peers))


def remote(src, dst, send_sem, recv_sem, at, device):
    return pltpu.make_async_remote_copy(
        src_ref=src, dst_ref=dst, send_sem=send_sem.at[at], recv_sem=recv_sem.at[at],
        device_id=device, device_id_type=MESH)


def front_kernel(dims, lens, img, txt, vectors, bias, own_w, own_o,
                 vec, normed, qkv, mixed, qkv_far, mixed_far, far_w, attended, attn, expert, expert_peer, cls, cls_peer,
                 rows, w, w2, ow, b, wf, far_bias, n_all, rest, m_all, m_far, q_own, q_far, a_send, a_recv, e_send, c_recv, held,
                 local_sem, send_sem, recv_sem):
    here = Place()
    i = pl.program_id(0)
    local, quarter, slab, ip = dims.local, dims.quarter, dims.slab, dims.ip
    two, one_head = parts_of(dims)
    count = quarter * slab
    model = img.shape[-1]
    at = i % 4
    whose = here.quarter(at % 2, 1 - at // 2)
    sent_w = [remote(own_w, wf.at[pl.ds(0, 3 * local)], send_sem, recv_sem, 0, here.near),
              remote(own_o, wf.at[pl.ds(3 * local, local)], send_sem, recv_sem, 1, here.near),
              remote(bias, far_bias, send_sem, recv_sem, 2, here.near)]
    sent_a = [remote(a_send.at[j], a_recv.at[j], send_sem, recv_sem, 3 + j, here.core) for j in range(2)]

    def e_over(j):
        return remote(e_send.at[j], expert_peer.at[j], send_sem, recv_sem, 5 + j, here.core)

    def e_here(j):
        return pltpu.make_async_copy(e_send.at[j], expert.at[j], local_sem.at[1 + j])

    sent_c = remote(cls, c_recv, send_sem, recv_sem, 5 + 2 * quarter, here.core)
    keep_w = pltpu.make_async_copy(wf, far_w, local_sem.at[0])
    sent_e = [e_over(j) for j in range(2 * quarter)]
    keep_e = [e_here(j) for j in range(2 * quarter)]

    @pl.when(i == 0)
    def _():
        meet([here.core, here.near])
        for copy in sent_w:
            copy.start()
        fill(vec, vectors)
        rows[...] = jnp.zeros_like(rows)
        b[...] = jnp.zeros_like(b)
        w[...] = jnp.zeros_like(w)
        cls[...] = jnp.zeros_like(cls)
        for t in range(3):
            copy_rows(w, t * 2 * two, own_w, t * local, local)
        b[0:1, 0:local] = bias[0:1, :]
        b[0:1, 4 * two:4 * two + local] = bias[1:2, :]

    def project(weights):
        proj = dot_t(n_all[at].reshape(count, model), weights[...]) + b[0:1, :]
        return proj.astype(BF16).reshape(quarter, slab, 6 * two)

    @pl.when(i < 4)
    def _():
        def one_norm(p, c):
            load_rows(dims, p, img, txt, rows)
            n, _ = normalise(rows[...])
            n_all[at, p] = (n * vector(vec, GAIN1) + vector(vec, SHIFT1)).astype(BF16)
            return c

        lax.fori_loop(0, quarter, one_norm, 0)
        proj = project(w)
        for t in range(3):
            q_own[:, :, t * two:(t + 1) * two] = proj[:, :, 2 * t * two:(2 * t + 1) * two]
            rest[at, :, :, t * two:(t + 1) * two] = proj[:, :, (2 * t + 1) * two:(2 * t + 2) * two]
        attend_tiles(dims, lens, whose, q_own, m_all.at[at])

        @pl.when(i % 2 == 0)
        def _():
            normed[...] = n_all[at]
            qkv[...] = q_own[...]
            mixed[...] = m_all[at]

    @pl.when(i == 4)
    def _():
        for copy in sent_w:
            copy.wait_recv()
        keep_w.start()
        w2[...] = jnp.zeros_like(w2)
        b[...] = jnp.zeros_like(b)
        for t in range(3):
            copy_rows(w2, t * 2 * two, wf, t * local, two)
            copy_rows(w2, t * 2 * two + two + one_head, wf, t * local + two, one_head)
        for t, to in ((0, 0), (1, 4 * two)):
            b[0:1, to:to + two] = far_bias[t:t + 1, 0:two]
            b[0:1, to + two + one_head:to + 2 * two] = far_bias[t:t + 1, two:]
        copy_rows(ow, 0, own_o, 0, two)
        copy_rows(ow, two, wf, 3 * local, two)
        copy_rows(ow, 2 * two, own_o, two, one_head)
        copy_rows(ow, 2 * two + one_head, wf, 3 * local + two, one_head)

    @pl.when(i >= 4)
    def _():
        proj = project(w2)
        for t in range(3):
            to = 2 * t * two
            q_far[:, :, to:to + two] = proj[:, :, to:to + two]
            q_far[:, :, to + two:to + 2 * two] = (
                proj[:, :, to + two:to + 2 * two] + rest[at, :, :, t * two:(t + 1) * two])
        attend_tiles(dims, lens, whose, q_far, m_far)

        @pl.when(i % 2 == 0)
        def _():
            qkv_far[...] = q_far[...]
            mixed_far[...] = m_far[...]

        part = dot(m_all[at].reshape(count, two), ow[0:two, :])
        part = part + dot(m_far[...].reshape(count, 2 * two), ow[two:, :])
        part = part.reshape(quarter, slab, model)

        @pl.when(i < 6)
        def _():
            a_send[at] = part.astype(BF16)

        for j in range(2):
            @pl.when(i == 4 + j)
            def _():
                sent_a[j].start()

        for j in range(2):
            @pl.when(i == 6 + j)
            def _():
                sent_a[j].wait_recv()

        @pl.when(i >= 6)
        def _():
            j = i - 6
            held[...] = part

            def one_residual(p, c):
                load_rows(dims, p, img, txt, rows)
                a = held[p] + a_recv[j, p].astype(F32)
                x = rows[...] + vector(vec, A_SCALE) * (a + vector(vec, A_BIAS))
                n, _ = normalise(x)
                e_img = n[0:ip] * vector(vec, GAIN2) + vector(vec, SHIFT2)
                e_txt = n[ip:] * vector(vec, GAIN2 + 1) + vector(vec, SHIFT2 + 1)
                r = j * quarter + p
                e_send[r, 0:ip, :] = e_img.astype(BF16)
                e_send[r, ip:, :] = e_txt.astype(BF16)
                e_over(r).start()
                e_here(r).start()
                for k, v in enumerate((x[0:1], x[ip:ip + 1], e_img[0:1], e_txt[0:1])):
                    cls[k, pl.ds(r, 1), :] = v

                @pl.when(j == 0)
                def _():
                    attended[p] = x
                    attn[p] = a

                return c

            lax.fori_loop(0, quarter, one_residual, 0)

    @pl.when(i == 7)
    def _():
        sent_c.start()
        keep_w.wait()
        for copy in keep_e:
            copy.wait()
        sent_c.wait()
        cls_peer[...] = c_recv[...]
        for copy in sent_e:
            copy.wait()
        for copy in sent_w + sent_a:
            copy.wait_send()


def fill(table, vectors):
    table[...] = jnp.zeros_like(table)
    at = 0
    for v in vectors:
        n = v.shape[0] if len(v.shape) == 2 else 1
        table[at:at + n, :] = v[...].reshape(n, table.shape[1])
        at += n


def front(dims, lens, img, txt, vectors, bias, own_w, own_o):
    model = img.shape[-1]
    quarter, slab, local = dims.quarter, dims.slab, dims.local
    held = pl.BlockSpec(memory_space=pltpu.VMEM)
    away = pl.BlockSpec(memory_space=pl.ANY)

    def states_at(i):
        return Place().quarter(i % 2, 1 - i % 4 // 2), 0, 0

    own_block = lambda cols: pl.BlockSpec((quarter, slab, cols), lambda i: (jnp.where(i < 2, 1, 0), 0, 0))
    far_block = lambda cols: pl.BlockSpec((quarter, slab, cols), lambda i: (jnp.where(i < 6, 1, 0), 0, 0))
    six = lambda cols: jax.ShapeDtypeStruct((2 * quarter, slab, cols), BF16)
    block = lambda cols: (quarter, slab, cols)
    n_remote = 6 + 2 * quarter
    return pl.pallas_call(
        lambda lens, img, txt, *refs: front_kernel(
            dims, lens, img, txt, refs[:len(vectors)], *refs[len(vectors):]),
        grid=(8,),
        in_specs=[pl.BlockSpec(memory_space=pltpu.SMEM),
                  pl.BlockSpec((quarter, dims.patches, model), states_at),
                  pl.BlockSpec((quarter, dims.caption, model), states_at)] + [held] * (3 + len(vectors)),
        out_specs=[held, own_block(model), own_block(384), own_block(128), far_block(768), far_block(256),
                   away, held, held, away, away, held, held],
        out_shape=[jax.ShapeDtypeStruct((16, model), F32), six(model), six(384), six(128), six(768), six(256),
                   jax.ShapeDtypeStruct((4 * local, model), BF16),
                   jax.ShapeDtypeStruct(block(model), F32), jax.ShapeDtypeStruct(block(model), F32),
                   six(model), six(model),
                   jax.ShapeDtypeStruct((4, 8, model), F32), jax.ShapeDtypeStruct((4, 8, model), F32)],
        scratch_shapes=[
            pltpu.VMEM((slab, model), F32), pltpu.VMEM((768, model), BF16), pltpu.VMEM((768, model), BF16),
            pltpu.VMEM((384, model), BF16), pltpu.VMEM((8, 768), F32), pltpu.VMEM((4 * local, model), BF16),
            pltpu.VMEM((2, local), F32),
            pltpu.VMEM((4,) + block(model), BF16), pltpu.VMEM((4,) + block(384), BF16),
            pltpu.VMEM((4,) + block(128), BF16), pltpu.VMEM(block(256), BF16),
            pltpu.VMEM(block(384), BF16), pltpu.VMEM(block(768), BF16),
            pltpu.VMEM((2,) + block(model), BF16), pltpu.VMEM((2,) + block(model), BF16),
            pltpu.VMEM((2 * quarter, slab, model), BF16), pltpu.VMEM((4, 8, model), F32),
            pltpu.VMEM(block(model), F32),
            pltpu.SemaphoreType.DMA((1 + 2 * quarter,)),
            pltpu.SemaphoreType.DMA((n_remote,)), pltpu.SemaphoreType.DMA((n_remote,)),
        ],
        compiler_params=params(collective_id=6, has_side_effects=True),
        cost_estimate=pl.CostEstimate(
            flops=16 * quarter * slab * model * 1152, bytes_accessed=40_000_000, transcendentals=0),
        name="front",
    )(lens, img, txt, *vectors, bias, own_w, own_o)


def middle_kernel(dims, total, img, txt, own, peer, cls_own, cls_peer, vec, up, up_bias, down, head_weight, scale,
                  dup, down_keep, down_send, dexp, d_own, d_near, bias_grad, class_e, c_act, c_dup, c_ddn, dcls,
                  head_in, dproj, gains, shifts, scalars,
                  bx, bd, rx, rd, x_near, x_far, ins, rows, part, parts, cls, back, cot, c_rows, extra, extras, hidden_in, weight, ddn, acc,
                  local_sem, send_sem, recv_sem):
    here = Place()
    ip, slab, quarter = dims.ip, dims.slab, dims.quarter
    i = pl.program_id(0)
    model = own.shape[-1]
    mp_peers = [here.core, here.near, here.across]
    fetch = pltpu.make_async_copy(head_weight, weight, local_sem.at[0])
    of = [here.quarter(0, 0), here.quarter(1, 0), here.quarter(0, 1), here.quarter(1, 1)]

    sent_x = [remote(bx.at[2 * j], rx.at[j], send_sem, recv_sem, j, here.core) for j in range(2)]
    sent_d = [remote(bd.at[2 * j], rd.at[j], send_sem, recv_sem, 2 + j, here.core) for j in range(2)]
    sent_near = remote(x_near, x_far, send_sem, recv_sem, 4, here.near)
    sent_part = [remote(part, parts.at[k], send_sem, recv_sem, 5 + k, mp_peers[k]) for k in range(3)]
    sent_extra = [remote(extra, extras.at[k], send_sem, recv_sem, 8 + k, mp_peers[k]) for k in range(3)]
    sent_cls = [remote(cls.at[here.b], cls.at[here.b], send_sem, recv_sem, 11 + k, here.batch[k]) for k in range(7)]

    @pl.when(i == 0)
    def _():
        fetch.start()
        acc[...] = jnp.zeros_like(acc)
        rows[...] = jnp.zeros_like(rows)
        bias_grad[...] = jnp.zeros_like(bias_grad)
        for m in range(2):
            e = jnp.concatenate([cls_own[2 + m], cls_peer[2 + m]], axis=0).astype(BF16)
            class_e[m] = e
            u = dot(e, up[m]) + up_bias[m:m + 1]
            hidden_in[m] = u
            part[m] = dot(gelu_low(u), down[m])
        meet(mp_peers + here.batch)
        for copy in sent_part:
            copy.start()
        ins[...] = peer[...]

    @pl.when(i == 1)
    def _():
        for copy in sent_part:
            copy.wait_recv()
        for m in range(2):
            cls[here.b, m] = jnp.zeros(cls.shape[2:], F32)
            for r in range(4):
                half, at = (cls_own, cls_peer)[r // 2], quarter * (r % 2)
                for p in range(quarter):
                    line = [d[m, own_row(dims, s, p):own_row(dims, s, p) + 1, :]
                            for d, s in ((part, r), (parts.at[0], r ^ 2), (parts.at[1], r ^ 1), (parts.at[2], r ^ 3))]
                    x = (line[0] + line[1]) + (line[2] + line[3]) + vector(vec, F_BIAS + m)
                    x = half[m, at + p:at + p + 1, :] + vector(vec, F_SCALE) * x
                    cls[here.b, m, pl.ds(4 * of[r] + p, 1), :] = x
        for copy in sent_cls:
            copy.start()
        ins[...] = own[...]

    @pl.when(i == 2)
    def _():
        ins[...] = peer[...]

    @pl.when(i == 3)
    def _():
        ins[...] = own[...]
        fetch.wait()
        for copy in sent_cls:
            copy.wait_recv()
        n_rows = 16 * cls.shape[0]
        sharp = jnp.exp(scale[...])
        col_at = lax.broadcasted_iota(jnp.int32, (1, n_rows), 1)
        row_at = lax.broadcasted_iota(jnp.int32, (n_rows, 1), 0)
        col_ok = (col_at % 4) < quarter
        row_ok = (row_at % 4) < quarter
        normal, inverse, proj, unit, embed = [], [], [], [], []
        for m in range(2):
            n, r = normalise(cls[:, m].reshape(n_rows, model))
            h = (n * vector(vec, H_GAIN + m) + vector(vec, H_SHIFT + m)).astype(BF16)
            head_in[m] = h
            y = dot(h, weight[m])
            u = lax.rsqrt(jnp.sum(y * y, axis=-1, keepdims=True) + 1e-6)
            normal.append(n)
            inverse.append(r)
            proj.append(y)
            unit.append(u)
            embed.append((y * u).astype(BF16))
        ok = row_ok & col_ok
        logits = sharp * dot_t(embed[0], embed[1])
        masked = jnp.where(ok, logits, -1e30)
        row_max = jnp.max(masked, axis=1, keepdims=True)
        row_lse = row_max + jnp.log(jnp.sum(jnp.exp(masked - row_max), axis=1, keepdims=True))
        col_max = jnp.max(masked, axis=0, keepdims=True)
        col_lse = col_max + jnp.log(jnp.sum(jnp.exp(masked - col_max), axis=0, keepdims=True))
        same = (row_at == col_at) & ok
        both = jnp.exp(masked - row_lse) + jnp.exp(masked - col_lse)
        dlogits = jnp.where(ok, jnp.where(same, both - 2.0, both) * (1.0 / (2 * total)), 0.0)
        diagonal = jnp.sum(jnp.where(same, logits, 0.0), axis=1, keepdims=True)
        lines = jnp.sum(jnp.where(row_ok, row_lse - 2.0 * diagonal, 0.0), axis=0, keepdims=True)
        lines = lines + jnp.sum(jnp.where(col_ok, col_lse, 0.0), axis=1, keepdims=True)
        slope = jnp.sum(jnp.sum(dlogits * logits, axis=1, keepdims=True), axis=0, keepdims=True)
        scalars[0:1, :] = jnp.broadcast_to(lines * (1.0 / (2 * total)), (1, 128))
        scalars[1:2, :] = jnp.broadcast_to(slope, (1, 128))
        pieces, left = [], dlogits
        for _ in range(3):
            pieces.append(left.astype(BF16))
            left = left - pieces[-1].astype(F32)
        dembed = [
            sharp * (dot(pieces[0], embed[1]) + (dot(pieces[1], embed[1]) + dot(pieces[2], embed[1]))),
            sharp * (t_dot(pieces[0], embed[0]) + (t_dot(pieces[1], embed[0]) + t_dot(pieces[2], embed[0]))),
        ]
        c_rows[...] = jnp.zeros_like(c_rows)
        dcls[...] = jnp.zeros_like(dcls)
        for m in range(2):
            for p in range(quarter):
                src = (img, txt)[m]
                cot[m, 8 * 3 + p:8 * 3 + p + 1, :] = src[p, 0:1, :].astype(F32)
        for m in range(2):
            u, y, d = unit[m], proj[m], dembed[m]
            dp = (u * d - u * u * u * y * jnp.sum(y * d, axis=-1, keepdims=True)).astype(BF16)
            dproj[m] = dp
            dh = dot_t(dp, weight[m])
            gains[m:m + 1, :] = jnp.sum(dh * normal[m], axis=0, keepdims=True)
            shifts[m:m + 1, :] = jnp.sum(dh, axis=0, keepdims=True)
            back[m] = norm_back(normal[m], inverse[m], dh * vector(vec, H_GAIN + m))
            for r in range(4):
                step = (3, 1, 2, 0)[r]
                for p in range(quarter):
                    g = back[m, pl.ds(16 * here.b + 4 * of[r] + p, 1), :]
                    at = own_row(dims, r, p)
                    c_rows[m, at:at + 1, :] = cot[m, 8 * step + p:8 * step + p + 1, :] + g
                    if r == 0:
                        dcls[p, m:m + 1, :] = g
            u = hidden_in[m]
            big, small = gelu_parts(u)
            c_act[m] = (u * big).astype(BF16)
            g = (c_rows[m] * vector(vec, F_SCALE)).astype(BF16)
            c_ddn[m] = g
            du = dot_t(g, down[m]) * (big + u * small)
            bias_grad[m:m + 1, :] += jnp.sum(du, axis=0, keepdims=True)
            low = du.astype(BF16)
            c_dup[m] = low
            acc[m] += t_dot(c_ddn[m], c_act[m])
            extra[m] = dot_t(low, up[m])
        for copy in sent_extra:
            copy.start()

    at = lax.broadcasted_iota(jnp.int32, (slab, 1), 0)
    inner = (at != 0) & (at != ip)

    def one(p, c):
        load_rows(dims, p, img, txt, rows)
        cot[0, pl.ds(8 * i + p, 1), :] = rows[0:1, :]
        cot[1, pl.ds(8 * i + p, 1), :] = rows[ip:ip + 1, :]
        ddn[p] = jnp.where(inner, rows[...] * vector(vec, F_SCALE), 0.0).astype(BF16)
        return c

    lax.fori_loop(0, quarter, one, 0)
    for m, lo, hi in ((0, 0, ip), (1, ip, slab)):
        count = quarter * (hi - lo)
        e = ins[:, lo:hi, :].reshape(count, model)
        u = dot(e, up[m]) + up_bias[m:m + 1]
        big, small = gelu_parts(u)
        a = (u * big).astype(BF16)
        slope = big + u * small
        bd[i, :, lo:hi, :] = dot(a, down[m]).astype(BF16).reshape(quarter, hi - lo, model)
        g = ddn[:, lo:hi, :].reshape(count, model)
        acc[m] += t_dot(g, a)
        du = dot_t(g, down[m]) * slope
        bias_grad[m:m + 1, :] += jnp.sum(du, axis=0, keepdims=True)
        low = du.astype(BF16)
        dup[:, lo:hi, :] = low.reshape(quarter, hi - lo, -1)
        bx[i, :, lo:hi, :] = dot_t(low, up[m]).astype(BF16).reshape(quarter, hi - lo, model)

    for j in range(2):
        @pl.when(i == 2 * j)
        def _():
            sent_x[j].start()
            sent_d[j].start()

    @pl.when(i == 1)
    def _():
        sent_x[0].wait_recv()

        def add_x(p, c):
            x_near[p] = (bx[1, p].astype(F32) + rx[0, p].astype(F32)).astype(BF16)
            return c

        lax.fori_loop(0, quarter, add_x, 0)
        sent_near.start()
        sent_d[0].wait_recv()

        def add_d(p, c):
            d_near[p] = (bd[1, p].astype(F32) + rd[0, p].astype(F32)).astype(BF16)
            return c

        lax.fori_loop(0, quarter, add_d, 0)

    @pl.when(i == 3)
    def _():
        piece = down_keep.shape[2]
        block = lambda j: pl.ds(pl.multiple_of(j * piece, piece), piece)
        for j in range(4):
            for m in range(2):
                down_keep[j, m] = acc[m, block(2 * j + here.x), :].astype(BF16)
                down_send[j, m] = acc[m, block(2 * j + 1 - here.x), :].astype(BF16)
        sent_d[1].wait_recv()

        def add_d(p, c):
            d_own[p] = bd[3, p].astype(F32) + rd[1, p].astype(F32)
            return c

        lax.fori_loop(0, quarter, add_d, 0)
        sent_x[1].wait_recv()
        sent_near.wait_recv()

        def add_x(p, c):
            dexp[p] = bx[3, p].astype(F32) + rx[1, p].astype(F32) + x_far[p].astype(F32)
            return c

        lax.fori_loop(0, quarter, add_x, 0)
        for copy in sent_extra:
            copy.wait_recv()
        for m in range(2):
            for p in range(quarter):
                line = [x[m, own_row(dims, r, p):own_row(dims, r, p) + 1, :]
                        for x, r in ((extra, 0), (extras.at[0], 2), (extras.at[1], 1), (extras.at[2], 3))]
                dexp[p, m * ip:m * ip + 1, :] += (line[0] + line[1]) + (line[2] + line[3])
        for copy in sent_x + sent_d + [sent_near] + sent_part + sent_extra + sent_cls:
            copy.wait_send()


def middle(dims, total, img, txt, own, peer, cls_own, cls_peer, vec, up, up_bias, down, weight, scale):
    model = own.shape[-1]
    hidden = up.shape[-1]
    slab, quarter = dims.slab, dims.quarter
    batch = 8

    def cot_at(i):
        here = Place()
        return here.quarter(1 - i // 2, 1 - i % 2), 0, 0

    held = pl.BlockSpec(memory_space=pltpu.VMEM)
    half = pl.BlockSpec((quarter, slab, model), lambda i: (jnp.where(i < 2, 1, 0), 0, 0))
    step = lambda cols: pl.BlockSpec((quarter, slab, cols), lambda i: (i, 0, 0))
    rows_of = lambda n, t: jax.ShapeDtypeStruct((n, slab, model), t)
    small = [((4, 2, model // 8, hidden), BF16)] * 2 + [((quarter, slab, model), F32), ((quarter, slab, model), F32), ((quarter, slab, model), BF16),
             ((2, hidden), F32), ((2, 16, model), BF16), ((2, 16, hidden), BF16), ((2, 16, hidden), BF16),
             ((2, 16, model), BF16), ((quarter, 8, model), F32), ((2, 16 * batch, model), BF16),
             ((2, 16 * batch, weight.shape[2]), BF16), ((2, model), F32), ((2, model), F32), ((2, 128), F32)]
    block = (quarter, slab, model)
    return pl.pallas_call(
        functools.partial(middle_kernel, dims, total),
        grid=(4,),
        in_specs=[pl.BlockSpec((quarter, dims.patches, model), cot_at),
                  pl.BlockSpec((quarter, dims.caption, model), cot_at)] + [half] * 2 + [held] * 6
        + [pl.BlockSpec(memory_space=pl.ANY), held],
        out_specs=[step(hidden)] + [held] * len(small),
        out_shape=[rows_of(4 * quarter, BF16)] + [jax.ShapeDtypeStruct(v, t) for v, t in small],
        scratch_shapes=[
            pltpu.VMEM((4,) + block, BF16), pltpu.VMEM((4,) + block, BF16),
            pltpu.VMEM((2,) + block, BF16), pltpu.VMEM((2,) + block, BF16),
            pltpu.VMEM(block, BF16), pltpu.VMEM(block, BF16), pltpu.VMEM(block, BF16),
            pltpu.VMEM((slab, model), F32),
            pltpu.VMEM((2, 16, model), F32), pltpu.VMEM((3, 2, 16, model), F32),
            pltpu.VMEM((batch, 2, 16, model), F32), pltpu.VMEM((2, 16 * batch, model), F32),
            pltpu.VMEM((2, 32, model), F32), pltpu.VMEM((2, 16, model), F32),
            pltpu.VMEM((2, 16, model), F32), pltpu.VMEM((3, 2, 16, model), F32),
            pltpu.VMEM((2, 16, hidden), F32), pltpu.VMEM(weight.shape, BF16),
            pltpu.VMEM(block, BF16), pltpu.VMEM((2, model, hidden), F32), pltpu.SemaphoreType.DMA((1,)),
            pltpu.SemaphoreType.DMA((18,)), pltpu.SemaphoreType.DMA((18,)),
        ],
        compiler_params=params(collective_id=2, has_side_effects=True),
        cost_estimate=pl.CostEstimate(
            flops=32 * quarter * slab * model * hidden, bytes_accessed=40_000_000, transcendentals=0),
        name="middle",
    )(img, txt, own, peer, cls_own, cls_peer, vec, up, up_bias, down, weight, scale)


def turn_kernel(dims, img, txt, peer, own, dup, ce, cu, down_keep, down_send, dexp, attended, attn, d_own, d_near, dcls, vec,
                down_sum, up_keep, up_send, dattended, dattn, dattn_peer, fin_img, fin_txt, sums,
                acc, d_far, n_peer, rows, side_keep, side_recv, e_in, dexp_in, attended_in, attn_in, d_own_in,
                local_sem, send_sem, recv_sem):
    here = Place()
    quarter, ip = dims.quarter, dims.ip
    i = pl.program_id(0)
    piece = side_keep.shape[2]
    sent_near = remote(d_near, d_far, send_sem, recv_sem, 0, here.near)

    def over(p):
        return remote(dattn.at[p], n_peer.at[p], send_sem, recv_sem, 1 + p, here.core)

    sent_core = [over(p) for p in range(quarter)]
    sent_side = remote(down_send, side_recv, send_sem, recv_sem, 1 + quarter, here.side)
    loaded = [pltpu.make_async_copy(src, dst, local_sem.at[j]) for j, (src, dst) in enumerate((
        (dexp, dexp_in), (attended, attended_in), (attn, attn_in), (d_own, d_own_in), (down_keep, side_keep)))]
    dexp, attended, attn, d_own = dexp_in, attended_in, attn_in, d_own_in
    spans = ((0, 0, ip), (1, ip, dims.slab))
    flat = lambda v: v.reshape(-1, v.shape[-1])
    block = lambda j: pl.ds(pl.multiple_of(j * piece, piece), piece)

    @pl.when(i == 0)
    def _():
        meet([here.core, here.near, here.side])
        sent_near.start()
        sent_side.start()
        for copy in loaded:
            copy.start()
        for m in range(2):
            acc[m] = t_dot(ce[m], cu[m])

    @pl.when(i % 2 == 0)
    def _():
        e_in[...] = peer[...]

    @pl.when(i % 2 == 1)
    def _():
        e_in[...] = own[...]

    for m, lo, hi in spans:
        acc[m] += t_dot(flat(e_in[:, lo:hi, :]), flat(dup[:, lo:hi, :]))

    @pl.when(i == 3)
    def _():
        for j in range(4):
            for m in range(2):
                up_keep[j, m] = acc[m, block(2 * j + here.x), :].astype(BF16)
                up_send[j, m] = acc[m, block(2 * j + 1 - here.x), :].astype(BF16)
        for copy in loaded:
            copy.wait()
        rows[...] = jnp.zeros_like(rows)
        sums[...] = jnp.zeros_like(sums)

        def load(p):
            load_rows(dims, p, img, txt, rows)
            rows[0:1, :] += dcls[p, 0:1, :]
            rows[ip:ip + 1, :] += dcls[p, 1:2, :]

        def norm(p, c):
            load(p)
            for m, lo, hi in ((0, 0, ip), (1, ip, dims.slab)):
                n, r = normalise(attended[p, lo:hi, :])
                dy = dexp[p, lo:hi, :]
                sums[m:m + 1, :] += jnp.sum(dy * n, axis=0, keepdims=True)
                sums[2 + m:3 + m, :] += jnp.sum(dy, axis=0, keepdims=True)
                d = rows[lo:hi, :] + norm_back(n, r, dy * vector(vec, GAIN2 + m))
                dattended[p, lo:hi, :] = d
                sd = d * vector(vec, A_SCALE)
                dattn[p, lo:hi, :] = sd.astype(BF16)
                a = attn[p, lo:hi, :] + vector(vec, A_BIAS)
                sums[4:5, :] += jnp.sum(d * a, axis=0, keepdims=True)
                sums[5:6, :] += jnp.sum(sd, axis=0, keepdims=True)
            over(p).start()
            return c

        lax.fori_loop(0, quarter, norm, 0)
        sent_near.wait_recv()

        def final(p, c):
            load(p)
            for m, lo, hi in ((0, 0, ip), (1, ip, dims.slab)):
                b = d_own[p, lo:hi, :] + d_far[p, lo:hi, :].astype(F32) + vector(vec, F_BIAS + m)
                f = attended[p, lo:hi, :] + vector(vec, F_SCALE) * b
                if m == 0:
                    fin_img[p] = f[0:dims.patches].astype(BF16)
                else:
                    fin_txt[p] = f[0:dims.caption].astype(BF16)
                g = rows[lo:hi, :]
                sums[6:7, :] += jnp.sum(g * b, axis=0, keepdims=True)
                sums[7 + m:8 + m, :] += jnp.sum(g, axis=0, keepdims=True) * vector(vec, F_SCALE)
            return c

        lax.fori_loop(0, quarter, final, 0)
        for p in range(quarter):
            sent_core[p].wait()
            dattn_peer[p] = n_peer[p]
        sent_side.wait()
        for j in range(4):
            down_sum[j] = (side_keep[j].astype(F32) + side_recv[j].astype(F32)).astype(BF16)
        sent_near.wait_send()


def turn(dims, img, txt, peer, own, dup, ce, cu, down_keep, down_send, dexp, attended, attn, d_own, d_near, dcls, vec):
    model = own.shape[-1]
    hidden = dup.shape[-1]
    slab, quarter = dims.slab, dims.quarter
    held = pl.BlockSpec(memory_space=pltpu.VMEM)

    def own_at(i):
        return Place().quarter(0, 0), 0, 0

    away = pl.BlockSpec(memory_space=pl.ANY)
    half = pl.BlockSpec((quarter, slab, model), lambda i: (jnp.where(i < 2, 1, 0), 0, 0))
    step = pl.BlockSpec((quarter, slab, hidden), lambda i: (i, 0, 0))
    block = (quarter, slab, model)
    part = (4, 2, model // 8, hidden)
    outs = [(part, BF16), (part, BF16), (part, BF16), (block, F32), (block, BF16), (block, BF16),
            ((quarter, dims.patches, model), BF16), ((quarter, dims.caption, model), BF16), ((16, model), F32)]
    return pl.pallas_call(
        functools.partial(turn_kernel, dims),
        grid=(4,),
        in_specs=[pl.BlockSpec((quarter, dims.patches, model), own_at),
                  pl.BlockSpec((quarter, dims.caption, model), own_at)] + [half] * 2 + [step]
        + [held] * 2 + [away] * 6 + [held] * 3,
        out_specs=[held] * len(outs),
        out_shape=[jax.ShapeDtypeStruct(v, t) for v, t in outs],
        scratch_shapes=[
            pltpu.VMEM((2, model, hidden), F32), pltpu.VMEM(block, BF16), pltpu.VMEM(block, BF16),
            pltpu.VMEM((slab, model), F32), pltpu.VMEM(part, BF16), pltpu.VMEM(part, BF16),
            pltpu.VMEM(block, BF16),
        ] + [pltpu.VMEM(block, F32)] * 4 + [
            pltpu.SemaphoreType.DMA((5,)),
            pltpu.SemaphoreType.DMA((2 + quarter,)), pltpu.SemaphoreType.DMA((2 + quarter,)),
        ],
        compiler_params=params(collective_id=3, has_side_effects=True),
        cost_estimate=pl.CostEstimate(
            flops=16 * quarter * slab * model * hidden, bytes_accessed=40_000_000, transcendentals=0),
        name="turn",
    )(img, txt, peer, own, dup, ce, cu, down_keep, down_send, dexp, attended, attn, d_own, d_near, dcls, vec)


def back_kernel(dims, lens, d_own, d_peer, normed, qkv_far, mixed_far, qkv_own, mixed_own, wq, wo, wf,
                fin_img, fin_txt, up_keep, up_send, down_sum,
                whole, grad_pair, grad_single, cols_far, cols_own, near_img, near_txt, far_sum, down_out, up_out,
                dattn, dm_far, dm_own, dq_far, dq_own, acc_far, acc_own, w_far, w_own, o_far, o_own, dn, grad_f,
                up_mine, up_side, up_sum, up_in, up_pass, up_last, down_mine, down_in, down_pass, down_last,
                n_send, n_recv, from_side, local_sem, send_sem, recv_sem):
    here = Place()
    i = pl.program_id(0)
    slab, quarter, local = dims.slab, dims.quarter, dims.local
    two, one_head = parts_of(dims)
    count = quarter * slab
    model = normed.shape[-1]
    piece = from_side.shape[1]
    block = lambda j: pl.ds(pl.multiple_of(j * piece, piece), piece)
    used = [0]

    def make(src, dst, device):
        at = used[0]
        used[0] += 1
        return remote(src, dst, send_sem, recv_sem, at, device)

    sent_near = [make(fin_img, near_img, here.near), make(fin_txt, near_txt, here.near)]
    sent_up = [make(up_send.at[j, m], up_side.at[m, j], here.side) for m in range(2) for j in range(4)]
    in_pair = lambda src, dst: [make(src.at[here.z_pair], dst.at[0], here.paired), make(src.at[here.z_rest], dst.at[1], here.paired)]
    sent_down = in_pair(down_sum, down_in)
    pass_down = make(down_pass, down_last, here.opposite)
    wide = grad_f.shape[1]
    sent_far = [make(grad_f.at[block(2 * j + 1 - here.x)], from_side.at[j, :, pl.ds(0, wide)], here.side) for j in range(4)]
    sent_far += [make(grad_single.at[block(2 * j + 1 - here.x)], from_side.at[j, :, pl.ds(wide, grad_single.shape[1])],
                      here.side) for j in range(4)]
    sent_pair = [in_pair(up_sum.at[m], up_in.at[m]) for m in range(2)]
    pass_up = [make(up_pass.at[m], up_last.at[m], here.opposite) for m in range(2)]
    sent_n = make(n_send, n_recv, here.core)
    loaded = [pltpu.make_async_copy(up_keep, up_mine, local_sem.at[0]),
              pltpu.make_async_copy(down_sum.at[here.z], down_mine.at[0], local_sem.at[1]),
              pltpu.make_async_copy(down_sum.at[here.z_far], down_mine.at[1], local_sem.at[2])]
    add = lambda *parts: functools.reduce(lambda p, q: p + q, [v.astype(F32) for v in parts])

    @pl.when(i == 0)
    def _():
        meet([here.core, here.near, here.side, here.paired, here.opposite])
        for copy in loaded + sent_near + sent_up + sent_down:
            copy.start()
        for acc, cols in ((acc_far, cols_far), (acc_own, cols_own)):
            acc[...] = jnp.zeros_like(acc)
            cols[...] = jnp.zeros_like(cols)
        for t in range(4):
            own, start = (wq, t * local) if t < 3 else (wo, 0)
            dst, at = (w_far, t * 2 * two) if t < 3 else (o_far, 0)
            copy_rows(dst, at, wf, t * local, two)
            copy_rows(dst, at + two, own, start + two, one_head)
            copy_rows(dst, at + two + one_head, wf, t * local + two, one_head)
            dst, at = (w_own, t * two) if t < 3 else (o_own, 0)
            copy_rows(dst, at, own, start, two)

    @pl.when(i % 2 == 0)
    def _():
        dattn[...] = d_peer[...]

    @pl.when(i % 2 == 1)
    def _():
        dattn[...] = d_own[...]

    whose = here.quarter(0, 1 - i % 2)

    @pl.when(i < 2)
    def _():
        part = back_step(dims, 2, lens, whose, dattn, normed, qkv_far, mixed_far, dm_far, dq_far, acc_far, cols_far,
                         w_far, o_far)
        dn[i] = part.reshape(quarter, slab, model)

    def sum_up(m):
        for j in range(4):
            sent_up[4 * m + j].wait_recv()
            up_sum[m, j] = add(up_mine[j, m], up_side[m, j]).astype(BF16)
        for copy in sent_pair[m]:
            copy.start()

    def pass_on(m):
        for copy in sent_pair[m]:
            copy.wait_recv()
        up_pass[m] = add(up_sum[m, here.z_far], up_in[m, 1]).astype(BF16)
        pass_up[m].start()

    @pl.when(i == 0)
    def _():
        for copy in loaded[1:]:
            copy.wait()
        for copy in sent_down:
            copy.wait_recv()
        down_pass[...] = add(down_mine[1], down_in[1]).astype(BF16)
        pass_down.start()
        loaded[0].wait()
        sum_up(0)

    @pl.when(i == 1)
    def _():
        for t in range(4):
            at = t * 2 * two
            to = 4 * two + t * one_head
            grad_f[:, t * two:(t + 1) * two] = acc_far[:, at:at + two].astype(BF16)
            grad_f[:, to:to + one_head] = acc_far[:, at + two + one_head:at + 2 * two].astype(BF16)
            grad_single[:, t * one_head:(t + 1) * one_head] = acc_far[:, at + two:at + two + one_head].astype(BF16)
        for copy in sent_far:
            copy.start()
        pass_on(0)
        sum_up(1)

    @pl.when(i >= 2)
    def _():
        part = back_step(dims, 1, lens, whose, dattn, normed, qkv_own, mixed_own, dm_own, dq_own, acc_own, cols_own,
                         w_own, o_own)
        total = part.reshape(quarter, slab, model) + dn[i - 2]

        @pl.when(i == 2)
        def _():
            n_send[...] = total.astype(BF16)
            sent_n.start()
            pass_on(1)

        @pl.when(i == 3)
        def _():
            whole[...] = total

    @pl.when(i == 3)
    def _():
        grad_pair[...] = acc_own[...].astype(BF16)
        sent_n.wait_recv()
        whole[...] += n_recv[...].astype(F32)
        down_out[...] = add(down_mine[0], down_in[0])
        for copy in sent_far:
            copy.wait_recv()
        for j in range(4):
            far_sum[j, :, 0:wide] = add(grad_f[block(2 * j + here.x), :], from_side[j, :, 0:wide]).astype(BF16)
            far_sum[j, :, wide:] = add(grad_single[block(2 * j + here.x), :], from_side[j, :, wide:]).astype(BF16)
        pass_down.wait_recv()
        down_out[...] += down_last[...].astype(F32)
        for m in range(2):
            pass_up[m].wait_recv()
            up_out[m] = add(up_sum[m, here.z], up_in[m, 0], up_last[m])
        for copy in sent_near:
            copy.wait_recv()
        for copy in sent_near + sent_up + sent_down + sent_far + sent_pair[0] + sent_pair[1] + pass_up + [pass_down, sent_n]:
            copy.wait_send()


def back(dims, lens, d_own, d_peer, normed, qkv_far, mixed_far, qkv_own, mixed_own, wq, wo, wf,
         fin_img, fin_txt, up_keep, up_send, down_sum):
    model = normed.shape[-1]
    slab, quarter = dims.slab, dims.quarter
    hidden = up_keep.shape[-1]
    piece = model // 8
    held = pl.BlockSpec(memory_space=pltpu.VMEM)
    away = pl.BlockSpec(memory_space=pl.ANY)
    spec = lambda cols, at: pl.BlockSpec((quarter, slab, cols), lambda i: (at(i), 0, 0))
    early, late = lambda i: jnp.maximum(1 - i, 0), lambda i: jnp.where(i < 3, 1, 0)
    rows = (quarter, slab, model)
    outs = [(held, rows, F32), (held, (model, 512), BF16), (held, (model, 256), BF16),
            (held, (1, 768), F32), (held, (1, 384), F32),
            (away, fin_img.shape, BF16), (away, fin_txt.shape, BF16),
            (held, (4, piece, model + 256), BF16), (held, (2, piece, hidden), F32), (held, (2, piece, hidden), F32)]
    slabs = lambda cols: pltpu.VMEM((quarter, slab, cols), BF16)
    return pl.pallas_call(
        functools.partial(back_kernel, dims),
        grid=(4,),
        in_specs=[pl.BlockSpec(memory_space=pltpu.SMEM), held, held, spec(model, lambda i: 1 - i % 2),
                  spec(768, early), spec(256, early), spec(384, late), spec(128, late), held, held, held]
        + [away] * 5,
        out_specs=[v[0] for v in outs],
        out_shape=[jax.ShapeDtypeStruct(v[1], v[2]) for v in outs],
        scratch_shapes=[
            slabs(model), slabs(256), slabs(128), slabs(768), slabs(384),
            pltpu.VMEM((model, 1024), F32), pltpu.VMEM((model, 512), F32),
            pltpu.VMEM((768, model), BF16), pltpu.VMEM((384, model), BF16),
            pltpu.VMEM((256, model), BF16), pltpu.VMEM((128, model), BF16),
            pltpu.VMEM((2,) + rows, F32), pltpu.VMEM((model, model), BF16),
            pltpu.VMEM((4, 2, piece, hidden), BF16), pltpu.VMEM((2, 4, piece, hidden), BF16),
            pltpu.VMEM((2, 4, piece, hidden), BF16), pltpu.VMEM((2, 2, piece, hidden), BF16),
            pltpu.VMEM((2, piece, hidden), BF16), pltpu.VMEM((2, piece, hidden), BF16),
            pltpu.VMEM((2, 2, piece, hidden), BF16), pltpu.VMEM((2, 2, piece, hidden), BF16),
            pltpu.VMEM((2, piece, hidden), BF16), pltpu.VMEM((2, piece, hidden), BF16),
            pltpu.VMEM(rows, BF16), pltpu.VMEM(rows, BF16), pltpu.VMEM((4, piece, model + 256), BF16),
            pltpu.SemaphoreType.DMA((3,)), pltpu.SemaphoreType.DMA((28,)), pltpu.SemaphoreType.DMA((28,)),
        ],
        compiler_params=params(collective_id=4, has_side_effects=True),
        cost_estimate=pl.CostEstimate(
            flops=24 * quarter * slab * model * 1152, bytes_accessed=30_000_000, transcendentals=0),
        name="back",
    )(lens, d_own, d_peer, normed, qkv_far, mixed_far, qkv_own, mixed_own, wq, wo, wf,
      fin_img, fin_txt, up_keep, up_send, down_sum)


V_ROWS, V_MP, V_HEADS, V_FAR = 16, 11, 13, 256


def finish_kernel(dims, dnormed, dattended, states_img, states_txt, vec, fin_img, fin_txt,
                  near_img, near_txt, grad_pair, grad_far, own_sums, up_sums, cols_own, cols_far,
                  core_img, core_txt, across_img, across_txt, back_img, back_txt, grad_out, v_out,
                  s_img, s_txt, d_img, d_txt, rows, xr, zs, z_in, z_pass, z_last, f_in, f_pass, f_last, far_sum, far_recv, vs, vr,
                  local_sem, send_sem, recv_sem):
    quarter = dims.quarter
    here = Place()
    z, x, m = here.z, here.x, here.m
    near_quarter = here.quarter(1, 0)
    used = [0]

    def send(src, dst, device):
        at = used[0]
        used[0] += 1
        return remote(src, dst, send_sem, recv_sem, at, device)

    loaded = [pltpu.make_async_copy(states_img.at[pl.ds(m * quarter, quarter)], s_img, local_sem.at[0]),
              pltpu.make_async_copy(states_txt.at[pl.ds(m * quarter, quarter)], s_txt, local_sem.at[1])]
    for copy in loaded:
        copy.start()
    meet([here.core, here.near, here.side, here.paired, here.opposite])

    piece = xr.shape[1]
    wide = grad_pair.shape[1]
    block = lambda j: pl.ds(pl.multiple_of(j * piece, piece), piece)
    x_copies = []
    for j in range(4):
        x_copies.append(send(grad_pair.at[block(2 * j + 1 - x)], xr.at[j], here.side))
        x_copies[-1].start()
    add = lambda *parts: functools.reduce(lambda p, q: p + q, [v.astype(F32) for v in parts])
    in_pair = lambda src, dst: [send(src.at[here.z_pair], dst.at[0], here.paired),
                                send(src.at[here.z_rest], dst.at[1], here.paired)]
    far_copies = in_pair(grad_far, f_in)
    for copy in far_copies:
        copy.start()

    fin_remote = [send(src, dst, here.core) for src, dst in (
        (fin_img, core_img), (fin_txt, core_txt), (near_img, across_img), (near_txt, across_txt))]

    rows[...] = jnp.zeros_like(rows)
    for copy in loaded:
        copy.wait()
    total = [jnp.zeros((1, rows.shape[1]), F32)] * 2
    back_local, to_near, to_other = [], [], []
    for p in range(quarter):
        load_rows(dims, p, s_img, s_txt, rows)
        n, r = normalise(rows[...])
        dy = dnormed[p]
        total[0] = total[0] + jnp.sum(dy * n, axis=0, keepdims=True)
        total[1] = total[1] + jnp.sum(dy, axis=0, keepdims=True)
        d = dattended[p] + norm_back(n, r, dy * vector(vec, GAIN1))
        d_img[p] = d[0:dims.patches].astype(BF16)
        d_txt[p] = d[dims.ip:dims.ip + dims.caption].astype(BF16)
        for j, (src, dst) in enumerate(((d_img, back_img), (d_txt, back_txt))):
            at = dst.at[m * quarter + p]
            to_near.append(send(src.at[p], at, here.near))
            to_near[-1].start()
            to_other.append(send(src.at[p], at, here.core))
            to_other[-1].start()
            back_local.append(pltpu.make_async_copy(src.at[p], at, local_sem.at[2 + 2 * p + j]))
            back_local[-1].start()
    for copy in fin_remote:
        copy.start()

    at = lax.broadcasted_iota(jnp.int32, (V_ROWS, 1), 0)
    two, one_head = parts_of(dims)
    vs[0] = jnp.zeros(vs.shape[1:], F32)
    vs[0, 0:1, :] = total[0]
    vs[0, 1:2, :] = total[1]
    vs[0, 2:V_MP, :] = own_sums[0:V_MP - 2, :]
    vs[0, V_MP:V_HEADS, :] = up_sums[...]
    for j in range(2):
        own_at, far_at = 2 * j * two, 4 * j * two
        vs[0, V_HEADS + j:V_HEADS + j + 1, 0:two] = cols_own[0:1, own_at:own_at + two]
        vs[0, V_HEADS + j:V_HEADS + j + 1, two:two + one_head] = cols_far[0:1, far_at + two:far_at + two + one_head]
        vs[0, V_HEADS + j:V_HEADS + j + 1, V_FAR:V_FAR + two] = cols_far[0:1, far_at:far_at + two]
        vs[0, V_HEADS + j:V_HEADS + j + 1, V_FAR + two:V_FAR + two + one_head] = cols_far[0:1, far_at + two + one_head:far_at + 2 * two]
    v = vs[0]
    v_copies = []

    def exchange(step, value, device):
        vs[step] = value
        copy = send(vs.at[step], vr.at[step], device)
        copy.start()
        copy.wait_recv()
        v_copies.append(copy)
        return vr[step]

    v = v + jnp.where(at < V_MP, exchange(0, v, here.core), 0.0)
    for copy in far_copies:
        copy.wait_recv()
    f_pass[...] = add(grad_far[here.z_far], f_in[1]).astype(BF16)
    far_copies.append(send(f_pass, f_last, here.opposite))
    far_copies[-1].start()
    v = v + exchange(1, v, here.side)
    v = v + exchange(2, v, here.paired)
    vs[3] = v
    v_far = send(vs.at[3], vr.at[3], here.opposite)
    v_far.start()

    def own_sum(j):
        return add(grad_pair[block(2 * j + x), :], xr[j])

    for copy in x_copies:
        copy.wait_recv()
    for j in range(4):
        zs[j] = own_sum(j).astype(BF16)
    z_copies = in_pair(zs, z_in)
    for copy in z_copies:
        copy.start()

    far_copies[-1].wait_recv()
    narrow = far_sum.shape[1]
    far_sum[...] = add(grad_far[z, :, 0:narrow], f_in[0, :, 0:narrow], f_last[:, 0:narrow]).astype(BF16)
    far_copy = send(far_sum, far_recv, here.near)
    far_copy.start()
    v_far.wait_recv()
    v = v + vr[3]
    for copy in z_copies:
        copy.wait_recv()
    z_pass[...] = add(zs[here.z_far], z_in[1]).astype(BF16)
    z_copies.append(send(z_pass, z_last, here.opposite))
    z_copies[-1].start()
    vs[4] = v
    v_near = send(vs.at[4], vr.at[4], here.near)
    v_near.start()
    for copy in back_local:
        copy.wait()
    onward = []
    for p in range(quarter):
        for j, dst in enumerate((back_img, back_txt)):
            to_near[2 * p + j].wait_recv()
            at_near = dst.at[near_quarter * quarter + p]
            onward.append(send(at_near, at_near, here.core))
            onward[-1].start()
    far_copy.wait_recv()
    z_copies[-1].wait_recv()
    grad_out[:, 0:wide] = own_sum(z) + add(far_recv[:, 0:wide], z_in[0], z_last[...])
    grad_out[:, wide:] = add(
        far_recv[:, wide:], grad_far[z, :, narrow:], f_in[0, :, narrow:], f_last[:, narrow:])
    v_near.wait_recv()
    there = vr[4]
    v_out[...] = v + jnp.where(at < V_MP, there, 0.0)
    width = two + one_head
    v_out[V_HEADS:V_HEADS + 2, 0:width] = v[V_HEADS:V_HEADS + 2, 0:width] + there[V_HEADS:V_HEADS + 2, V_FAR:V_FAR + width]
    for copy in to_other + fin_remote + onward:
        copy.wait()
    for copy in x_copies + far_copies + to_near + z_copies + v_copies + [far_copy, v_near, v_far]:
        copy.wait_send()


def finish(dims, dnormed, dattended, states_img, states_txt, vec, fin_img, fin_txt,
           near_img, near_txt, grad_pair, grad_far, *tables):
    pairs, patches, model = states_img.shape
    caption = states_txt.shape[1]
    quarter, slab = dims.quarter, dims.slab
    piece, cols = grad_far.shape[1], model
    wide, all_cols = grad_pair.shape[1], grad_far.shape[2]
    held = pl.BlockSpec(memory_space=pltpu.VMEM)
    away = pl.BlockSpec(memory_space=pl.ANY)
    n_remote = 7 * quarter + 28
    return pl.pallas_call(
        functools.partial(finish_kernel, dims),
        in_specs=[held, held] + [away] * 2 + [held] + [away] * 4 + [held] * 6,
        out_specs=[away] * 6 + [held] * 2,
        out_shape=[jax.ShapeDtypeStruct(v.shape, BF16) for v in (fin_img, fin_txt) * 2] + [
            jax.ShapeDtypeStruct((pairs, patches, model), BF16),
            jax.ShapeDtypeStruct((pairs, caption, model), BF16),
            jax.ShapeDtypeStruct((piece, cols), F32),
            jax.ShapeDtypeStruct((V_ROWS, model), F32),
        ],
        scratch_shapes=[
            pltpu.VMEM((quarter, patches, model), BF16),
            pltpu.VMEM((quarter, caption, model), BF16),
            pltpu.VMEM((quarter, patches, model), BF16),
            pltpu.VMEM((quarter, caption, model), BF16),
            pltpu.VMEM((slab, model), F32),
            pltpu.VMEM((4, piece, wide), BF16), pltpu.VMEM((4, piece, wide), BF16),
            pltpu.VMEM((2, piece, wide), BF16), pltpu.VMEM((piece, wide), BF16), pltpu.VMEM((piece, wide), BF16),
            pltpu.VMEM((2, piece, all_cols), BF16), pltpu.VMEM((piece, all_cols), BF16), pltpu.VMEM((piece, all_cols), BF16),
            pltpu.VMEM((piece, cols), BF16), pltpu.VMEM((piece, cols), BF16),
            pltpu.VMEM((5, V_ROWS, model), F32),
            pltpu.VMEM((5, V_ROWS, model), F32),
            pltpu.SemaphoreType.DMA((2 + 2 * quarter,)),
            pltpu.SemaphoreType.DMA((n_remote,)),
            pltpu.SemaphoreType.DMA((n_remote,)),
        ],
        compiler_params=params(collective_id=1, has_side_effects=True),
        name="finish",
    )(dnormed, dattended, states_img, states_txt, vec, fin_img, fin_txt,
      near_img, near_txt, grad_pair, grad_far, *tables)


def spread_kernel(dims, cols, sums, grad, gains, shifts, up, down, head_in, dproj, *refs):
    forward, refs = refs[:8], refs[8:]
    back_img, back_txt, *refs = refs
    outs, refs = refs[:12], refs[12:]
    (qkv, out_w, up_out, down_out, head_out, out_img, out_txt, grad_img, grad_txt,
     turned, held_img, held_txt, in_sem, out_sem) = refs
    here = Place()
    quarter = dims.quarter
    whose = [here.quarter(0, 0), here.quarter(1, 0), here.quarter(0, 1), here.quarter(1, 1)]
    place = lambda q: pl.ds(q * quarter, quarter)
    comes, goes = [], []
    for r in range(4):
        for j, (held, src, dst, back, to) in enumerate((
            (held_img, forward[2 * r], out_img, back_img, grad_img), (held_txt, forward[2 * r + 1], out_txt, back_txt, grad_txt),
        )):
            for k, (source, target, q) in enumerate(((src, dst, whose[r]), (back.at[place(r)], to, r))):
                at = 4 * r + 2 * j + k
                comes.append(pltpu.make_async_copy(source, held.at[2 * r + k], in_sem.at[at]))
                goes.append(pltpu.make_async_copy(held.at[2 * r + k], target.at[place(q)], out_sem.at[at]))
    for copy in comes:
        copy.start()
    turn_by = sums.shape[1] - here.b * cols

    def slice_of(value):
        return pltpu.roll(value, turn_by, 1)[:, 0:cols]

    mine = slice_of(sums[...])
    for out, (lo, count) in zip(outs[:8], ((0, 1), (1, 1), (7, 1), (6, 1), (2, 2), (4, 2), (9, 2), (8, 1))):
        out[...] = mine[lo:lo + count, :]
    wide = jnp.concatenate([gains[...], shifts[...], jnp.zeros((4, sums.shape[1]), F32)], axis=0)
    heads = slice_of(wide)
    outs[8][...] = heads[0:2, :]
    outs[9][...] = heads[2:4, :]
    outs[10][...] = sums[V_MP:V_MP + 2, :]
    outs[11][...] = sums[V_HEADS:V_HEADS + 2, 0:outs[11].shape[1]]
    two, one = 2 * HEAD_DIM, HEAD_DIM
    for t in range(3):
        qkv[t, :, 0:two] = grad[:, t * two:(t + 1) * two]
        qkv[t, :, two:two + one] = grad[:, 4 * two + t * one:4 * two + (t + 1) * one]
    turned[...] = jnp.zeros_like(turned)
    turned[0:cols, 0:two] = grad[:, 3 * two:4 * two]
    turned[0:cols, two:two + one] = grad[:, 4 * two + 3 * one:4 * two + 4 * one]
    out_w[...] = turned[...].T[0:two + one, 0:cols]
    up_out[...] = up[...]
    down_out[...] = down[...]
    for come, go in zip(comes, goes):
        come.wait()
        go.start()
    for m in range(2):
        part = pltpu.roll(head_in[m].astype(F32), turn_by, 1)[:, 0:128].astype(BF16)
        head_out[m] = t_dot(part, dproj[m])[0:cols]
    for go in goes:
        go.wait()


def spread(dims, sums, grad, gains, shifts, up, down, head_in, dproj, forward, back_img, back_txt):
    cols, model = grad.shape[0], sums.shape[1]
    local, quarter = dims.local, dims.quarter
    assert cols <= 128
    shapes = [(1, cols)] * 4 + [(2, cols)] * 3 + [(1, cols)] + [(2, cols)] * 2 + [(2, model), (2, local)]
    shapes += [(3, cols, local), (local, cols), up.shape, down.shape, (2, cols, dproj.shape[2])]
    held = pl.BlockSpec(memory_space=pltpu.VMEM)
    away = pl.BlockSpec(memory_space=pl.ANY)
    args = (sums, grad, gains, shifts, up, down, head_in, dproj)
    return pl.pallas_call(
        functools.partial(spread_kernel, dims, cols),
        in_specs=[held] * len(args) + [away] * 10,
        out_specs=[held] * len(shapes) + [away] * 4,
        out_shape=[jax.ShapeDtypeStruct(v, F32) for v in shapes]
        + [jax.ShapeDtypeStruct(v.shape, BF16) for v in (back_img, back_txt) * 2],
        scratch_shapes=[
            pltpu.VMEM((128, 256), F32),
            pltpu.VMEM((8, quarter, dims.patches, model), BF16), pltpu.VMEM((8, quarter, dims.caption, model), BF16),
            pltpu.SemaphoreType.DMA((16,)), pltpu.SemaphoreType.DMA((16,)),
        ],
        compiler_params=params(),
        cost_estimate=pl.CostEstimate(flops=1_000_000, bytes_accessed=20_000_000, transcendentals=0),
        name="spread",
    )(*args, *forward, back_img, back_txt)


def per_device(
    image_states, text_states, caption_lengths, image_cotangent, text_cotangent,
    first_gain, first_shift, query_key_value, query_value_bias, output_weight, output_bias,
    attention_scale, expert_gain, expert_shift, expert_up, expert_up_bias, expert_down,
    expert_down_bias, feedforward_scale, head_gain, head_shift, head_weight, logit_scale,
):
    pairs, patches, model = image_states.shape
    caption = text_states.shape[1]
    local = query_key_value.shape[2]
    quarter = pairs // 4
    batch_size = lax.axis_size("batch")
    assert lax.axis_size("mp") == 4 and pairs == 4 * quarter and quarter <= 3
    assert batch_size & (batch_size - 1) == 0
    assert local == 3 * HEAD_DIM
    ip, tp = up16(patches), up16(caption)
    dims = Dims(patches, caption, ip, tp, ip + tp, quarter, local)
    me = lax.axis_index("mp")
    batch_at = lax.axis_index("batch")
    order = me ^ jnp.asarray(ORDER, jnp.int32)
    vectors = (first_gain, first_shift, attention_scale, output_bias, expert_gain, expert_shift,
               feedforward_scale, expert_down_bias, head_gain, head_shift)
    own_w = jnp.transpose(query_key_value, (1, 2, 0)).reshape(3 * local, model)
    one_kernel = batch_size == 8 and model // batch_size % 32 == 0 and expert_up.shape[2] == model
    if one_kernel:
        (vec, normed, qkv_own, mixed_own, qkv_far, mixed_far, wf, attended, attn, e_own, e_peer, cls_own, cls_peer) = front(
            dims, caption_lengths, image_states, text_states, vectors, query_value_bias, own_w, output_weight)
    else:
        vec = jnp.concatenate([v.reshape(-1, model) for v in vectors] + [jnp.zeros((1, model), F32)])
        wo = jnp.concatenate([own_w, output_weight])
        wf = to_y(wo)
        far_bias = to_y(query_value_bias)
        normed, qkv_own, rest, mixed_own = attend_own(
            dims, order, caption_lengths, image_states, text_states, vec, query_value_bias, wo)
        qkv_far, mixed_far, a_keep, a_send = attend_far(
            dims, order, caption_lengths, normed, rest, mixed_own, far_bias, wo, wf)
        a_recv = to_core(a_send)
        attended, attn, e_own, cls_own = residual(
            dims, order, a_keep, a_recv, image_states, text_states, vec)
        e_peer = to_core(e_own)
        cls_peer = to_core(cls_own)
    if one_kernel:
        (dup, down_keep, down_send, dexp, d_own, d_near, up_sums, class_e, _, c_dup, _, dcls, head_in, dproj,
         grad_head_gain, grad_head_shift, scalars) = middle(
            dims, pairs * batch_size, image_cotangent, text_cotangent, e_own, e_peer, cls_own, cls_peer, vec,
            expert_up, expert_up_bias, expert_down, head_weight, logit_scale.reshape(1, 1))
        down_sum, up_keep, up_send, dattended, dattn, dattn_peer, fin_img, fin_txt, own_sums = turn(
            dims, image_cotangent, text_cotangent, e_peer, e_own, dup, class_e, c_dup, down_keep, down_send,
            dexp, attended, attn, d_own, d_near, dcls, vec)
    else:
        class_part, class_e = class_forward(dims, cls_own, cls_peer, expert_up, expert_up_bias, expert_down)
        class_parts = from_others(class_part, "mp", 1, 4)

        act_a, dup_a, ddn_a, d_send3, d_keep1, x_send3, x_keep1, bias_a, cot_a = experts(
            dims, "experts_a", 1, order[jnp.asarray([3, 1])], e_peer, e_own, image_cotangent, text_cotangent,
            tie(vec, class_part), expert_up, expert_up_bias, expert_down)
        x_recv1 = to_core(x_send3)
        d_recv1 = to_core(d_send3)
        final_class = class_final(
            dims, order, cls_own, cls_peer, class_parts, tie(vec, bias_a))
        class_blocks = gather_batch(final_class[None])
        x_near = add_low(x_keep1, x_recv1)
        x_far = to_y(x_near)
        act_b, dup_b, ddn_b, d_send2, d_keep0, x_send2, x_keep0, bias_b, cot_b = experts(
            dims, "experts_b", 0, order[jnp.asarray([2, 0])], e_peer, e_own, image_cotangent, text_cotangent,
            tie(vec, final_class, x_near), expert_up, expert_up_bias, expert_down)
        x_recv0 = to_core(x_send2)
        d_recv0 = to_core(d_send2)

        head_in, dproj, dclass, grad_head_gain, grad_head_shift, scalars = (contrast if batch_size <= 8 else contrast_large)(
            dims, pairs * batch_size, batch_at.reshape(1), class_blocks, tie(vec, bias_b), head_weight,
             logit_scale.reshape(1, 1))
        c_act, c_dup, c_ddn, c_dexp, c_bias, dcls = class_back(
            dims, order, class_e, cot_a, cot_b, dclass, vec, expert_up, expert_up_bias, expert_down)
        extras = from_others(c_dexp, "mp", 1, 4)
        d_far = to_y(add_low(d_keep1, tie(d_recv1, c_dexp)))
        expert_grad = expert_grads(
            dims, e_peer, e_own, act_a, dup_a, ddn_a, act_b, dup_b, ddn_b, class_e, c_act, c_dup, c_ddn)
        expert_sum = lax.psum_scatter(expert_grad, "batch", scatter_dimension=1, tiled=True)

        dattended, dattn, sums_two = norm_two(
            dims, order, x_keep0, x_recv0, x_far, attended, a_keep, a_recv, image_cotangent, text_cotangent,
            dcls, extras, tie(vec, expert_grad))
        dattn_peer = to_core(dattn)
        fin_img, fin_txt, sums_fin = final_rows(
            dims, order, d_keep0, d_recv0, d_far, attended, image_cotangent, text_cotangent, dcls,
            tie(vec, sums_two))
        own_sums = jnp.concatenate([sums_two[:6], sums_fin[:3]])
        up_sums = bias_a + bias_b + c_bias
    contrast_loss = scalars[0, :1]
    grad_logit_scale = scalars[1, :1]
    if one_kernel:
        (dnormed, grad_o01, grad_o2, cols_far, cols_own, near_img, near_txt, far_sum, grad_down,
         grad_up) = back(
            dims, caption_lengths, dattn, dattn_peer, normed, qkv_far, mixed_far, qkv_own, mixed_own,
            own_w, output_weight, wf, fin_img, fin_txt, up_keep, up_send, down_sum)
    else:
        n_keep, n_send, grad_far, grad_o2, cols_far = attend_back(
            dims, True, order, caption_lengths, dattn, dattn_peer, normed, qkv_far, mixed_far, own_w, output_weight, wf)
        n_keep, n_send, grad_o01, cols_own = attend_back(
            dims, False, order, caption_lengths, dattn, dattn_peer, normed, qkv_own, mixed_own, own_w, output_weight, wf,
            prior=(n_keep, n_send))
    cols = model // batch_size
    mine = lambda v, axis: lax.dynamic_slice_in_dim(v, batch_at * cols, cols, axis=axis)
    pair, single = 2 * HEAD_DIM, HEAD_DIM
    if one_kernel:
        core_img, core_txt, across_img, across_txt, back_img, back_txt, attn_grad, sums = finish(
            dims, dnormed, dattended, image_states, text_states, vec, fin_img, fin_txt,
            near_img, near_txt, grad_o01, far_sum, own_sums, up_sums, cols_own, cols_far)
        forward = (fin_img, fin_txt, near_img, near_txt, core_img, core_txt, across_img, across_txt)
        (*vectors, grad_qkv, grad_output_weight, grad_up, grad_down, grad_head_weight,
         image_output, text_output, image_grad, text_grad) = spread(
            dims, sums, attn_grad, grad_head_gain, grad_head_shift, grad_up, grad_down, head_in, dproj,
            forward, back_img, back_txt)
        flat = lambda v: v.reshape(-1)
        return (
            image_output,
            text_output,
            contrast_loss,
            image_grad,
            text_grad,
            flat(vectors[0]),
            flat(vectors[1]),
            jnp.transpose(grad_qkv, (1, 0, 2)),
            vectors[11],
            grad_output_weight,
            flat(vectors[2]),
            flat(vectors[3]),
            vectors[4],
            vectors[5],
            grad_up,
            vectors[10],
            jnp.transpose(grad_down, (0, 2, 1)),
            vectors[6],
            flat(vectors[7]),
            vectors[8],
            vectors[9],
            grad_head_weight,
            grad_logit_scale,
        )
    else:
        grad_head_weight = jnp.einsum("mnc,mne->mce", mine(head_in, 2), dproj, preferred_element_type=F32)
        grad_expert_up = expert_sum[:2].astype(F32)
        grad_expert_down = jnp.transpose(expert_sum[2:].astype(F32), (0, 2, 1))
        cols_own = cols_own.reshape(3, pair)[::2]
        cols_far = cols_far.reshape(3, 2 * pair)[::2]
        heads = jnp.concatenate([cols_own, cols_far[:, pair:pair + single]], axis=1)
        heads_far = jnp.concatenate([cols_far[:, :pair], cols_far[:, pair + single:]], axis=1)
        n_recv = to_core(n_send)
        d_img, d_txt, sums_one = norm_one(
            dims, order, n_keep, n_recv, dattended, image_states, text_states, vec)
        image_output = gather_rows(fin_img, me)
        text_output = gather_rows(fin_txt, me)
        image_grad = gather_rows(d_img, me)
        text_grad = gather_rows(d_txt, me)
        grad_own = jnp.concatenate([grad_o01, grad_o2], axis=1)
        grad_far = lax.psum_scatter(grad_far, "batch", scatter_dimension=0, tiled=True)
        grad_own = lax.psum_scatter(grad_own, "batch", scatter_dimension=0, tiled=True)
        attn_grad = grad_own.astype(F32) + to_y(grad_far).astype(F32)
        heads = heads + to_y(heads_far)
        own_sums = sum_over(jnp.concatenate([sums_one[:2], own_sums]), "mp")
        flat = jnp.concatenate([own_sums.reshape(-1), heads.reshape(-1), up_sums.reshape(-1)])
        count = flat.shape[0]
        flat = jnp.pad(flat, (0, -count % 1024)).reshape(-1, 128)
        flat = sum_over(flat, "batch").reshape(-1)[:count]
        done = own_sums.shape[0]
        own_sums = mine(flat[:done * model].reshape(done, model), 1)
        heads = flat[done * model:done * model + 2 * local].reshape(2, local)
        grad_expert_up_bias = flat[done * model + 2 * local:].reshape(up_sums.shape)
    attn_grad = jnp.concatenate(
        [attn_grad[:, :4 * pair].reshape(cols, 4, pair), attn_grad[:, 4 * pair:].reshape(cols, 4, single)], axis=2)
    grad_query_key_value = attn_grad[:, :3]
    grad_output_weight = jnp.transpose(attn_grad[:, 3])
    return (
        image_output,
        text_output,
        contrast_loss,
        image_grad,
        text_grad,
        own_sums[0],
        own_sums[1],
        grad_query_key_value,
        heads,
        grad_output_weight,
        own_sums[7],
        own_sums[6],
        own_sums[2:4],
        own_sums[4:6],
        grad_expert_up,
        grad_expert_up_bias,
        grad_expert_down,
        own_sums[9:11],
        own_sums[8],
        mine(grad_head_gain, 1),
        mine(grad_head_shift, 1),
        grad_head_weight,
        grad_logit_scale,
    )


def solution(mesh):
    return jax.shard_map(
        per_device,
        mesh=mesh,
        in_specs=(
            P("batch", None, None),
            P("batch", None, None),
            P("batch"),
            P("batch", None, None),
            P("batch", None, None),
            P(),
            P(),
            P(None, None, "mp"),
            P(None, "mp"),
            P("mp", None),
            P(),
            P(),
            P(),
            P(),
            P(None, None, "mp"),
            P(None, "mp"),
            P(None, "mp", None),
            P(),
            P(),
            P(),
            P(),
            P(),
            P(),
        ),
        out_specs=(
            P("batch", None, None),
            P("batch", None, None),
            P(),
            P("batch", None, None),
            P("batch", None, None),
            P("batch"),
            P("batch"),
            P("batch", None, "mp"),
            P(None, "mp"),
            P("mp", "batch"),
            P("batch"),
            P("batch"),
            P(None, "batch"),
            P(None, "batch"),
            P(None, "batch", "mp"),
            P(None, "mp"),
            P(None, "mp", "batch"),
            P(None, "batch"),
            P("batch"),
            P(None, "batch"),
            P(None, "batch"),
            P(None, "batch", None),
            P(),
        ),
        check_vma=False,
    )
```

```python
import functools
from typing import NamedTuple

import jax
import jax.numpy as jnp
from jax import lax
from jax.experimental import pallas as pl
from jax.experimental.pallas import tpu as pltpu
from jax.sharding import PartitionSpec as P

HEAD_DIM = 64
F32 = jnp.float32
BF16 = jnp.bfloat16
NEG = -1e9
EPS = 1e-5
ORDER = (0, 2, 1, 3)

VMEM_LIMIT = 60 * 1024 * 1024


def params(**kw):
    return pltpu.CompilerParams(vmem_limit_bytes=VMEM_LIMIT, **kw)


def up16(n):
    return -(-n // 16) * 16


def dot(a, b):
    return jnp.dot(a, b, preferred_element_type=F32)


def dot_t(a, b):
    return lax.dot_general(a, b, (((1,), (1,)), ((), ())), preferred_element_type=F32)


def t_dot(a, b):
    return lax.dot_general(a, b, (((0,), (0,)), ((), ())), preferred_element_type=F32)


def normalise(x):
    c = x - jnp.mean(x, axis=-1, keepdims=True)
    v = jnp.mean(c * c, axis=-1, keepdims=True)
    r = lax.rsqrt(v + EPS)
    return c * r, r


def norm_back(n, r, dn):
    a = jnp.mean(dn, axis=-1, keepdims=True)
    b = jnp.mean(dn * n, axis=-1, keepdims=True)
    return (dn - a - n * b) * r


def gelu_parts(u):
    big = 0.5 * (1.0 + lax.erf(u * 0.7071067811865476))
    small = 0.3989422804014327 * jnp.exp(-0.5 * u * u)
    return big, small


def gelu_low(u):
    return (u * (0.5 * (1.0 + lax.erf(u * 0.7071067811865476)))).astype(BF16)


def softmax_rows(scores):
    m = jnp.max(scores, axis=-1, keepdims=True)
    e = jnp.exp(scores - m)
    return e * (1.0 / jnp.sum(e, axis=-1, keepdims=True))


def tie(value, *after):
    return lax.optimization_barrier((value,) + after)[0]


def load_rows(dims, p, img, txt, rows):
    rows[0:dims.patches, :] = img[p].astype(F32)
    rows[dims.ip:dims.ip + dims.caption, :] = txt[p].astype(F32)


def spec_whole(a):
    return pl.BlockSpec(a.shape, lambda *_: (0,) * a.ndim)


class Dims(NamedTuple):
    patches: int
    caption: int
    ip: int
    tp: int
    slab: int
    quarter: int
    local: int


GAIN1, SHIFT1, A_SCALE, A_BIAS, GAIN2, SHIFT2, F_SCALE, F_BIAS, H_GAIN, H_SHIFT = 0, 1, 2, 3, 4, 6, 8, 9, 11, 13


def vector(table, at, count=1):
    return table[at:at + count, :]


def copy_rows(dst, at, src, start, count):
    dst[at:at + count, :] = src[start:start + count, :]


def parts_of(dims):
    return 2 * HEAD_DIM, HEAD_DIM


def key_tail(dims, length):
    at = dims.patches // 16 * 16
    return ((0, dims.ip, at, dims.patches), (dims.ip, dims.slab, 0, length))


def hide(scores, start, limit):
    if start >= scores.shape[0]:
        return scores
    tail = scores[start:]
    at = start + lax.broadcasted_iota(jnp.int32, (tail.shape[0], 1), 0)
    tail = jnp.where(at < limit, tail, NEG)
    return tail if start == 0 else jnp.concatenate([scores[:start], tail], axis=0)


def split_pair(value):
    low = lax.broadcasted_iota(jnp.int32, (1, 128), 1) < HEAD_DIM
    zero = jnp.zeros_like(value)
    return jnp.concatenate([jnp.where(low, value, zero), jnp.where(low, zero, value)], axis=0)


def join_pair(value):
    low = lax.broadcasted_iota(jnp.int32, (1, 128), 1) < HEAD_DIM
    half = value.shape[0] // 2
    return jnp.where(low, value[:half], value[half:])


def softmax_keys(scores):
    e = jnp.exp(scores - jnp.max(scores, axis=0, keepdims=True))
    return e * (1.0 / jnp.sum(e, axis=0, keepdims=True))


def pair_weights(q, k, start, limit):
    return softmax_keys(hide(dot_t(k, split_pair(q)), start, limit))


def scaled(q):
    return q * jnp.asarray(HEAD_DIM ** -0.5, BF16)


def attend_tiles(dims, lens, quarter_at, qkv, mixed):
    tiles = mixed.shape[-1] // 128

    def one_pair(p, c):
        length = lens[quarter_at * dims.quarter + p]
        for lo, hi, start, limit in key_tail(dims, length):
            for g in range(tiles):
                q, k, v = [qkv[p, lo:hi, (t * tiles + g) * 128:(t * tiles + g + 1) * 128] for t in range(3)]
                w = pair_weights(scaled(q), k, start, limit).astype(BF16)
                mixed[p, lo:hi, g * 128:(g + 1) * 128] = join_pair(t_dot(w, v)).astype(BF16)
        return c

    lax.fori_loop(0, dims.quarter, one_pair, 0)


def attend_own_kernel(dims, order, lens, img, txt, vec, bias, wo, normed, qkv, rest, mixed, rows, w, b):
    i = pl.program_id(0)
    local = dims.local
    two, one_head = parts_of(dims)

    @pl.when(i == 0)
    def _():
        rows[...] = jnp.zeros_like(rows)
        w[...] = jnp.zeros_like(w)
        b[...] = jnp.zeros_like(b)
        for t in range(3):
            copy_rows(w, t * 2 * two, wo, t * local, local)
        b[0:1, 0:local] = bias[0:1, :]
        b[0:1, 4 * two:4 * two + local] = bias[1:2, :]

    def one_norm(p, c):
        load_rows(dims, p, img, txt, rows)
        n, _ = normalise(rows[...])
        normed[p] = (n * vector(vec, GAIN1) + vector(vec, SHIFT1)).astype(BF16)
        return c

    lax.fori_loop(0, dims.quarter, one_norm, 0)
    model = normed.shape[-1]
    proj = (dot_t(normed[...].reshape(dims.quarter * dims.slab, model), w[...]) + b[0:1, :]).astype(BF16)
    proj = proj.reshape(dims.quarter, dims.slab, 6 * two)
    for t in range(3):
        qkv[:, :, t * two:(t + 1) * two] = proj[:, :, 2 * t * two:(2 * t + 1) * two]
        rest[:, :, t * two:(t + 1) * two] = proj[:, :, (2 * t + 1) * two:(2 * t + 2) * two]
    attend_tiles(dims, lens, order[i], qkv, mixed)


def attend_own(dims, order, lens, img, txt, vec, bias, wo):
    model = img.shape[-1]
    pairs = 4 * dims.quarter
    block = lambda cols: pl.BlockSpec((dims.quarter, dims.slab, cols), lambda i, o, n: (i, 0, 0))
    shape = lambda cols: jax.ShapeDtypeStruct((pairs, dims.slab, cols), BF16)
    return pl.pallas_call(
        functools.partial(attend_own_kernel, dims),
        grid_spec=pltpu.PrefetchScalarGridSpec(
            num_scalar_prefetch=2,
            grid=(4,),
            in_specs=[
                pl.BlockSpec((dims.quarter, dims.patches, model), lambda i, o, n: (o[i], 0, 0)),
                pl.BlockSpec((dims.quarter, dims.caption, model), lambda i, o, n: (o[i], 0, 0)),
                spec_whole(vec), spec_whole(bias), spec_whole(wo),
            ],
            out_specs=[block(model), block(384), block(384), block(128)],
            scratch_shapes=[pltpu.VMEM((dims.slab, model), F32), pltpu.VMEM((768, model), BF16),
                            pltpu.VMEM((8, 768), F32)],
        ),
        out_shape=[shape(model), shape(384), shape(384), shape(128)],
        compiler_params=params(),
        cost_estimate=pl.CostEstimate(
            flops=1536 * pairs * dims.slab * model, bytes_accessed=30_000_000, transcendentals=0),
        name="attend_own",
    )(order, lens, img, txt, vec, bias, wo)


def attend_far_kernel(dims, order, lens, normed, rest, own, bias, wo, wf, qkv, mixed, keep, send, w, ow, b):
    i = pl.program_id(0)
    local = dims.local
    two, one_head = parts_of(dims)
    count = dims.quarter * dims.slab
    model = normed.shape[-1]

    @pl.when(i == 0)
    def _():
        w[...] = jnp.zeros_like(w)
        b[...] = jnp.zeros_like(b)
        for t in range(3):
            copy_rows(w, t * 2 * two, wf, t * local, two)
            copy_rows(w, t * 2 * two + two + one_head, wf, t * local + two, one_head)
        for t, at in ((0, 0), (1, 4 * two)):
            b[0:1, at:at + two] = bias[t:t + 1, 0:two]
            b[0:1, at + two + one_head:at + 2 * two] = bias[t:t + 1, two:]
        copy_rows(ow, 0, wo, 3 * local, two)
        copy_rows(ow, two, wf, 3 * local, two)
        copy_rows(ow, 2 * two, wo, 3 * local + two, one_head)
        copy_rows(ow, 2 * two + one_head, wf, 3 * local + two, one_head)

    proj = (dot_t(normed[...].reshape(count, model), w[...]) + b[0:1, :]).astype(BF16)
    proj = proj.reshape(dims.quarter, dims.slab, 6 * two)
    for t in range(3):
        at = 2 * t * two
        qkv[:, :, at:at + two] = proj[:, :, at:at + two]
        qkv[:, :, at + two:at + 2 * two] = proj[:, :, at + two:at + 2 * two] + rest[:, :, t * two:(t + 1) * two]
    attend_tiles(dims, lens, order[(i + 2) % 4], qkv, mixed)
    part = dot(own[...].reshape(count, two), ow[0:two, :])
    part = part + dot(mixed[...].reshape(count, 2 * two), ow[two:, :])
    part = part.astype(BF16).reshape(dims.quarter, dims.slab, model)

    @pl.when(i < 2)
    def _():
        send[...] = part

    @pl.when(i >= 2)
    def _():
        keep[...] = part


def attend_far(dims, order, lens, normed, rest, own, bias, wo, wf):
    model = normed.shape[-1]
    pairs = 4 * dims.quarter
    at = lambda i: (i + 2) % 4
    block = lambda cols, f: pl.BlockSpec((dims.quarter, dims.slab, cols), lambda i, o, n: (f(i), 0, 0))
    shape = lambda count, cols: jax.ShapeDtypeStruct((count, dims.slab, cols), BF16)
    return pl.pallas_call(
        functools.partial(attend_far_kernel, dims),
        grid_spec=pltpu.PrefetchScalarGridSpec(
            num_scalar_prefetch=2,
            grid=(4,),
            in_specs=[
                block(model, at), block(384, at), block(128, at),
                spec_whole(bias), spec_whole(wo), spec_whole(wf),
            ],
            out_specs=[
                block(768, at), block(256, at),
                block(model, lambda i: jnp.maximum(i - 2, 0)), block(model, lambda i: jnp.minimum(i, 1)),
            ],
            scratch_shapes=[pltpu.VMEM((768, model), BF16), pltpu.VMEM((384, model), BF16),
                            pltpu.VMEM((8, 768), F32)],
        ),
        out_shape=[
            shape(pairs, 768), shape(pairs, 256),
            shape(2 * dims.quarter, model), shape(2 * dims.quarter, model),
        ],
        compiler_params=params(),
        cost_estimate=pl.CostEstimate(
            flops=2304 * pairs * dims.slab * model, bytes_accessed=30_000_000, transcendentals=0),
        name="attend_far",
    )(order, lens, normed, rest, own, bias, wo, wf)


def residual_kernel(dims, order, keep, recv, img, txt, vec, attended, attn, expert, cls, rows):
    i = pl.program_id(0)
    ip = dims.ip

    @pl.when(i == 0)
    def _():
        rows[...] = jnp.zeros_like(rows)
        cls[...] = jnp.zeros_like(cls)

    load_rows(dims, 0, img, txt, rows)
    a = keep[0].astype(F32) + recv[0].astype(F32)
    x = rows[...] + vector(vec, A_SCALE) * (a + vector(vec, A_BIAS))
    n, _ = normalise(x)
    e_img = n[0:ip] * vector(vec, GAIN2) + vector(vec, SHIFT2)
    e_txt = n[ip:] * vector(vec, GAIN2 + 1) + vector(vec, SHIFT2 + 1)
    expert[0, 0:ip, :] = e_img.astype(BF16)
    expert[0, ip:, :] = e_txt.astype(BF16)
    for j, v in enumerate((x[0:1], x[ip:ip + 1], e_img[0:1], e_txt[0:1])):
        cls[j, pl.ds(i, 1), :] = v

    @pl.when(i < dims.quarter)
    def _():
        attended[0] = x
        attn[0] = a


def residual(dims, order, keep, recv, img, txt, vec):
    model = img.shape[-1]
    quarter = dims.quarter
    block = pl.BlockSpec((1, dims.slab, model), lambda i, o: (i, 0, 0))
    pair = lambda i, o: (o[i // quarter] * quarter + i % quarter, 0, 0)
    return pl.pallas_call(
        functools.partial(residual_kernel, dims),
        grid_spec=pltpu.PrefetchScalarGridSpec(
            num_scalar_prefetch=1,
            grid=(2 * quarter,),
            in_specs=[
                block, block,
                pl.BlockSpec((1, dims.patches, model), pair),
                pl.BlockSpec((1, dims.caption, model), pair),
                spec_whole(vec),
            ],
            out_specs=[
                pl.BlockSpec((1, dims.slab, model), lambda i, o: (jnp.minimum(i, quarter - 1), 0, 0)),
                pl.BlockSpec((1, dims.slab, model), lambda i, o: (jnp.minimum(i, quarter - 1), 0, 0)),
                block,
                pl.BlockSpec((4, 8, model), lambda i, o: (0, 0, 0)),
            ],
            scratch_shapes=[pltpu.VMEM((dims.slab, model), F32)],
        ),
        out_shape=[
            jax.ShapeDtypeStruct((quarter, dims.slab, model), F32),
            jax.ShapeDtypeStruct((quarter, dims.slab, model), F32),
            jax.ShapeDtypeStruct((2 * quarter, dims.slab, model), BF16),
            jax.ShapeDtypeStruct((4, 8, model), F32),
        ],
        compiler_params=params(),
        cost_estimate=pl.CostEstimate(flops=40_000_000, bytes_accessed=20_000_000, transcendentals=0),
        name="residual",
    )(order, keep, recv, img, txt, vec)


def expert_kernel(dims, seq, peer, own, img, txt, vec, up, up_bias, down,
                  act, dup, ddown, d_send, d_keep, x_send, x_keep, bias_grad, cot, ins, rows):
    ip, slab, quarter = dims.ip, dims.slab, dims.quarter
    i = pl.program_id(0)
    model = own.shape[-1]

    @pl.when(i == 0)
    def _():
        rows[...] = jnp.zeros_like(rows)
        bias_grad[...] = jnp.zeros_like(bias_grad)
        cot[...] = jnp.zeros_like(cot)
        ins[...] = peer[...]

    @pl.when(i == 1)
    def _():
        ins[...] = own[...]

    at = lax.broadcasted_iota(jnp.int32, (slab, 1), 0)
    inner = (at != 0) & (at != ip)

    def one(p, c):
        load_rows(dims, p, img, txt, rows)
        cot[0, pl.ds(8 * i + p, 1), :] = rows[0:1, :]
        cot[1, pl.ds(8 * i + p, 1), :] = rows[ip:ip + 1, :]
        ddown[p] = jnp.where(inner, rows[...] * vector(vec, F_SCALE), 0.0).astype(BF16)
        return c

    lax.fori_loop(0, quarter, one, 0)
    for m, lo, hi in ((0, 0, ip), (1, ip, slab)):
        count = quarter * (hi - lo)
        e = ins[:, lo:hi, :].reshape(count, model)
        u = dot(e, up[m]) + up_bias[m:m + 1]
        big, small = gelu_parts(u)
        a = (u * big).astype(BF16)
        act[:, lo:hi, :] = a.reshape(quarter, hi - lo, -1)
        slope = big + u * small
        d = dot(a, down[m]).astype(BF16).reshape(quarter, hi - lo, model)
        g = ddown[:, lo:hi, :].reshape(count, model)
        du = dot_t(g, down[m]) * slope
        bias_grad[m:m + 1, :] += jnp.sum(du, axis=0, keepdims=True)
        low = du.astype(BF16)
        dup[:, lo:hi, :] = low.reshape(quarter, hi - lo, -1)
        x = dot_t(low, up[m]).astype(BF16).reshape(quarter, hi - lo, model)

        @pl.when(i == 0)
        def _():
            d_send[:, lo:hi, :] = d
            x_send[:, lo:hi, :] = x

        @pl.when(i == 1)
        def _():
            d_keep[:, lo:hi, :] = d
            x_keep[:, lo:hi, :] = x


def experts(dims, name, half, seq, peer, own, img, txt, vec, up, up_bias, down):
    model = own.shape[-1]
    hidden = up.shape[-1]
    slab, quarter = dims.slab, dims.quarter
    fixed = pl.BlockSpec((quarter, slab, model), lambda i, o: (half, 0, 0))
    first = pl.BlockSpec((quarter, slab, model), lambda i, o: (0, 0, 0))
    step = lambda cols: pl.BlockSpec((quarter, slab, cols), lambda i, o: (i, 0, 0))
    shape = lambda n, cols: jax.ShapeDtypeStruct((n * quarter, slab, cols), BF16)
    return pl.pallas_call(
        functools.partial(expert_kernel, dims),
        grid_spec=pltpu.PrefetchScalarGridSpec(
            num_scalar_prefetch=1,
            grid=(2,),
            in_specs=[
                fixed, fixed,
                pl.BlockSpec((quarter, dims.patches, model), lambda i, o: (o[i], 0, 0)),
                pl.BlockSpec((quarter, dims.caption, model), lambda i, o: (o[i], 0, 0)),
                spec_whole(vec), spec_whole(up), spec_whole(up_bias), spec_whole(down),
            ],
            out_specs=[
                step(hidden), step(hidden), step(model),
                first, first, first, first,
                pl.BlockSpec((2, hidden), lambda i, o: (0, 0)),
                pl.BlockSpec((2, 16, model), lambda i, o: (0, 0, 0)),
            ],
            scratch_shapes=[pltpu.VMEM((quarter, slab, model), BF16), pltpu.VMEM((slab, model), F32)],
        ),
        out_shape=[
            shape(2, hidden), shape(2, hidden), shape(2, model),
            shape(1, model), shape(1, model), shape(1, model), shape(1, model),
            jax.ShapeDtypeStruct((2, hidden), F32),
            jax.ShapeDtypeStruct((2, 16, model), F32),
        ],
        compiler_params=params(),
        cost_estimate=pl.CostEstimate(
            flops=16 * quarter * slab * model * hidden, bytes_accessed=20_000_000, transcendentals=0),
        name=name,
    )(seq, peer, own, img, txt, vec, up, up_bias, down)


def expert_grads_kernel(dims, peer, own, act_a, dup_a, ddn_a, act_b, dup_b, ddn_b, ce, ca, cu, cd, out, acc):
    i = pl.program_id(0)

    def add(e, dup, ddn, act):
        for m, lo, hi in ((0, 0, dims.ip), (1, dims.ip, dims.slab)):
            count = dims.quarter * (hi - lo)
            flat = lambda ref: ref[:, lo:hi, :].reshape(count, -1)
            acc[m] += t_dot(flat(e), flat(dup))
            acc[2 + m] += t_dot(flat(ddn), flat(act))

    @pl.when(i == 0)
    def _():
        for m in range(2):
            acc[m] = t_dot(ce[m], cu[m])
            acc[2 + m] = t_dot(cd[m], ca[m])

    for j, refs in enumerate((
        (peer, dup_a, ddn_a, act_a), (own, dup_a, ddn_a, act_a),
        (peer, dup_b, ddn_b, act_b), (own, dup_b, ddn_b, act_b),
    )):
        @pl.when(i == j)
        def _():
            add(*refs)

    @pl.when(i == 3)
    def _():
        out[...] = acc[...].astype(BF16)


def expert_grads(dims, peer, own, act_a, dup_a, ddn_a, act_b, dup_b, ddn_b, ce, ca, cu, cd):
    model = own.shape[-1]
    hidden = act_a.shape[-1]
    slab, quarter = dims.slab, dims.quarter
    assert hidden == model
    half = pl.BlockSpec((quarter, slab, model), lambda i: (jnp.where(i < 2, 1, 0), 0, 0))
    first = pl.BlockSpec((quarter, slab, hidden), lambda i: (jnp.minimum(i, 1), 0, 0))
    last = pl.BlockSpec((quarter, slab, hidden), lambda i: (jnp.maximum(i - 2, 0), 0, 0))
    return pl.pallas_call(
        functools.partial(expert_grads_kernel, dims),
        grid=(4,),
        in_specs=[half, half, first, first, first, last, last, last] + [spec_whole(v) for v in (ce, ca, cu, cd)],
        out_specs=pl.BlockSpec((4, model, hidden), lambda i: (0, 0, 0)),
        scratch_shapes=[pltpu.VMEM((4, model, hidden), F32)],
        out_shape=jax.ShapeDtypeStruct((4, model, hidden), BF16),
        compiler_params=params(),
        cost_estimate=pl.CostEstimate(
            flops=16 * quarter * slab * model * hidden, bytes_accessed=40_000_000, transcendentals=0),
        name="expert_grads",
    )(peer, own, act_a, dup_a, ddn_a, act_b, dup_b, ddn_b, ce, ca, cu, cd)


def own_row(dims, r, p):
    return 8 * (r // 2) + dims.quarter * (r % 2) + p


def class_forward_kernel(dims, near, far, up, up_bias, down, out, rows):
    for m in range(2):
        e = jnp.concatenate([near[2 + m], far[2 + m]], axis=0).astype(BF16)
        rows[m] = e
        u = dot(e, up[m]) + up_bias[m:m + 1]
        out[m] = dot(gelu_low(u), down[m])


def class_forward(dims, near, far, up, up_bias, down):
    shape = (2, 16, near.shape[-1])
    return pl.pallas_call(
        functools.partial(class_forward_kernel, dims),
        out_shape=[jax.ShapeDtypeStruct(shape, F32), jax.ShapeDtypeStruct(shape, BF16)],
        compiler_params=params(),
        cost_estimate=pl.CostEstimate(flops=200_000_000, bytes_accessed=5_000_000, transcendentals=0),
        name="class_forward",
    )(near, far, up, up_bias, down)


def class_final_kernel(dims, order, near, far, d0, d1, d2, d3, vec, out):
    q = dims.quarter
    for m in range(2):
        out[m] = jnp.zeros(out.shape[1:], F32)
        for r in range(4):
            half, at = (near, far)[r // 2], q * (r % 2)
            for p in range(q):
                rows = [d[m, own_row(dims, s, p):own_row(dims, s, p) + 1, :]
                        for d, s in ((d0, r), (d1, r ^ 2), (d2, r ^ 1), (d3, r ^ 3))]
                total = (rows[0] + rows[1]) + (rows[2] + rows[3])
                x = half[m, at + p:at + p + 1, :] + vector(vec, F_SCALE) * (total + vector(vec, F_BIAS + m))
                out[m, pl.ds(4 * order[r] + p, 1), :] = x


def class_final(dims, order, near, far, parts, vec):
    shape = (2, 16, near.shape[-1])
    args = (near, far) + tuple(parts) + (vec,)
    return pl.pallas_call(
        functools.partial(class_final_kernel, dims),
        grid_spec=pltpu.PrefetchScalarGridSpec(
            num_scalar_prefetch=1, grid=(1,),
            in_specs=[spec_whole(v) for v in args],
            out_specs=pl.BlockSpec(shape, lambda i, o: (0, 0, 0)),
        ),
        out_shape=jax.ShapeDtypeStruct(shape, F32),
        compiler_params=params(),
        cost_estimate=pl.CostEstimate(flops=1_000_000, bytes_accessed=1_000_000, transcendentals=0),
        name="class_final",
    )(order, *args)


def class_back_kernel(dims, order, e, cot_a, cot_b, dclass, vec, up, up_bias, down,
                      act, dup, ddown, dexp, bias_grad, dcls, rows):
    q = dims.quarter
    rows[...] = jnp.zeros_like(rows)
    dcls[...] = jnp.zeros_like(dcls)
    for m in range(2):
        for r in range(4):
            cot, base = (cot_b, cot_a)[r % 2], 8 * (1 - r // 2)
            for p in range(q):
                d = dclass[m, pl.ds(4 * order[r] + p, 1), :]
                at = own_row(dims, r, p)
                rows[m, at:at + 1, :] = cot[m, base + p:base + p + 1, :] + d
                if r == 0:
                    dcls[p, m:m + 1, :] = d
        u = dot(e[m], up[m]) + up_bias[m:m + 1]
        big, small = gelu_parts(u)
        act[m] = (u * big).astype(BF16)
        g = (rows[m] * vector(vec, F_SCALE)).astype(BF16)
        ddown[m] = g
        du = dot_t(g, down[m]) * (big + u * small)
        bias_grad[m:m + 1, :] = jnp.sum(du, axis=0, keepdims=True)
        low = du.astype(BF16)
        dup[m] = low
        dexp[m] = dot_t(low, up[m])


def class_back(dims, order, e, cot_a, cot_b, dclass, vec, up, up_bias, down):
    hidden, model = up.shape[-1], e.shape[-1]
    args = (e, cot_a, cot_b, dclass, vec, up, up_bias, down)
    shapes = [((2, 16, hidden), BF16), ((2, 16, hidden), BF16), ((2, 16, model), BF16), ((2, 16, model), F32),
              ((2, hidden), F32), ((dims.quarter, 8, model), F32)]
    return pl.pallas_call(
        functools.partial(class_back_kernel, dims),
        grid_spec=pltpu.PrefetchScalarGridSpec(
            num_scalar_prefetch=1, grid=(1,),
            in_specs=[spec_whole(v) for v in args],
            out_specs=[pl.BlockSpec(s, lambda i, o, n=len(s): (0,) * n) for s, _ in shapes],
            scratch_shapes=[pltpu.VMEM((2, 16, model), F32)],
        ),
        out_shape=[jax.ShapeDtypeStruct(s, t) for s, t in shapes],
        compiler_params=params(),
        cost_estimate=pl.CostEstimate(flops=300_000_000, bytes_accessed=5_000_000, transcendentals=0),
        name="class_back",
    )(order, *args)


def contrast_kernel(dims, total, at, blocks, vec, weight, scale,
                    head_in, dproj, dcls, gains, shifts, scalars, cls, back):
    me = at[0]
    span = blocks[0].shape[0]
    for k, block in enumerate(blocks):
        for j in range(span):
            for m in range(2):
                cls[m, pl.ds(pl.multiple_of(16 * (me ^ (k * span + j)), 16), 16), :] = block[j, m]
    n_rows = cls.shape[1]
    sharp = jnp.exp(scale[...])
    col_at = lax.broadcasted_iota(jnp.int32, (1, n_rows), 1)
    row_at = lax.broadcasted_iota(jnp.int32, (n_rows, 1), 0)
    col_ok = (col_at % 4) < dims.quarter
    row_ok = (row_at % 4) < dims.quarter
    normal, inverse, proj, unit, embed = [], [], [], [], []
    for m in range(2):
        n, r = normalise(cls[m])
        h = (n * vector(vec, H_GAIN + m) + vector(vec, H_SHIFT + m)).astype(BF16)
        head_in[m] = h
        y = dot(h, weight[m])
        u = lax.rsqrt(jnp.sum(y * y, axis=-1, keepdims=True) + 1e-6)
        normal.append(n)
        inverse.append(r)
        proj.append(y)
        unit.append(u)
        embed.append((y * u).astype(BF16))
    ok = row_ok & col_ok
    logits = sharp * dot_t(embed[0], embed[1])
    masked = jnp.where(ok, logits, -1e30)
    row_max = jnp.max(masked, axis=1, keepdims=True)
    row_lse = row_max + jnp.log(jnp.sum(jnp.exp(masked - row_max), axis=1, keepdims=True))
    col_max = jnp.max(masked, axis=0, keepdims=True)
    col_lse = col_max + jnp.log(jnp.sum(jnp.exp(masked - col_max), axis=0, keepdims=True))
    same = (row_at == col_at) & ok
    both = jnp.exp(masked - row_lse) + jnp.exp(masked - col_lse)
    dlogits = jnp.where(ok, jnp.where(same, both - 2.0, both) * (1.0 / (2 * total)), 0.0)
    diagonal = jnp.sum(jnp.where(same, logits, 0.0), axis=1, keepdims=True)
    rows = jnp.where(row_ok, row_lse - 2.0 * diagonal, 0.0)
    cols = jnp.where(col_ok, col_lse, 0.0)
    loss = (jnp.sum(rows, axis=0, keepdims=True) + jnp.sum(cols, axis=1, keepdims=True)) * (1.0 / (2 * total))
    slope = jnp.sum(jnp.sum(dlogits * logits, axis=1, keepdims=True), axis=0, keepdims=True)
    scalars[0:1, :] = jnp.broadcast_to(loss, (1, 128))
    scalars[1:2, :] = jnp.broadcast_to(slope, (1, 128))
    high = lax.Precision.HIGHEST
    wide = [e.astype(F32) for e in embed]
    dembed = [
        sharp * jnp.dot(dlogits, wide[1], precision=high, preferred_element_type=F32),
        sharp * lax.dot_general(dlogits, wide[0], (((0,), (0,)), ((), ())), precision=high,
                                preferred_element_type=F32),
    ]
    for m in range(2):
        u, y, d = unit[m], proj[m], dembed[m]
        dp = (u * d - u * u * u * y * jnp.sum(y * d, axis=-1, keepdims=True)).astype(BF16)
        dproj[m] = dp
        dh = dot_t(dp, weight[m])
        gains[m:m + 1, :] = jnp.sum(dh * normal[m], axis=0, keepdims=True)
        shifts[m:m + 1, :] = jnp.sum(dh, axis=0, keepdims=True)
        back[m] = norm_back(normal[m], inverse[m], dh * vector(vec, H_GAIN + m))
        dcls[m] = back[m, pl.ds(pl.multiple_of(16 * me, 16), 16), :]


def contrast(dims, total, at, blocks, vec, weight, scale):
    model = weight.shape[1]
    rows = 16 * len(blocks) * blocks[0].shape[0]
    args = tuple(blocks) + (vec, weight, scale)
    shapes = [((2, rows, model), BF16), ((2, rows, weight.shape[2]), BF16), ((2, 16, model), F32),
              ((2, model), F32), ((2, model), F32), ((2, 128), F32)]

    def kernel(at, *refs):
        contrast_kernel(dims, total, at, refs[:len(blocks)], *refs[len(blocks):])

    return pl.pallas_call(
        kernel,
        grid_spec=pltpu.PrefetchScalarGridSpec(
            num_scalar_prefetch=1, grid=(1,),
            in_specs=[spec_whole(v) for v in args],
            out_specs=[pl.BlockSpec(s, lambda i, o, n=len(s): (0,) * n) for s, _ in shapes],
            scratch_shapes=[pltpu.VMEM((2, rows, model), F32)] * 2,
        ),
        out_shape=[jax.ShapeDtypeStruct(s, t) for s, t in shapes],
        compiler_params=params(),
        cost_estimate=pl.CostEstimate(flops=1_000_000_000, bytes_accessed=5_000_000, transcendentals=0),
        name="contrast",
    )(at, *args)


def contrast_large(dims, total, at, blocks, vec, weight, scale):
    model = weight.shape[1]
    held = jnp.concatenate(blocks)
    held = held[jnp.arange(held.shape[0]) ^ at[0]]
    rows = jnp.asarray([r for r in range(16) if r % 4 < dims.quarter])
    cls = jnp.transpose(held[:, :, rows], (1, 0, 2, 3)).reshape(2, -1, model)
    gain, shift = vec[H_GAIN:H_GAIN + 2, None], vec[H_SHIFT:H_SHIFT + 2, None]
    n, r = normalise(cls)
    head_in = (n * gain + shift).astype(BF16)
    proj = jnp.einsum("mrc,mce->mre", head_in, weight, preferred_element_type=F32)
    unit = lax.rsqrt(jnp.sum(proj * proj, axis=-1, keepdims=True) + 1e-6)
    embed = (proj * unit).astype(BF16)
    sharp = jnp.exp(scale[0, 0])
    logits = sharp * dot_t(embed[0], embed[1])
    row_lse = jax.nn.logsumexp(logits, axis=1, keepdims=True)
    col_lse = jax.nn.logsumexp(logits, axis=0, keepdims=True)
    dlogits = jnp.exp(logits - row_lse) + jnp.exp(logits - col_lse) - 2.0 * jnp.eye(total, dtype=F32)
    dlogits = dlogits / (2 * total)
    loss = (jnp.sum(row_lse) + jnp.sum(col_lse) - 2.0 * jnp.trace(logits)) / (2 * total)
    slope = jnp.sum(dlogits * logits)
    high = lax.Precision.HIGHEST
    wide = embed.astype(F32)
    dembed = sharp * jnp.stack([
        jnp.dot(dlogits, wide[1], precision=high, preferred_element_type=F32),
        jnp.dot(dlogits.T, wide[0], precision=high, preferred_element_type=F32)])
    dproj = (unit * dembed - unit ** 3 * proj * jnp.sum(proj * dembed, axis=-1, keepdims=True)).astype(BF16)
    dh = jnp.einsum("mre,mce->mrc", dproj, weight, preferred_element_type=F32)
    back = norm_back(n, r, dh * gain)
    pairs = 4 * dims.quarter
    own = lax.dynamic_slice_in_dim(back, at[0] * pairs, pairs, axis=1)
    dcls = jnp.zeros((2, 16, model), F32).at[:, rows].set(own)
    scalars = jnp.broadcast_to(jnp.stack([loss, slope])[:, None], (2, 128))
    return head_in, dproj, dcls, jnp.sum(dh * n, axis=1), jnp.sum(dh, axis=1), scalars


def own_pair(rows_of):
    return lambda i, o: (o[0] * rows_of + i, 0, 0)


def own_call(kernel, dims, name, order, blocks, img, txt, others, outs, scratch):
    model = img.shape[-1]
    block = pl.BlockSpec((1, dims.slab, model), lambda i, o: (i, 0, 0))
    specs = {
        "slab": (block, (dims.quarter, dims.slab, model)),
        "img": (pl.BlockSpec((1, dims.patches, model), lambda i, o: (i, 0, 0)), (dims.quarter, dims.patches, model)),
        "txt": (pl.BlockSpec((1, dims.caption, model), lambda i, o: (i, 0, 0)), (dims.quarter, dims.caption, model)),
        "sums": (pl.BlockSpec((8, model), lambda i, o: (0, 0)), (8, model)),
    }
    return pl.pallas_call(
        functools.partial(kernel, dims),
        grid_spec=pltpu.PrefetchScalarGridSpec(
            num_scalar_prefetch=1,
            grid=(dims.quarter,),
            in_specs=[block] * len(blocks) + [
                pl.BlockSpec((1, dims.patches, model), own_pair(dims.quarter)),
                pl.BlockSpec((1, dims.caption, model), own_pair(dims.quarter)),
            ] + [spec_whole(v) for v in others],
            out_specs=[specs[kind][0] for kind, _ in outs],
            scratch_shapes=[pltpu.VMEM((dims.slab, model), F32)] * scratch,
        ),
        out_shape=[jax.ShapeDtypeStruct(specs[kind][1], dtype) for kind, dtype in outs],
        compiler_params=params(),
        cost_estimate=pl.CostEstimate(flops=40_000_000, bytes_accessed=15_000_000, transcendentals=0),
        name=name,
    )(order, *blocks, img, txt, *others)


def start_own(rows, sums):
    @pl.when(pl.program_id(0) == 0)
    def _():
        rows[...] = jnp.zeros_like(rows)
        sums[...] = jnp.zeros_like(sums)


def add_class(dims, dcls, rows):
    i = pl.program_id(0)
    rows[0:1, :] += dcls[i, 0:1, :]
    rows[dims.ip:dims.ip + 1, :] += dcls[i, 1:2, :]


def final_kernel(dims, order, keep, recv, far, attended, img, txt, dcls, vec, fin_img, fin_txt, sums, rows):
    start_own(rows, sums)
    load_rows(dims, 0, img, txt, rows)
    add_class(dims, dcls, rows)
    for m, lo, hi in ((0, 0, dims.ip), (1, dims.ip, dims.slab)):
        b = keep[0, lo:hi].astype(F32) + recv[0, lo:hi].astype(F32) + far[0, lo:hi].astype(F32)
        b = b + vector(vec, F_BIAS + m)
        f = attended[0, lo:hi, :] + vector(vec, F_SCALE) * b
        if m == 0:
            fin_img[0] = f[0:dims.patches].astype(BF16)
        else:
            fin_txt[0] = f[0:dims.caption].astype(BF16)
        g = rows[lo:hi, :]
        sums[0:1, :] += jnp.sum(g * b, axis=0, keepdims=True)
        sums[1 + m:2 + m, :] += jnp.sum(g, axis=0, keepdims=True) * vector(vec, F_SCALE)


def final_rows(dims, order, keep, recv, far, attended, img, txt, dcls, vec):
    return own_call(final_kernel, dims, "final_rows", order, (keep, recv, far, attended), img, txt,
                    (dcls, vec), (("img", BF16), ("txt", BF16), ("sums", F32)), 1)


def norm_two_kernel(dims, order, keep, recv, far, attended, a_keep, a_recv, img, txt, dcls, x0, x1, x2, x3,
                    vec, dattended, dattn, sums, rows, ups):
    i = pl.program_id(0)
    start_own(rows, sums)
    load_rows(dims, 0, img, txt, rows)
    add_class(dims, dcls, rows)
    ups[...] = keep[0].astype(F32) + recv[0].astype(F32) + far[0].astype(F32)
    for m, at in ((0, 0), (1, dims.ip)):
        extra = [x[m, pl.ds(own_row(dims, r, 0) + i, 1), :] for x, r in ((x0, 0), (x1, 2), (x2, 1), (x3, 3))]
        ups[at:at + 1, :] += (extra[0] + extra[1]) + (extra[2] + extra[3])
    for m, lo, hi in ((0, 0, dims.ip), (1, dims.ip, dims.slab)):
        n, r = normalise(attended[0, lo:hi, :])
        dy = ups[lo:hi, :]
        sums[m:m + 1, :] += jnp.sum(dy * n, axis=0, keepdims=True)
        sums[2 + m:3 + m, :] += jnp.sum(dy, axis=0, keepdims=True)
        d = rows[lo:hi, :] + norm_back(n, r, dy * vector(vec, GAIN2 + m))
        dattended[0, lo:hi, :] = d
        sd = d * vector(vec, A_SCALE)
        dattn[0, lo:hi, :] = sd.astype(BF16)
        a = a_keep[0, lo:hi, :].astype(F32) + a_recv[0, lo:hi, :].astype(F32) + vector(vec, A_BIAS)
        sums[4:5, :] += jnp.sum(d * a, axis=0, keepdims=True)
        sums[5:6, :] += jnp.sum(sd, axis=0, keepdims=True)


def norm_two(dims, order, keep, recv, far, attended, a_keep, a_recv, img, txt, dcls, parts, vec):
    return own_call(norm_two_kernel, dims, "norm_two", order, (keep, recv, far, attended, a_keep, a_recv), img, txt,
                    (dcls,) + tuple(parts) + (vec,), (("slab", F32), ("slab", BF16), ("sums", F32)), 2)


def norm_one_kernel(dims, order, keep, recv, dattended, img, txt, vec, d_img, d_txt, sums, rows):
    start_own(rows, sums)
    load_rows(dims, 0, img, txt, rows)
    n, r = normalise(rows[...])
    dy = keep[0].astype(F32) + recv[0].astype(F32)
    sums[0:1, :] += jnp.sum(dy * n, axis=0, keepdims=True)
    sums[1:2, :] += jnp.sum(dy, axis=0, keepdims=True)
    d = dattended[0] + norm_back(n, r, dy * vector(vec, GAIN1))
    d_img[0] = d[0:dims.patches].astype(BF16)
    d_txt[0] = d[dims.ip:dims.ip + dims.caption].astype(BF16)


def norm_one(dims, order, keep, recv, dattended, img, txt, vec):
    return own_call(norm_one_kernel, dims, "norm_one", order, (keep, recv, dattended), img, txt,
                    (vec,), (("img", BF16), ("txt", BF16), ("sums", F32)), 1)


def back_step(dims, tiles, lens, whose, dattn, normed, qkv, mixed, dmixed, dqkv, acc, col_sums, w, ow):
    quarter, slab = dims.quarter, dims.slab
    count, width = quarter * slab, tiles * 128
    model = normed.shape[-1]
    d_rows = dattn[...].reshape(count, model)
    dmixed[...] = dot_t(d_rows, ow[...]).astype(BF16).reshape(quarter, slab, width)

    def one_pair(p, c):
        length = lens[whose * quarter + p]
        for lo, hi, start, limit in key_tail(dims, length):
            for g in range(tiles):
                at = [slice((t * tiles + g) * 128, (t * tiles + g + 1) * 128) for t in range(3)]
                q, k, v = [qkv[p, lo:hi, c] for c in at]
                q = scaled(q)
                qq = split_pair(q)
                dd = split_pair(dmixed[p, lo:hi, g * 128:(g + 1) * 128])
                w_ = softmax_keys(hide(dot_t(k, qq), start, limit))
                dw = dot_t(v, dd)
                dqkv[p, lo:hi, at[2]] = dot(w_.astype(BF16), dd).astype(BF16)
                ds = (w_ * (dw - jnp.sum(w_ * dw, axis=0, keepdims=True))).astype(BF16)
                dqkv[p, lo:hi, at[1]] = dot(ds, qq).astype(BF16)
                dqkv[p, lo:hi, at[0]] = (join_pair(t_dot(ds, k)) * HEAD_DIM ** -0.5).astype(BF16)
        return c

    lax.fori_loop(0, quarter, one_pair, 0)
    dp = dqkv[...].reshape(count, 3 * width)
    part = dot(dp, w[...])
    acc[:, 0:3 * width] += t_dot(normed[...].reshape(count, model), dp)
    acc[:, 3 * width:] += t_dot(d_rows, mixed[...].reshape(count, width))
    col_sums[...] += jnp.sum(dp.astype(F32), axis=0, keepdims=True)
    return part


def attend_back_kernel(dims, far, order, lens, d_own, d_peer, normed, qkv, mixed, wq, wo, wf, *refs):
    if not far:
        prior_keep, prior_send, *refs = refs
    keep, send, grad, *refs = refs
    if far:
        grad_rest, *refs = refs
    col_sums, dattn, dmixed, dqkv, acc, w, ow = refs
    i = pl.program_id(0)
    slab, quarter, local = dims.slab, dims.quarter, dims.local
    two, one_head = parts_of(dims)
    tiles = 2 if far else 1
    width = tiles * two
    count = quarter * slab
    model = normed.shape[-1]

    @pl.when(i == 0)
    def _():
        dattn[...] = d_own[...]
        acc[...] = jnp.zeros_like(acc)
        col_sums[...] = jnp.zeros_like(col_sums)
        for t in range(4):
            dst, at = (w, t * width) if t < 3 else (ow, 0)
            own, start = (wq, t * local) if t < 3 else (wo, 0)
            if far:
                copy_rows(dst, at, wf, t * local, two)
                copy_rows(dst, at + two, own, start + two, one_head)
                copy_rows(dst, at + two + one_head, wf, t * local + two, one_head)
            else:
                copy_rows(dst, at, own, start, two)

    @pl.when(i == 1)
    def _():
        dattn[...] = d_peer[...]

    part = back_step(dims, tiles, lens, order[2 * i], dattn, normed, qkv, mixed,
                     dmixed, dqkv, acc, col_sums, w, ow)

    @pl.when(i == 0)
    def _():
        prior = 0.0 if far else prior_keep[...].reshape(count, model).astype(F32)
        keep[...] = (part + prior).astype(BF16).reshape(quarter, slab, model)

    @pl.when(i == 1)
    def _():
        prior = 0.0 if far else prior_send[...].reshape(count, model).astype(F32)
        send[...] = (part + prior).astype(BF16).reshape(quarter, slab, model)
        for t in range(4):
            grad[:, t * two:(t + 1) * two] = acc[:, t * width:t * width + two].astype(BF16)
            if far:
                at = t * width + two
                to = 4 * two + t * one_head
                grad[:, to:to + one_head] = acc[:, at + one_head:at + two].astype(BF16)
                grad_rest[:, t * one_head:(t + 1) * one_head] = acc[:, at:at + one_head].astype(BF16)


def attend_back(dims, far, order, lens, d_own, d_peer, normed, qkv, mixed, wq, wo, wf, prior=()):
    model = normed.shape[-1]
    slab, quarter = dims.slab, dims.quarter
    width = 256 if far else 128
    one = pl.BlockSpec((quarter, slab, model), lambda i, o, n: (0, 0, 0))
    stride = normed.shape[0] // (2 * quarter)
    step = lambda cols: pl.BlockSpec((quarter, slab, cols), lambda i, o, n: (stride * i, 0, 0))
    grads = (768, 256) if far else (512,)
    specs = [one, one] + [pl.BlockSpec((model, n), lambda i, o, n_: (0, 0)) for n in grads]
    specs += [pl.BlockSpec((1, 3 * width), lambda i, o, n: (0, 0))]
    shapes = [
        jax.ShapeDtypeStruct((quarter, slab, model), BF16),
        jax.ShapeDtypeStruct((quarter, slab, model), BF16),
    ] + [jax.ShapeDtypeStruct((model, n), BF16) for n in grads] + [jax.ShapeDtypeStruct((1, 3 * width), F32)]
    scratch = [
        pltpu.VMEM((quarter, slab, model), BF16),
        pltpu.VMEM((quarter, slab, width), BF16),
        pltpu.VMEM((quarter, slab, 3 * width), BF16),
        pltpu.VMEM((model, 4 * width), F32),
        pltpu.VMEM((3 * width, model), BF16),
        pltpu.VMEM((width, model), BF16),
    ]
    return pl.pallas_call(
        functools.partial(attend_back_kernel, dims, far),
        grid_spec=pltpu.PrefetchScalarGridSpec(
            num_scalar_prefetch=2,
            grid=(2,),
            in_specs=[one, one, step(model), step(3 * width), step(width), spec_whole(wq), spec_whole(wo),
                      spec_whole(wf)] + [one] * len(prior),
            out_specs=specs,
            scratch_shapes=scratch,
        ),
        out_shape=shapes,
        compiler_params=params(),
        cost_estimate=pl.CostEstimate(
            flops=32 * quarter * slab * model * width, bytes_accessed=20_000_000, transcendentals=0),
        name="attend_back_far" if far else "attend_back_own",
    )(order, lens, d_own, d_peer, normed, qkv, mixed, wq, wo, wf, *prior)


def swap(value, axis, bit):
    size = lax.axis_size(axis)
    return lax.ppermute(value, axis, [(j, j ^ bit) for j in range(size)])


def to_core(value):
    return swap(value, "mp", 1)


def to_y(value):
    return swap(value, "mp", 2)


def from_others(value, axis, first, count):
    return [value] + [swap(value, axis, k * first) for k in range(1, count)]


def add_tree(parts):
    while len(parts) > 1:
        parts = [a + b for a, b in zip(parts[::2], parts[1::2])]
    return parts[0]


def sum_over(value, axis):
    first = 1
    while first < lax.axis_size(axis):
        count = min(8, lax.axis_size(axis) // first)
        value = add_tree(from_others(value, axis, first, count))
        first *= count
    return value


def gather_batch(value):
    parts = [value]
    first = 1
    size = lax.axis_size("batch")
    while first < size:
        count = min(8, size // first)
        whole = jnp.concatenate(parts) if len(parts) > 1 else parts[0]
        parts = from_others(whole, "batch", first, count)
        first *= count
    return parts


def gather_rows(own, me):
    near = jnp.stack([own, to_y(own)])
    far = to_core(near)
    out = jnp.zeros((4,) + own.shape, own.dtype)
    for r, value in enumerate((near[0], near[1], far[0], far[1])):
        out = lax.dynamic_update_slice(out, value[None], (me ^ ORDER[r],) + (0,) * own.ndim)
    return out.reshape((4 * own.shape[0],) + own.shape[1:])


def add_low(a, b):
    return (a.astype(F32) + b.astype(F32)).astype(BF16)


MESH = pl.DeviceIdType.MESH


class Place:
    def __init__(self):
        self.b, self.m = lax.axis_index("batch"), lax.axis_index("mp")
        self.z, self.x = self.b // 2, self.b % 2
        self.y, self.c = self.m // 2, self.m % 2
        self.core = (self.b, 2 * self.y + 1 - self.c)
        self.near = (self.b, 2 * (1 - self.y) + self.c)
        self.across = (self.b, 2 * (1 - self.y) + 1 - self.c)
        self.side = (2 * self.z + 1 - self.x, self.m)
        self.z_pair = self.z + 1 - 2 * (self.z % 2)
        self.z_far = (self.z + 2) % 4
        self.z_rest = (self.z_pair + 2) % 4
        self.paired = (2 * self.z_pair + self.x, self.m)
        self.opposite = (2 * self.z_far + self.x, self.m)
        self.batch = [((self.b + k) % 8, self.m) for k in range(1, 8)]

    def quarter(self, far_y, far_core):
        return 2 * ((self.y + far_y) % 2) + (self.c + far_core) % 2


def meet(peers):
    barrier = pltpu.get_barrier_semaphore()
    for peer in peers:
        pl.semaphore_signal(barrier, inc=1, device_id=peer, device_id_type=MESH)
    pl.semaphore_wait(barrier, len(peers))


def remote(src, dst, send_sem, recv_sem, at, device):
    return pltpu.make_async_remote_copy(
        src_ref=src, dst_ref=dst, send_sem=send_sem.at[at], recv_sem=recv_sem.at[at],
        device_id=device, device_id_type=MESH)


def front_kernel(dims, lens, img, txt, vectors, bias, own_w, own_o,
                 vec, normed, qkv, mixed, qkv_far, mixed_far, far_w, attended, attn, expert, expert_peer, cls, cls_peer,
                 rows, w, w2, ow, b, wf, far_bias, n_all, rest, m_all, m_far, q_own, q_far, a_send, a_recv, e_send, c_recv, held,
                 local_sem, send_sem, recv_sem):
    here = Place()
    i = pl.program_id(0)
    local, quarter, slab, ip = dims.local, dims.quarter, dims.slab, dims.ip
    two, one_head = parts_of(dims)
    count = quarter * slab
    model = img.shape[-1]
    at = i % 4
    whose = here.quarter(at % 2, 1 - at // 2)
    sent_w = [remote(own_w, wf.at[pl.ds(0, 3 * local)], send_sem, recv_sem, 0, here.near),
              remote(own_o, wf.at[pl.ds(3 * local, local)], send_sem, recv_sem, 1, here.near),
              remote(bias, far_bias, send_sem, recv_sem, 2, here.near)]
    sent_a = [remote(a_send.at[j], a_recv.at[j], send_sem, recv_sem, 3 + j, here.core) for j in range(2)]

    def e_over(j):
        return remote(e_send.at[j], expert_peer.at[j], send_sem, recv_sem, 5 + j, here.core)

    def e_here(j):
        return pltpu.make_async_copy(e_send.at[j], expert.at[j], local_sem.at[1 + j])

    sent_c = remote(cls, c_recv, send_sem, recv_sem, 5 + 2 * quarter, here.core)
    keep_w = pltpu.make_async_copy(wf, far_w, local_sem.at[0])
    sent_e = [e_over(j) for j in range(2 * quarter)]
    keep_e = [e_here(j) for j in range(2 * quarter)]

    @pl.when(i == 0)
    def _():
        meet([here.core, here.near])
        for copy in sent_w:
            copy.start()
        fill(vec, vectors)
        rows[...] = jnp.zeros_like(rows)
        b[...] = jnp.zeros_like(b)
        w[...] = jnp.zeros_like(w)
        cls[...] = jnp.zeros_like(cls)
        for t in range(3):
            copy_rows(w, t * 2 * two, own_w, t * local, local)
        b[0:1, 0:local] = bias[0:1, :]
        b[0:1, 4 * two:4 * two + local] = bias[1:2, :]

    def project(weights):
        proj = dot_t(n_all[at].reshape(count, model), weights[...]) + b[0:1, :]
        return proj.astype(BF16).reshape(quarter, slab, 6 * two)

    @pl.when(i < 4)
    def _():
        def one_norm(p, c):
            load_rows(dims, p, img, txt, rows)
            n, _ = normalise(rows[...])
            n_all[at, p] = (n * vector(vec, GAIN1) + vector(vec, SHIFT1)).astype(BF16)
            return c

        lax.fori_loop(0, quarter, one_norm, 0)
        proj = project(w)
        for t in range(3):
            q_own[:, :, t * two:(t + 1) * two] = proj[:, :, 2 * t * two:(2 * t + 1) * two]
            rest[at, :, :, t * two:(t + 1) * two] = proj[:, :, (2 * t + 1) * two:(2 * t + 2) * two]
        attend_tiles(dims, lens, whose, q_own, m_all.at[at])

        @pl.when(i % 2 == 0)
        def _():
            normed[...] = n_all[at]
            qkv[...] = q_own[...]
            mixed[...] = m_all[at]

    @pl.when(i == 4)
    def _():
        for copy in sent_w:
            copy.wait_recv()
        keep_w.start()
        w2[...] = jnp.zeros_like(w2)
        b[...] = jnp.zeros_like(b)
        for t in range(3):
            copy_rows(w2, t * 2 * two, wf, t * local, two)
            copy_rows(w2, t * 2 * two + two + one_head, wf, t * local + two, one_head)
        for t, to in ((0, 0), (1, 4 * two)):
            b[0:1, to:to + two] = far_bias[t:t + 1, 0:two]
            b[0:1, to + two + one_head:to + 2 * two] = far_bias[t:t + 1, two:]
        copy_rows(ow, 0, own_o, 0, two)
        copy_rows(ow, two, wf, 3 * local, two)
        copy_rows(ow, 2 * two, own_o, two, one_head)
        copy_rows(ow, 2 * two + one_head, wf, 3 * local + two, one_head)

    @pl.when(i >= 4)
    def _():
        proj = project(w2)
        for t in range(3):
            to = 2 * t * two
            q_far[:, :, to:to + two] = proj[:, :, to:to + two]
            q_far[:, :, to + two:to + 2 * two] = (
                proj[:, :, to + two:to + 2 * two] + rest[at, :, :, t * two:(t + 1) * two])
        attend_tiles(dims, lens, whose, q_far, m_far)

        @pl.when(i % 2 == 0)
        def _():
            qkv_far[...] = q_far[...]
            mixed_far[...] = m_far[...]

        part = dot(m_all[at].reshape(count, two), ow[0:two, :])
        part = part + dot(m_far[...].reshape(count, 2 * two), ow[two:, :])
        part = part.reshape(quarter, slab, model)

        @pl.when(i < 6)
        def _():
            a_send[at] = part.astype(BF16)

        for j in range(2):
            @pl.when(i == 4 + j)
            def _():
                sent_a[j].start()

        for j in range(2):
            @pl.when(i == 6 + j)
            def _():
                sent_a[j].wait_recv()

        @pl.when(i >= 6)
        def _():
            j = i - 6
            held[...] = part

            def one_residual(p, c):
                load_rows(dims, p, img, txt, rows)
                a = held[p] + a_recv[j, p].astype(F32)
                x = rows[...] + vector(vec, A_SCALE) * (a + vector(vec, A_BIAS))
                n, _ = normalise(x)
                e_img = n[0:ip] * vector(vec, GAIN2) + vector(vec, SHIFT2)
                e_txt = n[ip:] * vector(vec, GAIN2 + 1) + vector(vec, SHIFT2 + 1)
                r = j * quarter + p
                e_send[r, 0:ip, :] = e_img.astype(BF16)
                e_send[r, ip:, :] = e_txt.astype(BF16)
                e_over(r).start()
                e_here(r).start()
                for k, v in enumerate((x[0:1], x[ip:ip + 1], e_img[0:1], e_txt[0:1])):
                    cls[k, pl.ds(r, 1), :] = v

                @pl.when(j == 0)
                def _():
                    attended[p] = x
                    attn[p] = a

                return c

            lax.fori_loop(0, quarter, one_residual, 0)

    @pl.when(i == 7)
    def _():
        sent_c.start()
        keep_w.wait()
        for copy in keep_e:
            copy.wait()
        sent_c.wait()
        cls_peer[...] = c_recv[...]
        for copy in sent_e:
            copy.wait()
        for copy in sent_w + sent_a:
            copy.wait_send()


def fill(table, vectors):
    table[...] = jnp.zeros_like(table)
    at = 0
    for v in vectors:
        n = v.shape[0] if len(v.shape) == 2 else 1
        table[at:at + n, :] = v[...].reshape(n, table.shape[1])
        at += n


def front(dims, lens, img, txt, vectors, bias, own_w, own_o):
    model = img.shape[-1]
    quarter, slab, local = dims.quarter, dims.slab, dims.local
    held = pl.BlockSpec(memory_space=pltpu.VMEM)
    away = pl.BlockSpec(memory_space=pl.ANY)

    def states_at(i):
        return Place().quarter(i % 2, 1 - i % 4 // 2), 0, 0

    own_block = lambda cols: pl.BlockSpec((quarter, slab, cols), lambda i: (jnp.where(i < 2, 1, 0), 0, 0))
    far_block = lambda cols: pl.BlockSpec((quarter, slab, cols), lambda i: (jnp.where(i < 6, 1, 0), 0, 0))
    six = lambda cols: jax.ShapeDtypeStruct((2 * quarter, slab, cols), BF16)
    block = lambda cols: (quarter, slab, cols)
    n_remote = 6 + 2 * quarter
    return pl.pallas_call(
        lambda lens, img, txt, *refs: front_kernel(
            dims, lens, img, txt, refs[:len(vectors)], *refs[len(vectors):]),
        grid=(8,),
        in_specs=[pl.BlockSpec(memory_space=pltpu.SMEM),
                  pl.BlockSpec((quarter, dims.patches, model), states_at),
                  pl.BlockSpec((quarter, dims.caption, model), states_at)] + [held] * (3 + len(vectors)),
        out_specs=[held, own_block(model), own_block(384), own_block(128), far_block(768), far_block(256),
                   away, held, held, away, away, held, held],
        out_shape=[jax.ShapeDtypeStruct((16, model), F32), six(model), six(384), six(128), six(768), six(256),
                   jax.ShapeDtypeStruct((4 * local, model), BF16),
                   jax.ShapeDtypeStruct(block(model), F32), jax.ShapeDtypeStruct(block(model), F32),
                   six(model), six(model),
                   jax.ShapeDtypeStruct((4, 8, model), F32), jax.ShapeDtypeStruct((4, 8, model), F32)],
        scratch_shapes=[
            pltpu.VMEM((slab, model), F32), pltpu.VMEM((768, model), BF16), pltpu.VMEM((768, model), BF16),
            pltpu.VMEM((384, model), BF16), pltpu.VMEM((8, 768), F32), pltpu.VMEM((4 * local, model), BF16),
            pltpu.VMEM((2, local), F32),
            pltpu.VMEM((4,) + block(model), BF16), pltpu.VMEM((4,) + block(384), BF16),
            pltpu.VMEM((4,) + block(128), BF16), pltpu.VMEM(block(256), BF16),
            pltpu.VMEM(block(384), BF16), pltpu.VMEM(block(768), BF16),
            pltpu.VMEM((2,) + block(model), BF16), pltpu.VMEM((2,) + block(model), BF16),
            pltpu.VMEM((2 * quarter, slab, model), BF16), pltpu.VMEM((4, 8, model), F32),
            pltpu.VMEM(block(model), F32),
            pltpu.SemaphoreType.DMA((1 + 2 * quarter,)),
            pltpu.SemaphoreType.DMA((n_remote,)), pltpu.SemaphoreType.DMA((n_remote,)),
        ],
        compiler_params=params(collective_id=6, has_side_effects=True),
        cost_estimate=pl.CostEstimate(
            flops=16 * quarter * slab * model * 1152, bytes_accessed=40_000_000, transcendentals=0),
        name="front",
    )(lens, img, txt, *vectors, bias, own_w, own_o)


def middle_kernel(dims, total, img, txt, own, peer, cls_own, cls_peer, vec, up, up_bias, down, head_weight, scale,
                  dup, down_keep, down_send, dexp, d_own, d_near, bias_grad, class_e, c_act, c_dup, c_ddn, dcls,
                  head_in, dproj, gains, shifts, scalars,
                  bx, bd, rx, rd, x_near, x_far, ins, rows, part, parts, cls, back, cot, c_rows, extra, extras, hidden_in, weight, ddn, acc, stage,
                  local_sem, send_sem, recv_sem):
    here = Place()
    ip, slab, quarter = dims.ip, dims.slab, dims.quarter
    i = pl.program_id(0)
    model = own.shape[-1]
    mp_peers = [here.core, here.near, here.across]
    fetch = pltpu.make_async_copy(head_weight, weight, local_sem.at[0])
    of = [here.quarter(0, 0), here.quarter(1, 0), here.quarter(0, 1), here.quarter(1, 1)]

    sent_x = [remote(bx.at[2 * j], rx.at[j], send_sem, recv_sem, j, here.core) for j in range(2)]
    sent_d = [remote(bd.at[2 * j], rd.at[j], send_sem, recv_sem, 2 + j, here.core) for j in range(2)]
    def near(p):
        return remote(x_near.at[p], x_far.at[p], send_sem, recv_sem, 18 + p, here.near)

    sent_near = [near(p) for p in range(quarter)]
    sent_part = [remote(part, parts.at[k], send_sem, recv_sem, 5 + k, mp_peers[k]) for k in range(3)]
    sent_extra = [remote(extra, extras.at[k], send_sem, recv_sem, 8 + k, mp_peers[k]) for k in range(3)]
    sent_cls = [remote(cls.at[here.b], cls.at[here.b], send_sem, recv_sem, 11 + k, here.batch[k]) for k in range(7)]

    @pl.when(i == 0)
    def _():
        fetch.start()
        acc[...] = jnp.zeros_like(acc)
        rows[...] = jnp.zeros_like(rows)
        bias_grad[...] = jnp.zeros_like(bias_grad)
        for m in range(2):
            e = jnp.concatenate([cls_own[2 + m], cls_peer[2 + m]], axis=0).astype(BF16)
            class_e[m] = e
            u = dot(e, up[m]) + up_bias[m:m + 1]
            hidden_in[m] = u
            part[m] = dot(gelu_low(u), down[m])
        meet(mp_peers + here.batch)
        for copy in sent_part:
            copy.start()
        ins[...] = peer[...]

    @pl.when(i == 1)
    def _():
        for copy in sent_part:
            copy.wait_recv()
        for m in range(2):
            cls[here.b, m] = jnp.zeros(cls.shape[2:], F32)
            for r in range(4):
                half, at = (cls_own, cls_peer)[r // 2], quarter * (r % 2)
                for p in range(quarter):
                    line = [d[m, own_row(dims, s, p):own_row(dims, s, p) + 1, :]
                            for d, s in ((part, r), (parts.at[0], r ^ 2), (parts.at[1], r ^ 1), (parts.at[2], r ^ 3))]
                    x = (line[0] + line[1]) + (line[2] + line[3]) + vector(vec, F_BIAS + m)
                    x = half[m, at + p:at + p + 1, :] + vector(vec, F_SCALE) * x
                    cls[here.b, m, pl.ds(4 * of[r] + p, 1), :] = x
        for copy in sent_cls:
            copy.start()
        ins[...] = own[...]

    @pl.when(i == 2)
    def _():
        ins[...] = peer[...]

    @pl.when(i == 3)
    def _():
        ins[...] = own[...]
        fetch.wait()
        for copy in sent_cls:
            copy.wait_recv()
        n_rows = 16 * cls.shape[0]
        sharp = jnp.exp(scale[...])
        col_at = lax.broadcasted_iota(jnp.int32, (1, n_rows), 1)
        row_at = lax.broadcasted_iota(jnp.int32, (n_rows, 1), 0)
        col_ok = (col_at % 4) < quarter
        row_ok = (row_at % 4) < quarter
        normal, inverse, proj, unit, embed = [], [], [], [], []
        for m in range(2):
            n, r = normalise(cls[:, m].reshape(n_rows, model))
            h = (n * vector(vec, H_GAIN + m) + vector(vec, H_SHIFT + m)).astype(BF16)
            head_in[m] = h
            y = dot(h, weight[m])
            u = lax.rsqrt(jnp.sum(y * y, axis=-1, keepdims=True) + 1e-6)
            normal.append(n)
            inverse.append(r)
            proj.append(y)
            unit.append(u)
            embed.append((y * u).astype(BF16))
        ok = row_ok & col_ok
        logits = sharp * dot_t(embed[0], embed[1])
        masked = jnp.where(ok, logits, -1e30)
        row_max = jnp.max(masked, axis=1, keepdims=True)
        row_lse = row_max + jnp.log(jnp.sum(jnp.exp(masked - row_max), axis=1, keepdims=True))
        col_max = jnp.max(masked, axis=0, keepdims=True)
        col_lse = col_max + jnp.log(jnp.sum(jnp.exp(masked - col_max), axis=0, keepdims=True))
        same = (row_at == col_at) & ok
        both = jnp.exp(masked - row_lse) + jnp.exp(masked - col_lse)
        dlogits = jnp.where(ok, jnp.where(same, both - 2.0, both) * (1.0 / (2 * total)), 0.0)
        diagonal = jnp.sum(jnp.where(same, logits, 0.0), axis=1, keepdims=True)
        lines = jnp.sum(jnp.where(row_ok, row_lse - 2.0 * diagonal, 0.0), axis=0, keepdims=True)
        lines = lines + jnp.sum(jnp.where(col_ok, col_lse, 0.0), axis=1, keepdims=True)
        slope = jnp.sum(jnp.sum(dlogits * logits, axis=1, keepdims=True), axis=0, keepdims=True)
        scalars[0:1, :] = jnp.broadcast_to(lines * (1.0 / (2 * total)), (1, 128))
        scalars[1:2, :] = jnp.broadcast_to(slope, (1, 128))
        pieces, left = [], dlogits
        for _ in range(3):
            pieces.append(left.astype(BF16))
            left = left - pieces[-1].astype(F32)
        dembed = [
            sharp * (dot(pieces[0], embed[1]) + (dot(pieces[1], embed[1]) + dot(pieces[2], embed[1]))),
            sharp * (t_dot(pieces[0], embed[0]) + (t_dot(pieces[1], embed[0]) + t_dot(pieces[2], embed[0]))),
        ]
        c_rows[...] = jnp.zeros_like(c_rows)
        dcls[...] = jnp.zeros_like(dcls)
        for m in range(2):
            for p in range(quarter):
                src = (img, txt)[m]
                cot[m, 8 * 3 + p:8 * 3 + p + 1, :] = src[p, 0:1, :].astype(F32)
        for m in range(2):
            u, y, d = unit[m], proj[m], dembed[m]
            dp = (u * d - u * u * u * y * jnp.sum(y * d, axis=-1, keepdims=True)).astype(BF16)
            dproj[m] = dp
            dh = dot_t(dp, weight[m])
            gains[m:m + 1, :] = jnp.sum(dh * normal[m], axis=0, keepdims=True)
            shifts[m:m + 1, :] = jnp.sum(dh, axis=0, keepdims=True)
            back[m] = norm_back(normal[m], inverse[m], dh * vector(vec, H_GAIN + m))
            for r in range(4):
                step = (3, 1, 2, 0)[r]
                for p in range(quarter):
                    g = back[m, pl.ds(16 * here.b + 4 * of[r] + p, 1), :]
                    at = own_row(dims, r, p)
                    c_rows[m, at:at + 1, :] = cot[m, 8 * step + p:8 * step + p + 1, :] + g
                    if r == 0:
                        dcls[p, m:m + 1, :] = g
            u = hidden_in[m]
            big, small = gelu_parts(u)
            c_act[m] = (u * big).astype(BF16)
            g = (c_rows[m] * vector(vec, F_SCALE)).astype(BF16)
            c_ddn[m] = g
            du = dot_t(g, down[m]) * (big + u * small)
            bias_grad[m:m + 1, :] += jnp.sum(du, axis=0, keepdims=True)
            low = du.astype(BF16)
            c_dup[m] = low
            acc[m] += t_dot(c_ddn[m], c_act[m])
            extra[m] = dot_t(low, up[m])
        for copy in sent_extra:
            copy.start()

    at = lax.broadcasted_iota(jnp.int32, (slab, 1), 0)
    inner = (at != 0) & (at != ip)

    def one(p, c):
        load_rows(dims, p, img, txt, rows)
        cot[0, pl.ds(8 * i + p, 1), :] = rows[0:1, :]
        cot[1, pl.ds(8 * i + p, 1), :] = rows[ip:ip + 1, :]
        ddn[p] = jnp.where(inner, rows[...] * vector(vec, F_SCALE), 0.0).astype(BF16)
        return c

    lax.fori_loop(0, quarter, one, 0)
    for m, lo, hi in ((0, 0, ip), (1, ip, slab)):
        count = quarter * (hi - lo)
        e = ins[:, lo:hi, :].reshape(count, model)
        u = dot(e, up[m]) + up_bias[m:m + 1]
        big, small = gelu_parts(u)
        a = (u * big).astype(BF16)
        slope = big + u * small
        bd[i, :, lo:hi, :] = dot(a, down[m]).astype(BF16).reshape(quarter, hi - lo, model)
        g = ddn[:, lo:hi, :].reshape(count, model)
        acc[m] += t_dot(g, a)
        du = dot_t(g, down[m]) * slope
        bias_grad[m:m + 1, :] += jnp.sum(du, axis=0, keepdims=True)
        low = du.astype(BF16)
        dup[:, lo:hi, :] = low.reshape(quarter, hi - lo, -1)
        bx[i, :, lo:hi, :] = dot_t(low, up[m]).astype(BF16).reshape(quarter, hi - lo, model)

    for j in range(2):
        @pl.when(i == 2 * j)
        def _():
            sent_x[j].start()
            sent_d[j].start()

    @pl.when(i == 1)
    def _():
        sent_x[0].wait_recv()

        def add_x(p, c):
            x_near[p] = (bx[1, p].astype(F32) + rx[0, p].astype(F32)).astype(BF16)
            return c

        lax.fori_loop(0, quarter, add_x, 0)
        for copy in sent_near:
            copy.start()
        sent_d[0].wait_recv()

        def add_d(p, c):
            d_near[p] = (bd[1, p].astype(F32) + rd[0, p].astype(F32)).astype(BF16)
            return c

        lax.fori_loop(0, quarter, add_d, 0)

    @pl.when(i == 3)
    def _():
        piece = stage.shape[3]
        block = lambda j: pl.ds(pl.multiple_of(j * piece, piece), piece)
        for j in range(4):
            for m in range(2):
                stage[0, j, m] = acc[m, block(2 * j + here.x), :].astype(BF16)
                stage[1, j, m] = acc[m, block(2 * j + 1 - here.x), :].astype(BF16)
        leave = [pltpu.make_async_copy(stage.at[k], dst, local_sem.at[1 + k])
                 for k, dst in enumerate((down_keep, down_send))]
        for copy in leave:
            copy.start()
        sent_d[1].wait_recv()

        def add_d(p, c):
            d_own[p] = bd[3, p].astype(F32) + rd[1, p].astype(F32)
            return c

        lax.fori_loop(0, quarter, add_d, 0)
        sent_x[1].wait_recv()

        def add_x(p, c):
            near(p).wait_recv()
            dexp[p] = bx[3, p].astype(F32) + rx[1, p].astype(F32) + x_far[p].astype(F32)
            return c

        lax.fori_loop(0, quarter, add_x, 0)
        for copy in sent_extra:
            copy.wait_recv()
        for m in range(2):
            for p in range(quarter):
                line = [x[m, own_row(dims, r, p):own_row(dims, r, p) + 1, :]
                        for x, r in ((extra, 0), (extras.at[0], 2), (extras.at[1], 1), (extras.at[2], 3))]
                dexp[p, m * ip:m * ip + 1, :] += (line[0] + line[1]) + (line[2] + line[3])
        for copy in leave:
            copy.wait()
        for copy in sent_x + sent_d + sent_near + sent_part + sent_extra + sent_cls:
            copy.wait_send()


def middle(dims, total, img, txt, own, peer, cls_own, cls_peer, vec, up, up_bias, down, weight, scale):
    model = own.shape[-1]
    hidden = up.shape[-1]
    slab, quarter = dims.slab, dims.quarter
    batch = 8

    def cot_at(i):
        here = Place()
        return here.quarter(1 - i // 2, 1 - i % 2), 0, 0

    held = pl.BlockSpec(memory_space=pltpu.VMEM)
    half = pl.BlockSpec((quarter, slab, model), lambda i: (jnp.where(i < 2, 1, 0), 0, 0))
    step = lambda cols: pl.BlockSpec((quarter, slab, cols), lambda i: (i, 0, 0))
    rows_of = lambda n, t: jax.ShapeDtypeStruct((n, slab, model), t)
    small = [((4, 2, model // 8, hidden), BF16)] * 2 + [((quarter, slab, model), F32), ((quarter, slab, model), F32), ((quarter, slab, model), BF16),
             ((2, hidden), F32), ((2, 16, model), BF16), ((2, 16, hidden), BF16), ((2, 16, hidden), BF16),
             ((2, 16, model), BF16), ((quarter, 8, model), F32), ((2, 16 * batch, model), BF16),
             ((2, 16 * batch, weight.shape[2]), BF16), ((2, model), F32), ((2, model), F32), ((2, 128), F32)]
    block = (quarter, slab, model)
    return pl.pallas_call(
        functools.partial(middle_kernel, dims, total),
        grid=(4,),
        in_specs=[pl.BlockSpec((quarter, dims.patches, model), cot_at),
                  pl.BlockSpec((quarter, dims.caption, model), cot_at)] + [half] * 2 + [held] * 6
        + [pl.BlockSpec(memory_space=pl.ANY), held],
        out_specs=[step(hidden)] + [pl.BlockSpec(memory_space=pl.ANY)] * 2 + [held] * (len(small) - 2),
        out_shape=[rows_of(4 * quarter, BF16)] + [jax.ShapeDtypeStruct(v, t) for v, t in small],
        scratch_shapes=[
            pltpu.VMEM((4,) + block, BF16), pltpu.VMEM((4,) + block, BF16),
            pltpu.VMEM((2,) + block, BF16), pltpu.VMEM((2,) + block, BF16),
            pltpu.VMEM(block, BF16), pltpu.VMEM(block, BF16), pltpu.VMEM(block, BF16),
            pltpu.VMEM((slab, model), F32),
            pltpu.VMEM((2, 16, model), F32), pltpu.VMEM((3, 2, 16, model), F32),
            pltpu.VMEM((batch, 2, 16, model), F32), pltpu.VMEM((2, 16 * batch, model), F32),
            pltpu.VMEM((2, 32, model), F32), pltpu.VMEM((2, 16, model), F32),
            pltpu.VMEM((2, 16, model), F32), pltpu.VMEM((3, 2, 16, model), F32),
            pltpu.VMEM((2, 16, hidden), F32), pltpu.VMEM(weight.shape, BF16),
            pltpu.VMEM(block, BF16), pltpu.VMEM((2, model, hidden), F32),
            pltpu.VMEM((2, 4, 2, model // 8, hidden), BF16), pltpu.SemaphoreType.DMA((3,)),
            pltpu.SemaphoreType.DMA((18 + quarter,)), pltpu.SemaphoreType.DMA((18 + quarter,)),
        ],
        compiler_params=params(collective_id=2, has_side_effects=True),
        cost_estimate=pl.CostEstimate(
            flops=32 * quarter * slab * model * hidden, bytes_accessed=40_000_000, transcendentals=0),
        name="middle",
    )(img, txt, own, peer, cls_own, cls_peer, vec, up, up_bias, down, weight, scale)


def turn_kernel(dims, img, txt, peer, own, dup, ce, cu, down_keep, down_send, dexp, attended, attn, d_own, d_near, dcls, vec,
                down_sum, up_keep, up_send, dattended, dattn, dattn_peer, fin_img, fin_txt, sums,
                acc, d_far, n_peer, rows, side_keep, side_recv, e_in, dexp_in, attended_in, attn_in, d_own_in,
                local_sem, send_sem, recv_sem):
    here = Place()
    quarter, ip = dims.quarter, dims.ip
    i = pl.program_id(0)
    piece = side_keep.shape[2]

    def near(p):
        return remote(d_near.at[p], d_far.at[p], send_sem, recv_sem, 2 + quarter + p, here.near)

    sent_near = [near(p) for p in range(quarter)]

    def over(p):
        return remote(dattn.at[p], n_peer.at[p], send_sem, recv_sem, 1 + p, here.core)

    sent_core = [over(p) for p in range(quarter)]
    sent_side = remote(down_send, side_recv, send_sem, recv_sem, 1 + quarter, here.side)
    loaded = [pltpu.make_async_copy(src, dst, local_sem.at[j]) for j, (src, dst) in enumerate((
        (dexp, dexp_in), (attended, attended_in), (attn, attn_in), (d_own, d_own_in), (down_keep, side_keep)))]
    dexp, attended, attn, d_own = dexp_in, attended_in, attn_in, d_own_in
    spans = ((0, 0, ip), (1, ip, dims.slab))
    flat = lambda v: v.reshape(-1, v.shape[-1])
    block = lambda j: pl.ds(pl.multiple_of(j * piece, piece), piece)

    @pl.when(i == 0)
    def _():
        meet([here.core, here.near, here.side])
        for copy in sent_near:
            copy.start()
        sent_side.start()
        for copy in loaded:
            copy.start()
        for m in range(2):
            acc[m] = t_dot(ce[m], cu[m])

    @pl.when(i % 2 == 0)
    def _():
        e_in[...] = peer[...]

    @pl.when(i % 2 == 1)
    def _():
        e_in[...] = own[...]

    for m, lo, hi in spans:
        acc[m] += t_dot(flat(e_in[:, lo:hi, :]), flat(dup[:, lo:hi, :]))

    @pl.when(i == 3)
    def _():
        for j in range(4):
            for m in range(2):
                up_keep[j, m] = acc[m, block(2 * j + here.x), :].astype(BF16)
                up_send[j, m] = acc[m, block(2 * j + 1 - here.x), :].astype(BF16)
        for copy in loaded:
            copy.wait()
        rows[...] = jnp.zeros_like(rows)
        sums[...] = jnp.zeros_like(sums)

        def load(p):
            load_rows(dims, p, img, txt, rows)
            rows[0:1, :] += dcls[p, 0:1, :]
            rows[ip:ip + 1, :] += dcls[p, 1:2, :]

        def norm(p, c):
            load(p)
            for m, lo, hi in ((0, 0, ip), (1, ip, dims.slab)):
                n, r = normalise(attended[p, lo:hi, :])
                dy = dexp[p, lo:hi, :]
                sums[m:m + 1, :] += jnp.sum(dy * n, axis=0, keepdims=True)
                sums[2 + m:3 + m, :] += jnp.sum(dy, axis=0, keepdims=True)
                d = rows[lo:hi, :] + norm_back(n, r, dy * vector(vec, GAIN2 + m))
                dattended[p, lo:hi, :] = d
                sd = d * vector(vec, A_SCALE)
                dattn[p, lo:hi, :] = sd.astype(BF16)
                a = attn[p, lo:hi, :] + vector(vec, A_BIAS)
                sums[4:5, :] += jnp.sum(d * a, axis=0, keepdims=True)
                sums[5:6, :] += jnp.sum(sd, axis=0, keepdims=True)
            over(p).start()
            return c

        lax.fori_loop(0, quarter, norm, 0)
        def final(p, c):
            load(p)
            near(p).wait_recv()
            for m, lo, hi in ((0, 0, ip), (1, ip, dims.slab)):
                b = d_own[p, lo:hi, :] + d_far[p, lo:hi, :].astype(F32) + vector(vec, F_BIAS + m)
                f = attended[p, lo:hi, :] + vector(vec, F_SCALE) * b
                if m == 0:
                    fin_img[p] = f[0:dims.patches].astype(BF16)
                else:
                    fin_txt[p] = f[0:dims.caption].astype(BF16)
                g = rows[lo:hi, :]
                sums[6:7, :] += jnp.sum(g * b, axis=0, keepdims=True)
                sums[7 + m:8 + m, :] += jnp.sum(g, axis=0, keepdims=True) * vector(vec, F_SCALE)
            return c

        lax.fori_loop(0, quarter, final, 0)
        for p in range(quarter):
            sent_core[p].wait()
            dattn_peer[p] = n_peer[p]
        sent_side.wait()
        for j in range(4):
            down_sum[j] = (side_keep[j].astype(F32) + side_recv[j].astype(F32)).astype(BF16)
        for copy in sent_near:
            copy.wait_send()


def turn(dims, img, txt, peer, own, dup, ce, cu, down_keep, down_send, dexp, attended, attn, d_own, d_near, dcls, vec):
    model = own.shape[-1]
    hidden = dup.shape[-1]
    slab, quarter = dims.slab, dims.quarter
    held = pl.BlockSpec(memory_space=pltpu.VMEM)

    def own_at(i):
        return Place().quarter(0, 0), 0, 0

    away = pl.BlockSpec(memory_space=pl.ANY)
    half = pl.BlockSpec((quarter, slab, model), lambda i: (jnp.where(i < 2, 1, 0), 0, 0))
    step = pl.BlockSpec((quarter, slab, hidden), lambda i: (i, 0, 0))
    block = (quarter, slab, model)
    part = (4, 2, model // 8, hidden)
    outs = [(part, BF16), (part, BF16), (part, BF16), (block, F32), (block, BF16), (block, BF16),
            ((quarter, dims.patches, model), BF16), ((quarter, dims.caption, model), BF16), ((16, model), F32)]
    return pl.pallas_call(
        functools.partial(turn_kernel, dims),
        grid=(4,),
        in_specs=[pl.BlockSpec((quarter, dims.patches, model), own_at),
                  pl.BlockSpec((quarter, dims.caption, model), own_at)] + [half] * 2 + [step]
        + [held] * 2 + [away] * 6 + [held] * 3,
        out_specs=[held] * len(outs),
        out_shape=[jax.ShapeDtypeStruct(v, t) for v, t in outs],
        scratch_shapes=[
            pltpu.VMEM((2, model, hidden), F32), pltpu.VMEM(block, BF16), pltpu.VMEM(block, BF16),
            pltpu.VMEM((slab, model), F32), pltpu.VMEM(part, BF16), pltpu.VMEM(part, BF16),
            pltpu.VMEM(block, BF16),
        ] + [pltpu.VMEM(block, F32)] * 4 + [
            pltpu.SemaphoreType.DMA((5,)),
            pltpu.SemaphoreType.DMA((2 + 2 * quarter,)), pltpu.SemaphoreType.DMA((2 + 2 * quarter,)),
        ],
        compiler_params=params(collective_id=3, has_side_effects=True),
        cost_estimate=pl.CostEstimate(
            flops=16 * quarter * slab * model * hidden, bytes_accessed=40_000_000, transcendentals=0),
        name="turn",
    )(img, txt, peer, own, dup, ce, cu, down_keep, down_send, dexp, attended, attn, d_own, d_near, dcls, vec)


def back_kernel(dims, lens, d_own, d_peer, normed, qkv_far, mixed_far, qkv_own, mixed_own, wq, wo, wf,
                fin_img, fin_txt, up_keep, up_send, down_sum,
                whole, grad_pair, grad_single, cols_far, cols_own, near_img, near_txt, far_sum, down_out, up_out,
                dattn, dm_far, dm_own, dq_far, dq_own, acc_far, acc_own, w_far, w_own, o_far, o_own, dn, grad_f,
                up_mine, up_side, up_sum, up_in, up_pass, up_last, down_mine, down_in, down_pass, down_last,
                n_send, n_recv, from_side, local_sem, send_sem, recv_sem):
    here = Place()
    i = pl.program_id(0)
    slab, quarter, local = dims.slab, dims.quarter, dims.local
    two, one_head = parts_of(dims)
    count = quarter * slab
    model = normed.shape[-1]
    piece = from_side.shape[1]
    block = lambda j: pl.ds(pl.multiple_of(j * piece, piece), piece)
    used = [0]

    def make(src, dst, device):
        at = used[0]
        used[0] += 1
        return remote(src, dst, send_sem, recv_sem, at, device)

    sent_near = [make(fin_img, near_img, here.near), make(fin_txt, near_txt, here.near)]
    sent_up = [make(up_send.at[j, m], up_side.at[m, j], here.side) for m in range(2) for j in range(4)]
    in_pair = lambda src, dst: [make(src.at[here.z_pair], dst.at[0], here.paired), make(src.at[here.z_rest], dst.at[1], here.paired)]
    sent_down = in_pair(down_sum, down_in)
    pass_down = make(down_pass, down_last, here.opposite)
    wide = grad_f.shape[1]
    sent_far = [make(grad_f.at[block(2 * j + 1 - here.x)], from_side.at[j, :, pl.ds(0, wide)], here.side) for j in range(4)]
    sent_far += [make(grad_single.at[block(2 * j + 1 - here.x)], from_side.at[j, :, pl.ds(wide, grad_single.shape[1])],
                      here.side) for j in range(4)]
    sent_pair = [in_pair(up_sum.at[m], up_in.at[m]) for m in range(2)]
    pass_up = [make(up_pass.at[m], up_last.at[m], here.opposite) for m in range(2)]
    sent_n = make(n_send, n_recv, here.core)
    loaded = [pltpu.make_async_copy(up_keep, up_mine, local_sem.at[0]),
              pltpu.make_async_copy(down_sum.at[here.z], down_mine.at[0], local_sem.at[1]),
              pltpu.make_async_copy(down_sum.at[here.z_far], down_mine.at[1], local_sem.at[2])]
    add = lambda *parts: functools.reduce(lambda p, q: p + q, [v.astype(F32) for v in parts])

    @pl.when(i == 0)
    def _():
        meet([here.core, here.near, here.side, here.paired, here.opposite])
        for copy in loaded + sent_near + sent_up + sent_down:
            copy.start()
        for acc, cols in ((acc_far, cols_far), (acc_own, cols_own)):
            acc[...] = jnp.zeros_like(acc)
            cols[...] = jnp.zeros_like(cols)
        for t in range(4):
            own, start = (wq, t * local) if t < 3 else (wo, 0)
            dst, at = (w_far, t * 2 * two) if t < 3 else (o_far, 0)
            copy_rows(dst, at, wf, t * local, two)
            copy_rows(dst, at + two, own, start + two, one_head)
            copy_rows(dst, at + two + one_head, wf, t * local + two, one_head)
            dst, at = (w_own, t * two) if t < 3 else (o_own, 0)
            copy_rows(dst, at, own, start, two)

    @pl.when(i % 2 == 0)
    def _():
        dattn[...] = d_peer[...]

    @pl.when(i % 2 == 1)
    def _():
        dattn[...] = d_own[...]

    whose = here.quarter(0, 1 - i % 2)

    @pl.when(i < 2)
    def _():
        part = back_step(dims, 2, lens, whose, dattn, normed, qkv_far, mixed_far, dm_far, dq_far, acc_far, cols_far,
                         w_far, o_far)
        dn[i] = part.reshape(quarter, slab, model)

    def sum_up(m):
        for j in range(4):
            sent_up[4 * m + j].wait_recv()
            up_sum[m, j] = add(up_mine[j, m], up_side[m, j]).astype(BF16)
        for copy in sent_pair[m]:
            copy.start()

    def pass_on(m):
        for copy in sent_pair[m]:
            copy.wait_recv()
        up_pass[m] = add(up_sum[m, here.z_far], up_in[m, 1]).astype(BF16)
        pass_up[m].start()

    @pl.when(i == 0)
    def _():
        for copy in loaded[1:]:
            copy.wait()
        for copy in sent_down:
            copy.wait_recv()
        down_pass[...] = add(down_mine[1], down_in[1]).astype(BF16)
        pass_down.start()
        loaded[0].wait()
        sum_up(0)

    @pl.when(i == 1)
    def _():
        for t in range(4):
            at = t * 2 * two
            to = 4 * two + t * one_head
            grad_f[:, t * two:(t + 1) * two] = acc_far[:, at:at + two].astype(BF16)
            grad_f[:, to:to + one_head] = acc_far[:, at + two + one_head:at + 2 * two].astype(BF16)
            grad_single[:, t * one_head:(t + 1) * one_head] = acc_far[:, at + two:at + two + one_head].astype(BF16)
        for copy in sent_far:
            copy.start()
        pass_on(0)
        sum_up(1)

    @pl.when(i >= 2)
    def _():
        part = back_step(dims, 1, lens, whose, dattn, normed, qkv_own, mixed_own, dm_own, dq_own, acc_own, cols_own,
                         w_own, o_own)
        total = part.reshape(quarter, slab, model) + dn[i - 2]

        @pl.when(i == 2)
        def _():
            n_send[...] = total.astype(BF16)
            sent_n.start()
            pass_on(1)

        @pl.when(i == 3)
        def _():
            whole[...] = total

    @pl.when(i == 3)
    def _():
        grad_pair[...] = acc_own[...].astype(BF16)
        sent_n.wait_recv()
        whole[...] += n_recv[...].astype(F32)
        down_out[...] = add(down_mine[0], down_in[0])
        for copy in sent_far:
            copy.wait_recv()
        for j in range(4):
            far_sum[j, :, 0:wide] = add(grad_f[block(2 * j + here.x), :], from_side[j, :, 0:wide]).astype(BF16)
            far_sum[j, :, wide:] = add(grad_single[block(2 * j + here.x), :], from_side[j, :, wide:]).astype(BF16)
        pass_down.wait_recv()
        down_out[...] += down_last[...].astype(F32)
        for m in range(2):
            pass_up[m].wait_recv()
            up_out[m] = add(up_sum[m, here.z], up_in[m, 0], up_last[m])
        for copy in sent_near:
            copy.wait_recv()
        for copy in sent_near + sent_up + sent_down + sent_far + sent_pair[0] + sent_pair[1] + pass_up + [pass_down, sent_n]:
            copy.wait_send()


def back(dims, lens, d_own, d_peer, normed, qkv_far, mixed_far, qkv_own, mixed_own, wq, wo, wf,
         fin_img, fin_txt, up_keep, up_send, down_sum):
    model = normed.shape[-1]
    slab, quarter = dims.slab, dims.quarter
    hidden = up_keep.shape[-1]
    piece = model // 8
    held = pl.BlockSpec(memory_space=pltpu.VMEM)
    away = pl.BlockSpec(memory_space=pl.ANY)
    spec = lambda cols, at: pl.BlockSpec((quarter, slab, cols), lambda i: (at(i), 0, 0))
    early, late = lambda i: jnp.maximum(1 - i, 0), lambda i: jnp.where(i < 3, 1, 0)
    rows = (quarter, slab, model)
    outs = [(held, rows, F32), (held, (model, 512), BF16), (held, (model, 256), BF16),
            (held, (1, 768), F32), (held, (1, 384), F32),
            (away, fin_img.shape, BF16), (away, fin_txt.shape, BF16),
            (held, (4, piece, model + 256), BF16), (held, (2, piece, hidden), F32), (held, (2, piece, hidden), F32)]
    slabs = lambda cols: pltpu.VMEM((quarter, slab, cols), BF16)
    return pl.pallas_call(
        functools.partial(back_kernel, dims),
        grid=(4,),
        in_specs=[pl.BlockSpec(memory_space=pltpu.SMEM), held, held, spec(model, lambda i: 1 - i % 2),
                  spec(768, early), spec(256, early), spec(384, late), spec(128, late), held, held, held]
        + [away] * 5,
        out_specs=[v[0] for v in outs],
        out_shape=[jax.ShapeDtypeStruct(v[1], v[2]) for v in outs],
        scratch_shapes=[
            slabs(model), slabs(256), slabs(128), slabs(768), slabs(384),
            pltpu.VMEM((model, 1024), F32), pltpu.VMEM((model, 512), F32),
            pltpu.VMEM((768, model), BF16), pltpu.VMEM((384, model), BF16),
            pltpu.VMEM((256, model), BF16), pltpu.VMEM((128, model), BF16),
            pltpu.VMEM((2,) + rows, F32), pltpu.VMEM((model, model), BF16),
            pltpu.VMEM((4, 2, piece, hidden), BF16), pltpu.VMEM((2, 4, piece, hidden), BF16),
            pltpu.VMEM((2, 4, piece, hidden), BF16), pltpu.VMEM((2, 2, piece, hidden), BF16),
            pltpu.VMEM((2, piece, hidden), BF16), pltpu.VMEM((2, piece, hidden), BF16),
            pltpu.VMEM((2, 2, piece, hidden), BF16), pltpu.VMEM((2, 2, piece, hidden), BF16),
            pltpu.VMEM((2, piece, hidden), BF16), pltpu.VMEM((2, piece, hidden), BF16),
            pltpu.VMEM(rows, BF16), pltpu.VMEM(rows, BF16), pltpu.VMEM((4, piece, model + 256), BF16),
            pltpu.SemaphoreType.DMA((3,)), pltpu.SemaphoreType.DMA((28,)), pltpu.SemaphoreType.DMA((28,)),
        ],
        compiler_params=params(collective_id=4, has_side_effects=True),
        cost_estimate=pl.CostEstimate(
            flops=24 * quarter * slab * model * 1152, bytes_accessed=30_000_000, transcendentals=0),
        name="back",
    )(lens, d_own, d_peer, normed, qkv_far, mixed_far, qkv_own, mixed_own, wq, wo, wf,
      fin_img, fin_txt, up_keep, up_send, down_sum)


V_ROWS, V_MP, V_HEADS, V_FAR = 16, 11, 13, 256


def finish_kernel(dims, dnormed, dattended, states_img, states_txt, vec, fin_img, fin_txt,
                  near_img, near_txt, grad_pair, grad_far, own_sums, up_sums, cols_own, cols_far,
                  core_img, core_txt, across_img, across_txt, back_img, back_txt, grad_out, v_out,
                  s_img, s_txt, d_img, d_txt, rows, xr, zs, z_in, z_pass, z_last, f_in, f_pass, f_last, far_sum, far_recv, vs, vr,
                  local_sem, send_sem, recv_sem):
    quarter = dims.quarter
    here = Place()
    z, x, m = here.z, here.x, here.m
    near_quarter = here.quarter(1, 0)
    used = [0]

    def send(src, dst, device):
        at = used[0]
        used[0] += 1
        return remote(src, dst, send_sem, recv_sem, at, device)

    loaded = [pltpu.make_async_copy(states_img.at[pl.ds(m * quarter, quarter)], s_img, local_sem.at[0]),
              pltpu.make_async_copy(states_txt.at[pl.ds(m * quarter, quarter)], s_txt, local_sem.at[1])]
    for copy in loaded:
        copy.start()
    meet([here.core, here.near, here.side, here.paired, here.opposite])

    piece = xr.shape[1]
    wide = grad_pair.shape[1]
    block = lambda j: pl.ds(pl.multiple_of(j * piece, piece), piece)
    x_copies = []
    for j in range(4):
        x_copies.append(send(grad_pair.at[block(2 * j + 1 - x)], xr.at[j], here.side))
        x_copies[-1].start()
    add = lambda *parts: functools.reduce(lambda p, q: p + q, [v.astype(F32) for v in parts])
    in_pair = lambda src, dst: [send(src.at[here.z_pair], dst.at[0], here.paired),
                                send(src.at[here.z_rest], dst.at[1], here.paired)]
    far_copies = in_pair(grad_far, f_in)
    for copy in far_copies:
        copy.start()

    fin_remote = [send(src, dst, here.core) for src, dst in (
        (fin_img, core_img), (fin_txt, core_txt), (near_img, across_img), (near_txt, across_txt))]

    rows[...] = jnp.zeros_like(rows)
    for copy in loaded:
        copy.wait()
    total = [jnp.zeros((1, rows.shape[1]), F32)] * 2
    back_local, to_near, to_other = [], [], []
    for p in range(quarter):
        load_rows(dims, p, s_img, s_txt, rows)
        n, r = normalise(rows[...])
        dy = dnormed[p]
        total[0] = total[0] + jnp.sum(dy * n, axis=0, keepdims=True)
        total[1] = total[1] + jnp.sum(dy, axis=0, keepdims=True)
        d = dattended[p] + norm_back(n, r, dy * vector(vec, GAIN1))
        d_img[p] = d[0:dims.patches].astype(BF16)
        d_txt[p] = d[dims.ip:dims.ip + dims.caption].astype(BF16)
        for j, (src, dst) in enumerate(((d_img, back_img), (d_txt, back_txt))):
            at = dst.at[m * quarter + p]
            to_near.append(send(src.at[p], at, here.near))
            to_near[-1].start()
            to_other.append(send(src.at[p], at, here.core))
            to_other[-1].start()
            back_local.append(pltpu.make_async_copy(src.at[p], at, local_sem.at[2 + 2 * p + j]))
            back_local[-1].start()
    for copy in fin_remote:
        copy.start()

    at = lax.broadcasted_iota(jnp.int32, (V_ROWS, 1), 0)
    two, one_head = parts_of(dims)
    vs[0] = jnp.zeros(vs.shape[1:], F32)
    vs[0, 0:1, :] = total[0]
    vs[0, 1:2, :] = total[1]
    vs[0, 2:V_MP, :] = own_sums[0:V_MP - 2, :]
    vs[0, V_MP:V_HEADS, :] = up_sums[...]
    for j in range(2):
        own_at, far_at = 2 * j * two, 4 * j * two
        vs[0, V_HEADS + j:V_HEADS + j + 1, 0:two] = cols_own[0:1, own_at:own_at + two]
        vs[0, V_HEADS + j:V_HEADS + j + 1, two:two + one_head] = cols_far[0:1, far_at + two:far_at + two + one_head]
        vs[0, V_HEADS + j:V_HEADS + j + 1, V_FAR:V_FAR + two] = cols_far[0:1, far_at:far_at + two]
        vs[0, V_HEADS + j:V_HEADS + j + 1, V_FAR + two:V_FAR + two + one_head] = cols_far[0:1, far_at + two + one_head:far_at + 2 * two]
    v = vs[0]
    v_copies = []

    def exchange(step, value, device):
        vs[step] = value
        copy = send(vs.at[step], vr.at[step], device)
        copy.start()
        copy.wait_recv()
        v_copies.append(copy)
        return vr[step]

    v = v + jnp.where(at < V_MP, exchange(0, v, here.core), 0.0)
    for copy in far_copies:
        copy.wait_recv()
    f_pass[...] = add(grad_far[here.z_far], f_in[1]).astype(BF16)
    far_copies.append(send(f_pass, f_last, here.opposite))
    far_copies[-1].start()
    v = v + exchange(1, v, here.side)
    v = v + exchange(2, v, here.paired)
    vs[3] = v
    v_far = send(vs.at[3], vr.at[3], here.opposite)
    v_far.start()

    def own_sum(j):
        return add(grad_pair[block(2 * j + x), :], xr[j])

    for copy in x_copies:
        copy.wait_recv()
    for j in range(4):
        zs[j] = own_sum(j).astype(BF16)
    z_copies = in_pair(zs, z_in)
    for copy in z_copies:
        copy.start()

    far_copies[-1].wait_recv()
    narrow = far_sum.shape[1]
    far_sum[...] = add(grad_far[z, :, 0:narrow], f_in[0, :, 0:narrow], f_last[:, 0:narrow]).astype(BF16)
    far_copy = send(far_sum, far_recv, here.near)
    far_copy.start()
    v_far.wait_recv()
    v = v + vr[3]
    for copy in z_copies:
        copy.wait_recv()
    z_pass[...] = add(zs[here.z_far], z_in[1]).astype(BF16)
    z_copies.append(send(z_pass, z_last, here.opposite))
    z_copies[-1].start()
    vs[4] = v
    v_near = send(vs.at[4], vr.at[4], here.near)
    v_near.start()
    for copy in back_local:
        copy.wait()
    onward = []
    for p in range(quarter):
        for j, dst in enumerate((back_img, back_txt)):
            to_near[2 * p + j].wait_recv()
            at_near = dst.at[near_quarter * quarter + p]
            onward.append(send(at_near, at_near, here.core))
            onward[-1].start()
    far_copy.wait_recv()
    z_copies[-1].wait_recv()
    grad_out[:, 0:wide] = own_sum(z) + add(far_recv[:, 0:wide], z_in[0], z_last[...])
    grad_out[:, wide:] = add(
        far_recv[:, wide:], grad_far[z, :, narrow:], f_in[0, :, narrow:], f_last[:, narrow:])
    v_near.wait_recv()
    there = vr[4]
    v_out[...] = v + jnp.where(at < V_MP, there, 0.0)
    width = two + one_head
    v_out[V_HEADS:V_HEADS + 2, 0:width] = v[V_HEADS:V_HEADS + 2, 0:width] + there[V_HEADS:V_HEADS + 2, V_FAR:V_FAR + width]
    for copy in to_other + fin_remote + onward:
        copy.wait()
    for copy in x_copies + far_copies + to_near + z_copies + v_copies + [far_copy, v_near, v_far]:
        copy.wait_send()


def finish(dims, dnormed, dattended, states_img, states_txt, vec, fin_img, fin_txt,
           near_img, near_txt, grad_pair, grad_far, *tables):
    pairs, patches, model = states_img.shape
    caption = states_txt.shape[1]
    quarter, slab = dims.quarter, dims.slab
    piece, cols = grad_far.shape[1], model
    wide, all_cols = grad_pair.shape[1], grad_far.shape[2]
    held = pl.BlockSpec(memory_space=pltpu.VMEM)
    away = pl.BlockSpec(memory_space=pl.ANY)
    n_remote = 7 * quarter + 28
    return pl.pallas_call(
        functools.partial(finish_kernel, dims),
        in_specs=[held, held] + [away] * 2 + [held] + [away] * 4 + [held] * 6,
        out_specs=[away] * 6 + [held] * 2,
        out_shape=[jax.ShapeDtypeStruct(v.shape, BF16) for v in (fin_img, fin_txt) * 2] + [
            jax.ShapeDtypeStruct((pairs, patches, model), BF16),
            jax.ShapeDtypeStruct((pairs, caption, model), BF16),
            jax.ShapeDtypeStruct((piece, cols), F32),
            jax.ShapeDtypeStruct((V_ROWS, model), F32),
        ],
        scratch_shapes=[
            pltpu.VMEM((quarter, patches, model), BF16),
            pltpu.VMEM((quarter, caption, model), BF16),
            pltpu.VMEM((quarter, patches, model), BF16),
            pltpu.VMEM((quarter, caption, model), BF16),
            pltpu.VMEM((slab, model), F32),
            pltpu.VMEM((4, piece, wide), BF16), pltpu.VMEM((4, piece, wide), BF16),
            pltpu.VMEM((2, piece, wide), BF16), pltpu.VMEM((piece, wide), BF16), pltpu.VMEM((piece, wide), BF16),
            pltpu.VMEM((2, piece, all_cols), BF16), pltpu.VMEM((piece, all_cols), BF16), pltpu.VMEM((piece, all_cols), BF16),
            pltpu.VMEM((piece, cols), BF16), pltpu.VMEM((piece, cols), BF16),
            pltpu.VMEM((5, V_ROWS, model), F32),
            pltpu.VMEM((5, V_ROWS, model), F32),
            pltpu.SemaphoreType.DMA((2 + 2 * quarter,)),
            pltpu.SemaphoreType.DMA((n_remote,)),
            pltpu.SemaphoreType.DMA((n_remote,)),
        ],
        compiler_params=params(collective_id=1, has_side_effects=True),
        name="finish",
    )(dnormed, dattended, states_img, states_txt, vec, fin_img, fin_txt,
      near_img, near_txt, grad_pair, grad_far, *tables)


def spread_kernel(dims, cols, sums, grad, gains, shifts, up, down, head_in, dproj, *refs):
    forward, refs = refs[:8], refs[8:]
    back_img, back_txt, *refs = refs
    outs, refs = refs[:12], refs[12:]
    (qkv, out_w, up_out, down_out, head_out, out_img, out_txt, grad_img, grad_txt,
     turned, held_img, held_txt, held_up, held_down, h_in, d_in, in_sem, out_sem) = refs
    here = Place()
    quarter = dims.quarter
    whose = [here.quarter(0, 0), here.quarter(1, 0), here.quarter(0, 1), here.quarter(1, 1)]
    place = lambda q: pl.ds(q * quarter, quarter)
    comes, goes = [], []
    for r in range(4):
        for j, (held, src, dst, back, to) in enumerate((
            (held_img, forward[2 * r], out_img, back_img, grad_img), (held_txt, forward[2 * r + 1], out_txt, back_txt, grad_txt),
        )):
            for k, (source, target, q) in enumerate(((src, dst, whose[r]), (back.at[place(r)], to, r))):
                at = 4 * r + 2 * j + k
                comes.append(pltpu.make_async_copy(source, held.at[2 * r + k], in_sem.at[at]))
                goes.append(pltpu.make_async_copy(held.at[2 * r + k], target.at[place(q)], out_sem.at[at]))
    for at, (src, held, dst) in enumerate(((up, held_up, up_out), (down, held_down, down_out))):
        comes.append(pltpu.make_async_copy(src, held, in_sem.at[16 + at]))
        goes.append(pltpu.make_async_copy(held, dst, out_sem.at[16 + at]))
    late = [pltpu.make_async_copy(head_in, h_in, in_sem.at[18]), pltpu.make_async_copy(dproj, d_in, in_sem.at[19])]
    for copy in late + comes:
        copy.start()
    turn_by = sums.shape[1] - here.b * cols

    def slice_of(value):
        return pltpu.roll(value, turn_by, 1)[:, 0:cols]

    mine = slice_of(sums[...])
    for out, (lo, count) in zip(outs[:8], ((0, 1), (1, 1), (7, 1), (6, 1), (2, 2), (4, 2), (9, 2), (8, 1))):
        out[...] = mine[lo:lo + count, :]
    wide = jnp.concatenate([gains[...], shifts[...], jnp.zeros((4, sums.shape[1]), F32)], axis=0)
    heads = slice_of(wide)
    outs[8][...] = heads[0:2, :]
    outs[9][...] = heads[2:4, :]
    outs[10][...] = sums[V_MP:V_MP + 2, :]
    outs[11][...] = sums[V_HEADS:V_HEADS + 2, 0:outs[11].shape[1]]
    two, one = 2 * HEAD_DIM, HEAD_DIM
    for t in range(3):
        qkv[t, :, 0:two] = grad[:, t * two:(t + 1) * two]
        qkv[t, :, two:two + one] = grad[:, 4 * two + t * one:4 * two + (t + 1) * one]
    turned[...] = jnp.zeros_like(turned)
    turned[0:cols, 0:two] = grad[:, 3 * two:4 * two]
    turned[0:cols, two:two + one] = grad[:, 4 * two + 3 * one:4 * two + 4 * one]
    out_w[...] = turned[...].T[0:two + one, 0:cols]
    for copy in late:
        copy.wait()
    for m in range(2):
        part = pltpu.roll(h_in[m].astype(F32), turn_by, 1)[:, 0:128].astype(BF16)
        head_out[m] = t_dot(part, d_in[m])[0:cols]
    for come, go in zip(comes, goes):
        come.wait()
        go.start()
    for go in goes:
        go.wait()


def spread(dims, sums, grad, gains, shifts, up, down, head_in, dproj, forward, back_img, back_txt):
    cols, model = grad.shape[0], sums.shape[1]
    local, quarter = dims.local, dims.quarter
    assert cols <= 128
    shapes = [(1, cols)] * 4 + [(2, cols)] * 3 + [(1, cols)] + [(2, cols)] * 2 + [(2, model), (2, local)]
    shapes += [(3, cols, local), (local, cols), up.shape, down.shape, (2, cols, dproj.shape[2])]
    held = pl.BlockSpec(memory_space=pltpu.VMEM)
    away = pl.BlockSpec(memory_space=pl.ANY)
    args = (sums, grad, gains, shifts, up, down, head_in, dproj)
    return pl.pallas_call(
        functools.partial(spread_kernel, dims, cols),
        in_specs=[held] * 4 + [away] * (len(args) - 4 + 10),
        out_specs=[held] * (len(shapes) - 3) + [away] * 2 + [held] + [away] * 4,
        out_shape=[jax.ShapeDtypeStruct(v, F32) for v in shapes]
        + [jax.ShapeDtypeStruct(v.shape, BF16) for v in (back_img, back_txt) * 2],
        scratch_shapes=[
            pltpu.VMEM((128, 256), F32),
            pltpu.VMEM((8, quarter, dims.patches, model), BF16), pltpu.VMEM((8, quarter, dims.caption, model), BF16),
            pltpu.VMEM(up.shape, F32), pltpu.VMEM(down.shape, F32),
            pltpu.VMEM(head_in.shape, BF16), pltpu.VMEM(dproj.shape, BF16),
            pltpu.SemaphoreType.DMA((20,)), pltpu.SemaphoreType.DMA((18,)),
        ],
        compiler_params=params(),
        cost_estimate=pl.CostEstimate(flops=1_000_000, bytes_accessed=20_000_000, transcendentals=0),
        name="spread",
    )(*args, *forward, back_img, back_txt)


def per_device(
    image_states, text_states, caption_lengths, image_cotangent, text_cotangent,
    first_gain, first_shift, query_key_value, query_value_bias, output_weight, output_bias,
    attention_scale, expert_gain, expert_shift, expert_up, expert_up_bias, expert_down,
    expert_down_bias, feedforward_scale, head_gain, head_shift, head_weight, logit_scale,
):
    pairs, patches, model = image_states.shape
    caption = text_states.shape[1]
    local = query_key_value.shape[2]
    quarter = pairs // 4
    batch_size = lax.axis_size("batch")
    assert lax.axis_size("mp") == 4 and pairs == 4 * quarter and quarter <= 3
    assert batch_size & (batch_size - 1) == 0
    assert local == 3 * HEAD_DIM
    ip, tp = up16(patches), up16(caption)
    dims = Dims(patches, caption, ip, tp, ip + tp, quarter, local)
    me = lax.axis_index("mp")
    batch_at = lax.axis_index("batch")
    order = me ^ jnp.asarray(ORDER, jnp.int32)
    vectors = (first_gain, first_shift, attention_scale, output_bias, expert_gain, expert_shift,
               feedforward_scale, expert_down_bias, head_gain, head_shift)
    own_w = jnp.transpose(query_key_value, (1, 2, 0)).reshape(3 * local, model)
    one_kernel = batch_size == 8 and model // batch_size % 32 == 0 and expert_up.shape[2] == model
    if one_kernel:
        (vec, normed, qkv_own, mixed_own, qkv_far, mixed_far, wf, attended, attn, e_own, e_peer, cls_own, cls_peer) = front(
            dims, caption_lengths, image_states, text_states, vectors, query_value_bias, own_w, output_weight)
    else:
        vec = jnp.concatenate([v.reshape(-1, model) for v in vectors] + [jnp.zeros((1, model), F32)])
        wo = jnp.concatenate([own_w, output_weight])
        wf = to_y(wo)
        far_bias = to_y(query_value_bias)
        normed, qkv_own, rest, mixed_own = attend_own(
            dims, order, caption_lengths, image_states, text_states, vec, query_value_bias, wo)
        qkv_far, mixed_far, a_keep, a_send = attend_far(
            dims, order, caption_lengths, normed, rest, mixed_own, far_bias, wo, wf)
        a_recv = to_core(a_send)
        attended, attn, e_own, cls_own = residual(
            dims, order, a_keep, a_recv, image_states, text_states, vec)
        e_peer = to_core(e_own)
        cls_peer = to_core(cls_own)
    if one_kernel:
        (dup, down_keep, down_send, dexp, d_own, d_near, up_sums, class_e, _, c_dup, _, dcls, head_in, dproj,
         grad_head_gain, grad_head_shift, scalars) = middle(
            dims, pairs * batch_size, image_cotangent, text_cotangent, e_own, e_peer, cls_own, cls_peer, vec,
            expert_up, expert_up_bias, expert_down, head_weight, logit_scale.reshape(1, 1))
        down_sum, up_keep, up_send, dattended, dattn, dattn_peer, fin_img, fin_txt, own_sums = turn(
            dims, image_cotangent, text_cotangent, e_peer, e_own, dup, class_e, c_dup, down_keep, down_send,
            dexp, attended, attn, d_own, d_near, dcls, vec)
    else:
        class_part, class_e = class_forward(dims, cls_own, cls_peer, expert_up, expert_up_bias, expert_down)
        class_parts = from_others(class_part, "mp", 1, 4)

        act_a, dup_a, ddn_a, d_send3, d_keep1, x_send3, x_keep1, bias_a, cot_a = experts(
            dims, "experts_a", 1, order[jnp.asarray([3, 1])], e_peer, e_own, image_cotangent, text_cotangent,
            tie(vec, class_part), expert_up, expert_up_bias, expert_down)
        x_recv1 = to_core(x_send3)
        d_recv1 = to_core(d_send3)
        final_class = class_final(
            dims, order, cls_own, cls_peer, class_parts, tie(vec, bias_a))
        class_blocks = gather_batch(final_class[None])
        x_near = add_low(x_keep1, x_recv1)
        x_far = to_y(x_near)
        act_b, dup_b, ddn_b, d_send2, d_keep0, x_send2, x_keep0, bias_b, cot_b = experts(
            dims, "experts_b", 0, order[jnp.asarray([2, 0])], e_peer, e_own, image_cotangent, text_cotangent,
            tie(vec, final_class, x_near), expert_up, expert_up_bias, expert_down)
        x_recv0 = to_core(x_send2)
        d_recv0 = to_core(d_send2)

        head_in, dproj, dclass, grad_head_gain, grad_head_shift, scalars = (contrast if batch_size <= 8 else contrast_large)(
            dims, pairs * batch_size, batch_at.reshape(1), class_blocks, tie(vec, bias_b), head_weight,
             logit_scale.reshape(1, 1))
        c_act, c_dup, c_ddn, c_dexp, c_bias, dcls = class_back(
            dims, order, class_e, cot_a, cot_b, dclass, vec, expert_up, expert_up_bias, expert_down)
        extras = from_others(c_dexp, "mp", 1, 4)
        d_far = to_y(add_low(d_keep1, tie(d_recv1, c_dexp)))
        expert_grad = expert_grads(
            dims, e_peer, e_own, act_a, dup_a, ddn_a, act_b, dup_b, ddn_b, class_e, c_act, c_dup, c_ddn)
        expert_sum = lax.psum_scatter(expert_grad, "batch", scatter_dimension=1, tiled=True)

        dattended, dattn, sums_two = norm_two(
            dims, order, x_keep0, x_recv0, x_far, attended, a_keep, a_recv, image_cotangent, text_cotangent,
            dcls, extras, tie(vec, expert_grad))
        dattn_peer = to_core(dattn)
        fin_img, fin_txt, sums_fin = final_rows(
            dims, order, d_keep0, d_recv0, d_far, attended, image_cotangent, text_cotangent, dcls,
            tie(vec, sums_two))
        own_sums = jnp.concatenate([sums_two[:6], sums_fin[:3]])
        up_sums = bias_a + bias_b + c_bias
    contrast_loss = scalars[0, :1]
    grad_logit_scale = scalars[1, :1]
    if one_kernel:
        (dnormed, grad_o01, grad_o2, cols_far, cols_own, near_img, near_txt, far_sum, grad_down,
         grad_up) = back(
            dims, caption_lengths, dattn, dattn_peer, normed, qkv_far, mixed_far, qkv_own, mixed_own,
            own_w, output_weight, wf, fin_img, fin_txt, up_keep, up_send, down_sum)
    else:
        n_keep, n_send, grad_far, grad_o2, cols_far = attend_back(
            dims, True, order, caption_lengths, dattn, dattn_peer, normed, qkv_far, mixed_far, own_w, output_weight, wf)
        n_keep, n_send, grad_o01, cols_own = attend_back(
            dims, False, order, caption_lengths, dattn, dattn_peer, normed, qkv_own, mixed_own, own_w, output_weight, wf,
            prior=(n_keep, n_send))
    cols = model // batch_size
    mine = lambda v, axis: lax.dynamic_slice_in_dim(v, batch_at * cols, cols, axis=axis)
    pair, single = 2 * HEAD_DIM, HEAD_DIM
    if one_kernel:
        core_img, core_txt, across_img, across_txt, back_img, back_txt, attn_grad, sums = finish(
            dims, dnormed, dattended, image_states, text_states, vec, fin_img, fin_txt,
            near_img, near_txt, grad_o01, far_sum, own_sums, up_sums, cols_own, cols_far)
        forward = (fin_img, fin_txt, near_img, near_txt, core_img, core_txt, across_img, across_txt)
        (*vectors, grad_qkv, grad_output_weight, grad_up, grad_down, grad_head_weight,
         image_output, text_output, image_grad, text_grad) = spread(
            dims, sums, attn_grad, grad_head_gain, grad_head_shift, grad_up, grad_down, head_in, dproj,
            forward, back_img, back_txt)
        flat = lambda v: v.reshape(-1)
        return (
            image_output,
            text_output,
            contrast_loss,
            image_grad,
            text_grad,
            flat(vectors[0]),
            flat(vectors[1]),
            jnp.transpose(grad_qkv, (1, 0, 2)),
            vectors[11],
            grad_output_weight,
            flat(vectors[2]),
            flat(vectors[3]),
            vectors[4],
            vectors[5],
            grad_up,
            vectors[10],
            jnp.transpose(grad_down, (0, 2, 1)),
            vectors[6],
            flat(vectors[7]),
            vectors[8],
            vectors[9],
            grad_head_weight,
            grad_logit_scale,
        )
    else:
        grad_head_weight = jnp.einsum("mnc,mne->mce", mine(head_in, 2), dproj, preferred_element_type=F32)
        grad_expert_up = expert_sum[:2].astype(F32)
        grad_expert_down = jnp.transpose(expert_sum[2:].astype(F32), (0, 2, 1))
        cols_own = cols_own.reshape(3, pair)[::2]
        cols_far = cols_far.reshape(3, 2 * pair)[::2]
        heads = jnp.concatenate([cols_own, cols_far[:, pair:pair + single]], axis=1)
        heads_far = jnp.concatenate([cols_far[:, :pair], cols_far[:, pair + single:]], axis=1)
        n_recv = to_core(n_send)
        d_img, d_txt, sums_one = norm_one(
            dims, order, n_keep, n_recv, dattended, image_states, text_states, vec)
        image_output = gather_rows(fin_img, me)
        text_output = gather_rows(fin_txt, me)
        image_grad = gather_rows(d_img, me)
        text_grad = gather_rows(d_txt, me)
        grad_own = jnp.concatenate([grad_o01, grad_o2], axis=1)
        grad_far = lax.psum_scatter(grad_far, "batch", scatter_dimension=0, tiled=True)
        grad_own = lax.psum_scatter(grad_own, "batch", scatter_dimension=0, tiled=True)
        attn_grad = grad_own.astype(F32) + to_y(grad_far).astype(F32)
        heads = heads + to_y(heads_far)
        own_sums = sum_over(jnp.concatenate([sums_one[:2], own_sums]), "mp")
        flat = jnp.concatenate([own_sums.reshape(-1), heads.reshape(-1), up_sums.reshape(-1)])
        count = flat.shape[0]
        flat = jnp.pad(flat, (0, -count % 1024)).reshape(-1, 128)
        flat = sum_over(flat, "batch").reshape(-1)[:count]
        done = own_sums.shape[0]
        own_sums = mine(flat[:done * model].reshape(done, model), 1)
        heads = flat[done * model:done * model + 2 * local].reshape(2, local)
        grad_expert_up_bias = flat[done * model + 2 * local:].reshape(up_sums.shape)
    attn_grad = jnp.concatenate(
        [attn_grad[:, :4 * pair].reshape(cols, 4, pair), attn_grad[:, 4 * pair:].reshape(cols, 4, single)], axis=2)
    grad_query_key_value = attn_grad[:, :3]
    grad_output_weight = jnp.transpose(attn_grad[:, 3])
    return (
        image_output,
        text_output,
        contrast_loss,
        image_grad,
        text_grad,
        own_sums[0],
        own_sums[1],
        grad_query_key_value,
        heads,
        grad_output_weight,
        own_sums[7],
        own_sums[6],
        own_sums[2:4],
        own_sums[4:6],
        grad_expert_up,
        grad_expert_up_bias,
        grad_expert_down,
        own_sums[9:11],
        own_sums[8],
        mine(grad_head_gain, 1),
        mine(grad_head_shift, 1),
        grad_head_weight,
        grad_logit_scale,
    )


def solution(mesh):
    return jax.shard_map(
        per_device,
        mesh=mesh,
        in_specs=(
            P("batch", None, None),
            P("batch", None, None),
            P("batch"),
            P("batch", None, None),
            P("batch", None, None),
            P(),
            P(),
            P(None, None, "mp"),
            P(None, "mp"),
            P("mp", None),
            P(),
            P(),
            P(),
            P(),
            P(None, None, "mp"),
            P(None, "mp"),
            P(None, "mp", None),
            P(),
            P(),
            P(),
            P(),
            P(),
            P(),
        ),
        out_specs=(
            P("batch", None, None),
            P("batch", None, None),
            P(),
            P("batch", None, None),
            P("batch", None, None),
            P("batch"),
            P("batch"),
            P("batch", None, "mp"),
            P(None, "mp"),
            P("mp", "batch"),
            P("batch"),
            P("batch"),
            P(None, "batch"),
            P(None, "batch"),
            P(None, "batch", "mp"),
            P(None, "mp"),
            P(None, "mp", "batch"),
            P(None, "batch"),
            P("batch"),
            P(None, "batch"),
            P(None, "batch"),
            P(None, "batch", None),
            P(),
        ),
        check_vma=False,
    )
```

```python
import functools
from typing import NamedTuple

import jax
import jax.numpy as jnp
from jax import lax
from jax.experimental import pallas as pl
from jax.experimental.pallas import tpu as pltpu
from jax.sharding import PartitionSpec as P

HEAD_DIM = 64
F32 = jnp.float32
BF16 = jnp.bfloat16
NEG = -1e9
EPS = 1e-5
ORDER = (0, 2, 1, 3)

VMEM_LIMIT = 60 * 1024 * 1024


def params(**kw):
    return pltpu.CompilerParams(vmem_limit_bytes=VMEM_LIMIT, **kw)


def up16(n):
    return -(-n // 16) * 16


def dot(a, b):
    return jnp.dot(a, b, preferred_element_type=F32)


def dot_t(a, b):
    return lax.dot_general(a, b, (((1,), (1,)), ((), ())), preferred_element_type=F32)


def t_dot(a, b):
    return lax.dot_general(a, b, (((0,), (0,)), ((), ())), preferred_element_type=F32)


def normalise(x):
    c = x - jnp.mean(x, axis=-1, keepdims=True)
    v = jnp.mean(c * c, axis=-1, keepdims=True)
    r = lax.rsqrt(v + EPS)
    return c * r, r


def norm_back(n, r, dn):
    a = jnp.mean(dn, axis=-1, keepdims=True)
    b = jnp.mean(dn * n, axis=-1, keepdims=True)
    return (dn - a - n * b) * r


def gelu_parts(u):
    big = 0.5 * (1.0 + lax.erf(u * 0.7071067811865476))
    small = 0.3989422804014327 * jnp.exp(-0.5 * u * u)
    return big, small


def gelu_low(u):
    return (u * (0.5 * (1.0 + lax.erf(u * 0.7071067811865476)))).astype(BF16)


def softmax_rows(scores):
    m = jnp.max(scores, axis=-1, keepdims=True)
    e = jnp.exp(scores - m)
    return e * (1.0 / jnp.sum(e, axis=-1, keepdims=True))


def tie(value, *after):
    return lax.optimization_barrier((value,) + after)[0]


def load_rows(dims, p, img, txt, rows):
    rows[0:dims.patches, :] = img[p].astype(F32)
    rows[dims.ip:dims.ip + dims.caption, :] = txt[p].astype(F32)


def spec_whole(a):
    return pl.BlockSpec(a.shape, lambda *_: (0,) * a.ndim)


class Dims(NamedTuple):
    patches: int
    caption: int
    ip: int
    tp: int
    slab: int
    quarter: int
    local: int


GAIN1, SHIFT1, A_SCALE, A_BIAS, GAIN2, SHIFT2, F_SCALE, F_BIAS, H_GAIN, H_SHIFT = 0, 1, 2, 3, 4, 6, 8, 9, 11, 13


def vector(table, at, count=1):
    return table[at:at + count, :]


def copy_rows(dst, at, src, start, count):
    dst[at:at + count, :] = src[start:start + count, :]


def parts_of(dims):
    return 2 * HEAD_DIM, HEAD_DIM


def key_tail(dims, length):
    at = dims.patches // 16 * 16
    return ((0, dims.ip, at, dims.patches), (dims.ip, dims.slab, 0, length))


def hide(scores, start, limit):
    if start >= scores.shape[0]:
        return scores
    tail = scores[start:]
    at = start + lax.broadcasted_iota(jnp.int32, (tail.shape[0], 1), 0)
    tail = jnp.where(at < limit, tail, NEG)
    return tail if start == 0 else jnp.concatenate([scores[:start], tail], axis=0)


def split_pair(value):
    low = lax.broadcasted_iota(jnp.int32, (1, 128), 1) < HEAD_DIM
    zero = jnp.zeros_like(value)
    return jnp.concatenate([jnp.where(low, value, zero), jnp.where(low, zero, value)], axis=0)


def join_pair(value):
    low = lax.broadcasted_iota(jnp.int32, (1, 128), 1) < HEAD_DIM
    half = value.shape[0] // 2
    return jnp.where(low, value[:half], value[half:])


def softmax_keys(scores):
    e = jnp.exp(scores - jnp.max(scores, axis=0, keepdims=True))
    return e * (1.0 / jnp.sum(e, axis=0, keepdims=True))


def pair_weights(q, k, start, limit):
    return softmax_keys(hide(dot_t(k, split_pair(q)), start, limit))


def scaled(q):
    return q * jnp.asarray(HEAD_DIM ** -0.5, BF16)


def attend_tiles(dims, lens, quarter_at, qkv, mixed):
    tiles = mixed.shape[-1] // 128

    def one_pair(p, c):
        length = lens[quarter_at * dims.quarter + p]
        for lo, hi, start, limit in key_tail(dims, length):
            for g in range(tiles):
                q, k, v = [qkv[p, lo:hi, (t * tiles + g) * 128:(t * tiles + g + 1) * 128] for t in range(3)]
                w = pair_weights(scaled(q), k, start, limit).astype(BF16)
                mixed[p, lo:hi, g * 128:(g + 1) * 128] = join_pair(t_dot(w, v)).astype(BF16)
        return c

    lax.fori_loop(0, dims.quarter, one_pair, 0)


def attend_own_kernel(dims, order, lens, img, txt, vec, bias, wo, normed, qkv, rest, mixed, rows, w, b):
    i = pl.program_id(0)
    local = dims.local
    two, one_head = parts_of(dims)

    @pl.when(i == 0)
    def _():
        rows[...] = jnp.zeros_like(rows)
        w[...] = jnp.zeros_like(w)
        b[...] = jnp.zeros_like(b)
        for t in range(3):
            copy_rows(w, t * 2 * two, wo, t * local, local)
        b[0:1, 0:local] = bias[0:1, :]
        b[0:1, 4 * two:4 * two + local] = bias[1:2, :]

    def one_norm(p, c):
        load_rows(dims, p, img, txt, rows)
        n, _ = normalise(rows[...])
        normed[p] = (n * vector(vec, GAIN1) + vector(vec, SHIFT1)).astype(BF16)
        return c

    lax.fori_loop(0, dims.quarter, one_norm, 0)
    model = normed.shape[-1]
    proj = (dot_t(normed[...].reshape(dims.quarter * dims.slab, model), w[...]) + b[0:1, :]).astype(BF16)
    proj = proj.reshape(dims.quarter, dims.slab, 6 * two)
    for t in range(3):
        qkv[:, :, t * two:(t + 1) * two] = proj[:, :, 2 * t * two:(2 * t + 1) * two]
        rest[:, :, t * two:(t + 1) * two] = proj[:, :, (2 * t + 1) * two:(2 * t + 2) * two]
    attend_tiles(dims, lens, order[i], qkv, mixed)


def attend_own(dims, order, lens, img, txt, vec, bias, wo):
    model = img.shape[-1]
    pairs = 4 * dims.quarter
    block = lambda cols: pl.BlockSpec((dims.quarter, dims.slab, cols), lambda i, o, n: (i, 0, 0))
    shape = lambda cols: jax.ShapeDtypeStruct((pairs, dims.slab, cols), BF16)
    return pl.pallas_call(
        functools.partial(attend_own_kernel, dims),
        grid_spec=pltpu.PrefetchScalarGridSpec(
            num_scalar_prefetch=2,
            grid=(4,),
            in_specs=[
                pl.BlockSpec((dims.quarter, dims.patches, model), lambda i, o, n: (o[i], 0, 0)),
                pl.BlockSpec((dims.quarter, dims.caption, model), lambda i, o, n: (o[i], 0, 0)),
                spec_whole(vec), spec_whole(bias), spec_whole(wo),
            ],
            out_specs=[block(model), block(384), block(384), block(128)],
            scratch_shapes=[pltpu.VMEM((dims.slab, model), F32), pltpu.VMEM((768, model), BF16),
                            pltpu.VMEM((8, 768), F32)],
        ),
        out_shape=[shape(model), shape(384), shape(384), shape(128)],
        compiler_params=params(),
        cost_estimate=pl.CostEstimate(
            flops=1536 * pairs * dims.slab * model, bytes_accessed=30_000_000, transcendentals=0),
        name="attend_own",
    )(order, lens, img, txt, vec, bias, wo)


def attend_far_kernel(dims, order, lens, normed, rest, own, bias, wo, wf, qkv, mixed, keep, send, w, ow, b):
    i = pl.program_id(0)
    local = dims.local
    two, one_head = parts_of(dims)
    count = dims.quarter * dims.slab
    model = normed.shape[-1]

    @pl.when(i == 0)
    def _():
        w[...] = jnp.zeros_like(w)
        b[...] = jnp.zeros_like(b)
        for t in range(3):
            copy_rows(w, t * 2 * two, wf, t * local, two)
            copy_rows(w, t * 2 * two + two + one_head, wf, t * local + two, one_head)
        for t, at in ((0, 0), (1, 4 * two)):
            b[0:1, at:at + two] = bias[t:t + 1, 0:two]
            b[0:1, at + two + one_head:at + 2 * two] = bias[t:t + 1, two:]
        copy_rows(ow, 0, wo, 3 * local, two)
        copy_rows(ow, two, wf, 3 * local, two)
        copy_rows(ow, 2 * two, wo, 3 * local + two, one_head)
        copy_rows(ow, 2 * two + one_head, wf, 3 * local + two, one_head)

    proj = (dot_t(normed[...].reshape(count, model), w[...]) + b[0:1, :]).astype(BF16)
    proj = proj.reshape(dims.quarter, dims.slab, 6 * two)
    for t in range(3):
        at = 2 * t * two
        qkv[:, :, at:at + two] = proj[:, :, at:at + two]
        qkv[:, :, at + two:at + 2 * two] = proj[:, :, at + two:at + 2 * two] + rest[:, :, t * two:(t + 1) * two]
    attend_tiles(dims, lens, order[(i + 2) % 4], qkv, mixed)
    part = dot(own[...].reshape(count, two), ow[0:two, :])
    part = part + dot(mixed[...].reshape(count, 2 * two), ow[two:, :])
    part = part.astype(BF16).reshape(dims.quarter, dims.slab, model)

    @pl.when(i < 2)
    def _():
        send[...] = part

    @pl.when(i >= 2)
    def _():
        keep[...] = part


def attend_far(dims, order, lens, normed, rest, own, bias, wo, wf):
    model = normed.shape[-1]
    pairs = 4 * dims.quarter
    at = lambda i: (i + 2) % 4
    block = lambda cols, f: pl.BlockSpec((dims.quarter, dims.slab, cols), lambda i, o, n: (f(i), 0, 0))
    shape = lambda count, cols: jax.ShapeDtypeStruct((count, dims.slab, cols), BF16)
    return pl.pallas_call(
        functools.partial(attend_far_kernel, dims),
        grid_spec=pltpu.PrefetchScalarGridSpec(
            num_scalar_prefetch=2,
            grid=(4,),
            in_specs=[
                block(model, at), block(384, at), block(128, at),
                spec_whole(bias), spec_whole(wo), spec_whole(wf),
            ],
            out_specs=[
                block(768, at), block(256, at),
                block(model, lambda i: jnp.maximum(i - 2, 0)), block(model, lambda i: jnp.minimum(i, 1)),
            ],
            scratch_shapes=[pltpu.VMEM((768, model), BF16), pltpu.VMEM((384, model), BF16),
                            pltpu.VMEM((8, 768), F32)],
        ),
        out_shape=[
            shape(pairs, 768), shape(pairs, 256),
            shape(2 * dims.quarter, model), shape(2 * dims.quarter, model),
        ],
        compiler_params=params(),
        cost_estimate=pl.CostEstimate(
            flops=2304 * pairs * dims.slab * model, bytes_accessed=30_000_000, transcendentals=0),
        name="attend_far",
    )(order, lens, normed, rest, own, bias, wo, wf)


def residual_kernel(dims, order, keep, recv, img, txt, vec, attended, attn, expert, cls, rows):
    i = pl.program_id(0)
    ip = dims.ip

    @pl.when(i == 0)
    def _():
        rows[...] = jnp.zeros_like(rows)
        cls[...] = jnp.zeros_like(cls)

    load_rows(dims, 0, img, txt, rows)
    a = keep[0].astype(F32) + recv[0].astype(F32)
    x = rows[...] + vector(vec, A_SCALE) * (a + vector(vec, A_BIAS))
    n, _ = normalise(x)
    e_img = n[0:ip] * vector(vec, GAIN2) + vector(vec, SHIFT2)
    e_txt = n[ip:] * vector(vec, GAIN2 + 1) + vector(vec, SHIFT2 + 1)
    expert[0, 0:ip, :] = e_img.astype(BF16)
    expert[0, ip:, :] = e_txt.astype(BF16)
    for j, v in enumerate((x[0:1], x[ip:ip + 1], e_img[0:1], e_txt[0:1])):
        cls[j, pl.ds(i, 1), :] = v

    @pl.when(i < dims.quarter)
    def _():
        attended[0] = x
        attn[0] = a


def residual(dims, order, keep, recv, img, txt, vec):
    model = img.shape[-1]
    quarter = dims.quarter
    block = pl.BlockSpec((1, dims.slab, model), lambda i, o: (i, 0, 0))
    pair = lambda i, o: (o[i // quarter] * quarter + i % quarter, 0, 0)
    return pl.pallas_call(
        functools.partial(residual_kernel, dims),
        grid_spec=pltpu.PrefetchScalarGridSpec(
            num_scalar_prefetch=1,
            grid=(2 * quarter,),
            in_specs=[
                block, block,
                pl.BlockSpec((1, dims.patches, model), pair),
                pl.BlockSpec((1, dims.caption, model), pair),
                spec_whole(vec),
            ],
            out_specs=[
                pl.BlockSpec((1, dims.slab, model), lambda i, o: (jnp.minimum(i, quarter - 1), 0, 0)),
                pl.BlockSpec((1, dims.slab, model), lambda i, o: (jnp.minimum(i, quarter - 1), 0, 0)),
                block,
                pl.BlockSpec((4, 8, model), lambda i, o: (0, 0, 0)),
            ],
            scratch_shapes=[pltpu.VMEM((dims.slab, model), F32)],
        ),
        out_shape=[
            jax.ShapeDtypeStruct((quarter, dims.slab, model), F32),
            jax.ShapeDtypeStruct((quarter, dims.slab, model), F32),
            jax.ShapeDtypeStruct((2 * quarter, dims.slab, model), BF16),
            jax.ShapeDtypeStruct((4, 8, model), F32),
        ],
        compiler_params=params(),
        cost_estimate=pl.CostEstimate(flops=40_000_000, bytes_accessed=20_000_000, transcendentals=0),
        name="residual",
    )(order, keep, recv, img, txt, vec)


def expert_kernel(dims, seq, peer, own, img, txt, vec, up, up_bias, down,
                  act, dup, ddown, d_send, d_keep, x_send, x_keep, bias_grad, cot, ins, rows):
    ip, slab, quarter = dims.ip, dims.slab, dims.quarter
    i = pl.program_id(0)
    model = own.shape[-1]

    @pl.when(i == 0)
    def _():
        rows[...] = jnp.zeros_like(rows)
        bias_grad[...] = jnp.zeros_like(bias_grad)
        cot[...] = jnp.zeros_like(cot)
        ins[...] = peer[...]

    @pl.when(i == 1)
    def _():
        ins[...] = own[...]

    at = lax.broadcasted_iota(jnp.int32, (slab, 1), 0)
    inner = (at != 0) & (at != ip)

    def one(p, c):
        load_rows(dims, p, img, txt, rows)
        cot[0, pl.ds(8 * i + p, 1), :] = rows[0:1, :]
        cot[1, pl.ds(8 * i + p, 1), :] = rows[ip:ip + 1, :]
        ddown[p] = jnp.where(inner, rows[...] * vector(vec, F_SCALE), 0.0).astype(BF16)
        return c

    lax.fori_loop(0, quarter, one, 0)
    for m, lo, hi in ((0, 0, ip), (1, ip, slab)):
        count = quarter * (hi - lo)
        e = ins[:, lo:hi, :].reshape(count, model)
        u = dot(e, up[m]) + up_bias[m:m + 1]
        big, small = gelu_parts(u)
        a = (u * big).astype(BF16)
        act[:, lo:hi, :] = a.reshape(quarter, hi - lo, -1)
        slope = big + u * small
        d = dot(a, down[m]).astype(BF16).reshape(quarter, hi - lo, model)
        g = ddown[:, lo:hi, :].reshape(count, model)
        du = dot_t(g, down[m]) * slope
        bias_grad[m:m + 1, :] += jnp.sum(du, axis=0, keepdims=True)
        low = du.astype(BF16)
        dup[:, lo:hi, :] = low.reshape(quarter, hi - lo, -1)
        x = dot_t(low, up[m]).astype(BF16).reshape(quarter, hi - lo, model)

        @pl.when(i == 0)
        def _():
            d_send[:, lo:hi, :] = d
            x_send[:, lo:hi, :] = x

        @pl.when(i == 1)
        def _():
            d_keep[:, lo:hi, :] = d
            x_keep[:, lo:hi, :] = x


def experts(dims, name, half, seq, peer, own, img, txt, vec, up, up_bias, down):
    model = own.shape[-1]
    hidden = up.shape[-1]
    slab, quarter = dims.slab, dims.quarter
    fixed = pl.BlockSpec((quarter, slab, model), lambda i, o: (half, 0, 0))
    first = pl.BlockSpec((quarter, slab, model), lambda i, o: (0, 0, 0))
    step = lambda cols: pl.BlockSpec((quarter, slab, cols), lambda i, o: (i, 0, 0))
    shape = lambda n, cols: jax.ShapeDtypeStruct((n * quarter, slab, cols), BF16)
    return pl.pallas_call(
        functools.partial(expert_kernel, dims),
        grid_spec=pltpu.PrefetchScalarGridSpec(
            num_scalar_prefetch=1,
            grid=(2,),
            in_specs=[
                fixed, fixed,
                pl.BlockSpec((quarter, dims.patches, model), lambda i, o: (o[i], 0, 0)),
                pl.BlockSpec((quarter, dims.caption, model), lambda i, o: (o[i], 0, 0)),
                spec_whole(vec), spec_whole(up), spec_whole(up_bias), spec_whole(down),
            ],
            out_specs=[
                step(hidden), step(hidden), step(model),
                first, first, first, first,
                pl.BlockSpec((2, hidden), lambda i, o: (0, 0)),
                pl.BlockSpec((2, 16, model), lambda i, o: (0, 0, 0)),
            ],
            scratch_shapes=[pltpu.VMEM((quarter, slab, model), BF16), pltpu.VMEM((slab, model), F32)],
        ),
        out_shape=[
            shape(2, hidden), shape(2, hidden), shape(2, model),
            shape(1, model), shape(1, model), shape(1, model), shape(1, model),
            jax.ShapeDtypeStruct((2, hidden), F32),
            jax.ShapeDtypeStruct((2, 16, model), F32),
        ],
        compiler_params=params(),
        cost_estimate=pl.CostEstimate(
            flops=16 * quarter * slab * model * hidden, bytes_accessed=20_000_000, transcendentals=0),
        name=name,
    )(seq, peer, own, img, txt, vec, up, up_bias, down)


def expert_grads_kernel(dims, peer, own, act_a, dup_a, ddn_a, act_b, dup_b, ddn_b, ce, ca, cu, cd, out, acc):
    i = pl.program_id(0)

    def add(e, dup, ddn, act):
        for m, lo, hi in ((0, 0, dims.ip), (1, dims.ip, dims.slab)):
            count = dims.quarter * (hi - lo)
            flat = lambda ref: ref[:, lo:hi, :].reshape(count, -1)
            acc[m] += t_dot(flat(e), flat(dup))
            acc[2 + m] += t_dot(flat(ddn), flat(act))

    @pl.when(i == 0)
    def _():
        for m in range(2):
            acc[m] = t_dot(ce[m], cu[m])
            acc[2 + m] = t_dot(cd[m], ca[m])

    for j, refs in enumerate((
        (peer, dup_a, ddn_a, act_a), (own, dup_a, ddn_a, act_a),
        (peer, dup_b, ddn_b, act_b), (own, dup_b, ddn_b, act_b),
    )):
        @pl.when(i == j)
        def _():
            add(*refs)

    @pl.when(i == 3)
    def _():
        out[...] = acc[...].astype(BF16)


def expert_grads(dims, peer, own, act_a, dup_a, ddn_a, act_b, dup_b, ddn_b, ce, ca, cu, cd):
    model = own.shape[-1]
    hidden = act_a.shape[-1]
    slab, quarter = dims.slab, dims.quarter
    assert hidden == model
    half = pl.BlockSpec((quarter, slab, model), lambda i: (jnp.where(i < 2, 1, 0), 0, 0))
    first = pl.BlockSpec((quarter, slab, hidden), lambda i: (jnp.minimum(i, 1), 0, 0))
    last = pl.BlockSpec((quarter, slab, hidden), lambda i: (jnp.maximum(i - 2, 0), 0, 0))
    return pl.pallas_call(
        functools.partial(expert_grads_kernel, dims),
        grid=(4,),
        in_specs=[half, half, first, first, first, last, last, last] + [spec_whole(v) for v in (ce, ca, cu, cd)],
        out_specs=pl.BlockSpec((4, model, hidden), lambda i: (0, 0, 0)),
        scratch_shapes=[pltpu.VMEM((4, model, hidden), F32)],
        out_shape=jax.ShapeDtypeStruct((4, model, hidden), BF16),
        compiler_params=params(),
        cost_estimate=pl.CostEstimate(
            flops=16 * quarter * slab * model * hidden, bytes_accessed=40_000_000, transcendentals=0),
        name="expert_grads",
    )(peer, own, act_a, dup_a, ddn_a, act_b, dup_b, ddn_b, ce, ca, cu, cd)


def own_row(dims, r, p):
    return 8 * (r // 2) + dims.quarter * (r % 2) + p


def class_forward_kernel(dims, near, far, up, up_bias, down, out, rows):
    for m in range(2):
        e = jnp.concatenate([near[2 + m], far[2 + m]], axis=0).astype(BF16)
        rows[m] = e
        u = dot(e, up[m]) + up_bias[m:m + 1]
        out[m] = dot(gelu_low(u), down[m])


def class_forward(dims, near, far, up, up_bias, down):
    shape = (2, 16, near.shape[-1])
    return pl.pallas_call(
        functools.partial(class_forward_kernel, dims),
        out_shape=[jax.ShapeDtypeStruct(shape, F32), jax.ShapeDtypeStruct(shape, BF16)],
        compiler_params=params(),
        cost_estimate=pl.CostEstimate(flops=200_000_000, bytes_accessed=5_000_000, transcendentals=0),
        name="class_forward",
    )(near, far, up, up_bias, down)


def class_final_kernel(dims, order, near, far, d0, d1, d2, d3, vec, out):
    q = dims.quarter
    for m in range(2):
        out[m] = jnp.zeros(out.shape[1:], F32)
        for r in range(4):
            half, at = (near, far)[r // 2], q * (r % 2)
            for p in range(q):
                rows = [d[m, own_row(dims, s, p):own_row(dims, s, p) + 1, :]
                        for d, s in ((d0, r), (d1, r ^ 2), (d2, r ^ 1), (d3, r ^ 3))]
                total = (rows[0] + rows[1]) + (rows[2] + rows[3])
                x = half[m, at + p:at + p + 1, :] + vector(vec, F_SCALE) * (total + vector(vec, F_BIAS + m))
                out[m, pl.ds(4 * order[r] + p, 1), :] = x


def class_final(dims, order, near, far, parts, vec):
    shape = (2, 16, near.shape[-1])
    args = (near, far) + tuple(parts) + (vec,)
    return pl.pallas_call(
        functools.partial(class_final_kernel, dims),
        grid_spec=pltpu.PrefetchScalarGridSpec(
            num_scalar_prefetch=1, grid=(1,),
            in_specs=[spec_whole(v) for v in args],
            out_specs=pl.BlockSpec(shape, lambda i, o: (0, 0, 0)),
        ),
        out_shape=jax.ShapeDtypeStruct(shape, F32),
        compiler_params=params(),
        cost_estimate=pl.CostEstimate(flops=1_000_000, bytes_accessed=1_000_000, transcendentals=0),
        name="class_final",
    )(order, *args)


def class_back_kernel(dims, order, e, cot_a, cot_b, dclass, vec, up, up_bias, down,
                      act, dup, ddown, dexp, bias_grad, dcls, rows):
    q = dims.quarter
    rows[...] = jnp.zeros_like(rows)
    dcls[...] = jnp.zeros_like(dcls)
    for m in range(2):
        for r in range(4):
            cot, base = (cot_b, cot_a)[r % 2], 8 * (1 - r // 2)
            for p in range(q):
                d = dclass[m, pl.ds(4 * order[r] + p, 1), :]
                at = own_row(dims, r, p)
                rows[m, at:at + 1, :] = cot[m, base + p:base + p + 1, :] + d
                if r == 0:
                    dcls[p, m:m + 1, :] = d
        u = dot(e[m], up[m]) + up_bias[m:m + 1]
        big, small = gelu_parts(u)
        act[m] = (u * big).astype(BF16)
        g = (rows[m] * vector(vec, F_SCALE)).astype(BF16)
        ddown[m] = g
        du = dot_t(g, down[m]) * (big + u * small)
        bias_grad[m:m + 1, :] = jnp.sum(du, axis=0, keepdims=True)
        low = du.astype(BF16)
        dup[m] = low
        dexp[m] = dot_t(low, up[m])


def class_back(dims, order, e, cot_a, cot_b, dclass, vec, up, up_bias, down):
    hidden, model = up.shape[-1], e.shape[-1]
    args = (e, cot_a, cot_b, dclass, vec, up, up_bias, down)
    shapes = [((2, 16, hidden), BF16), ((2, 16, hidden), BF16), ((2, 16, model), BF16), ((2, 16, model), F32),
              ((2, hidden), F32), ((dims.quarter, 8, model), F32)]
    return pl.pallas_call(
        functools.partial(class_back_kernel, dims),
        grid_spec=pltpu.PrefetchScalarGridSpec(
            num_scalar_prefetch=1, grid=(1,),
            in_specs=[spec_whole(v) for v in args],
            out_specs=[pl.BlockSpec(s, lambda i, o, n=len(s): (0,) * n) for s, _ in shapes],
            scratch_shapes=[pltpu.VMEM((2, 16, model), F32)],
        ),
        out_shape=[jax.ShapeDtypeStruct(s, t) for s, t in shapes],
        compiler_params=params(),
        cost_estimate=pl.CostEstimate(flops=300_000_000, bytes_accessed=5_000_000, transcendentals=0),
        name="class_back",
    )(order, *args)


def contrast_kernel(dims, total, at, blocks, vec, weight, scale,
                    head_in, dproj, dcls, gains, shifts, scalars, cls, back):
    me = at[0]
    span = blocks[0].shape[0]
    for k, block in enumerate(blocks):
        for j in range(span):
            for m in range(2):
                cls[m, pl.ds(pl.multiple_of(16 * (me ^ (k * span + j)), 16), 16), :] = block[j, m]
    n_rows = cls.shape[1]
    sharp = jnp.exp(scale[...])
    col_at = lax.broadcasted_iota(jnp.int32, (1, n_rows), 1)
    row_at = lax.broadcasted_iota(jnp.int32, (n_rows, 1), 0)
    col_ok = (col_at % 4) < dims.quarter
    row_ok = (row_at % 4) < dims.quarter
    normal, inverse, proj, unit, embed = [], [], [], [], []
    for m in range(2):
        n, r = normalise(cls[m])
        h = (n * vector(vec, H_GAIN + m) + vector(vec, H_SHIFT + m)).astype(BF16)
        head_in[m] = h
        y = dot(h, weight[m])
        u = lax.rsqrt(jnp.sum(y * y, axis=-1, keepdims=True) + 1e-6)
        normal.append(n)
        inverse.append(r)
        proj.append(y)
        unit.append(u)
        embed.append((y * u).astype(BF16))
    ok = row_ok & col_ok
    logits = sharp * dot_t(embed[0], embed[1])
    masked = jnp.where(ok, logits, -1e30)
    row_max = jnp.max(masked, axis=1, keepdims=True)
    row_lse = row_max + jnp.log(jnp.sum(jnp.exp(masked - row_max), axis=1, keepdims=True))
    col_max = jnp.max(masked, axis=0, keepdims=True)
    col_lse = col_max + jnp.log(jnp.sum(jnp.exp(masked - col_max), axis=0, keepdims=True))
    same = (row_at == col_at) & ok
    both = jnp.exp(masked - row_lse) + jnp.exp(masked - col_lse)
    dlogits = jnp.where(ok, jnp.where(same, both - 2.0, both) * (1.0 / (2 * total)), 0.0)
    diagonal = jnp.sum(jnp.where(same, logits, 0.0), axis=1, keepdims=True)
    rows = jnp.where(row_ok, row_lse - 2.0 * diagonal, 0.0)
    cols = jnp.where(col_ok, col_lse, 0.0)
    loss = (jnp.sum(rows, axis=0, keepdims=True) + jnp.sum(cols, axis=1, keepdims=True)) * (1.0 / (2 * total))
    slope = jnp.sum(jnp.sum(dlogits * logits, axis=1, keepdims=True), axis=0, keepdims=True)
    scalars[0:1, :] = jnp.broadcast_to(loss, (1, 128))
    scalars[1:2, :] = jnp.broadcast_to(slope, (1, 128))
    high = lax.Precision.HIGHEST
    wide = [e.astype(F32) for e in embed]
    dembed = [
        sharp * jnp.dot(dlogits, wide[1], precision=high, preferred_element_type=F32),
        sharp * lax.dot_general(dlogits, wide[0], (((0,), (0,)), ((), ())), precision=high,
                                preferred_element_type=F32),
    ]
    for m in range(2):
        u, y, d = unit[m], proj[m], dembed[m]
        dp = (u * d - u * u * u * y * jnp.sum(y * d, axis=-1, keepdims=True)).astype(BF16)
        dproj[m] = dp
        dh = dot_t(dp, weight[m])
        gains[m:m + 1, :] = jnp.sum(dh * normal[m], axis=0, keepdims=True)
        shifts[m:m + 1, :] = jnp.sum(dh, axis=0, keepdims=True)
        back[m] = norm_back(normal[m], inverse[m], dh * vector(vec, H_GAIN + m))
        dcls[m] = back[m, pl.ds(pl.multiple_of(16 * me, 16), 16), :]


def contrast(dims, total, at, blocks, vec, weight, scale):
    model = weight.shape[1]
    rows = 16 * len(blocks) * blocks[0].shape[0]
    args = tuple(blocks) + (vec, weight, scale)
    shapes = [((2, rows, model), BF16), ((2, rows, weight.shape[2]), BF16), ((2, 16, model), F32),
              ((2, model), F32), ((2, model), F32), ((2, 128), F32)]

    def kernel(at, *refs):
        contrast_kernel(dims, total, at, refs[:len(blocks)], *refs[len(blocks):])

    return pl.pallas_call(
        kernel,
        grid_spec=pltpu.PrefetchScalarGridSpec(
            num_scalar_prefetch=1, grid=(1,),
            in_specs=[spec_whole(v) for v in args],
            out_specs=[pl.BlockSpec(s, lambda i, o, n=len(s): (0,) * n) for s, _ in shapes],
            scratch_shapes=[pltpu.VMEM((2, rows, model), F32)] * 2,
        ),
        out_shape=[jax.ShapeDtypeStruct(s, t) for s, t in shapes],
        compiler_params=params(),
        cost_estimate=pl.CostEstimate(flops=1_000_000_000, bytes_accessed=5_000_000, transcendentals=0),
        name="contrast",
    )(at, *args)


def contrast_large(dims, total, at, blocks, vec, weight, scale):
    model = weight.shape[1]
    held = jnp.concatenate(blocks)
    held = held[jnp.arange(held.shape[0]) ^ at[0]]
    rows = jnp.asarray([r for r in range(16) if r % 4 < dims.quarter])
    cls = jnp.transpose(held[:, :, rows], (1, 0, 2, 3)).reshape(2, -1, model)
    gain, shift = vec[H_GAIN:H_GAIN + 2, None], vec[H_SHIFT:H_SHIFT + 2, None]
    n, r = normalise(cls)
    head_in = (n * gain + shift).astype(BF16)
    proj = jnp.einsum("mrc,mce->mre", head_in, weight, preferred_element_type=F32)
    unit = lax.rsqrt(jnp.sum(proj * proj, axis=-1, keepdims=True) + 1e-6)
    embed = (proj * unit).astype(BF16)
    sharp = jnp.exp(scale[0, 0])
    logits = sharp * dot_t(embed[0], embed[1])
    row_lse = jax.nn.logsumexp(logits, axis=1, keepdims=True)
    col_lse = jax.nn.logsumexp(logits, axis=0, keepdims=True)
    dlogits = jnp.exp(logits - row_lse) + jnp.exp(logits - col_lse) - 2.0 * jnp.eye(total, dtype=F32)
    dlogits = dlogits / (2 * total)
    loss = (jnp.sum(row_lse) + jnp.sum(col_lse) - 2.0 * jnp.trace(logits)) / (2 * total)
    slope = jnp.sum(dlogits * logits)
    high = lax.Precision.HIGHEST
    wide = embed.astype(F32)
    dembed = sharp * jnp.stack([
        jnp.dot(dlogits, wide[1], precision=high, preferred_element_type=F32),
        jnp.dot(dlogits.T, wide[0], precision=high, preferred_element_type=F32)])
    dproj = (unit * dembed - unit ** 3 * proj * jnp.sum(proj * dembed, axis=-1, keepdims=True)).astype(BF16)
    dh = jnp.einsum("mre,mce->mrc", dproj, weight, preferred_element_type=F32)
    back = norm_back(n, r, dh * gain)
    pairs = 4 * dims.quarter
    own = lax.dynamic_slice_in_dim(back, at[0] * pairs, pairs, axis=1)
    dcls = jnp.zeros((2, 16, model), F32).at[:, rows].set(own)
    scalars = jnp.broadcast_to(jnp.stack([loss, slope])[:, None], (2, 128))
    return head_in, dproj, dcls, jnp.sum(dh * n, axis=1), jnp.sum(dh, axis=1), scalars


def own_pair(rows_of):
    return lambda i, o: (o[0] * rows_of + i, 0, 0)


def own_call(kernel, dims, name, order, blocks, img, txt, others, outs, scratch):
    model = img.shape[-1]
    block = pl.BlockSpec((1, dims.slab, model), lambda i, o: (i, 0, 0))
    specs = {
        "slab": (block, (dims.quarter, dims.slab, model)),
        "img": (pl.BlockSpec((1, dims.patches, model), lambda i, o: (i, 0, 0)), (dims.quarter, dims.patches, model)),
        "txt": (pl.BlockSpec((1, dims.caption, model), lambda i, o: (i, 0, 0)), (dims.quarter, dims.caption, model)),
        "sums": (pl.BlockSpec((8, model), lambda i, o: (0, 0)), (8, model)),
    }
    return pl.pallas_call(
        functools.partial(kernel, dims),
        grid_spec=pltpu.PrefetchScalarGridSpec(
            num_scalar_prefetch=1,
            grid=(dims.quarter,),
            in_specs=[block] * len(blocks) + [
                pl.BlockSpec((1, dims.patches, model), own_pair(dims.quarter)),
                pl.BlockSpec((1, dims.caption, model), own_pair(dims.quarter)),
            ] + [spec_whole(v) for v in others],
            out_specs=[specs[kind][0] for kind, _ in outs],
            scratch_shapes=[pltpu.VMEM((dims.slab, model), F32)] * scratch,
        ),
        out_shape=[jax.ShapeDtypeStruct(specs[kind][1], dtype) for kind, dtype in outs],
        compiler_params=params(),
        cost_estimate=pl.CostEstimate(flops=40_000_000, bytes_accessed=15_000_000, transcendentals=0),
        name=name,
    )(order, *blocks, img, txt, *others)


def start_own(rows, sums):
    @pl.when(pl.program_id(0) == 0)
    def _():
        rows[...] = jnp.zeros_like(rows)
        sums[...] = jnp.zeros_like(sums)


def add_class(dims, dcls, rows):
    i = pl.program_id(0)
    rows[0:1, :] += dcls[i, 0:1, :]
    rows[dims.ip:dims.ip + 1, :] += dcls[i, 1:2, :]


def final_kernel(dims, order, keep, recv, far, attended, img, txt, dcls, vec, fin_img, fin_txt, sums, rows):
    start_own(rows, sums)
    load_rows(dims, 0, img, txt, rows)
    add_class(dims, dcls, rows)
    for m, lo, hi in ((0, 0, dims.ip), (1, dims.ip, dims.slab)):
        b = keep[0, lo:hi].astype(F32) + recv[0, lo:hi].astype(F32) + far[0, lo:hi].astype(F32)
        b = b + vector(vec, F_BIAS + m)
        f = attended[0, lo:hi, :] + vector(vec, F_SCALE) * b
        if m == 0:
            fin_img[0] = f[0:dims.patches].astype(BF16)
        else:
            fin_txt[0] = f[0:dims.caption].astype(BF16)
        g = rows[lo:hi, :]
        sums[0:1, :] += jnp.sum(g * b, axis=0, keepdims=True)
        sums[1 + m:2 + m, :] += jnp.sum(g, axis=0, keepdims=True) * vector(vec, F_SCALE)


def final_rows(dims, order, keep, recv, far, attended, img, txt, dcls, vec):
    return own_call(final_kernel, dims, "final_rows", order, (keep, recv, far, attended), img, txt,
                    (dcls, vec), (("img", BF16), ("txt", BF16), ("sums", F32)), 1)


def norm_two_kernel(dims, order, keep, recv, far, attended, a_keep, a_recv, img, txt, dcls, x0, x1, x2, x3,
                    vec, dattended, dattn, sums, rows, ups):
    i = pl.program_id(0)
    start_own(rows, sums)
    load_rows(dims, 0, img, txt, rows)
    add_class(dims, dcls, rows)
    ups[...] = keep[0].astype(F32) + recv[0].astype(F32) + far[0].astype(F32)
    for m, at in ((0, 0), (1, dims.ip)):
        extra = [x[m, pl.ds(own_row(dims, r, 0) + i, 1), :] for x, r in ((x0, 0), (x1, 2), (x2, 1), (x3, 3))]
        ups[at:at + 1, :] += (extra[0] + extra[1]) + (extra[2] + extra[3])
    for m, lo, hi in ((0, 0, dims.ip), (1, dims.ip, dims.slab)):
        n, r = normalise(attended[0, lo:hi, :])
        dy = ups[lo:hi, :]
        sums[m:m + 1, :] += jnp.sum(dy * n, axis=0, keepdims=True)
        sums[2 + m:3 + m, :] += jnp.sum(dy, axis=0, keepdims=True)
        d = rows[lo:hi, :] + norm_back(n, r, dy * vector(vec, GAIN2 + m))
        dattended[0, lo:hi, :] = d
        sd = d * vector(vec, A_SCALE)
        dattn[0, lo:hi, :] = sd.astype(BF16)
        a = a_keep[0, lo:hi, :].astype(F32) + a_recv[0, lo:hi, :].astype(F32) + vector(vec, A_BIAS)
        sums[4:5, :] += jnp.sum(d * a, axis=0, keepdims=True)
        sums[5:6, :] += jnp.sum(sd, axis=0, keepdims=True)


def norm_two(dims, order, keep, recv, far, attended, a_keep, a_recv, img, txt, dcls, parts, vec):
    return own_call(norm_two_kernel, dims, "norm_two", order, (keep, recv, far, attended, a_keep, a_recv), img, txt,
                    (dcls,) + tuple(parts) + (vec,), (("slab", F32), ("slab", BF16), ("sums", F32)), 2)


def norm_one_kernel(dims, order, keep, recv, dattended, img, txt, vec, d_img, d_txt, sums, rows):
    start_own(rows, sums)
    load_rows(dims, 0, img, txt, rows)
    n, r = normalise(rows[...])
    dy = keep[0].astype(F32) + recv[0].astype(F32)
    sums[0:1, :] += jnp.sum(dy * n, axis=0, keepdims=True)
    sums[1:2, :] += jnp.sum(dy, axis=0, keepdims=True)
    d = dattended[0] + norm_back(n, r, dy * vector(vec, GAIN1))
    d_img[0] = d[0:dims.patches].astype(BF16)
    d_txt[0] = d[dims.ip:dims.ip + dims.caption].astype(BF16)


def norm_one(dims, order, keep, recv, dattended, img, txt, vec):
    return own_call(norm_one_kernel, dims, "norm_one", order, (keep, recv, dattended), img, txt,
                    (vec,), (("img", BF16), ("txt", BF16), ("sums", F32)), 1)


def back_step(dims, tiles, lens, whose, dattn, normed, qkv, mixed, dmixed, dqkv, acc, col_sums, w, ow):
    quarter, slab = dims.quarter, dims.slab
    count, width = quarter * slab, tiles * 128
    model = normed.shape[-1]
    d_rows = dattn[...].reshape(count, model)
    dmixed[...] = dot_t(d_rows, ow[...]).astype(BF16).reshape(quarter, slab, width)

    def one_pair(p, c):
        length = lens[whose * quarter + p]
        for lo, hi, start, limit in key_tail(dims, length):
            for g in range(tiles):
                at = [slice((t * tiles + g) * 128, (t * tiles + g + 1) * 128) for t in range(3)]
                q, k, v = [qkv[p, lo:hi, c] for c in at]
                q = scaled(q)
                qq = split_pair(q)
                dd = split_pair(dmixed[p, lo:hi, g * 128:(g + 1) * 128])
                w_ = softmax_keys(hide(dot_t(k, qq), start, limit))
                dw = dot_t(v, dd)
                dqkv[p, lo:hi, at[2]] = dot(w_.astype(BF16), dd).astype(BF16)
                ds = (w_ * (dw - jnp.sum(w_ * dw, axis=0, keepdims=True))).astype(BF16)
                dqkv[p, lo:hi, at[1]] = dot(ds, qq).astype(BF16)
                dqkv[p, lo:hi, at[0]] = (join_pair(t_dot(ds, k)) * HEAD_DIM ** -0.5).astype(BF16)
        return c

    lax.fori_loop(0, quarter, one_pair, 0)
    dp = dqkv[...].reshape(count, 3 * width)
    part = dot(dp, w[...])
    acc[:, 0:3 * width] += t_dot(normed[...].reshape(count, model), dp)
    acc[:, 3 * width:] += t_dot(d_rows, mixed[...].reshape(count, width))
    col_sums[...] += jnp.sum(dp.astype(F32), axis=0, keepdims=True)
    return part


def attend_back_kernel(dims, far, order, lens, d_own, d_peer, normed, qkv, mixed, wq, wo, wf, *refs):
    if not far:
        prior_keep, prior_send, *refs = refs
    keep, send, grad, *refs = refs
    if far:
        grad_rest, *refs = refs
    col_sums, dattn, dmixed, dqkv, acc, w, ow = refs
    i = pl.program_id(0)
    slab, quarter, local = dims.slab, dims.quarter, dims.local
    two, one_head = parts_of(dims)
    tiles = 2 if far else 1
    width = tiles * two
    count = quarter * slab
    model = normed.shape[-1]

    @pl.when(i == 0)
    def _():
        dattn[...] = d_own[...]
        acc[...] = jnp.zeros_like(acc)
        col_sums[...] = jnp.zeros_like(col_sums)
        for t in range(4):
            dst, at = (w, t * width) if t < 3 else (ow, 0)
            own, start = (wq, t * local) if t < 3 else (wo, 0)
            if far:
                copy_rows(dst, at, wf, t * local, two)
                copy_rows(dst, at + two, own, start + two, one_head)
                copy_rows(dst, at + two + one_head, wf, t * local + two, one_head)
            else:
                copy_rows(dst, at, own, start, two)

    @pl.when(i == 1)
    def _():
        dattn[...] = d_peer[...]

    part = back_step(dims, tiles, lens, order[2 * i], dattn, normed, qkv, mixed,
                     dmixed, dqkv, acc, col_sums, w, ow)

    @pl.when(i == 0)
    def _():
        prior = 0.0 if far else prior_keep[...].reshape(count, model).astype(F32)
        keep[...] = (part + prior).astype(BF16).reshape(quarter, slab, model)

    @pl.when(i == 1)
    def _():
        prior = 0.0 if far else prior_send[...].reshape(count, model).astype(F32)
        send[...] = (part + prior).astype(BF16).reshape(quarter, slab, model)
        for t in range(4):
            grad[:, t * two:(t + 1) * two] = acc[:, t * width:t * width + two].astype(BF16)
            if far:
                at = t * width + two
                to = 4 * two + t * one_head
                grad[:, to:to + one_head] = acc[:, at + one_head:at + two].astype(BF16)
                grad_rest[:, t * one_head:(t + 1) * one_head] = acc[:, at:at + one_head].astype(BF16)


def attend_back(dims, far, order, lens, d_own, d_peer, normed, qkv, mixed, wq, wo, wf, prior=()):
    model = normed.shape[-1]
    slab, quarter = dims.slab, dims.quarter
    width = 256 if far else 128
    one = pl.BlockSpec((quarter, slab, model), lambda i, o, n: (0, 0, 0))
    stride = normed.shape[0] // (2 * quarter)
    step = lambda cols: pl.BlockSpec((quarter, slab, cols), lambda i, o, n: (stride * i, 0, 0))
    grads = (768, 256) if far else (512,)
    specs = [one, one] + [pl.BlockSpec((model, n), lambda i, o, n_: (0, 0)) for n in grads]
    specs += [pl.BlockSpec((1, 3 * width), lambda i, o, n: (0, 0))]
    shapes = [
        jax.ShapeDtypeStruct((quarter, slab, model), BF16),
        jax.ShapeDtypeStruct((quarter, slab, model), BF16),
    ] + [jax.ShapeDtypeStruct((model, n), BF16) for n in grads] + [jax.ShapeDtypeStruct((1, 3 * width), F32)]
    scratch = [
        pltpu.VMEM((quarter, slab, model), BF16),
        pltpu.VMEM((quarter, slab, width), BF16),
        pltpu.VMEM((quarter, slab, 3 * width), BF16),
        pltpu.VMEM((model, 4 * width), F32),
        pltpu.VMEM((3 * width, model), BF16),
        pltpu.VMEM((width, model), BF16),
    ]
    return pl.pallas_call(
        functools.partial(attend_back_kernel, dims, far),
        grid_spec=pltpu.PrefetchScalarGridSpec(
            num_scalar_prefetch=2,
            grid=(2,),
            in_specs=[one, one, step(model), step(3 * width), step(width), spec_whole(wq), spec_whole(wo),
                      spec_whole(wf)] + [one] * len(prior),
            out_specs=specs,
            scratch_shapes=scratch,
        ),
        out_shape=shapes,
        compiler_params=params(),
        cost_estimate=pl.CostEstimate(
            flops=32 * quarter * slab * model * width, bytes_accessed=20_000_000, transcendentals=0),
        name="attend_back_far" if far else "attend_back_own",
    )(order, lens, d_own, d_peer, normed, qkv, mixed, wq, wo, wf, *prior)


def swap(value, axis, bit):
    size = lax.axis_size(axis)
    return lax.ppermute(value, axis, [(j, j ^ bit) for j in range(size)])


def to_core(value):
    return swap(value, "mp", 1)


def to_y(value):
    return swap(value, "mp", 2)


def from_others(value, axis, first, count):
    return [value] + [swap(value, axis, k * first) for k in range(1, count)]


def add_tree(parts):
    while len(parts) > 1:
        parts = [a + b for a, b in zip(parts[::2], parts[1::2])]
    return parts[0]


def sum_over(value, axis):
    first = 1
    while first < lax.axis_size(axis):
        count = min(8, lax.axis_size(axis) // first)
        value = add_tree(from_others(value, axis, first, count))
        first *= count
    return value


def gather_batch(value):
    parts = [value]
    first = 1
    size = lax.axis_size("batch")
    while first < size:
        count = min(8, size // first)
        whole = jnp.concatenate(parts) if len(parts) > 1 else parts[0]
        parts = from_others(whole, "batch", first, count)
        first *= count
    return parts


def gather_rows(own, me):
    near = jnp.stack([own, to_y(own)])
    far = to_core(near)
    out = jnp.zeros((4,) + own.shape, own.dtype)
    for r, value in enumerate((near[0], near[1], far[0], far[1])):
        out = lax.dynamic_update_slice(out, value[None], (me ^ ORDER[r],) + (0,) * own.ndim)
    return out.reshape((4 * own.shape[0],) + own.shape[1:])


def add_low(a, b):
    return (a.astype(F32) + b.astype(F32)).astype(BF16)


MESH = pl.DeviceIdType.MESH


class Place:
    def __init__(self):
        self.b, self.m = lax.axis_index("batch"), lax.axis_index("mp")
        self.z, self.x = self.b // 2, self.b % 2
        self.y, self.c = self.m // 2, self.m % 2
        self.core = (self.b, 2 * self.y + 1 - self.c)
        self.near = (self.b, 2 * (1 - self.y) + self.c)
        self.across = (self.b, 2 * (1 - self.y) + 1 - self.c)
        self.side = (2 * self.z + 1 - self.x, self.m)
        self.z_pair = self.z + 1 - 2 * (self.z % 2)
        self.z_far = (self.z + 2) % 4
        self.z_rest = (self.z_pair + 2) % 4
        self.paired = (2 * self.z_pair + self.x, self.m)
        self.opposite = (2 * self.z_far + self.x, self.m)
        self.batch = [((self.b + k) % 8, self.m) for k in range(1, 8)]

    def quarter(self, far_y, far_core):
        return 2 * ((self.y + far_y) % 2) + (self.c + far_core) % 2


def meet(peers):
    barrier = pltpu.get_barrier_semaphore()
    for peer in peers:
        pl.semaphore_signal(barrier, inc=1, device_id=peer, device_id_type=MESH)
    pl.semaphore_wait(barrier, len(peers))


def remote(src, dst, send_sem, recv_sem, at, device):
    return pltpu.make_async_remote_copy(
        src_ref=src, dst_ref=dst, send_sem=send_sem.at[at], recv_sem=recv_sem.at[at],
        device_id=device, device_id_type=MESH)


def front_kernel(dims, lens, img, txt, vectors, bias, own_w, own_o,
                 vec, normed, qkv, mixed, qkv_far, mixed_far, far_w, attended, attn, expert, expert_peer, cls, cls_peer,
                 rows, w, w2, ow, b, wf, far_bias, n_all, rest, m_all, m_far, q_own, q_far, a_send, a_recv, e_send, c_recv, held,
                 local_sem, send_sem, recv_sem):
    here = Place()
    i = pl.program_id(0)
    local, quarter, slab, ip = dims.local, dims.quarter, dims.slab, dims.ip
    two, one_head = parts_of(dims)
    count = quarter * slab
    model = img.shape[-1]
    at = i % 4
    whose = here.quarter(at % 2, 1 - at // 2)
    sent_w = [remote(own_w, wf.at[pl.ds(0, 3 * local)], send_sem, recv_sem, 0, here.near),
              remote(own_o, wf.at[pl.ds(3 * local, local)], send_sem, recv_sem, 1, here.near),
              remote(bias, far_bias, send_sem, recv_sem, 2, here.near)]
    sent_a = [remote(a_send.at[j], a_recv.at[j], send_sem, recv_sem, 3 + j, here.core) for j in range(2)]

    def e_over(j):
        return remote(e_send.at[j], expert_peer.at[j], send_sem, recv_sem, 5 + j, here.core)

    def e_here(j):
        return pltpu.make_async_copy(e_send.at[j], expert.at[j], local_sem.at[1 + j])

    sent_c = remote(cls, c_recv, send_sem, recv_sem, 5 + 2 * quarter, here.core)
    keep_w = pltpu.make_async_copy(wf, far_w, local_sem.at[0])
    sent_e = [e_over(j) for j in range(2 * quarter)]
    keep_e = [e_here(j) for j in range(2 * quarter)]

    @pl.when(i == 0)
    def _():
        meet([here.core, here.near])
        for copy in sent_w:
            copy.start()
        fill(vec, vectors)
        rows[...] = jnp.zeros_like(rows)
        b[...] = jnp.zeros_like(b)
        w[...] = jnp.zeros_like(w)
        cls[...] = jnp.zeros_like(cls)
        for t in range(3):
            copy_rows(w, t * 2 * two, own_w, t * local, local)
        b[0:1, 0:local] = bias[0:1, :]
        b[0:1, 4 * two:4 * two + local] = bias[1:2, :]

    def project(weights):
        proj = dot_t(n_all[at].reshape(count, model), weights[...]) + b[0:1, :]
        return proj.astype(BF16).reshape(quarter, slab, 6 * two)

    @pl.when(i < 4)
    def _():
        def one_norm(p, c):
            load_rows(dims, p, img, txt, rows)
            n, _ = normalise(rows[...])
            n_all[at, p] = (n * vector(vec, GAIN1) + vector(vec, SHIFT1)).astype(BF16)
            return c

        lax.fori_loop(0, quarter, one_norm, 0)
        proj = project(w)
        for t in range(3):
            q_own[:, :, t * two:(t + 1) * two] = proj[:, :, 2 * t * two:(2 * t + 1) * two]
            rest[at, :, :, t * two:(t + 1) * two] = proj[:, :, (2 * t + 1) * two:(2 * t + 2) * two]
        attend_tiles(dims, lens, whose, q_own, m_all.at[at])

        @pl.when(i % 2 == 0)
        def _():
            normed[...] = n_all[at]
            qkv[...] = q_own[...]
            mixed[...] = m_all[at]

    @pl.when(i == 4)
    def _():
        for copy in sent_w:
            copy.wait_recv()
        keep_w.start()
        w2[...] = jnp.zeros_like(w2)
        b[...] = jnp.zeros_like(b)
        for t in range(3):
            copy_rows(w2, t * 2 * two, wf, t * local, two)
            copy_rows(w2, t * 2 * two + two + one_head, wf, t * local + two, one_head)
        for t, to in ((0, 0), (1, 4 * two)):
            b[0:1, to:to + two] = far_bias[t:t + 1, 0:two]
            b[0:1, to + two + one_head:to + 2 * two] = far_bias[t:t + 1, two:]
        copy_rows(ow, 0, own_o, 0, two)
        copy_rows(ow, two, wf, 3 * local, two)
        copy_rows(ow, 2 * two, own_o, two, one_head)
        copy_rows(ow, 2 * two + one_head, wf, 3 * local + two, one_head)

    @pl.when(i >= 4)
    def _():
        proj = project(w2)
        for t in range(3):
            to = 2 * t * two
            q_far[:, :, to:to + two] = proj[:, :, to:to + two]
            q_far[:, :, to + two:to + 2 * two] = (
                proj[:, :, to + two:to + 2 * two] + rest[at, :, :, t * two:(t + 1) * two])
        attend_tiles(dims, lens, whose, q_far, m_far)

        @pl.when(i % 2 == 0)
        def _():
            qkv_far[...] = q_far[...]
            mixed_far[...] = m_far[...]

        part = dot(m_all[at].reshape(count, two), ow[0:two, :])
        part = part + dot(m_far[...].reshape(count, 2 * two), ow[two:, :])
        part = part.reshape(quarter, slab, model)

        @pl.when(i < 6)
        def _():
            a_send[at] = part.astype(BF16)

        for j in range(2):
            @pl.when(i == 4 + j)
            def _():
                sent_a[j].start()

        for j in range(2):
            @pl.when(i == 6 + j)
            def _():
                sent_a[j].wait_recv()

        @pl.when(i >= 6)
        def _():
            j = i - 6
            held[...] = part

            def one_residual(p, c):
                load_rows(dims, p, img, txt, rows)
                a = held[p] + a_recv[j, p].astype(F32)
                x = rows[...] + vector(vec, A_SCALE) * (a + vector(vec, A_BIAS))
                n, _ = normalise(x)
                e_img = n[0:ip] * vector(vec, GAIN2) + vector(vec, SHIFT2)
                e_txt = n[ip:] * vector(vec, GAIN2 + 1) + vector(vec, SHIFT2 + 1)
                r = j * quarter + p
                e_send[r, 0:ip, :] = e_img.astype(BF16)
                e_send[r, ip:, :] = e_txt.astype(BF16)
                e_over(r).start()
                e_here(r).start()
                for k, v in enumerate((x[0:1], x[ip:ip + 1], e_img[0:1], e_txt[0:1])):
                    cls[k, pl.ds(r, 1), :] = v

                @pl.when(j == 0)
                def _():
                    attended[p] = x
                    attn[p] = a

                return c

            lax.fori_loop(0, quarter, one_residual, 0)

    @pl.when(i == 7)
    def _():
        sent_c.start()
        keep_w.wait()
        for copy in keep_e:
            copy.wait()
        sent_c.wait()
        cls_peer[...] = c_recv[...]
        for copy in sent_e:
            copy.wait()
        for copy in sent_w + sent_a:
            copy.wait_send()


def fill(table, vectors):
    table[...] = jnp.zeros_like(table)
    at = 0
    for v in vectors:
        n = v.shape[0] if len(v.shape) == 2 else 1
        table[at:at + n, :] = v[...].reshape(n, table.shape[1])
        at += n


def front(dims, lens, img, txt, vectors, bias, own_w, own_o):
    model = img.shape[-1]
    quarter, slab, local = dims.quarter, dims.slab, dims.local
    held = pl.BlockSpec(memory_space=pltpu.VMEM)
    away = pl.BlockSpec(memory_space=pl.ANY)

    def states_at(i):
        return Place().quarter(i % 2, 1 - i % 4 // 2), 0, 0

    own_block = lambda cols: pl.BlockSpec((quarter, slab, cols), lambda i: (jnp.where(i < 2, 1, 0), 0, 0))
    far_block = lambda cols: pl.BlockSpec((quarter, slab, cols), lambda i: (jnp.where(i < 6, 1, 0), 0, 0))
    six = lambda cols: jax.ShapeDtypeStruct((2 * quarter, slab, cols), BF16)
    block = lambda cols: (quarter, slab, cols)
    n_remote = 6 + 2 * quarter
    return pl.pallas_call(
        lambda lens, img, txt, *refs: front_kernel(
            dims, lens, img, txt, refs[:len(vectors)], *refs[len(vectors):]),
        grid=(8,),
        in_specs=[pl.BlockSpec(memory_space=pltpu.SMEM),
                  pl.BlockSpec((quarter, dims.patches, model), states_at),
                  pl.BlockSpec((quarter, dims.caption, model), states_at)] + [held] * (3 + len(vectors)),
        out_specs=[held, own_block(model), own_block(384), own_block(128), far_block(768), far_block(256),
                   away, held, held, away, away, held, held],
        out_shape=[jax.ShapeDtypeStruct((16, model), F32), six(model), six(384), six(128), six(768), six(256),
                   jax.ShapeDtypeStruct((4 * local, model), BF16),
                   jax.ShapeDtypeStruct(block(model), F32), jax.ShapeDtypeStruct(block(model), F32),
                   six(model), six(model),
                   jax.ShapeDtypeStruct((4, 8, model), F32), jax.ShapeDtypeStruct((4, 8, model), F32)],
        scratch_shapes=[
            pltpu.VMEM((slab, model), F32), pltpu.VMEM((768, model), BF16), pltpu.VMEM((768, model), BF16),
            pltpu.VMEM((384, model), BF16), pltpu.VMEM((8, 768), F32), pltpu.VMEM((4 * local, model), BF16),
            pltpu.VMEM((2, local), F32),
            pltpu.VMEM((4,) + block(model), BF16), pltpu.VMEM((4,) + block(384), BF16),
            pltpu.VMEM((4,) + block(128), BF16), pltpu.VMEM(block(256), BF16),
            pltpu.VMEM(block(384), BF16), pltpu.VMEM(block(768), BF16),
            pltpu.VMEM((2,) + block(model), BF16), pltpu.VMEM((2,) + block(model), BF16),
            pltpu.VMEM((2 * quarter, slab, model), BF16), pltpu.VMEM((4, 8, model), F32),
            pltpu.VMEM(block(model), F32),
            pltpu.SemaphoreType.DMA((1 + 2 * quarter,)),
            pltpu.SemaphoreType.DMA((n_remote,)), pltpu.SemaphoreType.DMA((n_remote,)),
        ],
        compiler_params=params(collective_id=6, has_side_effects=True),
        cost_estimate=pl.CostEstimate(
            flops=16 * quarter * slab * model * 1152, bytes_accessed=40_000_000, transcendentals=0),
        name="front",
    )(lens, img, txt, *vectors, bias, own_w, own_o)


def middle_kernel(dims, total, img, txt, own, peer, cls_own, cls_peer, vec, up, up_bias, down, head_weight, scale,
                  dup, down_keep, down_send, dexp, d_own, d_near, bias_grad, class_e, c_act, c_dup, c_ddn, dcls,
                  head_in, dproj, gains, shifts, scalars,
                  bx, bd, rx, rd, x_near, x_far, ins, rows, part, parts, cls, back, cot, c_rows, extra, extras, hidden_in, weight, ddn, acc, stage,
                  local_sem, send_sem, recv_sem):
    here = Place()
    ip, slab, quarter = dims.ip, dims.slab, dims.quarter
    i = pl.program_id(0)
    model = own.shape[-1]
    mp_peers = [here.core, here.near, here.across]
    fetch = pltpu.make_async_copy(head_weight, weight, local_sem.at[0])
    of = [here.quarter(0, 0), here.quarter(1, 0), here.quarter(0, 1), here.quarter(1, 1)]

    sent_x = [remote(bx.at[2 * j], rx.at[j], send_sem, recv_sem, j, here.core) for j in range(2)]
    sent_d = [remote(bd.at[2 * j], rd.at[j], send_sem, recv_sem, 2 + j, here.core) for j in range(2)]
    def near(p):
        return remote(x_near.at[p], x_far.at[p], send_sem, recv_sem, 18 + p, here.near)

    sent_near = [near(p) for p in range(quarter)]
    sent_part = [remote(part, parts.at[k], send_sem, recv_sem, 5 + k, mp_peers[k]) for k in range(3)]
    sent_extra = [remote(extra, extras.at[k], send_sem, recv_sem, 8 + k, mp_peers[k]) for k in range(3)]
    sent_cls = [remote(cls.at[here.b], cls.at[here.b], send_sem, recv_sem, 11 + k, here.batch[k]) for k in range(7)]

    @pl.when(i == 0)
    def _():
        fetch.start()
        acc[...] = jnp.zeros_like(acc)
        rows[...] = jnp.zeros_like(rows)
        bias_grad[...] = jnp.zeros_like(bias_grad)
        for m in range(2):
            e = jnp.concatenate([cls_own[2 + m], cls_peer[2 + m]], axis=0).astype(BF16)
            class_e[m] = e
            u = dot(e, up[m]) + up_bias[m:m + 1]
            hidden_in[m] = u
            part[m] = dot(gelu_low(u), down[m])
        meet(mp_peers + here.batch)
        for copy in sent_part:
            copy.start()
        ins[...] = peer[...]

    @pl.when(i == 1)
    def _():
        for copy in sent_part:
            copy.wait_recv()
        for m in range(2):
            cls[here.b, m] = jnp.zeros(cls.shape[2:], F32)
            for r in range(4):
                half, at = (cls_own, cls_peer)[r // 2], quarter * (r % 2)
                for p in range(quarter):
                    line = [d[m, own_row(dims, s, p):own_row(dims, s, p) + 1, :]
                            for d, s in ((part, r), (parts.at[0], r ^ 2), (parts.at[1], r ^ 1), (parts.at[2], r ^ 3))]
                    x = (line[0] + line[1]) + (line[2] + line[3]) + vector(vec, F_BIAS + m)
                    x = half[m, at + p:at + p + 1, :] + vector(vec, F_SCALE) * x
                    cls[here.b, m, pl.ds(4 * of[r] + p, 1), :] = x
        for copy in sent_cls:
            copy.start()
        ins[...] = own[...]

    @pl.when(i == 2)
    def _():
        ins[...] = peer[...]

    @pl.when(i == 3)
    def _():
        ins[...] = own[...]
        fetch.wait()
        for copy in sent_cls:
            copy.wait_recv()
        n_rows = 16 * cls.shape[0]
        sharp = jnp.exp(scale[...])
        col_at = lax.broadcasted_iota(jnp.int32, (1, n_rows), 1)
        row_at = lax.broadcasted_iota(jnp.int32, (n_rows, 1), 0)
        col_ok = (col_at % 4) < quarter
        row_ok = (row_at % 4) < quarter
        normal, inverse, proj, unit, embed = [], [], [], [], []
        for m in range(2):
            n, r = normalise(cls[:, m].reshape(n_rows, model))
            h = (n * vector(vec, H_GAIN + m) + vector(vec, H_SHIFT + m)).astype(BF16)
            head_in[m] = h
            y = dot(h, weight[m])
            u = lax.rsqrt(jnp.sum(y * y, axis=-1, keepdims=True) + 1e-6)
            normal.append(n)
            inverse.append(r)
            proj.append(y)
            unit.append(u)
            embed.append((y * u).astype(BF16))
        ok = row_ok & col_ok
        logits = sharp * dot_t(embed[0], embed[1])
        masked = jnp.where(ok, logits, -1e30)
        row_max = jnp.max(masked, axis=1, keepdims=True)
        row_lse = row_max + jnp.log(jnp.sum(jnp.exp(masked - row_max), axis=1, keepdims=True))
        col_max = jnp.max(masked, axis=0, keepdims=True)
        col_lse = col_max + jnp.log(jnp.sum(jnp.exp(masked - col_max), axis=0, keepdims=True))
        same = (row_at == col_at) & ok
        both = jnp.exp(masked - row_lse) + jnp.exp(masked - col_lse)
        dlogits = jnp.where(ok, jnp.where(same, both - 2.0, both) * (1.0 / (2 * total)), 0.0)
        diagonal = jnp.sum(jnp.where(same, logits, 0.0), axis=1, keepdims=True)
        lines = jnp.sum(jnp.where(row_ok, row_lse - 2.0 * diagonal, 0.0), axis=0, keepdims=True)
        lines = lines + jnp.sum(jnp.where(col_ok, col_lse, 0.0), axis=1, keepdims=True)
        slope = jnp.sum(jnp.sum(dlogits * logits, axis=1, keepdims=True), axis=0, keepdims=True)
        scalars[0:1, :] = jnp.broadcast_to(lines * (1.0 / (2 * total)), (1, 128))
        scalars[1:2, :] = jnp.broadcast_to(slope, (1, 128))
        pieces, left = [], dlogits
        for _ in range(3):
            pieces.append(left.astype(BF16))
            left = left - pieces[-1].astype(F32)
        dembed = [
            sharp * (dot(pieces[0], embed[1]) + (dot(pieces[1], embed[1]) + dot(pieces[2], embed[1]))),
            sharp * (t_dot(pieces[0], embed[0]) + (t_dot(pieces[1], embed[0]) + t_dot(pieces[2], embed[0]))),
        ]
        c_rows[...] = jnp.zeros_like(c_rows)
        dcls[...] = jnp.zeros_like(dcls)
        for m in range(2):
            for p in range(quarter):
                src = (img, txt)[m]
                cot[m, 8 * 3 + p:8 * 3 + p + 1, :] = src[p, 0:1, :].astype(F32)
        for m in range(2):
            u, y, d = unit[m], proj[m], dembed[m]
            dp = (u * d - u * u * u * y * jnp.sum(y * d, axis=-1, keepdims=True)).astype(BF16)
            dproj[m] = dp
            dh = dot_t(dp, weight[m])
            gains[m:m + 1, :] = jnp.sum(dh * normal[m], axis=0, keepdims=True)
            shifts[m:m + 1, :] = jnp.sum(dh, axis=0, keepdims=True)
            back[m] = norm_back(normal[m], inverse[m], dh * vector(vec, H_GAIN + m))
            for r in range(4):
                step = (3, 1, 2, 0)[r]
                for p in range(quarter):
                    g = back[m, pl.ds(16 * here.b + 4 * of[r] + p, 1), :]
                    at = own_row(dims, r, p)
                    c_rows[m, at:at + 1, :] = cot[m, 8 * step + p:8 * step + p + 1, :] + g
                    if r == 0:
                        dcls[p, m:m + 1, :] = g
            u = hidden_in[m]
            big, small = gelu_parts(u)
            c_act[m] = (u * big).astype(BF16)
            g = (c_rows[m] * vector(vec, F_SCALE)).astype(BF16)
            c_ddn[m] = g
            du = dot_t(g, down[m]) * (big + u * small)
            bias_grad[m:m + 1, :] += jnp.sum(du, axis=0, keepdims=True)
            low = du.astype(BF16)
            c_dup[m] = low
            acc[m] += t_dot(c_ddn[m], c_act[m])
            extra[m] = dot_t(low, up[m])
        for copy in sent_extra:
            copy.start()

    at = lax.broadcasted_iota(jnp.int32, (slab, 1), 0)
    inner = (at != 0) & (at != ip)

    def one(p, c):
        load_rows(dims, p, img, txt, rows)
        cot[0, pl.ds(8 * i + p, 1), :] = rows[0:1, :]
        cot[1, pl.ds(8 * i + p, 1), :] = rows[ip:ip + 1, :]
        ddn[p] = jnp.where(inner, rows[...] * vector(vec, F_SCALE), 0.0).astype(BF16)
        return c

    lax.fori_loop(0, quarter, one, 0)
    for m, lo, hi in ((0, 0, ip), (1, ip, slab)):
        count = quarter * (hi - lo)
        e = ins[:, lo:hi, :].reshape(count, model)
        u = dot(e, up[m]) + up_bias[m:m + 1]
        big, small = gelu_parts(u)
        a = (u * big).astype(BF16)
        slope = big + u * small
        bd[i, :, lo:hi, :] = dot(a, down[m]).astype(BF16).reshape(quarter, hi - lo, model)
        g = ddn[:, lo:hi, :].reshape(count, model)
        acc[m] += t_dot(g, a)
        du = dot_t(g, down[m]) * slope
        bias_grad[m:m + 1, :] += jnp.sum(du, axis=0, keepdims=True)
        low = du.astype(BF16)
        dup[:, lo:hi, :] = low.reshape(quarter, hi - lo, -1)
        bx[i, :, lo:hi, :] = dot_t(low, up[m]).astype(BF16).reshape(quarter, hi - lo, model)

    for j in range(2):
        @pl.when(i == 2 * j)
        def _():
            sent_x[j].start()
            sent_d[j].start()

    @pl.when(i == 1)
    def _():
        sent_x[0].wait_recv()

        def add_x(p, c):
            x_near[p] = (bx[1, p].astype(F32) + rx[0, p].astype(F32)).astype(BF16)
            near(p).start()
            return c

        lax.fori_loop(0, quarter, add_x, 0)
        sent_d[0].wait_recv()

        def add_d(p, c):
            d_near[p] = (bd[1, p].astype(F32) + rd[0, p].astype(F32)).astype(BF16)
            return c

        lax.fori_loop(0, quarter, add_d, 0)

    @pl.when(i == 3)
    def _():
        piece = stage.shape[3]
        block = lambda j: pl.ds(pl.multiple_of(j * piece, piece), piece)
        for j in range(4):
            for m in range(2):
                stage[0, j, m] = acc[m, block(2 * j + here.x), :].astype(BF16)
                stage[1, j, m] = acc[m, block(2 * j + 1 - here.x), :].astype(BF16)
        leave = [pltpu.make_async_copy(stage.at[k], dst, local_sem.at[1 + k])
                 for k, dst in enumerate((down_keep, down_send))]
        for copy in leave:
            copy.start()
        sent_d[1].wait_recv()

        def add_d(p, c):
            d_own[p] = bd[3, p].astype(F32) + rd[1, p].astype(F32)
            return c

        lax.fori_loop(0, quarter, add_d, 0)
        sent_x[1].wait_recv()

        def add_x(p, c):
            near(p).wait_recv()
            dexp[p] = bx[3, p].astype(F32) + rx[1, p].astype(F32) + x_far[p].astype(F32)
            return c

        lax.fori_loop(0, quarter, add_x, 0)
        for copy in sent_extra:
            copy.wait_recv()
        for m in range(2):
            for p in range(quarter):
                line = [x[m, own_row(dims, r, p):own_row(dims, r, p) + 1, :]
                        for x, r in ((extra, 0), (extras.at[0], 2), (extras.at[1], 1), (extras.at[2], 3))]
                dexp[p, m * ip:m * ip + 1, :] += (line[0] + line[1]) + (line[2] + line[3])
        for copy in leave:
            copy.wait()
        for copy in sent_x + sent_d + sent_near + sent_part + sent_extra + sent_cls:
            copy.wait_send()


def middle(dims, total, img, txt, own, peer, cls_own, cls_peer, vec, up, up_bias, down, weight, scale):
    model = own.shape[-1]
    hidden = up.shape[-1]
    slab, quarter = dims.slab, dims.quarter
    batch = 8

    def cot_at(i):
        here = Place()
        return here.quarter(1 - i // 2, 1 - i % 2), 0, 0

    held = pl.BlockSpec(memory_space=pltpu.VMEM)
    half = pl.BlockSpec((quarter, slab, model), lambda i: (jnp.where(i < 2, 1, 0), 0, 0))
    step = lambda cols: pl.BlockSpec((quarter, slab, cols), lambda i: (i, 0, 0))
    rows_of = lambda n, t: jax.ShapeDtypeStruct((n, slab, model), t)
    small = [((4, 2, model // 8, hidden), BF16)] * 2 + [((quarter, slab, model), F32), ((quarter, slab, model), F32), ((quarter, slab, model), BF16),
             ((2, hidden), F32), ((2, 16, model), BF16), ((2, 16, hidden), BF16), ((2, 16, hidden), BF16),
             ((2, 16, model), BF16), ((quarter, 8, model), F32), ((2, 16 * batch, model), BF16),
             ((2, 16 * batch, weight.shape[2]), BF16), ((2, model), F32), ((2, model), F32), ((2, 128), F32)]
    block = (quarter, slab, model)
    return pl.pallas_call(
        functools.partial(middle_kernel, dims, total),
        grid=(4,),
        in_specs=[pl.BlockSpec((quarter, dims.patches, model), cot_at),
                  pl.BlockSpec((quarter, dims.caption, model), cot_at)] + [half] * 2 + [held] * 6
        + [pl.BlockSpec(memory_space=pl.ANY), held],
        out_specs=[step(hidden)] + [pl.BlockSpec(memory_space=pl.ANY)] * 2 + [held] * (len(small) - 2),
        out_shape=[rows_of(4 * quarter, BF16)] + [jax.ShapeDtypeStruct(v, t) for v, t in small],
        scratch_shapes=[
            pltpu.VMEM((4,) + block, BF16), pltpu.VMEM((4,) + block, BF16),
            pltpu.VMEM((2,) + block, BF16), pltpu.VMEM((2,) + block, BF16),
            pltpu.VMEM(block, BF16), pltpu.VMEM(block, BF16), pltpu.VMEM(block, BF16),
            pltpu.VMEM((slab, model), F32),
            pltpu.VMEM((2, 16, model), F32), pltpu.VMEM((3, 2, 16, model), F32),
            pltpu.VMEM((batch, 2, 16, model), F32), pltpu.VMEM((2, 16 * batch, model), F32),
            pltpu.VMEM((2, 32, model), F32), pltpu.VMEM((2, 16, model), F32),
            pltpu.VMEM((2, 16, model), F32), pltpu.VMEM((3, 2, 16, model), F32),
            pltpu.VMEM((2, 16, hidden), F32), pltpu.VMEM(weight.shape, BF16),
            pltpu.VMEM(block, BF16), pltpu.VMEM((2, model, hidden), F32),
            pltpu.VMEM((2, 4, 2, model // 8, hidden), BF16), pltpu.SemaphoreType.DMA((3,)),
            pltpu.SemaphoreType.DMA((18 + quarter,)), pltpu.SemaphoreType.DMA((18 + quarter,)),
        ],
        compiler_params=params(collective_id=2, has_side_effects=True),
        cost_estimate=pl.CostEstimate(
            flops=32 * quarter * slab * model * hidden, bytes_accessed=40_000_000, transcendentals=0),
        name="middle",
    )(img, txt, own, peer, cls_own, cls_peer, vec, up, up_bias, down, weight, scale)


def turn_kernel(dims, img, txt, peer, own, dup, ce, cu, down_keep, down_send, dexp, attended, attn, d_own, d_near, dcls, vec,
                down_sum, up_keep, up_send, dattended, dattn, dattn_peer, fin_img, fin_txt, sums,
                acc, d_far, n_peer, rows, side_keep, side_recv, e_in, dexp_in, attended_in, attn_in, d_own_in,
                local_sem, send_sem, recv_sem):
    here = Place()
    quarter, ip = dims.quarter, dims.ip
    i = pl.program_id(0)
    piece = side_keep.shape[2]

    def near(p):
        return remote(d_near.at[p], d_far.at[p], send_sem, recv_sem, 2 + quarter + p, here.near)

    sent_near = [near(p) for p in range(quarter)]

    def over(p):
        return remote(dattn.at[p], n_peer.at[p], send_sem, recv_sem, 1 + p, here.core)

    sent_core = [over(p) for p in range(quarter)]
    sent_side = remote(down_send, side_recv, send_sem, recv_sem, 1 + quarter, here.side)
    loaded = [pltpu.make_async_copy(src, dst, local_sem.at[j]) for j, (src, dst) in enumerate((
        (dexp, dexp_in), (attended, attended_in), (attn, attn_in), (d_own, d_own_in), (down_keep, side_keep)))]
    dexp, attended, attn, d_own = dexp_in, attended_in, attn_in, d_own_in
    spans = ((0, 0, ip), (1, ip, dims.slab))
    flat = lambda v: v.reshape(-1, v.shape[-1])
    block = lambda j: pl.ds(pl.multiple_of(j * piece, piece), piece)

    @pl.when(i == 0)
    def _():
        meet([here.core, here.near, here.side])
        for copy in sent_near:
            copy.start()
        sent_side.start()
        for copy in loaded:
            copy.start()
        for m in range(2):
            acc[m] = t_dot(ce[m], cu[m])

    @pl.when(i % 2 == 0)
    def _():
        e_in[...] = peer[...]

    @pl.when(i % 2 == 1)
    def _():
        e_in[...] = own[...]

    for m, lo, hi in spans:
        acc[m] += t_dot(flat(e_in[:, lo:hi, :]), flat(dup[:, lo:hi, :]))

    @pl.when(i == 3)
    def _():
        for j in range(4):
            for m in range(2):
                up_keep[j, m] = acc[m, block(2 * j + here.x), :].astype(BF16)
                up_send[j, m] = acc[m, block(2 * j + 1 - here.x), :].astype(BF16)
        for copy in loaded:
            copy.wait()
        rows[...] = jnp.zeros_like(rows)
        sums[...] = jnp.zeros_like(sums)

        def load(p):
            load_rows(dims, p, img, txt, rows)
            rows[0:1, :] += dcls[p, 0:1, :]
            rows[ip:ip + 1, :] += dcls[p, 1:2, :]

        def norm(p, c):
            load(p)
            for m, lo, hi in ((0, 0, ip), (1, ip, dims.slab)):
                n, r = normalise(attended[p, lo:hi, :])
                dy = dexp[p, lo:hi, :]
                sums[m:m + 1, :] += jnp.sum(dy * n, axis=0, keepdims=True)
                sums[2 + m:3 + m, :] += jnp.sum(dy, axis=0, keepdims=True)
                d = rows[lo:hi, :] + norm_back(n, r, dy * vector(vec, GAIN2 + m))
                dattended[p, lo:hi, :] = d
                sd = d * vector(vec, A_SCALE)
                dattn[p, lo:hi, :] = sd.astype(BF16)
                a = attn[p, lo:hi, :] + vector(vec, A_BIAS)
                sums[4:5, :] += jnp.sum(d * a, axis=0, keepdims=True)
                sums[5:6, :] += jnp.sum(sd, axis=0, keepdims=True)
            over(p).start()
            return c

        lax.fori_loop(0, quarter, norm, 0)
        def final(p, c):
            load(p)
            near(p).wait_recv()
            for m, lo, hi in ((0, 0, ip), (1, ip, dims.slab)):
                b = d_own[p, lo:hi, :] + d_far[p, lo:hi, :].astype(F32) + vector(vec, F_BIAS + m)
                f = attended[p, lo:hi, :] + vector(vec, F_SCALE) * b
                if m == 0:
                    fin_img[p] = f[0:dims.patches].astype(BF16)
                else:
                    fin_txt[p] = f[0:dims.caption].astype(BF16)
                g = rows[lo:hi, :]
                sums[6:7, :] += jnp.sum(g * b, axis=0, keepdims=True)
                sums[7 + m:8 + m, :] += jnp.sum(g, axis=0, keepdims=True) * vector(vec, F_SCALE)
            return c

        lax.fori_loop(0, quarter, final, 0)
        for p in range(quarter):
            sent_core[p].wait()
            dattn_peer[p] = n_peer[p]
        sent_side.wait()
        for j in range(4):
            down_sum[j] = (side_keep[j].astype(F32) + side_recv[j].astype(F32)).astype(BF16)
        for copy in sent_near:
            copy.wait_send()


def turn(dims, img, txt, peer, own, dup, ce, cu, down_keep, down_send, dexp, attended, attn, d_own, d_near, dcls, vec):
    model = own.shape[-1]
    hidden = dup.shape[-1]
    slab, quarter = dims.slab, dims.quarter
    held = pl.BlockSpec(memory_space=pltpu.VMEM)

    def own_at(i):
        return Place().quarter(0, 0), 0, 0

    away = pl.BlockSpec(memory_space=pl.ANY)
    half = pl.BlockSpec((quarter, slab, model), lambda i: (jnp.where(i < 2, 1, 0), 0, 0))
    step = pl.BlockSpec((quarter, slab, hidden), lambda i: (i, 0, 0))
    block = (quarter, slab, model)
    part = (4, 2, model // 8, hidden)
    outs = [(part, BF16), (part, BF16), (part, BF16), (block, F32), (block, BF16), (block, BF16),
            ((quarter, dims.patches, model), BF16), ((quarter, dims.caption, model), BF16), ((16, model), F32)]
    return pl.pallas_call(
        functools.partial(turn_kernel, dims),
        grid=(4,),
        in_specs=[pl.BlockSpec((quarter, dims.patches, model), own_at),
                  pl.BlockSpec((quarter, dims.caption, model), own_at)] + [half] * 2 + [step]
        + [held] * 2 + [away] * 6 + [held] * 3,
        out_specs=[held] * len(outs),
        out_shape=[jax.ShapeDtypeStruct(v, t) for v, t in outs],
        scratch_shapes=[
            pltpu.VMEM((2, model, hidden), F32), pltpu.VMEM(block, BF16), pltpu.VMEM(block, BF16),
            pltpu.VMEM((slab, model), F32), pltpu.VMEM(part, BF16), pltpu.VMEM(part, BF16),
            pltpu.VMEM(block, BF16),
        ] + [pltpu.VMEM(block, F32)] * 4 + [
            pltpu.SemaphoreType.DMA((5,)),
            pltpu.SemaphoreType.DMA((2 + 2 * quarter,)), pltpu.SemaphoreType.DMA((2 + 2 * quarter,)),
        ],
        compiler_params=params(collective_id=3, has_side_effects=True),
        cost_estimate=pl.CostEstimate(
            flops=16 * quarter * slab * model * hidden, bytes_accessed=40_000_000, transcendentals=0),
        name="turn",
    )(img, txt, peer, own, dup, ce, cu, down_keep, down_send, dexp, attended, attn, d_own, d_near, dcls, vec)


def back_kernel(dims, lens, d_own, d_peer, normed, qkv_far, mixed_far, qkv_own, mixed_own, wq, wo, wf,
                fin_img, fin_txt, up_keep, up_send, down_sum,
                whole, grad_pair, grad_single, cols_far, cols_own, near_img, near_txt, far_sum, down_out, up_out,
                dattn, dm_far, dm_own, dq_far, dq_own, acc_far, acc_own, w_far, w_own, o_far, o_own, dn, grad_f,
                up_mine, up_side, up_sum, up_in, up_pass, up_last, down_mine, down_in, down_pass, down_last,
                n_send, n_recv, from_side, local_sem, send_sem, recv_sem):
    here = Place()
    i = pl.program_id(0)
    slab, quarter, local = dims.slab, dims.quarter, dims.local
    two, one_head = parts_of(dims)
    count = quarter * slab
    model = normed.shape[-1]
    piece = from_side.shape[1]
    block = lambda j: pl.ds(pl.multiple_of(j * piece, piece), piece)
    used = [0]

    def make(src, dst, device):
        at = used[0]
        used[0] += 1
        return remote(src, dst, send_sem, recv_sem, at, device)

    sent_near = [make(fin_img, near_img, here.near), make(fin_txt, near_txt, here.near)]
    sent_up = [make(up_send.at[j, m], up_side.at[m, j], here.side) for m in range(2) for j in range(4)]
    in_pair = lambda src, dst: [make(src.at[here.z_pair], dst.at[0], here.paired), make(src.at[here.z_rest], dst.at[1], here.paired)]
    sent_down = in_pair(down_sum, down_in)
    pass_down = make(down_pass, down_last, here.opposite)
    wide = grad_f.shape[1]
    sent_far = [make(grad_f.at[block(2 * j + 1 - here.x)], from_side.at[j, :, pl.ds(0, wide)], here.side) for j in range(4)]
    sent_far += [make(grad_single.at[block(2 * j + 1 - here.x)], from_side.at[j, :, pl.ds(wide, grad_single.shape[1])],
                      here.side) for j in range(4)]
    sent_pair = [in_pair(up_sum.at[m], up_in.at[m]) for m in range(2)]
    pass_up = [make(up_pass.at[m], up_last.at[m], here.opposite) for m in range(2)]
    sent_n = make(n_send, n_recv, here.core)
    loaded = [pltpu.make_async_copy(up_keep, up_mine, local_sem.at[0]),
              pltpu.make_async_copy(down_sum.at[here.z], down_mine.at[0], local_sem.at[1]),
              pltpu.make_async_copy(down_sum.at[here.z_far], down_mine.at[1], local_sem.at[2])]
    add = lambda *parts: functools.reduce(lambda p, q: p + q, [v.astype(F32) for v in parts])

    @pl.when(i == 0)
    def _():
        meet([here.core, here.near, here.side, here.paired, here.opposite])
        for copy in loaded + sent_near + sent_up + sent_down:
            copy.start()
        for acc, cols in ((acc_far, cols_far), (acc_own, cols_own)):
            acc[...] = jnp.zeros_like(acc)
            cols[...] = jnp.zeros_like(cols)
        for t in range(4):
            own, start = (wq, t * local) if t < 3 else (wo, 0)
            dst, at = (w_far, t * 2 * two) if t < 3 else (o_far, 0)
            copy_rows(dst, at, wf, t * local, two)
            copy_rows(dst, at + two, own, start + two, one_head)
            copy_rows(dst, at + two + one_head, wf, t * local + two, one_head)
            dst, at = (w_own, t * two) if t < 3 else (o_own, 0)
            copy_rows(dst, at, own, start, two)

    @pl.when(i % 2 == 0)
    def _():
        dattn[...] = d_peer[...]

    @pl.when(i % 2 == 1)
    def _():
        dattn[...] = d_own[...]

    whose = here.quarter(0, 1 - i % 2)

    @pl.when(i < 2)
    def _():
        part = back_step(dims, 2, lens, whose, dattn, normed, qkv_far, mixed_far, dm_far, dq_far, acc_far, cols_far,
                         w_far, o_far)
        dn[i] = part.reshape(quarter, slab, model)

    def sum_up(m):
        for j in range(4):
            sent_up[4 * m + j].wait_recv()
            up_sum[m, j] = add(up_mine[j, m], up_side[m, j]).astype(BF16)
        for copy in sent_pair[m]:
            copy.start()

    def pass_on(m):
        for copy in sent_pair[m]:
            copy.wait_recv()
        up_pass[m] = add(up_sum[m, here.z_far], up_in[m, 1]).astype(BF16)
        pass_up[m].start()

    @pl.when(i == 0)
    def _():
        for copy in loaded[1:]:
            copy.wait()
        for copy in sent_down:
            copy.wait_recv()
        down_pass[...] = add(down_mine[1], down_in[1]).astype(BF16)
        pass_down.start()
        loaded[0].wait()
        sum_up(0)

    @pl.when(i == 1)
    def _():
        for t in range(4):
            at = t * 2 * two
            to = 4 * two + t * one_head
            grad_f[:, t * two:(t + 1) * two] = acc_far[:, at:at + two].astype(BF16)
            grad_f[:, to:to + one_head] = acc_far[:, at + two + one_head:at + 2 * two].astype(BF16)
            grad_single[:, t * one_head:(t + 1) * one_head] = acc_far[:, at + two:at + two + one_head].astype(BF16)
        for copy in sent_far:
            copy.start()
        pass_on(0)
        sum_up(1)

    @pl.when(i >= 2)
    def _():
        part = back_step(dims, 1, lens, whose, dattn, normed, qkv_own, mixed_own, dm_own, dq_own, acc_own, cols_own,
                         w_own, o_own)
        total = part.reshape(quarter, slab, model) + dn[i - 2]

        @pl.when(i == 2)
        def _():
            n_send[...] = total.astype(BF16)
            sent_n.start()
            pass_on(1)

        @pl.when(i == 3)
        def _():
            whole[...] = total

    @pl.when(i == 3)
    def _():
        grad_pair[...] = acc_own[...].astype(BF16)
        sent_n.wait_recv()
        whole[...] += n_recv[...].astype(F32)
        down_out[...] = add(down_mine[0], down_in[0])
        for copy in sent_far:
            copy.wait_recv()
        for j in range(4):
            far_sum[j, :, 0:wide] = add(grad_f[block(2 * j + here.x), :], from_side[j, :, 0:wide]).astype(BF16)
            far_sum[j, :, wide:] = add(grad_single[block(2 * j + here.x), :], from_side[j, :, wide:]).astype(BF16)
        pass_down.wait_recv()
        down_out[...] += down_last[...].astype(F32)
        for m in range(2):
            pass_up[m].wait_recv()
            up_out[m] = add(up_sum[m, here.z], up_in[m, 0], up_last[m])
        for copy in sent_near:
            copy.wait_recv()
        for copy in sent_near + sent_up + sent_down + sent_far + sent_pair[0] + sent_pair[1] + pass_up + [pass_down, sent_n]:
            copy.wait_send()


def back(dims, lens, d_own, d_peer, normed, qkv_far, mixed_far, qkv_own, mixed_own, wq, wo, wf,
         fin_img, fin_txt, up_keep, up_send, down_sum):
    model = normed.shape[-1]
    slab, quarter = dims.slab, dims.quarter
    hidden = up_keep.shape[-1]
    piece = model // 8
    held = pl.BlockSpec(memory_space=pltpu.VMEM)
    away = pl.BlockSpec(memory_space=pl.ANY)
    spec = lambda cols, at: pl.BlockSpec((quarter, slab, cols), lambda i: (at(i), 0, 0))
    early, late = lambda i: jnp.maximum(1 - i, 0), lambda i: jnp.where(i < 3, 1, 0)
    rows = (quarter, slab, model)
    outs = [(held, rows, F32), (held, (model, 512), BF16), (held, (model, 256), BF16),
            (held, (1, 768), F32), (held, (1, 384), F32),
            (away, fin_img.shape, BF16), (away, fin_txt.shape, BF16),
            (held, (4, piece, model + 256), BF16), (held, (2, piece, hidden), F32), (held, (2, piece, hidden), F32)]
    slabs = lambda cols: pltpu.VMEM((quarter, slab, cols), BF16)
    return pl.pallas_call(
        functools.partial(back_kernel, dims),
        grid=(4,),
        in_specs=[pl.BlockSpec(memory_space=pltpu.SMEM), held, held, spec(model, lambda i: 1 - i % 2),
                  spec(768, early), spec(256, early), spec(384, late), spec(128, late), held, held, held]
        + [away] * 5,
        out_specs=[v[0] for v in outs],
        out_shape=[jax.ShapeDtypeStruct(v[1], v[2]) for v in outs],
        scratch_shapes=[
            slabs(model), slabs(256), slabs(128), slabs(768), slabs(384),
            pltpu.VMEM((model, 1024), F32), pltpu.VMEM((model, 512), F32),
            pltpu.VMEM((768, model), BF16), pltpu.VMEM((384, model), BF16),
            pltpu.VMEM((256, model), BF16), pltpu.VMEM((128, model), BF16),
            pltpu.VMEM((2,) + rows, F32), pltpu.VMEM((model, model), BF16),
            pltpu.VMEM((4, 2, piece, hidden), BF16), pltpu.VMEM((2, 4, piece, hidden), BF16),
            pltpu.VMEM((2, 4, piece, hidden), BF16), pltpu.VMEM((2, 2, piece, hidden), BF16),
            pltpu.VMEM((2, piece, hidden), BF16), pltpu.VMEM((2, piece, hidden), BF16),
            pltpu.VMEM((2, 2, piece, hidden), BF16), pltpu.VMEM((2, 2, piece, hidden), BF16),
            pltpu.VMEM((2, piece, hidden), BF16), pltpu.VMEM((2, piece, hidden), BF16),
            pltpu.VMEM(rows, BF16), pltpu.VMEM(rows, BF16), pltpu.VMEM((4, piece, model + 256), BF16),
            pltpu.SemaphoreType.DMA((3,)), pltpu.SemaphoreType.DMA((28,)), pltpu.SemaphoreType.DMA((28,)),
        ],
        compiler_params=params(collective_id=4, has_side_effects=True),
        cost_estimate=pl.CostEstimate(
            flops=24 * quarter * slab * model * 1152, bytes_accessed=30_000_000, transcendentals=0),
        name="back",
    )(lens, d_own, d_peer, normed, qkv_far, mixed_far, qkv_own, mixed_own, wq, wo, wf,
      fin_img, fin_txt, up_keep, up_send, down_sum)


V_ROWS, V_MP, V_HEADS, V_FAR = 16, 11, 13, 256


def finish_kernel(dims, dnormed, dattended, states_img, states_txt, vec, fin_img, fin_txt,
                  near_img, near_txt, grad_pair, grad_far, own_sums, up_sums, cols_own, cols_far,
                  core_img, core_txt, across_img, across_txt, back_img, back_txt, grad_out, v_out,
                  n_in, a_in, s_img, s_txt, d_img, d_txt, rows, xr, zs, z_in, z_pass, z_last, f_in, f_pass, f_last, far_sum, far_recv, vs, vr,
                  local_sem, send_sem, recv_sem):
    quarter = dims.quarter
    here = Place()
    z, x, m = here.z, here.x, here.m
    near_quarter = here.quarter(1, 0)
    used = [0]

    def send(src, dst, device):
        at = used[0]
        used[0] += 1
        return remote(src, dst, send_sem, recv_sem, at, device)

    loaded = [pltpu.make_async_copy(states_img.at[pl.ds(m * quarter, quarter)], s_img, local_sem.at[0]),
              pltpu.make_async_copy(states_txt.at[pl.ds(m * quarter, quarter)], s_txt, local_sem.at[1])]
    count = 2 + 2 * quarter
    pairs_in = [pltpu.make_async_copy(src.at[p], dst.at[p], local_sem.at[count + 2 * p + k])
                for p in range(quarter) for k, (src, dst) in enumerate(((dnormed, n_in), (dattended, a_in)))]
    for copy in loaded + pairs_in:
        copy.start()
    meet([here.core, here.near, here.side, here.paired, here.opposite])

    piece = xr.shape[1]
    wide = grad_pair.shape[1]
    block = lambda j: pl.ds(pl.multiple_of(j * piece, piece), piece)
    x_copies = []
    for j in range(4):
        x_copies.append(send(grad_pair.at[block(2 * j + 1 - x)], xr.at[j], here.side))
        x_copies[-1].start()
    add = lambda *parts: functools.reduce(lambda p, q: p + q, [v.astype(F32) for v in parts])
    in_pair = lambda src, dst: [send(src.at[here.z_pair], dst.at[0], here.paired),
                                send(src.at[here.z_rest], dst.at[1], here.paired)]
    far_copies = in_pair(grad_far, f_in)
    for copy in far_copies:
        copy.start()

    fin_remote = [send(src, dst, here.core) for src, dst in (
        (fin_img, core_img), (fin_txt, core_txt), (near_img, across_img), (near_txt, across_txt))]

    rows[...] = jnp.zeros_like(rows)
    for copy in loaded:
        copy.wait()
    total = [jnp.zeros((1, rows.shape[1]), F32)] * 2
    back_local, to_near, to_other = [], [], []
    for p in range(quarter):
        load_rows(dims, p, s_img, s_txt, rows)
        n, r = normalise(rows[...])
        for copy in pairs_in[2 * p:2 * p + 2]:
            copy.wait()
        dy = n_in[p]
        total[0] = total[0] + jnp.sum(dy * n, axis=0, keepdims=True)
        total[1] = total[1] + jnp.sum(dy, axis=0, keepdims=True)
        d = a_in[p] + norm_back(n, r, dy * vector(vec, GAIN1))
        d_img[p] = d[0:dims.patches].astype(BF16)
        d_txt[p] = d[dims.ip:dims.ip + dims.caption].astype(BF16)
        for j, (src, dst) in enumerate(((d_img, back_img), (d_txt, back_txt))):
            at = dst.at[m * quarter + p]
            to_near.append(send(src.at[p], at, here.near))
            to_near[-1].start()
            to_other.append(send(src.at[p], at, here.core))
            to_other[-1].start()
            back_local.append(pltpu.make_async_copy(src.at[p], at, local_sem.at[2 + 2 * p + j]))
            back_local[-1].start()
    for copy in fin_remote:
        copy.start()

    at = lax.broadcasted_iota(jnp.int32, (V_ROWS, 1), 0)
    two, one_head = parts_of(dims)
    vs[0] = jnp.zeros(vs.shape[1:], F32)
    vs[0, 0:1, :] = total[0]
    vs[0, 1:2, :] = total[1]
    vs[0, 2:V_MP, :] = own_sums[0:V_MP - 2, :]
    vs[0, V_MP:V_HEADS, :] = up_sums[...]
    for j in range(2):
        own_at, far_at = 2 * j * two, 4 * j * two
        vs[0, V_HEADS + j:V_HEADS + j + 1, 0:two] = cols_own[0:1, own_at:own_at + two]
        vs[0, V_HEADS + j:V_HEADS + j + 1, two:two + one_head] = cols_far[0:1, far_at + two:far_at + two + one_head]
        vs[0, V_HEADS + j:V_HEADS + j + 1, V_FAR:V_FAR + two] = cols_far[0:1, far_at:far_at + two]
        vs[0, V_HEADS + j:V_HEADS + j + 1, V_FAR + two:V_FAR + two + one_head] = cols_far[0:1, far_at + two + one_head:far_at + 2 * two]
    v = vs[0]
    v_copies = []

    def exchange(step, value, device):
        vs[step] = value
        copy = send(vs.at[step], vr.at[step], device)
        copy.start()
        copy.wait_recv()
        v_copies.append(copy)
        return vr[step]

    v = v + jnp.where(at < V_MP, exchange(0, v, here.core), 0.0)
    for copy in far_copies:
        copy.wait_recv()
    f_pass[...] = add(grad_far[here.z_far], f_in[1]).astype(BF16)
    far_copies.append(send(f_pass, f_last, here.opposite))
    far_copies[-1].start()
    v = v + exchange(1, v, here.side)
    v = v + exchange(2, v, here.paired)
    vs[3] = v
    v_far = send(vs.at[3], vr.at[3], here.opposite)
    v_far.start()

    def own_sum(j):
        return add(grad_pair[block(2 * j + x), :], xr[j])

    for copy in x_copies:
        copy.wait_recv()
    for j in range(4):
        zs[j] = own_sum(j).astype(BF16)
    z_copies = in_pair(zs, z_in)
    for copy in z_copies:
        copy.start()

    far_copies[-1].wait_recv()
    narrow = far_sum.shape[1]
    far_sum[...] = add(grad_far[z, :, 0:narrow], f_in[0, :, 0:narrow], f_last[:, 0:narrow]).astype(BF16)
    far_copy = send(far_sum, far_recv, here.near)
    far_copy.start()
    v_far.wait_recv()
    v = v + vr[3]
    for copy in z_copies:
        copy.wait_recv()
    z_pass[...] = add(zs[here.z_far], z_in[1]).astype(BF16)
    z_copies.append(send(z_pass, z_last, here.opposite))
    z_copies[-1].start()
    vs[4] = v
    v_near = send(vs.at[4], vr.at[4], here.near)
    v_near.start()
    for copy in back_local:
        copy.wait()
    onward = []
    for p in range(quarter):
        for j, dst in enumerate((back_img, back_txt)):
            to_near[2 * p + j].wait_recv()
            at_near = dst.at[near_quarter * quarter + p]
            onward.append(send(at_near, at_near, here.core))
            onward[-1].start()
    far_copy.wait_recv()
    z_copies[-1].wait_recv()
    grad_out[:, 0:wide] = own_sum(z) + add(far_recv[:, 0:wide], z_in[0], z_last[...])
    grad_out[:, wide:] = add(
        far_recv[:, wide:], grad_far[z, :, narrow:], f_in[0, :, narrow:], f_last[:, narrow:])
    v_near.wait_recv()
    there = vr[4]
    v_out[...] = v + jnp.where(at < V_MP, there, 0.0)
    width = two + one_head
    v_out[V_HEADS:V_HEADS + 2, 0:width] = v[V_HEADS:V_HEADS + 2, 0:width] + there[V_HEADS:V_HEADS + 2, V_FAR:V_FAR + width]
    for copy in to_other + fin_remote + onward:
        copy.wait()
    for copy in x_copies + far_copies + to_near + z_copies + v_copies + [far_copy, v_near, v_far]:
        copy.wait_send()


def finish(dims, dnormed, dattended, states_img, states_txt, vec, fin_img, fin_txt,
           near_img, near_txt, grad_pair, grad_far, *tables):
    pairs, patches, model = states_img.shape
    caption = states_txt.shape[1]
    quarter, slab = dims.quarter, dims.slab
    piece, cols = grad_far.shape[1], model
    wide, all_cols = grad_pair.shape[1], grad_far.shape[2]
    held = pl.BlockSpec(memory_space=pltpu.VMEM)
    away = pl.BlockSpec(memory_space=pl.ANY)
    n_remote = 7 * quarter + 28
    return pl.pallas_call(
        functools.partial(finish_kernel, dims),
        in_specs=[away] * 4 + [held] + [away] * 4 + [held] * 6,
        out_specs=[away] * 6 + [held] * 2,
        out_shape=[jax.ShapeDtypeStruct(v.shape, BF16) for v in (fin_img, fin_txt) * 2] + [
            jax.ShapeDtypeStruct((pairs, patches, model), BF16),
            jax.ShapeDtypeStruct((pairs, caption, model), BF16),
            jax.ShapeDtypeStruct((piece, cols), F32),
            jax.ShapeDtypeStruct((V_ROWS, model), F32),
        ],
        scratch_shapes=[
            pltpu.VMEM((quarter, slab, model), F32), pltpu.VMEM((quarter, slab, model), F32),
            pltpu.VMEM((quarter, patches, model), BF16),
            pltpu.VMEM((quarter, caption, model), BF16),
            pltpu.VMEM((quarter, patches, model), BF16),
            pltpu.VMEM((quarter, caption, model), BF16),
            pltpu.VMEM((slab, model), F32),
            pltpu.VMEM((4, piece, wide), BF16), pltpu.VMEM((4, piece, wide), BF16),
            pltpu.VMEM((2, piece, wide), BF16), pltpu.VMEM((piece, wide), BF16), pltpu.VMEM((piece, wide), BF16),
            pltpu.VMEM((2, piece, all_cols), BF16), pltpu.VMEM((piece, all_cols), BF16), pltpu.VMEM((piece, all_cols), BF16),
            pltpu.VMEM((piece, cols), BF16), pltpu.VMEM((piece, cols), BF16),
            pltpu.VMEM((5, V_ROWS, model), F32),
            pltpu.VMEM((5, V_ROWS, model), F32),
            pltpu.SemaphoreType.DMA((2 + 4 * quarter,)),
            pltpu.SemaphoreType.DMA((n_remote,)),
            pltpu.SemaphoreType.DMA((n_remote,)),
        ],
        compiler_params=params(collective_id=1, has_side_effects=True),
        name="finish",
    )(dnormed, dattended, states_img, states_txt, vec, fin_img, fin_txt,
      near_img, near_txt, grad_pair, grad_far, *tables)


def spread_kernel(dims, cols, sums, grad, gains, shifts, up, down, head_in, dproj, *refs):
    forward, refs = refs[:8], refs[8:]
    back_img, back_txt, *refs = refs
    outs, refs = refs[:12], refs[12:]
    (qkv, out_w, up_out, down_out, head_out, out_img, out_txt, grad_img, grad_txt,
     turned, held_img, held_txt, held_up, held_down, h_in, d_in, in_sem, out_sem) = refs
    here = Place()
    quarter = dims.quarter
    whose = [here.quarter(0, 0), here.quarter(1, 0), here.quarter(0, 1), here.quarter(1, 1)]
    place = lambda q: pl.ds(q * quarter, quarter)
    comes, goes = [], []
    for r in range(4):
        for j, (held, src, dst, back, to) in enumerate((
            (held_img, forward[2 * r], out_img, back_img, grad_img), (held_txt, forward[2 * r + 1], out_txt, back_txt, grad_txt),
        )):
            for k, (source, target, q) in enumerate(((src, dst, whose[r]), (back.at[place(r)], to, r))):
                at = 4 * r + 2 * j + k
                comes.append(pltpu.make_async_copy(source, held.at[2 * r + k], in_sem.at[at]))
                goes.append(pltpu.make_async_copy(held.at[2 * r + k], target.at[place(q)], out_sem.at[at]))
    for at, (src, held, dst) in enumerate(((up, held_up, up_out), (down, held_down, down_out))):
        comes.append(pltpu.make_async_copy(src, held, in_sem.at[16 + at]))
        goes.append(pltpu.make_async_copy(held, dst, out_sem.at[16 + at]))
    late = [pltpu.make_async_copy(head_in, h_in, in_sem.at[18]), pltpu.make_async_copy(dproj, d_in, in_sem.at[19])]
    for copy in late + comes:
        copy.start()
    turn_by = sums.shape[1] - here.b * cols

    def slice_of(value):
        return pltpu.roll(value, turn_by, 1)[:, 0:cols]

    mine = slice_of(sums[...])
    for out, (lo, count) in zip(outs[:8], ((0, 1), (1, 1), (7, 1), (6, 1), (2, 2), (4, 2), (9, 2), (8, 1))):
        out[...] = mine[lo:lo + count, :]
    wide = jnp.concatenate([gains[...], shifts[...], jnp.zeros((4, sums.shape[1]), F32)], axis=0)
    heads = slice_of(wide)
    outs[8][...] = heads[0:2, :]
    outs[9][...] = heads[2:4, :]
    outs[10][...] = sums[V_MP:V_MP + 2, :]
    outs[11][...] = sums[V_HEADS:V_HEADS + 2, 0:outs[11].shape[1]]
    two, one = 2 * HEAD_DIM, HEAD_DIM
    for t in range(3):
        qkv[t, :, 0:two] = grad[:, t * two:(t + 1) * two]
        qkv[t, :, two:two + one] = grad[:, 4 * two + t * one:4 * two + (t + 1) * one]
    turned[...] = jnp.zeros_like(turned)
    turned[0:cols, 0:two] = grad[:, 3 * two:4 * two]
    turned[0:cols, two:two + one] = grad[:, 4 * two + 3 * one:4 * two + 4 * one]
    out_w[...] = turned[...].T[0:two + one, 0:cols]
    for copy in late:
        copy.wait()
    for m in range(2):
        part = pltpu.roll(h_in[m].astype(F32), turn_by, 1)[:, 0:128].astype(BF16)
        head_out[m] = t_dot(part, d_in[m])[0:cols]
    for come, go in zip(comes, goes):
        come.wait()
        go.start()
    for go in goes:
        go.wait()


def spread(dims, sums, grad, gains, shifts, up, down, head_in, dproj, forward, back_img, back_txt):
    cols, model = grad.shape[0], sums.shape[1]
    local, quarter = dims.local, dims.quarter
    assert cols <= 128
    shapes = [(1, cols)] * 4 + [(2, cols)] * 3 + [(1, cols)] + [(2, cols)] * 2 + [(2, model), (2, local)]
    shapes += [(3, cols, local), (local, cols), up.shape, down.shape, (2, cols, dproj.shape[2])]
    held = pl.BlockSpec(memory_space=pltpu.VMEM)
    away = pl.BlockSpec(memory_space=pl.ANY)
    args = (sums, grad, gains, shifts, up, down, head_in, dproj)
    return pl.pallas_call(
        functools.partial(spread_kernel, dims, cols),
        in_specs=[held] * 4 + [away] * (len(args) - 4 + 10),
        out_specs=[held] * (len(shapes) - 3) + [away] * 2 + [held] + [away] * 4,
        out_shape=[jax.ShapeDtypeStruct(v, F32) for v in shapes]
        + [jax.ShapeDtypeStruct(v.shape, BF16) for v in (back_img, back_txt) * 2],
        scratch_shapes=[
            pltpu.VMEM((128, 256), F32),
            pltpu.VMEM((8, quarter, dims.patches, model), BF16), pltpu.VMEM((8, quarter, dims.caption, model), BF16),
            pltpu.VMEM(up.shape, F32), pltpu.VMEM(down.shape, F32),
            pltpu.VMEM(head_in.shape, BF16), pltpu.VMEM(dproj.shape, BF16),
            pltpu.SemaphoreType.DMA((20,)), pltpu.SemaphoreType.DMA((18,)),
        ],
        compiler_params=params(),
        cost_estimate=pl.CostEstimate(flops=1_000_000, bytes_accessed=20_000_000, transcendentals=0),
        name="spread",
    )(*args, *forward, back_img, back_txt)


def per_device(
    image_states, text_states, caption_lengths, image_cotangent, text_cotangent,
    first_gain, first_shift, query_key_value, query_value_bias, output_weight, output_bias,
    attention_scale, expert_gain, expert_shift, expert_up, expert_up_bias, expert_down,
    expert_down_bias, feedforward_scale, head_gain, head_shift, head_weight, logit_scale,
):
    pairs, patches, model = image_states.shape
    caption = text_states.shape[1]
    local = query_key_value.shape[2]
    quarter = pairs // 4
    batch_size = lax.axis_size("batch")
    assert lax.axis_size("mp") == 4 and pairs == 4 * quarter and quarter <= 3
    assert batch_size & (batch_size - 1) == 0
    assert local == 3 * HEAD_DIM
    ip, tp = up16(patches), up16(caption)
    dims = Dims(patches, caption, ip, tp, ip + tp, quarter, local)
    me = lax.axis_index("mp")
    batch_at = lax.axis_index("batch")
    order = me ^ jnp.asarray(ORDER, jnp.int32)
    vectors = (first_gain, first_shift, attention_scale, output_bias, expert_gain, expert_shift,
               feedforward_scale, expert_down_bias, head_gain, head_shift)
    own_w = jnp.transpose(query_key_value, (1, 2, 0)).reshape(3 * local, model)
    one_kernel = batch_size == 8 and model // batch_size % 32 == 0 and expert_up.shape[2] == model
    if one_kernel:
        (vec, normed, qkv_own, mixed_own, qkv_far, mixed_far, wf, attended, attn, e_own, e_peer, cls_own, cls_peer) = front(
            dims, caption_lengths, image_states, text_states, vectors, query_value_bias, own_w, output_weight)
    else:
        vec = jnp.concatenate([v.reshape(-1, model) for v in vectors] + [jnp.zeros((1, model), F32)])
        wo = jnp.concatenate([own_w, output_weight])
        wf = to_y(wo)
        far_bias = to_y(query_value_bias)
        normed, qkv_own, rest, mixed_own = attend_own(
            dims, order, caption_lengths, image_states, text_states, vec, query_value_bias, wo)
        qkv_far, mixed_far, a_keep, a_send = attend_far(
            dims, order, caption_lengths, normed, rest, mixed_own, far_bias, wo, wf)
        a_recv = to_core(a_send)
        attended, attn, e_own, cls_own = residual(
            dims, order, a_keep, a_recv, image_states, text_states, vec)
        e_peer = to_core(e_own)
        cls_peer = to_core(cls_own)
    if one_kernel:
        (dup, down_keep, down_send, dexp, d_own, d_near, up_sums, class_e, _, c_dup, _, dcls, head_in, dproj,
         grad_head_gain, grad_head_shift, scalars) = middle(
            dims, pairs * batch_size, image_cotangent, text_cotangent, e_own, e_peer, cls_own, cls_peer, vec,
            expert_up, expert_up_bias, expert_down, head_weight, logit_scale.reshape(1, 1))
        down_sum, up_keep, up_send, dattended, dattn, dattn_peer, fin_img, fin_txt, own_sums = turn(
            dims, image_cotangent, text_cotangent, e_peer, e_own, dup, class_e, c_dup, down_keep, down_send,
            dexp, attended, attn, d_own, d_near, dcls, vec)
    else:
        class_part, class_e = class_forward(dims, cls_own, cls_peer, expert_up, expert_up_bias, expert_down)
        class_parts = from_others(class_part, "mp", 1, 4)

        act_a, dup_a, ddn_a, d_send3, d_keep1, x_send3, x_keep1, bias_a, cot_a = experts(
            dims, "experts_a", 1, order[jnp.asarray([3, 1])], e_peer, e_own, image_cotangent, text_cotangent,
            tie(vec, class_part), expert_up, expert_up_bias, expert_down)
        x_recv1 = to_core(x_send3)
        d_recv1 = to_core(d_send3)
        final_class = class_final(
            dims, order, cls_own, cls_peer, class_parts, tie(vec, bias_a))
        class_blocks = gather_batch(final_class[None])
        x_near = add_low(x_keep1, x_recv1)
        x_far = to_y(x_near)
        act_b, dup_b, ddn_b, d_send2, d_keep0, x_send2, x_keep0, bias_b, cot_b = experts(
            dims, "experts_b", 0, order[jnp.asarray([2, 0])], e_peer, e_own, image_cotangent, text_cotangent,
            tie(vec, final_class, x_near), expert_up, expert_up_bias, expert_down)
        x_recv0 = to_core(x_send2)
        d_recv0 = to_core(d_send2)

        head_in, dproj, dclass, grad_head_gain, grad_head_shift, scalars = (contrast if batch_size <= 8 else contrast_large)(
            dims, pairs * batch_size, batch_at.reshape(1), class_blocks, tie(vec, bias_b), head_weight,
             logit_scale.reshape(1, 1))
        c_act, c_dup, c_ddn, c_dexp, c_bias, dcls = class_back(
            dims, order, class_e, cot_a, cot_b, dclass, vec, expert_up, expert_up_bias, expert_down)
        extras = from_others(c_dexp, "mp", 1, 4)
        d_far = to_y(add_low(d_keep1, tie(d_recv1, c_dexp)))
        expert_grad = expert_grads(
            dims, e_peer, e_own, act_a, dup_a, ddn_a, act_b, dup_b, ddn_b, class_e, c_act, c_dup, c_ddn)
        expert_sum = lax.psum_scatter(expert_grad, "batch", scatter_dimension=1, tiled=True)

        dattended, dattn, sums_two = norm_two(
            dims, order, x_keep0, x_recv0, x_far, attended, a_keep, a_recv, image_cotangent, text_cotangent,
            dcls, extras, tie(vec, expert_grad))
        dattn_peer = to_core(dattn)
        fin_img, fin_txt, sums_fin = final_rows(
            dims, order, d_keep0, d_recv0, d_far, attended, image_cotangent, text_cotangent, dcls,
            tie(vec, sums_two))
        own_sums = jnp.concatenate([sums_two[:6], sums_fin[:3]])
        up_sums = bias_a + bias_b + c_bias
    contrast_loss = scalars[0, :1]
    grad_logit_scale = scalars[1, :1]
    if one_kernel:
        (dnormed, grad_o01, grad_o2, cols_far, cols_own, near_img, near_txt, far_sum, grad_down,
         grad_up) = back(
            dims, caption_lengths, dattn, dattn_peer, normed, qkv_far, mixed_far, qkv_own, mixed_own,
            own_w, output_weight, wf, fin_img, fin_txt, up_keep, up_send, down_sum)
    else:
        n_keep, n_send, grad_far, grad_o2, cols_far = attend_back(
            dims, True, order, caption_lengths, dattn, dattn_peer, normed, qkv_far, mixed_far, own_w, output_weight, wf)
        n_keep, n_send, grad_o01, cols_own = attend_back(
            dims, False, order, caption_lengths, dattn, dattn_peer, normed, qkv_own, mixed_own, own_w, output_weight, wf,
            prior=(n_keep, n_send))
    cols = model // batch_size
    mine = lambda v, axis: lax.dynamic_slice_in_dim(v, batch_at * cols, cols, axis=axis)
    pair, single = 2 * HEAD_DIM, HEAD_DIM
    if one_kernel:
        core_img, core_txt, across_img, across_txt, back_img, back_txt, attn_grad, sums = finish(
            dims, dnormed, dattended, image_states, text_states, vec, fin_img, fin_txt,
            near_img, near_txt, grad_o01, far_sum, own_sums, up_sums, cols_own, cols_far)
        forward = (fin_img, fin_txt, near_img, near_txt, core_img, core_txt, across_img, across_txt)
        (*vectors, grad_qkv, grad_output_weight, grad_up, grad_down, grad_head_weight,
         image_output, text_output, image_grad, text_grad) = spread(
            dims, sums, attn_grad, grad_head_gain, grad_head_shift, grad_up, grad_down, head_in, dproj,
            forward, back_img, back_txt)
        flat = lambda v: v.reshape(-1)
        return (
            image_output,
            text_output,
            contrast_loss,
            image_grad,
            text_grad,
            flat(vectors[0]),
            flat(vectors[1]),
            jnp.transpose(grad_qkv, (1, 0, 2)),
            vectors[11],
            grad_output_weight,
            flat(vectors[2]),
            flat(vectors[3]),
            vectors[4],
            vectors[5],
            grad_up,
            vectors[10],
            jnp.transpose(grad_down, (0, 2, 1)),
            vectors[6],
            flat(vectors[7]),
            vectors[8],
            vectors[9],
            grad_head_weight,
            grad_logit_scale,
        )
    else:
        grad_head_weight = jnp.einsum("mnc,mne->mce", mine(head_in, 2), dproj, preferred_element_type=F32)
        grad_expert_up = expert_sum[:2].astype(F32)
        grad_expert_down = jnp.transpose(expert_sum[2:].astype(F32), (0, 2, 1))
        cols_own = cols_own.reshape(3, pair)[::2]
        cols_far = cols_far.reshape(3, 2 * pair)[::2]
        heads = jnp.concatenate([cols_own, cols_far[:, pair:pair + single]], axis=1)
        heads_far = jnp.concatenate([cols_far[:, :pair], cols_far[:, pair + single:]], axis=1)
        n_recv = to_core(n_send)
        d_img, d_txt, sums_one = norm_one(
            dims, order, n_keep, n_recv, dattended, image_states, text_states, vec)
        image_output = gather_rows(fin_img, me)
        text_output = gather_rows(fin_txt, me)
        image_grad = gather_rows(d_img, me)
        text_grad = gather_rows(d_txt, me)
        grad_own = jnp.concatenate([grad_o01, grad_o2], axis=1)
        grad_far = lax.psum_scatter(grad_far, "batch", scatter_dimension=0, tiled=True)
        grad_own = lax.psum_scatter(grad_own, "batch", scatter_dimension=0, tiled=True)
        attn_grad = grad_own.astype(F32) + to_y(grad_far).astype(F32)
        heads = heads + to_y(heads_far)
        own_sums = sum_over(jnp.concatenate([sums_one[:2], own_sums]), "mp")
        flat = jnp.concatenate([own_sums.reshape(-1), heads.reshape(-1), up_sums.reshape(-1)])
        count = flat.shape[0]
        flat = jnp.pad(flat, (0, -count % 1024)).reshape(-1, 128)
        flat = sum_over(flat, "batch").reshape(-1)[:count]
        done = own_sums.shape[0]
        own_sums = mine(flat[:done * model].reshape(done, model), 1)
        heads = flat[done * model:done * model + 2 * local].reshape(2, local)
        grad_expert_up_bias = flat[done * model + 2 * local:].reshape(up_sums.shape)
    attn_grad = jnp.concatenate(
        [attn_grad[:, :4 * pair].reshape(cols, 4, pair), attn_grad[:, 4 * pair:].reshape(cols, 4, single)], axis=2)
    grad_query_key_value = attn_grad[:, :3]
    grad_output_weight = jnp.transpose(attn_grad[:, 3])
    return (
        image_output,
        text_output,
        contrast_loss,
        image_grad,
        text_grad,
        own_sums[0],
        own_sums[1],
        grad_query_key_value,
        heads,
        grad_output_weight,
        own_sums[7],
        own_sums[6],
        own_sums[2:4],
        own_sums[4:6],
        grad_expert_up,
        grad_expert_up_bias,
        grad_expert_down,
        own_sums[9:11],
        own_sums[8],
        mine(grad_head_gain, 1),
        mine(grad_head_shift, 1),
        grad_head_weight,
        grad_logit_scale,
    )


def solution(mesh):
    return jax.shard_map(
        per_device,
        mesh=mesh,
        in_specs=(
            P("batch", None, None),
            P("batch", None, None),
            P("batch"),
            P("batch", None, None),
            P("batch", None, None),
            P(),
            P(),
            P(None, None, "mp"),
            P(None, "mp"),
            P("mp", None),
            P(),
            P(),
            P(),
            P(),
            P(None, None, "mp"),
            P(None, "mp"),
            P(None, "mp", None),
            P(),
            P(),
            P(),
            P(),
            P(),
            P(),
        ),
        out_specs=(
            P("batch", None, None),
            P("batch", None, None),
            P(),
            P("batch", None, None),
            P("batch", None, None),
            P("batch"),
            P("batch"),
            P("batch", None, "mp"),
            P(None, "mp"),
            P("mp", "batch"),
            P("batch"),
            P("batch"),
            P(None, "batch"),
            P(None, "batch"),
            P(None, "batch", "mp"),
            P(None, "mp"),
            P(None, "mp", "batch"),
            P(None, "batch"),
            P("batch"),
            P(None, "batch"),
            P(None, "batch"),
            P(None, "batch", None),
            P(),
        ),
        check_vma=False,
    )
```
